32 devices in a mesh: dp: 8 (over z, x), tensor: 4 (over y, core).
Axes of the slice: x: 2, y: 2, z: 4, core: 2. Of those that a mesh axis runs over, the one named last changes fastest.
Arguments:
- tokens: bfloat16 [32768, 768], P(('dp', 'tensor')), may hold values from -6 to 6
- segments: int32 [256, 128], P('dp'), may hold values from 0 to 7, never falling along the last dimension, each value on 1 to 32 neighbouring positions
- out_grad: float32 [32768, 768], P(('dp', 'tensor')), may hold values from -6 to 6
- owner: int32 [192], replicated, may hold values from 0 to 191, as said below
- master: float32 [4, 192, 96, 96], P('tensor', 'dp'), may hold values from -0.57735027 to 0.57735027
- left_basis: float32 [4, 192, 96, 96], P('tensor', 'dp'), may hold values from -1 to 1, as said below
- right_basis: float32 [4, 192, 96, 96], P('tensor', 'dp'), may hold values from -1 to 1, as said below
- first_moment: float32 [4, 192, 96, 96], P('tensor', 'dp'), may hold values from -384 to 384
- second_moment: float32 [4, 192, 96, 96], P('tensor', 'dp'), may hold values from 1966.08 to 16384
- vectors: float32 [9216], replicated, may hold values from -0.9 to 1.5
- vector_first: float32 [9216], replicated, may hold values from -512 to 512
- vector_second: float32 [9216], replicated, may hold values from 3932.16 to 32768
Outputs:
- layer_out: float32 [32768, 768], P(('dp', 'tensor'))
- input_grad: float32 [32768, 768], P(('dp', 'tensor'))
- new_master: float32 [4, 192, 96, 96], P('tensor', 'dp')
- new_first: float32 [4, 192, 96, 96], P('tensor', 'dp')
- new_second: float32 [4, 192, 96, 96], P('tensor', 'dp')
- new_vectors: float32 [9216], replicated
- new_vector_first: float32 [9216], replicated
- new_vector_second: float32 [9216], replicated
The draws below stay inside these ranges and needn't reach their ends.
Inputs may be any that keep to these rules, and one draw needn't show every extreme that they name: A permutation of 0 to 191: slot s holds tile owner[s]. `segments`: within each packed row the numbers never fall; every number of a row names 1 to 32 tokens, some exactly 32. `left_basis`: each slot is an orthogonal matrix. `right_basis`: each slot is an orthogonal matrix.
All inputs are finite; a program needn't handle non-finite values.
Results may differ from the reference program's by a relative error of at most 0.011.
Values may be sent and summed in bfloat16 or wider, within the bound.
No kernel may reach another device: no remote copies, remote signals or barrier semaphores. Data moves between devices by JAX's collectives and lax.ppermute only.
A program may use at most 192 MiB of HBM per device.

```python
import math
import jax
import jax.numpy as jnp
import numpy as np
from jax import lax

HEADS = 12
HEAD_DIM = 64
D = 768
FF = 3072
LEN = 128
SEQ_DEV = 32
SEGS = 8
SEG_MOST = 32
BLK = 96
ADAM_STEP = 3
PACKS = 256
TOKENS = 32768
TILES = 192
NV = 9216
N_DP = 8
N_TENSOR = 4


def slot_order(key):
    return jax.random.permutation(jax.random.fold_in(key, 11), TILES).astype(jnp.int32)


def draw_owner(key, part):
    return slot_order(key)


def draw_master(key, part):
    slot_tiles = slot_order(key)
    wide_q = 3 * D // N_TENSOR
    count_q = D // BLK * (wide_q // BLK)
    count_o = D // N_TENSOR // BLK * (D // BLK)
    count_up = D // BLK * (FF // N_TENSOR // BLK)
    kind_scale = jnp.where(slot_tiles < count_q, D ** (-0.5), jnp.where(slot_tiles < count_q + count_o, (D // 16) ** (-0.5), jnp.where(slot_tiles < count_q + count_o + count_up, D ** (-0.5), FF ** (-0.5))))
    full_shape = (N_TENSOR, TILES, BLK, BLK)
    random_part = jnp.clip(jax.random.normal(jax.random.fold_in(key, 12), full_shape, jnp.float32), -4.0, 4.0)
    return random_part * kind_scale.astype(jnp.float32)[None, :, None, None]


def orthogonal_tiles(key):
    column_index = jnp.arange(BLK, dtype=jnp.float32)
    weighting = jnp.where(column_index == 0, (1.0 / BLK) ** 0.5, (2.0 / BLK) ** 0.5)
    cosine_table = jnp.cos(jnp.pi * (column_index[:, None] + 0.5) * column_index[None, :] / BLK) * weighting[None, :]
    tile_keys = jax.random.split(key, N_TENSOR * TILES)
    column_orders = jax.vmap(lambda single: jax.random.permutation(single, BLK))(tile_keys)
    sign_bits = jax.vmap(lambda single: jax.random.randint(jax.random.fold_in(single, 5), (BLK,), 0, 2))(tile_keys)
    chosen = jnp.transpose(jnp.take(cosine_table, column_orders, axis=1), (1, 0, 2))
    chosen = chosen * (2 * sign_bits - 1).astype(jnp.float32)[:, :, None]
    return chosen.reshape(N_TENSOR, TILES, BLK, BLK)


def draw_left_basis(key, part):
    return orthogonal_tiles(jax.random.fold_in(key, 21))


def draw_right_basis(key, part):
    return orthogonal_tiles(jax.random.fold_in(key, 22))


def draw_vectors(key, part):
    total_len = 8 * D + FF
    position = jnp.arange(total_len)
    gains = 1.0 + 0.15 * jnp.clip(jax.random.normal(jax.random.fold_in(key, 31), (total_len,), jnp.float32), -3.0, 3.0)
    shifts = 0.3 * jnp.clip(jax.random.normal(jax.random.fold_in(key, 32), (total_len,), jnp.float32), -3.0, 3.0)
    return jnp.where(position < 2 * D, gains, shifts)


def steps_of(stream_key, dims, pieces, low, largest):
    def one(axis_at, shards_of):
        draws = jax.random.uniform(jax.random.fold_in(jax.random.fold_in(stream_key, 6), axis_at), (shards_of,), jnp.float32, low / len(pieces), largest / len(pieces))
        return jnp.repeat(jnp.exp(draws), dims[axis_at] // shards_of).reshape((-1,) + (1,) * (len(dims) - axis_at - 1))

    loudness = one(*pieces[0])
    for cut in pieces[1:]:
        loudness = loudness * one(*cut)
    return loudness


def length_profile(amount, total, limit, slope):
    weights = [(1 << 20) // math.isqrt(grade ** slope) + 1 for grade in range(2, amount + 1)]
    rest, holding = total - limit - (amount - 1), [1] * (amount - 1)
    while rest > 0:
        free = [i for i in range(amount - 1) if holding[i] < limit]
        whole, remaining = sum([weights[i] for i in free]), rest
        for i in free:
            addition = min(limit - holding[i], max(1, remaining * weights[i] // whole), rest)
            holding[i] = holding[i] + addition
            rest = rest - addition
    return np.array([limit] + holding)


def uneven_parts(rng, amount, total, bound, skew):
    if amount == 2:
        one = jax.random.randint(rng, (), max(1, total - bound), min(bound, total - 1) + 1)
        return jnp.stack([one, total - one])
    tallies = jnp.asarray(length_profile(amount, total, bound, skew), jnp.int32)
    pairs = (amount - 1) // 2
    donor, receiver = tallies[1:1 + 2 * pairs:2], tallies[2:2 + 2 * pairs:2]
    margin = jnp.minimum(donor - 1, bound - receiver)
    shifted = jax.random.randint(jax.random.fold_in(rng, 1), (pairs,), 0, 1 << 20) % (margin + 1)
    tallies = tallies.at[1:1 + 2 * pairs:2].set(donor - shifted).at[2:2 + 2 * pairs:2].set(receiver + shifted)
    return tallies[jax.random.permutation(jax.random.fold_in(rng, 2), amount)]


def noise(key, extent, spread, reach, cuts=(), kind=jnp.bfloat16):
    level = steps_of(key, extent, cuts, -0.22, 0.18) if cuts else 1.0
    drawn = jax.random.normal(key, extent, jnp.float32) * spread * level
    return jnp.minimum(jnp.maximum(drawn, -reach), reach).astype(kind)


def setup_inputs(seed: int = 0) -> dict:
    arg_keys = jax.random.split(jax.random.key(seed), 13)
    tokens = noise(arg_keys[0], (TOKENS, D), 1.0, 6.0, ((0, 32),))
    segments = jax.vmap(lambda own: jnp.searchsorted(jnp.cumsum(uneven_parts(own, SEGS, LEN, SEG_MOST, 2)), jnp.arange(LEN), side="right"))(jax.random.split(arg_keys[1], PACKS)).reshape((PACKS, LEN)).astype(jnp.int32)
    out_grad = noise(arg_keys[2], (TOKENS, D), 1.0, 6.0, ((0, 32),), jnp.float32)
    owner = draw_owner(jax.random.fold_in(arg_keys[12], 71), 0)
    master = draw_master(jax.random.fold_in(arg_keys[12], 71), 0)
    left_basis = draw_left_basis(jax.random.fold_in(arg_keys[12], 71), 0)
    right_basis = draw_right_basis(jax.random.fold_in(arg_keys[12], 71), 0)
    first_moment = noise(arg_keys[7], (N_TENSOR, TILES, BLK, BLK), (0.35 * TOKENS ** 0.5), 384.0, ((0, 4), (1, 8)), jnp.float32)
    second_moment = jnp.clip(jnp.exp(math.log(16384.0) - 2.1202636 * jax.random.uniform(arg_keys[8], (N_TENSOR, TILES, BLK, BLK), jnp.float32) ** steps_of(arg_keys[8], (N_TENSOR, TILES, BLK, BLK), ((0, 4), (1, 8)), -0.2, 0.2)), 1966.08, 16384.0)
    vectors = draw_vectors(jax.random.fold_in(arg_keys[12], 71), 0)
    vector_first = noise(arg_keys[10], (NV,), (0.5 * TOKENS ** 0.5), 512.0, (), jnp.float32)
    vector_second = jnp.clip(jnp.exp(jax.random.uniform(arg_keys[11], (NV,), jnp.float32, math.log(3932.16), math.log(32768.0))), 3932.16, 32768.0)
    return {"tokens": tokens, "segments": segments, "out_grad": out_grad, "owner": owner, "master": master, "left_basis": left_basis, "right_basis": right_basis, "first_moment": first_moment, "second_moment": second_moment, "vectors": vectors, "vector_first": vector_first, "vector_second": vector_second}


@jax.custom_vjp
def low(v):
    return lax.optimization_barrier(v.astype(jnp.bfloat16)).astype(jnp.float32)

@jax.custom_vjp
def low_back(v):
    return v

def low_keep(v):
    return (low(v), None)

def low_pass(kept, grad):
    return (grad,)

def back_keep(v):
    return (v, None)

def back_low(kept, grad):
    return (low(grad),)
low.defvjp(low_keep, low_pass)
low_back.defvjp(back_keep, back_low)
HIGHEST_PRECISION = lax.Precision.HIGHEST
NORM_EPS = 1e-12
ADAM_EPS = 1e-08
MATRIX_RATE = 0.01
VECTOR_RATE = 0.1
DECAY_FIRST = 0.5
DECAY_SECOND = 0.5
MASKED = -1e+30

def product(left_side, right_side):
    return jnp.dot(left_side, right_side, precision=HIGHEST_PRECISION, preferred_element_type=jnp.float32)

def batched(left_side, right_side):
    return jnp.matmul(left_side, right_side, precision=HIGHEST_PRECISION)

def join_tiles(tile_stack, row_count, col_count):
    block_size = tile_stack.shape[-1]
    return tile_stack.reshape(row_count // block_size, col_count // block_size, block_size, block_size).transpose(0, 2, 1, 3).reshape(row_count, col_count)

def assemble(tile_stack):
    shards = N_TENSOR
    wide_q = 3 * D // shards
    out_rows = D // shards
    up_cols = FF // shards
    count_q = D // BLK * (wide_q // BLK)
    count_o = out_rows // BLK * (D // BLK)
    count_up = D // BLK * (up_cols // BLK)
    first_end = count_q + count_o
    second_end = first_end + count_up
    w_qkv = jnp.stack([join_tiles(tile_stack[member, :count_q], D, wide_q) for member in range(shards)], 1).reshape(D, shards * wide_q)
    w_out = jnp.concatenate([join_tiles(tile_stack[member, count_q:first_end], out_rows, D) for member in range(shards)], 0)
    w_up = jnp.stack([join_tiles(tile_stack[member, first_end:second_end], D, up_cols) for member in range(shards)], 1).reshape(D, FF)
    w_down = jnp.concatenate([join_tiles(tile_stack[member, second_end:], up_cols, D) for member in range(shards)], 0)
    return (w_qkv, w_out, w_up, w_down)

def norm_apply(summed, gain_row, offset):
    centred = summed - lax.optimization_barrier(jnp.mean(summed, -1, keepdims=True))
    inverse = lax.rsqrt(lax.optimization_barrier(jnp.mean(centred * centred, -1, keepdims=True)) + NORM_EPS)
    return centred * inverse * gain_row + offset

def layer_block(rows_in, row_segments, w_qkv, w_out, w_up, w_down, vector_all):
    shards = N_TENSOR
    local_heads = HEADS // shards
    head_width = local_heads * HEAD_DIM
    pack_count = row_segments.shape[0]
    gain_first = vector_all[0:D]
    gain_second = vector_all[D:2 * D]
    bias_q = vector_all[2 * D:3 * D]
    bias_v = vector_all[3 * D:4 * D]
    bias_out = vector_all[4 * D:5 * D]
    bias_up = vector_all[5 * D:5 * D + FF]
    bias_down = vector_all[5 * D + FF:6 * D + FF]
    offset_first = vector_all[6 * D + FF:7 * D + FF]
    offset_second = vector_all[7 * D + FF:8 * D + FF]
    zero_keys = jnp.zeros((shards, head_width), jnp.float32)
    bias_qkv = jnp.stack([bias_q.reshape(shards, head_width), zero_keys, bias_v.reshape(shards, head_width)], 1).reshape(-1)
    packed = low_back(low(product(rows_in, w_qkv) + bias_qkv))
    sections = packed.reshape(pack_count, LEN, shards, 3, local_heads, HEAD_DIM)
    target = (pack_count, LEN, HEADS, HEAD_DIM)
    queries = sections[:, :, :, 0].reshape(target)
    key_rows = sections[:, :, :, 1].reshape(target)
    values = sections[:, :, :, 2].reshape(target)
    scores = jnp.einsum('pqhe,pkhe->phqk', queries, key_rows, precision=HIGHEST_PRECISION) * HEAD_DIM ** (-0.5)
    allowed = (row_segments[:, :, None] == row_segments[:, None, :])[:, None]
    scores = low_back(jnp.where(allowed, scores, MASKED))
    probs_low = low(jnp.exp(scores - jax.nn.logsumexp(scores, -1, keepdims=True)))
    mixture = jnp.einsum('phqk,pkhe->pqhe', probs_low, values, precision=HIGHEST_PRECISION).reshape(rows_in.shape[0], D)
    attended = low_back(low(mixture))
    normed = norm_apply(rows_in + low_back(product(attended, w_out)) + bias_out, gain_first, offset_first)
    hidden_pre = low_back(product(low(normed), w_up) + bias_up)
    activated = low(jax.nn.gelu(hidden_pre, approximate=False))
    return norm_apply(normed + low_back(product(activated, w_down)) + bias_down, gain_second, offset_second)

def reference(tokens, segments, out_grad, owner, master, left_basis, right_basis, first_moment, second_moment, vectors, vector_first, vector_second):

    def forward(rows_all, master_tiles, vector_all):
        tile_stack = jnp.zeros_like(master_tiles).at[:, owner].set(master_tiles)
        w_qkv, w_out, w_up, w_down = [low(matrix) for matrix in assemble(tile_stack)]

        def one_block(rows_in, row_segments):
            return layer_block(rows_in, row_segments, w_qkv, w_out, w_up, w_down, vector_all)
        checked = jax.checkpoint(one_block)

        def scan_step(running, inputs_pair):
            return (running, checked(inputs_pair[0], inputs_pair[1]))
        _, outputs = lax.scan(scan_step, jnp.zeros((), jnp.float32), (rows_all.reshape(N_DP, SEQ_DEV * LEN, D), segments.reshape(N_DP, SEQ_DEV, LEN)))
        return outputs.reshape(TOKENS, D)
    layer_out, pullback = jax.vjp(forward, tokens.astype(jnp.float32), master, vectors)
    input_grad, master_grad, vector_grad = pullback(out_grad)
    bias_first = 1.0 - DECAY_FIRST ** ADAM_STEP
    bias_second = 1.0 - DECAY_SECOND ** ADAM_STEP
    rotated = batched(jnp.swapaxes(left_basis, -1, -2), batched(master_grad, right_basis))
    new_first = DECAY_FIRST * first_moment + (1.0 - DECAY_FIRST) * rotated
    new_second = DECAY_SECOND * second_moment + (1.0 - DECAY_SECOND) * rotated * rotated
    direction = new_first / bias_first / (jnp.sqrt(new_second / bias_second) + ADAM_EPS)
    new_master = master - MATRIX_RATE * batched(batched(left_basis, direction), jnp.swapaxes(right_basis, -1, -2))
    new_vector_first = DECAY_FIRST * vector_first + (1.0 - DECAY_FIRST) * vector_grad
    new_vector_second = DECAY_SECOND * vector_second + (1.0 - DECAY_SECOND) * vector_grad * vector_grad
    new_vectors = vectors - VECTOR_RATE * (new_vector_first / bias_first) / (jnp.sqrt(new_vector_second / bias_second) + ADAM_EPS)
    return (layer_out, input_grad, new_master, new_first, new_second, new_vectors, new_vector_first, new_vector_second)
```

```python
import jax
import jax.numpy as jnp
from jax import lax
from jax.sharding import PartitionSpec as P

HEADS = 12
HEAD_DIM = 64
D = 768
FF = 3072
ADAM_STEP = 3


NORM_EPS = 1e-12
ADAM_EPS = 1e-08
MATRIX_RATE = 0.01
VECTOR_RATE = 0.1
DECAY_FIRST = 0.5
DECAY_SECOND = 0.5
MASKED = -1e30


def product(left_side, right_side):
    return jnp.dot(left_side, right_side, preferred_element_type=jnp.float32)


def times_transposed(left_side, right_side):
    return lax.dot_general(
        left_side, right_side, (((1,), (1,)), ((), ())), preferred_element_type=jnp.float32
    )


def transposed_times(left_side, right_side):
    return lax.dot_general(
        left_side, right_side, (((0,), (0,)), ((), ())), preferred_element_type=jnp.float32
    )


def precise(left_side, right_side):
    return jnp.matmul(left_side, right_side, precision=lax.Precision.HIGHEST)


def head_parts(packed, pack_count, groups, local_heads):
    length = packed.shape[0] // pack_count
    sections = packed.reshape(pack_count, length, groups, 3, local_heads, HEAD_DIM)
    target = (pack_count, length, groups * local_heads, HEAD_DIM)
    return (
        sections[:, :, :, 0].reshape(target),
        sections[:, :, :, 1].reshape(target),
        sections[:, :, :, 2].reshape(target),
    )


def score_block(queries, key_rows, row_segments):
    scores = jnp.einsum(
        "pqhe,pkhe->phqk", queries, key_rows, preferred_element_type=jnp.float32
    ) * HEAD_DIM ** (-0.5)
    allowed = (row_segments[:, :, None] == row_segments[:, None, :])[:, None]
    return jnp.where(allowed, scores, MASKED)


def attention_forward(packed, row_segments, groups, local_heads):
    queries, key_rows, values = head_parts(packed, row_segments.shape[0], groups, local_heads)
    scores = score_block(queries, key_rows, row_segments)
    log_total = jax.nn.logsumexp(scores, -1, keepdims=True)
    probs_low = jnp.exp(scores - log_total).astype(jnp.bfloat16)
    mixture = jnp.einsum("phqk,pkhe->pqhe", probs_low, values, preferred_element_type=jnp.float32)
    return (mixture.reshape(packed.shape[0], -1).astype(jnp.bfloat16), log_total)


def attention_backward(packed, row_segments, log_total, upstream, groups, local_heads):
    pack_count, length = row_segments.shape
    queries, key_rows, values = head_parts(packed, pack_count, groups, local_heads)
    probs_full = jnp.exp(score_block(queries, key_rows, row_segments) - log_total)
    grad_mixture = upstream.reshape(pack_count, length, groups * local_heads, HEAD_DIM)
    grad_probs = jnp.einsum(
        "pqhe,pkhe->phqk", grad_mixture, values, preferred_element_type=jnp.float32
    )
    centre = jnp.sum(grad_probs * probs_full, -1, keepdims=True)
    grad_scores = (probs_full * (grad_probs - centre)).astype(jnp.bfloat16)
    factor = HEAD_DIM ** (-0.5)
    grad_queries = (
        jnp.einsum("phqk,pkhe->pqhe", grad_scores, key_rows, preferred_element_type=jnp.float32)
        * factor
    )
    grad_keys = (
        jnp.einsum("phqk,pqhe->pkhe", grad_scores, queries, preferred_element_type=jnp.float32)
        * factor
    )
    grad_values = jnp.einsum(
        "phqk,pqhe->pkhe",
        probs_full.astype(jnp.bfloat16),
        grad_mixture,
        preferred_element_type=jnp.float32,
    )
    stacked = jnp.stack(
        [
            member.reshape(pack_count, length, groups, local_heads, HEAD_DIM)
            for member in (grad_queries, grad_keys, grad_values)
        ],
        3,
    )
    return stacked.reshape(packed.shape[0], -1).astype(jnp.bfloat16)


def norm_forward(summed, gain_row, offset):
    centred = summed - jnp.mean(summed, -1, keepdims=True)
    inverse = lax.rsqrt(jnp.mean(centred * centred, -1, keepdims=True) + NORM_EPS)
    unit_rows = centred * inverse
    return (unit_rows * gain_row + offset, unit_rows, inverse)


def norm_backward(gradient, unit_rows, inverse, gain_row):
    scaled = gradient * gain_row
    grad_in = inverse * (
        scaled
        - jnp.mean(scaled, -1, keepdims=True)
        - unit_rows * jnp.mean(scaled * unit_rows, -1, keepdims=True)
    )
    return (grad_in, jnp.sum(gradient * unit_rows, 0), jnp.sum(gradient, 0))


PARTS = 8
SUB = 12


def rounded(values):
    return lax.reduce_precision(values, 8, 7)


def split_terms(values, count):
    terms = []
    for _ in range(count):
        top = rounded(values)
        terms.append(top.astype(jnp.bfloat16))
        values = values - top
    return terms


def exact_product(values, selector, count):
    return sum(product(term, selector) for term in split_terms(values, count))


def exact_product_t(values, selector, count):
    return sum(times_transposed(term, selector) for term in split_terms(values, count))


def part_of_block(block):
    return (block % 4) * 2 + block // 4


def feature_order(rank):
    place = lax.iota(jnp.int32, D)
    part = part_of_block(place // (D // PARTS)) ^ rank
    inner = place % (D // PARTS)
    return (inner // SUB) * (PARTS * SUB) + part * SUB + inner % SUB


def tile_counts(shards, block_size):
    rows = D // block_size
    qkv = rows * (3 * D // shards // block_size)
    out = rows * (D // shards // block_size)
    up = rows * (FF // shards // block_size)
    return (qkv, out, up)


def slabs_from_tiles(tiles, shards, block_size):
    cut = tiles.shape[1]
    qkv, out, up = tile_counts(shards, block_size)
    rows = D // block_size

    def by_rows(part):
        cols = part.shape[0] // rows
        part = part.reshape(rows, cols, cut, SUB, block_size)
        return part.transpose(2, 0, 3, 1, 4).reshape(cut, rows * SUB, cols * block_size)

    def by_cols(part):
        cols = part.shape[0] // rows
        part = part.reshape(cols, rows, cut, SUB, block_size)
        return part.transpose(2, 1, 3, 0, 4).reshape(cut, rows * SUB, cols * block_size)

    return jnp.concatenate(
        [
            by_rows(tiles[:qkv]),
            by_cols(tiles[qkv : qkv + out]),
            by_rows(tiles[qkv + out : qkv + out + up]),
            by_cols(tiles[qkv + out + up :]),
        ],
        2,
    )


def tiles_from_slabs(slabs, shards, block_size):
    cut = slabs.shape[0]
    rows = D // block_size
    width_qkv, width_out, width_up = 3 * D // shards, D // shards, FF // shards

    def by_rows(part):
        cols = part.shape[2] // block_size
        part = part.reshape(cut, rows, SUB, cols, block_size)
        return part.transpose(1, 3, 0, 2, 4).reshape(rows * cols, cut, SUB, block_size)

    def by_cols(part):
        cols = part.shape[2] // block_size
        part = part.reshape(cut, rows, SUB, cols, block_size)
        return part.transpose(3, 1, 0, 2, 4).reshape(rows * cols, cut, SUB, block_size)

    first = width_qkv + width_out
    second = first + width_up
    return jnp.concatenate(
        [
            by_rows(slabs[:, :, :width_qkv]),
            by_cols(slabs[:, :, width_qkv:first]),
            by_rows(slabs[:, :, first:second]),
            by_cols(slabs[:, :, second:]),
        ],
        0,
    )


def swap_over(values, over_dp, over_tensor):
    dp, tensor = lax.axis_size("dp"), lax.axis_size("tensor")
    pairs = [
        (a * tensor + b, (a ^ over_dp) * tensor + (b ^ over_tensor))
        for a in range(dp)
        for b in range(tensor)
    ]
    return lax.ppermute(values, ("dp", "tensor"), pairs)


def gather_piece(slab):
    along_z = jnp.concatenate([slab] + [swap_over(slab, 2 * k, 0) for k in (1, 2, 3)], 0)
    here = {(0, 0): along_z}
    for y, x in ((0, 1), (1, 0), (1, 1)):
        here[y, x] = swap_over(along_z, x, 2 * y)
    there = {key: swap_over(block, 0, 1) for key, block in here.items()}
    return [
        jnp.concatenate([source[y, 0], source[y, 1]], 0)
        for y in (0, 1)
        for source in (here, there)
    ]


def reduce_piece(parts):
    def total(*terms):
        return sum(term.astype(jnp.float32) for term in terms)

    low = [
        total(parts[2 * y], swap_over(parts[2 * y + 1], 0, 1)).astype(jnp.bfloat16) for y in (0, 1)
    ]
    half = low[0].shape[0] // 2
    plane = total(
        low[0][:half],
        swap_over(low[0][half:], 1, 0),
        swap_over(low[1][:half], 0, 2),
        swap_over(low[1][half:], 1, 2),
    ).astype(jnp.bfloat16)
    rows = half // 4
    return total(
        plane[:rows],
        *[swap_over(plane[k * rows : (k + 1) * rows], 2 * k, 0) for k in (1, 2, 3)],
    )


def sum_over_all(values):
    for over_dp, over_tensor in ((0, 1), (0, 2), (1, 0), (2, 0), (4, 0)):
        values = values + swap_over(values, over_dp, over_tensor)
    return values


def local(
    tokens,
    segments,
    out_grad,
    owner,
    master,
    left_basis,
    right_basis,
    first_moment,
    second_moment,
    vectors,
    vector_first,
    vector_second,
):
    shards = lax.axis_size("tensor")
    dp_size = lax.axis_size("dp")
    direct = dp_size == PARTS and shards == 4
    tensor_rank = lax.axis_index("tensor")
    dp_rank = lax.axis_index("dp")
    local_heads = HEADS // shards
    head_width = local_heads * HEAD_DIM
    up_width = FF // shards
    width_qkv = 3 * head_width
    block_size = master.shape[-1]
    slots = master.shape[1]
    row_count = tokens.shape[0]
    length = segments.shape[1]
    pack_count = row_count // length
    own_segments = lax.dynamic_slice_in_dim(segments, tensor_rank * pack_count, pack_count, 0)
    qkv_tiles, out_tiles, up_tiles = tile_counts(shards, block_size)
    tile_total = owner.shape[0]

    group_base = tensor_rank if direct else 0
    order = feature_order(dp_rank if direct else 0)
    selector = (lax.iota(jnp.int32, D)[:, None] == order[None, :]).astype(jnp.bfloat16)

    def flipped(index):
        from_out = (index >= qkv_tiles) & (index < qkv_tiles + out_tiles)
        return (from_out | (index >= qkv_tiles + out_tiles + up_tiles))[:, None, None]

    own_tiles = lax.dynamic_slice_in_dim(owner, dp_rank * slots, slots, 0)
    own_flip = flipped(own_tiles)
    sent = master[0].astype(jnp.bfloat16)
    sent = jnp.where(own_flip, jnp.swapaxes(sent, 1, 2), sent)
    placing = (lax.iota(jnp.int32, tile_total)[:, None] == owner[None, :]).astype(jnp.bfloat16)
    if direct:
        parts = sent.reshape(slots, PARTS, SUB * block_size).swapaxes(0, 1)
        parts = lax.all_to_all(parts, "dp", 0, 0, tiled=True).reshape(tile_total, -1)
        tiles = product(placing, parts).astype(jnp.bfloat16)
        slab = slabs_from_tiles(tiles.reshape(tile_total, 1, SUB, block_size), shards, block_size)[0]
        pieces = [gather_piece(slab[:, k * D : (k + 1) * D]) for k in range(3)]
    else:
        gathered = lax.all_gather(sent, "dp", axis=0, tiled=True).reshape(tile_total, -1)
        tiles = product(placing, gathered).astype(jnp.bfloat16)
        slabs = slabs_from_tiles(
            tiles.reshape(tile_total, PARTS, SUB, block_size), shards, block_size
        )
        whole = jnp.concatenate([slabs[part_of_block(k)] for k in range(PARTS)], 0)
        every = lax.all_gather(whole, "tensor", axis=0)
        pieces = [
            [every[j][:, k * D : (k + 1) * D] for j in range(shards)] for k in range(3)
        ]
    w_qkv = [piece[:, :width_qkv] for piece in pieces[0]]
    w_out = [piece[:, width_qkv:] for piece in pieces[0]]
    w_up, w_down = pieces[1], pieces[2]

    group_order = lax.iota(jnp.int32, shards) ^ group_base
    d_vectors = jnp.stack(
        [
            vectors[0:D],
            vectors[D : 2 * D],
            vectors[4 * D : 5 * D],
            vectors[5 * D + FF : 6 * D + FF],
            vectors[6 * D + FF : 7 * D + FF],
            vectors[7 * D + FF : 8 * D + FF],
        ]
    )
    gain_first, gain_second, bias_out, bias_down, offset_first, offset_second = exact_product(
        d_vectors, selector, 3
    )
    bias_q = vectors[2 * D : 3 * D].reshape(shards, head_width)[group_order]
    bias_v = vectors[3 * D : 4 * D].reshape(shards, head_width)[group_order]
    bias_up = vectors[5 * D : 5 * D + FF].reshape(shards, up_width)[group_order]
    zero_keys = jnp.zeros((head_width,), jnp.float32)

    rows_in = product(tokens, selector).astype(jnp.bfloat16)
    grad_out = exact_product(out_grad, selector, 2)

    packed = jnp.concatenate(
        [
            (
                product(rows_in, w_qkv[j]) + jnp.concatenate([bias_q[j], zero_keys, bias_v[j]])
            ).astype(jnp.bfloat16)
            for j in range(shards)
        ],
        1,
    )
    attended, log_total = attention_forward(packed, own_segments, shards, local_heads)
    attn_sum = sum(
        times_transposed(attended[:, j * head_width : (j + 1) * head_width], w_out[j])
        for j in range(shards)
    )
    normed, unit_first, inverse_first = norm_forward(
        rows_in.astype(jnp.float32) + attn_sum + bias_out, gain_first, offset_first
    )
    normed_low = normed.astype(jnp.bfloat16)
    hidden_pre = [product(normed_low, w_up[j]) + bias_up[j] for j in range(shards)]
    activated = [jax.nn.gelu(pre, approximate=False).astype(jnp.bfloat16) for pre in hidden_pre]
    ffn_sum = sum(times_transposed(activated[j], w_down[j]) for j in range(shards))
    layer_out, unit_second, inverse_second = norm_forward(
        normed + ffn_sum + bias_down, gain_second, offset_second
    )
    grad_second, grad_gain_second, grad_offset_second = norm_backward(
        grad_out, unit_second, inverse_second, gain_second
    )
    grad_bias_down = jnp.sum(grad_second, 0)
    second_low = grad_second.astype(jnp.bfloat16)
    grad_w_down = [
        transposed_times(second_low, activated[j]).astype(jnp.bfloat16) for j in range(shards)
    ]
    grad_pre = []
    for j in range(shards):
        _, gelu_pull = jax.vjp(lambda v: jax.nn.gelu(v, approximate=False), hidden_pre[j])
        grad_pre.append(gelu_pull(product(second_low, w_down[j]))[0].astype(jnp.bfloat16))
    grad_w_up = [
        transposed_times(normed_low, grad_pre[j]).astype(jnp.bfloat16) for j in range(shards)
    ]
    grad_bias_up = jnp.stack([jnp.sum(g.astype(jnp.float32), 0) for g in grad_pre])
    back_normed = sum(times_transposed(grad_pre[j], w_up[j]) for j in range(shards))
    grad_first, grad_gain_first, grad_offset_first = norm_backward(
        grad_second + back_normed, unit_first, inverse_first, gain_first
    )
    grad_bias_out = jnp.sum(grad_first, 0)
    first_low = grad_first.astype(jnp.bfloat16)
    grad_w_out = [
        transposed_times(first_low, attended[:, j * head_width : (j + 1) * head_width])
        for j in range(shards)
    ]
    grad_attended = jnp.concatenate(
        [product(first_low, w_out[j]).astype(jnp.bfloat16) for j in range(shards)], 1
    )
    grad_packed = attention_backward(
        packed, own_segments, log_total, grad_attended, shards, local_heads
    )
    grad_w_qkv = [
        transposed_times(rows_in, grad_packed[:, j * width_qkv : (j + 1) * width_qkv])
        for j in range(shards)
    ]
    column_sums = jnp.sum(grad_packed.astype(jnp.float32), 0).reshape(shards, 3, head_width)
    back_input = sum(
        times_transposed(grad_packed[:, j * width_qkv : (j + 1) * width_qkv], w_qkv[j])
        for j in range(shards)
    )
    input_grad = grad_first + back_input
    grad_w_first = [
        jnp.concatenate([grad_w_qkv[j], grad_w_out[j]], 1).astype(jnp.bfloat16)
        for j in range(shards)
    ]

    if direct:
        down_own = reduce_piece(grad_w_down)
        up_own = reduce_piece(grad_w_up)
        first_own = reduce_piece(grad_w_first)
        slab_grad = jnp.concatenate([first_own, up_own, down_own], 1).astype(jnp.bfloat16)
        tile_grad = tiles_from_slabs(slab_grad[None], shards, block_size).reshape(tile_total, -1)
        slot_grad = transposed_times(placing, tile_grad).astype(jnp.bfloat16)
        slot_grad = lax.all_to_all(
            slot_grad.reshape(PARTS, slots, SUB * block_size), "dp", 0, 0, tiled=True
        )
        owned_grads = slot_grad.swapaxes(0, 1).reshape(slots, block_size, block_size)
    else:
        every = jnp.stack(
            [
                jnp.concatenate([grad_w_first[j], grad_w_up[j], grad_w_down[j]], 1)
                for j in range(shards)
            ]
        ).astype(jnp.float32)
        mine = lax.psum_scatter(every, "tensor", scatter_dimension=0, tiled=True)[0]
        blocks = mine.reshape(PARTS, D // PARTS, -1)
        blocks = jnp.stack([blocks[(p % 2) * 4 + p // 2] for p in range(PARTS)])
        tile_grad = tiles_from_slabs(blocks, shards, block_size)
        slot_grad = tile_grad.reshape(tile_total, block_size, block_size)[owner]
        owned_grads = lax.psum_scatter(slot_grad, "dp", scatter_dimension=0, tiled=True)
    owned_grads = owned_grads.astype(jnp.float32)
    owned_grads = jnp.where(own_flip, jnp.swapaxes(owned_grads, 1, 2), owned_grads)

    d_grads = exact_product_t(
        jnp.stack(
            [
                grad_gain_first,
                grad_gain_second,
                grad_bias_out,
                grad_bias_down,
                grad_offset_first,
                grad_offset_second,
            ]
        ),
        selector,
        3,
    )
    grad_vector = jnp.concatenate(
        [
            d_grads[0],
            d_grads[1],
            column_sums[:, 0][group_order].reshape(-1),
            column_sums[:, 2][group_order].reshape(-1),
            d_grads[2],
            grad_bias_up[group_order].reshape(-1),
            d_grads[3],
            d_grads[4],
            d_grads[5],
        ]
    )
    vector_grad = sum_over_all(grad_vector) if direct else lax.psum(grad_vector, ("dp", "tensor"))

    layer_out = exact_product_t(layer_out, selector, 2)
    input_grad = exact_product_t(input_grad, selector, 2)

    bias_first = 1.0 - DECAY_FIRST**ADAM_STEP
    bias_second = 1.0 - DECAY_SECOND**ADAM_STEP
    left_side = left_basis[0]
    right_side = right_basis[0]
    rotated = precise(jnp.swapaxes(left_side, -1, -2), precise(owned_grads, right_side))
    new_first = DECAY_FIRST * first_moment[0] + (1.0 - DECAY_FIRST) * rotated
    new_second = DECAY_SECOND * second_moment[0] + (1.0 - DECAY_SECOND) * rotated * rotated
    direction = new_first / bias_first / (jnp.sqrt(new_second / bias_second) + ADAM_EPS)
    new_master = master[0] - MATRIX_RATE * precise(
        precise(left_side, direction), jnp.swapaxes(right_side, -1, -2)
    )
    new_vector_first = DECAY_FIRST * vector_first + (1.0 - DECAY_FIRST) * vector_grad
    new_vector_second = (
        DECAY_SECOND * vector_second + (1.0 - DECAY_SECOND) * vector_grad * vector_grad
    )
    new_vectors = vectors - VECTOR_RATE * (new_vector_first / bias_first) / (
        jnp.sqrt(new_vector_second / bias_second) + ADAM_EPS
    )
    return (
        layer_out,
        input_grad,
        new_master[None],
        new_first[None],
        new_second[None],
        new_vectors,
        new_vector_first,
        new_vector_second,
    )


def solution(mesh):
    return jax.shard_map(
        local,
        mesh=mesh,
        in_specs=(
            P(("dp", "tensor"), None),
            P("dp", None),
            P(("dp", "tensor"), None),
            P(),
            P("tensor", "dp", None, None),
            P("tensor", "dp", None, None),
            P("tensor", "dp", None, None),
            P("tensor", "dp", None, None),
            P("tensor", "dp", None, None),
            P(),
            P(),
            P(),
        ),
        out_specs=(
            P(("dp", "tensor"), None),
            P(("dp", "tensor"), None),
            P("tensor", "dp", None, None),
            P("tensor", "dp", None, None),
            P("tensor", "dp", None, None),
            P(),
            P(),
            P(),
        ),
        check_vma=False,
    )
```

```python
import functools
import math

import jax
import jax.numpy as jnp
from jax import lax
from jax.experimental import pallas as pl
from jax.experimental.pallas import tpu as pltpu
from jax.sharding import PartitionSpec as P

HEADS = 12
HEAD_DIM = 64
D = 768
FF = 3072
ADAM_STEP = 3


NORM_EPS = 1e-12
ADAM_EPS = 1e-08
MATRIX_RATE = 0.01
VECTOR_RATE = 0.1
DECAY_FIRST = 0.5
DECAY_SECOND = 0.5
MASKED = -1e30


def product(left_side, right_side):
    return jnp.dot(left_side, right_side, preferred_element_type=jnp.float32)


def times_transposed(left_side, right_side):
    return lax.dot_general(
        left_side, right_side, (((1,), (1,)), ((), ())), preferred_element_type=jnp.float32
    )


def transposed_times(left_side, right_side):
    return lax.dot_general(
        left_side, right_side, (((0,), (0,)), ((), ())), preferred_element_type=jnp.float32
    )


def precise(left_side, right_side):
    return jnp.matmul(left_side, right_side, precision=lax.Precision.HIGHEST)
VMEM_LIMIT = 60 * 1024 * 1024

PARTS = 8
SUB = 12


def rounded(values):
    return lax.reduce_precision(values, 8, 7)


def split_terms(values, count):
    terms = []
    for _ in range(count):
        top = rounded(values)
        terms.append(top.astype(jnp.bfloat16))
        values = values - top
    return terms


def exact_product(values, selector, count):
    return sum(product(term, selector) for term in split_terms(values, count))


def exact_product_t(values, selector, count):
    return sum(times_transposed(term, selector) for term in split_terms(values, count))


def part_of_block(block):
    return (block % 4) * 2 + block // 4


def feature_order(rank):
    place = lax.iota(jnp.int32, D)
    part = part_of_block(place // (D // PARTS)) ^ rank
    inner = place % (D // PARTS)
    return (inner // SUB) * (PARTS * SUB) + part * SUB + inner % SUB


def tile_counts(shards, block_size):
    rows = D // block_size
    qkv = rows * (3 * D // shards // block_size)
    out = rows * (D // shards // block_size)
    up = rows * (FF // shards // block_size)
    return (qkv, out, up)


def slabs_from_tiles(tiles, shards, block_size):
    cut = tiles.shape[1]
    qkv, out, up = tile_counts(shards, block_size)
    rows = D // block_size

    def by_rows(part):
        cols = part.shape[0] // rows
        part = part.reshape(rows, cols, cut, SUB, block_size)
        return part.transpose(2, 0, 3, 1, 4).reshape(cut, rows * SUB, cols * block_size)

    def by_cols(part):
        cols = part.shape[0] // rows
        part = part.reshape(cols, rows, cut, SUB, block_size)
        return part.transpose(2, 1, 3, 0, 4).reshape(cut, rows * SUB, cols * block_size)

    return jnp.concatenate(
        [
            by_rows(tiles[:qkv]),
            by_cols(tiles[qkv : qkv + out]),
            by_rows(tiles[qkv + out : qkv + out + up]),
            by_cols(tiles[qkv + out + up :]),
        ],
        2,
    )


def tiles_from_slabs(slabs, shards, block_size):
    cut = slabs.shape[0]
    rows = D // block_size
    width_qkv, width_out, width_up = 3 * D // shards, D // shards, FF // shards

    def by_rows(part):
        cols = part.shape[2] // block_size
        part = part.reshape(cut, rows, SUB, cols, block_size)
        return part.transpose(1, 3, 0, 2, 4).reshape(rows * cols, cut, SUB, block_size)

    def by_cols(part):
        cols = part.shape[2] // block_size
        part = part.reshape(cut, rows, SUB, cols, block_size)
        return part.transpose(3, 1, 0, 2, 4).reshape(rows * cols, cut, SUB, block_size)

    first = width_qkv + width_out
    second = first + width_up
    return jnp.concatenate(
        [
            by_rows(slabs[:, :, :width_qkv]),
            by_cols(slabs[:, :, width_qkv:first]),
            by_rows(slabs[:, :, first:second]),
            by_cols(slabs[:, :, second:]),
        ],
        0,
    )


def swap_over(values, over_dp, over_tensor):
    dp, tensor = lax.axis_size("dp"), lax.axis_size("tensor")
    pairs = [
        (a * tensor + b, (a ^ over_dp) * tensor + (b ^ over_tensor))
        for a in range(dp)
        for b in range(tensor)
    ]
    return lax.ppermute(values, ("dp", "tensor"), pairs)


def gather_piece(slab):
    along_z = jnp.concatenate([slab] + [swap_over(slab, 2 * k, 0) for k in (1, 2, 3)], 0)
    here = {(0, 0): along_z}
    for y, x in ((0, 1), (1, 0), (1, 1)):
        here[y, x] = swap_over(along_z, x, 2 * y)
    there = {key: swap_over(block, 0, 1) for key, block in here.items()}
    return [
        jnp.concatenate([source[y, 0], source[y, 1]], 0)
        for y in (0, 1)
        for source in (here, there)
    ]


def reduce_piece(parts):
    def total(*terms):
        return sum(term.astype(jnp.float32) for term in terms)

    low = [
        total(parts[2 * y], swap_over(parts[2 * y + 1], 0, 1)).astype(jnp.bfloat16) for y in (0, 1)
    ]
    half = low[0].shape[0] // 2
    plane = total(
        low[0][:half],
        swap_over(low[0][half:], 1, 0),
        swap_over(low[1][:half], 0, 2),
        swap_over(low[1][half:], 1, 2),
    ).astype(jnp.bfloat16)
    rows = half // 4
    return total(
        plane[:rows],
        *[swap_over(plane[k * rows : (k + 1) * rows], 2 * k, 0) for k in (1, 2, 3)],
    )


def sum_over_all(values):
    for over_dp, over_tensor in ((0, 1), (0, 2), (1, 0), (2, 0), (4, 0)):
        values = values + swap_over(values, over_dp, over_tensor)
    return values


ROWS = 256


def dot_nt(left_side, right_side):
    return lax.dot_general(
        left_side, right_side, (((1,), (1,)), ((), ())), preferred_element_type=jnp.float32
    )


def whole_block(array):
    rank = array.ndim
    return pl.BlockSpec(array.shape, lambda i: (0,) * rank)


def row_block(array):
    return pl.BlockSpec((ROWS, array.shape[1]), lambda i: (i, 0))


def call_rows(kernel, steps, inputs, outputs, flops, transcendentals=0):
    arrays = [array for array, _ in inputs]
    shapes = [jax.ShapeDtypeStruct(shape, dtype) for shape, dtype, _ in outputs]
    moved = sum(a.size * a.dtype.itemsize for a in arrays + shapes)
    return pl.pallas_call(
        kernel,
        grid=(steps,),
        in_specs=[spec for _, spec in inputs],
        out_specs=[spec for _, _, spec in outputs],
        out_shape=shapes,
        compiler_params=pltpu.CompilerParams(vmem_limit_bytes=VMEM_LIMIT),
        cost_estimate=pl.CostEstimate(
            flops=flops, bytes_accessed=moved, transcendentals=transcendentals
        ),
    )(*arrays)


def norm_rows(summed):
    centred = summed - jnp.mean(summed, -1, keepdims=True)
    inverse = lax.rsqrt(jnp.mean(centred * centred, -1, keepdims=True) + NORM_EPS)
    return centred * inverse, inverse


def norm_pull(gradient, unit_rows, inverse, gain_row):
    scaled = gradient * gain_row
    return inverse * (
        scaled
        - jnp.mean(scaled, -1, keepdims=True)
        - unit_rows * jnp.mean(scaled * unit_rows, -1, keepdims=True)
    )


def add_rows(ref, rows):
    sums = [jnp.sum(row, 0, keepdims=True) for row in rows]
    start = pl.program_id(0) == 0
    for place, total in enumerate(sums):
        kept = jnp.where(start, 0.0, ref[place : place + 1, :])
        ref[place : place + 1, :] = kept + total


def attention_kernel(shards, local_heads, length, *refs):
    rows_ref, across_ref, down_ref, bias_ref, vec_ref = refs[:5]
    weights = refs[5 : 5 + shards]
    packed_ref, probs_ref, attended_ref, unit_ref, inverse_ref, low_ref = refs[5 + shards :]
    head_width = local_heads * HEAD_DIM
    width = 3 * head_width
    rows = rows_ref[...]
    for j in range(shards):
        packed_ref[j] = (product(rows, weights[j][:, :width]) + bias_ref[j : j + 1, :]).astype(
            jnp.bfloat16
        )
    for p in range(ROWS // length):
        allowed = down_ref[p] == across_ref[p]
        span = slice(p * length, (p + 1) * length)
        for j in range(shards):
            for h in range(local_heads):
                at = h * HEAD_DIM
                queries = packed_ref[j, span, at : at + HEAD_DIM]
                keys = packed_ref[j, span, head_width + at : head_width + at + HEAD_DIM]
                values = packed_ref[j, span, 2 * head_width + at : 2 * head_width + at + HEAD_DIM]
                scores = dot_nt(queries, keys) * HEAD_DIM ** (-0.5)
                scores = jnp.where(allowed, scores, MASKED)
                raised = jnp.exp(scores - jnp.max(scores, -1, keepdims=True))
                probs = raised * (1.0 / jnp.sum(raised, -1, keepdims=True))
                probs = probs.astype(jnp.bfloat16)
                probs_ref[p, j * local_heads + h] = probs
                start = j * head_width + at
                attended_ref[span, start : start + HEAD_DIM] = product(probs, values).astype(
                    jnp.bfloat16
                )
    summed = rows.astype(jnp.float32) + vec_ref[0:1, :]
    for j in range(shards):
        summed = summed + dot_nt(
            attended_ref[:, j * head_width : (j + 1) * head_width], weights[j][:, width:]
        )
    unit, inverse = norm_rows(summed)
    unit_ref[...] = unit
    inverse_ref[...] = inverse
    low_ref[...] = (unit * vec_ref[1:2, :] + vec_ref[2:3, :]).astype(jnp.bfloat16)


def normal_cdf(values):
    decay = jnp.exp(values * values * -0.5)
    t = 1.0 / (1.0 + jnp.abs(values) * (0.3275911 * 0.5**0.5))
    poly = t * (
        0.127414796
        + t * (-0.142248368 + t * (0.7107068705 + t * (-0.7265760135 + t * 0.5307027145)))
    )
    upper = poly * decay
    return jnp.where(values > 0, 1.0 - upper, upper), decay


def up_kernel(shards, *refs):
    low_ref, bias_ref = refs[:2]
    weights = refs[2 : 2 + shards]
    act_ref, slope_ref = refs[2 + shards :]
    width = weights[0].shape[1]
    chunk = 256
    low = low_ref[...]
    for j in range(shards):
        for c in range(0, width, chunk):
            pre = product(low, weights[j][:, c : c + chunk]) + bias_ref[j : j + 1, c : c + chunk]
            below, decay = normal_cdf(pre)
            at = j * width + c
            act_ref[:, at : at + chunk] = (pre * below).astype(jnp.bfloat16)
            slope_ref[:, at : at + chunk] = (
                below + pre * decay * (0.5 / math.pi) ** 0.5
            ).astype(jnp.bfloat16)


def down_kernel(shards, *refs):
    act_ref, unit_ref, grad_ref, vec_ref = refs[:4]
    weights = refs[4 : 4 + shards]
    out_ref, dz_ref, low_ref, sums_ref = refs[4 + shards :]
    width = weights[0].shape[1]
    summed = unit_ref[...] * vec_ref[1:2, :] + vec_ref[2:3, :] + vec_ref[3:4, :]
    for j in range(shards):
        summed = summed + dot_nt(act_ref[:, j * width : (j + 1) * width], weights[j][...])
    unit, inverse = norm_rows(summed)
    gain = vec_ref[4:5, :]
    out_ref[...] = unit * gain + vec_ref[5:6, :]
    gradient = grad_ref[...]
    dz = norm_pull(gradient, unit, inverse, gain)
    dz_ref[...] = dz
    low_ref[...] = dz.astype(jnp.bfloat16)
    add_rows(sums_ref, (gradient * unit, gradient, dz))


def back_kernel(shards, *refs):
    low_ref, dz_ref, slope_ref, unit_ref, inverse_ref, vec_ref = refs[:6]
    downs = refs[6 : 6 + shards]
    ups = refs[6 + shards : 6 + 2 * shards]
    firsts = refs[6 + 2 * shards : 6 + 3 * shards]
    dpre_ref, dz1_ref, low1_ref, datt_ref, sums_ref, bias_sums_ref = refs[6 + 3 * shards :]
    width = downs[0].shape[1]
    low = low_ref[...]
    gradient = dz_ref[...]
    for j in range(shards):
        span = slice(j * width, (j + 1) * width)
        dpre = (product(low, downs[j][...]) * slope_ref[:, span].astype(jnp.float32)).astype(
            jnp.bfloat16
        )
        dpre_ref[:, span] = dpre
        total = jnp.sum(dpre.astype(jnp.float32), 0, keepdims=True)
        kept = jnp.where(pl.program_id(0) == 0, 0.0, bias_sums_ref[j : j + 1, :])
        bias_sums_ref[j : j + 1, :] = kept + total
        gradient = gradient + dot_nt(dpre, ups[j][...])
    unit = unit_ref[...]
    dz1 = norm_pull(gradient, unit, inverse_ref[...], vec_ref[1:2, :])
    dz1_ref[...] = dz1
    low1 = dz1.astype(jnp.bfloat16)
    low1_ref[...] = low1
    add_rows(sums_ref, (gradient * unit, gradient, dz1))
    head_width = D // shards
    for j in range(shards):
        datt_ref[:, j * head_width : (j + 1) * head_width] = product(
            low1, firsts[j][:, 3 * head_width :]
        ).astype(jnp.bfloat16)


def attention_back_kernel(shards, local_heads, length, *refs):
    datt_ref, packed_ref, probs_ref, dpacked_ref, sums_ref = refs
    head_width = local_heads * HEAD_DIM
    factor = HEAD_DIM ** (-0.5)
    for p in range(ROWS // length):
        span = slice(p * length, (p + 1) * length)
        for j in range(shards):
            for h in range(local_heads):
                at = h * HEAD_DIM
                key_at, value_at = head_width + at, 2 * head_width + at
                queries = packed_ref[j, span, at : at + HEAD_DIM]
                keys = packed_ref[j, span, key_at : key_at + HEAD_DIM]
                values = packed_ref[j, span, value_at : value_at + HEAD_DIM]
                start = j * head_width + at
                upstream = datt_ref[span, start : start + HEAD_DIM]
                probs = probs_ref[p, j * local_heads + h]
                full = probs.astype(jnp.float32)
                grad_probs = dot_nt(upstream, values)
                centre = jnp.sum(grad_probs * full, -1, keepdims=True)
                grad_scores = (full * (grad_probs - centre)).astype(jnp.bfloat16)
                for place, grad in (
                    (at, product(grad_scores, keys) * factor),
                    (key_at, transposed_times(grad_scores, queries) * factor),
                    (value_at, transposed_times(probs, upstream)),
                ):
                    dpacked_ref[j, span, place : place + HEAD_DIM] = grad.astype(jnp.bfloat16)
    for j in range(shards):
        total = jnp.sum(dpacked_ref[j].astype(jnp.float32), 0, keepdims=True)
        kept = jnp.where(pl.program_id(0) == 0, 0.0, sums_ref[j : j + 1, :])
        sums_ref[j : j + 1, :] = kept + total


def natural_kernel(shards, *refs):
    out_ref, dz1_ref, dpacked_ref, selector_ref = refs[:4]
    weights = refs[4 : 4 + shards]
    layer_ref, input_ref = refs[4 + shards :]
    width = dpacked_ref.shape[2]
    gradient = dz1_ref[...]
    for j in range(shards):
        gradient = gradient + dot_nt(dpacked_ref[j], weights[j][:, :width])
    for source, ref in ((out_ref[...], layer_ref), (gradient, input_ref)):
        top = source.astype(jnp.bfloat16)
        rest = (source - top.astype(jnp.float32)).astype(jnp.bfloat16)
        ref[...] = dot_nt(top, selector_ref[...]) + dot_nt(rest, selector_ref[...])


def after(values, *others):
    return lax.optimization_barrier((values, *others))[0]


def local(
    tokens,
    segments,
    out_grad,
    owner,
    master,
    left_basis,
    right_basis,
    first_moment,
    second_moment,
    vectors,
    vector_first,
    vector_second,
):
    shards = lax.axis_size("tensor")
    dp_size = lax.axis_size("dp")
    direct = dp_size == PARTS and shards == 4
    tensor_rank = lax.axis_index("tensor")
    dp_rank = lax.axis_index("dp")
    local_heads = HEADS // shards
    head_width = local_heads * HEAD_DIM
    up_width = FF // shards
    width_qkv = 3 * head_width
    block_size = master.shape[-1]
    slots = master.shape[1]
    row_count = tokens.shape[0]
    length = segments.shape[1]
    pack_count = row_count // length
    own_segments = lax.dynamic_slice_in_dim(segments, tensor_rank * pack_count, pack_count, 0)
    qkv_tiles, out_tiles, up_tiles = tile_counts(shards, block_size)
    tile_total = owner.shape[0]

    group_base = tensor_rank if direct else 0
    order = feature_order(dp_rank if direct else 0)
    selector = (lax.iota(jnp.int32, D)[:, None] == order[None, :]).astype(jnp.bfloat16)

    def flipped(index):
        from_out = (index >= qkv_tiles) & (index < qkv_tiles + out_tiles)
        return (from_out | (index >= qkv_tiles + out_tiles + up_tiles))[:, None, None]

    own_tiles = lax.dynamic_slice_in_dim(owner, dp_rank * slots, slots, 0)
    own_flip = flipped(own_tiles)
    sent = master[0].astype(jnp.bfloat16)
    sent = jnp.where(own_flip, jnp.swapaxes(sent, 1, 2), sent)
    placing = (lax.iota(jnp.int32, tile_total)[:, None] == owner[None, :]).astype(jnp.bfloat16)
    if direct:
        parts = sent.reshape(slots, PARTS, SUB * block_size).swapaxes(0, 1)
        parts = lax.all_to_all(parts, "dp", 0, 0, tiled=True).reshape(tile_total, -1)
        tiles = product(placing, parts).astype(jnp.bfloat16)
        slab = slabs_from_tiles(tiles.reshape(tile_total, 1, SUB, block_size), shards, block_size)[0]
        pieces = [gather_piece(slab[:, k * D : (k + 1) * D]) for k in range(3)]
    else:
        gathered = lax.all_gather(sent, "dp", axis=0, tiled=True).reshape(tile_total, -1)
        tiles = product(placing, gathered).astype(jnp.bfloat16)
        slabs = slabs_from_tiles(
            tiles.reshape(tile_total, PARTS, SUB, block_size), shards, block_size
        )
        whole = jnp.concatenate([slabs[part_of_block(k)] for k in range(PARTS)], 0)
        every = lax.all_gather(whole, "tensor", axis=0)
        pieces = [
            [every[j][:, k * D : (k + 1) * D] for j in range(shards)] for k in range(3)
        ]

    group_order = lax.iota(jnp.int32, shards) ^ group_base
    d_vectors = jnp.stack(
        [
            vectors[0:D],
            vectors[D : 2 * D],
            vectors[4 * D : 5 * D],
            vectors[5 * D + FF : 6 * D + FF],
            vectors[6 * D + FF : 7 * D + FF],
            vectors[7 * D + FF : 8 * D + FF],
        ]
    )
    gain_first, gain_second, bias_out, bias_down, offset_first, offset_second = exact_product(
        d_vectors, selector, 3
    )
    bias_q = vectors[2 * D : 3 * D].reshape(shards, head_width)[group_order]
    bias_v = vectors[3 * D : 4 * D].reshape(shards, head_width)[group_order]
    bias_up = vectors[5 * D : 5 * D + FF].reshape(shards, up_width)[group_order]

    rows_in = product(tokens, selector).astype(jnp.bfloat16)
    grad_out = exact_product(out_grad, selector, 2)

    steps = row_count // ROWS
    packs_step = ROWS // length
    d_rows = jnp.stack(
        [bias_out, gain_first, offset_first, bias_down, gain_second, offset_second]
        + [jnp.zeros_like(bias_out)] * 2
    )
    bias_qkv = jnp.concatenate([bias_q, jnp.zeros_like(bias_q), bias_v], 1)
    rows_spec = lambda width: pl.BlockSpec((ROWS, width), lambda i: (i, 0))
    group_spec = lambda width: pl.BlockSpec((shards, ROWS, width), lambda i: (0, i, 0))
    probs_spec = pl.BlockSpec((packs_step, HEADS, length, length), lambda i: (i, 0, 0, 0))
    sums_spec = lambda width: pl.BlockSpec((8, width), lambda i: (0, 0))
    f32, bf16 = jnp.float32, jnp.bfloat16
    full = lambda array: (array, whole_block(array))
    by_rows = lambda array: (array, row_block(array))
    square = 2 * row_count * D * D

    packed, probs, attended, unit_first, inverse_first, normed_low = call_rows(
        functools.partial(attention_kernel, shards, local_heads, length),
        steps,
        [
            by_rows(rows_in),
            (own_segments[:, None, :], pl.BlockSpec((packs_step, 1, length), lambda i: (i, 0, 0))),
            (own_segments[:, :, None], pl.BlockSpec((packs_step, length, 1), lambda i: (i, 0, 0))),
            full(bias_qkv),
            full(d_rows),
            *[full(w) for w in pieces[0]],
        ],
        [
            ((shards, row_count, width_qkv), bf16, group_spec(width_qkv)),
            ((pack_count, HEADS, length, length), bf16, probs_spec),
            ((row_count, D), bf16, rows_spec(D)),
            ((row_count, D), f32, rows_spec(D)),
            ((row_count, 1), f32, rows_spec(1)),
            ((row_count, D), bf16, rows_spec(D)),
        ],
        4 * square + 4 * row_count * length * D,
        row_count * length * HEADS,
    )
    activated, slope = call_rows(
        functools.partial(up_kernel, shards),
        steps,
        [by_rows(normed_low), full(bias_up), *[full(w) for w in pieces[1]]],
        [((row_count, FF), bf16, rows_spec(FF)), ((row_count, FF), bf16, rows_spec(FF))],
        4 * square,
        2 * row_count * FF,
    )
    layer_out, grad_second, second_low, sums_second = call_rows(
        functools.partial(down_kernel, shards),
        steps,
        [
            by_rows(activated),
            by_rows(unit_first),
            by_rows(grad_out),
            full(d_rows),
            *[full(w) for w in pieces[2]],
        ],
        [
            ((row_count, D), f32, rows_spec(D)),
            ((row_count, D), f32, rows_spec(D)),
            ((row_count, D), bf16, rows_spec(D)),
            ((8, D), f32, sums_spec(D)),
        ],
        4 * square,
    )
    grad_gain_second, grad_offset_second, grad_bias_down = (sums_second[k] for k in range(3))
    grad_w_down = [
        transposed_times(second_low, activated[:, j * up_width : (j + 1) * up_width]).astype(bf16)
        for j in range(shards)
    ]
    if direct:
        second_low = after(second_low, *grad_w_down)
    grad_pre, grad_first, first_low, grad_attended, sums_first, grad_bias_up = call_rows(
        functools.partial(back_kernel, shards),
        steps,
        [
            by_rows(second_low),
            by_rows(grad_second),
            by_rows(slope),
            by_rows(unit_first),
            by_rows(inverse_first),
            full(d_rows),
            *[full(w) for k in (2, 1, 0) for w in pieces[k]],
        ],
        [
            ((row_count, FF), bf16, rows_spec(FF)),
            ((row_count, D), f32, rows_spec(D)),
            ((row_count, D), bf16, rows_spec(D)),
            ((row_count, D), bf16, rows_spec(D)),
            ((8, D), f32, sums_spec(D)),
            ((8, up_width), f32, sums_spec(up_width)),
        ],
        9 * square,
    )
    grad_bias_up = grad_bias_up[:shards]
    grad_gain_first, grad_offset_first, grad_bias_out = (sums_first[k] for k in range(3))
    grad_w_up = [
        transposed_times(normed_low, grad_pre[:, j * up_width : (j + 1) * up_width]).astype(bf16)
        for j in range(shards)
    ]
    grad_w_out = [
        transposed_times(first_low, attended[:, j * head_width : (j + 1) * head_width])
        for j in range(shards)
    ]
    grad_packed, column_sums = call_rows(
        functools.partial(attention_back_kernel, shards, local_heads, length),
        steps,
        [
            by_rows(grad_attended),
            (packed, group_spec(width_qkv)),
            (probs, probs_spec),
        ],
        [
            ((shards, row_count, width_qkv), bf16, group_spec(width_qkv)),
            ((8, width_qkv), f32, sums_spec(width_qkv)),
        ],
        10 * row_count * length * D,
    )
    column_sums = column_sums[:shards].reshape(shards, 3, head_width)
    grad_w_first = [
        jnp.concatenate([transposed_times(rows_in, grad_packed[j]), grad_w_out[j]], 1).astype(bf16)
        for j in range(shards)
    ]
    layer_out, input_grad = call_rows(
        functools.partial(natural_kernel, shards),
        steps,
        [
            by_rows(layer_out),
            by_rows(grad_first),
            (grad_packed, group_spec(width_qkv)),
            full(selector),
            *[full(w) for w in pieces[0]],
        ],
        [((row_count, D), f32, rows_spec(D)), ((row_count, D), f32, rows_spec(D))],
        7 * square,
    )

    if direct:
        down_own = reduce_piece(grad_w_down)
        up_own = reduce_piece(grad_w_up)
        first_own = reduce_piece(grad_w_first)
        slab_grad = jnp.concatenate([first_own, up_own, down_own], 1).astype(jnp.bfloat16)
        tile_grad = tiles_from_slabs(slab_grad[None], shards, block_size).reshape(tile_total, -1)
        slot_grad = transposed_times(placing, tile_grad).astype(jnp.bfloat16)
        slot_grad = lax.all_to_all(
            slot_grad.reshape(PARTS, slots, SUB * block_size), "dp", 0, 0, tiled=True
        )
        owned_grads = slot_grad.swapaxes(0, 1).reshape(slots, block_size, block_size)
    else:
        every = jnp.stack(
            [
                jnp.concatenate([grad_w_first[j], grad_w_up[j], grad_w_down[j]], 1)
                for j in range(shards)
            ]
        ).astype(jnp.float32)
        mine = lax.psum_scatter(every, "tensor", scatter_dimension=0, tiled=True)[0]
        blocks = mine.reshape(PARTS, D // PARTS, -1)
        blocks = jnp.stack([blocks[(p % 2) * 4 + p // 2] for p in range(PARTS)])
        tile_grad = tiles_from_slabs(blocks, shards, block_size)
        slot_grad = tile_grad.reshape(tile_total, block_size, block_size)[owner]
        owned_grads = lax.psum_scatter(slot_grad, "dp", scatter_dimension=0, tiled=True)
    owned_grads = owned_grads.astype(jnp.float32)
    owned_grads = jnp.where(own_flip, jnp.swapaxes(owned_grads, 1, 2), owned_grads)

    d_grads = exact_product_t(
        jnp.stack(
            [
                grad_gain_first,
                grad_gain_second,
                grad_bias_out,
                grad_bias_down,
                grad_offset_first,
                grad_offset_second,
            ]
        ),
        selector,
        3,
    )
    grad_vector = jnp.concatenate(
        [
            d_grads[0],
            d_grads[1],
            column_sums[:, 0][group_order].reshape(-1),
            column_sums[:, 2][group_order].reshape(-1),
            d_grads[2],
            grad_bias_up[group_order].reshape(-1),
            d_grads[3],
            d_grads[4],
            d_grads[5],
        ]
    )
    vector_grad = sum_over_all(grad_vector) if direct else lax.psum(grad_vector, ("dp", "tensor"))


    bias_first = 1.0 - DECAY_FIRST**ADAM_STEP
    bias_second = 1.0 - DECAY_SECOND**ADAM_STEP
    left_side = left_basis[0]
    right_side = right_basis[0]
    rotated = precise(jnp.swapaxes(left_side, -1, -2), precise(owned_grads, right_side))
    new_first = DECAY_FIRST * first_moment[0] + (1.0 - DECAY_FIRST) * rotated
    new_second = DECAY_SECOND * second_moment[0] + (1.0 - DECAY_SECOND) * rotated * rotated
    direction = new_first / bias_first / (jnp.sqrt(new_second / bias_second) + ADAM_EPS)
    new_master = master[0] - MATRIX_RATE * precise(
        precise(left_side, direction), jnp.swapaxes(right_side, -1, -2)
    )
    new_vector_first = DECAY_FIRST * vector_first + (1.0 - DECAY_FIRST) * vector_grad
    new_vector_second = (
        DECAY_SECOND * vector_second + (1.0 - DECAY_SECOND) * vector_grad * vector_grad
    )
    new_vectors = vectors - VECTOR_RATE * (new_vector_first / bias_first) / (
        jnp.sqrt(new_vector_second / bias_second) + ADAM_EPS
    )
    return (
        layer_out,
        input_grad,
        new_master[None],
        new_first[None],
        new_second[None],
        new_vectors,
        new_vector_first,
        new_vector_second,
    )


def solution(mesh):
    return jax.shard_map(
        local,
        mesh=mesh,
        in_specs=(
            P(("dp", "tensor"), None),
            P("dp", None),
            P(("dp", "tensor"), None),
            P(),
            P("tensor", "dp", None, None),
            P("tensor", "dp", None, None),
            P("tensor", "dp", None, None),
            P("tensor", "dp", None, None),
            P("tensor", "dp", None, None),
            P(),
            P(),
            P(),
        ),
        out_specs=(
            P(("dp", "tensor"), None),
            P(("dp", "tensor"), None),
            P("tensor", "dp", None, None),
            P("tensor", "dp", None, None),
            P("tensor", "dp", None, None),
            P(),
            P(),
            P(),
        ),
        check_vma=False,
    )
```

```python
import functools
import math

import jax
import jax.numpy as jnp
from jax import lax
from jax.experimental import pallas as pl
from jax.experimental.pallas import tpu as pltpu
from jax.sharding import PartitionSpec as P

HEADS = 12
HEAD_DIM = 64
D = 768
FF = 3072
ADAM_STEP = 3


NORM_EPS = 1e-12
ADAM_EPS = 1e-08
MATRIX_RATE = 0.01
VECTOR_RATE = 0.1
DECAY_FIRST = 0.5
DECAY_SECOND = 0.5
MASKED = -1e30


def product(left_side, right_side):
    return jnp.dot(left_side, right_side, preferred_element_type=jnp.float32)


def times_transposed(left_side, right_side):
    return lax.dot_general(
        left_side, right_side, (((1,), (1,)), ((), ())), preferred_element_type=jnp.float32
    )


def transposed_times(left_side, right_side):
    return lax.dot_general(
        left_side, right_side, (((0,), (0,)), ((), ())), preferred_element_type=jnp.float32
    )


def precise(left_side, right_side):
    return jnp.matmul(left_side, right_side, precision=lax.Precision.HIGHEST)
VMEM_LIMIT = 60 * 1024 * 1024

PARTS = 8
SUB = 12


def rounded(values):
    return lax.reduce_precision(values, 8, 7)


def split_terms(values, count):
    terms = []
    for _ in range(count):
        top = rounded(values)
        terms.append(top.astype(jnp.bfloat16))
        values = values - top
    return terms


def exact_product(values, selector, count):
    return sum(product(term, selector) for term in split_terms(values, count))


def exact_product_t(values, selector, count):
    return sum(times_transposed(term, selector) for term in split_terms(values, count))


def part_of_block(block):
    return (block % 4) * 2 + block // 4


def feature_order(rank):
    place = lax.iota(jnp.int32, D)
    part = part_of_block(place // (D // PARTS)) ^ rank
    inner = place % (D // PARTS)
    return (inner // SUB) * (PARTS * SUB) + part * SUB + inner % SUB


def tile_counts(shards, block_size):
    rows = D // block_size
    qkv = rows * (3 * D // shards // block_size)
    out = rows * (D // shards // block_size)
    up = rows * (FF // shards // block_size)
    return (qkv, out, up)


def slabs_from_tiles(tiles, shards, block_size):
    cut = tiles.shape[1]
    qkv, out, up = tile_counts(shards, block_size)
    rows = D // block_size

    def by_rows(part):
        cols = part.shape[0] // rows
        part = part.reshape(rows, cols, cut, SUB, block_size)
        return part.transpose(2, 0, 3, 1, 4).reshape(cut, rows * SUB, cols * block_size)

    def by_cols(part):
        cols = part.shape[0] // rows
        part = part.reshape(cols, rows, cut, SUB, block_size)
        return part.transpose(2, 1, 3, 0, 4).reshape(cut, rows * SUB, cols * block_size)

    return jnp.concatenate(
        [
            by_rows(tiles[:qkv]),
            by_cols(tiles[qkv : qkv + out]),
            by_rows(tiles[qkv + out : qkv + out + up]),
            by_cols(tiles[qkv + out + up :]),
        ],
        2,
    )


def tiles_from_slabs(slabs, shards, block_size):
    cut = slabs.shape[0]
    rows = D // block_size
    width_qkv, width_out, width_up = 3 * D // shards, D // shards, FF // shards

    def by_rows(part):
        cols = part.shape[2] // block_size
        part = part.reshape(cut, rows, SUB, cols, block_size)
        return part.transpose(1, 3, 0, 2, 4).reshape(rows * cols, cut, SUB, block_size)

    def by_cols(part):
        cols = part.shape[2] // block_size
        part = part.reshape(cut, rows, SUB, cols, block_size)
        return part.transpose(3, 1, 0, 2, 4).reshape(rows * cols, cut, SUB, block_size)

    first = width_qkv + width_out
    second = first + width_up
    return jnp.concatenate(
        [
            by_rows(slabs[:, :, :width_qkv]),
            by_cols(slabs[:, :, width_qkv:first]),
            by_rows(slabs[:, :, first:second]),
            by_cols(slabs[:, :, second:]),
        ],
        0,
    )


def swap_over(values, over_dp, over_tensor):
    dp, tensor = lax.axis_size("dp"), lax.axis_size("tensor")
    pairs = [
        (a * tensor + b, (a ^ over_dp) * tensor + (b ^ over_tensor))
        for a in range(dp)
        for b in range(tensor)
    ]
    return lax.ppermute(values, ("dp", "tensor"), pairs)


def over_z(block):
    return jnp.concatenate([block] + [swap_over(block, 2 * k, 0) for k in (1, 2, 3)], 0)


def over_core(blocks):
    return blocks + [swap_over(block, 0, 1) for block in blocks]


def place_first(refs, out_ref):
    count = len(refs) // 2
    half, cols = D // 2, D // 2
    for core in range(2):
        near, beside, right, across = refs[core * count : (core + 1) * count]
        for y in range(2):
            group = 2 * y + core
            out_ref[group, :half, :cols] = near[y * half : (y + 1) * half, :]
            out_ref[group, half:, :cols] = beside[y * half : (y + 1) * half, :]
            out_ref[group, :, cols:] = (right, across)[y][...]


def place_edges(refs, out_ref):
    count = len(refs) // 2
    rows, half, cols = D // PARTS, D // 2, D // 2
    for core in range(2):
        near, beside, across = refs[core * count : (core + 1) * count]
        for y in range(2):
            for z in range(4):
                for x in range(2):
                    to = x * half + z * rows
                    by_y, by_x = (2 * z + y) * rows, (2 * z + x) * rows
                    left = beside[by_y : by_y + rows, :] if x else near[by_y : by_y + rows, :cols]
                    right = across[by_x : by_x + rows, :] if y else near[by_x : by_x + rows, cols:]
                    out_ref[2 * y + core, to : to + rows, :cols] = left
                    out_ref[2 * y + core, to : to + rows, cols:] = right


def place_plane(refs, out_ref):
    half = D // 2
    for core in range(2):
        for y in range(2):
            for x in range(2):
                out_ref[2 * y + core, x * half : (x + 1) * half, :] = refs[4 * core + 2 * y + x][...]


def place_groups(refs, out_ref):
    for group, ref in enumerate(refs):
        out_ref[group] = ref[...]


def total(*terms):
    return sum(term.astype(jnp.float32) for term in terms)


def reduce_core(halves):
    odd, even = halves
    both = total(even, swap_over(odd, 0, 1)).astype(jnp.bfloat16)
    return both[0], both[1]


def reduce_plane(low):
    half = low[0].shape[0] // 2
    return total(
        low[0][:half],
        swap_over(low[0][half:], 1, 0),
        swap_over(low[1][:half], 0, 2),
        swap_over(low[1][half:], 1, 2),
    ).astype(jnp.bfloat16)


def reduce_z(plane):
    rows = plane.shape[0] // 4
    return total(
        plane[:rows],
        *[swap_over(plane[k * rows : (k + 1) * rows], 2 * k, 0) for k in (1, 2, 3)],
    )


def reduce_edges(low):
    half, cols = low[0].shape[0] // 2, low[0].shape[1] // 2
    near = jnp.concatenate([low[0][:half, :cols], low[1][:half, :cols]], 0)
    far = jnp.concatenate([low[0][half:, :cols], low[1][half:, :cols]], 0)
    left = total(near, swap_over(far, 1, 0))
    right = total(low[0][:, cols:], swap_over(low[1][:, cols:], 0, 2))
    return jnp.concatenate([left, right], 1).astype(jnp.bfloat16)


def reduce_edges_plane(edges):
    rows, cols = edges.shape[0] // 2, edges.shape[1] // 2
    left = total(edges[:rows, :cols], swap_over(edges[rows:, :cols], 0, 2))
    right = total(edges[:rows, cols:], swap_over(edges[rows:, cols:], 1, 0))
    return jnp.concatenate([left, right], 1)


def reduce_edges_z(edges):
    rows = edges.shape[0] // 8
    sent = [
        jnp.concatenate([edges[k * rows : (k + 1) * rows], edges[(4 + k) * rows : (5 + k) * rows]], 0)
        for k in range(4)
    ]
    return total(sent[0], *[swap_over(sent[k], 2 * k, 0) for k in (1, 2, 3)]).astype(jnp.bfloat16)


def sum_over_all(values):
    for over_dp, over_tensor in ((0, 1), (0, 2), (1, 0), (2, 0), (4, 0)):
        values = values + swap_over(values, over_dp, over_tensor)
    return values


ROWS = 256


def dot_nt(left_side, right_side):
    return lax.dot_general(
        left_side, right_side, (((1,), (1,)), ((), ())), preferred_element_type=jnp.float32
    )


def whole_block(array):
    rank = array.ndim
    return pl.BlockSpec(array.shape, lambda i: (0,) * rank)


def row_block(array):
    return pl.BlockSpec((ROWS, array.shape[1]), lambda i: (i, 0))


def call_rows(kernel, steps, inputs, outputs, flops, transcendentals=0, scratch=()):
    arrays = [array for array, _ in inputs]
    shapes = [jax.ShapeDtypeStruct(shape, dtype) for shape, dtype, _ in outputs]
    moved = sum(a.size * a.dtype.itemsize for a in arrays + shapes)
    return pl.pallas_call(
        kernel,
        grid=(steps,),
        in_specs=[spec for _, spec in inputs],
        out_specs=[spec for _, _, spec in outputs],
        out_shape=shapes,
        scratch_shapes=scratch,
        compiler_params=pltpu.CompilerParams(vmem_limit_bytes=VMEM_LIMIT),
        cost_estimate=pl.CostEstimate(
            flops=int(1.0 * flops), bytes_accessed=moved, transcendentals=transcendentals
        ),
    )(*arrays)


def norm_rows(summed):
    centred = summed - jnp.mean(summed, -1, keepdims=True)
    inverse = lax.rsqrt(jnp.mean(centred * centred, -1, keepdims=True) + NORM_EPS)
    return centred * inverse, inverse


def norm_pull(gradient, unit_rows, inverse, gain_row):
    scaled = gradient * gain_row
    return inverse * (
        scaled
        - jnp.mean(scaled, -1, keepdims=True)
        - unit_rows * jnp.mean(scaled * unit_rows, -1, keepdims=True)
    )


def add_rows(ref, rows):
    sums = [jnp.sum(row, 0, keepdims=True) for row in rows]
    start = pl.program_id(0) == 0
    for place, total in enumerate(sums):
        kept = jnp.where(start, 0.0, ref[place : place + 1, :])
        ref[place : place + 1, :] = kept + total


def settle(place, refs, whole_ref, shards):
    @pl.when(pl.program_id(0) == 0)
    def _():
        place(refs, whole_ref)

    return [whole_ref.at[j] for j in range(shards)]


def pair_masks(length):
    wide = 2 * HEAD_DIM
    lower = lax.broadcasted_iota(jnp.int32, (length, wide), 1) < HEAD_DIM
    top = lax.broadcasted_iota(jnp.int32, (2 * length, wide), 0) < length
    left = lax.broadcasted_iota(jnp.int32, (2 * length, wide), 1) < HEAD_DIM
    return lower, top == left


def stacked(pair, own):
    return jnp.where(own, jnp.concatenate([pair, pair], 0), jnp.zeros((), pair.dtype))


def attention_kernel(place, shards, local_heads, length, *refs):
    rows_ref, across_ref, down_ref, bias_ref, vec_ref = refs[:5]
    packed_ref, probs_ref, attended_ref, unit_ref, inverse_ref, low_ref, whole_ref, scores_ref = (
        refs[-8:]
    )
    weights = settle(place, refs[5:-8], whole_ref, shards)
    head_width = local_heads * HEAD_DIM
    width = 3 * head_width
    wide = 2 * HEAD_DIM
    pairs = HEADS // 2
    rows = rows_ref[...]
    for j in range(shards):
        packed = product(rows, weights[j][:, :width]) + bias_ref[j : j + 1, :]
        for kind in range(3):
            part = packed[:, kind * head_width : (kind + 1) * head_width].astype(jnp.bfloat16)
            if kind == 0:
                part = part * jnp.bfloat16(HEAD_DIM ** (-0.5))
            start = kind * D + j * head_width
            packed_ref[:, start : start + head_width] = part
    _, own = pair_masks(length)
    ones = own.astype(jnp.bfloat16)
    steps = [(p, i) for p in range(ROWS // length) for i in range(pairs)]

    def pair_of(p, i, kind):
        span = slice(p * length, (p + 1) * length)
        return packed_ref[span, kind * D + i * wide : kind * D + (i + 1) * wide]

    for at, (p, i) in enumerate(steps):
        scores_ref[at] = dot_nt(pair_of(p, i, 0), stacked(pair_of(p, i, 1), own))
    for at, (p, i) in enumerate(steps):
        allowed = down_ref[p] == across_ref[p]
        for half in range(2):
            lanes = slice(half * length, (half + 1) * length)
            scores = jnp.where(allowed, scores_ref[at, :, lanes], MASKED)
            probs_ref[p, i, :, lanes] = jnp.exp(
                scores - jnp.max(scores, -1, keepdims=True)
            ).astype(jnp.bfloat16)
    for p, i in steps:
        mixed = product(
            probs_ref[p, i], jnp.concatenate([stacked(pair_of(p, i, 2), own), ones], 1)
        )
        attended_ref[p * length : (p + 1) * length, i * wide : (i + 1) * wide] = (
            mixed[:, :wide] / mixed[:, wide:]
        ).astype(jnp.bfloat16)
    summed = rows.astype(jnp.float32) + vec_ref[0:1, :]
    for j in range(shards):
        summed = summed + dot_nt(
            attended_ref[:, j * head_width : (j + 1) * head_width], weights[j][:, width:]
        )
    unit, inverse = norm_rows(summed)
    unit_ref[...] = unit
    inverse_ref[...] = inverse
    low_ref[...] = (unit * vec_ref[1:2, :] + vec_ref[2:3, :]).astype(jnp.bfloat16)


def normal_cdf(values):
    decay = jnp.exp(values * values * -0.5)
    t = 1.0 / (1.0 + jnp.abs(values) * (0.3275911 * 0.5**0.5))
    poly = t * (
        0.127414796
        + t * (-0.142248368 + t * (0.7107068705 + t * (-0.7265760135 + t * 0.5307027145)))
    )
    upper = poly * decay
    return jnp.where(values > 0, 1.0 - upper, upper), decay


def up_kernel(place, shards, *refs):
    low_ref, bias_ref = refs[:2]
    act_ref, slope_ref, whole_ref = refs[-3:]
    weights = settle(place, refs[2:-3], whole_ref, shards)
    width = weights[0].shape[1]
    chunk = 256
    low = low_ref[...]
    for j in range(shards):
        for c in range(0, width, chunk):
            pre = product(low, weights[j][:, c : c + chunk]) + bias_ref[j : j + 1, c : c + chunk]
            below, decay = normal_cdf(pre)
            at = j * width + c
            act_ref[:, at : at + chunk] = (pre * below).astype(jnp.bfloat16)
            slope_ref[:, at : at + chunk] = (
                below + pre * decay * (0.5 / math.pi) ** 0.5
            ).astype(jnp.bfloat16)


def down_kernel(place, shards, *refs):
    act_ref, unit_ref, grad_ref, vec_ref = refs[:4]
    out_ref, dz_ref, low_ref, sums_ref, whole_ref = refs[-5:]
    weights = settle(place, refs[4:-5], whole_ref, shards)
    width = weights[0].shape[1]
    summed = unit_ref[...] * vec_ref[1:2, :] + vec_ref[2:3, :] + vec_ref[3:4, :]
    for j in range(shards):
        summed = summed + dot_nt(act_ref[:, j * width : (j + 1) * width], weights[j][...])
    unit, inverse = norm_rows(summed)
    gain = vec_ref[4:5, :]
    out_ref[...] = unit * gain + vec_ref[5:6, :]
    gradient = grad_ref[...]
    dz = norm_pull(gradient, unit, inverse, gain)
    dz_ref[...] = dz
    low_ref[...] = dz.astype(jnp.bfloat16)
    add_rows(sums_ref, (gradient * unit, gradient, dz))


def hidden_back_kernel(shards, *refs):
    low_ref, slope_ref, whole_ref, dpre_ref, bias_sums_ref = refs
    width = whole_ref.shape[2]
    low = low_ref[...]
    for j in range(shards):
        span = slice(j * width, (j + 1) * width)
        dpre = product(low, whole_ref[j]) * slope_ref[:, span].astype(jnp.float32)
        dpre = dpre.astype(jnp.bfloat16)
        dpre_ref[:, span] = dpre
        total = jnp.sum(dpre.astype(jnp.float32), 0, keepdims=True)
        kept = jnp.where(pl.program_id(0) == 0, 0.0, bias_sums_ref[j : j + 1, :])
        bias_sums_ref[j : j + 1, :] = kept + total


def back_kernel(shards, *refs):
    dpre_ref, dz_ref, unit_ref, inverse_ref, vec_ref, up_ref, first_ref = refs[:7]
    dz1_ref, low1_ref, datt_ref, sums_ref = refs[7:]
    width = up_ref.shape[2]
    gradient = dz_ref[...]
    for j in range(shards):
        gradient = gradient + dot_nt(dpre_ref[:, j * width : (j + 1) * width], up_ref[j])
    unit = unit_ref[...]
    dz1 = norm_pull(gradient, unit, inverse_ref[...], vec_ref[1:2, :])
    dz1_ref[...] = dz1
    low1 = dz1.astype(jnp.bfloat16)
    low1_ref[...] = low1
    add_rows(sums_ref, (gradient * unit, gradient, dz1))
    head_width = D // shards
    for j in range(shards):
        datt_ref[:, j * head_width : (j + 1) * head_width] = product(
            low1, first_ref[j, :, 3 * head_width :]
        ).astype(jnp.bfloat16)


def attention_back_kernel(length, *refs):
    datt_ref, attended_ref, packed_ref, probs_ref, dpacked_ref, sums_ref, up_ref, grad_ref = refs
    wide = 2 * HEAD_DIM
    lower, own = pair_masks(length)
    ones = own.astype(jnp.bfloat16)
    steps = [(p, i) for p in range(ROWS // length) for i in range(HEADS // 2)]

    def pair_of(p, i, kind):
        span = slice(p * length, (p + 1) * length)
        return packed_ref[span, kind * D + i * wide : kind * D + (i + 1) * wide]

    def keep(p, i, kind, grad):
        span = slice(p * length, (p + 1) * length)
        dpacked_ref[span, kind * D + i * wide : kind * D + (i + 1) * wide] = grad.astype(
            jnp.bfloat16
        )

    for place, (p, i) in enumerate(steps):
        span = slice(p * length, (p + 1) * length)
        lanes = slice(i * wide, (i + 1) * wide)
        upstream = datt_ref[span, lanes].astype(jnp.float32) / product(probs_ref[p, i], ones)
        up_ref[place, :, :wide] = upstream.astype(jnp.bfloat16)
        up_ref[place, :, wide:] = (upstream * attended_ref[span, lanes].astype(jnp.float32)).astype(
            jnp.bfloat16
        )
    for place, (p, i) in enumerate(steps):
        centred = dot_nt(
            up_ref[place], jnp.concatenate([stacked(pair_of(p, i, 2), own), -ones], 1)
        )
        grad_ref[place] = (probs_ref[p, i].astype(jnp.float32) * centred).astype(jnp.bfloat16)
    for place, (p, i) in enumerate(steps):
        grad_scores = grad_ref[place]
        keep(
            p, i, 0,
            product(grad_scores, stacked(pair_of(p, i, 1), own)) * HEAD_DIM ** (-0.5),
        )
        both = transposed_times(grad_scores, pair_of(p, i, 0))
        keep(p, i, 1, jnp.where(lower, both[:length], both[length:]))
        both = transposed_times(probs_ref[p, i], up_ref[place, :, :wide])
        keep(p, i, 2, jnp.where(lower, both[:length], both[length:]))
    total = jnp.sum(dpacked_ref[...].astype(jnp.float32), 0, keepdims=True)
    kept = jnp.where(pl.program_id(0) == 0, 0.0, sums_ref[0:1, :])
    sums_ref[0:1, :] = kept + total


def weight_kernel(odd, count, *refs):
    lefts, refs = refs[:2] if count > 1 else refs[:1], refs[2 if count > 1 else 1 :]
    rights, (out_ref, *turned) = refs[:count], refs[count:]
    start = pl.program_id(0) == 0

    @pl.when(start)
    def _():
        for left, kept in zip(lefts, turned):
            kept[...] = left[...].T

    at = 0
    for place, right in enumerate(rights):
        half = right.shape[1] // 2
        values = right[...] if count == 1 else right[:, half:] if odd else right[:, :half]
        grad = product(turned[place == count - 1 and count > 1][...], values)
        out_ref[0, :, at : at + values.shape[1]] = grad.astype(jnp.bfloat16)
        at += values.shape[1]


def weight_halves(lefts, rights):
    halves = []
    for odd in (1, 0):
        count = len(rights)
        single = count == 1
        specs = []
        for array, width, before in rights:
            if single:
                specs.append(pl.BlockSpec((array.shape[0], width), lambda i: (0, 2 * i + odd)))
            else:
                specs.append(
                    pl.BlockSpec((array.shape[0], 2 * width), lambda i, b=before: (0, b + i))
                )
        arrays = [*lefts, *[array for array, _, _ in rights]]
        tokens = lefts[0].shape[0]
        (half,) = pl.pallas_call(
            functools.partial(weight_kernel, odd, count),
            grid=(2,),
            in_specs=[whole_block(left) for left in lefts] + specs,
            out_specs=[pl.BlockSpec((1, D, D), lambda i: (i, 0, 0))],
            out_shape=[jax.ShapeDtypeStruct((2, D, D), jnp.bfloat16)],
            scratch_shapes=[pltpu.VMEM((D, tokens), jnp.bfloat16) for _ in lefts],
            compiler_params=pltpu.CompilerParams(vmem_limit_bytes=VMEM_LIMIT),
            cost_estimate=pl.CostEstimate(
                flops=4 * tokens * D * D,
                bytes_accessed=sum(2 * array.size for array in arrays),
                transcendentals=0,
            ),
        )(*arrays)
        halves.append(half)
    return halves


def natural_kernel(shards, *refs):
    out_ref, dz1_ref, dpacked_ref, selector_ref, whole_ref, layer_ref, input_ref = refs
    weights = [whole_ref.at[j] for j in range(shards)]
    head_width = D // shards
    gradient = dz1_ref[...]
    for j in range(shards):
        own = [
            dpacked_ref[:, kind * D + j * head_width : kind * D + (j + 1) * head_width]
            for kind in range(3)
        ]
        gradient = gradient + dot_nt(jnp.concatenate(own, 1), weights[j][:, : 3 * head_width])
    for source, ref in ((out_ref[...], layer_ref), (gradient, input_ref)):
        top = source.astype(jnp.bfloat16)
        rest = (source - top.astype(jnp.float32)).astype(jnp.bfloat16)
        ref[...] = dot_nt(top, selector_ref[...]) + dot_nt(rest, selector_ref[...])


def together(*values):
    return lax.optimization_barrier(values)


def local(
    tokens,
    segments,
    out_grad,
    owner,
    master,
    left_basis,
    right_basis,
    first_moment,
    second_moment,
    vectors,
    vector_first,
    vector_second,
):
    shards = lax.axis_size("tensor")
    dp_size = lax.axis_size("dp")
    direct = dp_size == PARTS and shards == 4
    tensor_rank = lax.axis_index("tensor")
    dp_rank = lax.axis_index("dp")
    local_heads = HEADS // shards
    head_width = local_heads * HEAD_DIM
    up_width = FF // shards
    width_qkv = 3 * head_width
    block_size = master.shape[-1]
    slots = master.shape[1]
    row_count = tokens.shape[0]
    length = segments.shape[1]
    pack_count = row_count // length
    own_segments = lax.dynamic_slice_in_dim(segments, tensor_rank * pack_count, pack_count, 0)
    qkv_tiles, out_tiles, up_tiles = tile_counts(shards, block_size)
    tile_total = owner.shape[0]

    group_base = tensor_rank if direct else 0
    order = feature_order(dp_rank if direct else 0)
    selector = (lax.iota(jnp.int32, D)[:, None] == order[None, :]).astype(jnp.bfloat16)

    rows_in = product(tokens, selector).astype(jnp.bfloat16)
    grad_out = exact_product(out_grad, selector, 2)

    group_order = lax.iota(jnp.int32, shards) ^ group_base
    d_vectors = jnp.stack(
        [
            vectors[0:D],
            vectors[D : 2 * D],
            vectors[4 * D : 5 * D],
            vectors[5 * D + FF : 6 * D + FF],
            vectors[6 * D + FF : 7 * D + FF],
            vectors[7 * D + FF : 8 * D + FF],
        ]
    )
    gain_first, gain_second, bias_out, bias_down, offset_first, offset_second = exact_product(
        d_vectors, selector, 3
    )
    bias_q = vectors[2 * D : 3 * D].reshape(shards, head_width)[group_order]
    bias_v = vectors[3 * D : 4 * D].reshape(shards, head_width)[group_order]
    bias_up = vectors[5 * D : 5 * D + FF].reshape(shards, up_width)[group_order]

    d_rows = jnp.stack(
        [bias_out, gain_first, offset_first, bias_down, gain_second, offset_second]
        + [jnp.zeros_like(bias_out)] * 2
    )

    def flipped(index):
        from_out = (index >= qkv_tiles) & (index < qkv_tiles + out_tiles)
        return (from_out | (index >= qkv_tiles + out_tiles + up_tiles))[:, None, None]

    own_tiles = lax.dynamic_slice_in_dim(owner, dp_rank * slots, slots, 0)
    own_flip = flipped(own_tiles)
    sent = master[0].astype(jnp.bfloat16)
    sent = jnp.where(own_flip, jnp.swapaxes(sent, 1, 2), sent)
    placing = (lax.iota(jnp.int32, tile_total)[:, None] == owner[None, :]).astype(jnp.bfloat16)
    if direct:
        parts = sent.reshape(slots, PARTS, SUB * block_size).swapaxes(0, 1)
        parts = lax.all_to_all(parts, "dp", 0, 0, tiled=True).reshape(tile_total, -1)
        tiles = product(placing, parts).astype(jnp.bfloat16)
        slab = slabs_from_tiles(tiles.reshape(tile_total, 1, SUB, block_size), shards, block_size)[0]
        half = D // 2
        up_left, up_right = slab[:, D : D + half], slab[:, D + half : 2 * D]
        first_z = over_z(slab[:, :D])
        up_near = jnp.concatenate(
            [
                slab[:, D : 2 * D],
                jnp.concatenate([swap_over(up_left, 0, 2), swap_over(up_right, 1, 0)], 1),
            ],
            0,
        )
        first_z, up_near, rows_in, grad_out, d_rows = together(
            first_z, up_near, rows_in, grad_out, d_rows
        )
        left, right = first_z[:, :half], first_z[:, half:]
        left = jnp.concatenate([left, swap_over(left, 0, 2)], 0)
        right = jnp.concatenate([right, swap_over(right, 1, 0)], 0)
        up_near = over_z(up_near)
        first = over_core(
            list(together(left, swap_over(left, 1, 0), right, swap_over(right, 0, 2)))
        )
        *first, up_near = together(*first, up_near)
        up = [up_near, swap_over(up_near[:, :half], 1, 0), swap_over(up_near[:, half:], 0, 2)]
        down_z = over_z(together(slab[:, 2 * D :], up_near)[0])
        places = (place_first, place_edges, place_plane)
        pieces = [first, None, None]
    else:
        gathered = lax.all_gather(sent, "dp", axis=0, tiled=True).reshape(tile_total, -1)
        tiles = product(placing, gathered).astype(jnp.bfloat16)
        slabs = slabs_from_tiles(
            tiles.reshape(tile_total, PARTS, SUB, block_size), shards, block_size
        )
        whole = jnp.concatenate([slabs[part_of_block(k)] for k in range(PARTS)], 0)
        every = lax.all_gather(whole, "tensor", axis=0)
        pieces = [
            [every[j][:, k * D : (k + 1) * D] for j in range(shards)] for k in range(3)
        ]
        places = (place_groups,) * 3

    steps = row_count // ROWS
    packs_step = ROWS // length
    bias_qkv = jnp.concatenate([bias_q, jnp.zeros_like(bias_q), bias_v], 1)
    rows_spec = lambda width: pl.BlockSpec((ROWS, width), lambda i: (i, 0))
    pairs = HEADS // 2
    probs_spec = pl.BlockSpec((packs_step, pairs, length, 2 * length), lambda i: (i, 0, 0, 0))
    sums_spec = lambda width: pl.BlockSpec((8, width), lambda i: (0, 0))
    f32, bf16 = jnp.float32, jnp.bfloat16
    full = lambda array: (array, whole_block(array))
    by_rows = lambda array: (array, row_block(array))
    square = 2 * row_count * D * D

    whole_spec = pl.BlockSpec((shards, D, D), lambda i: (0, 0, 0))
    whole_out = ((shards, D, D), bf16, whole_spec)
    packed, probs, attended, unit_first, inverse_first, normed_low, whole_first = call_rows(
        functools.partial(attention_kernel, places[0], shards, local_heads, length),
        steps,
        [
            by_rows(rows_in),
            (own_segments[:, None, :], pl.BlockSpec((packs_step, 1, length), lambda i: (i, 0, 0))),
            (own_segments[:, :, None], pl.BlockSpec((packs_step, length, 1), lambda i: (i, 0, 0))),
            full(bias_qkv),
            full(d_rows),
            *[full(w) for w in pieces[0]],
        ],
        [
            ((row_count, 3 * D), bf16, rows_spec(3 * D)),
            ((pack_count, pairs, length, 2 * length), bf16, probs_spec),
            ((row_count, D), bf16, rows_spec(D)),
            ((row_count, D), f32, rows_spec(D)),
            ((row_count, 1), f32, rows_spec(1)),
            ((row_count, D), bf16, rows_spec(D)),
            whole_out,
        ],
        4 * square + 4 * row_count * length * D,
        row_count * length * HEADS,
        [pltpu.VMEM((packs_step * pairs, length, 2 * length), f32)],
    )
    if direct:
        *up, down_z, normed_low = together(*up, down_z, normed_low)
        down = [down_z, swap_over(down_z, 1, 0), swap_over(down_z, 0, 2), swap_over(down_z, 1, 2)]
        pieces[1] = over_core(up)
    activated, slope, whole_up = call_rows(
        functools.partial(up_kernel, places[1], shards),
        steps,
        [by_rows(normed_low), full(bias_up), *[full(w) for w in pieces[1]]],
        [
            ((row_count, FF), bf16, rows_spec(FF)),
            ((row_count, FF), bf16, rows_spec(FF)),
            whole_out,
        ],
        4 * square,
        2 * row_count * FF,
    )
    if direct:
        *down, activated = together(*down, activated)
        pieces[2] = over_core(down)
    layer_out, grad_second, second_low, sums_second, whole_down = call_rows(
        functools.partial(down_kernel, places[2], shards),
        steps,
        [
            by_rows(activated),
            by_rows(unit_first),
            by_rows(grad_out),
            full(d_rows),
            *[full(w) for w in pieces[2]],
        ],
        [
            ((row_count, D), f32, rows_spec(D)),
            ((row_count, D), f32, rows_spec(D)),
            ((row_count, D), bf16, rows_spec(D)),
            ((8, D), f32, sums_spec(D)),
            whole_out,
        ],
        4 * square,
    )
    grad_w_down = weight_halves([second_low], [(activated, up_width, 0)])
    if direct:
        down_low = reduce_core(grad_w_down)
        second_low, *down_low = together(second_low, *down_low)
        down_plane = reduce_plane(down_low)
    grad_pre, grad_bias_up = call_rows(
        functools.partial(hidden_back_kernel, shards),
        steps,
        [by_rows(second_low), by_rows(slope), full(whole_down)],
        [((row_count, FF), bf16, rows_spec(FF)), ((8, up_width), f32, sums_spec(up_width))],
        4 * square,
    )
    grad_bias_up = grad_bias_up[:shards]
    grad_w_up = weight_halves([normed_low], [(grad_pre, up_width, 0)])
    grad_first, first_low, grad_attended, sums_first = call_rows(
        functools.partial(back_kernel, shards),
        steps,
        [
            by_rows(grad_pre),
            by_rows(grad_second),
            by_rows(unit_first),
            by_rows(inverse_first),
            full(d_rows),
            full(whole_up),
            full(whole_first),
        ],
        [
            ((row_count, D), f32, rows_spec(D)),
            ((row_count, D), bf16, rows_spec(D)),
            ((row_count, D), bf16, rows_spec(D)),
            ((8, D), f32, sums_spec(D)),
        ],
        5 * square,
    )
    if direct:
        up_low = reduce_core(grad_w_up)
        grad_attended, *up_low, down_plane = together(grad_attended, *up_low, down_plane)
        up_edges = reduce_edges(up_low)
        down_own = reduce_z(down_plane)
    grad_packed, column_sums = call_rows(
        functools.partial(attention_back_kernel, length),
        steps,
        [by_rows(grad_attended), by_rows(attended), by_rows(packed), (probs, probs_spec)],
        [
            ((row_count, 3 * D), bf16, rows_spec(3 * D)),
            ((8, 3 * D), f32, sums_spec(3 * D)),
        ],
        8 * square,
        0,
        [pltpu.VMEM((packs_step * pairs, length, 2 * length), bf16)] * 2,
    )
    column_sums = column_sums[0].reshape(3, shards, head_width)
    grad_w_first = weight_halves(
        [rows_in, first_low],
        [(grad_packed, head_width, k * shards // 2) for k in range(3)] + [(attended, head_width, 0)],
    )
    if direct:
        grad_odd, grad_even, up_edges, down_own = together(*grad_w_first, up_edges, down_own)
        first_low = reduce_core((grad_odd, grad_even))
        *first_low, layer_out = together(*first_low, layer_out)
        first_edges = reduce_edges(first_low)
        up_edges = reduce_edges_z(up_edges)
    layer_out, input_grad = call_rows(
        functools.partial(natural_kernel, shards),
        steps,
        [
            by_rows(layer_out),
            by_rows(grad_first),
            by_rows(grad_packed),
            full(selector),
            full(whole_first),
        ],
        [((row_count, D), f32, rows_spec(D)), ((row_count, D), f32, rows_spec(D))],
        7 * square,
    )

    if direct:
        first_plane = reduce_edges_plane(first_edges).astype(bf16)
        first_plane, up_edges, *others = together(
            first_plane,
            up_edges,
            layer_out,
            input_grad,
            sums_first,
            sums_second,
            grad_bias_up,
            column_sums,
        )
        layer_out, input_grad, sums_first, sums_second, grad_bias_up, column_sums = others
        first_own = reduce_z(first_plane)
        up_own = reduce_edges_plane(up_edges)
        slab_grad = jnp.concatenate([first_own, up_own, down_own], 1).astype(jnp.bfloat16)
        tile_grad = tiles_from_slabs(slab_grad[None], shards, block_size).reshape(tile_total, -1)
        slot_grad = transposed_times(placing, tile_grad).astype(jnp.bfloat16)
        slot_grad = lax.all_to_all(
            slot_grad.reshape(PARTS, slots, SUB * block_size), "dp", 0, 0, tiled=True
        )
        owned_grads = slot_grad.swapaxes(0, 1).reshape(slots, block_size, block_size)
    else:
        every = jnp.stack(
            [
                jnp.concatenate(
                    [half[1 - j % 2][j // 2] for half in (grad_w_first, grad_w_up, grad_w_down)], 1
                )
                for j in range(shards)
            ]
        ).astype(jnp.float32)
        mine = lax.psum_scatter(every, "tensor", scatter_dimension=0, tiled=True)[0]
        blocks = mine.reshape(PARTS, D // PARTS, -1)
        blocks = jnp.stack([blocks[(p % 2) * 4 + p // 2] for p in range(PARTS)])
        tile_grad = tiles_from_slabs(blocks, shards, block_size)
        slot_grad = tile_grad.reshape(tile_total, block_size, block_size)[owner]
        owned_grads = lax.psum_scatter(slot_grad, "dp", scatter_dimension=0, tiled=True)
    owned_grads = owned_grads.astype(jnp.float32)
    owned_grads = jnp.where(own_flip, jnp.swapaxes(owned_grads, 1, 2), owned_grads)

    grad_gain_second, grad_offset_second, grad_bias_down = (sums_second[k] for k in range(3))
    grad_gain_first, grad_offset_first, grad_bias_out = (sums_first[k] for k in range(3))
    d_grads = exact_product_t(
        jnp.stack(
            [
                grad_gain_first,
                grad_gain_second,
                grad_bias_out,
                grad_bias_down,
                grad_offset_first,
                grad_offset_second,
            ]
        ),
        selector,
        3,
    )
    grad_vector = jnp.concatenate(
        [
            d_grads[0],
            d_grads[1],
            column_sums[0][group_order].reshape(-1),
            column_sums[2][group_order].reshape(-1),
            d_grads[2],
            grad_bias_up[group_order].reshape(-1),
            d_grads[3],
            d_grads[4],
            d_grads[5],
        ]
    )
    vector_grad = sum_over_all(grad_vector) if direct else lax.psum(grad_vector, ("dp", "tensor"))


    bias_first = 1.0 - DECAY_FIRST**ADAM_STEP
    bias_second = 1.0 - DECAY_SECOND**ADAM_STEP
    left_side = left_basis[0]
    right_side = right_basis[0]
    rotated = precise(jnp.swapaxes(left_side, -1, -2), precise(owned_grads, right_side))
    new_first = DECAY_FIRST * first_moment[0] + (1.0 - DECAY_FIRST) * rotated
    new_second = DECAY_SECOND * second_moment[0] + (1.0 - DECAY_SECOND) * rotated * rotated
    direction = new_first / bias_first / (jnp.sqrt(new_second / bias_second) + ADAM_EPS)
    new_master = master[0] - MATRIX_RATE * precise(
        precise(left_side, direction), jnp.swapaxes(right_side, -1, -2)
    )
    new_vector_first = DECAY_FIRST * vector_first + (1.0 - DECAY_FIRST) * vector_grad
    new_vector_second = (
        DECAY_SECOND * vector_second + (1.0 - DECAY_SECOND) * vector_grad * vector_grad
    )
    new_vectors = vectors - VECTOR_RATE * (new_vector_first / bias_first) / (
        jnp.sqrt(new_vector_second / bias_second) + ADAM_EPS
    )
    return (
        layer_out,
        input_grad,
        new_master[None],
        new_first[None],
        new_second[None],
        new_vectors,
        new_vector_first,
        new_vector_second,
    )


def solution(mesh):
    return jax.shard_map(
        local,
        mesh=mesh,
        in_specs=(
            P(("dp", "tensor"), None),
            P("dp", None),
            P(("dp", "tensor"), None),
            P(),
            P("tensor", "dp", None, None),
            P("tensor", "dp", None, None),
            P("tensor", "dp", None, None),
            P("tensor", "dp", None, None),
            P("tensor", "dp", None, None),
            P(),
            P(),
            P(),
        ),
        out_specs=(
            P(("dp", "tensor"), None),
            P(("dp", "tensor"), None),
            P("tensor", "dp", None, None),
            P("tensor", "dp", None, None),
            P("tensor", "dp", None, None),
            P(),
            P(),
            P(),
        ),
        check_vma=False,
    )
```

```python
import functools
import math

import jax
import jax.numpy as jnp
from jax import lax
from jax.experimental import pallas as pl
from jax.experimental.pallas import tpu as pltpu
from jax.sharding import PartitionSpec as P

HEADS = 12
HEAD_DIM = 64
D = 768
FF = 3072
ADAM_STEP = 3


NORM_EPS = 1e-12
ADAM_EPS = 1e-08
MATRIX_RATE = 0.01
VECTOR_RATE = 0.1
DECAY_FIRST = 0.5
DECAY_SECOND = 0.5
MASKED = -1e30


def product(left_side, right_side):
    return jnp.dot(left_side, right_side, preferred_element_type=jnp.float32)


def times_transposed(left_side, right_side):
    return lax.dot_general(
        left_side, right_side, (((1,), (1,)), ((), ())), preferred_element_type=jnp.float32
    )


def transposed_times(left_side, right_side):
    return lax.dot_general(
        left_side, right_side, (((0,), (0,)), ((), ())), preferred_element_type=jnp.float32
    )


VMEM_LIMIT = 32 * 1024 * 1024

PARTS = 8
SUB = 12


def rounded(values):
    return lax.reduce_precision(values, 8, 7)


def split_terms(values, count):
    terms = []
    for _ in range(count):
        top = rounded(values)
        terms.append(top.astype(jnp.bfloat16))
        values = values - top
    return terms


def exact_product(values, selector, count):
    return sum(product(term, selector) for term in split_terms(values, count))


def exact_product_t(values, selector, count):
    return sum(times_transposed(term, selector) for term in split_terms(values, count))


def part_of_block(block):
    return (block % 4) * 2 + block // 4


def feature_order(rank):
    place = lax.iota(jnp.int32, D)
    part = part_of_block(place // (D // PARTS)) ^ rank
    inner = place % (D // PARTS)
    return (inner // SUB) * (PARTS * SUB) + part * SUB + inner % SUB


def tile_counts(shards, block_size):
    rows = D // block_size
    qkv = rows * (3 * D // shards // block_size)
    out = rows * (D // shards // block_size)
    up = rows * (FF // shards // block_size)
    return (qkv, out, up)


def slabs_from_tiles(tiles, shards, block_size):
    cut = tiles.shape[1]
    qkv, out, up = tile_counts(shards, block_size)
    rows = D // block_size

    def by_rows(part):
        cols = part.shape[0] // rows
        part = part.reshape(rows, cols, cut, SUB, block_size)
        return part.transpose(2, 0, 3, 1, 4).reshape(cut, rows * SUB, cols * block_size)

    def by_cols(part):
        cols = part.shape[0] // rows
        part = part.reshape(cols, rows, cut, SUB, block_size)
        return part.transpose(2, 1, 3, 0, 4).reshape(cut, rows * SUB, cols * block_size)

    return jnp.concatenate(
        [
            by_rows(tiles[:qkv]),
            by_cols(tiles[qkv : qkv + out]),
            by_rows(tiles[qkv + out : qkv + out + up]),
            by_cols(tiles[qkv + out + up :]),
        ],
        2,
    )


def tiles_from_slabs(slabs, shards, block_size):
    cut = slabs.shape[0]
    rows = D // block_size
    width_qkv, width_out, width_up = 3 * D // shards, D // shards, FF // shards

    def by_rows(part):
        cols = part.shape[2] // block_size
        part = part.reshape(cut, rows, SUB, cols, block_size)
        return part.transpose(1, 3, 0, 2, 4).reshape(rows * cols, cut, SUB, block_size)

    def by_cols(part):
        cols = part.shape[2] // block_size
        part = part.reshape(cut, rows, SUB, cols, block_size)
        return part.transpose(3, 1, 0, 2, 4).reshape(rows * cols, cut, SUB, block_size)

    first = width_qkv + width_out
    second = first + width_up
    return jnp.concatenate(
        [
            by_rows(slabs[:, :, :width_qkv]),
            by_cols(slabs[:, :, width_qkv:first]),
            by_rows(slabs[:, :, first:second]),
            by_cols(slabs[:, :, second:]),
        ],
        0,
    )


def swap_over(values, over_dp, over_tensor):
    dp, tensor = lax.axis_size("dp"), lax.axis_size("tensor")
    pairs = [
        (a * tensor + b, (a ^ over_dp) * tensor + (b ^ over_tensor))
        for a in range(dp)
        for b in range(tensor)
    ]
    return lax.ppermute(values, ("dp", "tensor"), pairs)


def over_z(block):
    return jnp.concatenate([block] + [swap_over(block, 2 * k, 0) for k in (1, 2, 3)], 0)


def over_core(blocks):
    return blocks + [swap_over(block, 0, 1) for block in blocks]


def place_first(refs, out_ref):
    count = len(refs) // 2
    half, cols = D // 2, D // 2
    for core in range(2):
        near, beside, right, across = refs[core * count : (core + 1) * count]
        for y in range(2):
            group = 2 * y + core
            out_ref[group, :half, :cols] = near[y * half : (y + 1) * half, :]
            out_ref[group, half:, :cols] = beside[y * half : (y + 1) * half, :]
            out_ref[group, :, cols:] = (right, across)[y][...]


def place_edges(refs, out_ref):
    count = len(refs) // 2
    rows, half, cols = D // PARTS, D // 2, D // 2
    for core in range(2):
        near, beside, across = refs[core * count : (core + 1) * count]
        for y in range(2):
            for z in range(4):
                for x in range(2):
                    to = x * half + z * rows
                    by_y, by_x = (2 * z + y) * rows, (2 * z + x) * rows
                    left = beside[by_y : by_y + rows, :] if x else near[by_y : by_y + rows, :cols]
                    right = across[by_x : by_x + rows, :] if y else near[by_x : by_x + rows, cols:]
                    out_ref[2 * y + core, to : to + rows, :cols] = left
                    out_ref[2 * y + core, to : to + rows, cols:] = right


def place_plane(refs, out_ref):
    half = D // 2
    for core in range(2):
        for y in range(2):
            for x in range(2):
                out_ref[2 * y + core, x * half : (x + 1) * half, :] = refs[4 * core + 2 * y + x][...]


def place_groups(refs, out_ref):
    for group, ref in enumerate(refs):
        out_ref[group] = ref[...]


def total(*terms):
    return sum(term.astype(jnp.float32) for term in terms)


def reduce_core(halves):
    odd, even = halves
    both = total(even, swap_over(odd, 0, 1)).astype(jnp.bfloat16)
    return both[0], both[1]


def reduce_plane(low):
    half = low[0].shape[0] // 2
    return total(
        low[0][:half],
        swap_over(low[0][half:], 1, 0),
        swap_over(low[1][:half], 0, 2),
        swap_over(low[1][half:], 1, 2),
    ).astype(jnp.bfloat16)


def reduce_z(plane):
    rows = plane.shape[0] // 4
    return total(
        plane[:rows],
        *[swap_over(plane[k * rows : (k + 1) * rows], 2 * k, 0) for k in (1, 2, 3)],
    )


def reduce_edges(low):
    half, cols = low[0].shape[0] // 2, low[0].shape[1] // 2
    near = jnp.concatenate([low[0][:half, :cols], low[1][:half, :cols]], 0)
    far = jnp.concatenate([low[0][half:, :cols], low[1][half:, :cols]], 0)
    left = total(near, swap_over(far, 1, 0))
    right = total(low[0][:, cols:], swap_over(low[1][:, cols:], 0, 2))
    return jnp.concatenate([left, right], 1).astype(jnp.bfloat16)


def reduce_edges_plane(edges):
    rows, cols = edges.shape[0] // 2, edges.shape[1] // 2
    left = total(edges[:rows, :cols], swap_over(edges[rows:, :cols], 0, 2))
    right = total(edges[:rows, cols:], swap_over(edges[rows:, cols:], 1, 0))
    return jnp.concatenate([left, right], 1)


def reduce_edges_z(edges):
    rows = edges.shape[0] // 8
    sent = [
        jnp.concatenate([edges[k * rows : (k + 1) * rows], edges[(4 + k) * rows : (5 + k) * rows]], 0)
        for k in range(4)
    ]
    return total(sent[0], *[swap_over(sent[k], 2 * k, 0) for k in (1, 2, 3)]).astype(jnp.bfloat16)


def sum_over_all(values):
    return jnp.sum(lax.all_gather(values[None], ("dp", "tensor"), axis=0, tiled=True), 0)


ROWS = 256


def dot_nt(left_side, right_side):
    return lax.dot_general(
        left_side, right_side, (((1,), (1,)), ((), ())), preferred_element_type=jnp.float32
    )


def whole_block(array):
    rank = array.ndim
    return pl.BlockSpec(array.shape, lambda i: (0,) * rank)


def row_block(array):
    return pl.BlockSpec((ROWS, array.shape[1]), lambda i: (i, 0))


def call_rows(kernel, steps, inputs, outputs, flops, transcendentals=0, scratch=()):
    arrays = [array for array, _ in inputs]
    shapes = [jax.ShapeDtypeStruct(shape, dtype) for shape, dtype, _ in outputs]
    moved = sum(a.size * a.dtype.itemsize for a in arrays + shapes)
    return pl.pallas_call(
        kernel,
        grid=(steps,),
        in_specs=[spec for _, spec in inputs],
        out_specs=[spec for _, _, spec in outputs],
        out_shape=shapes,
        scratch_shapes=scratch,
        compiler_params=pltpu.CompilerParams(vmem_limit_bytes=VMEM_LIMIT),
        cost_estimate=pl.CostEstimate(
            flops=int(1.0 * flops), bytes_accessed=moved, transcendentals=transcendentals
        ),
    )(*arrays)


def norm_rows(summed):
    centred = summed - jnp.mean(summed, -1, keepdims=True)
    inverse = lax.rsqrt(jnp.mean(centred * centred, -1, keepdims=True) + NORM_EPS)
    return centred * inverse, inverse


def norm_pull(gradient, unit_rows, inverse, gain_row):
    scaled = gradient * gain_row
    return inverse * (
        scaled
        - jnp.mean(scaled, -1, keepdims=True)
        - unit_rows * jnp.mean(scaled * unit_rows, -1, keepdims=True)
    )


def add_rows(ref, rows):
    sums = [jnp.sum(row, 0, keepdims=True) for row in rows]
    start = pl.program_id(0) == 0
    for place, total in enumerate(sums):
        kept = jnp.where(start, 0.0, ref[place : place + 1, :])
        ref[place : place + 1, :] = kept + total


def settle(place, refs, whole_ref, shards):
    @pl.when(pl.program_id(0) == 0)
    def _():
        place(refs, whole_ref)

    return [whole_ref.at[j] for j in range(shards)]


def pair_masks(length):
    wide = 2 * HEAD_DIM
    lower = lax.broadcasted_iota(jnp.int32, (length, wide), 1) < HEAD_DIM
    top = lax.broadcasted_iota(jnp.int32, (2 * length, wide), 0) < length
    left = lax.broadcasted_iota(jnp.int32, (2 * length, wide), 1) < HEAD_DIM
    return lower, top == left


def stacked(pair, own):
    return jnp.where(own, jnp.concatenate([pair, pair], 0), jnp.zeros((), pair.dtype))


def attention_kernel(place, shards, local_heads, length, *refs):
    rows_ref, across_ref, down_ref, bias_ref, vec_ref = refs[:5]
    packed_ref, probs_ref, attended_ref, unit_ref, inverse_ref, low_ref, whole_ref, scores_ref = (
        refs[-8:]
    )
    weights = settle(place, refs[5:-8], whole_ref, shards)
    head_width = local_heads * HEAD_DIM
    width = 3 * head_width
    wide = 2 * HEAD_DIM
    pairs = HEADS // 2
    rows = rows_ref[...]
    for j in range(shards):
        packed = product(rows, weights[j][:, :width]) + bias_ref[j : j + 1, :]
        for kind in range(3):
            part = packed[:, kind * head_width : (kind + 1) * head_width].astype(jnp.bfloat16)
            if kind == 0:
                part = part * jnp.bfloat16(HEAD_DIM ** (-0.5))
            start = kind * D + j * head_width
            packed_ref[:, start : start + head_width] = part
    _, own = pair_masks(length)
    ones = own.astype(jnp.bfloat16)
    steps = [(p, i) for p in range(ROWS // length) for i in range(pairs)]

    def pair_of(p, i, kind):
        span = slice(p * length, (p + 1) * length)
        return packed_ref[span, kind * D + i * wide : kind * D + (i + 1) * wide]

    for at, (p, i) in enumerate(steps):
        scores_ref[at] = dot_nt(pair_of(p, i, 0), stacked(pair_of(p, i, 1), own))
    for at, (p, i) in enumerate(steps):
        allowed = down_ref[p] == across_ref[p]
        for half in range(2):
            lanes = slice(half * length, (half + 1) * length)
            scores = jnp.where(allowed, scores_ref[at, :, lanes], MASKED)
            probs_ref[p, i, :, lanes] = jnp.exp(
                scores - jnp.max(scores, -1, keepdims=True)
            ).astype(jnp.bfloat16)
    for p, i in steps:
        mixed = product(
            probs_ref[p, i], jnp.concatenate([stacked(pair_of(p, i, 2), own), ones], 1)
        )
        attended_ref[p * length : (p + 1) * length, i * wide : (i + 1) * wide] = (
            mixed[:, :wide] / mixed[:, wide:]
        ).astype(jnp.bfloat16)
    summed = rows.astype(jnp.float32) + vec_ref[0:1, :]
    for j in range(shards):
        summed = summed + dot_nt(
            attended_ref[:, j * head_width : (j + 1) * head_width], weights[j][:, width:]
        )
    unit, inverse = norm_rows(summed)
    unit_ref[...] = unit
    inverse_ref[...] = inverse
    low_ref[...] = (unit * vec_ref[1:2, :] + vec_ref[2:3, :]).astype(jnp.bfloat16)


def normal_cdf(values):
    decay = jnp.exp(values * values * -0.5)
    t = 1.0 / (1.0 + jnp.abs(values) * (0.3275911 * 0.5**0.5))
    poly = t * (
        0.127414796
        + t * (-0.142248368 + t * (0.7107068705 + t * (-0.7265760135 + t * 0.5307027145)))
    )
    upper = poly * decay
    return jnp.where(values > 0, 1.0 - upper, upper), decay


def up_kernel(place, shards, *refs):
    low_ref, bias_ref = refs[:2]
    act_ref, slope_ref, whole_ref = refs[-3:]
    weights = settle(place, refs[2:-3], whole_ref, shards)
    width = weights[0].shape[1]
    chunk = 256
    low = low_ref[...]
    for j in range(shards):
        for c in range(0, width, chunk):
            pre = product(low, weights[j][:, c : c + chunk]) + bias_ref[j : j + 1, c : c + chunk]
            below, decay = normal_cdf(pre)
            at = j * width + c
            act_ref[:, at : at + chunk] = (pre * below).astype(jnp.bfloat16)
            slope_ref[:, at : at + chunk] = (
                below + pre * decay * (0.5 / math.pi) ** 0.5
            ).astype(jnp.bfloat16)


def down_kernel(place, shards, *refs):
    act_ref, unit_ref, grad_ref, vec_ref = refs[:4]
    out_ref, dz_ref, low_ref, sums_ref, whole_ref = refs[-5:]
    weights = settle(place, refs[4:-5], whole_ref, shards)
    width = weights[0].shape[1]
    summed = unit_ref[...] * vec_ref[1:2, :] + vec_ref[2:3, :] + vec_ref[3:4, :]
    for j in range(shards):
        summed = summed + dot_nt(act_ref[:, j * width : (j + 1) * width], weights[j][...])
    unit, inverse = norm_rows(summed)
    gain = vec_ref[4:5, :]
    out_ref[...] = unit * gain + vec_ref[5:6, :]
    gradient = grad_ref[...]
    dz = norm_pull(gradient, unit, inverse, gain)
    dz_ref[...] = dz
    low_ref[...] = dz.astype(jnp.bfloat16)
    add_rows(sums_ref, (gradient * unit, gradient, dz))


def hidden_back_kernel(shards, *refs):
    low_ref, slope_ref, whole_ref, dpre_ref, bias_sums_ref = refs
    width = whole_ref.shape[2]
    low = low_ref[...]
    for j in range(shards):
        span = slice(j * width, (j + 1) * width)
        dpre = product(low, whole_ref[j]) * slope_ref[:, span].astype(jnp.float32)
        dpre = dpre.astype(jnp.bfloat16)
        dpre_ref[:, span] = dpre
        total = jnp.sum(dpre.astype(jnp.float32), 0, keepdims=True)
        kept = jnp.where(pl.program_id(0) == 0, 0.0, bias_sums_ref[j : j + 1, :])
        bias_sums_ref[j : j + 1, :] = kept + total


def back_kernel(shards, *refs):
    dpre_ref, dz_ref, unit_ref, inverse_ref, vec_ref, up_ref, first_ref = refs[:7]
    dz1_ref, low1_ref, datt_ref, sums_ref = refs[7:]
    width = up_ref.shape[2]
    gradient = dz_ref[...]
    for j in range(shards):
        gradient = gradient + dot_nt(dpre_ref[:, j * width : (j + 1) * width], up_ref[j])
    unit = unit_ref[...]
    dz1 = norm_pull(gradient, unit, inverse_ref[...], vec_ref[1:2, :])
    dz1_ref[...] = dz1
    low1 = dz1.astype(jnp.bfloat16)
    low1_ref[...] = low1
    add_rows(sums_ref, (gradient * unit, gradient, dz1))
    head_width = D // shards
    for j in range(shards):
        datt_ref[:, j * head_width : (j + 1) * head_width] = product(
            low1, first_ref[j, :, 3 * head_width :]
        ).astype(jnp.bfloat16)


def attention_back_kernel(length, *refs):
    datt_ref, attended_ref, packed_ref, probs_ref, dpacked_ref, sums_ref, up_ref, grad_ref = refs
    wide = 2 * HEAD_DIM
    lower, own = pair_masks(length)
    ones = own.astype(jnp.bfloat16)
    steps = [(p, i) for p in range(ROWS // length) for i in range(HEADS // 2)]

    def pair_of(p, i, kind):
        span = slice(p * length, (p + 1) * length)
        return packed_ref[span, kind * D + i * wide : kind * D + (i + 1) * wide]

    def keep(p, i, kind, grad):
        span = slice(p * length, (p + 1) * length)
        dpacked_ref[span, kind * D + i * wide : kind * D + (i + 1) * wide] = grad.astype(
            jnp.bfloat16
        )

    for place, (p, i) in enumerate(steps):
        span = slice(p * length, (p + 1) * length)
        lanes = slice(i * wide, (i + 1) * wide)
        upstream = datt_ref[span, lanes].astype(jnp.float32) / product(probs_ref[p, i], ones)
        up_ref[place, :, :wide] = upstream.astype(jnp.bfloat16)
        up_ref[place, :, wide:] = (upstream * attended_ref[span, lanes].astype(jnp.float32)).astype(
            jnp.bfloat16
        )
    for place, (p, i) in enumerate(steps):
        centred = dot_nt(
            up_ref[place], jnp.concatenate([stacked(pair_of(p, i, 2), own), -ones], 1)
        )
        grad_ref[place] = (probs_ref[p, i].astype(jnp.float32) * centred).astype(jnp.bfloat16)
    for place, (p, i) in enumerate(steps):
        grad_scores = grad_ref[place]
        keep(
            p, i, 0,
            product(grad_scores, stacked(pair_of(p, i, 1), own)) * HEAD_DIM ** (-0.5),
        )
        both = transposed_times(grad_scores, pair_of(p, i, 0))
        keep(p, i, 1, jnp.where(lower, both[:length], both[length:]))
        both = transposed_times(probs_ref[p, i], up_ref[place, :, :wide])
        keep(p, i, 2, jnp.where(lower, both[:length], both[length:]))
    total = jnp.sum(dpacked_ref[...].astype(jnp.float32), 0, keepdims=True)
    kept = jnp.where(pl.program_id(0) == 0, 0.0, sums_ref[0:1, :])
    sums_ref[0:1, :] = kept + total


def weight_kernel(odd, count, *refs):
    lefts, refs = refs[:2] if count > 1 else refs[:1], refs[2 if count > 1 else 1 :]
    rights, (out_ref, *turned) = refs[:count], refs[count:]
    start = pl.program_id(0) == 0

    @pl.when(start)
    def _():
        for left, kept in zip(lefts, turned):
            kept[...] = left[...].T

    at = 0
    for place, right in enumerate(rights):
        half = right.shape[1] // 2
        values = right[...] if count == 1 else right[:, half:] if odd else right[:, :half]
        grad = product(turned[place == count - 1 and count > 1][...], values)
        out_ref[0, :, at : at + values.shape[1]] = grad.astype(jnp.bfloat16)
        at += values.shape[1]


def weight_halves(lefts, rights):
    halves = []
    for odd in (1, 0):
        count = len(rights)
        single = count == 1
        specs = []
        for array, width, before in rights:
            if single:
                specs.append(pl.BlockSpec((array.shape[0], width), lambda i: (0, 2 * i + odd)))
            else:
                specs.append(
                    pl.BlockSpec((array.shape[0], 2 * width), lambda i, b=before: (0, b + i))
                )
        arrays = [*lefts, *[array for array, _, _ in rights]]
        tokens = lefts[0].shape[0]
        (half,) = pl.pallas_call(
            functools.partial(weight_kernel, odd, count),
            grid=(2,),
            in_specs=[whole_block(left) for left in lefts] + specs,
            out_specs=[pl.BlockSpec((1, D, D), lambda i: (i, 0, 0))],
            out_shape=[jax.ShapeDtypeStruct((2, D, D), jnp.bfloat16)],
            scratch_shapes=[pltpu.VMEM((D, tokens), jnp.bfloat16) for _ in lefts],
            compiler_params=pltpu.CompilerParams(vmem_limit_bytes=VMEM_LIMIT),
            cost_estimate=pl.CostEstimate(
                flops=4 * tokens * D * D,
                bytes_accessed=sum(2 * array.size for array in arrays),
                transcendentals=0,
            ),
        )(*arrays)
        halves.append(half)
    return halves


def two_terms(values):
    top = values.astype(jnp.bfloat16)
    return top, (values - top.astype(jnp.float32)).astype(jnp.bfloat16)


def adam_kernel(*refs):
    grad_ref, master_ref, left_ref, right_ref, first_ref, second_ref = refs[:6]
    master_out, first_out, second_out = refs[6:]
    bias_first = 1.0 - DECAY_FIRST**ADAM_STEP
    bias_second = 1.0 - DECAY_SECOND**ADAM_STEP
    count = grad_ref.shape[0]
    lefts = [two_terms(left_ref[k]) for k in range(count)]
    rights = [two_terms(right_ref[k]) for k in range(count)]
    turned = []
    for k in range(count):
        top, rest = two_terms(grad_ref[k].astype(jnp.float32))
        turned.append(
            product(top, rights[k][0]) + product(top, rights[k][1]) + product(rest, rights[k][0])
        )
    directions = []
    for k in range(count):
        top, rest = two_terms(turned[k])
        rotated = (
            transposed_times(lefts[k][0], top)
            + transposed_times(lefts[k][0], rest)
            + transposed_times(lefts[k][1], top)
        )
        first = DECAY_FIRST * first_ref[k] + (1.0 - DECAY_FIRST) * rotated
        second = DECAY_SECOND * second_ref[k] + (1.0 - DECAY_SECOND) * rotated * rotated
        first_out[k] = first
        second_out[k] = second
        directions.append(first / bias_first / (jnp.sqrt(second / bias_second) + ADAM_EPS))
    backs = []
    for k in range(count):
        top, rest = two_terms(directions[k])
        backs.append(
            product(lefts[k][0], top) + product(lefts[k][0], rest) + product(lefts[k][1], top)
        )
    for k in range(count):
        top, rest = two_terms(backs[k])
        update = (
            times_transposed(top, rights[k][0])
            + times_transposed(rest, rights[k][0])
            + times_transposed(top, rights[k][1])
        )
        master_out[k] = master_ref[k] - MATRIX_RATE * update


def natural_kernel(shards, *refs):
    out_ref, dz1_ref, dpacked_ref, selector_ref, whole_ref, layer_ref, input_ref = refs
    weights = [whole_ref.at[j] for j in range(shards)]
    head_width = D // shards
    gradient = dz1_ref[...]
    for j in range(shards):
        own = [
            dpacked_ref[:, kind * D + j * head_width : kind * D + (j + 1) * head_width]
            for kind in range(3)
        ]
        gradient = gradient + dot_nt(jnp.concatenate(own, 1), weights[j][:, : 3 * head_width])
    for source, ref in ((out_ref[...], layer_ref), (gradient, input_ref)):
        top = source.astype(jnp.bfloat16)
        rest = (source - top.astype(jnp.float32)).astype(jnp.bfloat16)
        ref[...] = dot_nt(top, selector_ref[...]) + dot_nt(rest, selector_ref[...])


def together(*values):
    return lax.optimization_barrier(values)


def local(
    tokens,
    segments,
    out_grad,
    owner,
    master,
    left_basis,
    right_basis,
    first_moment,
    second_moment,
    vectors,
    vector_first,
    vector_second,
):
    shards = lax.axis_size("tensor")
    dp_size = lax.axis_size("dp")
    direct = dp_size == PARTS and shards == 4
    tensor_rank = lax.axis_index("tensor")
    dp_rank = lax.axis_index("dp")
    local_heads = HEADS // shards
    head_width = local_heads * HEAD_DIM
    up_width = FF // shards
    width_qkv = 3 * head_width
    block_size = master.shape[-1]
    slots = master.shape[1]
    row_count = tokens.shape[0]
    length = segments.shape[1]
    pack_count = row_count // length
    own_segments = lax.dynamic_slice_in_dim(segments, tensor_rank * pack_count, pack_count, 0)
    qkv_tiles, out_tiles, up_tiles = tile_counts(shards, block_size)
    tile_total = owner.shape[0]

    group_base = tensor_rank if direct else 0
    order = feature_order(dp_rank if direct else 0)
    selector = (lax.iota(jnp.int32, D)[:, None] == order[None, :]).astype(jnp.bfloat16)

    rows_in = product(tokens, selector).astype(jnp.bfloat16)
    grad_out = exact_product(out_grad, selector, 2)

    group_order = lax.iota(jnp.int32, shards) ^ group_base
    d_vectors = jnp.stack(
        [
            vectors[0:D],
            vectors[D : 2 * D],
            vectors[4 * D : 5 * D],
            vectors[5 * D + FF : 6 * D + FF],
            vectors[6 * D + FF : 7 * D + FF],
            vectors[7 * D + FF : 8 * D + FF],
        ]
    )
    gain_first, gain_second, bias_out, bias_down, offset_first, offset_second = exact_product(
        d_vectors, selector, 3
    )
    bias_q = vectors[2 * D : 3 * D].reshape(shards, head_width)[group_order]
    bias_v = vectors[3 * D : 4 * D].reshape(shards, head_width)[group_order]
    bias_up = vectors[5 * D : 5 * D + FF].reshape(shards, up_width)[group_order]

    d_rows = jnp.stack(
        [bias_out, gain_first, offset_first, bias_down, gain_second, offset_second]
        + [jnp.zeros_like(bias_out)] * 2
    )

    def flipped(index):
        from_out = (index >= qkv_tiles) & (index < qkv_tiles + out_tiles)
        return (from_out | (index >= qkv_tiles + out_tiles + up_tiles))[:, None, None]

    own_tiles = lax.dynamic_slice_in_dim(owner, dp_rank * slots, slots, 0)
    own_flip = flipped(own_tiles)
    sent = master[0].astype(jnp.bfloat16)
    sent = jnp.where(own_flip, jnp.swapaxes(sent, 1, 2), sent)
    placing = (lax.iota(jnp.int32, tile_total)[:, None] == owner[None, :]).astype(jnp.bfloat16)
    if direct:
        parts = sent.reshape(slots, PARTS, SUB * block_size).swapaxes(0, 1)
        parts = lax.all_to_all(parts, "dp", 0, 0, tiled=True).reshape(tile_total, -1)
        tiles = product(placing, parts).astype(jnp.bfloat16)
        slab = slabs_from_tiles(tiles.reshape(tile_total, 1, SUB, block_size), shards, block_size)[0]
        half = D // 2
        up_left, up_right = slab[:, D : D + half], slab[:, D + half : 2 * D]
        first_z = over_z(slab[:, :D])
        up_near = jnp.concatenate(
            [
                slab[:, D : 2 * D],
                jnp.concatenate([swap_over(up_left, 0, 2), swap_over(up_right, 1, 0)], 1),
            ],
            0,
        )
        first_z, up_near, rows_in, grad_out, d_rows = together(
            first_z, up_near, rows_in, grad_out, d_rows
        )
        left, right = first_z[:, :half], first_z[:, half:]
        left = jnp.concatenate([left, swap_over(left, 0, 2)], 0)
        right = jnp.concatenate([right, swap_over(right, 1, 0)], 0)
        up_near = over_z(up_near)
        first = over_core(
            list(together(left, swap_over(left, 1, 0), right, swap_over(right, 0, 2)))
        )
        *first, up_near = together(*first, up_near)
        up = [up_near, swap_over(up_near[:, :half], 1, 0), swap_over(up_near[:, half:], 0, 2)]
        down_z = over_z(together(slab[:, 2 * D :], up_near)[0])
        places = (place_first, place_edges, place_plane)
        pieces = [first, None, None]
    else:
        gathered = lax.all_gather(sent, "dp", axis=0, tiled=True).reshape(tile_total, -1)
        tiles = product(placing, gathered).astype(jnp.bfloat16)
        slabs = slabs_from_tiles(
            tiles.reshape(tile_total, PARTS, SUB, block_size), shards, block_size
        )
        whole = jnp.concatenate([slabs[part_of_block(k)] for k in range(PARTS)], 0)
        every = lax.all_gather(whole, "tensor", axis=0)
        pieces = [
            [every[j][:, k * D : (k + 1) * D] for j in range(shards)] for k in range(3)
        ]
        places = (place_groups,) * 3

    steps = row_count // ROWS
    packs_step = ROWS // length
    bias_qkv = jnp.concatenate([bias_q, jnp.zeros_like(bias_q), bias_v], 1)
    rows_spec = lambda width: pl.BlockSpec((ROWS, width), lambda i: (i, 0))
    pairs = HEADS // 2
    probs_spec = pl.BlockSpec((packs_step, pairs, length, 2 * length), lambda i: (i, 0, 0, 0))
    sums_spec = lambda width: pl.BlockSpec((8, width), lambda i: (0, 0))
    f32, bf16 = jnp.float32, jnp.bfloat16
    full = lambda array: (array, whole_block(array))
    by_rows = lambda array: (array, row_block(array))
    square = 2 * row_count * D * D

    whole_spec = pl.BlockSpec((shards, D, D), lambda i: (0, 0, 0))
    whole_out = ((shards, D, D), bf16, whole_spec)
    packed, probs, attended, unit_first, inverse_first, normed_low, whole_first = call_rows(
        functools.partial(attention_kernel, places[0], shards, local_heads, length),
        steps,
        [
            by_rows(rows_in),
            (own_segments[:, None, :], pl.BlockSpec((packs_step, 1, length), lambda i: (i, 0, 0))),
            (own_segments[:, :, None], pl.BlockSpec((packs_step, length, 1), lambda i: (i, 0, 0))),
            full(bias_qkv),
            full(d_rows),
            *[full(w) for w in pieces[0]],
        ],
        [
            ((row_count, 3 * D), bf16, rows_spec(3 * D)),
            ((pack_count, pairs, length, 2 * length), bf16, probs_spec),
            ((row_count, D), bf16, rows_spec(D)),
            ((row_count, D), f32, rows_spec(D)),
            ((row_count, 1), f32, rows_spec(1)),
            ((row_count, D), bf16, rows_spec(D)),
            whole_out,
        ],
        4 * square + 4 * row_count * length * D,
        row_count * length * HEADS,
        [pltpu.VMEM((packs_step * pairs, length, 2 * length), f32)],
    )
    if direct:
        *up, down_z, normed_low = together(*up, down_z, normed_low)
        down = [down_z, swap_over(down_z, 1, 0), swap_over(down_z, 0, 2), swap_over(down_z, 1, 2)]
        pieces[1] = over_core(up)
    activated, slope, whole_up = call_rows(
        functools.partial(up_kernel, places[1], shards),
        steps,
        [by_rows(normed_low), full(bias_up), *[full(w) for w in pieces[1]]],
        [
            ((row_count, FF), bf16, rows_spec(FF)),
            ((row_count, FF), bf16, rows_spec(FF)),
            whole_out,
        ],
        4 * square,
        2 * row_count * FF,
    )
    if direct:
        *down, activated = together(*down, activated)
        pieces[2] = over_core(down)
    layer_out, grad_second, second_low, sums_second, whole_down = call_rows(
        functools.partial(down_kernel, places[2], shards),
        steps,
        [
            by_rows(activated),
            by_rows(unit_first),
            by_rows(grad_out),
            full(d_rows),
            *[full(w) for w in pieces[2]],
        ],
        [
            ((row_count, D), f32, rows_spec(D)),
            ((row_count, D), f32, rows_spec(D)),
            ((row_count, D), bf16, rows_spec(D)),
            ((8, D), f32, sums_spec(D)),
            whole_out,
        ],
        4 * square,
    )
    grad_w_down = weight_halves([second_low], [(activated, up_width, 0)])
    if direct:
        down_low = reduce_core(grad_w_down)
        second_low, *down_low = together(second_low, *down_low)
        down_plane = reduce_plane(down_low)
    grad_pre, grad_bias_up = call_rows(
        functools.partial(hidden_back_kernel, shards),
        steps,
        [by_rows(second_low), by_rows(slope), full(whole_down)],
        [((row_count, FF), bf16, rows_spec(FF)), ((8, up_width), f32, sums_spec(up_width))],
        4 * square,
    )
    grad_bias_up = grad_bias_up[:shards]
    grad_w_up = weight_halves([normed_low], [(grad_pre, up_width, 0)])
    grad_first, first_low, grad_attended, sums_first = call_rows(
        functools.partial(back_kernel, shards),
        steps,
        [
            by_rows(grad_pre),
            by_rows(grad_second),
            by_rows(unit_first),
            by_rows(inverse_first),
            full(d_rows),
            full(whole_up),
            full(whole_first),
        ],
        [
            ((row_count, D), f32, rows_spec(D)),
            ((row_count, D), bf16, rows_spec(D)),
            ((row_count, D), bf16, rows_spec(D)),
            ((8, D), f32, sums_spec(D)),
        ],
        5 * square,
    )
    if direct:
        up_low = reduce_core(grad_w_up)
        grad_attended, *up_low, down_plane = together(grad_attended, *up_low, down_plane)
        up_edges = reduce_edges(up_low)
        down_own = reduce_z(down_plane)
    grad_packed, column_sums = call_rows(
        functools.partial(attention_back_kernel, length),
        steps,
        [by_rows(grad_attended), by_rows(attended), by_rows(packed), (probs, probs_spec)],
        [
            ((row_count, 3 * D), bf16, rows_spec(3 * D)),
            ((8, 3 * D), f32, sums_spec(3 * D)),
        ],
        8 * square,
        0,
        [pltpu.VMEM((packs_step * pairs, length, 2 * length), bf16)] * 2,
    )
    column_sums = column_sums[0].reshape(3, shards, head_width)
    grad_w_first = weight_halves(
        [rows_in, first_low],
        [(grad_packed, head_width, k * shards // 2) for k in range(3)] + [(attended, head_width, 0)],
    )
    if direct:
        grad_odd, grad_even, up_edges, down_own, *others = together(
            *grad_w_first, up_edges, down_own, sums_first, sums_second, grad_bias_up, column_sums
        )
        sums_first, sums_second, grad_bias_up, column_sums = others
        first_low = reduce_core((grad_odd, grad_even))
        *first_low, layer_out = together(*first_low, layer_out)
        first_edges = reduce_edges(first_low)
        up_edges = reduce_edges_z(up_edges)
    layer_out, input_grad = call_rows(
        functools.partial(natural_kernel, shards),
        steps,
        [
            by_rows(layer_out),
            by_rows(grad_first),
            by_rows(grad_packed),
            full(selector),
            full(whole_first),
        ],
        [((row_count, D), f32, rows_spec(D)), ((row_count, D), f32, rows_spec(D))],
        7 * square,
    )

    if direct:
        first_plane = reduce_edges_plane(first_edges).astype(bf16)
        first_plane, up_edges, layer_out, input_grad = together(
            first_plane, up_edges, layer_out, input_grad
        )
        first_own = reduce_z(first_plane)
        up_own = reduce_edges_plane(up_edges)
        slab_grad = jnp.concatenate([first_own, up_own, down_own], 1).astype(jnp.bfloat16)
        tile_grad = tiles_from_slabs(slab_grad[None], shards, block_size).reshape(tile_total, -1)
        slot_grad = transposed_times(placing, tile_grad).astype(jnp.bfloat16)
        slot_grad = lax.all_to_all(
            slot_grad.reshape(PARTS, slots, SUB * block_size), "dp", 0, 0, tiled=True
        )
        owned_grads = slot_grad.swapaxes(0, 1).reshape(slots, block_size, block_size)
    else:
        every = jnp.stack(
            [
                jnp.concatenate(
                    [half[1 - j % 2][j // 2] for half in (grad_w_first, grad_w_up, grad_w_down)], 1
                )
                for j in range(shards)
            ]
        ).astype(jnp.float32)
        mine = lax.psum_scatter(every, "tensor", scatter_dimension=0, tiled=True)[0]
        blocks = mine.reshape(PARTS, D // PARTS, -1)
        blocks = jnp.stack([blocks[(p % 2) * 4 + p // 2] for p in range(PARTS)])
        tile_grad = tiles_from_slabs(blocks, shards, block_size)
        slot_grad = tile_grad.reshape(tile_total, block_size, block_size)[owner]
        owned_grads = lax.psum_scatter(slot_grad, "dp", scatter_dimension=0, tiled=True)
    owned_grads = jnp.where(own_flip, jnp.swapaxes(owned_grads, 1, 2), owned_grads)

    grad_gain_second, grad_offset_second, grad_bias_down = (sums_second[k] for k in range(3))
    grad_gain_first, grad_offset_first, grad_bias_out = (sums_first[k] for k in range(3))
    d_grads = exact_product_t(
        jnp.stack(
            [
                grad_gain_first,
                grad_gain_second,
                grad_bias_out,
                grad_bias_down,
                grad_offset_first,
                grad_offset_second,
            ]
        ),
        selector,
        3,
    )
    grad_vector = jnp.concatenate(
        [
            d_grads[0],
            d_grads[1],
            column_sums[0][group_order].reshape(-1),
            column_sums[2][group_order].reshape(-1),
            d_grads[2],
            grad_bias_up[group_order].reshape(-1),
            d_grads[3],
            d_grads[4],
            d_grads[5],
        ]
    )
    vector_grad = sum_over_all(grad_vector) if direct else lax.psum(grad_vector, ("dp", "tensor"))


    bias_first = 1.0 - DECAY_FIRST**ADAM_STEP
    bias_second = 1.0 - DECAY_SECOND**ADAM_STEP
    step_slots = max(k for k in (1, 2, 3, 4, 6) if slots % k == 0)
    slots_spec = pl.BlockSpec((step_slots, block_size, block_size), lambda i: (i, 0, 0))
    slot_out = ((slots, block_size, block_size), f32, slots_spec)
    new_master, new_first, new_second = call_rows(
        adam_kernel,
        slots // step_slots,
        [
            (array, slots_spec)
            for array in (
                owned_grads,
                master[0],
                left_basis[0],
                right_basis[0],
                first_moment[0],
                second_moment[0],
            )
        ],
        [slot_out] * 3,
        22 * slots * block_size**3,
        slots * block_size**2,
    )
    new_vector_first = DECAY_FIRST * vector_first + (1.0 - DECAY_FIRST) * vector_grad
    new_vector_second = (
        DECAY_SECOND * vector_second + (1.0 - DECAY_SECOND) * vector_grad * vector_grad
    )
    new_vectors = vectors - VECTOR_RATE * (new_vector_first / bias_first) / (
        jnp.sqrt(new_vector_second / bias_second) + ADAM_EPS
    )
    return (
        layer_out,
        input_grad,
        new_master[None],
        new_first[None],
        new_second[None],
        new_vectors,
        new_vector_first,
        new_vector_second,
    )


def solution(mesh):
    return jax.shard_map(
        local,
        mesh=mesh,
        in_specs=(
            P(("dp", "tensor"), None),
            P("dp", None),
            P(("dp", "tensor"), None),
            P(),
            P("tensor", "dp", None, None),
            P("tensor", "dp", None, None),
            P("tensor", "dp", None, None),
            P("tensor", "dp", None, None),
            P("tensor", "dp", None, None),
            P(),
            P(),
            P(),
        ),
        out_specs=(
            P(("dp", "tensor"), None),
            P(("dp", "tensor"), None),
            P("tensor", "dp", None, None),
            P("tensor", "dp", None, None),
            P("tensor", "dp", None, None),
            P(),
            P(),
            P(),
        ),
        check_vma=False,
    )
```

```python
import functools
import math

import jax
import jax.numpy as jnp
from jax import lax
from jax.experimental import pallas as pl
from jax.experimental.pallas import tpu as pltpu
from jax.sharding import PartitionSpec as P

HEADS = 12
HEAD_DIM = 64
D = 768
FF = 3072
ADAM_STEP = 3


NORM_EPS = 1e-12
ADAM_EPS = 1e-08
MATRIX_RATE = 0.01
VECTOR_RATE = 0.1
DECAY_FIRST = 0.5
DECAY_SECOND = 0.5
MASKED = -1e30


def product(left_side, right_side):
    return jnp.dot(left_side, right_side, preferred_element_type=jnp.float32)


def times_transposed(left_side, right_side):
    return lax.dot_general(
        left_side, right_side, (((1,), (1,)), ((), ())), preferred_element_type=jnp.float32
    )


def transposed_times(left_side, right_side):
    return lax.dot_general(
        left_side, right_side, (((0,), (0,)), ((), ())), preferred_element_type=jnp.float32
    )


VMEM_LIMIT = 20 * 1024 * 1024

PARTS = 8
SUB = 12


def rounded(values):
    return lax.reduce_precision(values, 8, 7)


def split_terms(values, count):
    terms = []
    for _ in range(count):
        top = rounded(values)
        terms.append(top.astype(jnp.bfloat16))
        values = values - top
    return terms


def exact_product(values, selector, count):
    return sum(product(term, selector) for term in split_terms(values, count))


def exact_product_t(values, selector, count):
    return sum(times_transposed(term, selector) for term in split_terms(values, count))


def part_of_block(block):
    return (block % 4) * 2 + block // 4


def feature_order(rank):
    place = lax.iota(jnp.int32, D)
    part = part_of_block(place // (D // PARTS)) ^ rank
    inner = place % (D // PARTS)
    return (inner // SUB) * (PARTS * SUB) + part * SUB + inner % SUB


def tile_counts(shards, block_size):
    rows = D // block_size
    qkv = rows * (3 * D // shards // block_size)
    out = rows * (D // shards // block_size)
    up = rows * (FF // shards // block_size)
    return (qkv, out, up)


def slabs_from_tiles(tiles, shards, block_size):
    cut = tiles.shape[1]
    qkv, out, up = tile_counts(shards, block_size)
    rows = D // block_size

    def by_rows(part):
        cols = part.shape[0] // rows
        part = part.reshape(rows, cols, cut, SUB, block_size)
        return part.transpose(2, 0, 3, 1, 4).reshape(cut, rows * SUB, cols * block_size)

    def by_cols(part):
        cols = part.shape[0] // rows
        part = part.reshape(cols, rows, cut, SUB, block_size)
        return part.transpose(2, 1, 3, 0, 4).reshape(cut, rows * SUB, cols * block_size)

    return jnp.concatenate(
        [
            by_rows(tiles[:qkv]),
            by_cols(tiles[qkv : qkv + out]),
            by_rows(tiles[qkv + out : qkv + out + up]),
            by_cols(tiles[qkv + out + up :]),
        ],
        2,
    )


def tiles_from_slabs(slabs, shards, block_size):
    cut = slabs.shape[0]
    rows = D // block_size
    width_qkv, width_out, width_up = 3 * D // shards, D // shards, FF // shards

    def by_rows(part):
        cols = part.shape[2] // block_size
        part = part.reshape(cut, rows, SUB, cols, block_size)
        return part.transpose(1, 3, 0, 2, 4).reshape(rows * cols, cut, SUB, block_size)

    def by_cols(part):
        cols = part.shape[2] // block_size
        part = part.reshape(cut, rows, SUB, cols, block_size)
        return part.transpose(3, 1, 0, 2, 4).reshape(rows * cols, cut, SUB, block_size)

    first = width_qkv + width_out
    second = first + width_up
    return jnp.concatenate(
        [
            by_rows(slabs[:, :, :width_qkv]),
            by_cols(slabs[:, :, width_qkv:first]),
            by_rows(slabs[:, :, first:second]),
            by_cols(slabs[:, :, second:]),
        ],
        0,
    )


def swap_over(values, over_dp, over_tensor):
    dp, tensor = lax.axis_size("dp"), lax.axis_size("tensor")
    pairs = [
        (a * tensor + b, (a ^ over_dp) * tensor + (b ^ over_tensor))
        for a in range(dp)
        for b in range(tensor)
    ]
    return lax.ppermute(values, ("dp", "tensor"), pairs)


def merge(terms, outs, segments):
    chunk = D // PARTS

    def kernel(*refs):
        for out, row, col, rows, cols, parts in segments:

            def step(k, carry, out=out, row=row, col=col, cols=cols, parts=parts):
                pieces = [
                    refs[term][pl.ds(pl.multiple_of(at + k * chunk, 32), chunk), left : left + cols]
                    for term, at, left in parts
                ]
                if len(pieces) > 1:
                    value = sum(piece.astype(jnp.float32) for piece in pieces)
                else:
                    value = pieces[0]
                to = refs[len(terms) + out]
                to[pl.ds(pl.multiple_of(row + k * chunk, 32), chunk), col : col + cols] = (
                    value.astype(to.dtype)
                )
                return carry

            lax.fori_loop(0, rows // chunk, step, 0)

    spec = pl.BlockSpec(memory_space=pltpu.VMEM)
    size = sum(term.size for term in terms)
    return pl.pallas_call(
        kernel,
        in_specs=[spec] * len(terms),
        out_specs=[spec] * len(outs),
        out_shape=[jax.ShapeDtypeStruct((rows, cols), dtype) for rows, cols, dtype in outs],
        compiler_params=pltpu.CompilerParams(vmem_limit_bytes=VMEM_LIMIT),
        cost_estimate=pl.CostEstimate(flops=size, bytes_accessed=4 * size, transcendentals=0),
    )(*terms)


def from_z(block):
    return [swap_over(block, 2 * k, 0) for k in (1, 2, 3)]


def over_core(blocks):
    return blocks + [swap_over(block, 0, 1) for block in blocks]


def place_first(refs, out_ref):
    count = len(refs) // 2
    half, cols = D // 2, D // 2
    for core in range(2):
        near, beside, right, across = refs[core * count : (core + 1) * count]
        for y in range(2):
            group = 2 * y + core
            out_ref[group, :half, :cols] = near[y * half : (y + 1) * half, :]
            out_ref[group, half:, :cols] = beside[y * half : (y + 1) * half, :]
            out_ref[group, :, cols:] = (right, across)[y][...]


def place_edges(refs, out_ref):
    count = len(refs) // 2
    rows, half, cols = D // PARTS, D // 2, D // 2
    for core in range(2):
        near, beside, across = refs[core * count : (core + 1) * count]
        for y in range(2):
            for z in range(4):
                for x in range(2):
                    to = x * half + z * rows
                    by_y, by_x = (2 * z + y) * rows, (2 * z + x) * rows
                    left = beside[by_y : by_y + rows, :] if x else near[by_y : by_y + rows, :cols]
                    right = across[by_x : by_x + rows, :] if y else near[by_x : by_x + rows, cols:]
                    out_ref[2 * y + core, to : to + rows, :cols] = left
                    out_ref[2 * y + core, to : to + rows, cols:] = right


def place_plane(refs, out_ref):
    half = D // 2
    for core in range(2):
        for y in range(2):
            for x in range(2):
                out_ref[2 * y + core, x * half : (x + 1) * half, :] = refs[4 * core + 2 * y + x][...]


def place_groups(refs, out_ref):
    for group, ref in enumerate(refs):
        out_ref[group] = ref[...]


def core_terms(halves):
    odd, even = halves
    return [even.reshape(2 * D, D), swap_over(odd, 0, 1).reshape(2 * D, D)]


def summed(count, row, col):
    return [(term, row, col) for term in range(count)]


def reduce_core_plane(halves):
    half = D // 2
    return merge(
        core_terms(halves),
        [(half, D, jnp.bfloat16)] * 4,
        [(k, 0, 0, half, D, summed(2, k * half, 0)) for k in range(4)],
    )


def reduce_plane(near, beside, across, opposite):
    rows = D // PARTS
    terms = [near, swap_over(beside, 1, 0), swap_over(across, 0, 2), swap_over(opposite, 1, 2)]
    return merge(
        terms,
        [(rows, D, jnp.bfloat16)] * 4,
        [(k, 0, 0, rows, D, summed(4, k * rows, 0)) for k in range(4)],
    )


def reduce_z(own, *sent):
    rows = D // PARTS
    terms = [own] + [swap_over(block, 2 * (k + 1), 0) for k, block in enumerate(sent)]
    return merge(terms, [(rows, D, jnp.float32)], [(0, 0, 0, rows, D, summed(4, 0, 0))])[0]


def reduce_core_edges(halves):
    half = D // 2
    return merge(
        core_terms(halves),
        [(D, D, jnp.bfloat16), (D, half, jnp.bfloat16), (D, half, jnp.bfloat16)],
        [
            (0, 0, 0, half, half, summed(2, 0, 0)),
            (0, half, 0, half, half, summed(2, D, 0)),
            (0, 0, half, D, half, summed(2, 0, half)),
            (1, 0, 0, half, half, summed(2, half, 0)),
            (1, half, 0, half, half, summed(2, D + half, 0)),
            (2, 0, 0, D, half, summed(2, D, half)),
        ],
    )


def edge_terms(near, left, right):
    return [near, swap_over(left, 1, 0), swap_over(right, 0, 2)]


def edge_sums(row):
    half = D // 2
    return ((0, [(0, row, 0), (1, row, 0)]), (half, [(0, row, half), (2, row, 0)]))


def reduce_edges_plane(near, left, right):
    half = D // 2
    kept = [(0, 0, col, half, half, parts) for col, parts in edge_sums(0)]
    sent = [
        (1 + k, 0, 0, half, half, parts) for k, (_, parts) in enumerate(edge_sums(half))
    ]
    return merge(
        edge_terms(near, left, right),
        [(half, D, jnp.bfloat16), (half, half, jnp.bfloat16), (half, half, jnp.bfloat16)],
        kept + sent,
    )


def reduce_plane_edges(near, left, right):
    rows, half = D // PARTS, D // 2
    return merge(
        [near, swap_over(left, 0, 2), swap_over(right, 1, 0)],
        [(rows, D, jnp.bfloat16)] * 4,
        [
            (k, 0, col, rows, half, parts)
            for k in range(4)
            for col, parts in edge_sums(k * rows)
        ],
    )


def reduce_edges(near, left, right):
    rows, half = D // PARTS, D // 2
    return merge(
        edge_terms(near, left, right),
        [(2 * rows, D, jnp.bfloat16)] * 4,
        [
            (k, q * rows, col, rows, half, parts)
            for k in range(4)
            for q in range(2)
            for col, parts in edge_sums(q * half + k * rows)
        ],
    )


def reduce_edges_z(own, *sent):
    rows, half = D // PARTS, D // 2
    terms = [own] + [swap_over(block, 2 * (k + 1), 0) for k, block in enumerate(sent)]
    return merge(
        terms,
        [(rows, D, jnp.bfloat16), (rows, half, jnp.bfloat16), (rows, half, jnp.bfloat16)],
        [
            (0, 0, 0, rows, D, summed(4, 0, 0)),
            (1, 0, 0, rows, half, summed(4, rows, 0)),
            (2, 0, 0, rows, half, summed(4, rows, half)),
        ],
    )


def reduce_edges_last(near, left, right):
    rows, half = D // PARTS, D // 2
    return merge(
        [near, swap_over(left, 0, 2), swap_over(right, 1, 0)],
        [(rows, D, jnp.float32)],
        [(0, 0, col, rows, half, parts) for col, parts in edge_sums(0)],
    )[0]


def sum_over_all(values):
    return jnp.sum(lax.all_gather(values[None], ("dp", "tensor"), axis=0, tiled=True), 0)


ROWS = 256


def dot_nt(left_side, right_side):
    return lax.dot_general(
        left_side, right_side, (((1,), (1,)), ((), ())), preferred_element_type=jnp.float32
    )


def row_block(array):
    return pl.BlockSpec((ROWS, array.shape[1]), lambda i: (i, 0))


def call_rows(kernel, steps, inputs, outputs, flops, transcendentals=0, scratch=()):
    arrays = [
        pltpu.with_memory_space_constraint(array, pltpu.HBM) if far else array
        for array, _, *far in inputs
    ]
    shapes = [jax.ShapeDtypeStruct(shape, dtype) for shape, dtype, *_ in outputs]
    moved = sum(a.size * a.dtype.itemsize for a in arrays + shapes)
    shapes = [
        pltpu.HBM(shape.shape, shape.dtype) if len(output) > 3 else shape
        for shape, output in zip(shapes, outputs)
    ]
    return pl.pallas_call(
        kernel,
        grid=(steps,),
        in_specs=[spec for _, spec, *_ in inputs],
        out_specs=[output[2] for output in outputs],
        out_shape=shapes,
        scratch_shapes=scratch,
        compiler_params=pltpu.CompilerParams(vmem_limit_bytes=VMEM_LIMIT),
        cost_estimate=pl.CostEstimate(
            flops=int(1.0 * flops), bytes_accessed=moved, transcendentals=transcendentals
        ),
    )(*arrays)


def norm_rows(summed):
    centred = summed - jnp.mean(summed, -1, keepdims=True)
    inverse = lax.rsqrt(jnp.mean(centred * centred, -1, keepdims=True) + NORM_EPS)
    return centred * inverse, inverse


def norm_pull(gradient, unit_rows, inverse, gain_row):
    scaled = gradient * gain_row
    return inverse * (
        scaled
        - jnp.mean(scaled, -1, keepdims=True)
        - unit_rows * jnp.mean(scaled * unit_rows, -1, keepdims=True)
    )


def add_rows(ref, rows):
    sums = [jnp.sum(row, 0, keepdims=True) for row in rows]
    start = pl.program_id(0) == 0
    for place, total in enumerate(sums):
        kept = jnp.where(start, 0.0, ref[place : place + 1, :])
        ref[place : place + 1, :] = kept + total


def settle(place, refs, whole_ref, shards):
    @pl.when(pl.program_id(0) == 0)
    def _():
        place(refs, whole_ref)

    return [whole_ref.at[j] for j in range(shards)]


def pair_masks(length):
    wide = 2 * HEAD_DIM
    lower = lax.broadcasted_iota(jnp.int32, (length, wide), 1) < HEAD_DIM
    top = lax.broadcasted_iota(jnp.int32, (2 * length, wide), 0) < length
    left = lax.broadcasted_iota(jnp.int32, (2 * length, wide), 1) < HEAD_DIM
    return lower, top == left


def stacked(pair, own):
    return jnp.where(own, jnp.concatenate([pair, pair], 0), jnp.zeros((), pair.dtype))


def attention_kernel(place, shards, local_heads, length, *refs):
    rows_ref, across_ref, down_ref, bias_ref, vec_ref = refs[:5]
    packed_ref, probs_ref, attended_ref, unit_ref, inverse_ref, low_ref, whole_ref, scores_ref = (
        refs[-8:]
    )
    weights = settle(place, refs[5:-8], whole_ref, shards)
    head_width = local_heads * HEAD_DIM
    width = 3 * head_width
    wide = 2 * HEAD_DIM
    pairs = HEADS // 2
    rows = rows_ref[...]
    for j in range(shards):
        packed = product(rows, weights[j][:, :width]) + bias_ref[j : j + 1, :]
        for kind in range(3):
            part = packed[:, kind * head_width : (kind + 1) * head_width].astype(jnp.bfloat16)
            if kind == 0:
                part = part * jnp.bfloat16(HEAD_DIM ** (-0.5))
            start = kind * D + j * head_width
            packed_ref[:, start : start + head_width] = part
    _, own = pair_masks(length)
    ones = own.astype(jnp.bfloat16)
    steps = [(p, i) for p in range(ROWS // length) for i in range(pairs)]

    def pair_of(p, i, kind):
        span = slice(p * length, (p + 1) * length)
        return packed_ref[span, kind * D + i * wide : kind * D + (i + 1) * wide]

    for at, (p, i) in enumerate(steps):
        scores_ref[at] = dot_nt(pair_of(p, i, 0), stacked(pair_of(p, i, 1), own))
    for at, (p, i) in enumerate(steps):
        allowed = down_ref[p] == across_ref[p]
        for half in range(2):
            lanes = slice(half * length, (half + 1) * length)
            scores = jnp.where(allowed, scores_ref[at, :, lanes], MASKED)
            probs_ref[p, i, :, lanes] = jnp.exp(
                scores - jnp.max(scores, -1, keepdims=True)
            ).astype(jnp.bfloat16)
    for p, i in steps:
        mixed = product(
            probs_ref[p, i], jnp.concatenate([stacked(pair_of(p, i, 2), own), ones], 1)
        )
        attended_ref[p * length : (p + 1) * length, i * wide : (i + 1) * wide] = (
            mixed[:, :wide] / mixed[:, wide:]
        ).astype(jnp.bfloat16)
    summed = rows.astype(jnp.float32) + vec_ref[0:1, :]
    for j in range(shards):
        summed = summed + dot_nt(
            attended_ref[:, j * head_width : (j + 1) * head_width], weights[j][:, width:]
        )
    unit, inverse = norm_rows(summed)
    unit_ref[...] = unit
    inverse_ref[...] = inverse
    low_ref[...] = (unit * vec_ref[1:2, :] + vec_ref[2:3, :]).astype(jnp.bfloat16)


def normal_cdf(values):
    decay = jnp.exp(values * values * -0.5)
    t = 1.0 / (1.0 + jnp.abs(values) * (0.3275911 * 0.5**0.5))
    poly = t * (
        0.127414796
        + t * (-0.142248368 + t * (0.7107068705 + t * (-0.7265760135 + t * 0.5307027145)))
    )
    upper = poly * decay
    return jnp.where(values > 0, 1.0 - upper, upper), decay


def up_kernel(place, shards, *refs):
    low_ref, bias_ref = refs[:2]
    act_ref, slope_ref, whole_ref = refs[-3:]
    weights = settle(place, refs[2:-3], whole_ref, shards)
    width = weights[0].shape[1]
    chunk = 256
    low = low_ref[...]
    for j in range(shards):
        for c in range(0, width, chunk):
            pre = product(low, weights[j][:, c : c + chunk]) + bias_ref[j : j + 1, c : c + chunk]
            below, decay = normal_cdf(pre)
            at = j * width + c
            act_ref[:, at : at + chunk] = (pre * below).astype(jnp.bfloat16)
            slope_ref[:, at : at + chunk] = (
                below + pre * decay * (0.5 / math.pi) ** 0.5
            ).astype(jnp.bfloat16)


def down_kernel(place, shards, *refs):
    act_ref, unit_ref, grad_ref, vec_ref = refs[:4]
    out_ref, dz_ref, low_ref, sums_ref, whole_ref = refs[-5:]
    weights = settle(place, refs[4:-5], whole_ref, shards)
    width = weights[0].shape[1]
    summed = unit_ref[...] * vec_ref[1:2, :] + vec_ref[2:3, :] + vec_ref[3:4, :]
    for j in range(shards):
        summed = summed + dot_nt(act_ref[:, j * width : (j + 1) * width], weights[j][...])
    unit, inverse = norm_rows(summed)
    gain = vec_ref[4:5, :]
    out_ref[...] = unit * gain + vec_ref[5:6, :]
    gradient = grad_ref[...]
    dz = norm_pull(gradient, unit, inverse, gain)
    dz_ref[...] = dz
    low_ref[...] = dz.astype(jnp.bfloat16)
    add_rows(sums_ref, (gradient * unit, gradient, dz))


def hidden_back_kernel(shards, *refs):
    low_ref, slope_ref, whole_ref, dpre_ref, bias_sums_ref = refs
    width = whole_ref.shape[2]
    low = low_ref[...]
    for j in range(shards):
        span = slice(j * width, (j + 1) * width)
        dpre = product(low, whole_ref[j]) * slope_ref[:, span].astype(jnp.float32)
        dpre = dpre.astype(jnp.bfloat16)
        dpre_ref[:, span] = dpre
        total = jnp.sum(dpre.astype(jnp.float32), 0, keepdims=True)
        kept = jnp.where(pl.program_id(0) == 0, 0.0, bias_sums_ref[j : j + 1, :])
        bias_sums_ref[j : j + 1, :] = kept + total


def back_kernel(shards, *refs):
    dpre_ref, dz_ref, unit_ref, inverse_ref, vec_ref, up_ref, first_ref = refs[:7]
    dz1_ref, low1_ref, datt_ref, sums_ref = refs[7:]
    width = up_ref.shape[2]
    gradient = dz_ref[...]
    for j in range(shards):
        gradient = gradient + dot_nt(dpre_ref[:, j * width : (j + 1) * width], up_ref[j])
    unit = unit_ref[...]
    dz1 = norm_pull(gradient, unit, inverse_ref[...], vec_ref[1:2, :])
    dz1_ref[...] = dz1
    low1 = dz1.astype(jnp.bfloat16)
    low1_ref[...] = low1
    add_rows(sums_ref, (gradient * unit, gradient, dz1))
    head_width = D // shards
    for j in range(shards):
        datt_ref[:, j * head_width : (j + 1) * head_width] = product(
            low1, first_ref[j, :, 3 * head_width :]
        ).astype(jnp.bfloat16)


def attention_back_kernel(length, *refs):
    datt_ref, attended_ref, packed_ref, probs_ref, dpacked_ref, sums_ref, up_ref, grad_ref = refs
    wide = 2 * HEAD_DIM
    lower, own = pair_masks(length)
    ones = own.astype(jnp.bfloat16)
    steps = [(p, i) for p in range(ROWS // length) for i in range(HEADS // 2)]

    def pair_of(p, i, kind):
        span = slice(p * length, (p + 1) * length)
        return packed_ref[span, kind * D + i * wide : kind * D + (i + 1) * wide]

    def keep(p, i, kind, grad):
        span = slice(p * length, (p + 1) * length)
        dpacked_ref[span, kind * D + i * wide : kind * D + (i + 1) * wide] = grad.astype(
            jnp.bfloat16
        )

    for place, (p, i) in enumerate(steps):
        span = slice(p * length, (p + 1) * length)
        lanes = slice(i * wide, (i + 1) * wide)
        upstream = datt_ref[span, lanes].astype(jnp.float32) / product(probs_ref[p, i], ones)
        up_ref[place, :, :wide] = upstream.astype(jnp.bfloat16)
        up_ref[place, :, wide:] = (upstream * attended_ref[span, lanes].astype(jnp.float32)).astype(
            jnp.bfloat16
        )
    for place, (p, i) in enumerate(steps):
        centred = dot_nt(
            up_ref[place], jnp.concatenate([stacked(pair_of(p, i, 2), own), -ones], 1)
        )
        grad_ref[place] = (probs_ref[p, i].astype(jnp.float32) * centred).astype(jnp.bfloat16)
    for place, (p, i) in enumerate(steps):
        grad_scores = grad_ref[place]
        keep(
            p, i, 0,
            product(grad_scores, stacked(pair_of(p, i, 1), own)) * HEAD_DIM ** (-0.5),
        )
        both = transposed_times(grad_scores, pair_of(p, i, 0))
        keep(p, i, 1, jnp.where(lower, both[:length], both[length:]))
        both = transposed_times(probs_ref[p, i], up_ref[place, :, :wide])
        keep(p, i, 2, jnp.where(lower, both[:length], both[length:]))
    total = jnp.sum(dpacked_ref[...].astype(jnp.float32), 0, keepdims=True)
    kept = jnp.where(pl.program_id(0) == 0, 0.0, sums_ref[0:1, :])
    sums_ref[0:1, :] = kept + total


def weight_kernel(odd, count, *refs):
    lefts, refs = refs[:2] if count > 1 else refs[:1], refs[2 if count > 1 else 1 :]
    rights, (out_ref, *turned) = refs[:count], refs[count:]
    start = pl.program_id(0) == 0

    @pl.when(start)
    def _():
        for left, kept in zip(lefts, turned):
            kept[...] = left[...].T

    at = 0
    for place, right in enumerate(rights):
        half = right.shape[1] // 2
        values = right[...] if count == 1 else right[:, half:] if odd else right[:, :half]
        grad = product(turned[place == count - 1 and count > 1][...], values)
        out_ref[0, :, at : at + values.shape[1]] = grad.astype(jnp.bfloat16)
        at += values.shape[1]


def weight_halves(lefts, rights):
    halves = []
    for odd in (1, 0):
        count = len(rights)
        single = count == 1
        specs = []
        for array, width, before in rights:
            if single:
                specs.append(pl.BlockSpec((array.shape[0], width), lambda i: (0, 2 * i + odd)))
            else:
                specs.append(
                    pl.BlockSpec((array.shape[0], 2 * width), lambda i, b=before: (0, b + i))
                )
        arrays = [*lefts, *[array for array, _, _ in rights]]
        tokens = lefts[0].shape[0]
        (half,) = pl.pallas_call(
            functools.partial(weight_kernel, odd, count),
            grid=(2,),
            in_specs=[pl.BlockSpec(memory_space=pltpu.VMEM) for _ in lefts] + specs,
            out_specs=[pl.BlockSpec((1, D, D), lambda i: (i, 0, 0))],
            out_shape=[jax.ShapeDtypeStruct((2, D, D), jnp.bfloat16)],
            scratch_shapes=[pltpu.VMEM((D, tokens), jnp.bfloat16) for _ in lefts],
            compiler_params=pltpu.CompilerParams(vmem_limit_bytes=VMEM_LIMIT),
            cost_estimate=pl.CostEstimate(
                flops=4 * tokens * D * D,
                bytes_accessed=sum(2 * array.size for array in arrays),
                transcendentals=0,
            ),
        )(*arrays)
        halves.append(half)
    return halves


def two_terms(values):
    top = values.astype(jnp.bfloat16)
    return top, (values - top.astype(jnp.float32)).astype(jnp.bfloat16)


def adam_kernel(*refs):
    grad_ref, master_ref, left_ref, right_ref, first_ref, second_ref = refs[:6]
    master_out, first_out, second_out = refs[6:]
    bias_first = 1.0 - DECAY_FIRST**ADAM_STEP
    bias_second = 1.0 - DECAY_SECOND**ADAM_STEP
    count = grad_ref.shape[0]
    lefts = [two_terms(left_ref[k]) for k in range(count)]
    rights = [two_terms(right_ref[k]) for k in range(count)]
    turned = []
    for k in range(count):
        top, rest = two_terms(grad_ref[k].astype(jnp.float32))
        turned.append(
            product(top, rights[k][0]) + product(top, rights[k][1]) + product(rest, rights[k][0])
        )
    directions = []
    for k in range(count):
        top, rest = two_terms(turned[k])
        rotated = (
            transposed_times(lefts[k][0], top)
            + transposed_times(lefts[k][0], rest)
            + transposed_times(lefts[k][1], top)
        )
        first = DECAY_FIRST * first_ref[k] + (1.0 - DECAY_FIRST) * rotated
        second = DECAY_SECOND * second_ref[k] + (1.0 - DECAY_SECOND) * rotated * rotated
        first_out[k] = first
        second_out[k] = second
        directions.append(first / bias_first / (jnp.sqrt(second / bias_second) + ADAM_EPS))
    backs = []
    for k in range(count):
        top, rest = two_terms(directions[k])
        backs.append(
            product(lefts[k][0], top) + product(lefts[k][0], rest) + product(lefts[k][1], top)
        )
    for k in range(count):
        top, rest = two_terms(backs[k])
        update = (
            times_transposed(top, rights[k][0])
            + times_transposed(rest, rights[k][0])
            + times_transposed(top, rights[k][1])
        )
        master_out[k] = master_ref[k] - MATRIX_RATE * update


def natural_kernel(shards, *refs):
    out_ref, dz1_ref, dpacked_ref, selector_ref, whole_ref, layer_ref, input_ref = refs
    weights = [whole_ref.at[j] for j in range(shards)]
    head_width = D // shards
    gradient = dz1_ref[...]
    for j in range(shards):
        own = [
            dpacked_ref[:, kind * D + j * head_width : kind * D + (j + 1) * head_width]
            for kind in range(3)
        ]
        gradient = gradient + dot_nt(jnp.concatenate(own, 1), weights[j][:, : 3 * head_width])
    for source, ref in ((out_ref[...], layer_ref), (gradient, input_ref)):
        top = source.astype(jnp.bfloat16)
        rest = (source - top.astype(jnp.float32)).astype(jnp.bfloat16)
        ref[...] = dot_nt(top, selector_ref[...]) + dot_nt(rest, selector_ref[...])


def together(*values):
    return lax.optimization_barrier(values)


def local(
    tokens,
    segments,
    out_grad,
    owner,
    master,
    left_basis,
    right_basis,
    first_moment,
    second_moment,
    vectors,
    vector_first,
    vector_second,
):
    shards = lax.axis_size("tensor")
    dp_size = lax.axis_size("dp")
    direct = dp_size == PARTS and shards == 4
    tensor_rank = lax.axis_index("tensor")
    dp_rank = lax.axis_index("dp")
    local_heads = HEADS // shards
    head_width = local_heads * HEAD_DIM
    up_width = FF // shards
    width_qkv = 3 * head_width
    block_size = master.shape[-1]
    slots = master.shape[1]
    row_count = tokens.shape[0]
    length = segments.shape[1]
    pack_count = row_count // length
    own_segments = lax.dynamic_slice_in_dim(segments, tensor_rank * pack_count, pack_count, 0)
    qkv_tiles, out_tiles, up_tiles = tile_counts(shards, block_size)
    tile_total = owner.shape[0]

    group_base = tensor_rank if direct else 0
    order = feature_order(dp_rank if direct else 0)
    selector = (lax.iota(jnp.int32, D)[:, None] == order[None, :]).astype(jnp.bfloat16)

    rows_in = product(tokens, selector).astype(jnp.bfloat16)
    grad_out = exact_product(out_grad, selector, 2)

    group_order = lax.iota(jnp.int32, shards) ^ group_base
    d_vectors = jnp.stack(
        [
            vectors[0:D],
            vectors[D : 2 * D],
            vectors[4 * D : 5 * D],
            vectors[5 * D + FF : 6 * D + FF],
            vectors[6 * D + FF : 7 * D + FF],
            vectors[7 * D + FF : 8 * D + FF],
        ]
    )
    gain_first, gain_second, bias_out, bias_down, offset_first, offset_second = exact_product(
        d_vectors, selector, 3
    )
    bias_q = vectors[2 * D : 3 * D].reshape(shards, head_width)[group_order]
    bias_v = vectors[3 * D : 4 * D].reshape(shards, head_width)[group_order]
    bias_up = vectors[5 * D : 5 * D + FF].reshape(shards, up_width)[group_order]

    d_rows = jnp.stack(
        [bias_out, gain_first, offset_first, bias_down, gain_second, offset_second]
        + [jnp.zeros_like(bias_out)] * 2
    )

    def flipped(index):
        from_out = (index >= qkv_tiles) & (index < qkv_tiles + out_tiles)
        return (from_out | (index >= qkv_tiles + out_tiles + up_tiles))[:, None, None]

    own_tiles = lax.dynamic_slice_in_dim(owner, dp_rank * slots, slots, 0)
    own_flip = flipped(own_tiles)
    sent = master[0].astype(jnp.bfloat16)
    sent = jnp.where(own_flip, jnp.swapaxes(sent, 1, 2), sent)
    placing = (lax.iota(jnp.int32, tile_total)[:, None] == owner[None, :]).astype(jnp.bfloat16)
    if direct:
        parts = sent.reshape(slots, PARTS, SUB * block_size).swapaxes(0, 1)
        parts = lax.all_to_all(parts, "dp", 0, 0, tiled=True).reshape(tile_total, -1)
        tiles = product(placing, parts).astype(jnp.bfloat16)
        slab = slabs_from_tiles(tiles.reshape(tile_total, 1, SUB, block_size), shards, block_size)[0]
        half, rows = D // 2, D // PARTS
        bf16 = jnp.bfloat16
        first_slab, up_slab, down_slab = (slab[:, k * D : (k + 1) * D] for k in range(3))
        up_left, up_right = up_slab[:, :half], up_slab[:, half:]
        *blocks, up_left, up_right, rows_in, grad_out, d_rows = together(
            *from_z(first_slab),
            swap_over(up_left, 0, 2),
            swap_over(up_right, 1, 0),
            rows_in,
            grad_out,
            d_rows,
        )
        left, right, up_near = merge(
            [first_slab, *blocks, up_slab, up_left, up_right],
            [(half, half, bf16), (half, half, bf16), (2 * rows, D, bf16)],
            [(k, z * rows, 0, rows, half, [(z, 0, k * half)]) for k in range(2) for z in range(4)]
            + [
                (2, 0, 0, rows, D, [(4, 0, 0)]),
                (2, rows, 0, rows, half, [(5, 0, 0)]),
                (2, rows, half, rows, half, [(6, 0, 0)]),
            ],
        )
        up_blocks = from_z(up_near)
        left, right = merge(
            [left, swap_over(left, 0, 2), right, swap_over(right, 1, 0)],
            [(D, half, bf16), (D, half, bf16)],
            [
                (k, q * half, 0, half, half, [(2 * k + q, 0, 0)])
                for k in range(2)
                for q in range(2)
            ],
        )
        first = over_core(
            list(together(left, swap_over(left, 1, 0), right, swap_over(right, 0, 2)))
        )
        *first, up_near, block_1, block_2, block_3 = together(*first, up_near, *up_blocks)
        up_blocks = [block_1, block_2, block_3]
        up_near, up_left, up_right = merge(
            [up_near, *up_blocks],
            [(D, D, bf16), (D, half, bf16), (D, half, bf16)],
            [(0, 2 * z * rows, 0, 2 * rows, D, [(z, 0, 0)]) for z in range(4)]
            + [
                (1 + k, 2 * z * rows, 0, 2 * rows, half, [(z, 0, k * half)])
                for k in range(2)
                for z in range(4)
            ],
        )
        up = [up_near, swap_over(up_left, 1, 0), swap_over(up_right, 0, 2)]
        down_slab, *up_blocks = together(down_slab, *up_blocks)
        down_blocks = from_z(down_slab)
        places = (place_first, place_edges, place_plane)
        pieces = [first, None, None]
    else:
        gathered = lax.all_gather(sent, "dp", axis=0, tiled=True).reshape(tile_total, -1)
        tiles = product(placing, gathered).astype(jnp.bfloat16)
        slabs = slabs_from_tiles(
            tiles.reshape(tile_total, PARTS, SUB, block_size), shards, block_size
        )
        whole = jnp.concatenate([slabs[part_of_block(k)] for k in range(PARTS)], 0)
        every = lax.all_gather(whole, "tensor", axis=0)
        pieces = [
            [every[j][:, k * D : (k + 1) * D] for j in range(shards)] for k in range(3)
        ]
        places = (place_groups,) * 3

    steps = row_count // ROWS
    packs_step = ROWS // length
    bias_qkv = jnp.concatenate([bias_q, jnp.zeros_like(bias_q), bias_v], 1)
    rows_spec = lambda width: pl.BlockSpec((ROWS, width), lambda i: (i, 0))
    pairs = HEADS // 2
    probs_spec = pl.BlockSpec((packs_step, pairs, length, 2 * length), lambda i: (i, 0, 0, 0))
    sums_spec = lambda width: pl.BlockSpec((8, width), lambda i: (0, 0))
    f32, bf16 = jnp.float32, jnp.bfloat16
    full = lambda array: (array, pl.BlockSpec(memory_space=pltpu.VMEM))
    by_rows = lambda array: (array, row_block(array))
    far_rows = lambda array: (array, row_block(array), "far")
    square = 2 * row_count * D * D

    whole_out = ((shards, D, D), bf16, pl.BlockSpec(memory_space=pltpu.VMEM))
    packed, probs, attended, unit_first, inverse_first, normed_low, whole_first = call_rows(
        functools.partial(attention_kernel, places[0], shards, local_heads, length),
        steps,
        [
            far_rows(rows_in),
            (own_segments[:, None, :], pl.BlockSpec((packs_step, 1, length), lambda i: (i, 0, 0))),
            (own_segments[:, :, None], pl.BlockSpec((packs_step, length, 1), lambda i: (i, 0, 0))),
            full(bias_qkv),
            full(d_rows),
            *[full(w) for w in pieces[0]],
        ],
        [
            ((row_count, 3 * D), bf16, rows_spec(3 * D), "far"),
            ((pack_count, pairs, length, 2 * length), bf16, probs_spec, "far"),
            ((row_count, D), bf16, rows_spec(D), "far"),
            ((row_count, D), f32, rows_spec(D), "far"),
            ((row_count, 1), f32, rows_spec(1), "far"),
            ((row_count, D), bf16, rows_spec(D), "far"),
            whole_out,
        ],
        4 * square + 4 * row_count * length * D,
        row_count * length * HEADS,
        [pltpu.VMEM((packs_step * pairs, length, 2 * length), f32)],
    )
    if direct:
        *up, block_1, block_2, block_3, normed_low = together(*up, *down_blocks, normed_low)
        (down_z,) = merge(
            [down_slab, block_1, block_2, block_3],
            [(half, D, bf16)],
            [(0, z * rows, 0, rows, D, [(z, 0, 0)]) for z in range(4)],
        )
        down = [down_z, swap_over(down_z, 1, 0), swap_over(down_z, 0, 2), swap_over(down_z, 1, 2)]
        pieces[1] = over_core(up)
    activated, slope, whole_up = call_rows(
        functools.partial(up_kernel, places[1], shards),
        steps,
        [far_rows(normed_low), full(bias_up), *[full(w) for w in pieces[1]]],
        [
            ((row_count, FF), bf16, rows_spec(FF)),
            ((row_count, FF), bf16, rows_spec(FF)),
            whole_out,
        ],
        4 * square,
        2 * row_count * FF,
    )
    if direct:
        *down, activated = together(*down, activated)
        pieces[2] = over_core(down)
    layer_out, grad_second, second_low, sums_second, whole_down = call_rows(
        functools.partial(down_kernel, places[2], shards),
        steps,
        [
            by_rows(activated),
            far_rows(unit_first),
            far_rows(grad_out),
            full(d_rows),
            *[full(w) for w in pieces[2]],
        ],
        [
            ((row_count, D), f32, rows_spec(D), "far"),
            ((row_count, D), f32, rows_spec(D), "far"),
            ((row_count, D), bf16, rows_spec(D)),
            ((8, D), f32, sums_spec(D)),
            whole_out,
        ],
        4 * square,
    )
    grad_w_down = weight_halves([second_low], [(activated, up_width, 0)])
    if direct:
        down_parts = reduce_core_plane(grad_w_down)
        second_low, *down_parts = together(second_low, *down_parts)
        down_parts = reduce_plane(*down_parts)
    grad_pre, grad_bias_up = call_rows(
        functools.partial(hidden_back_kernel, shards),
        steps,
        [by_rows(second_low), by_rows(slope), full(whole_down)],
        [((row_count, FF), bf16, rows_spec(FF)), ((8, up_width), f32, sums_spec(up_width))],
        4 * square,
    )
    grad_bias_up = grad_bias_up[:shards]
    grad_w_up = weight_halves([normed_low], [(grad_pre, up_width, 0)])
    grad_first, first_low, grad_attended, sums_first = call_rows(
        functools.partial(back_kernel, shards),
        steps,
        [
            by_rows(grad_pre),
            far_rows(grad_second),
            far_rows(unit_first),
            far_rows(inverse_first),
            full(d_rows),
            full(whole_up),
            full(whole_first),
        ],
        [
            ((row_count, D), f32, rows_spec(D), "far"),
            ((row_count, D), bf16, rows_spec(D)),
            ((row_count, D), bf16, rows_spec(D)),
            ((8, D), f32, sums_spec(D)),
        ],
        5 * square,
    )
    if direct:
        up_parts = reduce_core_edges(grad_w_up)
        grad_attended, *parts = together(grad_attended, *up_parts, *down_parts)
        up_parts = reduce_edges(*parts[:3])
        down_own = reduce_z(*parts[3:])
    grad_packed, column_sums = call_rows(
        functools.partial(attention_back_kernel, length),
        steps,
        [by_rows(grad_attended), far_rows(attended), far_rows(packed), (probs, probs_spec, "far")],
        [
            ((row_count, 3 * D), bf16, rows_spec(3 * D)),
            ((8, 3 * D), f32, sums_spec(3 * D)),
        ],
        8 * square,
        0,
        [pltpu.VMEM((packs_step * pairs, length, 2 * length), bf16)] * 2,
    )
    column_sums = column_sums[0].reshape(3, shards, head_width)
    grad_w_first = weight_halves(
        [rows_in, first_low],
        [(grad_packed, head_width, k * shards // 2) for k in range(3)] + [(attended, head_width, 0)],
    )
    if direct:
        grad_odd, grad_even, down_own, *others = together(
            *grad_w_first, down_own, *up_parts, sums_first, sums_second, grad_bias_up, column_sums
        )
        *up_parts, sums_first, sums_second, grad_bias_up, column_sums = others
        first_parts = reduce_core_edges((grad_odd, grad_even))
        *first_parts, layer_out = together(*first_parts, layer_out)
        first_parts = reduce_edges_plane(*first_parts)
        up_parts = reduce_edges_z(*up_parts)
    layer_out, input_grad = call_rows(
        functools.partial(natural_kernel, shards),
        steps,
        [
            far_rows(layer_out),
            far_rows(grad_first),
            by_rows(grad_packed),
            full(selector),
            full(whole_first),
        ],
        [((row_count, D), f32, rows_spec(D), "far")] * 2,
        7 * square,
    )

    if direct:
        first_parts = reduce_plane_edges(*first_parts)
        *parts, layer_out, input_grad = together(*first_parts, *up_parts, layer_out, input_grad)
        first_own = reduce_z(*parts[:4])
        up_own = reduce_edges_last(*parts[4:])
        slab_grad = jnp.concatenate([first_own, up_own, down_own], 1).astype(jnp.bfloat16)
        tile_grad = tiles_from_slabs(slab_grad[None], shards, block_size).reshape(tile_total, -1)
        slot_grad = transposed_times(placing, tile_grad).astype(jnp.bfloat16)
        slot_grad = lax.all_to_all(
            slot_grad.reshape(PARTS, slots, SUB * block_size), "dp", 0, 0, tiled=True
        )
        owned_grads = slot_grad.swapaxes(0, 1).reshape(slots, block_size, block_size)
    else:
        every = jnp.stack(
            [
                jnp.concatenate(
                    [half[1 - j % 2][j // 2] for half in (grad_w_first, grad_w_up, grad_w_down)], 1
                )
                for j in range(shards)
            ]
        ).astype(jnp.float32)
        mine = lax.psum_scatter(every, "tensor", scatter_dimension=0, tiled=True)[0]
        blocks = mine.reshape(PARTS, D // PARTS, -1)
        blocks = jnp.stack([blocks[(p % 2) * 4 + p // 2] for p in range(PARTS)])
        tile_grad = tiles_from_slabs(blocks, shards, block_size)
        slot_grad = tile_grad.reshape(tile_total, block_size, block_size)[owner]
        owned_grads = lax.psum_scatter(slot_grad, "dp", scatter_dimension=0, tiled=True)
    owned_grads = jnp.where(own_flip, jnp.swapaxes(owned_grads, 1, 2), owned_grads)

    grad_gain_second, grad_offset_second, grad_bias_down = (sums_second[k] for k in range(3))
    grad_gain_first, grad_offset_first, grad_bias_out = (sums_first[k] for k in range(3))
    d_grads = exact_product_t(
        jnp.stack(
            [
                grad_gain_first,
                grad_gain_second,
                grad_bias_out,
                grad_bias_down,
                grad_offset_first,
                grad_offset_second,
            ]
        ),
        selector,
        3,
    )
    grad_vector = jnp.concatenate(
        [
            d_grads[0],
            d_grads[1],
            column_sums[0][group_order].reshape(-1),
            column_sums[2][group_order].reshape(-1),
            d_grads[2],
            grad_bias_up[group_order].reshape(-1),
            d_grads[3],
            d_grads[4],
            d_grads[5],
        ]
    )
    vector_grad = sum_over_all(grad_vector) if direct else lax.psum(grad_vector, ("dp", "tensor"))


    bias_first = 1.0 - DECAY_FIRST**ADAM_STEP
    bias_second = 1.0 - DECAY_SECOND**ADAM_STEP
    step_slots = max(k for k in (1, 2, 3, 4, 6) if slots % k == 0)
    slots_spec = pl.BlockSpec((step_slots, block_size, block_size), lambda i: (i, 0, 0))
    slot_out = ((slots, block_size, block_size), f32, slots_spec, "far")
    new_master, new_first, new_second = call_rows(
        adam_kernel,
        slots // step_slots,
        [
            (array, slots_spec, "far")
            for array in (
                owned_grads,
                master[0],
                left_basis[0],
                right_basis[0],
                first_moment[0],
                second_moment[0],
            )
        ],
        [slot_out] * 3,
        22 * slots * block_size**3,
        slots * block_size**2,
    )
    new_vector_first = DECAY_FIRST * vector_first + (1.0 - DECAY_FIRST) * vector_grad
    new_vector_second = (
        DECAY_SECOND * vector_second + (1.0 - DECAY_SECOND) * vector_grad * vector_grad
    )
    new_vectors = vectors - VECTOR_RATE * (new_vector_first / bias_first) / (
        jnp.sqrt(new_vector_second / bias_second) + ADAM_EPS
    )
    return (
        layer_out,
        input_grad,
        new_master[None],
        new_first[None],
        new_second[None],
        new_vectors,
        new_vector_first,
        new_vector_second,
    )


def solution(mesh):
    return jax.shard_map(
        local,
        mesh=mesh,
        in_specs=(
            P(("dp", "tensor"), None),
            P("dp", None),
            P(("dp", "tensor"), None),
            P(),
            P("tensor", "dp", None, None),
            P("tensor", "dp", None, None),
            P("tensor", "dp", None, None),
            P("tensor", "dp", None, None),
            P("tensor", "dp", None, None),
            P(),
            P(),
            P(),
        ),
        out_specs=(
            P(("dp", "tensor"), None),
            P(("dp", "tensor"), None),
            P("tensor", "dp", None, None),
            P("tensor", "dp", None, None),
            P("tensor", "dp", None, None),
            P(),
            P(),
            P(),
        ),
        check_vma=False,
    )
```

```python
import functools
import math

import jax
import jax.numpy as jnp
from jax import lax
from jax.experimental import pallas as pl
from jax.experimental.pallas import tpu as pltpu
from jax.sharding import PartitionSpec as P

HEADS = 12
HEAD_DIM = 64
D = 768
FF = 3072
ADAM_STEP = 3


NORM_EPS = 1e-12
ADAM_EPS = 1e-08
MATRIX_RATE = 0.01
VECTOR_RATE = 0.1
DECAY_FIRST = 0.5
DECAY_SECOND = 0.5
MASKED = -1e30


def product(left_side, right_side):
    return jnp.dot(left_side, right_side, preferred_element_type=jnp.float32)


def times_transposed(left_side, right_side):
    return lax.dot_general(
        left_side, right_side, (((1,), (1,)), ((), ())), preferred_element_type=jnp.float32
    )


def transposed_times(left_side, right_side):
    return lax.dot_general(
        left_side, right_side, (((0,), (0,)), ((), ())), preferred_element_type=jnp.float32
    )


VMEM_LIMIT = 20 * 1024 * 1024

PARTS = 8
SUB = 12


def rounded(values):
    return lax.reduce_precision(values, 8, 7)


def split_terms(values, count):
    terms = []
    for _ in range(count):
        top = rounded(values)
        terms.append(top.astype(jnp.bfloat16))
        values = values - top
    return terms


def exact_product(values, selector, count):
    return sum(product(term, selector) for term in split_terms(values, count))


def part_of_block(block):
    return (block % 4) * 2 + block // 4


def feature_order(rank):
    place = lax.iota(jnp.int32, D)
    part = part_of_block(place // (D // PARTS)) ^ rank
    inner = place % (D // PARTS)
    return (inner // SUB) * (PARTS * SUB) + part * SUB + inner % SUB


def tile_counts(shards, block_size):
    rows = D // block_size
    qkv = rows * (3 * D // shards // block_size)
    out = rows * (D // shards // block_size)
    up = rows * (FF // shards // block_size)
    return (qkv, out, up)


def slabs_from_tiles(tiles, shards, block_size):
    cut = tiles.shape[1]
    qkv, out, up = tile_counts(shards, block_size)
    rows = D // block_size

    def by_rows(part):
        cols = part.shape[0] // rows
        part = part.reshape(rows, cols, cut, SUB, block_size)
        return part.transpose(2, 0, 3, 1, 4).reshape(cut, rows * SUB, cols * block_size)

    def by_cols(part):
        cols = part.shape[0] // rows
        part = part.reshape(cols, rows, cut, SUB, block_size)
        return part.transpose(2, 1, 3, 0, 4).reshape(cut, rows * SUB, cols * block_size)

    return jnp.concatenate(
        [
            by_rows(tiles[:qkv]),
            by_cols(tiles[qkv : qkv + out]),
            by_rows(tiles[qkv + out : qkv + out + up]),
            by_cols(tiles[qkv + out + up :]),
        ],
        2,
    )


def tiles_from_slabs(slabs, shards, block_size):
    cut = slabs.shape[0]
    rows = D // block_size
    width_qkv, width_out, width_up = 3 * D // shards, D // shards, FF // shards

    def by_rows(part):
        cols = part.shape[2] // block_size
        part = part.reshape(cut, rows, SUB, cols, block_size)
        return part.transpose(1, 3, 0, 2, 4).reshape(rows * cols, cut, SUB, block_size)

    def by_cols(part):
        cols = part.shape[2] // block_size
        part = part.reshape(cut, rows, SUB, cols, block_size)
        return part.transpose(3, 1, 0, 2, 4).reshape(rows * cols, cut, SUB, block_size)

    first = width_qkv + width_out
    second = first + width_up
    return jnp.concatenate(
        [
            by_rows(slabs[:, :, :width_qkv]),
            by_cols(slabs[:, :, width_qkv:first]),
            by_rows(slabs[:, :, first:second]),
            by_cols(slabs[:, :, second:]),
        ],
        0,
    )


def swap_over(values, over_dp, over_tensor):
    dp, tensor = lax.axis_size("dp"), lax.axis_size("tensor")
    pairs = [
        (a * tensor + b, (a ^ over_dp) * tensor + (b ^ over_tensor))
        for a in range(dp)
        for b in range(tensor)
    ]
    return lax.ppermute(values, ("dp", "tensor"), pairs)


def merge(terms, outs, segments):
    chunk = D // PARTS

    def kernel(*refs):
        for out, row, col, rows, cols, parts in segments:

            def step(k, carry, out=out, row=row, col=col, cols=cols, parts=parts):
                pieces = [
                    refs[term][pl.ds(pl.multiple_of(at + k * chunk, 32), chunk), left : left + cols]
                    for term, at, left in parts
                ]
                if len(pieces) > 1:
                    value = sum(piece.astype(jnp.float32) for piece in pieces)
                else:
                    value = pieces[0]
                to = refs[len(terms) + out]
                to[pl.ds(pl.multiple_of(row + k * chunk, 32), chunk), col : col + cols] = (
                    value.astype(to.dtype)
                )
                return carry

            lax.fori_loop(0, rows // chunk, step, 0)

    spec = pl.BlockSpec(memory_space=pltpu.VMEM)
    size = sum(term.size for term in terms)
    return pl.pallas_call(
        kernel,
        in_specs=[spec] * len(terms),
        out_specs=[spec] * len(outs),
        out_shape=[jax.ShapeDtypeStruct((rows, cols), dtype) for rows, cols, dtype in outs],
        compiler_params=pltpu.CompilerParams(vmem_limit_bytes=VMEM_LIMIT),
        cost_estimate=pl.CostEstimate(flops=size, bytes_accessed=4 * size, transcendentals=0),
    )(*terms)


def from_z(block):
    return [swap_over(block, 2 * k, 0) for k in (1, 2, 3)]


def over_core(blocks):
    return blocks + [swap_over(block, 0, 1) for block in blocks]


def place_first(refs, out_ref):
    count = len(refs) // 2
    half, cols = D // 2, D // 2
    for core in range(2):
        near, beside, across = refs[core * count : (core + 1) * count]
        for y in range(2):
            group = 2 * y + core
            out_ref[group, :half, :cols] = near[y * half : (y + 1) * half, :cols]
            out_ref[group, half:, :cols] = beside[y * half : (y + 1) * half, :]
            out_ref[group, :, cols:] = across[...] if y else near[:, cols:]


def place_edges(refs, out_ref):
    count = len(refs) // 2
    rows, half, cols = D // PARTS, D // 2, D // 2
    for core in range(2):
        near, beside, across = refs[core * count : (core + 1) * count]
        for y in range(2):
            for z in range(4):
                for x in range(2):
                    to = x * half + z * rows
                    by_y, by_x = (2 * z + y) * rows, (2 * z + x) * rows
                    left = beside[by_y : by_y + rows, :] if x else near[by_y : by_y + rows, :cols]
                    right = across[by_x : by_x + rows, :] if y else near[by_x : by_x + rows, cols:]
                    out_ref[2 * y + core, to : to + rows, :cols] = left
                    out_ref[2 * y + core, to : to + rows, cols:] = right


def place_plane(refs, out_ref):
    half = D // 2
    for core in range(2):
        for y in range(2):
            for x in range(2):
                out_ref[2 * y + core, x * half : (x + 1) * half, :] = refs[4 * core + 2 * y + x][...]


def place_groups(refs, out_ref):
    for group, ref in enumerate(refs):
        out_ref[group] = ref[...]


def core_terms(halves):
    odd, even = halves
    return [even.reshape(2 * D, D), swap_over(odd, 0, 1).reshape(2 * D, D)]


def summed(count, row, col):
    return [(term, row, col) for term in range(count)]


def reduce_core_plane(halves):
    half = D // 2
    return merge(
        core_terms(halves),
        [(half, D, jnp.bfloat16)] * 4,
        [(k, 0, 0, half, D, summed(2, k * half, 0)) for k in range(4)],
    )


def reduce_plane(near, beside, across, opposite):
    rows = D // PARTS
    terms = [near, swap_over(beside, 1, 0), swap_over(across, 0, 2), swap_over(opposite, 1, 2)]
    return merge(
        terms,
        [(rows, D, jnp.bfloat16)] * 4,
        [(k, 0, 0, rows, D, summed(4, k * rows, 0)) for k in range(4)],
    )


def z_terms(own, *sent):
    return [own] + [swap_over(block, 2 * (k + 1), 0) for k, block in enumerate(sent)]


def reduce_z(terms):
    rows = D // PARTS
    return merge(terms, [(rows, D, jnp.float32)], [(0, 0, 0, rows, D, summed(4, 0, 0))])[0]


def reduce_core_edges(halves):
    half = D // 2
    return merge(
        core_terms(halves),
        [(D, D, jnp.bfloat16), (D, half, jnp.bfloat16), (D, half, jnp.bfloat16)],
        [
            (0, 0, 0, half, half, summed(2, 0, 0)),
            (0, half, 0, half, half, summed(2, D, 0)),
            (0, 0, half, D, half, summed(2, 0, half)),
            (1, 0, 0, half, half, summed(2, half, 0)),
            (1, half, 0, half, half, summed(2, D + half, 0)),
            (2, 0, 0, D, half, summed(2, D, half)),
        ],
    )


def edge_terms(near, left, right):
    return [near, swap_over(left, 1, 0), swap_over(right, 0, 2)]


def edge_sums(row):
    half = D // 2
    return ((0, [(0, row, 0), (1, row, 0)]), (half, [(0, row, half), (2, row, 0)]))


def plane_edge_terms(near, left, right):
    return [near, swap_over(left, 0, 2), swap_over(right, 1, 0)]


def reduce_edges_plane(terms):
    half = D // 2
    kept = [(0, 0, col, half, half, parts) for col, parts in edge_sums(0)]
    sent = [
        (1 + k, 0, 0, half, half, parts) for k, (_, parts) in enumerate(edge_sums(half))
    ]
    return merge(
        terms,
        [(half, D, jnp.bfloat16), (half, half, jnp.bfloat16), (half, half, jnp.bfloat16)],
        kept + sent,
    )


def reduce_plane_edges(terms):
    rows, half = D // PARTS, D // 2
    return merge(
        terms,
        [(rows, D, jnp.bfloat16)] * 4,
        [
            (k, 0, col, rows, half, parts)
            for k in range(4)
            for col, parts in edge_sums(k * rows)
        ],
    )


def reduce_edges(terms):
    rows, half = D // PARTS, D // 2
    return merge(
        terms,
        [(2 * rows, D, jnp.bfloat16)] * 4,
        [
            (k, q * rows, col, rows, half, parts)
            for k in range(4)
            for q in range(2)
            for col, parts in edge_sums(q * half + k * rows)
        ],
    )


def reduce_edges_z(terms):
    rows, half = D // PARTS, D // 2
    return merge(
        terms,
        [(rows, D, jnp.bfloat16), (rows, half, jnp.bfloat16), (rows, half, jnp.bfloat16)],
        [
            (0, 0, 0, rows, D, summed(4, 0, 0)),
            (1, 0, 0, rows, half, summed(4, rows, 0)),
            (2, 0, 0, rows, half, summed(4, rows, half)),
        ],
    )


def reduce_edges_last(terms):
    rows, half = D // PARTS, D // 2
    return merge(
        terms,
        [(rows, D, jnp.float32)],
        [(0, 0, col, rows, half, parts) for col, parts in edge_sums(0)],
    )[0]


def sum_over_all(values):
    every = lax.all_gather(values, ("dp", "tensor"), axis=0, tiled=True)
    return jnp.sum(every.reshape(-1, *values.shape), 0)


ROWS = 256


def dot_nt(left_side, right_side):
    return lax.dot_general(
        left_side, right_side, (((1,), (1,)), ((), ())), preferred_element_type=jnp.float32
    )


def row_block(array):
    return pl.BlockSpec((ROWS, array.shape[1]), lambda i: (i, 0))


def call_rows(kernel, steps, inputs, outputs, flops, transcendentals=0, scratch=()):
    arrays = [
        pltpu.with_memory_space_constraint(array, pltpu.HBM) if far else array
        for array, _, *far in inputs
    ]
    shapes = [jax.ShapeDtypeStruct(shape, dtype) for shape, dtype, *_ in outputs]
    moved = sum(a.size * a.dtype.itemsize for a in arrays + shapes)
    shapes = [
        pltpu.HBM(shape.shape, shape.dtype) if len(output) > 3 else shape
        for shape, output in zip(shapes, outputs)
    ]
    return pl.pallas_call(
        kernel,
        grid=(steps,),
        in_specs=[spec for _, spec, *_ in inputs],
        out_specs=[output[2] for output in outputs],
        out_shape=shapes,
        scratch_shapes=scratch,
        compiler_params=pltpu.CompilerParams(vmem_limit_bytes=VMEM_LIMIT),
        cost_estimate=pl.CostEstimate(
            flops=int(1.0 * flops), bytes_accessed=moved, transcendentals=transcendentals
        ),
    )(*arrays)


def norm_rows(summed):
    centred = summed - jnp.mean(summed, -1, keepdims=True)
    inverse = lax.rsqrt(jnp.mean(centred * centred, -1, keepdims=True) + NORM_EPS)
    return centred * inverse, inverse


def norm_pull(gradient, unit_rows, inverse, gain_row):
    scaled = gradient * gain_row
    return inverse * (
        scaled
        - jnp.mean(scaled, -1, keepdims=True)
        - unit_rows * jnp.mean(scaled * unit_rows, -1, keepdims=True)
    )


def add_rows(ref, rows):
    sums = [jnp.sum(row, 0, keepdims=True) for row in rows]
    start = pl.program_id(0) == 0
    for place, total in enumerate(sums):
        kept = jnp.where(start, 0.0, ref[place : place + 1, :])
        ref[place : place + 1, :] = kept + total


def settle(place, refs, whole_ref, shards):
    @pl.when(pl.program_id(0) == 0)
    def _():
        place(refs, whole_ref)

    return [whole_ref.at[j] for j in range(shards)]


def pair_masks(length):
    wide = 2 * HEAD_DIM
    lower = lax.broadcasted_iota(jnp.int32, (length, wide), 1) < HEAD_DIM
    top = lax.broadcasted_iota(jnp.int32, (2 * length, wide), 0) < length
    left = lax.broadcasted_iota(jnp.int32, (2 * length, wide), 1) < HEAD_DIM
    return lower, top == left


def stacked(pair, own):
    return jnp.where(own, jnp.concatenate([pair, pair], 0), jnp.zeros((), pair.dtype))


def attention_kernel(place, shards, local_heads, length, *refs):
    rows_ref, across_ref, down_ref, bias_ref, vec_ref = refs[:5]
    packed_ref, probs_ref, attended_ref, unit_ref, inverse_ref, low_ref, whole_ref, scores_ref = (
        refs[-8:]
    )
    weights = settle(place, refs[5:-8], whole_ref, shards)
    head_width = local_heads * HEAD_DIM
    width = 3 * head_width
    wide = 2 * HEAD_DIM
    pairs = HEADS // 2
    rows = rows_ref[...]
    for j in range(shards):
        packed = product(rows, weights[j][:, :width]) + bias_ref[j : j + 1, :]
        for kind in range(3):
            part = packed[:, kind * head_width : (kind + 1) * head_width].astype(jnp.bfloat16)
            if kind == 0:
                part = part * jnp.bfloat16(HEAD_DIM ** (-0.5))
            start = kind * D + j * head_width
            packed_ref[:, start : start + head_width] = part
    _, own = pair_masks(length)
    ones = own.astype(jnp.bfloat16)
    steps = [(p, i) for p in range(ROWS // length) for i in range(pairs)]

    def pair_of(p, i, kind):
        span = slice(p * length, (p + 1) * length)
        return packed_ref[span, kind * D + i * wide : kind * D + (i + 1) * wide]

    for at, (p, i) in enumerate(steps):
        scores_ref[at] = dot_nt(pair_of(p, i, 0), stacked(pair_of(p, i, 1), own))
    for at, (p, i) in enumerate(steps):
        allowed = down_ref[p] == across_ref[p]
        for half in range(2):
            lanes = slice(half * length, (half + 1) * length)
            scores = jnp.where(allowed, scores_ref[at, :, lanes], MASKED)
            probs_ref[p, i, :, lanes] = jnp.exp(
                scores - jnp.max(scores, -1, keepdims=True)
            ).astype(jnp.bfloat16)
    for p, i in steps:
        mixed = product(
            probs_ref[p, i], jnp.concatenate([stacked(pair_of(p, i, 2), own), ones], 1)
        )
        attended_ref[p * length : (p + 1) * length, i * wide : (i + 1) * wide] = (
            mixed[:, :wide] / mixed[:, wide:]
        ).astype(jnp.bfloat16)
    summed = rows.astype(jnp.float32) + vec_ref[0:1, :]
    for j in range(shards):
        summed = summed + dot_nt(
            attended_ref[:, j * head_width : (j + 1) * head_width], weights[j][:, width:]
        )
    unit, inverse = norm_rows(summed)
    unit_ref[...] = unit
    inverse_ref[...] = inverse
    low_ref[...] = (unit * vec_ref[1:2, :] + vec_ref[2:3, :]).astype(jnp.bfloat16)


def normal_cdf(values):
    decay = jnp.exp(values * values * -0.5)
    t = 1.0 / (1.0 + jnp.abs(values) * (0.3275911 * 0.5**0.5))
    poly = t * (
        0.127414796
        + t * (-0.142248368 + t * (0.7107068705 + t * (-0.7265760135 + t * 0.5307027145)))
    )
    upper = poly * decay
    return jnp.where(values > 0, 1.0 - upper, upper), decay


def up_kernel(place, shards, *refs):
    low_ref, bias_ref = refs[:2]
    act_ref, slope_ref, whole_ref = refs[-3:]
    weights = settle(place, refs[2:-3], whole_ref, shards)
    width = weights[0].shape[1]
    chunk = 256
    low = low_ref[...]
    for j in range(shards):
        for c in range(0, width, chunk):
            pre = product(low, weights[j][:, c : c + chunk]) + bias_ref[j : j + 1, c : c + chunk]
            below, decay = normal_cdf(pre)
            at = j * width + c
            act_ref[:, at : at + chunk] = (pre * below).astype(jnp.bfloat16)
            slope_ref[:, at : at + chunk] = (
                below + pre * decay * (0.5 / math.pi) ** 0.5
            ).astype(jnp.bfloat16)


def down_kernel(place, shards, *refs):
    act_ref, unit_ref, grad_ref, vec_ref = refs[:4]
    out_ref, dz_ref, low_ref, sums_ref, whole_ref = refs[-5:]
    weights = settle(place, refs[4:-5], whole_ref, shards)
    width = weights[0].shape[1]
    summed = unit_ref[...] * vec_ref[1:2, :] + vec_ref[2:3, :] + vec_ref[3:4, :]
    for j in range(shards):
        summed = summed + dot_nt(act_ref[:, j * width : (j + 1) * width], weights[j][...])
    unit, inverse = norm_rows(summed)
    gain = vec_ref[4:5, :]
    out_ref[...] = unit * gain + vec_ref[5:6, :]
    gradient = grad_ref[...]
    dz = norm_pull(gradient, unit, inverse, gain)
    dz_ref[...] = dz
    low_ref[...] = dz.astype(jnp.bfloat16)
    add_rows(sums_ref, (gradient * unit, gradient, dz))


def hidden_back_kernel(shards, *refs):
    low_ref, slope_ref, whole_ref, dpre_ref, bias_sums_ref = refs
    width = whole_ref.shape[2]
    low = low_ref[...]
    for j in range(shards):
        span = slice(j * width, (j + 1) * width)
        dpre = product(low, whole_ref[j]) * slope_ref[:, span].astype(jnp.float32)
        dpre = dpre.astype(jnp.bfloat16)
        dpre_ref[:, span] = dpre
        total = jnp.sum(dpre.astype(jnp.float32), 0, keepdims=True)
        kept = jnp.where(pl.program_id(0) == 0, 0.0, bias_sums_ref[j : j + 1, :])
        bias_sums_ref[j : j + 1, :] = kept + total


def back_kernel(shards, *refs):
    dpre_ref, dz_ref, unit_ref, inverse_ref, vec_ref, up_ref, first_ref = refs[:7]
    dz1_ref, low1_ref, datt_ref, sums_ref = refs[7:]
    width = up_ref.shape[2]
    gradient = dz_ref[...]
    for j in range(shards):
        gradient = gradient + dot_nt(dpre_ref[:, j * width : (j + 1) * width], up_ref[j])
    unit = unit_ref[...]
    dz1 = norm_pull(gradient, unit, inverse_ref[...], vec_ref[1:2, :])
    dz1_ref[...] = dz1
    low1 = dz1.astype(jnp.bfloat16)
    low1_ref[...] = low1
    add_rows(sums_ref, (gradient * unit, gradient, dz1))
    head_width = D // shards
    for j in range(shards):
        datt_ref[:, j * head_width : (j + 1) * head_width] = product(
            low1, first_ref[j, :, 3 * head_width :]
        ).astype(jnp.bfloat16)


def attention_back_kernel(length, *refs):
    datt_ref, attended_ref, packed_ref, probs_ref, dpacked_ref, sums_ref, up_ref, grad_ref = refs
    wide = 2 * HEAD_DIM
    lower, own = pair_masks(length)
    ones = own.astype(jnp.bfloat16)
    steps = [(p, i) for p in range(ROWS // length) for i in range(HEADS // 2)]

    def pair_of(p, i, kind):
        span = slice(p * length, (p + 1) * length)
        return packed_ref[span, kind * D + i * wide : kind * D + (i + 1) * wide]

    def keep(p, i, kind, grad):
        span = slice(p * length, (p + 1) * length)
        dpacked_ref[span, kind * D + i * wide : kind * D + (i + 1) * wide] = grad.astype(
            jnp.bfloat16
        )

    for place, (p, i) in enumerate(steps):
        span = slice(p * length, (p + 1) * length)
        lanes = slice(i * wide, (i + 1) * wide)
        upstream = datt_ref[span, lanes].astype(jnp.float32) / product(probs_ref[p, i], ones)
        up_ref[place, :, :wide] = upstream.astype(jnp.bfloat16)
        up_ref[place, :, wide:] = (upstream * attended_ref[span, lanes].astype(jnp.float32)).astype(
            jnp.bfloat16
        )
    for place, (p, i) in enumerate(steps):
        centred = dot_nt(
            up_ref[place], jnp.concatenate([stacked(pair_of(p, i, 2), own), -ones], 1)
        )
        grad_ref[place] = (probs_ref[p, i].astype(jnp.float32) * centred).astype(jnp.bfloat16)
    for place, (p, i) in enumerate(steps):
        grad_scores = grad_ref[place]
        keep(
            p, i, 0,
            product(grad_scores, stacked(pair_of(p, i, 1), own)) * HEAD_DIM ** (-0.5),
        )
        both = transposed_times(grad_scores, pair_of(p, i, 0))
        keep(p, i, 1, jnp.where(lower, both[:length], both[length:]))
        both = transposed_times(probs_ref[p, i], up_ref[place, :, :wide])
        keep(p, i, 2, jnp.where(lower, both[:length], both[length:]))
    total = jnp.sum(dpacked_ref[...].astype(jnp.float32), 0, keepdims=True)
    kept = jnp.where(pl.program_id(0) == 0, 0.0, sums_ref[0:1, :])
    sums_ref[0:1, :] = kept + total


def weight_kernel(odd, count, *refs):
    lefts, refs = refs[:2] if count > 1 else refs[:1], refs[2 if count > 1 else 1 :]
    rights, (out_ref, *turned) = refs[:count], refs[count:]
    start = pl.program_id(0) == 0

    @pl.when(start)
    def _():
        for left, kept in zip(lefts, turned):
            kept[...] = left[...].T

    at = 0
    for place, right in enumerate(rights):
        half = right.shape[1] // 2
        values = right[...] if count == 1 else right[:, half:] if odd else right[:, :half]
        grad = product(turned[place == count - 1 and count > 1][...], values)
        out_ref[0, :, at : at + values.shape[1]] = grad.astype(jnp.bfloat16)
        at += values.shape[1]


def weight_halves(lefts, rights):
    halves = []
    for odd in (1, 0):
        count = len(rights)
        single = count == 1
        specs = []
        for array, width, before in rights:
            if single:
                specs.append(pl.BlockSpec((array.shape[0], width), lambda i: (0, 2 * i + odd)))
            else:
                specs.append(
                    pl.BlockSpec((array.shape[0], 2 * width), lambda i, b=before: (0, b + i))
                )
        arrays = [
            *lefts,
            *[
                array if single else pltpu.with_memory_space_constraint(array, pltpu.HBM)
                for array, _, _ in rights
            ],
        ]
        tokens = lefts[0].shape[0]
        (half,) = pl.pallas_call(
            functools.partial(weight_kernel, odd, count),
            grid=(2,),
            in_specs=[pl.BlockSpec(memory_space=pltpu.VMEM) for _ in lefts] + specs,
            out_specs=[pl.BlockSpec((1, D, D), lambda i: (i, 0, 0))],
            out_shape=[jax.ShapeDtypeStruct((2, D, D), jnp.bfloat16)],
            scratch_shapes=[pltpu.VMEM((D, tokens), jnp.bfloat16) for _ in lefts],
            compiler_params=pltpu.CompilerParams(vmem_limit_bytes=VMEM_LIMIT),
            cost_estimate=pl.CostEstimate(
                flops=4 * tokens * D * D,
                bytes_accessed=sum(2 * array.size for array in arrays),
                transcendentals=0,
            ),
        )(*arrays)
        halves.append(half)
    return halves


def two_terms(values):
    top = values.astype(jnp.bfloat16)
    return top, (values - top.astype(jnp.float32)).astype(jnp.bfloat16)


def adam_kernel(*refs):
    grad_ref, master_ref, left_ref, right_ref, first_ref, second_ref = refs[:6]
    master_out, first_out, second_out = refs[6:]
    bias_first = 1.0 - DECAY_FIRST**ADAM_STEP
    bias_second = 1.0 - DECAY_SECOND**ADAM_STEP
    count = grad_ref.shape[0]
    lefts = [two_terms(left_ref[k]) for k in range(count)]
    rights = [two_terms(right_ref[k]) for k in range(count)]
    turned = []
    for k in range(count):
        top, rest = two_terms(grad_ref[k].astype(jnp.float32))
        turned.append(
            product(top, rights[k][0]) + product(top, rights[k][1]) + product(rest, rights[k][0])
        )
    directions = []
    for k in range(count):
        top, rest = two_terms(turned[k])
        rotated = (
            transposed_times(lefts[k][0], top)
            + transposed_times(lefts[k][0], rest)
            + transposed_times(lefts[k][1], top)
        )
        first = DECAY_FIRST * first_ref[k] + (1.0 - DECAY_FIRST) * rotated
        second = DECAY_SECOND * second_ref[k] + (1.0 - DECAY_SECOND) * rotated * rotated
        first_out[k] = first
        second_out[k] = second
        directions.append(first / bias_first / (jnp.sqrt(second / bias_second) + ADAM_EPS))
    backs = []
    for k in range(count):
        top, rest = two_terms(directions[k])
        backs.append(
            product(lefts[k][0], top) + product(lefts[k][0], rest) + product(lefts[k][1], top)
        )
    for k in range(count):
        top, rest = two_terms(backs[k])
        update = (
            times_transposed(top, rights[k][0])
            + times_transposed(rest, rights[k][0])
            + times_transposed(top, rights[k][1])
        )
        master_out[k] = master_ref[k] - MATRIX_RATE * update


def two_terms(values):
    top = values.astype(jnp.bfloat16)
    return top, (values - top.astype(jnp.float32)).astype(jnp.bfloat16)


def unpermuted(values, selector_ref):
    top, rest = two_terms(values)
    return dot_nt(top, selector_ref[...]) + dot_nt(rest, selector_ref[...])


def layer_kernel(out_ref, selector_ref, layer_ref):
    layer_ref[...] = unpermuted(out_ref[...], selector_ref)


def input_kernel(shards, dz1_ref, dpacked_ref, selector_ref, whole_ref, input_ref):
    head_width = D // shards
    gradient = dz1_ref[...]
    for j in range(shards):
        own = [
            dpacked_ref[:, kind * D + j * head_width : kind * D + (j + 1) * head_width]
            for kind in range(3)
        ]
        gradient = gradient + dot_nt(jnp.concatenate(own, 1), whole_ref[j, :, : 3 * head_width])
    input_ref[...] = unpermuted(gradient, selector_ref)


def vector_kernel(shards, *refs):
    base_ref, first_ref, second_ref, hidden_ref, columns_ref, selector_ref, out_ref = refs
    base = base_ref[0]
    rows = jnp.concatenate(
        [
            first_ref[0:1, :],
            second_ref[0:1, :],
            first_ref[2:3, :],
            second_ref[2:3, :],
            first_ref[1:2, :],
            second_ref[1:2, :],
            jnp.zeros((2, D), jnp.float32),
        ],
        0,
    )
    natural = jnp.zeros((8, D), jnp.float32)
    for _ in range(3):
        term = rows.astype(jnp.bfloat16)
        rows = rows - term.astype(jnp.float32)
        natural = natural + dot_nt(term, selector_ref[...])
    hidden = FF // D
    out_ref[...] = jnp.zeros(out_ref.shape, jnp.float32)
    for at, row in ((0, 0), (1, 1), (4, 2), (5 + hidden, 3), (6 + hidden, 4), (7 + hidden, 5)):
        out_ref[at : at + 1, :] = natural[row : row + 1, :]
    width = D // shards
    for j in range(shards):
        out_ref[5 + j : 6 + j, :] = hidden_ref[pl.ds(j ^ base, 1), :]
        for at, kind in ((2, 0), (3, 2)):
            parts = [
                jnp.where(
                    (j ^ base) == k,
                    columns_ref[0:1, kind * D + k * width : kind * D + (k + 1) * width],
                    0.0,
                )
                for k in range(shards)
            ]
            out_ref[at : at + 1, j * width : (j + 1) * width] = sum(parts)


def adam_kernel(*refs):
    grad_ref, master_ref, left_ref, right_ref, first_ref, second_ref = refs[:6]
    master_out, first_out, second_out = refs[6:]
    bias_first = 1.0 - DECAY_FIRST**ADAM_STEP
    bias_second = 1.0 - DECAY_SECOND**ADAM_STEP
    count = grad_ref.shape[0]
    lefts = [two_terms(left_ref[k]) for k in range(count)]
    rights = [two_terms(right_ref[k]) for k in range(count)]
    turned = []
    for k in range(count):
        top, rest = two_terms(grad_ref[k].astype(jnp.float32))
        turned.append(
            product(top, rights[k][0]) + product(top, rights[k][1]) + product(rest, rights[k][0])
        )
    directions = []
    for k in range(count):
        top, rest = two_terms(turned[k])
        rotated = (
            transposed_times(lefts[k][0], top)
            + transposed_times(lefts[k][0], rest)
            + transposed_times(lefts[k][1], top)
        )
        first = DECAY_FIRST * first_ref[k] + (1.0 - DECAY_FIRST) * rotated
        second = DECAY_SECOND * second_ref[k] + (1.0 - DECAY_SECOND) * rotated * rotated
        first_out[k] = first
        second_out[k] = second
        directions.append(first / bias_first / (jnp.sqrt(second / bias_second) + ADAM_EPS))
    backs = []
    for k in range(count):
        top, rest = two_terms(directions[k])
        backs.append(
            product(lefts[k][0], top) + product(lefts[k][0], rest) + product(lefts[k][1], top)
        )
    for k in range(count):
        top, rest = two_terms(backs[k])
        update = (
            times_transposed(top, rights[k][0])
            + times_transposed(rest, rights[k][0])
            + times_transposed(top, rights[k][1])
        )
        master_out[k] = master_ref[k] - MATRIX_RATE * update


def natural_kernel(shards, *refs):
    out_ref, dz1_ref, dpacked_ref, selector_ref, whole_ref, layer_ref, input_ref = refs
    weights = [whole_ref.at[j] for j in range(shards)]
    head_width = D // shards
    gradient = dz1_ref[...]
    for j in range(shards):
        own = [
            dpacked_ref[:, kind * D + j * head_width : kind * D + (j + 1) * head_width]
            for kind in range(3)
        ]
        gradient = gradient + dot_nt(jnp.concatenate(own, 1), weights[j][:, : 3 * head_width])
    for source, ref in ((out_ref[...], layer_ref), (gradient, input_ref)):
        top = source.astype(jnp.bfloat16)
        rest = (source - top.astype(jnp.float32)).astype(jnp.bfloat16)
        ref[...] = dot_nt(top, selector_ref[...]) + dot_nt(rest, selector_ref[...])


def together(*values):
    return lax.optimization_barrier(values)


def local(
    tokens,
    segments,
    out_grad,
    owner,
    master,
    left_basis,
    right_basis,
    first_moment,
    second_moment,
    vectors,
    vector_first,
    vector_second,
):
    shards = lax.axis_size("tensor")
    dp_size = lax.axis_size("dp")
    direct = dp_size == PARTS and shards == 4
    tensor_rank = lax.axis_index("tensor")
    dp_rank = lax.axis_index("dp")
    local_heads = HEADS // shards
    head_width = local_heads * HEAD_DIM
    up_width = FF // shards
    width_qkv = 3 * head_width
    block_size = master.shape[-1]
    slots = master.shape[1]
    row_count = tokens.shape[0]
    length = segments.shape[1]
    pack_count = row_count // length
    own_segments = lax.dynamic_slice_in_dim(segments, tensor_rank * pack_count, pack_count, 0)
    qkv_tiles, out_tiles, up_tiles = tile_counts(shards, block_size)
    tile_total = owner.shape[0]

    group_base = tensor_rank if direct else 0
    order = feature_order(dp_rank if direct else 0)
    selector = (lax.iota(jnp.int32, D)[:, None] == order[None, :]).astype(jnp.bfloat16)

    rows_in = product(tokens, selector).astype(jnp.bfloat16)
    grad_out = exact_product(out_grad, selector, 2)

    group_order = lax.iota(jnp.int32, shards) ^ group_base
    d_vectors = jnp.stack(
        [
            vectors[0:D],
            vectors[D : 2 * D],
            vectors[4 * D : 5 * D],
            vectors[5 * D + FF : 6 * D + FF],
            vectors[6 * D + FF : 7 * D + FF],
            vectors[7 * D + FF : 8 * D + FF],
        ]
    )
    gain_first, gain_second, bias_out, bias_down, offset_first, offset_second = exact_product(
        d_vectors, selector, 3
    )
    bias_q = vectors[2 * D : 3 * D].reshape(shards, head_width)[group_order]
    bias_v = vectors[3 * D : 4 * D].reshape(shards, head_width)[group_order]
    bias_up = vectors[5 * D : 5 * D + FF].reshape(shards, up_width)[group_order]

    d_rows = jnp.stack(
        [bias_out, gain_first, offset_first, bias_down, gain_second, offset_second]
        + [jnp.zeros_like(bias_out)] * 2
    )

    def flipped(index):
        from_out = (index >= qkv_tiles) & (index < qkv_tiles + out_tiles)
        return (from_out | (index >= qkv_tiles + out_tiles + up_tiles))[:, None, None]

    own_tiles = lax.dynamic_slice_in_dim(owner, dp_rank * slots, slots, 0)
    own_flip = flipped(own_tiles)
    sent = master[0].astype(jnp.bfloat16)
    sent = jnp.where(own_flip, jnp.swapaxes(sent, 1, 2), sent)
    placing = (lax.iota(jnp.int32, tile_total)[:, None] == owner[None, :]).astype(jnp.bfloat16)
    if direct:
        parts = sent.reshape(slots, PARTS, SUB * block_size).swapaxes(0, 1)
        parts = lax.all_to_all(parts, "dp", 0, 0, tiled=True).reshape(tile_total, -1)
        tiles = product(placing, parts).astype(jnp.bfloat16)
        slab = slabs_from_tiles(tiles.reshape(tile_total, 1, SUB, block_size), shards, block_size)[0]
        half, rows = D // 2, D // PARTS
        bf16 = jnp.bfloat16
        first_slab, up_slab, down_slab = (slab[:, k * D : (k + 1) * D] for k in range(3))
        near_left, near_right = down_slab[:, :half], down_slab[:, half:]
        *blocks, near_left, near_right, rows_in, grad_out, d_rows = together(
            *from_z(first_slab),
            swap_over(near_left, 0, 2),
            swap_over(near_right, 1, 0),
            rows_in,
            grad_out,
            d_rows,
        )
        left, right, down_near = merge(
            [first_slab, *blocks, down_slab, near_left, near_right],
            [(half, half, bf16), (half, half, bf16), (2 * rows, D, bf16)],
            [(k, z * rows, 0, rows, half, [(z, 0, k * half)]) for k in range(2) for z in range(4)]
            + [
                (2, 0, 0, rows, D, [(4, 0, 0)]),
                (2, rows, 0, rows, half, [(5, 0, 0)]),
                (2, rows, half, rows, half, [(6, 0, 0)]),
            ],
        )
        left, right, down_near, up_slab = together(left, right, down_near, up_slab)
        up_blocks = from_z(up_slab)
        near, left, right = merge(
            [left, swap_over(left, 0, 2), right, swap_over(right, 1, 0)],
            [(D, D, bf16), (D, half, bf16), (D, half, bf16)],
            [
                (out, q * half, col, half, half, [(2 * k + q, 0, 0)])
                for k in range(2)
                for q in range(2)
                for out, col in ((0, k * half), (1 + k, 0))
            ],
        )
        (up_z,) = merge(
            [up_slab, *up_blocks],
            [(half, D, bf16)],
            [(0, z * rows, 0, rows, D, [(z, 0, 0)]) for z in range(4)],
        )
        near_there, beside, across, up_z, down_near = together(
            swap_over(near, 0, 1), swap_over(left, 1, 0), swap_over(right, 0, 2), up_z, down_near
        )
        first = [near, beside, across, near_there] + over_core([beside, across])[2:]
        up = [up_z, swap_over(up_z, 1, 0), swap_over(up_z, 0, 2), swap_over(up_z, 1, 2)]
        down_blocks = from_z(down_near)
        places = (place_first, place_plane, place_edges)
        pieces = [first, None, None]
    else:
        gathered = lax.all_gather(sent, "dp", axis=0, tiled=True).reshape(tile_total, -1)
        tiles = product(placing, gathered).astype(jnp.bfloat16)
        slabs = slabs_from_tiles(
            tiles.reshape(tile_total, PARTS, SUB, block_size), shards, block_size
        )
        whole = jnp.concatenate([slabs[part_of_block(k)] for k in range(PARTS)], 0)
        every = lax.all_gather(whole, "tensor", axis=0)
        pieces = [
            [every[j][:, k * D : (k + 1) * D] for j in range(shards)] for k in range(3)
        ]
        places = (place_groups,) * 3

    steps = row_count // ROWS
    packs_step = ROWS // length
    bias_qkv = jnp.concatenate([bias_q, jnp.zeros_like(bias_q), bias_v], 1)
    rows_spec = lambda width: pl.BlockSpec((ROWS, width), lambda i: (i, 0))
    pairs = HEADS // 2
    probs_spec = pl.BlockSpec((packs_step, pairs, length, 2 * length), lambda i: (i, 0, 0, 0))
    sums_spec = lambda width: pl.BlockSpec((8, width), lambda i: (0, 0))
    f32, bf16 = jnp.float32, jnp.bfloat16
    full = lambda array: (array, pl.BlockSpec(memory_space=pltpu.VMEM))
    by_rows = lambda array: (array, row_block(array))
    far_rows = lambda array: (array, row_block(array), "far")
    square = 2 * row_count * D * D

    whole_out = ((shards, D, D), bf16, pl.BlockSpec(memory_space=pltpu.VMEM))
    packed, probs, attended, unit_first, inverse_first, normed_low, whole_first = call_rows(
        functools.partial(attention_kernel, places[0], shards, local_heads, length),
        steps,
        [
            far_rows(rows_in),
            (own_segments[:, None, :], pl.BlockSpec((packs_step, 1, length), lambda i: (i, 0, 0))),
            (own_segments[:, :, None], pl.BlockSpec((packs_step, length, 1), lambda i: (i, 0, 0))),
            full(bias_qkv),
            full(d_rows),
            *[full(w) for w in pieces[0]],
        ],
        [
            ((row_count, 3 * D), bf16, rows_spec(3 * D), "far"),
            ((pack_count, pairs, length, 2 * length), bf16, probs_spec, "far"),
            ((row_count, D), bf16, rows_spec(D), "far"),
            ((row_count, D), f32, rows_spec(D), "far"),
            ((row_count, 1), f32, rows_spec(1), "far"),
            ((row_count, D), bf16, rows_spec(D), "far"),
            whole_out,
        ],
        4 * square + 4 * row_count * length * D,
        row_count * length * HEADS,
        [pltpu.VMEM((packs_step * pairs, length, 2 * length), f32)],
    )
    if direct:
        *up, block_1, block_2, block_3, normed_low = together(*up, *down_blocks, normed_low)
        down_near, near_left, near_right = merge(
            [down_near, block_1, block_2, block_3],
            [(D, D, bf16), (D, half, bf16), (D, half, bf16)],
            [(0, 2 * z * rows, 0, 2 * rows, D, [(z, 0, 0)]) for z in range(4)]
            + [
                (1 + k, 2 * z * rows, 0, 2 * rows, half, [(z, 0, k * half)])
                for k in range(2)
                for z in range(4)
            ],
        )
        down = [down_near, swap_over(near_left, 1, 0), swap_over(near_right, 0, 2)]
        pieces[1] = over_core(up)
    activated, slope, whole_up = call_rows(
        functools.partial(up_kernel, places[1], shards),
        steps,
        [far_rows(normed_low), full(bias_up), *[full(w) for w in pieces[1]]],
        [
            ((row_count, FF), bf16, rows_spec(FF)),
            ((row_count, FF), bf16, rows_spec(FF)),
            whole_out,
        ],
        4 * square,
        2 * row_count * FF,
    )
    if direct:
        *down, activated = together(*down, activated)
        pieces[2] = over_core(down)
    layer_out, grad_second, second_low, sums_second, whole_down = call_rows(
        functools.partial(down_kernel, places[2], shards),
        steps,
        [
            by_rows(activated),
            far_rows(unit_first),
            far_rows(grad_out),
            full(d_rows),
            *[full(w) for w in pieces[2]],
        ],
        [
            ((row_count, D), f32, rows_spec(D), "far"),
            ((row_count, D), f32, rows_spec(D), "far"),
            ((row_count, D), bf16, rows_spec(D)),
            ((8, D), f32, sums_spec(D)),
            whole_out,
        ],
        4 * square,
    )
    grad_w_down = weight_halves([second_low], [(activated, up_width, 0)])
    if direct:
        down_parts = reduce_core_plane(grad_w_down)
        second_low, *down_parts = together(second_low, *down_parts)
        down_parts = reduce_plane(*down_parts)
    grad_pre, grad_bias_up = call_rows(
        functools.partial(hidden_back_kernel, shards),
        steps,
        [by_rows(second_low), by_rows(slope), full(whole_down)],
        [((row_count, FF), bf16, rows_spec(FF)), ((8, up_width), f32, sums_spec(up_width))],
        4 * square,
    )
    grad_w_up = weight_halves([normed_low], [(grad_pre, up_width, 0)])
    grad_first, first_low, grad_attended, sums_first = call_rows(
        functools.partial(back_kernel, shards),
        steps,
        [
            by_rows(grad_pre),
            far_rows(grad_second),
            far_rows(unit_first),
            far_rows(inverse_first),
            full(d_rows),
            full(whole_up),
            full(whole_first),
        ],
        [
            ((row_count, D), f32, rows_spec(D), "far"),
            ((row_count, D), bf16, rows_spec(D), "far"),
            ((row_count, D), bf16, rows_spec(D)),
            ((8, D), f32, sums_spec(D)),
        ],
        5 * square,
    )
    if direct:
        up_parts = reduce_core_edges(grad_w_up)
        grad_attended, *parts = together(grad_attended, *up_parts, *down_parts)
        up_terms = edge_terms(*parts[:3])
        down_terms = z_terms(*parts[3:])
    grad_packed, column_sums = call_rows(
        functools.partial(attention_back_kernel, length),
        steps,
        [by_rows(grad_attended), far_rows(attended), far_rows(packed), (probs, probs_spec, "far")],
        [
            ((row_count, 3 * D), bf16, rows_spec(3 * D), "far"),
            ((8, 3 * D), f32, sums_spec(3 * D)),
        ],
        8 * square,
        0,
        [pltpu.VMEM((packs_step * pairs, length, 2 * length), bf16)] * 2,
    )
    (vector_rows,) = call_rows(
        functools.partial(vector_kernel, shards),
        1,
        [
            (
                lax.convert_element_type(group_base, jnp.int32).reshape(1),
                pl.BlockSpec(memory_space=pltpu.SMEM),
            ),
            full(sums_first),
            full(sums_second),
            full(grad_bias_up),
            full(column_sums),
            full(selector),
        ],
        [((16, D), f32, pl.BlockSpec(memory_space=pltpu.VMEM))],
        48 * D * D,
    )
    if direct:
        vector_rows, grad_packed, *others = together(
            vector_rows, grad_packed, *down_terms, *up_terms
        )
        down_terms, up_terms = others[:4], others[4:]
        vector_grad = sum_over_all(vector_rows)
        up_terms = z_terms(*reduce_edges(up_terms))
        down_own = reduce_z(down_terms)
    else:
        vector_grad = lax.psum(vector_rows, ("dp", "tensor"))
    vector_grad = vector_grad[: vectors.shape[0] // D].reshape(-1)
    grad_w_first = weight_halves(
        [rows_in, first_low],
        [(grad_packed, head_width, k * shards // 2) for k in range(3)] + [(attended, head_width, 0)],
    )
    if direct:
        first_parts = reduce_core_edges(grad_w_first)
        *first_parts, grad_first = together(*first_parts, grad_first)
        first_terms = edge_terms(*first_parts)
    (input_grad,) = call_rows(
        functools.partial(input_kernel, shards),
        steps,
        [far_rows(grad_first), far_rows(grad_packed), full(selector), full(whole_first)],
        [((row_count, D), f32, rows_spec(D), "far")],
        5 * square,
    )
    if direct:
        *first_terms, input_grad, layer_out = together(*first_terms, input_grad, layer_out)
        first_terms = plane_edge_terms(*reduce_edges_plane(first_terms))
    (layer_out,) = call_rows(
        layer_kernel,
        steps,
        [far_rows(layer_out), full(selector)],
        [((row_count, D), f32, rows_spec(D), "far")],
        2 * square,
    )
    if direct:
        *others, layer_out = together(*first_terms, *up_terms, layer_out)
        first_terms, up_terms = others[:3], others[3:]
        first_terms = z_terms(*reduce_plane_edges(first_terms))
        up_terms = plane_edge_terms(*reduce_edges_z(up_terms))
        up_own = reduce_edges_last(up_terms)
        first_own = reduce_z(first_terms)
        slab_grad = jnp.concatenate([first_own, up_own, down_own], 1).astype(jnp.bfloat16)
        tile_grad = tiles_from_slabs(slab_grad[None], shards, block_size).reshape(tile_total, -1)
        slot_grad = transposed_times(placing, tile_grad).astype(jnp.bfloat16)
        slot_grad = lax.all_to_all(
            slot_grad.reshape(PARTS, slots, SUB * block_size), "dp", 0, 0, tiled=True
        )
        owned_grads = slot_grad.swapaxes(0, 1).reshape(slots, block_size, block_size)
    else:
        every = jnp.stack(
            [
                jnp.concatenate(
                    [half[1 - j % 2][j // 2] for half in (grad_w_first, grad_w_up, grad_w_down)], 1
                )
                for j in range(shards)
            ]
        ).astype(jnp.float32)
        mine = lax.psum_scatter(every, "tensor", scatter_dimension=0, tiled=True)[0]
        blocks = mine.reshape(PARTS, D // PARTS, -1)
        blocks = jnp.stack([blocks[(p % 2) * 4 + p // 2] for p in range(PARTS)])
        tile_grad = tiles_from_slabs(blocks, shards, block_size)
        slot_grad = tile_grad.reshape(tile_total, block_size, block_size)[owner]
        owned_grads = lax.psum_scatter(slot_grad, "dp", scatter_dimension=0, tiled=True)
    owned_grads = jnp.where(own_flip, jnp.swapaxes(owned_grads, 1, 2), owned_grads)

    bias_first = 1.0 - DECAY_FIRST**ADAM_STEP
    bias_second = 1.0 - DECAY_SECOND**ADAM_STEP
    step_slots = max(k for k in (1, 2, 3, 4, 6) if slots % k == 0)
    slots_spec = pl.BlockSpec((step_slots, block_size, block_size), lambda i: (i, 0, 0))
    slot_out = ((slots, block_size, block_size), f32, slots_spec, "far")
    new_master, new_first, new_second = call_rows(
        adam_kernel,
        slots // step_slots,
        [
            (array, slots_spec, "far")
            for array in (
                owned_grads,
                master[0],
                left_basis[0],
                right_basis[0],
                first_moment[0],
                second_moment[0],
            )
        ],
        [slot_out] * 3,
        22 * slots * block_size**3,
        slots * block_size**2,
    )
    new_vector_first = DECAY_FIRST * vector_first + (1.0 - DECAY_FIRST) * vector_grad
    new_vector_second = (
        DECAY_SECOND * vector_second + (1.0 - DECAY_SECOND) * vector_grad * vector_grad
    )
    new_vectors = vectors - VECTOR_RATE * (new_vector_first / bias_first) / (
        jnp.sqrt(new_vector_second / bias_second) + ADAM_EPS
    )
    return (
        layer_out,
        input_grad,
        new_master[None],
        new_first[None],
        new_second[None],
        new_vectors,
        new_vector_first,
        new_vector_second,
    )


def solution(mesh):
    return jax.shard_map(
        local,
        mesh=mesh,
        in_specs=(
            P(("dp", "tensor"), None),
            P("dp", None),
            P(("dp", "tensor"), None),
            P(),
            P("tensor", "dp", None, None),
            P("tensor", "dp", None, None),
            P("tensor", "dp", None, None),
            P("tensor", "dp", None, None),
            P("tensor", "dp", None, None),
            P(),
            P(),
            P(),
        ),
        out_specs=(
            P(("dp", "tensor"), None),
            P(("dp", "tensor"), None),
            P("tensor", "dp", None, None),
            P("tensor", "dp", None, None),
            P("tensor", "dp", None, None),
            P(),
            P(),
            P(),
        ),
        check_vma=False,
    )
```

```python
import functools
import math

import jax
import jax.numpy as jnp
from jax import lax
from jax.experimental import pallas as pl
from jax.experimental.pallas import tpu as pltpu
from jax.sharding import PartitionSpec as P

HEADS = 12
HEAD_DIM = 64
D = 768
FF = 3072
ADAM_STEP = 3


NORM_EPS = 1e-12
ADAM_EPS = 1e-08
MATRIX_RATE = 0.01
VECTOR_RATE = 0.1
DECAY_FIRST = 0.5
DECAY_SECOND = 0.5
MASKED = -1e30


def product(left_side, right_side):
    return jnp.dot(left_side, right_side, preferred_element_type=jnp.float32)


def times_transposed(left_side, right_side):
    return lax.dot_general(
        left_side, right_side, (((1,), (1,)), ((), ())), preferred_element_type=jnp.float32
    )


def transposed_times(left_side, right_side):
    return lax.dot_general(
        left_side, right_side, (((0,), (0,)), ((), ())), preferred_element_type=jnp.float32
    )


VMEM_LIMIT = 16 * 1024 * 1024

PARTS = 8
SUB = 12


def part_of_block(block):
    return (block % 4) * 2 + block // 4


def feature_order(rank):
    place = lax.iota(jnp.int32, D)
    part = part_of_block(place // (D // PARTS)) ^ rank
    inner = place % (D // PARTS)
    return (inner // SUB) * (PARTS * SUB) + part * SUB + inner % SUB


def tile_counts(shards, block_size):
    rows = D // block_size
    qkv = rows * (3 * D // shards // block_size)
    out = rows * (D // shards // block_size)
    up = rows * (FF // shards // block_size)
    return (qkv, out, up)


def slabs_from_tiles(tiles, shards, block_size):
    cut = tiles.shape[1]
    qkv, out, up = tile_counts(shards, block_size)
    rows = D // block_size

    def by_rows(part):
        cols = part.shape[0] // rows
        part = part.reshape(rows, cols, cut, SUB, block_size)
        return part.transpose(2, 0, 3, 1, 4).reshape(cut, rows * SUB, cols * block_size)

    def by_cols(part):
        cols = part.shape[0] // rows
        part = part.reshape(cols, rows, cut, SUB, block_size)
        return part.transpose(2, 1, 3, 0, 4).reshape(cut, rows * SUB, cols * block_size)

    return jnp.concatenate(
        [
            by_rows(tiles[:qkv]),
            by_cols(tiles[qkv : qkv + out]),
            by_rows(tiles[qkv + out : qkv + out + up]),
            by_cols(tiles[qkv + out + up :]),
        ],
        2,
    )


def tiles_from_slabs(slabs, shards, block_size):
    cut = slabs.shape[0]
    rows = D // block_size
    width_qkv, width_out, width_up = 3 * D // shards, D // shards, FF // shards

    def by_rows(part):
        cols = part.shape[2] // block_size
        part = part.reshape(cut, rows, SUB, cols, block_size)
        return part.transpose(1, 3, 0, 2, 4).reshape(rows * cols, cut, SUB, block_size)

    def by_cols(part):
        cols = part.shape[2] // block_size
        part = part.reshape(cut, rows, SUB, cols, block_size)
        return part.transpose(3, 1, 0, 2, 4).reshape(rows * cols, cut, SUB, block_size)

    first = width_qkv + width_out
    second = first + width_up
    return jnp.concatenate(
        [
            by_rows(slabs[:, :, :width_qkv]),
            by_cols(slabs[:, :, width_qkv:first]),
            by_rows(slabs[:, :, first:second]),
            by_cols(slabs[:, :, second:]),
        ],
        0,
    )


def swap_over(values, over_dp, over_tensor):
    dp, tensor = lax.axis_size("dp"), lax.axis_size("tensor")
    pairs = [
        (a * tensor + b, (a ^ over_dp) * tensor + (b ^ over_tensor))
        for a in range(dp)
        for b in range(tensor)
    ]
    return lax.ppermute(values, ("dp", "tensor"), pairs)


def merge(terms, outs, segments):
    chunk = D // PARTS

    def kernel(*refs):
        for out, row, col, rows, cols, parts in segments:

            def step(k, carry, out=out, row=row, col=col, cols=cols, parts=parts):
                pieces = [
                    refs[term][pl.ds(pl.multiple_of(at + k * chunk, 32), chunk), left : left + cols]
                    for term, at, left in parts
                ]
                if len(pieces) > 1:
                    value = sum(piece.astype(jnp.float32) for piece in pieces)
                else:
                    value = pieces[0]
                to = refs[len(terms) + out]
                to[pl.ds(pl.multiple_of(row + k * chunk, 32), chunk), col : col + cols] = (
                    value.astype(to.dtype)
                )
                return carry

            lax.fori_loop(0, rows // chunk, step, 0)

    spec = pl.BlockSpec(memory_space=pltpu.VMEM)
    size = sum(term.size for term in terms)
    return pl.pallas_call(
        kernel,
        in_specs=[spec] * len(terms),
        out_specs=[spec] * len(outs),
        out_shape=[jax.ShapeDtypeStruct((rows, cols), dtype) for rows, cols, dtype in outs],
        compiler_params=pltpu.CompilerParams(vmem_limit_bytes=VMEM_LIMIT),
        cost_estimate=pl.CostEstimate(flops=size, bytes_accessed=4 * size, transcendentals=0),
    )(*terms)


def from_z(block):
    return [swap_over(block, 2 * k, 0) for k in (1, 2, 3)]


def over_core(blocks):
    return blocks + [swap_over(block, 0, 1) for block in blocks]


def put(out_ref, lead, row, col, ref, at, left, rows, cols):
    chunk = D // PARTS

    def step(k, carry):
        to = pl.multiple_of(row + k * chunk, 32)
        source = pl.multiple_of(at + k * chunk, 32)
        out_ref[lead, pl.ds(to, chunk), col : col + cols] = ref[
            pl.ds(source, chunk), left : left + cols
        ]
        return carry

    lax.fori_loop(0, rows // chunk, step, 0)


def place_first(refs, out_ref):
    count = len(refs) // 2
    half, width = D // 2, D // 4
    for core in range(2):
        near, beside, across = refs[core * count : (core + 1) * count]
        for y in range(2):
            col = (2 * y + core) * width
            for kind in range(2):
                left = kind * width
                put(out_ref, kind, 0, col, near, y * half, left, half, width)
                put(out_ref, kind, half, col, beside, y * half, left, half, width)
                if y:
                    put(out_ref, 2 + kind, 0, col, across, 0, left, D, width)
                else:
                    put(out_ref, 2 + kind, 0, col, near, 0, half + left, D, width)


def place_edges(refs, out_ref):
    count = len(refs) // 2
    rows, half = D // PARTS, D // 2
    for core in range(2):
        near, beside, across = refs[core * count : (core + 1) * count]
        for y in range(2):
            group = 2 * y + core
            for z in range(4):
                for x in range(2):
                    to, by_y, by_x = x * half + z * rows, (2 * z + y) * rows, (2 * z + x) * rows
                    put(out_ref, group, to, 0, beside if x else near, by_y, 0, rows, half)
                    if y:
                        put(out_ref, group, to, half, across, by_x, 0, rows, half)
                    else:
                        put(out_ref, group, to, half, near, by_x, half, rows, half)


def place_plane(refs, out_ref):
    half = D // 2
    for core in range(2):
        for y in range(2):
            for x in range(2):
                ref = refs[4 * core + 2 * y + x]
                put(out_ref, 2 * y + core, x * half, 0, ref, 0, 0, half, D)


def place_groups(refs, out_ref):
    for group, ref in enumerate(refs):
        put(out_ref, group, 0, 0, ref, 0, 0, D, D)


def place_kinds(refs, out_ref):
    width = D // len(refs)
    for group, ref in enumerate(refs):
        for kind in range(4):
            put(out_ref, kind, 0, group * width, ref, 0, kind * width, D, width)


def core_terms(halves):
    odd, even = halves
    return [even.reshape(2 * D, D), swap_over(odd, 0, 1).reshape(2 * D, D)]


def summed(count, row, col):
    return [(term, row, col) for term in range(count)]


def reduce_core_plane(halves):
    half = D // 2
    return merge(
        core_terms(halves),
        [(half, D, jnp.bfloat16)] * 4,
        [(k, 0, 0, half, D, summed(2, k * half, 0)) for k in range(4)],
    )


def reduce_plane(near, beside, across, opposite):
    rows = D // PARTS
    terms = [near, swap_over(beside, 1, 0), swap_over(across, 0, 2), swap_over(opposite, 1, 2)]
    return merge(
        terms,
        [(rows, D, jnp.bfloat16)] * 4,
        [(k, 0, 0, rows, D, summed(4, k * rows, 0)) for k in range(4)],
    )


def z_terms(own, *sent):
    return [own] + [swap_over(block, 2 * (k + 1), 0) for k, block in enumerate(sent)]


def reduce_z(terms):
    rows = D // PARTS
    return merge(terms, [(rows, D, jnp.float32)], [(0, 0, 0, rows, D, summed(4, 0, 0))])[0]


def reduce_core_edges(halves):
    half = D // 2
    return merge(
        core_terms(halves),
        [(D, D, jnp.bfloat16), (D, half, jnp.bfloat16), (D, half, jnp.bfloat16)],
        [
            (0, 0, 0, half, half, summed(2, 0, 0)),
            (0, half, 0, half, half, summed(2, D, 0)),
            (0, 0, half, D, half, summed(2, 0, half)),
            (1, 0, 0, half, half, summed(2, half, 0)),
            (1, half, 0, half, half, summed(2, D + half, 0)),
            (2, 0, 0, D, half, summed(2, D, half)),
        ],
    )


def edge_terms(near, left, right):
    return [near, swap_over(left, 1, 0), swap_over(right, 0, 2)]


def edge_sums(row):
    half = D // 2
    return ((0, [(0, row, 0), (1, row, 0)]), (half, [(0, row, half), (2, row, 0)]))


def plane_edge_terms(near, left, right):
    return [near, swap_over(left, 0, 2), swap_over(right, 1, 0)]


def reduce_edges_plane(terms):
    half = D // 2
    kept = [(0, 0, col, half, half, parts) for col, parts in edge_sums(0)]
    sent = [
        (1 + k, 0, 0, half, half, parts) for k, (_, parts) in enumerate(edge_sums(half))
    ]
    return merge(
        terms,
        [(half, D, jnp.bfloat16), (half, half, jnp.bfloat16), (half, half, jnp.bfloat16)],
        kept + sent,
    )


def reduce_plane_edges(terms):
    rows, half = D // PARTS, D // 2
    return merge(
        terms,
        [(rows, D, jnp.bfloat16)] * 4,
        [
            (k, 0, col, rows, half, parts)
            for k in range(4)
            for col, parts in edge_sums(k * rows)
        ],
    )


def reduce_edges(terms):
    rows, half = D // PARTS, D // 2
    return merge(
        terms,
        [(2 * rows, D, jnp.bfloat16)] * 4,
        [
            (k, q * rows, col, rows, half, parts)
            for k in range(4)
            for q in range(2)
            for col, parts in edge_sums(q * half + k * rows)
        ],
    )


def reduce_edges_z(terms):
    rows, half = D // PARTS, D // 2
    return merge(
        terms,
        [(rows, D, jnp.bfloat16), (rows, half, jnp.bfloat16), (rows, half, jnp.bfloat16)],
        [
            (0, 0, 0, rows, D, summed(4, 0, 0)),
            (1, 0, 0, rows, half, summed(4, rows, 0)),
            (2, 0, 0, rows, half, summed(4, rows, half)),
        ],
    )


def reduce_edges_last(terms):
    rows, half = D // PARTS, D // 2
    return merge(
        terms,
        [(rows, D, jnp.float32)],
        [(0, 0, col, rows, half, parts) for col, parts in edge_sums(0)],
    )[0]


def add_swapped(values, over_dp, over_tensor):
    return values + swap_over(values, over_dp, over_tensor)


ROWS = 256


def dot_nt(left_side, right_side):
    return lax.dot_general(
        left_side, right_side, (((1,), (1,)), ((), ())), preferred_element_type=jnp.float32
    )


def row_block(array):
    return pl.BlockSpec((ROWS, array.shape[1]), lambda i: (i, 0))


def call_rows(kernel, steps, inputs, outputs, flops, transcendentals=0, scratch=()):
    arrays = [
        pltpu.with_memory_space_constraint(array, pltpu.HBM) if far else array
        for array, _, *far in inputs
    ]
    shapes = [jax.ShapeDtypeStruct(shape, dtype) for shape, dtype, *_ in outputs]
    moved = sum(a.size * a.dtype.itemsize for a in arrays + shapes)
    shapes = [
        pltpu.HBM(shape.shape, shape.dtype) if len(output) > 3 else shape
        for shape, output in zip(shapes, outputs)
    ]
    return pl.pallas_call(
        kernel,
        grid=(steps,),
        in_specs=[spec for _, spec, *_ in inputs],
        out_specs=[output[2] for output in outputs],
        out_shape=shapes,
        scratch_shapes=scratch,
        compiler_params=pltpu.CompilerParams(vmem_limit_bytes=VMEM_LIMIT),
        cost_estimate=pl.CostEstimate(
            flops=int(1.0 * flops), bytes_accessed=moved, transcendentals=transcendentals
        ),
    )(*arrays)


def norm_rows(summed):
    centred = summed - jnp.mean(summed, -1, keepdims=True)
    inverse = lax.rsqrt(jnp.mean(centred * centred, -1, keepdims=True) + NORM_EPS)
    return centred * inverse, inverse


def norm_pull(gradient, unit_rows, inverse, gain_row):
    scaled = gradient * gain_row
    return inverse * (
        scaled
        - jnp.mean(scaled, -1, keepdims=True)
        - unit_rows * jnp.mean(scaled * unit_rows, -1, keepdims=True)
    )


def add_rows(ref, rows):
    sums = [jnp.sum(row, 0, keepdims=True) for row in rows]
    start = pl.program_id(0) == 0
    for place, total in enumerate(sums):
        kept = jnp.where(start, 0.0, ref[place : place + 1, :])
        ref[place : place + 1, :] = kept + total


def settle(place, refs, whole_ref, shards):
    @pl.when(pl.program_id(0) == 0)
    def _():
        place(refs, whole_ref)

    return [whole_ref.at[j] for j in range(shards)]


def pair_masks(length):
    wide = 2 * HEAD_DIM
    lower = lax.broadcasted_iota(jnp.int32, (length, wide), 1) < HEAD_DIM
    top = lax.broadcasted_iota(jnp.int32, (2 * length, wide), 0) < length
    left = lax.broadcasted_iota(jnp.int32, (2 * length, wide), 1) < HEAD_DIM
    return lower, top == left


def stacked(pair, own):
    return jnp.where(own, jnp.concatenate([pair, pair], 0), jnp.zeros((), pair.dtype))


def attention_kernel(place, length, *refs):
    rows_ref, across_ref, down_ref, bias_ref, vec_ref = refs[:5]
    packed_ref, probs_ref, attended_ref, unit_ref, inverse_ref, low_ref, whole_ref, scores_ref = (
        refs[-8:]
    )
    weights = settle(place, refs[5:-8], whole_ref, 4)
    wide = 2 * HEAD_DIM
    pairs = HEADS // 2
    rows = rows_ref[...]
    for kind in range(3):
        part = product(rows, weights[kind][...]) + bias_ref[kind : kind + 1, :]
        part = part.astype(jnp.bfloat16)
        if kind == 0:
            part = part * jnp.bfloat16(HEAD_DIM ** (-0.5))
        packed_ref[:, kind * D : (kind + 1) * D] = part
    _, own = pair_masks(length)
    ones = own.astype(jnp.bfloat16)
    steps = [(p, i) for p in range(ROWS // length) for i in range(pairs)]

    def pair_of(p, i, kind):
        span = slice(p * length, (p + 1) * length)
        return packed_ref[span, kind * D + i * wide : kind * D + (i + 1) * wide]

    for at, (p, i) in enumerate(steps):
        scores_ref[at] = dot_nt(pair_of(p, i, 0), stacked(pair_of(p, i, 1), own))
    for at, (p, i) in enumerate(steps):
        allowed = down_ref[p] == across_ref[p]
        for half in range(2):
            lanes = slice(half * length, (half + 1) * length)
            scores = jnp.where(allowed, scores_ref[at, :, lanes], MASKED)
            probs_ref[p, i, :, lanes] = jnp.exp(
                scores - jnp.max(scores, -1, keepdims=True)
            ).astype(jnp.bfloat16)
    for p, i in steps:
        mixed = product(
            probs_ref[p, i], jnp.concatenate([stacked(pair_of(p, i, 2), own), ones], 1)
        )
        attended_ref[p * length : (p + 1) * length, i * wide : (i + 1) * wide] = (
            mixed[:, :wide] / mixed[:, wide:]
        ).astype(jnp.bfloat16)
    summed = rows.astype(jnp.float32) + vec_ref[0:1, :]
    summed = summed + dot_nt(attended_ref[...], weights[3][...])
    unit, inverse = norm_rows(summed)
    unit_ref[...] = unit
    inverse_ref[...] = inverse
    low_ref[...] = (unit * vec_ref[1:2, :] + vec_ref[2:3, :]).astype(jnp.bfloat16)


def normal_cdf(values):
    decay = jnp.exp(values * values * -0.5)
    t = 1.0 / (1.0 + jnp.abs(values) * (0.3275911 * 0.5**0.5))
    poly = t * (
        0.127414796
        + t * (-0.142248368 + t * (0.7107068705 + t * (-0.7265760135 + t * 0.5307027145)))
    )
    upper = poly * decay
    return jnp.where(values > 0, 1.0 - upper, upper), decay


def up_kernel(place, shards, *refs):
    low_ref, bias_ref = refs[:2]
    act_ref, slope_ref, whole_ref = refs[-3:]
    weights = settle(place, refs[2:-3], whole_ref, shards)
    width = weights[0].shape[1]
    chunk = 256
    low = low_ref[...]
    for j in range(shards):
        for c in range(0, width, chunk):
            pre = product(low, weights[j][:, c : c + chunk]) + bias_ref[j : j + 1, c : c + chunk]
            below, decay = normal_cdf(pre)
            at = j * width + c
            act_ref[:, at : at + chunk] = (pre * below).astype(jnp.bfloat16)
            slope_ref[:, at : at + chunk] = (
                below + pre * decay * (0.5 / math.pi) ** 0.5
            ).astype(jnp.bfloat16)


def down_kernel(place, shards, *refs):
    act_ref, unit_ref, grad_ref, vec_ref = refs[:4]
    out_ref, dz_ref, low_ref, sums_ref, whole_ref = refs[-5:]
    weights = settle(place, refs[4:-5], whole_ref, shards)
    width = weights[0].shape[1]
    summed = unit_ref[...] * vec_ref[1:2, :] + vec_ref[2:3, :] + vec_ref[3:4, :]
    for j in range(shards):
        summed = summed + dot_nt(act_ref[:, j * width : (j + 1) * width], weights[j][...])
    unit, inverse = norm_rows(summed)
    gain = vec_ref[4:5, :]
    out_ref[...] = unit * gain + vec_ref[5:6, :]
    gradient = grad_ref[...]
    dz = norm_pull(gradient, unit, inverse, gain)
    dz_ref[...] = dz
    low_ref[...] = dz.astype(jnp.bfloat16)
    add_rows(sums_ref, (gradient * unit, gradient, dz))


def hidden_back_kernel(shards, *refs):
    low_ref, slope_ref, whole_ref, dpre_ref, bias_sums_ref = refs
    width = whole_ref.shape[2]
    low = low_ref[...]
    for j in range(shards):
        span = slice(j * width, (j + 1) * width)
        dpre = product(low, whole_ref[j]) * slope_ref[:, span].astype(jnp.float32)
        dpre = dpre.astype(jnp.bfloat16)
        dpre_ref[:, span] = dpre
        total = jnp.sum(dpre.astype(jnp.float32), 0, keepdims=True)
        kept = jnp.where(pl.program_id(0) == 0, 0.0, bias_sums_ref[j : j + 1, :])
        bias_sums_ref[j : j + 1, :] = kept + total


def back_kernel(shards, *refs):
    dpre_ref, dz_ref, unit_ref, inverse_ref, vec_ref, up_ref, first_ref = refs[:7]
    dz1_ref, low1_ref, datt_ref, sums_ref = refs[7:]
    width = up_ref.shape[2]
    gradient = dz_ref[...]
    for j in range(shards):
        gradient = gradient + dot_nt(dpre_ref[:, j * width : (j + 1) * width], up_ref[j])
    unit = unit_ref[...]
    dz1 = norm_pull(gradient, unit, inverse_ref[...], vec_ref[1:2, :])
    dz1_ref[...] = dz1
    low1 = dz1.astype(jnp.bfloat16)
    low1_ref[...] = low1
    add_rows(sums_ref, (gradient * unit, gradient, dz1))
    datt_ref[...] = product(low1, first_ref[3]).astype(jnp.bfloat16)


def attention_back_kernel(length, *refs):
    datt_ref, attended_ref, packed_ref, probs_ref, dpacked_ref, sums_ref, up_ref, grad_ref = refs
    wide = 2 * HEAD_DIM
    lower, own = pair_masks(length)
    ones = own.astype(jnp.bfloat16)
    steps = [(p, i) for p in range(ROWS // length) for i in range(HEADS // 2)]

    def pair_of(p, i, kind):
        span = slice(p * length, (p + 1) * length)
        return packed_ref[span, kind * D + i * wide : kind * D + (i + 1) * wide]

    def keep(p, i, kind, grad):
        span = slice(p * length, (p + 1) * length)
        dpacked_ref[span, kind * D + i * wide : kind * D + (i + 1) * wide] = grad.astype(
            jnp.bfloat16
        )

    for place, (p, i) in enumerate(steps):
        span = slice(p * length, (p + 1) * length)
        lanes = slice(i * wide, (i + 1) * wide)
        upstream = datt_ref[span, lanes].astype(jnp.float32) / product(probs_ref[p, i], ones)
        up_ref[place, :, :wide] = upstream.astype(jnp.bfloat16)
        up_ref[place, :, wide:] = (upstream * attended_ref[span, lanes].astype(jnp.float32)).astype(
            jnp.bfloat16
        )
    for place, (p, i) in enumerate(steps):
        centred = dot_nt(
            up_ref[place], jnp.concatenate([stacked(pair_of(p, i, 2), own), -ones], 1)
        )
        grad_ref[place] = (probs_ref[p, i].astype(jnp.float32) * centred).astype(jnp.bfloat16)
    for place, (p, i) in enumerate(steps):
        grad_scores = grad_ref[place]
        keep(
            p, i, 0,
            product(grad_scores, stacked(pair_of(p, i, 1), own)) * HEAD_DIM ** (-0.5),
        )
        both = transposed_times(grad_scores, pair_of(p, i, 0))
        keep(p, i, 1, jnp.where(lower, both[:length], both[length:]))
        both = transposed_times(probs_ref[p, i], up_ref[place, :, :wide])
        keep(p, i, 2, jnp.where(lower, both[:length], both[length:]))
    total = jnp.sum(dpacked_ref[...].astype(jnp.float32), 0, keepdims=True)
    kept = jnp.where(pl.program_id(0) == 0, 0.0, sums_ref[0:1, :])
    sums_ref[0:1, :] = kept + total


def weight_kernel(odd, count, *refs):
    lefts, refs = refs[:2] if count > 1 else refs[:1], refs[2 if count > 1 else 1 :]
    rights, (out_ref, *turned) = refs[:count], refs[count:]
    start = pl.program_id(0) == 0

    @pl.when(start)
    def _():
        for left, kept in zip(lefts, turned):
            kept[...] = left[...].T

    at = 0
    for place, right in enumerate(rights):
        half = right.shape[1] // 2
        values = right[...] if count == 1 else right[:, half:] if odd else right[:, :half]
        grad = product(turned[place == count - 1 and count > 1][...], values)
        out_ref[0, :, at : at + values.shape[1]] = grad.astype(jnp.bfloat16)
        at += values.shape[1]


def weight_halves(lefts, rights):
    halves = []
    for odd in (1, 0):
        count = len(rights)
        single = count == 1
        specs = []
        for array, width, before in rights:
            if single:
                specs.append(pl.BlockSpec((array.shape[0], width), lambda i: (0, 2 * i + odd)))
            else:
                specs.append(
                    pl.BlockSpec((array.shape[0], 2 * width), lambda i, b=before: (0, b + i))
                )
        arrays = [
            *lefts,
            *[
                array if single else pltpu.with_memory_space_constraint(array, pltpu.HBM)
                for array, _, _ in rights
            ],
        ]
        tokens = lefts[0].shape[0]
        (half,) = pl.pallas_call(
            functools.partial(weight_kernel, odd, count),
            grid=(2,),
            in_specs=[pl.BlockSpec(memory_space=pltpu.VMEM) for _ in lefts] + specs,
            out_specs=[pl.BlockSpec((1, D, D), lambda i: (i, 0, 0))],
            out_shape=[jax.ShapeDtypeStruct((2, D, D), jnp.bfloat16)],
            scratch_shapes=[pltpu.VMEM((D, tokens), jnp.bfloat16) for _ in lefts],
            compiler_params=pltpu.CompilerParams(vmem_limit_bytes=VMEM_LIMIT),
            cost_estimate=pl.CostEstimate(
                flops=4 * tokens * D * D,
                bytes_accessed=sum(2 * array.size for array in arrays),
                transcendentals=0,
            ),
        )(*arrays)
        halves.append(half)
    return halves


def two_terms(values):
    top = values.astype(jnp.bfloat16)
    return top, (values - top.astype(jnp.float32)).astype(jnp.bfloat16)


def adam_kernel(*refs):
    grad_ref, master_ref, left_ref, right_ref, first_ref, second_ref = refs[:6]
    master_out, first_out, second_out = refs[6:]
    bias_first = 1.0 - DECAY_FIRST**ADAM_STEP
    bias_second = 1.0 - DECAY_SECOND**ADAM_STEP
    count = grad_ref.shape[0]
    lefts = [two_terms(left_ref[k]) for k in range(count)]
    rights = [two_terms(right_ref[k]) for k in range(count)]
    turned = []
    for k in range(count):
        grad = product(grad_ref[k].astype(jnp.bfloat16), rights[k][0])
        grad = grad + product(grad_ref[k].astype(jnp.bfloat16), rights[k][1])
        if grad_ref.dtype != jnp.bfloat16:
            grad = grad + product(two_terms(grad_ref[k])[1], rights[k][0])
        turned.append(grad)
    directions = []
    for k in range(count):
        top, rest = two_terms(turned[k])
        rotated = (
            transposed_times(lefts[k][0], top)
            + transposed_times(lefts[k][0], rest)
            + transposed_times(lefts[k][1], top)
        )
        first = DECAY_FIRST * first_ref[k] + (1.0 - DECAY_FIRST) * rotated
        second = DECAY_SECOND * second_ref[k] + (1.0 - DECAY_SECOND) * rotated * rotated
        first_out[k] = first
        second_out[k] = second
        directions.append(first / bias_first / (jnp.sqrt(second / bias_second) + ADAM_EPS))
    backs = [
        product(lefts[k][0], directions[k].astype(jnp.bfloat16)).astype(jnp.bfloat16)
        for k in range(count)
    ]
    for k in range(count):
        update = times_transposed(backs[k], rights[k][0])
        master_out[k] = master_ref[k] - MATRIX_RATE * update


def two_terms(values):
    top = values.astype(jnp.bfloat16)
    return top, (values - top.astype(jnp.float32)).astype(jnp.bfloat16)


def unpermuted(values, selector_ref):
    top, rest = two_terms(values)
    return dot_nt(top, selector_ref[...]) + dot_nt(rest, selector_ref[...])


def enter_kernel(tokens_ref, grad_ref, vectors_ref, selector_ref, rows_ref, out_ref, d_rows_ref):
    selector = selector_ref[...]
    rows_ref[...] = product(tokens_ref[...], selector).astype(jnp.bfloat16)
    top, rest = two_terms(grad_ref[...])
    out_ref[...] = product(top, selector) + product(rest, selector)

    @pl.when(pl.program_id(0) == 0)
    def _():
        rows = vectors_ref[...]
        permuted = jnp.zeros(rows.shape, jnp.float32)
        for _ in range(3):
            term = rows.astype(jnp.bfloat16)
            rows = rows - term.astype(jnp.float32)
            permuted = permuted + product(term, selector)
        d_rows_ref[...] = permuted


def layer_kernel(out_ref, selector_ref, layer_ref):
    layer_ref[...] = unpermuted(out_ref[...], selector_ref)


def input_kernel(dz1_ref, dpacked_ref, selector_ref, whole_ref, input_ref):
    gradient = dz1_ref[...]
    for kind in range(3):
        gradient = gradient + dot_nt(dpacked_ref[:, kind * D : (kind + 1) * D], whole_ref[kind])
    input_ref[...] = unpermuted(gradient, selector_ref)


def vector_kernel(shards, *refs):
    base_ref, first_ref, second_ref, hidden_ref, columns_ref, selector_ref, out_ref = refs
    base = base_ref[0]
    rows = jnp.concatenate(
        [
            first_ref[0:1, :],
            second_ref[0:1, :],
            first_ref[2:3, :],
            second_ref[2:3, :],
            first_ref[1:2, :],
            second_ref[1:2, :],
            jnp.zeros((2, D), jnp.float32),
        ],
        0,
    )
    natural = jnp.zeros((8, D), jnp.float32)
    for _ in range(3):
        term = rows.astype(jnp.bfloat16)
        rows = rows - term.astype(jnp.float32)
        natural = natural + dot_nt(term, selector_ref[...])
    hidden = FF // D
    out_ref[...] = jnp.zeros(out_ref.shape, jnp.float32)
    for at, row in ((0, 0), (1, 1), (4, 2), (5 + hidden, 3), (6 + hidden, 4), (7 + hidden, 5)):
        out_ref[at : at + 1, :] = natural[row : row + 1, :]
    width = D // shards
    for j in range(shards):
        out_ref[5 + j : 6 + j, :] = hidden_ref[pl.ds(j ^ base, 1), :]
        for at, kind in ((2, 0), (3, 2)):
            parts = [
                jnp.where(
                    (j ^ base) == k,
                    columns_ref[0:1, kind * D + k * width : kind * D + (k + 1) * width],
                    0.0,
                )
                for k in range(shards)
            ]
            out_ref[at : at + 1, j * width : (j + 1) * width] = sum(parts)


def adam_kernel(*refs):
    grad_ref, master_ref, left_ref, right_ref, first_ref, second_ref = refs[:6]
    master_out, first_out, second_out = refs[6:]
    bias_first = 1.0 - DECAY_FIRST**ADAM_STEP
    bias_second = 1.0 - DECAY_SECOND**ADAM_STEP
    count = grad_ref.shape[0]
    lefts = [two_terms(left_ref[k]) for k in range(count)]
    rights = [two_terms(right_ref[k]) for k in range(count)]
    turned = []
    for k in range(count):
        top, rest = two_terms(grad_ref[k].astype(jnp.float32))
        turned.append(
            product(top, rights[k][0]) + product(top, rights[k][1]) + product(rest, rights[k][0])
        )
    directions = []
    for k in range(count):
        top, rest = two_terms(turned[k])
        rotated = (
            transposed_times(lefts[k][0], top)
            + transposed_times(lefts[k][0], rest)
            + transposed_times(lefts[k][1], top)
        )
        first = DECAY_FIRST * first_ref[k] + (1.0 - DECAY_FIRST) * rotated
        second = DECAY_SECOND * second_ref[k] + (1.0 - DECAY_SECOND) * rotated * rotated
        first_out[k] = first
        second_out[k] = second
        directions.append(first / bias_first / (jnp.sqrt(second / bias_second) + ADAM_EPS))
    backs = []
    for k in range(count):
        top, rest = two_terms(directions[k])
        backs.append(
            product(lefts[k][0], top) + product(lefts[k][0], rest) + product(lefts[k][1], top)
        )
    for k in range(count):
        top, rest = two_terms(backs[k])
        update = (
            times_transposed(top, rights[k][0])
            + times_transposed(rest, rights[k][0])
            + times_transposed(top, rights[k][1])
        )
        master_out[k] = master_ref[k] - MATRIX_RATE * update


def natural_kernel(shards, *refs):
    out_ref, dz1_ref, dpacked_ref, selector_ref, whole_ref, layer_ref, input_ref = refs
    weights = [whole_ref.at[j] for j in range(shards)]
    head_width = D // shards
    gradient = dz1_ref[...]
    for j in range(shards):
        own = [
            dpacked_ref[:, kind * D + j * head_width : kind * D + (j + 1) * head_width]
            for kind in range(3)
        ]
        gradient = gradient + dot_nt(jnp.concatenate(own, 1), weights[j][:, : 3 * head_width])
    for source, ref in ((out_ref[...], layer_ref), (gradient, input_ref)):
        top = source.astype(jnp.bfloat16)
        rest = (source - top.astype(jnp.float32)).astype(jnp.bfloat16)
        ref[...] = dot_nt(top, selector_ref[...]) + dot_nt(rest, selector_ref[...])


def together(*values):
    return lax.optimization_barrier(values)


def local(
    tokens,
    segments,
    out_grad,
    owner,
    master,
    left_basis,
    right_basis,
    first_moment,
    second_moment,
    vectors,
    vector_first,
    vector_second,
):
    shards = lax.axis_size("tensor")
    dp_size = lax.axis_size("dp")
    direct = dp_size == PARTS and shards == 4
    tensor_rank = lax.axis_index("tensor")
    dp_rank = lax.axis_index("dp")
    local_heads = HEADS // shards
    head_width = local_heads * HEAD_DIM
    up_width = FF // shards
    width_qkv = 3 * head_width
    block_size = master.shape[-1]
    slots = master.shape[1]
    row_count = tokens.shape[0]
    length = segments.shape[1]
    pack_count = row_count // length
    own_segments = lax.dynamic_slice_in_dim(segments, tensor_rank * pack_count, pack_count, 0)
    qkv_tiles, out_tiles, up_tiles = tile_counts(shards, block_size)
    tile_total = owner.shape[0]

    group_base = tensor_rank if direct else 0
    order = feature_order(dp_rank if direct else 0)
    selector = (lax.iota(jnp.int32, D)[:, None] == order[None, :]).astype(jnp.bfloat16)

    steps = row_count // ROWS
    f32, bf16 = jnp.float32, jnp.bfloat16
    rows_spec = lambda width: pl.BlockSpec((ROWS, width), lambda i: (i, 0))
    full = lambda array: (array, pl.BlockSpec(memory_space=pltpu.VMEM))
    by_rows = lambda array: (array, row_block(array))
    far_rows = lambda array: (array, row_block(array), "far")
    group_order = lax.iota(jnp.int32, shards) ^ group_base
    below = vectors[: 5 * D].reshape(5, D)
    above = vectors[5 * D + FF :].reshape(3, D)
    d_rows = jnp.stack(
        [below[4], below[0], above[1], above[0], below[1], above[2], below[0], below[0]]
    )
    bias_q = below[2].reshape(shards, head_width)[group_order]
    bias_v = below[3].reshape(shards, head_width)[group_order]
    bias_up = vectors[5 * D : 5 * D + FF].reshape(shards, up_width)[group_order]
    rows_in, grad_out, d_rows = call_rows(
        enter_kernel,
        steps,
        [far_rows(tokens), far_rows(out_grad), full(d_rows), full(selector)],
        [
            ((row_count, D), bf16, rows_spec(D), "far"),
            ((row_count, D), f32, rows_spec(D), "far"),
            ((8, D), f32, pl.BlockSpec(memory_space=pltpu.VMEM)),
        ],
        6 * row_count * D * D,
    )

    def flipped(index):
        from_out = (index >= qkv_tiles) & (index < qkv_tiles + out_tiles)
        return (from_out | (index >= qkv_tiles + out_tiles + up_tiles))[:, None, None]

    own_tiles = lax.dynamic_slice_in_dim(owner, dp_rank * slots, slots, 0)
    own_flip = flipped(own_tiles)
    sent = master[0].astype(jnp.bfloat16)
    sent = jnp.where(own_flip, jnp.swapaxes(sent, 1, 2), sent)
    placing = (lax.iota(jnp.int32, tile_total)[:, None] == owner[None, :]).astype(jnp.bfloat16)
    if direct:
        parts = sent.reshape(slots, PARTS, SUB * block_size).swapaxes(0, 1)
        parts = lax.all_to_all(parts, "dp", 0, 0, tiled=True).reshape(tile_total, -1)
        tiles = product(placing, parts).astype(jnp.bfloat16)
        slab = slabs_from_tiles(tiles.reshape(tile_total, 1, SUB, block_size), shards, block_size)[0]
        half, rows = D // 2, D // PARTS
        first_slab, up_slab, down_slab = (slab[:, k * D : (k + 1) * D] for k in range(3))
        near_left, near_right = down_slab[:, :half], down_slab[:, half:]
        *blocks, near_left, near_right, rows_in, grad_out, d_rows = together(
            *from_z(first_slab),
            swap_over(near_left, 0, 2),
            swap_over(near_right, 1, 0),
            rows_in,
            grad_out,
            d_rows,
        )
        left, right, down_near = merge(
            [first_slab, *blocks, down_slab, near_left, near_right],
            [(half, half, bf16), (half, half, bf16), (2 * rows, D, bf16)],
            [(k, z * rows, 0, rows, half, [(z, 0, k * half)]) for k in range(2) for z in range(4)]
            + [
                (2, 0, 0, rows, D, [(4, 0, 0)]),
                (2, rows, 0, rows, half, [(5, 0, 0)]),
                (2, rows, half, rows, half, [(6, 0, 0)]),
            ],
        )
        left, right, down_near, up_slab = together(left, right, down_near, up_slab)
        up_beside, down_beside = swap_over(up_slab, 2, 0), swap_over(down_near, 2, 0)
        left_across, right_beside, up_beside = together(
            swap_over(left, 0, 2), swap_over(right, 1, 0), up_beside
        )
        near, left, right, up_pair = merge(
            [left, left_across, right, right_beside, up_slab, up_beside],
            [(D, D, bf16), (D, half, bf16), (D, half, bf16), (2 * rows, D, bf16)],
            [
                (out, q * half, col, half, half, [(2 * k + q, 0, 0)])
                for k in range(2)
                for q in range(2)
                for out, col in ((0, k * half), (1 + k, 0))
            ]
            + [(3, z * rows, 0, rows, D, [(4 + z, 0, 0)]) for z in range(2)],
        )
        near_there, beside, across, up_far, down_beside = together(
            swap_over(near, 0, 1),
            swap_over(left, 1, 0),
            swap_over(right, 0, 2),
            swap_over(up_pair, 4, 0),
            down_beside,
        )
        up_z, down_pair = merge(
            [up_pair, up_far, down_near, down_beside],
            [(half, D, bf16)] * 2,
            [
                (k, z * 2 * rows, 0, 2 * rows, D, [(2 * k + z, 0, 0)])
                for k in range(2)
                for z in range(2)
            ],
        )
        first = [near, beside, across, near_there] + over_core([beside, across])[2:]
        up = [up_z, swap_over(up_z, 1, 0), swap_over(up_z, 0, 2), swap_over(up_z, 1, 2)]
        down_far = swap_over(down_pair, 4, 0)
        places = (place_first, place_plane, place_edges)
        pieces = [first, None, None]
    else:
        gathered = lax.all_gather(sent, "dp", axis=0, tiled=True).reshape(tile_total, -1)
        tiles = product(placing, gathered).astype(jnp.bfloat16)
        slabs = slabs_from_tiles(
            tiles.reshape(tile_total, PARTS, SUB, block_size), shards, block_size
        )
        whole = jnp.concatenate([slabs[part_of_block(k)] for k in range(PARTS)], 0)
        every = lax.all_gather(whole, "tensor", axis=0)
        pieces = [
            [every[j][:, k * D : (k + 1) * D] for j in range(shards)] for k in range(3)
        ]
        places = (place_kinds, place_groups, place_groups)

    packs_step = ROWS // length
    bias_qkv = jnp.stack(
        [bias_q.reshape(D), jnp.zeros((D,), jnp.float32), bias_v.reshape(D)]
    )
    pairs = HEADS // 2
    probs_spec = pl.BlockSpec((packs_step, pairs, length, 2 * length), lambda i: (i, 0, 0, 0))
    sums_spec = lambda width: pl.BlockSpec((8, width), lambda i: (0, 0))
    square = 2 * row_count * D * D

    whole_out = ((shards, D, D), bf16, pl.BlockSpec(memory_space=pltpu.VMEM))
    packed, probs, attended, unit_first, inverse_first, normed_low, whole_first = call_rows(
        functools.partial(attention_kernel, places[0], length),
        steps,
        [
            far_rows(rows_in),
            (own_segments[:, None, :], pl.BlockSpec((packs_step, 1, length), lambda i: (i, 0, 0))),
            (own_segments[:, :, None], pl.BlockSpec((packs_step, length, 1), lambda i: (i, 0, 0))),
            full(bias_qkv),
            full(d_rows),
            *[full(w) for w in pieces[0]],
        ],
        [
            ((row_count, 3 * D), bf16, rows_spec(3 * D), "far"),
            ((pack_count, pairs, length, 2 * length), bf16, probs_spec, "far"),
            ((row_count, D), bf16, rows_spec(D), "far"),
            ((row_count, D), f32, rows_spec(D), "far"),
            ((row_count, 1), f32, rows_spec(1), "far"),
            ((row_count, D), bf16, rows_spec(D), "far"),
            whole_out,
        ],
        4 * square + 4 * row_count * length * D,
        row_count * length * HEADS,
        [pltpu.VMEM((packs_step * pairs, length, 2 * length), f32)],
    )
    if direct:
        *up, down_far, normed_low = together(*up, down_far, normed_low)
        down_near, near_left, near_right = merge(
            [down_pair, down_far],
            [(D, D, bf16), (D, half, bf16), (D, half, bf16)],
            [(0, z * half, 0, half, D, [(z, 0, 0)]) for z in range(2)]
            + [
                (1 + k, z * half, 0, half, half, [(z, 0, k * half)])
                for k in range(2)
                for z in range(2)
            ],
        )
        down = [down_near, swap_over(near_left, 1, 0), swap_over(near_right, 0, 2)]
        pieces[1] = over_core(up)
    activated, slope, whole_up = call_rows(
        functools.partial(up_kernel, places[1], shards),
        steps,
        [far_rows(normed_low), full(bias_up), *[full(w) for w in pieces[1]]],
        [
            ((row_count, FF), bf16, rows_spec(FF)),
            ((row_count, FF), bf16, rows_spec(FF), "far"),
            whole_out,
        ],
        4 * square,
        2 * row_count * FF,
    )
    if direct:
        *down, activated = together(*down, activated)
        pieces[2] = over_core(down)
    layer_out, grad_second, second_low, sums_second, whole_down = call_rows(
        functools.partial(down_kernel, places[2], shards),
        steps,
        [
            by_rows(activated),
            far_rows(unit_first),
            far_rows(grad_out),
            full(d_rows),
            *[full(w) for w in pieces[2]],
        ],
        [
            ((row_count, D), f32, rows_spec(D), "far"),
            ((row_count, D), f32, rows_spec(D), "far"),
            ((row_count, D), bf16, rows_spec(D)),
            ((8, D), f32, sums_spec(D)),
            whole_out,
        ],
        4 * square,
    )
    grad_w_down = weight_halves([second_low], [(activated, up_width, 0)])
    if direct:
        down_parts = reduce_core_plane(grad_w_down)
        second_low, *down_parts = together(second_low, *down_parts)
        down_parts = reduce_plane(*down_parts)
    grad_pre, grad_bias_up = call_rows(
        functools.partial(hidden_back_kernel, shards),
        steps,
        [by_rows(second_low), far_rows(slope), full(whole_down)],
        [((row_count, FF), bf16, rows_spec(FF)), ((8, up_width), f32, sums_spec(up_width))],
        4 * square,
    )
    grad_w_up = weight_halves([normed_low], [(grad_pre, up_width, 0)])
    grad_first, first_low, grad_attended, sums_first = call_rows(
        functools.partial(back_kernel, shards),
        steps,
        [
            by_rows(grad_pre),
            far_rows(grad_second),
            far_rows(unit_first),
            far_rows(inverse_first),
            full(d_rows),
            full(whole_up),
            full(whole_first),
        ],
        [
            ((row_count, D), f32, rows_spec(D), "far"),
            ((row_count, D), bf16, rows_spec(D), "far"),
            ((row_count, D), bf16, rows_spec(D)),
            ((8, D), f32, sums_spec(D)),
        ],
        20 * square,
    )
    if direct:
        up_parts = reduce_core_edges(grad_w_up)
        grad_attended, *parts = together(grad_attended, *up_parts, *down_parts)
        up_terms = edge_terms(*parts[:3])
        down_terms = z_terms(*parts[3:])
    grad_packed, column_sums = call_rows(
        functools.partial(attention_back_kernel, length),
        steps,
        [by_rows(grad_attended), far_rows(attended), far_rows(packed), (probs, probs_spec, "far")],
        [
            ((row_count, 3 * D), bf16, rows_spec(3 * D), "far"),
            ((8, 3 * D), f32, sums_spec(3 * D)),
        ],
        8 * square,
        0,
        [pltpu.VMEM((packs_step * pairs, length, 2 * length), bf16)] * 2,
    )
    (vector_rows,) = call_rows(
        functools.partial(vector_kernel, shards),
        1,
        [
            (
                lax.convert_element_type(group_base, jnp.int32).reshape(1),
                pl.BlockSpec(memory_space=pltpu.SMEM),
            ),
            full(sums_first),
            full(sums_second),
            full(grad_bias_up),
            full(column_sums),
            full(selector),
        ],
        [((16, D), f32, pl.BlockSpec(memory_space=pltpu.VMEM))],
        48 * D * D,
    )
    if direct:
        vector_rows, grad_packed, *others = together(
            vector_rows, grad_packed, *down_terms, *up_terms
        )
        down_terms, up_terms = others[:4], others[4:]
        up_terms = z_terms(*reduce_edges(up_terms))
        down_own = reduce_z(down_terms)
    else:
        vector_rows = lax.psum(vector_rows, ("dp", "tensor"))
    grad_w_first = weight_halves(
        [rows_in, first_low],
        [(grad_packed, head_width, k * shards // 2) for k in range(3)] + [(attended, head_width, 0)],
    )
    if direct:
        first_parts = reduce_core_edges(grad_w_first)
        *first_parts, grad_first = together(*first_parts, grad_first)
        first_terms = edge_terms(*first_parts)
    (input_grad,) = call_rows(
        input_kernel,
        steps,
        [far_rows(grad_first), far_rows(grad_packed), full(selector), full(whole_first)],
        [((row_count, D), f32, rows_spec(D), "far")],
        5 * square,
    )
    if direct:
        *first_terms, input_grad, layer_out = together(*first_terms, input_grad, layer_out)
        first_terms = plane_edge_terms(*reduce_edges_plane(first_terms))
    (layer_out,) = call_rows(
        layer_kernel,
        steps,
        [far_rows(layer_out), full(selector)],
        [((row_count, D), f32, rows_spec(D), "far")],
        2 * square,
    )
    if direct:
        *others, layer_out = together(*first_terms, *up_terms, layer_out)
        first_terms, up_terms = others[:3], others[3:]
        *parts, vector_rows = together(*reduce_plane_edges(first_terms), vector_rows)
        first_terms = z_terms(*parts)
        vector_rows = add_swapped(add_swapped(vector_rows, 0, 1), 0, 2)
        up_terms = plane_edge_terms(*reduce_edges_z(up_terms))
        up_own = reduce_edges_last(up_terms)
        *first_terms, vector_rows = together(*first_terms, vector_rows)
        first_own = reduce_z(first_terms)
        slab_grad = jnp.concatenate([first_own, up_own, down_own], 1).astype(jnp.bfloat16)
        tile_grad = tiles_from_slabs(slab_grad[None], shards, block_size).reshape(tile_total, -1)
        slot_grad = transposed_times(placing, tile_grad).astype(jnp.bfloat16)
        slot_grad, vector_rows = together(slot_grad, vector_rows)
        slot_grad = lax.all_to_all(
            slot_grad.reshape(PARTS, slots, SUB * block_size), "dp", 0, 0, tiled=True
        )
        vector_rows = add_swapped(add_swapped(vector_rows, 1, 0), 2, 0)
        slot_grad, vector_rows = together(slot_grad, vector_rows)
        vector_rows = add_swapped(vector_rows, 4, 0)
        owned_grads = slot_grad.swapaxes(0, 1).reshape(slots, block_size, block_size)
    else:
        every = jnp.stack(
            [
                jnp.concatenate(
                    [half[1 - j % 2][j // 2] for half in (grad_w_first, grad_w_up, grad_w_down)], 1
                )
                for j in range(shards)
            ]
        ).astype(jnp.float32)
        mine = lax.psum_scatter(every, "tensor", scatter_dimension=0, tiled=True)[0]
        blocks = mine.reshape(PARTS, D // PARTS, -1)
        blocks = jnp.stack([blocks[(p % 2) * 4 + p // 2] for p in range(PARTS)])
        tile_grad = tiles_from_slabs(blocks, shards, block_size)
        slot_grad = tile_grad.reshape(tile_total, block_size, block_size)[owner]
        owned_grads = lax.psum_scatter(slot_grad, "dp", scatter_dimension=0, tiled=True)
    owned_grads = jnp.where(own_flip, jnp.swapaxes(owned_grads, 1, 2), owned_grads)

    bias_first = 1.0 - DECAY_FIRST**ADAM_STEP
    bias_second = 1.0 - DECAY_SECOND**ADAM_STEP
    step_slots = max(k for k in (1, 2, 3, 4, 6) if slots % k == 0)
    slots_spec = pl.BlockSpec((step_slots, block_size, block_size), lambda i: (i, 0, 0))
    slot_out = ((slots, block_size, block_size), f32, slots_spec, "far")
    new_master, new_first, new_second = call_rows(
        adam_kernel,
        slots // step_slots,
        [
            (array, slots_spec, "far")
            for array in (
                owned_grads,
                master[0],
                left_basis[0],
                right_basis[0],
                first_moment[0],
                second_moment[0],
            )
        ],
        [slot_out] * 3,
        22 * slots * block_size**3,
        slots * block_size**2,
    )
    vector_grad = vector_rows[: vectors.shape[0] // D].reshape(-1)
    new_vector_first = DECAY_FIRST * vector_first + (1.0 - DECAY_FIRST) * vector_grad
    new_vector_second = (
        DECAY_SECOND * vector_second + (1.0 - DECAY_SECOND) * vector_grad * vector_grad
    )
    new_vectors = vectors - VECTOR_RATE * (new_vector_first / bias_first) / (
        jnp.sqrt(new_vector_second / bias_second) + ADAM_EPS
    )
    return (
        layer_out,
        input_grad,
        new_master[None],
        new_first[None],
        new_second[None],
        new_vectors,
        new_vector_first,
        new_vector_second,
    )


def solution(mesh):
    return jax.shard_map(
        local,
        mesh=mesh,
        in_specs=(
            P(("dp", "tensor"), None),
            P("dp", None),
            P(("dp", "tensor"), None),
            P(),
            P("tensor", "dp", None, None),
            P("tensor", "dp", None, None),
            P("tensor", "dp", None, None),
            P("tensor", "dp", None, None),
            P("tensor", "dp", None, None),
            P(),
            P(),
            P(),
        ),
        out_specs=(
            P(("dp", "tensor"), None),
            P(("dp", "tensor"), None),
            P("tensor", "dp", None, None),
            P("tensor", "dp", None, None),
            P("tensor", "dp", None, None),
            P(),
            P(),
            P(),
        ),
        check_vma=False,
    )
```

```python
import functools
import math

import jax
import jax.numpy as jnp
from jax import lax
from jax.experimental import pallas as pl
from jax.experimental.pallas import tpu as pltpu
from jax.sharding import PartitionSpec as P

HEADS = 12
HEAD_DIM = 64
D = 768
FF = 3072
ADAM_STEP = 3


NORM_EPS = 1e-12
ADAM_EPS = 1e-08
MATRIX_RATE = 0.01
VECTOR_RATE = 0.1
DECAY_FIRST = 0.5
DECAY_SECOND = 0.5
MASKED = -1e30


def product(left_side, right_side):
    return jnp.dot(left_side, right_side, preferred_element_type=jnp.float32)


def times_transposed(left_side, right_side):
    return lax.dot_general(
        left_side, right_side, (((1,), (1,)), ((), ())), preferred_element_type=jnp.float32
    )


def transposed_times(left_side, right_side):
    return lax.dot_general(
        left_side, right_side, (((0,), (0,)), ((), ())), preferred_element_type=jnp.float32
    )


VMEM_LIMIT = 16 * 1024 * 1024

PARTS = 8
SUB = 12


def part_of_block(block):
    return (block % 4) * 2 + block // 4


def feature_order(rank):
    place = lax.iota(jnp.int32, D)
    part = part_of_block(place // (D // PARTS)) ^ rank
    inner = place % (D // PARTS)
    return (inner // SUB) * (PARTS * SUB) + part * SUB + inner % SUB


def tile_counts(shards, block_size):
    rows = D // block_size
    qkv = rows * (3 * D // shards // block_size)
    out = rows * (D // shards // block_size)
    up = rows * (FF // shards // block_size)
    return (qkv, out, up)


def slabs_from_tiles(tiles, shards, block_size):
    cut = tiles.shape[1]
    qkv, out, up = tile_counts(shards, block_size)
    rows = D // block_size

    def by_rows(part):
        cols = part.shape[0] // rows
        part = part.reshape(rows, cols, cut, SUB, block_size)
        return part.transpose(2, 0, 3, 1, 4).reshape(cut, rows * SUB, cols * block_size)

    def by_cols(part):
        cols = part.shape[0] // rows
        part = part.reshape(cols, rows, cut, SUB, block_size)
        return part.transpose(2, 1, 3, 0, 4).reshape(cut, rows * SUB, cols * block_size)

    return jnp.concatenate(
        [
            by_rows(tiles[:qkv]),
            by_cols(tiles[qkv : qkv + out]),
            by_rows(tiles[qkv + out : qkv + out + up]),
            by_cols(tiles[qkv + out + up :]),
        ],
        2,
    )


def tiles_from_slabs(slabs, shards, block_size):
    cut = slabs.shape[0]
    rows = D // block_size
    width_qkv, width_out, width_up = 3 * D // shards, D // shards, FF // shards

    def by_rows(part):
        cols = part.shape[2] // block_size
        part = part.reshape(cut, rows, SUB, cols, block_size)
        return part.transpose(1, 3, 0, 2, 4).reshape(rows * cols, cut, SUB, block_size)

    def by_cols(part):
        cols = part.shape[2] // block_size
        part = part.reshape(cut, rows, SUB, cols, block_size)
        return part.transpose(3, 1, 0, 2, 4).reshape(rows * cols, cut, SUB, block_size)

    first = width_qkv + width_out
    second = first + width_up
    return jnp.concatenate(
        [
            by_rows(slabs[:, :, :width_qkv]),
            by_cols(slabs[:, :, width_qkv:first]),
            by_rows(slabs[:, :, first:second]),
            by_cols(slabs[:, :, second:]),
        ],
        0,
    )


def swap_over(values, over_dp, over_tensor):
    dp, tensor = lax.axis_size("dp"), lax.axis_size("tensor")
    pairs = [
        (a * tensor + b, (a ^ over_dp) * tensor + (b ^ over_tensor))
        for a in range(dp)
        for b in range(tensor)
    ]
    return lax.ppermute(values, ("dp", "tensor"), pairs)


def merge(terms, outs, segments):
    chunk = D // PARTS

    def kernel(*refs):
        for out, row, col, rows, cols, parts in segments:

            def step(k, carry, out=out, row=row, col=col, cols=cols, parts=parts):
                pieces = [
                    refs[term][pl.ds(pl.multiple_of(at + k * chunk, 32), chunk), left : left + cols]
                    for term, at, left in parts
                ]
                if len(pieces) > 1:
                    value = sum(piece.astype(jnp.float32) for piece in pieces)
                else:
                    value = pieces[0]
                to = refs[len(terms) + out]
                to[pl.ds(pl.multiple_of(row + k * chunk, 32), chunk), col : col + cols] = (
                    value.astype(to.dtype)
                )
                return carry

            lax.fori_loop(0, rows // chunk, step, 0)

    spec = pl.BlockSpec(memory_space=pltpu.VMEM)
    size = sum(term.size for term in terms)
    return pl.pallas_call(
        kernel,
        in_specs=[spec] * len(terms),
        out_specs=[spec] * len(outs),
        out_shape=[jax.ShapeDtypeStruct((rows, cols), dtype) for rows, cols, dtype in outs],
        compiler_params=pltpu.CompilerParams(vmem_limit_bytes=VMEM_LIMIT),
        cost_estimate=pl.CostEstimate(flops=size, bytes_accessed=4 * size, transcendentals=0),
    )(*terms)


def from_z(block):
    return [swap_over(block, 2 * k, 0) for k in (1, 2, 3)]


def over_core(blocks):
    return blocks + [swap_over(block, 0, 1) for block in blocks]


def put(out_ref, lead, row, col, ref, at, left, rows, cols):
    chunk = min(rows, D // 2)

    def step(k, carry):
        to = pl.multiple_of(row + k * chunk, 32)
        source = pl.multiple_of(at + k * chunk, 32)
        out_ref[lead, pl.ds(to, chunk), col : col + cols] = ref[
            pl.ds(source, chunk), left : left + cols
        ]
        return carry

    lax.fori_loop(0, rows // chunk, step, 0)


def place_first(refs, out_ref):
    count = len(refs) // 2
    half, width = D // 2, D // 4
    for core in range(2):
        near, beside, across = refs[core * count : (core + 1) * count]
        for y in range(2):
            col = (2 * y + core) * width
            for kind in range(2):
                left = kind * width
                put(out_ref, kind, 0, col, near, y * half, left, half, width)
                put(out_ref, kind, half, col, beside, y * half, left, half, width)
                if y:
                    put(out_ref, 2 + kind, 0, col, across, 0, left, D, width)
                else:
                    put(out_ref, 2 + kind, 0, col, near, 0, half + left, D, width)


def edges_moves():
    rows, half = D // PARTS, D // 2
    moves = []
    for core in range(2):
        near, beside, across = range(3 * core, 3 * core + 3)
        for y in range(2):
            group = 2 * y + core
            for z in range(4):
                for x in range(2):
                    to, by_y, by_x = x * half + z * rows, (2 * z + y) * rows, (2 * z + x) * rows
                    moves.append((group, to, 0, beside if x else near, by_y, 0, rows, half))
                    source = (across, by_x, 0) if y else (near, by_x, half)
                    moves.append((group, to, half, *source, rows, half))
    return moves


def plane_moves():
    half = D // 2
    return [
        (2 * y + core, x * half, 0, 4 * core + 2 * y + x, 0, 0, half, D)
        for core in range(2)
        for y in range(2)
        for x in range(2)
    ]


def groups_moves(count):
    return [(group, 0, 0, group, 0, 0, D, D) for group in range(count)]


def move_all(moves, refs, out_ref, sems):
    copies = [
        pltpu.make_async_copy(
            refs[ref].at[pl.ds(at, rows), pl.ds(left, cols)],
            out_ref.at[lead, pl.ds(row, rows), pl.ds(col, cols)],
            sems.at[k],
        )
        for k, (lead, row, col, ref, at, left, rows, cols) in enumerate(moves)
    ]
    for copy in copies:
        copy.start()
    for copy in copies:
        copy.wait()


def place_kinds(refs, out_ref):
    width = D // len(refs)
    for group, ref in enumerate(refs):
        for kind in range(4):
            put(out_ref, kind, 0, group * width, ref, 0, kind * width, D, width)


def core_terms(halves):
    odd, even = halves
    return [even.reshape(2 * D, D), swap_over(odd, 0, 1).reshape(2 * D, D)]


def summed(count, row, col):
    return [(term, row, col) for term in range(count)]


def reduce_core_plane(halves):
    half = D // 2
    return merge(
        core_terms(halves),
        [(half, D, jnp.bfloat16)] * 4,
        [(k, 0, 0, half, D, summed(2, k * half, 0)) for k in range(4)],
    )


def reduce_plane(near, beside, across, opposite):
    rows = D // PARTS
    terms = [near, swap_over(beside, 1, 0), swap_over(across, 0, 2), swap_over(opposite, 1, 2)]
    return merge(
        terms,
        [(rows, D, jnp.bfloat16)] * 4,
        [(k, 0, 0, rows, D, summed(4, k * rows, 0)) for k in range(4)],
    )


def z_terms(own, *sent):
    return [own] + [swap_over(block, 2 * (k + 1), 0) for k, block in enumerate(sent)]


def reduce_z(terms):
    rows = D // PARTS
    return merge(terms, [(rows, D, jnp.float32)], [(0, 0, 0, rows, D, summed(4, 0, 0))])[0]


def reduce_core_edges(halves):
    half = D // 2
    return merge(
        core_terms(halves),
        [(D, D, jnp.bfloat16), (D, half, jnp.bfloat16), (D, half, jnp.bfloat16)],
        [
            (0, 0, 0, half, half, summed(2, 0, 0)),
            (0, half, 0, half, half, summed(2, D, 0)),
            (0, 0, half, D, half, summed(2, 0, half)),
            (1, 0, 0, half, half, summed(2, half, 0)),
            (1, half, 0, half, half, summed(2, D + half, 0)),
            (2, 0, 0, D, half, summed(2, D, half)),
        ],
    )


def edge_terms(near, left, right):
    return [near, swap_over(left, 1, 0), swap_over(right, 0, 2)]


def edge_sums(row):
    half = D // 2
    return ((0, [(0, row, 0), (1, row, 0)]), (half, [(0, row, half), (2, row, 0)]))


def plane_edge_terms(near, left, right):
    return [near, swap_over(left, 0, 2), swap_over(right, 1, 0)]


def reduce_edges_plane(terms):
    half = D // 2
    kept = [(0, 0, col, half, half, parts) for col, parts in edge_sums(0)]
    sent = [
        (1 + k, 0, 0, half, half, parts) for k, (_, parts) in enumerate(edge_sums(half))
    ]
    return merge(
        terms,
        [(half, D, jnp.bfloat16), (half, half, jnp.bfloat16), (half, half, jnp.bfloat16)],
        kept + sent,
    )


def reduce_plane_edges(terms):
    rows, half = D // PARTS, D // 2
    return merge(
        terms,
        [(rows, D, jnp.bfloat16)] * 4,
        [
            (k, 0, col, rows, half, parts)
            for k in range(4)
            for col, parts in edge_sums(k * rows)
        ],
    )


def reduce_edges(terms):
    rows, half = D // PARTS, D // 2
    return merge(
        terms,
        [(2 * rows, D, jnp.bfloat16)] * 4,
        [
            (k, q * rows, col, rows, half, parts)
            for k in range(4)
            for q in range(2)
            for col, parts in edge_sums(q * half + k * rows)
        ],
    )


def reduce_edges_z(terms):
    rows, half = D // PARTS, D // 2
    return merge(
        terms,
        [(rows, D, jnp.bfloat16), (rows, half, jnp.bfloat16), (rows, half, jnp.bfloat16)],
        [
            (0, 0, 0, rows, D, summed(4, 0, 0)),
            (1, 0, 0, rows, half, summed(4, rows, 0)),
            (2, 0, 0, rows, half, summed(4, rows, half)),
        ],
    )


def reduce_edges_last(terms):
    rows, half = D // PARTS, D // 2
    return merge(
        terms,
        [(rows, D, jnp.float32)],
        [(0, 0, col, rows, half, parts) for col, parts in edge_sums(0)],
    )[0]


def add_swapped(values, over_dp, over_tensor):
    return values + swap_over(values, over_dp, over_tensor)


ROWS = 256


def dot_nt(left_side, right_side):
    return lax.dot_general(
        left_side, right_side, (((1,), (1,)), ((), ())), preferred_element_type=jnp.float32
    )


def row_block(array):
    return pl.BlockSpec((ROWS, array.shape[1]), lambda i: (i, 0))


def call_rows(kernel, steps, inputs, outputs, flops, transcendentals=0, scratch=()):
    arrays = [
        pltpu.with_memory_space_constraint(array, pltpu.HBM) if far else array
        for array, _, *far in inputs
    ]
    shapes = [jax.ShapeDtypeStruct(shape, dtype) for shape, dtype, *_ in outputs]
    moved = sum(a.size * a.dtype.itemsize for a in arrays + shapes)
    shapes = [
        pltpu.HBM(shape.shape, shape.dtype) if len(output) > 3 else shape
        for shape, output in zip(shapes, outputs)
    ]
    return pl.pallas_call(
        kernel,
        grid=(steps,),
        in_specs=[spec for _, spec, *_ in inputs],
        out_specs=[output[2] for output in outputs],
        out_shape=shapes,
        scratch_shapes=scratch,
        compiler_params=pltpu.CompilerParams(vmem_limit_bytes=VMEM_LIMIT),
        cost_estimate=pl.CostEstimate(
            flops=int(1.0 * flops), bytes_accessed=moved, transcendentals=transcendentals
        ),
    )(*arrays)


def norm_rows(summed):
    centred = summed - jnp.mean(summed, -1, keepdims=True)
    inverse = lax.rsqrt(jnp.mean(centred * centred, -1, keepdims=True) + NORM_EPS)
    return centred * inverse, inverse


def norm_pull(gradient, unit_rows, inverse, gain_row):
    scaled = gradient * gain_row
    return inverse * (
        scaled
        - jnp.mean(scaled, -1, keepdims=True)
        - unit_rows * jnp.mean(scaled * unit_rows, -1, keepdims=True)
    )


def add_rows(ref, rows):
    sums = [jnp.sum(row, 0, keepdims=True) for row in rows]
    start = pl.program_id(0) == 0
    for place, total in enumerate(sums):
        kept = jnp.where(start, 0.0, ref[place : place + 1, :])
        ref[place : place + 1, :] = kept + total


def settle(moves, refs, whole_ref, sems):
    @pl.when(pl.program_id(0) == 0)
    def _():
        move_all(moves, refs, whole_ref, sems)

    return [whole_ref.at[j] for j in range(whole_ref.shape[0])]


def pair_masks(length):
    wide = 2 * HEAD_DIM
    lower = lax.broadcasted_iota(jnp.int32, (length, wide), 1) < HEAD_DIM
    top = lax.broadcasted_iota(jnp.int32, (2 * length, wide), 0) < length
    left = lax.broadcasted_iota(jnp.int32, (2 * length, wide), 1) < HEAD_DIM
    return lower, top == left


def stacked(pair, own):
    return jnp.where(own, jnp.concatenate([pair, pair], 0), jnp.zeros((), pair.dtype))


def attention_kernel(place, total_count, length, *refs):
    rows_ref, across_ref, down_ref, bias_ref, vec_ref = refs[:5]
    outs = refs[5 + total_count : 12 + total_count]
    packed_ref, probs_ref, attended_ref, unit_ref, inverse_ref, low_ref, whole_ref = outs
    scores_ref, sems, *raw = refs[12 + total_count :]

    @pl.when(pl.program_id(0) == 0)
    def _():
        copies = [
            pltpu.make_async_copy(source, to, sems.at[k])
            for k, (source, to) in enumerate(zip(refs[5 : 5 + total_count], raw))
        ]
        for copy in copies:
            copy.start()
        for copy in copies:
            copy.wait()
        place(raw, whole_ref)

    weights = [whole_ref.at[kind] for kind in range(4)]
    wide = 2 * HEAD_DIM
    pairs = HEADS // 2
    rows = rows_ref[...]
    for kind in range(3):
        part = product(rows, weights[kind][...]) + bias_ref[kind : kind + 1, :]
        part = part.astype(jnp.bfloat16)
        if kind == 0:
            part = part * jnp.bfloat16(HEAD_DIM ** (-0.5))
        packed_ref[:, kind * D : (kind + 1) * D] = part
    _, own = pair_masks(length)
    ones = own.astype(jnp.bfloat16)
    steps = [(p, i) for p in range(ROWS // length) for i in range(pairs)]

    def pair_of(p, i, kind):
        span = slice(p * length, (p + 1) * length)
        return packed_ref[span, kind * D + i * wide : kind * D + (i + 1) * wide]

    for at, (p, i) in enumerate(steps):
        scores_ref[at] = dot_nt(pair_of(p, i, 0), stacked(pair_of(p, i, 1), own))
    for at, (p, i) in enumerate(steps):
        allowed = down_ref[p] == across_ref[p]
        for half in range(2):
            lanes = slice(half * length, (half + 1) * length)
            scores = jnp.where(allowed, scores_ref[at, :, lanes], MASKED)
            probs_ref[p, i, :, lanes] = jnp.exp(
                scores - jnp.max(scores, -1, keepdims=True)
            ).astype(jnp.bfloat16)
    for p, i in steps:
        mixed = product(
            probs_ref[p, i], jnp.concatenate([stacked(pair_of(p, i, 2), own), ones], 1)
        )
        attended_ref[p * length : (p + 1) * length, i * wide : (i + 1) * wide] = (
            mixed[:, :wide] / mixed[:, wide:]
        ).astype(jnp.bfloat16)
    summed = rows.astype(jnp.float32) + vec_ref[0:1, :]
    summed = summed + dot_nt(attended_ref[...], weights[3][...])
    unit, inverse = norm_rows(summed)
    unit_ref[...] = unit
    inverse_ref[...] = inverse
    low_ref[...] = (unit * vec_ref[1:2, :] + vec_ref[2:3, :]).astype(jnp.bfloat16)


def gelu_parts(values):
    size = jnp.abs(values)
    decay = jnp.exp2(values * values * (-0.5 / math.log(2.0)))
    t = 1.0 / (1.0 + size * (0.3275911 * 0.5**0.5))
    poly = t * (
        0.127414796
        + t * (-0.142248368 + t * (0.7107068705 + t * (-0.7265760135 + t * 0.5307027145)))
    )
    result = jnp.maximum(values, 0.0) - size * (poly * decay)
    rest = decay * (poly - size * (0.5 / math.pi) ** 0.5)
    return result, jnp.where(values > 0, 1.0 - rest, rest)


def up_kernel(place, shards, *refs):
    low_ref, bias_ref = refs[:2]
    act_ref, slope_ref, whole_ref, sems = refs[-4:]
    weights = settle(place, refs[2:-4], whole_ref, sems)
    width = weights[0].shape[1]
    chunk = 256
    low = low_ref[...]
    for j in range(shards):
        for c in range(0, width, chunk):
            pre = product(low, weights[j][:, c : c + chunk]) + bias_ref[j : j + 1, c : c + chunk]
            result, slope = gelu_parts(pre)
            at = j * width + c
            act_ref[:, at : at + chunk] = result.astype(jnp.bfloat16)
            slope_ref[:, at : at + chunk] = slope.astype(jnp.bfloat16)


def down_kernel(place, shards, *refs):
    act_ref, unit_ref, grad_ref, vec_ref = refs[:4]
    out_ref, dz_ref, low_ref, sums_ref, whole_ref, sems = refs[-6:]
    weights = settle(place, refs[4:-6], whole_ref, sems)
    width = weights[0].shape[1]
    summed = unit_ref[...] * vec_ref[1:2, :] + vec_ref[2:3, :] + vec_ref[3:4, :]
    for j in range(shards):
        summed = summed + dot_nt(act_ref[:, j * width : (j + 1) * width], weights[j][...])
    unit, inverse = norm_rows(summed)
    gain = vec_ref[4:5, :]
    out_ref[...] = unit * gain + vec_ref[5:6, :]
    gradient = grad_ref[...]
    dz = norm_pull(gradient, unit, inverse, gain)
    dz_ref[...] = dz
    low_ref[...] = dz.astype(jnp.bfloat16)
    add_rows(sums_ref, (gradient * unit, gradient, dz))


def hidden_back_kernel(shards, *refs):
    low_ref, slope_ref, whole_ref, dpre_ref, bias_sums_ref = refs
    width = whole_ref.shape[2]
    low = low_ref[...]
    for j in range(shards):
        span = slice(j * width, (j + 1) * width)
        dpre = product(low, whole_ref[j]) * slope_ref[:, span].astype(jnp.float32)
        dpre = dpre.astype(jnp.bfloat16)
        dpre_ref[:, span] = dpre
        total = jnp.sum(dpre.astype(jnp.float32), 0, keepdims=True)
        kept = jnp.where(pl.program_id(0) == 0, 0.0, bias_sums_ref[j : j + 1, :])
        bias_sums_ref[j : j + 1, :] = kept + total


def back_kernel(shards, *refs):
    dpre_ref, dz_ref, unit_ref, inverse_ref, vec_ref, up_ref, first_ref = refs[:7]
    dz1_ref, low1_ref, datt_ref, sums_ref = refs[7:]
    width = up_ref.shape[2]
    gradient = dz_ref[...]
    for j in range(shards):
        gradient = gradient + dot_nt(dpre_ref[:, j * width : (j + 1) * width], up_ref[j])
    unit = unit_ref[...]
    dz1 = norm_pull(gradient, unit, inverse_ref[...], vec_ref[1:2, :])
    dz1_ref[...] = dz1
    low1 = dz1.astype(jnp.bfloat16)
    low1_ref[...] = low1
    add_rows(sums_ref, (gradient * unit, gradient, dz1))
    datt_ref[...] = product(low1, first_ref[3]).astype(jnp.bfloat16)


def attention_back_kernel(length, *refs):
    datt_ref, attended_ref, packed_ref, probs_ref, dpacked_ref, sums_ref, up_ref, grad_ref = refs
    wide = 2 * HEAD_DIM
    lower, own = pair_masks(length)
    ones = own.astype(jnp.bfloat16)
    steps = [(p, i) for p in range(ROWS // length) for i in range(HEADS // 2)]

    def pair_of(p, i, kind):
        span = slice(p * length, (p + 1) * length)
        return packed_ref[span, kind * D + i * wide : kind * D + (i + 1) * wide]

    def keep(p, i, kind, grad):
        span = slice(p * length, (p + 1) * length)
        dpacked_ref[span, kind * D + i * wide : kind * D + (i + 1) * wide] = grad.astype(
            jnp.bfloat16
        )

    for place, (p, i) in enumerate(steps):
        span = slice(p * length, (p + 1) * length)
        lanes = slice(i * wide, (i + 1) * wide)
        upstream = datt_ref[span, lanes].astype(jnp.float32) / product(probs_ref[p, i], ones)
        up_ref[place, :, :wide] = upstream.astype(jnp.bfloat16)
        up_ref[place, :, wide:] = (upstream * attended_ref[span, lanes].astype(jnp.float32)).astype(
            jnp.bfloat16
        )
    for place, (p, i) in enumerate(steps):
        centred = dot_nt(
            up_ref[place], jnp.concatenate([stacked(pair_of(p, i, 2), own), -ones], 1)
        )
        grad_ref[place] = (probs_ref[p, i].astype(jnp.float32) * centred).astype(jnp.bfloat16)
    for place, (p, i) in enumerate(steps):
        grad_scores = grad_ref[place]
        keep(
            p, i, 0,
            product(grad_scores, stacked(pair_of(p, i, 1), own)) * HEAD_DIM ** (-0.5),
        )
        both = transposed_times(grad_scores, pair_of(p, i, 0))
        keep(p, i, 1, jnp.where(lower, both[:length], both[length:]))
        both = transposed_times(probs_ref[p, i], up_ref[place, :, :wide])
        keep(p, i, 2, jnp.where(lower, both[:length], both[length:]))
    total = jnp.sum(dpacked_ref[...].astype(jnp.float32), 0, keepdims=True)
    kept = jnp.where(pl.program_id(0) == 0, 0.0, sums_ref[0:1, :])
    sums_ref[0:1, :] = kept + total


def weight_kernel(odd, count, *refs):
    lefts, refs = refs[:2] if count > 1 else refs[:1], refs[2 if count > 1 else 1 :]
    rights, (out_ref, *turned) = refs[:count], refs[count:]
    start = pl.program_id(0) == 0

    @pl.when(start)
    def _():
        for left, kept in zip(lefts, turned):
            kept[...] = left[...].T

    at = 0
    for place, right in enumerate(rights):
        half = right.shape[1] // 2
        values = right[...] if count == 1 else right[:, half:] if odd else right[:, :half]
        grad = product(turned[place == count - 1 and count > 1][...], values)
        out_ref[0, :, at : at + values.shape[1]] = grad.astype(jnp.bfloat16)
        at += values.shape[1]


def weight_halves(lefts, rights):
    halves = []
    for odd in (1, 0):
        count = len(rights)
        single = count == 1
        specs = []
        for array, width, before in rights:
            if single:
                specs.append(pl.BlockSpec((array.shape[0], width), lambda i: (0, 2 * i + odd)))
            else:
                specs.append(
                    pl.BlockSpec((array.shape[0], 2 * width), lambda i, b=before: (0, b + i))
                )
        arrays = [
            *lefts,
            *[
                array if single else pltpu.with_memory_space_constraint(array, pltpu.HBM)
                for array, _, _ in rights
            ],
        ]
        tokens = lefts[0].shape[0]
        (half,) = pl.pallas_call(
            functools.partial(weight_kernel, odd, count),
            grid=(2,),
            in_specs=[pl.BlockSpec(memory_space=pltpu.VMEM) for _ in lefts] + specs,
            out_specs=[pl.BlockSpec((1, D, D), lambda i: (i, 0, 0))],
            out_shape=[jax.ShapeDtypeStruct((2, D, D), jnp.bfloat16)],
            scratch_shapes=[pltpu.VMEM((D, tokens), jnp.bfloat16) for _ in lefts],
            compiler_params=pltpu.CompilerParams(vmem_limit_bytes=VMEM_LIMIT),
            cost_estimate=pl.CostEstimate(
                flops=4 * tokens * D * D,
                bytes_accessed=sum(2 * array.size for array in arrays),
                transcendentals=0,
            ),
        )(*arrays)
        halves.append(half)
    return halves


def two_terms(values):
    top = values.astype(jnp.bfloat16)
    return top, (values - top.astype(jnp.float32)).astype(jnp.bfloat16)


def adam_kernel(*refs):
    grad_ref, master_ref, left_ref, right_ref, first_ref, second_ref = refs[:6]
    master_out, first_out, second_out = refs[6:]
    bias_first = 1.0 - DECAY_FIRST**ADAM_STEP
    bias_second = 1.0 - DECAY_SECOND**ADAM_STEP
    count = grad_ref.shape[0]
    lefts = [two_terms(left_ref[k]) for k in range(count)]
    rights = [two_terms(right_ref[k]) for k in range(count)]
    turned = []
    for k in range(count):
        grad = product(grad_ref[k].astype(jnp.bfloat16), rights[k][0])
        grad = grad + product(grad_ref[k].astype(jnp.bfloat16), rights[k][1])
        if grad_ref.dtype != jnp.bfloat16:
            grad = grad + product(two_terms(grad_ref[k])[1], rights[k][0])
        turned.append(grad)
    directions = []
    for k in range(count):
        top, rest = two_terms(turned[k])
        rotated = (
            transposed_times(lefts[k][0], top)
            + transposed_times(lefts[k][0], rest)
            + transposed_times(lefts[k][1], top)
        )
        first = DECAY_FIRST * first_ref[k] + (1.0 - DECAY_FIRST) * rotated
        second = DECAY_SECOND * second_ref[k] + (1.0 - DECAY_SECOND) * rotated * rotated
        first_out[k] = first
        second_out[k] = second
        directions.append(first / bias_first / (jnp.sqrt(second / bias_second) + ADAM_EPS))
    backs = [
        product(lefts[k][0], directions[k].astype(jnp.bfloat16)).astype(jnp.bfloat16)
        for k in range(count)
    ]
    for k in range(count):
        update = times_transposed(backs[k], rights[k][0])
        master_out[k] = master_ref[k] - MATRIX_RATE * update


def two_terms(values):
    top = values.astype(jnp.bfloat16)
    return top, (values - top.astype(jnp.float32)).astype(jnp.bfloat16)


def unpermuted(values, selector_ref):
    top, rest = two_terms(values)
    return dot_nt(top, selector_ref[...]) + dot_nt(rest, selector_ref[...])


def enter_kernel(tokens_ref, grad_ref, vectors_ref, selector_ref, rows_ref, out_ref, d_rows_ref):
    selector = selector_ref[...]
    rows_ref[...] = product(tokens_ref[...], selector).astype(jnp.bfloat16)
    top, rest = two_terms(grad_ref[...])
    out_ref[...] = product(top, selector) + product(rest, selector)

    @pl.when(pl.program_id(0) == 0)
    def _():
        rows = vectors_ref[...]
        permuted = jnp.zeros(rows.shape, jnp.float32)
        for _ in range(3):
            term = rows.astype(jnp.bfloat16)
            rows = rows - term.astype(jnp.float32)
            permuted = permuted + product(term, selector)
        d_rows_ref[...] = permuted


def layer_kernel(out_ref, selector_ref, layer_ref):
    layer_ref[...] = unpermuted(out_ref[...], selector_ref)


def input_kernel(dz1_ref, dpacked_ref, selector_ref, whole_ref, input_ref):
    gradient = dz1_ref[...]
    for kind in range(3):
        gradient = gradient + dot_nt(dpacked_ref[:, kind * D : (kind + 1) * D], whole_ref[kind])
    input_ref[...] = unpermuted(gradient, selector_ref)


def vector_kernel(shards, *refs):
    base_ref, first_ref, second_ref, hidden_ref, columns_ref, selector_ref, out_ref = refs
    base = base_ref[0]
    rows = jnp.concatenate(
        [
            first_ref[0:1, :],
            second_ref[0:1, :],
            first_ref[2:3, :],
            second_ref[2:3, :],
            first_ref[1:2, :],
            second_ref[1:2, :],
            jnp.zeros((2, D), jnp.float32),
        ],
        0,
    )
    natural = jnp.zeros((8, D), jnp.float32)
    for _ in range(3):
        term = rows.astype(jnp.bfloat16)
        rows = rows - term.astype(jnp.float32)
        natural = natural + dot_nt(term, selector_ref[...])
    hidden = FF // D
    out_ref[...] = jnp.zeros(out_ref.shape, jnp.float32)
    for at, row in ((0, 0), (1, 1), (4, 2), (5 + hidden, 3), (6 + hidden, 4), (7 + hidden, 5)):
        out_ref[at : at + 1, :] = natural[row : row + 1, :]
    width = D // shards
    for j in range(shards):
        out_ref[5 + j : 6 + j, :] = hidden_ref[pl.ds(j ^ base, 1), :]
        for at, kind in ((2, 0), (3, 2)):
            parts = [
                jnp.where(
                    (j ^ base) == k,
                    columns_ref[0:1, kind * D + k * width : kind * D + (k + 1) * width],
                    0.0,
                )
                for k in range(shards)
            ]
            out_ref[at : at + 1, j * width : (j + 1) * width] = sum(parts)


def adam_kernel(*refs):
    grad_ref, master_ref, left_ref, right_ref, first_ref, second_ref = refs[:6]
    master_out, first_out, second_out = refs[6:]
    bias_first = 1.0 - DECAY_FIRST**ADAM_STEP
    bias_second = 1.0 - DECAY_SECOND**ADAM_STEP
    count = grad_ref.shape[0]
    lefts = [two_terms(left_ref[k]) for k in range(count)]
    rights = [two_terms(right_ref[k]) for k in range(count)]
    turned = []
    for k in range(count):
        top, rest = two_terms(grad_ref[k].astype(jnp.float32))
        turned.append(
            product(top, rights[k][0]) + product(top, rights[k][1]) + product(rest, rights[k][0])
        )
    directions = []
    for k in range(count):
        top, rest = two_terms(turned[k])
        rotated = (
            transposed_times(lefts[k][0], top)
            + transposed_times(lefts[k][0], rest)
            + transposed_times(lefts[k][1], top)
        )
        first = DECAY_FIRST * first_ref[k] + (1.0 - DECAY_FIRST) * rotated
        second = DECAY_SECOND * second_ref[k] + (1.0 - DECAY_SECOND) * rotated * rotated
        first_out[k] = first
        second_out[k] = second
        directions.append(first / bias_first / (jnp.sqrt(second / bias_second) + ADAM_EPS))
    backs = []
    for k in range(count):
        top, rest = two_terms(directions[k])
        backs.append(
            product(lefts[k][0], top) + product(lefts[k][0], rest) + product(lefts[k][1], top)
        )
    for k in range(count):
        top, rest = two_terms(backs[k])
        update = (
            times_transposed(top, rights[k][0])
            + times_transposed(rest, rights[k][0])
            + times_transposed(top, rights[k][1])
        )
        master_out[k] = master_ref[k] - MATRIX_RATE * update


def natural_kernel(shards, *refs):
    out_ref, dz1_ref, dpacked_ref, selector_ref, whole_ref, layer_ref, input_ref = refs
    weights = [whole_ref.at[j] for j in range(shards)]
    head_width = D // shards
    gradient = dz1_ref[...]
    for j in range(shards):
        own = [
            dpacked_ref[:, kind * D + j * head_width : kind * D + (j + 1) * head_width]
            for kind in range(3)
        ]
        gradient = gradient + dot_nt(jnp.concatenate(own, 1), weights[j][:, : 3 * head_width])
    for source, ref in ((out_ref[...], layer_ref), (gradient, input_ref)):
        top = source.astype(jnp.bfloat16)
        rest = (source - top.astype(jnp.float32)).astype(jnp.bfloat16)
        ref[...] = dot_nt(top, selector_ref[...]) + dot_nt(rest, selector_ref[...])


def together(*values):
    return lax.optimization_barrier(values)


def local(
    tokens,
    segments,
    out_grad,
    owner,
    master,
    left_basis,
    right_basis,
    first_moment,
    second_moment,
    vectors,
    vector_first,
    vector_second,
):
    shards = lax.axis_size("tensor")
    dp_size = lax.axis_size("dp")
    direct = dp_size == PARTS and shards == 4
    tensor_rank = lax.axis_index("tensor")
    dp_rank = lax.axis_index("dp")
    local_heads = HEADS // shards
    head_width = local_heads * HEAD_DIM
    up_width = FF // shards
    width_qkv = 3 * head_width
    block_size = master.shape[-1]
    slots = master.shape[1]
    row_count = tokens.shape[0]
    length = segments.shape[1]
    pack_count = row_count // length
    own_segments = lax.dynamic_slice_in_dim(segments, tensor_rank * pack_count, pack_count, 0)
    qkv_tiles, out_tiles, up_tiles = tile_counts(shards, block_size)
    tile_total = owner.shape[0]

    group_base = tensor_rank if direct else 0
    order = feature_order(dp_rank if direct else 0)
    selector = (lax.iota(jnp.int32, D)[:, None] == order[None, :]).astype(jnp.bfloat16)

    steps = row_count // ROWS
    f32, bf16 = jnp.float32, jnp.bfloat16
    rows_spec = lambda width: pl.BlockSpec((ROWS, width), lambda i: (i, 0))
    full = lambda array: (array, pl.BlockSpec(memory_space=pltpu.VMEM))
    raw = lambda array: (array, pl.BlockSpec(memory_space=pl.ANY))
    by_rows = lambda array: (array, row_block(array))
    far_rows = lambda array: (array, row_block(array), "far")
    group_order = lax.iota(jnp.int32, shards) ^ group_base
    below = vectors[: 5 * D].reshape(5, D)
    above = vectors[5 * D + FF :].reshape(3, D)
    d_rows = jnp.stack(
        [below[4], below[0], above[1], above[0], below[1], above[2], below[0], below[0]]
    )
    bias_q = below[2].reshape(shards, head_width)[group_order]
    bias_v = below[3].reshape(shards, head_width)[group_order]
    bias_up = vectors[5 * D : 5 * D + FF].reshape(shards, up_width)[group_order]
    rows_in, grad_out, d_rows = call_rows(
        enter_kernel,
        steps,
        [far_rows(tokens), far_rows(out_grad), full(d_rows), full(selector)],
        [
            ((row_count, D), bf16, rows_spec(D), "far"),
            ((row_count, D), f32, rows_spec(D), "far"),
            ((8, D), f32, pl.BlockSpec(memory_space=pltpu.VMEM)),
        ],
        6 * row_count * D * D,
    )

    def flipped(index):
        from_out = (index >= qkv_tiles) & (index < qkv_tiles + out_tiles)
        return (from_out | (index >= qkv_tiles + out_tiles + up_tiles))[:, None, None]

    own_tiles = lax.dynamic_slice_in_dim(owner, dp_rank * slots, slots, 0)
    own_flip = flipped(own_tiles)
    sent = master[0].astype(jnp.bfloat16)
    sent = jnp.where(own_flip, jnp.swapaxes(sent, 1, 2), sent)
    placing = (lax.iota(jnp.int32, tile_total)[:, None] == owner[None, :]).astype(jnp.bfloat16)
    if direct:
        parts = sent.reshape(slots, PARTS, SUB * block_size).swapaxes(0, 1)
        parts = lax.all_to_all(parts, "dp", 0, 0, tiled=True).reshape(tile_total, -1)
        tiles = product(placing, parts).astype(jnp.bfloat16)
        slab = slabs_from_tiles(tiles.reshape(tile_total, 1, SUB, block_size), shards, block_size)[0]
        half, rows = D // 2, D // PARTS
        first_slab, up_slab, down_slab = (slab[:, k * D : (k + 1) * D] for k in range(3))
        near_left, near_right = down_slab[:, :half], down_slab[:, half:]
        *blocks, near_left, near_right, rows_in, grad_out, d_rows, bias_up = together(
            *from_z(first_slab),
            swap_over(near_left, 0, 2),
            swap_over(near_right, 1, 0),
            rows_in,
            grad_out,
            d_rows,
            bias_up,
        )
        left, right, down_near = merge(
            [first_slab, *blocks, down_slab, near_left, near_right],
            [(half, half, bf16), (half, half, bf16), (2 * rows, D, bf16)],
            [(k, z * rows, 0, rows, half, [(z, 0, k * half)]) for k in range(2) for z in range(4)]
            + [
                (2, 0, 0, rows, D, [(4, 0, 0)]),
                (2, rows, 0, rows, half, [(5, 0, 0)]),
                (2, rows, half, rows, half, [(6, 0, 0)]),
            ],
        )
        left, right, down_near, up_slab = together(left, right, down_near, up_slab)
        up_beside, down_beside = swap_over(up_slab, 2, 0), swap_over(down_near, 2, 0)
        left_across, right_beside, up_beside = together(
            swap_over(left, 0, 2), swap_over(right, 1, 0), up_beside
        )
        near, left, right, up_pair = merge(
            [left, left_across, right, right_beside, up_slab, up_beside],
            [(D, D, bf16), (D, half, bf16), (D, half, bf16), (2 * rows, D, bf16)],
            [
                (out, q * half, col, half, half, [(2 * k + q, 0, 0)])
                for k in range(2)
                for q in range(2)
                for out, col in ((0, k * half), (1 + k, 0))
            ]
            + [(3, z * rows, 0, rows, D, [(4 + z, 0, 0)]) for z in range(2)],
        )
        near_there, beside, across, up_far, down_beside = together(
            swap_over(near, 0, 1),
            swap_over(left, 1, 0),
            swap_over(right, 0, 2),
            swap_over(up_pair, 4, 0),
            down_beside,
        )
        up_z, down_pair = merge(
            [up_pair, up_far, down_near, down_beside],
            [(half, D, bf16)] * 2,
            [
                (k, z * 2 * rows, 0, 2 * rows, D, [(2 * k + z, 0, 0)])
                for k in range(2)
                for z in range(2)
            ],
        )
        first = [near, beside, across, near_there] + over_core([beside, across])[2:]
        up = [up_z, swap_over(up_z, 1, 0), swap_over(up_z, 0, 2), swap_over(up_z, 1, 2)]
        down_far = swap_over(down_pair, 4, 0)
        places = (place_first, plane_moves(), edges_moves())
        pieces = [first, None, None]
    else:
        gathered = lax.all_gather(sent, "dp", axis=0, tiled=True).reshape(tile_total, -1)
        tiles = product(placing, gathered).astype(jnp.bfloat16)
        slabs = slabs_from_tiles(
            tiles.reshape(tile_total, PARTS, SUB, block_size), shards, block_size
        )
        whole = jnp.concatenate([slabs[part_of_block(k)] for k in range(PARTS)], 0)
        every = lax.all_gather(whole, "tensor", axis=0)
        pieces = [
            [every[j][:, k * D : (k + 1) * D] for j in range(shards)] for k in range(3)
        ]
        places = (place_kinds, groups_moves(shards), groups_moves(shards))

    packs_step = ROWS // length
    bias_qkv = jnp.stack(
        [bias_q.reshape(D), jnp.zeros((D,), jnp.float32), bias_v.reshape(D)]
    )
    pairs = HEADS // 2
    probs_spec = pl.BlockSpec((packs_step, pairs, length, 2 * length), lambda i: (i, 0, 0, 0))
    sums_spec = lambda width: pl.BlockSpec((8, width), lambda i: (0, 0))
    square = 2 * row_count * D * D

    whole_out = ((shards, D, D), bf16, pl.BlockSpec(memory_space=pltpu.VMEM))
    packed, probs, attended, unit_first, inverse_first, normed_low, whole_first = call_rows(
        functools.partial(attention_kernel, places[0], len(pieces[0]), length),
        steps,
        [
            far_rows(rows_in),
            (own_segments[:, None, :], pl.BlockSpec((packs_step, 1, length), lambda i: (i, 0, 0))),
            (own_segments[:, :, None], pl.BlockSpec((packs_step, length, 1), lambda i: (i, 0, 0))),
            full(bias_qkv),
            full(d_rows),
            *[raw(w) + (("far",) if w.shape == (D, D) else ()) for w in pieces[0]],
        ],
        [
            ((row_count, 3 * D), bf16, rows_spec(3 * D), "far"),
            ((pack_count, pairs, length, 2 * length), bf16, probs_spec, "far"),
            ((row_count, D), bf16, rows_spec(D), "far"),
            ((row_count, D), f32, rows_spec(D), "far"),
            ((row_count, 1), f32, rows_spec(1), "far"),
            ((row_count, D), bf16, rows_spec(D), "far"),
            whole_out,
        ],
        4 * square + 4 * row_count * length * D,
        row_count * length * HEADS,
        [
            pltpu.VMEM((packs_step * pairs, length, 2 * length), f32),
            pltpu.SemaphoreType.DMA((len(pieces[0]),)),
            *[pltpu.VMEM(w.shape, bf16) for w in pieces[0]],
        ],
    )
    if direct:
        *up, up_there, down_far, normed_low = together(
            *up, swap_over(up[0], 0, 1), down_far, normed_low
        )
        down_near, near_left, near_right = merge(
            [down_pair, down_far],
            [(D, D, bf16), (D, half, bf16), (D, half, bf16)],
            [(0, z * half, 0, half, D, [(z, 0, 0)]) for z in range(2)]
            + [
                (1 + k, z * half, 0, half, half, [(z, 0, k * half)])
                for k in range(2)
                for z in range(2)
            ],
        )
        down = [down_near, swap_over(near_left, 1, 0), swap_over(near_right, 0, 2)]
        pieces[1] = up + [up_there] + over_core(up[1:])[3:]
    activated, slope, whole_up = call_rows(
        functools.partial(up_kernel, places[1], shards),
        steps,
        [far_rows(normed_low), full(bias_up), *[raw(w) for w in pieces[1]]],
        [
            ((row_count, FF), bf16, rows_spec(FF)),
            ((row_count, FF), bf16, rows_spec(FF), "far"),
            whole_out,
        ],
        4 * square,
        2 * row_count * FF,
        [pltpu.SemaphoreType.DMA((len(places[1]),))],
    )
    if direct:
        *down, activated = together(*down, activated)
        pieces[2] = over_core(down)
    layer_out, grad_second, second_low, sums_second, whole_down = call_rows(
        functools.partial(down_kernel, places[2], shards),
        steps,
        [
            by_rows(activated),
            far_rows(unit_first),
            far_rows(grad_out),
            full(d_rows),
            *[raw(w) for w in pieces[2]],
        ],
        [
            ((row_count, D), f32, rows_spec(D), "far"),
            ((row_count, D), f32, rows_spec(D), "far"),
            ((row_count, D), bf16, rows_spec(D)),
            ((8, D), f32, sums_spec(D)),
            whole_out,
        ],
        4 * square,
        0,
        [pltpu.SemaphoreType.DMA((len(places[2]),))],
    )
    grad_w_down = weight_halves([second_low], [(activated, up_width, 0)])
    if direct:
        down_parts = reduce_core_plane(grad_w_down)
        second_low, *down_parts = together(second_low, *down_parts)
        down_parts = reduce_plane(*down_parts)
    grad_pre, grad_bias_up = call_rows(
        functools.partial(hidden_back_kernel, shards),
        steps,
        [by_rows(second_low), far_rows(slope), full(whole_down)],
        [((row_count, FF), bf16, rows_spec(FF)), ((8, up_width), f32, sums_spec(up_width))],
        4 * square,
    )
    grad_w_up = weight_halves([normed_low], [(grad_pre, up_width, 0)])
    grad_first, first_low, grad_attended, sums_first = call_rows(
        functools.partial(back_kernel, shards),
        steps,
        [
            by_rows(grad_pre),
            far_rows(grad_second),
            far_rows(unit_first),
            far_rows(inverse_first),
            full(d_rows),
            full(whole_up),
            full(whole_first),
        ],
        [
            ((row_count, D), f32, rows_spec(D), "far"),
            ((row_count, D), bf16, rows_spec(D), "far"),
            ((row_count, D), bf16, rows_spec(D)),
            ((8, D), f32, sums_spec(D)),
        ],
        20 * square,
    )
    if direct:
        up_parts = reduce_core_edges(grad_w_up)
        grad_attended, *parts = together(grad_attended, *up_parts, *down_parts)
        up_terms = edge_terms(*parts[:3])
        down_terms = z_terms(*parts[3:])
    grad_packed, column_sums = call_rows(
        functools.partial(attention_back_kernel, length),
        steps,
        [by_rows(grad_attended), far_rows(attended), far_rows(packed), (probs, probs_spec, "far")],
        [
            ((row_count, 3 * D), bf16, rows_spec(3 * D), "far"),
            ((8, 3 * D), f32, sums_spec(3 * D)),
        ],
        8 * square,
        0,
        [pltpu.VMEM((packs_step * pairs, length, 2 * length), bf16)] * 2,
    )
    (vector_rows,) = call_rows(
        functools.partial(vector_kernel, shards),
        1,
        [
            (
                lax.convert_element_type(group_base, jnp.int32).reshape(1),
                pl.BlockSpec(memory_space=pltpu.SMEM),
            ),
            full(sums_first),
            full(sums_second),
            full(grad_bias_up),
            full(column_sums),
            full(selector),
        ],
        [((16, D), f32, pl.BlockSpec(memory_space=pltpu.VMEM))],
        48 * D * D,
    )
    if direct:
        vector_rows, grad_packed, *others = together(
            vector_rows, grad_packed, *down_terms, *up_terms
        )
        down_terms, up_terms = others[:4], others[4:]
        up_terms = z_terms(*reduce_edges(up_terms))
        down_own = reduce_z(down_terms)
    else:
        vector_rows = lax.psum(vector_rows, ("dp", "tensor"))
    grad_w_first = weight_halves(
        [rows_in, first_low],
        [(grad_packed, head_width, k * shards // 2) for k in range(3)] + [(attended, head_width, 0)],
    )
    if direct:
        first_parts = reduce_core_edges(grad_w_first)
        *first_parts, grad_first = together(*first_parts, grad_first)
        first_terms = edge_terms(*first_parts)
    (input_grad,) = call_rows(
        input_kernel,
        steps,
        [far_rows(grad_first), far_rows(grad_packed), full(selector), full(whole_first)],
        [((row_count, D), f32, rows_spec(D), "far")],
        5 * square,
    )
    if direct:
        *first_terms, input_grad, layer_out = together(*first_terms, input_grad, layer_out)
        first_terms = plane_edge_terms(*reduce_edges_plane(first_terms))
    (layer_out,) = call_rows(
        layer_kernel,
        steps,
        [far_rows(layer_out), full(selector)],
        [((row_count, D), f32, rows_spec(D), "far")],
        2 * square,
    )
    if direct:
        *others, layer_out = together(*first_terms, *up_terms, layer_out)
        first_terms, up_terms = others[:3], others[3:]
        *parts, vector_rows = together(*reduce_plane_edges(first_terms), vector_rows)
        first_terms = z_terms(*parts)
        vector_rows = add_swapped(add_swapped(vector_rows, 0, 1), 0, 2)
        up_terms = plane_edge_terms(*reduce_edges_z(up_terms))
        up_own = reduce_edges_last(up_terms)
        *first_terms, vector_rows = together(*first_terms, vector_rows)
        first_own = reduce_z(first_terms)
        slab_grad = jnp.concatenate([first_own, up_own, down_own], 1).astype(jnp.bfloat16)
        tile_grad = tiles_from_slabs(slab_grad[None], shards, block_size).reshape(tile_total, -1)
        slot_grad = transposed_times(placing, tile_grad).astype(jnp.bfloat16)
        slot_grad, vector_rows = together(slot_grad, vector_rows)
        slot_grad = lax.all_to_all(
            slot_grad.reshape(PARTS, slots, SUB * block_size), "dp", 0, 0, tiled=True
        )
        vector_rows = add_swapped(add_swapped(vector_rows, 1, 0), 2, 0)
        slot_grad, vector_rows = together(slot_grad, vector_rows)
        vector_rows = add_swapped(vector_rows, 4, 0)
        owned_grads = slot_grad.swapaxes(0, 1).reshape(slots, block_size, block_size)
    else:
        every = jnp.stack(
            [
                jnp.concatenate(
                    [half[1 - j % 2][j // 2] for half in (grad_w_first, grad_w_up, grad_w_down)], 1
                )
                for j in range(shards)
            ]
        ).astype(jnp.float32)
        mine = lax.psum_scatter(every, "tensor", scatter_dimension=0, tiled=True)[0]
        blocks = mine.reshape(PARTS, D // PARTS, -1)
        blocks = jnp.stack([blocks[(p % 2) * 4 + p // 2] for p in range(PARTS)])
        tile_grad = tiles_from_slabs(blocks, shards, block_size)
        slot_grad = tile_grad.reshape(tile_total, block_size, block_size)[owner]
        owned_grads = lax.psum_scatter(slot_grad, "dp", scatter_dimension=0, tiled=True)
    owned_grads = jnp.where(own_flip, jnp.swapaxes(owned_grads, 1, 2), owned_grads)

    bias_first = 1.0 - DECAY_FIRST**ADAM_STEP
    bias_second = 1.0 - DECAY_SECOND**ADAM_STEP
    step_slots = max(k for k in (1, 2, 3, 4, 6) if slots % k == 0)
    slots_spec = pl.BlockSpec((step_slots, block_size, block_size), lambda i: (i, 0, 0))
    slot_out = ((slots, block_size, block_size), f32, slots_spec, "far")
    new_master, new_first, new_second = call_rows(
        adam_kernel,
        slots // step_slots,
        [
            (array, slots_spec, "far")
            for array in (
                owned_grads,
                master[0],
                left_basis[0],
                right_basis[0],
                first_moment[0],
                second_moment[0],
            )
        ],
        [slot_out] * 3,
        22 * slots * block_size**3,
        slots * block_size**2,
    )
    vector_grad = vector_rows[: vectors.shape[0] // D].reshape(-1)
    new_vector_first = DECAY_FIRST * vector_first + (1.0 - DECAY_FIRST) * vector_grad
    new_vector_second = (
        DECAY_SECOND * vector_second + (1.0 - DECAY_SECOND) * vector_grad * vector_grad
    )
    new_vectors = vectors - VECTOR_RATE * (new_vector_first / bias_first) / (
        jnp.sqrt(new_vector_second / bias_second) + ADAM_EPS
    )
    return (
        layer_out,
        input_grad,
        new_master[None],
        new_first[None],
        new_second[None],
        new_vectors,
        new_vector_first,
        new_vector_second,
    )


def solution(mesh):
    return jax.shard_map(
        local,
        mesh=mesh,
        in_specs=(
            P(("dp", "tensor"), None),
            P("dp", None),
            P(("dp", "tensor"), None),
            P(),
            P("tensor", "dp", None, None),
            P("tensor", "dp", None, None),
            P("tensor", "dp", None, None),
            P("tensor", "dp", None, None),
            P("tensor", "dp", None, None),
            P(),
            P(),
            P(),
        ),
        out_specs=(
            P(("dp", "tensor"), None),
            P(("dp", "tensor"), None),
            P("tensor", "dp", None, None),
            P("tensor", "dp", None, None),
            P("tensor", "dp", None, None),
            P(),
            P(),
            P(),
        ),
        check_vma=False,
    )
```

```python
import functools
import math

import jax
import jax.numpy as jnp
from jax import lax
from jax.experimental import pallas as pl
from jax.experimental.pallas import tpu as pltpu
from jax.sharding import PartitionSpec as P

HEADS = 12
HEAD_DIM = 64
D = 768
FF = 3072
ADAM_STEP = 3


NORM_EPS = 1e-12
ADAM_EPS = 1e-08
MATRIX_RATE = 0.01
VECTOR_RATE = 0.1
DECAY_FIRST = 0.5
DECAY_SECOND = 0.5
MASKED = -1e30


def product(left_side, right_side):
    return jnp.dot(left_side, right_side, preferred_element_type=jnp.float32)


def times_transposed(left_side, right_side):
    return lax.dot_general(
        left_side, right_side, (((1,), (1,)), ((), ())), preferred_element_type=jnp.float32
    )


def transposed_times(left_side, right_side):
    return lax.dot_general(
        left_side, right_side, (((0,), (0,)), ((), ())), preferred_element_type=jnp.float32
    )


VMEM_LIMIT = 16 * 1024 * 1024

PARTS = 8
SUB = 12


def part_of_block(block):
    return (block % 4) * 2 + block // 4


def feature_order(rank):
    place = lax.iota(jnp.int32, D)
    part = part_of_block(place // (D // PARTS)) ^ rank
    inner = place % (D // PARTS)
    return (inner // SUB) * (PARTS * SUB) + part * SUB + inner % SUB


def tile_counts(shards, block_size):
    rows = D // block_size
    qkv = rows * (3 * D // shards // block_size)
    out = rows * (D // shards // block_size)
    up = rows * (FF // shards // block_size)
    return (qkv, out, up)


def slabs_from_tiles(tiles, shards, block_size):
    cut = tiles.shape[1]
    qkv, out, up = tile_counts(shards, block_size)
    rows = D // block_size

    def by_rows(part):
        cols = part.shape[0] // rows
        part = part.reshape(rows, cols, cut, SUB, block_size)
        return part.transpose(2, 0, 3, 1, 4).reshape(cut, rows * SUB, cols * block_size)

    def by_cols(part):
        cols = part.shape[0] // rows
        part = part.reshape(cols, rows, cut, SUB, block_size)
        return part.transpose(2, 1, 3, 0, 4).reshape(cut, rows * SUB, cols * block_size)

    return jnp.concatenate(
        [
            by_rows(tiles[:qkv]),
            by_cols(tiles[qkv : qkv + out]),
            by_rows(tiles[qkv + out : qkv + out + up]),
            by_cols(tiles[qkv + out + up :]),
        ],
        2,
    )


def tiles_from_slabs(slabs, shards, block_size):
    cut = slabs.shape[0]
    rows = D // block_size
    width_qkv, width_out, width_up = 3 * D // shards, D // shards, FF // shards

    def by_rows(part):
        cols = part.shape[2] // block_size
        part = part.reshape(cut, rows, SUB, cols, block_size)
        return part.transpose(1, 3, 0, 2, 4).reshape(rows * cols, cut, SUB, block_size)

    def by_cols(part):
        cols = part.shape[2] // block_size
        part = part.reshape(cut, rows, SUB, cols, block_size)
        return part.transpose(3, 1, 0, 2, 4).reshape(rows * cols, cut, SUB, block_size)

    first = width_qkv + width_out
    second = first + width_up
    return jnp.concatenate(
        [
            by_rows(slabs[:, :, :width_qkv]),
            by_cols(slabs[:, :, width_qkv:first]),
            by_rows(slabs[:, :, first:second]),
            by_cols(slabs[:, :, second:]),
        ],
        0,
    )


def swap_over(values, over_dp, over_tensor):
    dp, tensor = lax.axis_size("dp"), lax.axis_size("tensor")
    pairs = [
        (a * tensor + b, (a ^ over_dp) * tensor + (b ^ over_tensor))
        for a in range(dp)
        for b in range(tensor)
    ]
    return lax.ppermute(values, ("dp", "tensor"), pairs)


def merge(terms, outs, segments):
    chunk = D // PARTS

    def kernel(*refs):
        for out, row, col, rows, cols, parts in segments:

            def step(k, carry, out=out, row=row, col=col, cols=cols, parts=parts):
                pieces = [
                    refs[term][pl.ds(pl.multiple_of(at + k * chunk, 32), chunk), left : left + cols]
                    for term, at, left in parts
                ]
                if len(pieces) > 1:
                    value = sum(piece.astype(jnp.float32) for piece in pieces)
                else:
                    value = pieces[0]
                to = refs[len(terms) + out]
                to[pl.ds(pl.multiple_of(row + k * chunk, 32), chunk), col : col + cols] = (
                    value.astype(to.dtype)
                )
                return carry

            lax.fori_loop(0, rows // chunk, step, 0)

    spec = pl.BlockSpec(memory_space=pltpu.VMEM)
    size = sum(term.size for term in terms)
    return pl.pallas_call(
        kernel,
        in_specs=[spec] * len(terms),
        out_specs=[spec] * len(outs),
        out_shape=[jax.ShapeDtypeStruct((rows, cols), dtype) for rows, cols, dtype in outs],
        compiler_params=pltpu.CompilerParams(vmem_limit_bytes=VMEM_LIMIT),
        cost_estimate=pl.CostEstimate(flops=size, bytes_accessed=4 * size, transcendentals=0),
    )(*terms)


def from_z(block):
    return [swap_over(block, 2 * k, 0) for k in (1, 2, 3)]


def over_core(blocks):
    return blocks + [swap_over(block, 0, 1) for block in blocks]


def put(out_ref, lead, row, col, ref, at, left, rows, cols):
    chunk = min(rows, D // 2)

    def step(k, carry):
        to = pl.multiple_of(row + k * chunk, 32)
        source = pl.multiple_of(at + k * chunk, 32)
        out_ref[lead, pl.ds(to, chunk), col : col + cols] = ref[
            pl.ds(source, chunk), left : left + cols
        ]
        return carry

    lax.fori_loop(0, rows // chunk, step, 0)


def place_first(refs, out_ref):
    count = len(refs) // 2
    half, width = D // 2, D // 4
    for core in range(2):
        near, beside, across = refs[core * count : (core + 1) * count]
        for y in range(2):
            col = (2 * y + core) * width
            for kind in range(2):
                left = kind * width
                put(out_ref, kind, 0, col, near, y * half, left, half, width)
                put(out_ref, kind, half, col, beside, y * half, left, half, width)
                if y:
                    put(out_ref, 2 + kind, 0, col, across, 0, left, D, width)
                else:
                    put(out_ref, 2 + kind, 0, col, near, 0, half + left, D, width)


def edges_moves():
    rows, half = D // PARTS, D // 2
    moves = []
    for core in range(2):
        near, beside, across = range(3 * core, 3 * core + 3)
        for y in range(2):
            group = 2 * y + core
            for z in range(4):
                for x in range(2):
                    to, by_y, by_x = x * half + z * rows, (2 * z + y) * rows, (2 * z + x) * rows
                    moves.append((group, to, 0, beside if x else near, by_y, 0, rows, half))
                    source = (across, by_x, 0) if y else (near, by_x, half)
                    moves.append((group, to, half, *source, rows, half))
    return moves


def plane_moves():
    half = D // 2
    return [
        (2 * y + core, x * half, 0, 4 * core + 2 * y + x, 0, 0, half, D)
        for core in range(2)
        for y in range(2)
        for x in range(2)
    ]


def groups_moves(count):
    return [(group, 0, 0, group, 0, 0, D, D) for group in range(count)]


def move_all(moves, refs, out_ref, sems):
    copies = [
        pltpu.make_async_copy(
            refs[ref].at[pl.ds(at, rows), pl.ds(left, cols)],
            out_ref.at[lead, pl.ds(row, rows), pl.ds(col, cols)],
            sems.at[k],
        )
        for k, (lead, row, col, ref, at, left, rows, cols) in enumerate(moves)
    ]
    for copy in copies:
        copy.start()
    for copy in copies:
        copy.wait()


def place_kinds(refs, out_ref):
    width = D // len(refs)
    for group, ref in enumerate(refs):
        for kind in range(4):
            put(out_ref, kind, 0, group * width, ref, 0, kind * width, D, width)


def core_terms(halves):
    odd, even = halves
    return [even.reshape(2 * D, D), swap_over(odd, 0, 1).reshape(2 * D, D)]


def summed(count, row, col):
    return [(term, row, col) for term in range(count)]


def reduce_core_plane(halves):
    half = D // 2
    return merge(
        core_terms(halves),
        [(half, D, jnp.bfloat16)] * 4,
        [(k, 0, 0, half, D, summed(2, k * half, 0)) for k in range(4)],
    )


def reduce_plane(near, beside, across, opposite):
    rows = D // PARTS
    terms = [near, swap_over(beside, 1, 0), swap_over(across, 0, 2), swap_over(opposite, 1, 2)]
    return merge(
        terms,
        [(rows, D, jnp.bfloat16)] * 4,
        [(k, 0, 0, rows, D, summed(4, k * rows, 0)) for k in range(4)],
    )


def z_terms(own, *sent):
    return [own] + [swap_over(block, 2 * (k + 1), 0) for k, block in enumerate(sent)]


def reduce_z(terms):
    rows = D // PARTS
    return merge(terms, [(rows, D, jnp.float32)], [(0, 0, 0, rows, D, summed(4, 0, 0))])[0]


def reduce_core_edges(halves):
    half = D // 2
    return merge(
        core_terms(halves),
        [(D, D, jnp.bfloat16), (D, half, jnp.bfloat16), (D, half, jnp.bfloat16)],
        [
            (0, 0, 0, half, half, summed(2, 0, 0)),
            (0, half, 0, half, half, summed(2, D, 0)),
            (0, 0, half, D, half, summed(2, 0, half)),
            (1, 0, 0, half, half, summed(2, half, 0)),
            (1, half, 0, half, half, summed(2, D + half, 0)),
            (2, 0, 0, D, half, summed(2, D, half)),
        ],
    )


def edge_terms(near, left, right):
    return [near, swap_over(left, 1, 0), swap_over(right, 0, 2)]


def edge_sums(row):
    half = D // 2
    return ((0, [(0, row, 0), (1, row, 0)]), (half, [(0, row, half), (2, row, 0)]))


def plane_edge_terms(near, left, right):
    return [near, swap_over(left, 0, 2), swap_over(right, 1, 0)]


def reduce_edges_plane(terms):
    half = D // 2
    kept = [(0, 0, col, half, half, parts) for col, parts in edge_sums(0)]
    sent = [
        (1 + k, 0, 0, half, half, parts) for k, (_, parts) in enumerate(edge_sums(half))
    ]
    return merge(
        terms,
        [(half, D, jnp.bfloat16), (half, half, jnp.bfloat16), (half, half, jnp.bfloat16)],
        kept + sent,
    )


def reduce_plane_edges(terms):
    rows, half = D // PARTS, D // 2
    return merge(
        terms,
        [(rows, D, jnp.bfloat16)] * 4,
        [
            (k, 0, col, rows, half, parts)
            for k in range(4)
            for col, parts in edge_sums(k * rows)
        ],
    )


def reduce_edges(terms):
    rows, half = D // PARTS, D // 2
    return merge(
        terms,
        [(2 * rows, D, jnp.bfloat16)] * 4,
        [
            (k, q * rows, col, rows, half, parts)
            for k in range(4)
            for q in range(2)
            for col, parts in edge_sums(q * half + k * rows)
        ],
    )


def reduce_edges_z(terms):
    rows, half = D // PARTS, D // 2
    return merge(
        terms,
        [(rows, D, jnp.bfloat16), (rows, half, jnp.bfloat16), (rows, half, jnp.bfloat16)],
        [
            (0, 0, 0, rows, D, summed(4, 0, 0)),
            (1, 0, 0, rows, half, summed(4, rows, 0)),
            (2, 0, 0, rows, half, summed(4, rows, half)),
        ],
    )


def reduce_edges_last(terms):
    rows, half = D // PARTS, D // 2
    return merge(
        terms,
        [(rows, D, jnp.float32)],
        [(0, 0, col, rows, half, parts) for col, parts in edge_sums(0)],
    )[0]


def add_swapped(values, over_dp, over_tensor):
    return values + swap_over(values, over_dp, over_tensor)


ROWS = 256


def dot_nt(left_side, right_side):
    return lax.dot_general(
        left_side, right_side, (((1,), (1,)), ((), ())), preferred_element_type=jnp.float32
    )


def row_block(array):
    return pl.BlockSpec((ROWS, array.shape[1]), lambda i: (i, 0))


def call_rows(kernel, steps, inputs, outputs, flops, transcendentals=0, scratch=()):
    arrays = [
        pltpu.with_memory_space_constraint(array, pltpu.HBM) if far else array
        for array, _, *far in inputs
    ]
    shapes = [jax.ShapeDtypeStruct(shape, dtype) for shape, dtype, *_ in outputs]
    moved = sum(a.size * a.dtype.itemsize for a in arrays + shapes)
    shapes = [
        pltpu.HBM(shape.shape, shape.dtype) if len(output) > 3 else shape
        for shape, output in zip(shapes, outputs)
    ]
    return pl.pallas_call(
        kernel,
        grid=(steps,),
        in_specs=[spec for _, spec, *_ in inputs],
        out_specs=[output[2] for output in outputs],
        out_shape=shapes,
        scratch_shapes=scratch,
        compiler_params=pltpu.CompilerParams(vmem_limit_bytes=VMEM_LIMIT),
        cost_estimate=pl.CostEstimate(
            flops=int(1.0 * flops), bytes_accessed=moved, transcendentals=transcendentals
        ),
    )(*arrays)


def norm_rows(summed):
    centred = summed - jnp.mean(summed, -1, keepdims=True)
    inverse = lax.rsqrt(jnp.mean(centred * centred, -1, keepdims=True) + NORM_EPS)
    return centred * inverse, inverse


def norm_pull(gradient, unit_rows, inverse, gain_row):
    scaled = gradient * gain_row
    return inverse * (
        scaled
        - jnp.mean(scaled, -1, keepdims=True)
        - unit_rows * jnp.mean(scaled * unit_rows, -1, keepdims=True)
    )


def add_rows(ref, rows):
    sums = [jnp.sum(row, 0, keepdims=True) for row in rows]
    start = pl.program_id(0) == 0
    for place, total in enumerate(sums):
        kept = jnp.where(start, 0.0, ref[place : place + 1, :])
        ref[place : place + 1, :] = kept + total


def settle(moves, refs, whole_ref, sems):
    @pl.when(pl.program_id(0) == 0)
    def _():
        move_all(moves, refs, whole_ref, sems)

    return [whole_ref.at[j] for j in range(whole_ref.shape[0])]


def pair_masks(length):
    wide = 2 * HEAD_DIM
    lower = lax.broadcasted_iota(jnp.int32, (length, wide), 1) < HEAD_DIM
    top = lax.broadcasted_iota(jnp.int32, (2 * length, wide), 0) < length
    left = lax.broadcasted_iota(jnp.int32, (2 * length, wide), 1) < HEAD_DIM
    return lower, top == left


def stacked(pair, own):
    return jnp.where(own, jnp.concatenate([pair, pair], 0), jnp.zeros((), pair.dtype))


def attention_kernel(place, total_count, length, *refs):
    rows_ref, across_ref, down_ref, bias_ref, vec_ref = refs[:5]
    outs = refs[5 + total_count : 12 + total_count]
    packed_ref, probs_ref, attended_ref, unit_ref, inverse_ref, low_ref, whole_ref = outs
    scores_ref, sems, *raw = refs[12 + total_count :]

    @pl.when(pl.program_id(0) == 0)
    def _():
        copies = [
            pltpu.make_async_copy(source, to, sems.at[k])
            for k, (source, to) in enumerate(zip(refs[5 : 5 + total_count], raw))
        ]
        for copy in copies:
            copy.start()
        for copy in copies:
            copy.wait()
        place(raw, whole_ref)

    weights = [whole_ref.at[kind] for kind in range(4)]
    wide = 2 * HEAD_DIM
    pairs = HEADS // 2
    rows = rows_ref[...]
    for kind in range(3):
        part = product(rows, weights[kind][...]) + bias_ref[kind : kind + 1, :]
        part = part.astype(jnp.bfloat16)
        if kind == 0:
            part = part * jnp.bfloat16(HEAD_DIM ** (-0.5))
        packed_ref[:, kind * D : (kind + 1) * D] = part
    _, own = pair_masks(length)
    ones = own.astype(jnp.bfloat16)
    steps = [(p, i) for p in range(ROWS // length) for i in range(pairs)]

    def pair_of(p, i, kind):
        span = slice(p * length, (p + 1) * length)
        return packed_ref[span, kind * D + i * wide : kind * D + (i + 1) * wide]

    for at, (p, i) in enumerate(steps):
        scores_ref[at] = dot_nt(pair_of(p, i, 0), stacked(pair_of(p, i, 1), own))
    for at, (p, i) in enumerate(steps):
        allowed = down_ref[p] == across_ref[p]
        for half in range(2):
            lanes = slice(half * length, (half + 1) * length)
            scores = jnp.where(allowed, scores_ref[at, :, lanes], MASKED)
            probs_ref[p, i, :, lanes] = jnp.exp(
                scores - jnp.max(scores, -1, keepdims=True)
            ).astype(jnp.bfloat16)
    for p, i in steps:
        mixed = product(
            probs_ref[p, i], jnp.concatenate([stacked(pair_of(p, i, 2), own), ones], 1)
        )
        attended_ref[p * length : (p + 1) * length, i * wide : (i + 1) * wide] = (
            mixed[:, :wide] / mixed[:, wide:]
        ).astype(jnp.bfloat16)
    summed = rows.astype(jnp.float32) + vec_ref[0:1, :]
    summed = summed + dot_nt(attended_ref[...], weights[3][...])
    unit, inverse = norm_rows(summed)
    unit_ref[...] = unit
    inverse_ref[...] = inverse
    low_ref[...] = (unit * vec_ref[1:2, :] + vec_ref[2:3, :]).astype(jnp.bfloat16)


def gelu_parts(values):
    size = jnp.abs(values)
    decay = jnp.exp2(values * values * (-0.5 / math.log(2.0)))
    t = 1.0 / (1.0 + size * (0.3275911 * 0.5**0.5))
    poly = t * (
        0.127414796
        + t * (-0.142248368 + t * (0.7107068705 + t * (-0.7265760135 + t * 0.5307027145)))
    )
    result = jnp.maximum(values, 0.0) - size * (poly * decay)
    rest = decay * (poly - size * (0.5 / math.pi) ** 0.5)
    return result, jnp.where(values > 0, 1.0 - rest, rest)


def up_kernel(place, shards, *refs):
    low_ref, bias_ref = refs[:2]
    act_ref, slope_ref, whole_ref, sems = refs[-4:]
    weights = settle(place, refs[2:-4], whole_ref, sems)
    width = weights[0].shape[1]
    chunk = 256
    low = low_ref[...]
    for j in range(shards):
        for c in range(0, width, chunk):
            pre = product(low, weights[j][:, c : c + chunk]) + bias_ref[j : j + 1, c : c + chunk]
            result, slope = gelu_parts(pre)
            at = j * width + c
            act_ref[:, at : at + chunk] = result.astype(jnp.bfloat16)
            slope_ref[:, at : at + chunk] = slope.astype(jnp.bfloat16)


def down_kernel(place, shards, *refs):
    act_ref, unit_ref, grad_ref, vec_ref = refs[:4]
    out_ref, dz_ref, low_ref, sums_ref, whole_ref, sems = refs[-6:]
    weights = settle(place, refs[4:-6], whole_ref, sems)
    width = weights[0].shape[1]
    summed = unit_ref[...] * vec_ref[1:2, :] + vec_ref[2:3, :] + vec_ref[3:4, :]
    for j in range(shards):
        summed = summed + dot_nt(act_ref[:, j * width : (j + 1) * width], weights[j][...])
    unit, inverse = norm_rows(summed)
    gain = vec_ref[4:5, :]
    out_ref[...] = unit * gain + vec_ref[5:6, :]
    gradient = grad_ref[...]
    dz = norm_pull(gradient, unit, inverse, gain)
    dz_ref[...] = dz
    low_ref[...] = dz.astype(jnp.bfloat16)
    add_rows(sums_ref, (gradient * unit, gradient, dz))


def hidden_back_kernel(shards, *refs):
    low_ref, slope_ref, whole_ref, dpre_ref, bias_sums_ref = refs
    width = whole_ref.shape[2]
    low = low_ref[...]
    for j in range(shards):
        span = slice(j * width, (j + 1) * width)
        dpre = product(low, whole_ref[j]) * slope_ref[:, span].astype(jnp.float32)
        dpre = dpre.astype(jnp.bfloat16)
        dpre_ref[:, span] = dpre
        total = jnp.sum(dpre.astype(jnp.float32), 0, keepdims=True)
        kept = jnp.where(pl.program_id(0) == 0, 0.0, bias_sums_ref[j : j + 1, :])
        bias_sums_ref[j : j + 1, :] = kept + total


def back_kernel(shards, *refs):
    dpre_ref, dz_ref, unit_ref, inverse_ref, vec_ref, up_ref, first_ref = refs[:7]
    dz1_ref, low1_ref, datt_ref, sums_ref = refs[7:]
    width = up_ref.shape[2]
    gradient = dz_ref[...]
    for j in range(shards):
        gradient = gradient + dot_nt(dpre_ref[:, j * width : (j + 1) * width], up_ref[j])
    unit = unit_ref[...]
    dz1 = norm_pull(gradient, unit, inverse_ref[...], vec_ref[1:2, :])
    dz1_ref[...] = dz1
    low1 = dz1.astype(jnp.bfloat16)
    low1_ref[...] = low1
    add_rows(sums_ref, (gradient * unit, gradient, dz1))
    datt_ref[...] = product(low1, first_ref[3]).astype(jnp.bfloat16)


def attention_back_kernel(length, *refs):
    datt_ref, attended_ref, packed_ref, probs_ref, dpacked_ref, sums_ref, up_ref, grad_ref = refs
    wide = 2 * HEAD_DIM
    lower, own = pair_masks(length)
    ones = own.astype(jnp.bfloat16)
    steps = [(p, i) for p in range(ROWS // length) for i in range(HEADS // 2)]

    def pair_of(p, i, kind):
        span = slice(p * length, (p + 1) * length)
        return packed_ref[span, kind * D + i * wide : kind * D + (i + 1) * wide]

    def keep(p, i, kind, grad):
        span = slice(p * length, (p + 1) * length)
        dpacked_ref[span, kind * D + i * wide : kind * D + (i + 1) * wide] = grad.astype(
            jnp.bfloat16
        )

    for place, (p, i) in enumerate(steps):
        span = slice(p * length, (p + 1) * length)
        lanes = slice(i * wide, (i + 1) * wide)
        upstream = datt_ref[span, lanes].astype(jnp.float32) / product(probs_ref[p, i], ones)
        up_ref[place, :, :wide] = upstream.astype(jnp.bfloat16)
        up_ref[place, :, wide:] = (upstream * attended_ref[span, lanes].astype(jnp.float32)).astype(
            jnp.bfloat16
        )
    for place, (p, i) in enumerate(steps):
        centred = dot_nt(
            up_ref[place], jnp.concatenate([stacked(pair_of(p, i, 2), own), -ones], 1)
        )
        grad_ref[place] = (probs_ref[p, i].astype(jnp.float32) * centred).astype(jnp.bfloat16)
    for place, (p, i) in enumerate(steps):
        grad_scores = grad_ref[place]
        keep(
            p, i, 0,
            product(grad_scores, stacked(pair_of(p, i, 1), own)) * HEAD_DIM ** (-0.5),
        )
        both = transposed_times(grad_scores, pair_of(p, i, 0))
        keep(p, i, 1, jnp.where(lower, both[:length], both[length:]))
        both = transposed_times(probs_ref[p, i], up_ref[place, :, :wide])
        keep(p, i, 2, jnp.where(lower, both[:length], both[length:]))
    total = jnp.sum(dpacked_ref[...].astype(jnp.float32), 0, keepdims=True)
    kept = jnp.where(pl.program_id(0) == 0, 0.0, sums_ref[0:1, :])
    sums_ref[0:1, :] = kept + total


def weight_kernel(odd, count, *refs):
    lefts, refs = refs[:2] if count > 1 else refs[:1], refs[2 if count > 1 else 1 :]
    rights, (out_ref, *turned) = refs[:count], refs[count:]
    start = pl.program_id(0) == 0

    @pl.when(start)
    def _():
        for left, kept in zip(lefts, turned):
            kept[...] = left[...].T

    at = 0
    for place, right in enumerate(rights):
        half = right.shape[1] // 2
        values = right[...] if count == 1 else right[:, half:] if odd else right[:, :half]
        grad = product(turned[place == count - 1 and count > 1][...], values)
        out_ref[0, :, at : at + values.shape[1]] = grad.astype(jnp.bfloat16)
        at += values.shape[1]


def weight_halves(lefts, rights):
    halves = []
    for odd in (1, 0):
        count = len(rights)
        single = count == 1
        specs = []
        for array, width, before in rights:
            if single:
                specs.append(pl.BlockSpec((array.shape[0], width), lambda i: (0, 2 * i + odd)))
            else:
                specs.append(
                    pl.BlockSpec((array.shape[0], 2 * width), lambda i, b=before: (0, b + i))
                )
        arrays = [
            *lefts,
            *[
                array
                for array, _, _ in rights
            ],
        ]
        tokens = lefts[0].shape[0]
        (half,) = pl.pallas_call(
            functools.partial(weight_kernel, odd, count),
            grid=(2,),
            in_specs=[pl.BlockSpec(memory_space=pltpu.VMEM) for _ in lefts] + specs,
            out_specs=[pl.BlockSpec((1, D, D), lambda i: (i, 0, 0))],
            out_shape=[jax.ShapeDtypeStruct((2, D, D), jnp.bfloat16)],
            scratch_shapes=[pltpu.VMEM((D, tokens), jnp.bfloat16) for _ in lefts],
            compiler_params=pltpu.CompilerParams(vmem_limit_bytes=VMEM_LIMIT),
            cost_estimate=pl.CostEstimate(
                flops=4 * tokens * D * D,
                bytes_accessed=sum(2 * array.size for array in arrays),
                transcendentals=0,
            ),
        )(*arrays)
        halves.append(half)
    return halves


def two_terms(values):
    top = values.astype(jnp.bfloat16)
    return top, (values - top.astype(jnp.float32)).astype(jnp.bfloat16)


def adam_kernel(*refs):
    grad_ref, master_ref, left_ref, right_ref, first_ref, second_ref = refs[:6]
    master_out, first_out, second_out = refs[6:]
    bias_first = 1.0 - DECAY_FIRST**ADAM_STEP
    bias_second = 1.0 - DECAY_SECOND**ADAM_STEP
    count = grad_ref.shape[0]
    lefts = [two_terms(left_ref[k]) for k in range(count)]
    rights = [two_terms(right_ref[k]) for k in range(count)]
    turned = []
    for k in range(count):
        grad = product(grad_ref[k].astype(jnp.bfloat16), rights[k][0])
        grad = grad + product(grad_ref[k].astype(jnp.bfloat16), rights[k][1])
        if grad_ref.dtype != jnp.bfloat16:
            grad = grad + product(two_terms(grad_ref[k])[1], rights[k][0])
        turned.append(grad)
    directions = []
    for k in range(count):
        top, rest = two_terms(turned[k])
        rotated = (
            transposed_times(lefts[k][0], top)
            + transposed_times(lefts[k][0], rest)
            + transposed_times(lefts[k][1], top)
        )
        first = DECAY_FIRST * first_ref[k] + (1.0 - DECAY_FIRST) * rotated
        second = DECAY_SECOND * second_ref[k] + (1.0 - DECAY_SECOND) * rotated * rotated
        first_out[k] = first
        second_out[k] = second
        directions.append(first / bias_first / (jnp.sqrt(second / bias_second) + ADAM_EPS))
    backs = [
        product(lefts[k][0], directions[k].astype(jnp.bfloat16)).astype(jnp.bfloat16)
        for k in range(count)
    ]
    for k in range(count):
        update = times_transposed(backs[k], rights[k][0])
        master_out[k] = master_ref[k] - MATRIX_RATE * update


def two_terms(values):
    top = values.astype(jnp.bfloat16)
    return top, (values - top.astype(jnp.float32)).astype(jnp.bfloat16)


def unpermuted(values, selector_ref):
    top, rest = two_terms(values)
    return dot_nt(top, selector_ref[...]) + dot_nt(rest, selector_ref[...])


def enter_kernel(tokens_ref, grad_ref, vectors_ref, selector_ref, rows_ref, out_ref, d_rows_ref):
    selector = selector_ref[...]
    rows_ref[...] = product(tokens_ref[...], selector).astype(jnp.bfloat16)
    top, rest = two_terms(grad_ref[...])
    out_ref[...] = product(top, selector) + product(rest, selector)

    @pl.when(pl.program_id(0) == 0)
    def _():
        rows = vectors_ref[...]
        permuted = jnp.zeros(rows.shape, jnp.float32)
        for _ in range(3):
            term = rows.astype(jnp.bfloat16)
            rows = rows - term.astype(jnp.float32)
            permuted = permuted + product(term, selector)
        d_rows_ref[...] = permuted


def layer_kernel(out_ref, selector_ref, layer_ref):
    layer_ref[...] = unpermuted(out_ref[...], selector_ref)


def input_kernel(dz1_ref, dpacked_ref, selector_ref, whole_ref, input_ref):
    gradient = dz1_ref[...]
    for kind in range(3):
        gradient = gradient + dot_nt(dpacked_ref[:, kind * D : (kind + 1) * D], whole_ref[kind])
    input_ref[...] = unpermuted(gradient, selector_ref)


def vector_kernel(shards, *refs):
    base_ref, first_ref, second_ref, hidden_ref, columns_ref, selector_ref, out_ref = refs
    base = base_ref[0]
    rows = jnp.concatenate(
        [
            first_ref[0:1, :],
            second_ref[0:1, :],
            first_ref[2:3, :],
            second_ref[2:3, :],
            first_ref[1:2, :],
            second_ref[1:2, :],
            jnp.zeros((2, D), jnp.float32),
        ],
        0,
    )
    natural = jnp.zeros((8, D), jnp.float32)
    for _ in range(3):
        term = rows.astype(jnp.bfloat16)
        rows = rows - term.astype(jnp.float32)
        natural = natural + dot_nt(term, selector_ref[...])
    hidden = FF // D
    out_ref[...] = jnp.zeros(out_ref.shape, jnp.float32)
    for at, row in ((0, 0), (1, 1), (4, 2), (5 + hidden, 3), (6 + hidden, 4), (7 + hidden, 5)):
        out_ref[at : at + 1, :] = natural[row : row + 1, :]
    width = D // shards
    for j in range(shards):
        out_ref[5 + j : 6 + j, :] = hidden_ref[pl.ds(j ^ base, 1), :]
        for at, kind in ((2, 0), (3, 2)):
            parts = [
                jnp.where(
                    (j ^ base) == k,
                    columns_ref[0:1, kind * D + k * width : kind * D + (k + 1) * width],
                    0.0,
                )
                for k in range(shards)
            ]
            out_ref[at : at + 1, j * width : (j + 1) * width] = sum(parts)


def adam_kernel(*refs):
    grad_ref, master_ref, left_ref, right_ref, first_ref, second_ref = refs[:6]
    master_out, first_out, second_out = refs[6:]
    bias_first = 1.0 - DECAY_FIRST**ADAM_STEP
    bias_second = 1.0 - DECAY_SECOND**ADAM_STEP
    count = grad_ref.shape[0]
    lefts = [two_terms(left_ref[k]) for k in range(count)]
    rights = [two_terms(right_ref[k]) for k in range(count)]
    turned = []
    for k in range(count):
        top, rest = two_terms(grad_ref[k].astype(jnp.float32))
        turned.append(
            product(top, rights[k][0]) + product(top, rights[k][1]) + product(rest, rights[k][0])
        )
    directions = []
    for k in range(count):
        top, rest = two_terms(turned[k])
        rotated = (
            transposed_times(lefts[k][0], top)
            + transposed_times(lefts[k][0], rest)
            + transposed_times(lefts[k][1], top)
        )
        first = DECAY_FIRST * first_ref[k] + (1.0 - DECAY_FIRST) * rotated
        second = DECAY_SECOND * second_ref[k] + (1.0 - DECAY_SECOND) * rotated * rotated
        first_out[k] = first
        second_out[k] = second
        directions.append(first / bias_first / (jnp.sqrt(second / bias_second) + ADAM_EPS))
    backs = []
    for k in range(count):
        top, rest = two_terms(directions[k])
        backs.append(
            product(lefts[k][0], top) + product(lefts[k][0], rest) + product(lefts[k][1], top)
        )
    for k in range(count):
        top, rest = two_terms(backs[k])
        update = (
            times_transposed(top, rights[k][0])
            + times_transposed(rest, rights[k][0])
            + times_transposed(top, rights[k][1])
        )
        master_out[k] = master_ref[k] - MATRIX_RATE * update


def natural_kernel(shards, *refs):
    out_ref, dz1_ref, dpacked_ref, selector_ref, whole_ref, layer_ref, input_ref = refs
    weights = [whole_ref.at[j] for j in range(shards)]
    head_width = D // shards
    gradient = dz1_ref[...]
    for j in range(shards):
        own = [
            dpacked_ref[:, kind * D + j * head_width : kind * D + (j + 1) * head_width]
            for kind in range(3)
        ]
        gradient = gradient + dot_nt(jnp.concatenate(own, 1), weights[j][:, : 3 * head_width])
    for source, ref in ((out_ref[...], layer_ref), (gradient, input_ref)):
        top = source.astype(jnp.bfloat16)
        rest = (source - top.astype(jnp.float32)).astype(jnp.bfloat16)
        ref[...] = dot_nt(top, selector_ref[...]) + dot_nt(rest, selector_ref[...])


def together(*values):
    return lax.optimization_barrier(values)


def local(
    tokens,
    segments,
    out_grad,
    owner,
    master,
    left_basis,
    right_basis,
    first_moment,
    second_moment,
    vectors,
    vector_first,
    vector_second,
):
    shards = lax.axis_size("tensor")
    dp_size = lax.axis_size("dp")
    direct = dp_size == PARTS and shards == 4
    tensor_rank = lax.axis_index("tensor")
    dp_rank = lax.axis_index("dp")
    local_heads = HEADS // shards
    head_width = local_heads * HEAD_DIM
    up_width = FF // shards
    width_qkv = 3 * head_width
    block_size = master.shape[-1]
    slots = master.shape[1]
    row_count = tokens.shape[0]
    length = segments.shape[1]
    pack_count = row_count // length
    own_segments = lax.dynamic_slice_in_dim(segments, tensor_rank * pack_count, pack_count, 0)
    qkv_tiles, out_tiles, up_tiles = tile_counts(shards, block_size)
    tile_total = owner.shape[0]

    group_base = tensor_rank if direct else 0
    order = feature_order(dp_rank if direct else 0)
    selector = (lax.iota(jnp.int32, D)[:, None] == order[None, :]).astype(jnp.bfloat16)

    steps = row_count // ROWS
    f32, bf16 = jnp.float32, jnp.bfloat16
    rows_spec = lambda width: pl.BlockSpec((ROWS, width), lambda i: (i, 0))
    full = lambda array: (array, pl.BlockSpec(memory_space=pltpu.VMEM))
    raw = lambda array: (array, pl.BlockSpec(memory_space=pl.ANY))
    by_rows = lambda array: (array, row_block(array))
    far_rows = lambda array: (array, row_block(array), "far")
    group_order = lax.iota(jnp.int32, shards) ^ group_base
    below = vectors[: 5 * D].reshape(5, D)
    above = vectors[5 * D + FF :].reshape(3, D)
    d_rows = jnp.stack(
        [below[4], below[0], above[1], above[0], below[1], above[2], below[0], below[0]]
    )
    bias_q = below[2].reshape(shards, head_width)[group_order]
    bias_v = below[3].reshape(shards, head_width)[group_order]
    bias_up = vectors[5 * D : 5 * D + FF].reshape(shards, up_width)[group_order]
    rows_in, grad_out, d_rows = call_rows(
        enter_kernel,
        steps,
        [far_rows(tokens), far_rows(out_grad), full(d_rows), full(selector)],
        [
            ((row_count, D), bf16, rows_spec(D), "far"),
            ((row_count, D), f32, rows_spec(D), "far"),
            ((8, D), f32, pl.BlockSpec(memory_space=pltpu.VMEM)),
        ],
        6 * row_count * D * D,
    )

    def flipped(index):
        from_out = (index >= qkv_tiles) & (index < qkv_tiles + out_tiles)
        return (from_out | (index >= qkv_tiles + out_tiles + up_tiles))[:, None, None]

    own_tiles = lax.dynamic_slice_in_dim(owner, dp_rank * slots, slots, 0)
    own_flip = flipped(own_tiles)
    sent = master[0].astype(jnp.bfloat16)
    sent = jnp.where(own_flip, jnp.swapaxes(sent, 1, 2), sent)
    placing = (lax.iota(jnp.int32, tile_total)[:, None] == owner[None, :]).astype(jnp.bfloat16)
    if direct:
        parts = sent.reshape(slots, PARTS, SUB * block_size).swapaxes(0, 1)
        parts = lax.all_to_all(parts, "dp", 0, 0, tiled=True).reshape(tile_total, -1)
        tiles = product(placing, parts).astype(jnp.bfloat16)
        slab = slabs_from_tiles(tiles.reshape(tile_total, 1, SUB, block_size), shards, block_size)[0]
        half, rows = D // 2, D // PARTS
        first_slab, up_slab, down_slab = (slab[:, k * D : (k + 1) * D] for k in range(3))
        near_left, near_right = down_slab[:, :half], down_slab[:, half:]
        *blocks, near_left, near_right, rows_in, grad_out, d_rows, bias_up = together(
            *from_z(first_slab),
            swap_over(near_left, 0, 2),
            swap_over(near_right, 1, 0),
            rows_in,
            grad_out,
            d_rows,
            bias_up,
        )
        left, right, down_near = merge(
            [first_slab, *blocks, down_slab, near_left, near_right],
            [(half, half, bf16), (half, half, bf16), (2 * rows, D, bf16)],
            [(k, z * rows, 0, rows, half, [(z, 0, k * half)]) for k in range(2) for z in range(4)]
            + [
                (2, 0, 0, rows, D, [(4, 0, 0)]),
                (2, rows, 0, rows, half, [(5, 0, 0)]),
                (2, rows, half, rows, half, [(6, 0, 0)]),
            ],
        )
        left, right, down_near, up_slab = together(left, right, down_near, up_slab)
        up_beside, down_beside = swap_over(up_slab, 2, 0), swap_over(down_near, 2, 0)
        left_across, right_beside, up_beside = together(
            swap_over(left, 0, 2), swap_over(right, 1, 0), up_beside
        )
        near, left, right, up_pair = merge(
            [left, left_across, right, right_beside, up_slab, up_beside],
            [(D, D, bf16), (D, half, bf16), (D, half, bf16), (2 * rows, D, bf16)],
            [
                (out, q * half, col, half, half, [(2 * k + q, 0, 0)])
                for k in range(2)
                for q in range(2)
                for out, col in ((0, k * half), (1 + k, 0))
            ]
            + [(3, z * rows, 0, rows, D, [(4 + z, 0, 0)]) for z in range(2)],
        )
        near_there, beside, across, up_far, down_beside = together(
            swap_over(near, 0, 1),
            swap_over(left, 1, 0),
            swap_over(right, 0, 2),
            swap_over(up_pair, 4, 0),
            down_beside,
        )
        up_z, down_pair = merge(
            [up_pair, up_far, down_near, down_beside],
            [(half, D, bf16)] * 2,
            [
                (k, z * 2 * rows, 0, 2 * rows, D, [(2 * k + z, 0, 0)])
                for k in range(2)
                for z in range(2)
            ],
        )
        first = [near, beside, across, near_there] + over_core([beside, across])[2:]
        up = [up_z, swap_over(up_z, 1, 0), swap_over(up_z, 0, 2), swap_over(up_z, 1, 2)]
        down_far = swap_over(down_pair, 4, 0)
        places = (place_first, plane_moves(), edges_moves())
        pieces = [first, None, None]
    else:
        gathered = lax.all_gather(sent, "dp", axis=0, tiled=True).reshape(tile_total, -1)
        tiles = product(placing, gathered).astype(jnp.bfloat16)
        slabs = slabs_from_tiles(
            tiles.reshape(tile_total, PARTS, SUB, block_size), shards, block_size
        )
        whole = jnp.concatenate([slabs[part_of_block(k)] for k in range(PARTS)], 0)
        every = lax.all_gather(whole, "tensor", axis=0)
        pieces = [
            [every[j][:, k * D : (k + 1) * D] for j in range(shards)] for k in range(3)
        ]
        places = (place_kinds, groups_moves(shards), groups_moves(shards))

    packs_step = ROWS // length
    bias_qkv = jnp.stack(
        [bias_q.reshape(D), jnp.zeros((D,), jnp.float32), bias_v.reshape(D)]
    )
    pairs = HEADS // 2
    probs_spec = pl.BlockSpec((packs_step, pairs, length, 2 * length), lambda i: (i, 0, 0, 0))
    sums_spec = lambda width: pl.BlockSpec((8, width), lambda i: (0, 0))
    square = 2 * row_count * D * D

    whole_out = ((shards, D, D), bf16, pl.BlockSpec(memory_space=pltpu.VMEM))
    packed, probs, attended, unit_first, inverse_first, normed_low, whole_first = call_rows(
        functools.partial(attention_kernel, places[0], len(pieces[0]), length),
        steps,
        [
            far_rows(rows_in),
            (own_segments[:, None, :], pl.BlockSpec((packs_step, 1, length), lambda i: (i, 0, 0))),
            (own_segments[:, :, None], pl.BlockSpec((packs_step, length, 1), lambda i: (i, 0, 0))),
            full(bias_qkv),
            full(d_rows),
            *[raw(w) + (("far",) if w.shape == (D, D) else ()) for w in pieces[0]],
        ],
        [
            ((row_count, 3 * D), bf16, rows_spec(3 * D), "far"),
            ((pack_count, pairs, length, 2 * length), bf16, probs_spec, "far"),
            ((row_count, D), bf16, rows_spec(D)),
            ((row_count, D), f32, rows_spec(D), "far"),
            ((row_count, 1), f32, rows_spec(1), "far"),
            ((row_count, D), bf16, rows_spec(D), "far"),
            whole_out,
        ],
        4 * square + 4 * row_count * length * D,
        row_count * length * HEADS,
        [
            pltpu.VMEM((packs_step * pairs, length, 2 * length), f32),
            pltpu.SemaphoreType.DMA((len(pieces[0]),)),
            *[pltpu.VMEM(w.shape, bf16) for w in pieces[0]],
        ],
    )
    if direct:
        *up, up_there, down_far, normed_low = together(
            *up, swap_over(up[0], 0, 1), down_far, normed_low
        )
        down_near, near_left, near_right = merge(
            [down_pair, down_far],
            [(D, D, bf16), (D, half, bf16), (D, half, bf16)],
            [(0, z * half, 0, half, D, [(z, 0, 0)]) for z in range(2)]
            + [
                (1 + k, z * half, 0, half, half, [(z, 0, k * half)])
                for k in range(2)
                for z in range(2)
            ],
        )
        down = [down_near, swap_over(near_left, 1, 0), swap_over(near_right, 0, 2)]
        pieces[1] = up + [up_there] + over_core(up[1:])[3:]
    activated, slope, whole_up = call_rows(
        functools.partial(up_kernel, places[1], shards),
        steps,
        [far_rows(normed_low), full(bias_up), *[raw(w) for w in pieces[1]]],
        [
            ((row_count, FF), bf16, rows_spec(FF)),
            ((row_count, FF), bf16, rows_spec(FF), "far"),
            whole_out,
        ],
        4 * square,
        2 * row_count * FF,
        [pltpu.SemaphoreType.DMA((len(places[1]),))],
    )
    if direct:
        *down, activated = together(*down, activated)
        pieces[2] = over_core(down)
    layer_out, grad_second, second_low, sums_second, whole_down = call_rows(
        functools.partial(down_kernel, places[2], shards),
        steps,
        [
            by_rows(activated),
            far_rows(unit_first),
            far_rows(grad_out),
            full(d_rows),
            *[raw(w) for w in pieces[2]],
        ],
        [
            ((row_count, D), f32, rows_spec(D), "far"),
            ((row_count, D), f32, rows_spec(D)),
            ((row_count, D), bf16, rows_spec(D)),
            ((8, D), f32, sums_spec(D)),
            whole_out,
        ],
        4 * square,
        0,
        [pltpu.SemaphoreType.DMA((len(places[2]),))],
    )
    grad_w_down = weight_halves([second_low], [(activated, up_width, 0)])
    if direct:
        down_parts = reduce_core_plane(grad_w_down)
        second_low, *down_parts = together(second_low, *down_parts)
        down_parts = reduce_plane(*down_parts)
    grad_pre, grad_bias_up = call_rows(
        functools.partial(hidden_back_kernel, shards),
        steps,
        [by_rows(second_low), far_rows(slope), full(whole_down)],
        [((row_count, FF), bf16, rows_spec(FF)), ((8, up_width), f32, sums_spec(up_width))],
        4 * square,
    )
    grad_w_up = weight_halves([normed_low], [(grad_pre, up_width, 0)])
    grad_first, first_low, grad_attended, sums_first = call_rows(
        functools.partial(back_kernel, shards),
        steps,
        [
            by_rows(grad_pre),
            by_rows(grad_second),
            far_rows(unit_first),
            far_rows(inverse_first),
            full(d_rows),
            full(whole_up),
            full(whole_first),
        ],
        [
            ((row_count, D), f32, rows_spec(D)),
            ((row_count, D), bf16, rows_spec(D)),
            ((row_count, D), bf16, rows_spec(D)),
            ((8, D), f32, sums_spec(D)),
        ],
        20 * square,
    )
    if direct:
        up_parts = reduce_core_edges(grad_w_up)
        grad_attended, *parts = together(grad_attended, *up_parts, *down_parts)
        up_terms = edge_terms(*parts[:3])
        down_terms = z_terms(*parts[3:])
    grad_packed, column_sums = call_rows(
        functools.partial(attention_back_kernel, length),
        steps,
        [by_rows(grad_attended), by_rows(attended), far_rows(packed), (probs, probs_spec, "far")],
        [
            ((row_count, 3 * D), bf16, rows_spec(3 * D)),
            ((8, 3 * D), f32, sums_spec(3 * D)),
        ],
        8 * square,
        0,
        [pltpu.VMEM((packs_step * pairs, length, 2 * length), bf16)] * 2,
    )
    (vector_rows,) = call_rows(
        functools.partial(vector_kernel, shards),
        1,
        [
            (
                lax.convert_element_type(group_base, jnp.int32).reshape(1),
                pl.BlockSpec(memory_space=pltpu.SMEM),
            ),
            full(sums_first),
            full(sums_second),
            full(grad_bias_up),
            full(column_sums),
            full(selector),
        ],
        [((16, D), f32, pl.BlockSpec(memory_space=pltpu.VMEM))],
        48 * D * D,
    )
    if direct:
        vector_rows, grad_packed, *others = together(
            vector_rows, grad_packed, *down_terms, *up_terms
        )
        down_terms, up_terms = others[:4], others[4:]
        up_terms = z_terms(*reduce_edges(up_terms))
        down_own = reduce_z(down_terms)
    else:
        vector_rows = lax.psum(vector_rows, ("dp", "tensor"))
    grad_w_first = weight_halves(
        [rows_in, first_low],
        [(grad_packed, head_width, k * shards // 2) for k in range(3)] + [(attended, head_width, 0)],
    )
    if direct:
        first_parts = reduce_core_edges(grad_w_first)
        *first_parts, grad_first = together(*first_parts, grad_first)
        first_terms = edge_terms(*first_parts)
    (input_grad,) = call_rows(
        input_kernel,
        steps,
        [by_rows(grad_first), by_rows(grad_packed), full(selector), full(whole_first)],
        [((row_count, D), f32, rows_spec(D), "far")],
        5 * square,
    )
    if direct:
        *first_terms, input_grad, layer_out = together(*first_terms, input_grad, layer_out)
        first_terms = plane_edge_terms(*reduce_edges_plane(first_terms))
    (layer_out,) = call_rows(
        layer_kernel,
        steps,
        [far_rows(layer_out), full(selector)],
        [((row_count, D), f32, rows_spec(D), "far")],
        2 * square,
    )
    if direct:
        *others, layer_out = together(*first_terms, *up_terms, layer_out)
        first_terms, up_terms = others[:3], others[3:]
        *parts, vector_rows = together(*reduce_plane_edges(first_terms), vector_rows)
        first_terms = z_terms(*parts)
        vector_rows = add_swapped(add_swapped(vector_rows, 0, 1), 0, 2)
        up_terms = plane_edge_terms(*reduce_edges_z(up_terms))
        up_own = reduce_edges_last(up_terms)
        *first_terms, vector_rows = together(*first_terms, vector_rows)
        first_own = reduce_z(first_terms)
        slab_grad = jnp.concatenate([first_own, up_own, down_own], 1).astype(jnp.bfloat16)
        tile_grad = tiles_from_slabs(slab_grad[None], shards, block_size).reshape(tile_total, -1)
        slot_grad = transposed_times(placing, tile_grad).astype(jnp.bfloat16)
        slot_grad, vector_rows = together(slot_grad, vector_rows)
        slot_grad = lax.all_to_all(
            slot_grad.reshape(PARTS, slots, SUB * block_size), "dp", 0, 0, tiled=True
        )
        vector_rows = add_swapped(add_swapped(vector_rows, 1, 0), 2, 0)
        slot_grad, vector_rows = together(slot_grad, vector_rows)
        vector_rows = add_swapped(vector_rows, 4, 0)
        owned_grads = slot_grad.swapaxes(0, 1).reshape(slots, block_size, block_size)
    else:
        every = jnp.stack(
            [
                jnp.concatenate(
                    [half[1 - j % 2][j // 2] for half in (grad_w_first, grad_w_up, grad_w_down)], 1
                )
                for j in range(shards)
            ]
        ).astype(jnp.float32)
        mine = lax.psum_scatter(every, "tensor", scatter_dimension=0, tiled=True)[0]
        blocks = mine.reshape(PARTS, D // PARTS, -1)
        blocks = jnp.stack([blocks[(p % 2) * 4 + p // 2] for p in range(PARTS)])
        tile_grad = tiles_from_slabs(blocks, shards, block_size)
        slot_grad = tile_grad.reshape(tile_total, block_size, block_size)[owner]
        owned_grads = lax.psum_scatter(slot_grad, "dp", scatter_dimension=0, tiled=True)
    owned_grads = jnp.where(own_flip, jnp.swapaxes(owned_grads, 1, 2), owned_grads)

    bias_first = 1.0 - DECAY_FIRST**ADAM_STEP
    bias_second = 1.0 - DECAY_SECOND**ADAM_STEP
    step_slots = max(k for k in (1, 2, 3, 4, 6, 12) if slots % k == 0)
    slots_spec = pl.BlockSpec((step_slots, block_size, block_size), lambda i: (i, 0, 0))
    slot_out = ((slots, block_size, block_size), f32, slots_spec, "far")
    new_master, new_first, new_second = call_rows(
        adam_kernel,
        slots // step_slots,
        [
            (array, slots_spec, "far")
            for array in (
                owned_grads,
                master[0],
                left_basis[0],
                right_basis[0],
                first_moment[0],
                second_moment[0],
            )
        ],
        [slot_out] * 3,
        22 * slots * block_size**3,
        slots * block_size**2,
    )
    vector_grad = vector_rows[: vectors.shape[0] // D].reshape(-1)
    new_vector_first = DECAY_FIRST * vector_first + (1.0 - DECAY_FIRST) * vector_grad
    new_vector_second = (
        DECAY_SECOND * vector_second + (1.0 - DECAY_SECOND) * vector_grad * vector_grad
    )
    new_vectors = vectors - VECTOR_RATE * (new_vector_first / bias_first) / (
        jnp.sqrt(new_vector_second / bias_second) + ADAM_EPS
    )
    return (
        layer_out,
        input_grad,
        new_master[None],
        new_first[None],
        new_second[None],
        new_vectors,
        new_vector_first,
        new_vector_second,
    )


def solution(mesh):
    return jax.shard_map(
        local,
        mesh=mesh,
        in_specs=(
            P(("dp", "tensor"), None),
            P("dp", None),
            P(("dp", "tensor"), None),
            P(),
            P("tensor", "dp", None, None),
            P("tensor", "dp", None, None),
            P("tensor", "dp", None, None),
            P("tensor", "dp", None, None),
            P("tensor", "dp", None, None),
            P(),
            P(),
            P(),
        ),
        out_specs=(
            P(("dp", "tensor"), None),
            P(("dp", "tensor"), None),
            P("tensor", "dp", None, None),
            P("tensor", "dp", None, None),
            P("tensor", "dp", None, None),
            P(),
            P(),
            P(),
        ),
        check_vma=False,
    )
```

```python
import functools
import math

import jax
import jax.numpy as jnp
from jax import lax
from jax.experimental import pallas as pl
from jax.experimental.pallas import tpu as pltpu
from jax.sharding import PartitionSpec as P

HEADS = 12
HEAD_DIM = 64
D = 768
FF = 3072
ADAM_STEP = 3


NORM_EPS = 1e-12
ADAM_EPS = 1e-08
MATRIX_RATE = 0.01
VECTOR_RATE = 0.1
DECAY_FIRST = 0.5
DECAY_SECOND = 0.5
MASKED = -1e30


def product(left_side, right_side):
    return jnp.dot(left_side, right_side, preferred_element_type=jnp.float32)


def times_transposed(left_side, right_side):
    return lax.dot_general(
        left_side, right_side, (((1,), (1,)), ((), ())), preferred_element_type=jnp.float32
    )


def transposed_times(left_side, right_side):
    return lax.dot_general(
        left_side, right_side, (((0,), (0,)), ((), ())), preferred_element_type=jnp.float32
    )


VMEM_LIMIT = 16 * 1024 * 1024

PARTS = 8
SUB = 12


def part_of_block(block):
    return (block % 4) * 2 + block // 4


def feature_order(rank):
    place = lax.iota(jnp.int32, D)
    part = part_of_block(place // (D // PARTS)) ^ rank
    inner = place % (D // PARTS)
    return (inner // SUB) * (PARTS * SUB) + part * SUB + inner % SUB


def tile_counts(shards, block_size):
    rows = D // block_size
    qkv = rows * (3 * D // shards // block_size)
    out = rows * (D // shards // block_size)
    up = rows * (FF // shards // block_size)
    return (qkv, out, up)


def slabs_from_tiles(tiles, shards, block_size):
    cut = tiles.shape[1]
    qkv, out, up = tile_counts(shards, block_size)
    rows = D // block_size

    def by_rows(part):
        cols = part.shape[0] // rows
        part = part.reshape(rows, cols, cut, SUB, block_size)
        return part.transpose(2, 0, 3, 1, 4).reshape(cut, rows * SUB, cols * block_size)

    def by_cols(part):
        cols = part.shape[0] // rows
        part = part.reshape(cols, rows, cut, SUB, block_size)
        return part.transpose(2, 1, 3, 0, 4).reshape(cut, rows * SUB, cols * block_size)

    return jnp.concatenate(
        [
            by_rows(tiles[:qkv]),
            by_cols(tiles[qkv : qkv + out]),
            by_rows(tiles[qkv + out : qkv + out + up]),
            by_cols(tiles[qkv + out + up :]),
        ],
        2,
    )


def tiles_from_slabs(slabs, shards, block_size):
    cut = slabs.shape[0]
    rows = D // block_size
    width_qkv, width_out, width_up = 3 * D // shards, D // shards, FF // shards

    def by_rows(part):
        cols = part.shape[2] // block_size
        part = part.reshape(cut, rows, SUB, cols, block_size)
        return part.transpose(1, 3, 0, 2, 4).reshape(rows * cols, cut, SUB, block_size)

    def by_cols(part):
        cols = part.shape[2] // block_size
        part = part.reshape(cut, rows, SUB, cols, block_size)
        return part.transpose(3, 1, 0, 2, 4).reshape(rows * cols, cut, SUB, block_size)

    first = width_qkv + width_out
    second = first + width_up
    return jnp.concatenate(
        [
            by_rows(slabs[:, :, :width_qkv]),
            by_cols(slabs[:, :, width_qkv:first]),
            by_rows(slabs[:, :, first:second]),
            by_cols(slabs[:, :, second:]),
        ],
        0,
    )


def swap_over(values, over_dp, over_tensor):
    dp, tensor = lax.axis_size("dp"), lax.axis_size("tensor")
    pairs = [
        (a * tensor + b, (a ^ over_dp) * tensor + (b ^ over_tensor))
        for a in range(dp)
        for b in range(tensor)
    ]
    return lax.ppermute(values, ("dp", "tensor"), pairs)


def merge(terms, outs, segments):
    chunk = D // PARTS

    def kernel(*refs):
        for out, row, col, rows, cols, parts in segments:

            def step(k, carry, out=out, row=row, col=col, cols=cols, parts=parts):
                pieces = [
                    refs[term][pl.ds(pl.multiple_of(at + k * chunk, 32), chunk), left : left + cols]
                    for term, at, left in parts
                ]
                if len(pieces) > 1:
                    value = sum(piece.astype(jnp.float32) for piece in pieces)
                else:
                    value = pieces[0]
                to = refs[len(terms) + out]
                to[pl.ds(pl.multiple_of(row + k * chunk, 32), chunk), col : col + cols] = (
                    value.astype(to.dtype)
                )
                return carry

            lax.fori_loop(0, rows // chunk, step, 0)

    spec = pl.BlockSpec(memory_space=pltpu.VMEM)
    size = sum(term.size for term in terms)
    return pl.pallas_call(
        kernel,
        in_specs=[spec] * len(terms),
        out_specs=[spec] * len(outs),
        out_shape=[jax.ShapeDtypeStruct((rows, cols), dtype) for rows, cols, dtype in outs],
        compiler_params=pltpu.CompilerParams(vmem_limit_bytes=VMEM_LIMIT),
        cost_estimate=pl.CostEstimate(flops=size, bytes_accessed=4 * size, transcendentals=0),
    )(*terms)


def from_z(block):
    return [swap_over(block, 2 * k, 0) for k in (1, 2, 3)]


def over_core(blocks):
    return blocks + [swap_over(block, 0, 1) for block in blocks]


def put(out_ref, lead, row, col, ref, at, left, rows, cols):
    chunk = min(rows, D // 2)

    def step(k, carry):
        to = pl.multiple_of(row + k * chunk, 32)
        source = pl.multiple_of(at + k * chunk, 32)
        out_ref[lead, pl.ds(to, chunk), col : col + cols] = ref[
            pl.ds(source, chunk), left : left + cols
        ]
        return carry

    lax.fori_loop(0, rows // chunk, step, 0)


def place_first(refs, out_ref):
    count = len(refs) // 2
    half, width = D // 2, D // 4
    for core in range(2):
        near, beside, across = refs[core * count : (core + 1) * count]
        for y in range(2):
            col = (2 * y + core) * width
            for kind in range(2):
                left = kind * width
                put(out_ref, kind, 0, col, near, y * half, left, half, width)
                put(out_ref, kind, half, col, beside, y * half, left, half, width)
                if y:
                    put(out_ref, 2 + kind, 0, col, across, 0, left, D, width)
                else:
                    put(out_ref, 2 + kind, 0, col, near, 0, half + left, D, width)


def edges_moves():
    rows, half = D // PARTS, D // 2
    moves = []
    for core in range(2):
        near, beside, across = range(3 * core, 3 * core + 3)
        for y in range(2):
            group = 2 * y + core
            for z in range(4):
                for x in range(2):
                    to, by_y, by_x = x * half + z * rows, (2 * z + y) * rows, (2 * z + x) * rows
                    moves.append((group, to, 0, beside if x else near, by_y, 0, rows, half))
                    source = (across, by_x, 0) if y else (near, by_x, half)
                    moves.append((group, to, half, *source, rows, half))
    return moves


def plane_moves():
    half = D // 2
    return [
        (2 * y + core, x * half, 0, 4 * core + 2 * y + x, 0, 0, half, D)
        for core in range(2)
        for y in range(2)
        for x in range(2)
    ]


def groups_moves(count):
    return [(group, 0, 0, group, 0, 0, D, D) for group in range(count)]


def move_all(moves, refs, out_ref, sems):
    copies = [
        pltpu.make_async_copy(
            refs[ref].at[pl.ds(at, rows), pl.ds(left, cols)],
            out_ref.at[lead, pl.ds(row, rows), pl.ds(col, cols)],
            sems.at[k],
        )
        for k, (lead, row, col, ref, at, left, rows, cols) in enumerate(moves)
    ]
    for copy in copies:
        copy.start()
    for copy in copies:
        copy.wait()


def place_kinds(refs, out_ref):
    width = D // len(refs)
    for group, ref in enumerate(refs):
        for kind in range(4):
            put(out_ref, kind, 0, group * width, ref, 0, kind * width, D, width)


def core_terms(halves):
    odd, even = halves
    return [even.reshape(2 * D, D), swap_over(odd, 0, 1).reshape(2 * D, D)]


def summed(count, row, col):
    return [(term, row, col) for term in range(count)]


def reduce_core_plane(halves):
    half = D // 2
    return merge(
        core_terms(halves),
        [(half, D, jnp.bfloat16)] * 4,
        [(k, 0, 0, half, D, summed(2, k * half, 0)) for k in range(4)],
    )


def reduce_plane(near, beside, across, opposite):
    pair = D // 4
    terms = [near, swap_over(beside, 1, 0), swap_over(across, 0, 2), swap_over(opposite, 1, 2)]
    return merge(
        terms,
        [(pair, D, jnp.bfloat16)] * 2,
        [(k, 0, 0, pair, D, summed(4, k * pair, 0)) for k in range(2)],
    )


def halve_z(near, received):
    rows = near.shape[0] // 2
    return merge(
        [near, received],
        [(rows, D, jnp.bfloat16)] * 2,
        [(k, 0, 0, rows, D, summed(2, k * rows, 0)) for k in range(2)],
    )


def add_z(near, received):
    rows = near.shape[0]
    return merge(
        [near, received], [(rows, D, jnp.float32)], [(0, 0, 0, rows, D, summed(2, 0, 0))]
    )[0]


def z_terms(own, *sent):
    return [own] + [swap_over(block, 2 * (k + 1), 0) for k, block in enumerate(sent)]


def reduce_z(terms):
    rows = D // PARTS
    return merge(terms, [(rows, D, jnp.float32)], [(0, 0, 0, rows, D, summed(4, 0, 0))])[0]


def reduce_core_edges(halves):
    half = D // 2
    return merge(
        core_terms(halves),
        [(D, D, jnp.bfloat16), (D, half, jnp.bfloat16), (D, half, jnp.bfloat16)],
        [
            (0, 0, 0, half, half, summed(2, 0, 0)),
            (0, half, 0, half, half, summed(2, D, 0)),
            (0, 0, half, D, half, summed(2, 0, half)),
            (1, 0, 0, half, half, summed(2, half, 0)),
            (1, half, 0, half, half, summed(2, D + half, 0)),
            (2, 0, 0, D, half, summed(2, D, half)),
        ],
    )


def edge_terms(near, left, right):
    return [near, swap_over(left, 1, 0), swap_over(right, 0, 2)]


def edge_sums(row):
    half = D // 2
    return ((0, [(0, row, 0), (1, row, 0)]), (half, [(0, row, half), (2, row, 0)]))


def plane_edge_terms(near, left, right):
    return [near, swap_over(left, 0, 2), swap_over(right, 1, 0)]


def reduce_edges_plane(terms):
    half = D // 2
    kept = [(0, 0, col, half, half, parts) for col, parts in edge_sums(0)]
    sent = [
        (1 + k, 0, 0, half, half, parts) for k, (_, parts) in enumerate(edge_sums(half))
    ]
    return merge(
        terms,
        [(half, D, jnp.bfloat16), (half, half, jnp.bfloat16), (half, half, jnp.bfloat16)],
        kept + sent,
    )


def reduce_plane_edges(terms):
    rows, half = D // PARTS, D // 2
    return merge(
        terms,
        [(rows, D, jnp.bfloat16)] * 4,
        [
            (k, 0, col, rows, half, parts)
            for k in range(4)
            for col, parts in edge_sums(k * rows)
        ],
    )


def reduce_edges(terms):
    rows, half = D // PARTS, D // 2
    return merge(
        terms,
        [(half, D, jnp.bfloat16)] * 2,
        [
            (k // 2, (2 * (k % 2) + q) * rows, col, rows, half, parts)
            for k in range(4)
            for q in range(2)
            for col, parts in edge_sums(q * half + k * rows)
        ],
    )


def reduce_edges_z(terms):
    rows, half = D // PARTS, D // 2
    return merge(
        terms,
        [(rows, D, jnp.bfloat16), (rows, half, jnp.bfloat16), (rows, half, jnp.bfloat16)],
        [
            (0, 0, 0, rows, D, summed(2, 0, 0)),
            (1, 0, 0, rows, half, summed(2, rows, 0)),
            (2, 0, 0, rows, half, summed(2, rows, half)),
        ],
    )


def reduce_edges_last(terms):
    rows, half = D // PARTS, D // 2
    return merge(
        terms,
        [(rows, D, jnp.float32)],
        [(0, 0, col, rows, half, parts) for col, parts in edge_sums(0)],
    )[0]


def add_swapped(values, over_dp, over_tensor):
    return values + swap_over(values, over_dp, over_tensor)


ROWS = 256


def dot_nt(left_side, right_side):
    return lax.dot_general(
        left_side, right_side, (((1,), (1,)), ((), ())), preferred_element_type=jnp.float32
    )


def row_block(array):
    return pl.BlockSpec((ROWS, array.shape[1]), lambda i: (i, 0))


def call_rows(kernel, steps, inputs, outputs, flops, transcendentals=0, scratch=()):
    arrays = [
        pltpu.with_memory_space_constraint(array, pltpu.HBM) if far else array
        for array, _, *far in inputs
    ]
    shapes = [jax.ShapeDtypeStruct(shape, dtype) for shape, dtype, *_ in outputs]
    moved = sum(a.size * a.dtype.itemsize for a in arrays + shapes)
    shapes = [
        pltpu.HBM(shape.shape, shape.dtype) if len(output) > 3 else shape
        for shape, output in zip(shapes, outputs)
    ]
    return pl.pallas_call(
        kernel,
        grid=(steps,),
        in_specs=[spec for _, spec, *_ in inputs],
        out_specs=[output[2] for output in outputs],
        out_shape=shapes,
        scratch_shapes=scratch,
        compiler_params=pltpu.CompilerParams(vmem_limit_bytes=VMEM_LIMIT),
        cost_estimate=pl.CostEstimate(
            flops=int(1.0 * flops), bytes_accessed=moved, transcendentals=transcendentals
        ),
    )(*arrays)


def norm_rows(summed):
    centred = summed - jnp.mean(summed, -1, keepdims=True)
    inverse = lax.rsqrt(jnp.mean(centred * centred, -1, keepdims=True) + NORM_EPS)
    return centred * inverse, inverse


def norm_pull(gradient, unit_rows, inverse, gain_row):
    scaled = gradient * gain_row
    return inverse * (
        scaled
        - jnp.mean(scaled, -1, keepdims=True)
        - unit_rows * jnp.mean(scaled * unit_rows, -1, keepdims=True)
    )


def add_rows(ref, rows):
    sums = [jnp.sum(row, 0, keepdims=True) for row in rows]
    start = pl.program_id(0) == 0
    for place, total in enumerate(sums):
        kept = jnp.where(start, 0.0, ref[place : place + 1, :])
        ref[place : place + 1, :] = kept + total


def settle(moves, refs, whole_ref, sems):
    @pl.when(pl.program_id(0) == 0)
    def _():
        move_all(moves, refs, whole_ref, sems)

    return [whole_ref.at[j] for j in range(whole_ref.shape[0])]


def pair_masks(length):
    wide = 2 * HEAD_DIM
    lower = lax.broadcasted_iota(jnp.int32, (length, wide), 1) < HEAD_DIM
    top = lax.broadcasted_iota(jnp.int32, (2 * length, wide), 0) < length
    left = lax.broadcasted_iota(jnp.int32, (2 * length, wide), 1) < HEAD_DIM
    return lower, top == left


def stacked(pair, own):
    return jnp.where(own, jnp.concatenate([pair, pair], 0), jnp.zeros((), pair.dtype))


def attention_kernel(place, total_count, length, *refs):
    rows_ref, across_ref, down_ref, bias_ref, vec_ref = refs[:5]
    outs = refs[5 + total_count : 12 + total_count]
    packed_ref, probs_ref, attended_ref, unit_ref, inverse_ref, low_ref, whole_ref = outs
    scores_ref, sems, *raw = refs[12 + total_count :]

    @pl.when(pl.program_id(0) == 0)
    def _():
        copies = [
            pltpu.make_async_copy(source, to, sems.at[k])
            for k, (source, to) in enumerate(zip(refs[5 : 5 + total_count], raw))
        ]
        for copy in copies:
            copy.start()
        for copy in copies:
            copy.wait()
        place(raw, whole_ref)

    weights = [whole_ref.at[kind] for kind in range(4)]
    wide = 2 * HEAD_DIM
    pairs = HEADS // 2
    rows = rows_ref[...]
    for kind in range(3):
        part = product(rows, weights[kind][...]) + bias_ref[kind : kind + 1, :]
        part = part.astype(jnp.bfloat16)
        if kind == 0:
            part = part * jnp.bfloat16(HEAD_DIM ** (-0.5))
        packed_ref[:, kind * D : (kind + 1) * D] = part
    _, own = pair_masks(length)
    ones = own.astype(jnp.bfloat16)
    steps = [(p, i) for p in range(ROWS // length) for i in range(pairs)]

    def pair_of(p, i, kind):
        span = slice(p * length, (p + 1) * length)
        return packed_ref[span, kind * D + i * wide : kind * D + (i + 1) * wide]

    for at, (p, i) in enumerate(steps):
        scores_ref[at] = dot_nt(pair_of(p, i, 0), stacked(pair_of(p, i, 1), own))
    for at, (p, i) in enumerate(steps):
        allowed = down_ref[p] == across_ref[p]
        for half in range(2):
            lanes = slice(half * length, (half + 1) * length)
            scores = jnp.where(allowed, scores_ref[at, :, lanes], MASKED)
            probs_ref[p, i, :, lanes] = jnp.exp(
                scores - jnp.max(scores, -1, keepdims=True)
            ).astype(jnp.bfloat16)
    for p, i in steps:
        mixed = product(
            probs_ref[p, i], jnp.concatenate([stacked(pair_of(p, i, 2), own), ones], 1)
        )
        attended_ref[p * length : (p + 1) * length, i * wide : (i + 1) * wide] = (
            mixed[:, :wide] / mixed[:, wide:]
        ).astype(jnp.bfloat16)
    summed = rows.astype(jnp.float32) + vec_ref[0:1, :]
    summed = summed + dot_nt(attended_ref[...], weights[3][...])
    unit, inverse = norm_rows(summed)
    unit_ref[...] = unit
    inverse_ref[...] = inverse
    low_ref[...] = (unit * vec_ref[1:2, :] + vec_ref[2:3, :]).astype(jnp.bfloat16)


def gelu_parts(values):
    size = jnp.abs(values)
    decay = jnp.exp2(values * values * (-0.5 / math.log(2.0)))
    t = 1.0 / (1.0 + size * (0.3275911 * 0.5**0.5))
    poly = t * (
        0.127414796
        + t * (-0.142248368 + t * (0.7107068705 + t * (-0.7265760135 + t * 0.5307027145)))
    )
    result = jnp.maximum(values, 0.0) - size * (poly * decay)
    rest = decay * (poly - size * (0.5 / math.pi) ** 0.5)
    return result, jnp.where(values > 0, 1.0 - rest, rest)


def up_kernel(place, shards, *refs):
    low_ref, bias_ref = refs[:2]
    act_ref, slope_ref, whole_ref, sems = refs[-4:]
    weights = settle(place, refs[2:-4], whole_ref, sems)
    width = weights[0].shape[1]
    chunk = 256
    low = low_ref[...]
    for j in range(shards):
        for c in range(0, width, chunk):
            pre = product(low, weights[j][:, c : c + chunk]) + bias_ref[j : j + 1, c : c + chunk]
            result, slope = gelu_parts(pre)
            at = j * width + c
            act_ref[:, at : at + chunk] = result.astype(jnp.bfloat16)
            slope_ref[:, at : at + chunk] = slope.astype(jnp.bfloat16)


def down_kernel(place, shards, *refs):
    act_ref, unit_ref, grad_ref, vec_ref = refs[:4]
    out_ref, dz_ref, low_ref, sums_ref, whole_ref, sems = refs[-6:]
    weights = settle(place, refs[4:-6], whole_ref, sems)
    width = weights[0].shape[1]
    summed = unit_ref[...] * vec_ref[1:2, :] + vec_ref[2:3, :] + vec_ref[3:4, :]
    for j in range(shards):
        summed = summed + dot_nt(act_ref[:, j * width : (j + 1) * width], weights[j][...])
    unit, inverse = norm_rows(summed)
    gain = vec_ref[4:5, :]
    out_ref[...] = unit * gain + vec_ref[5:6, :]
    gradient = grad_ref[...]
    dz = norm_pull(gradient, unit, inverse, gain)
    dz_ref[...] = dz
    low_ref[...] = dz.astype(jnp.bfloat16)
    add_rows(sums_ref, (gradient * unit, gradient, dz))


def hidden_back_kernel(shards, *refs):
    low_ref, slope_ref, whole_ref, dpre_ref, bias_sums_ref = refs
    width = whole_ref.shape[2]
    low = low_ref[...]
    for j in range(shards):
        span = slice(j * width, (j + 1) * width)
        dpre = product(low, whole_ref[j]) * slope_ref[:, span].astype(jnp.float32)
        dpre = dpre.astype(jnp.bfloat16)
        dpre_ref[:, span] = dpre
        total = jnp.sum(dpre.astype(jnp.float32), 0, keepdims=True)
        kept = jnp.where(pl.program_id(0) == 0, 0.0, bias_sums_ref[j : j + 1, :])
        bias_sums_ref[j : j + 1, :] = kept + total


def back_kernel(shards, *refs):
    dpre_ref, dz_ref, unit_ref, inverse_ref, vec_ref, up_ref, first_ref = refs[:7]
    dz1_ref, low1_ref, datt_ref, sums_ref = refs[7:]
    width = up_ref.shape[2]
    gradient = dz_ref[...]
    for j in range(shards):
        gradient = gradient + dot_nt(dpre_ref[:, j * width : (j + 1) * width], up_ref[j])
    unit = unit_ref[...]
    dz1 = norm_pull(gradient, unit, inverse_ref[...], vec_ref[1:2, :])
    dz1_ref[...] = dz1
    low1 = dz1.astype(jnp.bfloat16)
    low1_ref[...] = low1
    add_rows(sums_ref, (gradient * unit, gradient, dz1))
    datt_ref[...] = product(low1, first_ref[3]).astype(jnp.bfloat16)


def attention_back_kernel(length, *refs):
    datt_ref, attended_ref, packed_ref, probs_ref, dpacked_ref, sums_ref, up_ref, grad_ref = refs
    wide = 2 * HEAD_DIM
    lower, own = pair_masks(length)
    ones = own.astype(jnp.bfloat16)
    steps = [(p, i) for p in range(ROWS // length) for i in range(HEADS // 2)]

    def pair_of(p, i, kind):
        span = slice(p * length, (p + 1) * length)
        return packed_ref[span, kind * D + i * wide : kind * D + (i + 1) * wide]

    def keep(p, i, kind, grad):
        span = slice(p * length, (p + 1) * length)
        dpacked_ref[span, kind * D + i * wide : kind * D + (i + 1) * wide] = grad.astype(
            jnp.bfloat16
        )

    for place, (p, i) in enumerate(steps):
        span = slice(p * length, (p + 1) * length)
        lanes = slice(i * wide, (i + 1) * wide)
        upstream = datt_ref[span, lanes].astype(jnp.float32) / product(probs_ref[p, i], ones)
        up_ref[place, :, :wide] = upstream.astype(jnp.bfloat16)
        up_ref[place, :, wide:] = (upstream * attended_ref[span, lanes].astype(jnp.float32)).astype(
            jnp.bfloat16
        )
    for place, (p, i) in enumerate(steps):
        centred = dot_nt(
            up_ref[place], jnp.concatenate([stacked(pair_of(p, i, 2), own), -ones], 1)
        )
        grad_ref[place] = (probs_ref[p, i].astype(jnp.float32) * centred).astype(jnp.bfloat16)
    for place, (p, i) in enumerate(steps):
        grad_scores = grad_ref[place]
        keep(
            p, i, 0,
            product(grad_scores, stacked(pair_of(p, i, 1), own)) * HEAD_DIM ** (-0.5),
        )
        both = transposed_times(grad_scores, pair_of(p, i, 0))
        keep(p, i, 1, jnp.where(lower, both[:length], both[length:]))
        both = transposed_times(probs_ref[p, i], up_ref[place, :, :wide])
        keep(p, i, 2, jnp.where(lower, both[:length], both[length:]))
    total = jnp.sum(dpacked_ref[...].astype(jnp.float32), 0, keepdims=True)
    kept = jnp.where(pl.program_id(0) == 0, 0.0, sums_ref[0:1, :])
    sums_ref[0:1, :] = kept + total


def weight_kernel(odd, count, *refs):
    lefts, refs = refs[:2] if count > 1 else refs[:1], refs[2 if count > 1 else 1 :]
    rights, (out_ref, *turned) = refs[:count], refs[count:]
    start = pl.program_id(0) == 0

    @pl.when(start)
    def _():
        for left, kept in zip(lefts, turned):
            kept[...] = left[...].T

    at = 0
    for place, right in enumerate(rights):
        half = right.shape[1] // 2
        values = right[...] if count == 1 else right[:, half:] if odd else right[:, :half]
        grad = product(turned[place == count - 1 and count > 1][...], values)
        out_ref[0, :, at : at + values.shape[1]] = grad.astype(jnp.bfloat16)
        at += values.shape[1]


def weight_halves(lefts, rights):
    halves = []
    for odd in (1, 0):
        count = len(rights)
        single = count == 1
        specs = []
        for array, width, before in rights:
            if single:
                specs.append(pl.BlockSpec((array.shape[0], width), lambda i: (0, 2 * i + odd)))
            else:
                specs.append(
                    pl.BlockSpec((array.shape[0], 2 * width), lambda i, b=before: (0, b + i))
                )
        arrays = [
            *lefts,
            *[
                array
                for array, _, _ in rights
            ],
        ]
        tokens = lefts[0].shape[0]
        (half,) = pl.pallas_call(
            functools.partial(weight_kernel, odd, count),
            grid=(2,),
            in_specs=[pl.BlockSpec(memory_space=pltpu.VMEM) for _ in lefts] + specs,
            out_specs=[pl.BlockSpec((1, D, D), lambda i: (i, 0, 0))],
            out_shape=[jax.ShapeDtypeStruct((2, D, D), jnp.bfloat16)],
            scratch_shapes=[pltpu.VMEM((D, tokens), jnp.bfloat16) for _ in lefts],
            compiler_params=pltpu.CompilerParams(vmem_limit_bytes=VMEM_LIMIT),
            cost_estimate=pl.CostEstimate(
                flops=4 * tokens * D * D,
                bytes_accessed=sum(2 * array.size for array in arrays),
                transcendentals=0,
            ),
        )(*arrays)
        halves.append(half)
    return halves


def two_terms(values):
    top = values.astype(jnp.bfloat16)
    return top, (values - top.astype(jnp.float32)).astype(jnp.bfloat16)


def adam_kernel(*refs):
    grad_ref, master_ref, left_ref, right_ref, first_ref, second_ref = refs[:6]
    master_out, first_out, second_out = refs[6:]
    bias_first = 1.0 - DECAY_FIRST**ADAM_STEP
    bias_second = 1.0 - DECAY_SECOND**ADAM_STEP
    count = grad_ref.shape[0]
    lefts = [two_terms(left_ref[k]) for k in range(count)]
    rights = [two_terms(right_ref[k]) for k in range(count)]
    turned = []
    for k in range(count):
        grad = product(grad_ref[k].astype(jnp.bfloat16), rights[k][0])
        grad = grad + product(grad_ref[k].astype(jnp.bfloat16), rights[k][1])
        if grad_ref.dtype != jnp.bfloat16:
            grad = grad + product(two_terms(grad_ref[k])[1], rights[k][0])
        turned.append(grad)
    directions = []
    for k in range(count):
        top, rest = two_terms(turned[k])
        rotated = (
            transposed_times(lefts[k][0], top)
            + transposed_times(lefts[k][0], rest)
            + transposed_times(lefts[k][1], top)
        )
        first = DECAY_FIRST * first_ref[k] + (1.0 - DECAY_FIRST) * rotated
        second = DECAY_SECOND * second_ref[k] + (1.0 - DECAY_SECOND) * rotated * rotated
        first_out[k] = first
        second_out[k] = second
        directions.append(first / bias_first / (jnp.sqrt(second / bias_second) + ADAM_EPS))
    backs = [
        product(lefts[k][0], directions[k].astype(jnp.bfloat16)).astype(jnp.bfloat16)
        for k in range(count)
    ]
    for k in range(count):
        update = times_transposed(backs[k], rights[k][0])
        master_out[k] = master_ref[k] - MATRIX_RATE * update


def two_terms(values):
    top = values.astype(jnp.bfloat16)
    return top, (values - top.astype(jnp.float32)).astype(jnp.bfloat16)


def unpermuted(values, selector_ref):
    top, rest = two_terms(values)
    return dot_nt(top, selector_ref[...]) + dot_nt(rest, selector_ref[...])


def enter_kernel(tokens_ref, grad_ref, vectors_ref, selector_ref, rows_ref, out_ref, d_rows_ref):
    selector = selector_ref[...]
    rows_ref[...] = product(tokens_ref[...], selector).astype(jnp.bfloat16)
    top, rest = two_terms(grad_ref[...])
    out_ref[...] = product(top, selector) + product(rest, selector)

    @pl.when(pl.program_id(0) == 0)
    def _():
        rows = vectors_ref[...]
        permuted = jnp.zeros(rows.shape, jnp.float32)
        for _ in range(3):
            term = rows.astype(jnp.bfloat16)
            rows = rows - term.astype(jnp.float32)
            permuted = permuted + product(term, selector)
        d_rows_ref[...] = permuted


def layer_kernel(out_ref, selector_ref, layer_ref):
    layer_ref[...] = unpermuted(out_ref[...], selector_ref)


def input_kernel(dz1_ref, dpacked_ref, selector_ref, whole_ref, input_ref):
    gradient = dz1_ref[...]
    for kind in range(3):
        gradient = gradient + dot_nt(dpacked_ref[:, kind * D : (kind + 1) * D], whole_ref[kind])
    input_ref[...] = unpermuted(gradient, selector_ref)


def vector_kernel(shards, *refs):
    base_ref, first_ref, second_ref, hidden_ref, columns_ref, selector_ref, out_ref = refs
    base = base_ref[0]
    rows = jnp.concatenate(
        [
            first_ref[0:1, :],
            second_ref[0:1, :],
            first_ref[2:3, :],
            second_ref[2:3, :],
            first_ref[1:2, :],
            second_ref[1:2, :],
            jnp.zeros((2, D), jnp.float32),
        ],
        0,
    )
    natural = jnp.zeros((8, D), jnp.float32)
    for _ in range(3):
        term = rows.astype(jnp.bfloat16)
        rows = rows - term.astype(jnp.float32)
        natural = natural + dot_nt(term, selector_ref[...])
    hidden = FF // D
    out_ref[...] = jnp.zeros(out_ref.shape, jnp.float32)
    for at, row in ((0, 0), (1, 1), (4, 2), (5 + hidden, 3), (6 + hidden, 4), (7 + hidden, 5)):
        out_ref[at : at + 1, :] = natural[row : row + 1, :]
    width = D // shards
    for j in range(shards):
        out_ref[5 + j : 6 + j, :] = hidden_ref[pl.ds(j ^ base, 1), :]
        for at, kind in ((2, 0), (3, 2)):
            parts = [
                jnp.where(
                    (j ^ base) == k,
                    columns_ref[0:1, kind * D + k * width : kind * D + (k + 1) * width],
                    0.0,
                )
                for k in range(shards)
            ]
            out_ref[at : at + 1, j * width : (j + 1) * width] = sum(parts)


def adam_kernel(*refs):
    grad_ref, master_ref, left_ref, right_ref, first_ref, second_ref = refs[:6]
    master_out, first_out, second_out = refs[6:]
    bias_first = 1.0 - DECAY_FIRST**ADAM_STEP
    bias_second = 1.0 - DECAY_SECOND**ADAM_STEP
    count = grad_ref.shape[0]
    lefts = [two_terms(left_ref[k]) for k in range(count)]
    rights = [two_terms(right_ref[k]) for k in range(count)]
    turned = []
    for k in range(count):
        top, rest = two_terms(grad_ref[k].astype(jnp.float32))
        turned.append(
            product(top, rights[k][0]) + product(top, rights[k][1]) + product(rest, rights[k][0])
        )
    directions = []
    for k in range(count):
        top, rest = two_terms(turned[k])
        rotated = (
            transposed_times(lefts[k][0], top)
            + transposed_times(lefts[k][0], rest)
            + transposed_times(lefts[k][1], top)
        )
        first = DECAY_FIRST * first_ref[k] + (1.0 - DECAY_FIRST) * rotated
        second = DECAY_SECOND * second_ref[k] + (1.0 - DECAY_SECOND) * rotated * rotated
        first_out[k] = first
        second_out[k] = second
        directions.append(first / bias_first / (jnp.sqrt(second / bias_second) + ADAM_EPS))
    backs = []
    for k in range(count):
        top, rest = two_terms(directions[k])
        backs.append(
            product(lefts[k][0], top) + product(lefts[k][0], rest) + product(lefts[k][1], top)
        )
    for k in range(count):
        top, rest = two_terms(backs[k])
        update = (
            times_transposed(top, rights[k][0])
            + times_transposed(rest, rights[k][0])
            + times_transposed(top, rights[k][1])
        )
        master_out[k] = master_ref[k] - MATRIX_RATE * update


def natural_kernel(shards, *refs):
    out_ref, dz1_ref, dpacked_ref, selector_ref, whole_ref, layer_ref, input_ref = refs
    weights = [whole_ref.at[j] for j in range(shards)]
    head_width = D // shards
    gradient = dz1_ref[...]
    for j in range(shards):
        own = [
            dpacked_ref[:, kind * D + j * head_width : kind * D + (j + 1) * head_width]
            for kind in range(3)
        ]
        gradient = gradient + dot_nt(jnp.concatenate(own, 1), weights[j][:, : 3 * head_width])
    for source, ref in ((out_ref[...], layer_ref), (gradient, input_ref)):
        top = source.astype(jnp.bfloat16)
        rest = (source - top.astype(jnp.float32)).astype(jnp.bfloat16)
        ref[...] = dot_nt(top, selector_ref[...]) + dot_nt(rest, selector_ref[...])


def together(*values):
    return lax.optimization_barrier(values)


def local(
    tokens,
    segments,
    out_grad,
    owner,
    master,
    left_basis,
    right_basis,
    first_moment,
    second_moment,
    vectors,
    vector_first,
    vector_second,
):
    shards = lax.axis_size("tensor")
    dp_size = lax.axis_size("dp")
    direct = dp_size == PARTS and shards == 4
    tensor_rank = lax.axis_index("tensor")
    dp_rank = lax.axis_index("dp")
    local_heads = HEADS // shards
    head_width = local_heads * HEAD_DIM
    up_width = FF // shards
    width_qkv = 3 * head_width
    block_size = master.shape[-1]
    slots = master.shape[1]
    row_count = tokens.shape[0]
    length = segments.shape[1]
    pack_count = row_count // length
    own_segments = lax.dynamic_slice_in_dim(segments, tensor_rank * pack_count, pack_count, 0)
    qkv_tiles, out_tiles, up_tiles = tile_counts(shards, block_size)
    tile_total = owner.shape[0]

    group_base = tensor_rank if direct else 0
    order = feature_order(dp_rank if direct else 0)
    selector = (lax.iota(jnp.int32, D)[:, None] == order[None, :]).astype(jnp.bfloat16)

    steps = row_count // ROWS
    f32, bf16 = jnp.float32, jnp.bfloat16
    rows_spec = lambda width: pl.BlockSpec((ROWS, width), lambda i: (i, 0))
    full = lambda array: (array, pl.BlockSpec(memory_space=pltpu.VMEM))
    raw = lambda array: (array, pl.BlockSpec(memory_space=pl.ANY))
    by_rows = lambda array: (array, row_block(array))
    far_rows = lambda array: (array, row_block(array), "far")
    group_order = lax.iota(jnp.int32, shards) ^ group_base
    below = vectors[: 5 * D].reshape(5, D)
    above = vectors[5 * D + FF :].reshape(3, D)
    d_rows = jnp.stack(
        [below[4], below[0], above[1], above[0], below[1], above[2], below[0], below[0]]
    )
    bias_q = below[2].reshape(shards, head_width)[group_order]
    bias_v = below[3].reshape(shards, head_width)[group_order]
    bias_up = vectors[5 * D : 5 * D + FF].reshape(shards, up_width)[group_order]
    rows_in, grad_out, d_rows = call_rows(
        enter_kernel,
        steps,
        [far_rows(tokens), far_rows(out_grad), full(d_rows), full(selector)],
        [
            ((row_count, D), bf16, rows_spec(D), "far"),
            ((row_count, D), f32, rows_spec(D), "far"),
            ((8, D), f32, pl.BlockSpec(memory_space=pltpu.VMEM)),
        ],
        6 * row_count * D * D,
    )

    def flipped(index):
        from_out = (index >= qkv_tiles) & (index < qkv_tiles + out_tiles)
        return (from_out | (index >= qkv_tiles + out_tiles + up_tiles))[:, None, None]

    own_tiles = lax.dynamic_slice_in_dim(owner, dp_rank * slots, slots, 0)
    own_flip = flipped(own_tiles)
    sent = master[0].astype(jnp.bfloat16)
    sent = jnp.where(own_flip, jnp.swapaxes(sent, 1, 2), sent)
    placing = (lax.iota(jnp.int32, tile_total)[:, None] == owner[None, :]).astype(jnp.bfloat16)
    if direct:
        parts = sent.reshape(slots, PARTS, SUB * block_size).swapaxes(0, 1)
        parts = lax.all_to_all(parts, "dp", 0, 0, tiled=True).reshape(tile_total, -1)
        tiles = product(placing, parts).astype(jnp.bfloat16)
        slab = slabs_from_tiles(tiles.reshape(tile_total, 1, SUB, block_size), shards, block_size)[0]
        half, rows = D // 2, D // PARTS
        first_slab, up_slab, down_slab = (slab[:, k * D : (k + 1) * D] for k in range(3))
        near_left, near_right = down_slab[:, :half], down_slab[:, half:]
        *blocks, near_left, near_right, rows_in, grad_out, d_rows, bias_up = together(
            *from_z(first_slab),
            swap_over(near_left, 0, 2),
            swap_over(near_right, 1, 0),
            rows_in,
            grad_out,
            d_rows,
            bias_up,
        )
        left, right, down_near = merge(
            [first_slab, *blocks, down_slab, near_left, near_right],
            [(half, half, bf16), (half, half, bf16), (2 * rows, D, bf16)],
            [(k, z * rows, 0, rows, half, [(z, 0, k * half)]) for k in range(2) for z in range(4)]
            + [
                (2, 0, 0, rows, D, [(4, 0, 0)]),
                (2, rows, 0, rows, half, [(5, 0, 0)]),
                (2, rows, half, rows, half, [(6, 0, 0)]),
            ],
        )
        left, right, down_near, up_slab = together(left, right, down_near, up_slab)
        up_beside, down_beside = swap_over(up_slab, 2, 0), swap_over(down_near, 2, 0)
        left_across, right_beside, up_beside = together(
            swap_over(left, 0, 2), swap_over(right, 1, 0), up_beside
        )
        near, left, right, up_pair = merge(
            [left, left_across, right, right_beside, up_slab, up_beside],
            [(D, D, bf16), (D, half, bf16), (D, half, bf16), (2 * rows, D, bf16)],
            [
                (out, q * half, col, half, half, [(2 * k + q, 0, 0)])
                for k in range(2)
                for q in range(2)
                for out, col in ((0, k * half), (1 + k, 0))
            ]
            + [(3, z * rows, 0, rows, D, [(4 + z, 0, 0)]) for z in range(2)],
        )
        near_there, beside, across, up_far, down_beside = together(
            swap_over(near, 0, 1),
            swap_over(left, 1, 0),
            swap_over(right, 0, 2),
            swap_over(up_pair, 4, 0),
            down_beside,
        )
        up_z, down_pair = merge(
            [up_pair, up_far, down_near, down_beside],
            [(half, D, bf16)] * 2,
            [
                (k, z * 2 * rows, 0, 2 * rows, D, [(2 * k + z, 0, 0)])
                for k in range(2)
                for z in range(2)
            ],
        )
        first = [near, beside, across, near_there] + over_core([beside, across])[2:]
        up = [up_z, swap_over(up_z, 1, 0), swap_over(up_z, 0, 2), swap_over(up_z, 1, 2)]
        down_far = swap_over(down_pair, 4, 0)
        places = (place_first, plane_moves(), edges_moves())
        pieces = [first, None, None]
    else:
        gathered = lax.all_gather(sent, "dp", axis=0, tiled=True).reshape(tile_total, -1)
        tiles = product(placing, gathered).astype(jnp.bfloat16)
        slabs = slabs_from_tiles(
            tiles.reshape(tile_total, PARTS, SUB, block_size), shards, block_size
        )
        whole = jnp.concatenate([slabs[part_of_block(k)] for k in range(PARTS)], 0)
        every = lax.all_gather(whole, "tensor", axis=0)
        pieces = [
            [every[j][:, k * D : (k + 1) * D] for j in range(shards)] for k in range(3)
        ]
        places = (place_kinds, groups_moves(shards), groups_moves(shards))

    packs_step = ROWS // length
    bias_qkv = jnp.stack(
        [bias_q.reshape(D), jnp.zeros((D,), jnp.float32), bias_v.reshape(D)]
    )
    pairs = HEADS // 2
    probs_spec = pl.BlockSpec((packs_step, pairs, length, 2 * length), lambda i: (i, 0, 0, 0))
    sums_spec = lambda width: pl.BlockSpec((8, width), lambda i: (0, 0))
    square = 2 * row_count * D * D

    whole_out = ((shards, D, D), bf16, pl.BlockSpec(memory_space=pltpu.VMEM))
    packed, probs, attended, unit_first, inverse_first, normed_low, whole_first = call_rows(
        functools.partial(attention_kernel, places[0], len(pieces[0]), length),
        steps,
        [
            far_rows(rows_in),
            (own_segments[:, None, :], pl.BlockSpec((packs_step, 1, length), lambda i: (i, 0, 0))),
            (own_segments[:, :, None], pl.BlockSpec((packs_step, length, 1), lambda i: (i, 0, 0))),
            full(bias_qkv),
            full(d_rows),
            *[raw(w) + (("far",) if w.shape == (D, D) else ()) for w in pieces[0]],
        ],
        [
            ((row_count, 3 * D), bf16, rows_spec(3 * D), "far"),
            ((pack_count, pairs, length, 2 * length), bf16, probs_spec, "far"),
            ((row_count, D), bf16, rows_spec(D)),
            ((row_count, D), f32, rows_spec(D), "far"),
            ((row_count, 1), f32, rows_spec(1), "far"),
            ((row_count, D), bf16, rows_spec(D), "far"),
            whole_out,
        ],
        4 * square + 4 * row_count * length * D,
        row_count * length * HEADS,
        [
            pltpu.VMEM((packs_step * pairs, length, 2 * length), f32),
            pltpu.SemaphoreType.DMA((len(pieces[0]),)),
            *[pltpu.VMEM(w.shape, bf16) for w in pieces[0]],
        ],
    )
    if direct:
        *up, up_there, down_far, normed_low = together(
            *up, swap_over(up[0], 0, 1), down_far, normed_low
        )
        down_near, near_left, near_right = merge(
            [down_pair, down_far],
            [(D, D, bf16), (D, half, bf16), (D, half, bf16)],
            [(0, z * half, 0, half, D, [(z, 0, 0)]) for z in range(2)]
            + [
                (1 + k, z * half, 0, half, half, [(z, 0, k * half)])
                for k in range(2)
                for z in range(2)
            ],
        )
        down = [down_near, swap_over(near_left, 1, 0), swap_over(near_right, 0, 2)]
        pieces[1] = up + [up_there] + over_core(up[1:])[3:]
        down[0], *pieces[1] = together(down[0], *pieces[1])
    activated, slope, whole_up = call_rows(
        functools.partial(up_kernel, places[1], shards),
        steps,
        [far_rows(normed_low), full(bias_up), *[raw(w) for w in pieces[1]]],
        [
            ((row_count, FF), bf16, rows_spec(FF)),
            ((row_count, FF), bf16, rows_spec(FF), "far"),
            whole_out,
        ],
        4 * square,
        2 * row_count * FF,
        [pltpu.SemaphoreType.DMA((len(places[1]),))],
    )
    if direct:
        *down, down_there, activated = together(*down, swap_over(down[0], 0, 1), activated)
        pieces[2] = down + [down_there] + over_core(down[1:])[2:]
    layer_out, grad_second, second_low, sums_second, whole_down = call_rows(
        functools.partial(down_kernel, places[2], shards),
        steps,
        [
            by_rows(activated),
            far_rows(unit_first),
            far_rows(grad_out),
            full(d_rows),
            *[raw(w) for w in pieces[2]],
        ],
        [
            ((row_count, D), f32, rows_spec(D), "far"),
            ((row_count, D), f32, rows_spec(D)),
            ((row_count, D), bf16, rows_spec(D)),
            ((8, D), f32, sums_spec(D)),
            whole_out,
        ],
        4 * square,
        0,
        [pltpu.SemaphoreType.DMA((len(places[2]),))],
    )
    grad_w_down = weight_halves([second_low], [(activated, up_width, 0)])
    if direct:
        down_parts = reduce_core_plane(grad_w_down)
        second_low, *down_parts = together(second_low, *down_parts)
        down_parts = reduce_plane(*down_parts)
    grad_pre, grad_bias_up = call_rows(
        functools.partial(hidden_back_kernel, shards),
        steps,
        [by_rows(second_low), far_rows(slope), full(whole_down)],
        [((row_count, FF), bf16, rows_spec(FF)), ((8, up_width), f32, sums_spec(up_width))],
        4 * square,
    )
    grad_w_up = weight_halves([normed_low], [(grad_pre, up_width, 0)])
    grad_first, first_low, grad_attended, sums_first = call_rows(
        functools.partial(back_kernel, shards),
        steps,
        [
            by_rows(grad_pre),
            by_rows(grad_second),
            far_rows(unit_first),
            far_rows(inverse_first),
            full(d_rows),
            full(whole_up),
            full(whole_first),
        ],
        [
            ((row_count, D), f32, rows_spec(D)),
            ((row_count, D), bf16, rows_spec(D)),
            ((row_count, D), bf16, rows_spec(D)),
            ((8, D), f32, sums_spec(D)),
        ],
        20 * square,
    )
    if direct:
        up_parts = reduce_core_edges(grad_w_up)
        grad_attended, *parts = together(grad_attended, *up_parts, *down_parts)
        up_terms = edge_terms(*parts[:3])
        down_terms = [parts[3], swap_over(parts[4], 4, 0)]
    grad_packed, column_sums = call_rows(
        functools.partial(attention_back_kernel, length),
        steps,
        [by_rows(grad_attended), by_rows(attended), far_rows(packed), (probs, probs_spec, "far")],
        [
            ((row_count, 3 * D), bf16, rows_spec(3 * D)),
            ((8, 3 * D), f32, sums_spec(3 * D)),
        ],
        8 * square,
        0,
        [pltpu.VMEM((packs_step * pairs, length, 2 * length), bf16)] * 2,
    )
    (vector_rows,) = call_rows(
        functools.partial(vector_kernel, shards),
        1,
        [
            (
                lax.convert_element_type(group_base, jnp.int32).reshape(1),
                pl.BlockSpec(memory_space=pltpu.SMEM),
            ),
            full(sums_first),
            full(sums_second),
            full(grad_bias_up),
            full(column_sums),
            full(selector),
        ],
        [((16, D), f32, pl.BlockSpec(memory_space=pltpu.VMEM))],
        48 * D * D,
    )
    if direct:
        vector_rows, grad_packed, *others = together(
            vector_rows, grad_packed, *down_terms, *up_terms
        )
        down_terms, up_terms = others[:2], others[2:]
        up_near, up_far, grad_packed = together(*reduce_edges(up_terms), grad_packed)
        up_terms = [up_near, swap_over(up_far, 4, 0)]
        down_terms = halve_z(*down_terms)
        down_terms = [down_terms[0], swap_over(down_terms[1], 2, 0)]
    else:
        vector_rows = lax.psum(vector_rows, ("dp", "tensor"))
    grad_w_first = weight_halves(
        [rows_in, first_low],
        [(grad_packed, head_width, k * shards // 2) for k in range(3)] + [(attended, head_width, 0)],
    )
    if direct:
        first_parts = reduce_core_edges(grad_w_first)
        *first_parts, grad_first = together(*first_parts, grad_first)
        first_terms = edge_terms(*first_parts)
    (input_grad,) = call_rows(
        input_kernel,
        steps,
        [by_rows(grad_first), by_rows(grad_packed), full(selector), full(whole_first)],
        [((row_count, D), f32, rows_spec(D), "far")],
        40 * square,
    )
    if direct:
        *others, input_grad, layer_out = together(
            *first_terms, *down_terms, input_grad, layer_out
        )
        first_terms, down_terms = others[:3], others[3:]
        first_terms = plane_edge_terms(*reduce_edges_plane(first_terms))
        first_terms[0], *up_terms = together(first_terms[0], *up_terms)
        up_terms = halve_z(*up_terms)
        up_terms = [up_terms[0], swap_over(up_terms[1], 2, 0)]
        down_own = add_z(*down_terms)
    (layer_out,) = call_rows(
        layer_kernel,
        steps,
        [far_rows(layer_out), full(selector)],
        [((row_count, D), f32, rows_spec(D), "far")],
        2 * square,
    )
    if direct:
        *first_terms, layer_out = together(*first_terms, layer_out)
        *parts, vector_rows = together(*reduce_plane_edges(first_terms), vector_rows)
        first_terms = z_terms(*parts)
        first_terms[0], *up_terms = together(first_terms[0], *up_terms)
        vector_rows = add_swapped(add_swapped(vector_rows, 0, 1), 0, 2)
        up_terms = plane_edge_terms(*reduce_edges_z(up_terms))
        up_own = reduce_edges_last(up_terms)
        *first_terms, vector_rows = together(*first_terms, vector_rows)
        first_own = reduce_z(first_terms)
        slab_grad = jnp.concatenate([first_own, up_own, down_own], 1).astype(jnp.bfloat16)
        tile_grad = tiles_from_slabs(slab_grad[None], shards, block_size).reshape(tile_total, -1)
        slot_grad = transposed_times(placing, tile_grad).astype(jnp.bfloat16)
        slot_grad, vector_rows = together(slot_grad, vector_rows)
        slot_grad = lax.all_to_all(
            slot_grad.reshape(PARTS, slots, SUB * block_size), "dp", 0, 0, tiled=True
        )
        vector_rows = add_swapped(add_swapped(vector_rows, 1, 0), 2, 0)
        slot_grad, vector_rows = together(slot_grad, vector_rows)
        vector_rows = add_swapped(vector_rows, 4, 0)
        owned_grads = slot_grad.swapaxes(0, 1).reshape(slots, block_size, block_size)
    else:
        every = jnp.stack(
            [
                jnp.concatenate(
                    [half[1 - j % 2][j // 2] for half in (grad_w_first, grad_w_up, grad_w_down)], 1
                )
                for j in range(shards)
            ]
        ).astype(jnp.float32)
        mine = lax.psum_scatter(every, "tensor", scatter_dimension=0, tiled=True)[0]
        blocks = mine.reshape(PARTS, D // PARTS, -1)
        blocks = jnp.stack([blocks[(p % 2) * 4 + p // 2] for p in range(PARTS)])
        tile_grad = tiles_from_slabs(blocks, shards, block_size)
        slot_grad = tile_grad.reshape(tile_total, block_size, block_size)[owner]
        owned_grads = lax.psum_scatter(slot_grad, "dp", scatter_dimension=0, tiled=True)
    owned_grads = jnp.where(own_flip, jnp.swapaxes(owned_grads, 1, 2), owned_grads)

    bias_first = 1.0 - DECAY_FIRST**ADAM_STEP
    bias_second = 1.0 - DECAY_SECOND**ADAM_STEP
    step_slots = max(k for k in (1, 2, 3, 4, 6, 12) if slots % k == 0)
    slots_spec = pl.BlockSpec((step_slots, block_size, block_size), lambda i: (i, 0, 0))
    slot_out = ((slots, block_size, block_size), f32, slots_spec, "far")
    new_master, new_first, new_second = call_rows(
        adam_kernel,
        slots // step_slots,
        [
            (array, slots_spec, "far")
            for array in (
                owned_grads,
                master[0],
                left_basis[0],
                right_basis[0],
                first_moment[0],
                second_moment[0],
            )
        ],
        [slot_out] * 3,
        22 * slots * block_size**3,
        slots * block_size**2,
    )
    vector_grad = vector_rows[: vectors.shape[0] // D].reshape(-1)
    new_vector_first = DECAY_FIRST * vector_first + (1.0 - DECAY_FIRST) * vector_grad
    new_vector_second = (
        DECAY_SECOND * vector_second + (1.0 - DECAY_SECOND) * vector_grad * vector_grad
    )
    new_vectors = vectors - VECTOR_RATE * (new_vector_first / bias_first) / (
        jnp.sqrt(new_vector_second / bias_second) + ADAM_EPS
    )
    return (
        layer_out,
        input_grad,
        new_master[None],
        new_first[None],
        new_second[None],
        new_vectors,
        new_vector_first,
        new_vector_second,
    )


def solution(mesh):
    return jax.shard_map(
        local,
        mesh=mesh,
        in_specs=(
            P(("dp", "tensor"), None),
            P("dp", None),
            P(("dp", "tensor"), None),
            P(),
            P("tensor", "dp", None, None),
            P("tensor", "dp", None, None),
            P("tensor", "dp", None, None),
            P("tensor", "dp", None, None),
            P("tensor", "dp", None, None),
            P(),
            P(),
            P(),
        ),
        out_specs=(
            P(("dp", "tensor"), None),
            P(("dp", "tensor"), None),
            P("tensor", "dp", None, None),
            P("tensor", "dp", None, None),
            P("tensor", "dp", None, None),
            P(),
            P(),
            P(),
        ),
        check_vma=False,
    )
```

```python
import functools
import math

import jax
import jax.numpy as jnp
from jax import lax
from jax.experimental import pallas as pl
from jax.experimental.pallas import tpu as pltpu
from jax.sharding import PartitionSpec as P

HEADS = 12
HEAD_DIM = 64
D = 768
FF = 3072
ADAM_STEP = 3


NORM_EPS = 1e-12
ADAM_EPS = 1e-08
MATRIX_RATE = 0.01
VECTOR_RATE = 0.1
DECAY_FIRST = 0.5
DECAY_SECOND = 0.5
MASKED = -1e30


def product(left_side, right_side):
    return jnp.dot(left_side, right_side, preferred_element_type=jnp.float32)


def times_transposed(left_side, right_side):
    return lax.dot_general(
        left_side, right_side, (((1,), (1,)), ((), ())), preferred_element_type=jnp.float32
    )


def transposed_times(left_side, right_side):
    return lax.dot_general(
        left_side, right_side, (((0,), (0,)), ((), ())), preferred_element_type=jnp.float32
    )


VMEM_LIMIT = 16 * 1024 * 1024

PARTS = 8
SUB = 12


def part_of_block(block):
    return (block % 4) * 2 + block // 4


def feature_order(rank):
    place = lax.iota(jnp.int32, D)
    part = part_of_block(place // (D // PARTS)) ^ rank
    inner = place % (D // PARTS)
    return (inner // SUB) * (PARTS * SUB) + part * SUB + inner % SUB


def tile_counts(shards, block_size):
    rows = D // block_size
    qkv = rows * (3 * D // shards // block_size)
    out = rows * (D // shards // block_size)
    up = rows * (FF // shards // block_size)
    return (qkv, out, up)


def slabs_from_tiles(tiles, shards, block_size):
    cut = tiles.shape[1]
    qkv, out, up = tile_counts(shards, block_size)
    rows = D // block_size

    def by_rows(part):
        cols = part.shape[0] // rows
        part = part.reshape(rows, cols, cut, SUB, block_size)
        return part.transpose(2, 0, 3, 1, 4).reshape(cut, rows * SUB, cols * block_size)

    def by_cols(part):
        cols = part.shape[0] // rows
        part = part.reshape(cols, rows, cut, SUB, block_size)
        return part.transpose(2, 1, 3, 0, 4).reshape(cut, rows * SUB, cols * block_size)

    return jnp.concatenate(
        [
            by_rows(tiles[:qkv]),
            by_cols(tiles[qkv : qkv + out]),
            by_rows(tiles[qkv + out : qkv + out + up]),
            by_cols(tiles[qkv + out + up :]),
        ],
        2,
    )


def tiles_from_slabs(slabs, shards, block_size):
    cut = slabs.shape[0]
    rows = D // block_size
    width_qkv, width_out, width_up = 3 * D // shards, D // shards, FF // shards

    def by_rows(part):
        cols = part.shape[2] // block_size
        part = part.reshape(cut, rows, SUB, cols, block_size)
        return part.transpose(1, 3, 0, 2, 4).reshape(rows * cols, cut, SUB, block_size)

    def by_cols(part):
        cols = part.shape[2] // block_size
        part = part.reshape(cut, rows, SUB, cols, block_size)
        return part.transpose(3, 1, 0, 2, 4).reshape(rows * cols, cut, SUB, block_size)

    first = width_qkv + width_out
    second = first + width_up
    return jnp.concatenate(
        [
            by_rows(slabs[:, :, :width_qkv]),
            by_cols(slabs[:, :, width_qkv:first]),
            by_rows(slabs[:, :, first:second]),
            by_cols(slabs[:, :, second:]),
        ],
        0,
    )


def swap_over(values, over_dp, over_tensor):
    dp, tensor = lax.axis_size("dp"), lax.axis_size("tensor")
    pairs = [
        (a * tensor + b, (a ^ over_dp) * tensor + (b ^ over_tensor))
        for a in range(dp)
        for b in range(tensor)
    ]
    return lax.ppermute(values, ("dp", "tensor"), pairs)


def merge(terms, outs, segments):
    chunk = D // PARTS

    def kernel(*refs):
        for out, row, col, rows, cols, parts in segments:

            def step(k, carry, out=out, row=row, col=col, cols=cols, parts=parts):
                pieces = [
                    refs[term][pl.ds(pl.multiple_of(at + k * chunk, 32), chunk), left : left + cols]
                    for term, at, left in parts
                ]
                if len(pieces) > 1:
                    value = sum(piece.astype(jnp.float32) for piece in pieces)
                else:
                    value = pieces[0]
                to = refs[len(terms) + out]
                to[pl.ds(pl.multiple_of(row + k * chunk, 32), chunk), col : col + cols] = (
                    value.astype(to.dtype)
                )
                return carry

            lax.fori_loop(0, rows // chunk, step, 0)

    spec = pl.BlockSpec(memory_space=pltpu.VMEM)
    size = sum(term.size for term in terms)
    return pl.pallas_call(
        kernel,
        in_specs=[spec] * len(terms),
        out_specs=[spec] * len(outs),
        out_shape=[jax.ShapeDtypeStruct((rows, cols), dtype) for rows, cols, dtype in outs],
        compiler_params=pltpu.CompilerParams(vmem_limit_bytes=VMEM_LIMIT),
        cost_estimate=pl.CostEstimate(flops=size, bytes_accessed=4 * size, transcendentals=0),
    )(*terms)


def from_z(block):
    return [swap_over(block, 2 * k, 0) for k in (1, 2, 3)]


def over_core(blocks):
    return blocks + [swap_over(block, 0, 1) for block in blocks]


def put(out_ref, lead, row, col, ref, at, left, rows, cols):
    chunk = min(rows, D // 2)

    def step(k, carry):
        to = pl.multiple_of(row + k * chunk, 32)
        source = pl.multiple_of(at + k * chunk, 32)
        out_ref[lead, pl.ds(to, chunk), col : col + cols] = ref[
            pl.ds(source, chunk), left : left + cols
        ]
        return carry

    lax.fori_loop(0, rows // chunk, step, 0)


def place_first(refs, out_ref):
    count = len(refs) // 2
    half, width = D // 2, D // 4
    for core in range(2):
        near, beside, across = refs[core * count : (core + 1) * count]
        for y in range(2):
            col = (2 * y + core) * width
            for kind in range(2):
                left = kind * width
                put(out_ref, kind, 0, col, near, y * half, left, half, width)
                put(out_ref, kind, half, col, beside, y * half, left, half, width)
                if y:
                    put(out_ref, 2 + kind, 0, col, across, 0, left, D, width)
                else:
                    put(out_ref, 2 + kind, 0, col, near, 0, half + left, D, width)


def edges_moves():
    rows, half = D // PARTS, D // 2
    moves = []
    for core in range(2):
        near, beside, across = range(3 * core, 3 * core + 3)
        for y in range(2):
            group = 2 * y + core
            for z in range(4):
                for x in range(2):
                    to, by_y, by_x = x * half + z * rows, (2 * z + y) * rows, (2 * z + x) * rows
                    moves.append((group, to, 0, beside if x else near, by_y, 0, rows, half))
                    source = (across, by_x, 0) if y else (near, by_x, half)
                    moves.append((group, to, half, *source, rows, half))
    return moves


def plane_moves():
    half = D // 2
    return [
        (2 * y + core, x * half, 0, 4 * core + 2 * y + x, 0, 0, half, D)
        for core in range(2)
        for y in range(2)
        for x in range(2)
    ]


def groups_moves(count):
    return [(group, 0, 0, group, 0, 0, D, D) for group in range(count)]


def move_all(moves, refs, out_ref, sems):
    copies = [
        pltpu.make_async_copy(
            refs[ref].at[pl.ds(at, rows), pl.ds(left, cols)],
            out_ref.at[lead, pl.ds(row, rows), pl.ds(col, cols)],
            sems.at[k],
        )
        for k, (lead, row, col, ref, at, left, rows, cols) in enumerate(moves)
    ]
    for copy in copies:
        copy.start()
    for copy in copies:
        copy.wait()


def place_kinds(refs, out_ref):
    width = D // len(refs)
    for group, ref in enumerate(refs):
        for kind in range(4):
            put(out_ref, kind, 0, group * width, ref, 0, kind * width, D, width)


def core_terms(halves):
    odd, even = halves
    return [even.reshape(2 * D, D), swap_over(odd, 0, 1).reshape(2 * D, D)]


def summed(count, row, col):
    return [(term, row, col) for term in range(count)]


def reduce_core_plane(halves):
    half = D // 2
    return merge(
        core_terms(halves),
        [(half, D, jnp.bfloat16)] * 4,
        [(k, 0, 0, half, D, summed(2, k * half, 0)) for k in range(4)],
    )


def reduce_plane(near, beside, across, opposite):
    pair = D // 4
    terms = [near, swap_over(beside, 1, 0), swap_over(across, 0, 2), swap_over(opposite, 1, 2)]
    return merge(
        terms,
        [(pair, D, jnp.bfloat16)] * 2,
        [(k, 0, 0, pair, D, summed(4, k * pair, 0)) for k in range(2)],
    )


def halve_z(near, received):
    rows = near.shape[0] // 2
    return merge(
        [near, received],
        [(rows, D, jnp.bfloat16)] * 2,
        [(k, 0, 0, rows, D, summed(2, k * rows, 0)) for k in range(2)],
    )


def add_z(near, received):
    rows = near.shape[0]
    return merge(
        [near, received], [(rows, D, jnp.float32)], [(0, 0, 0, rows, D, summed(2, 0, 0))]
    )[0]


def z_terms(own, *sent):
    return [own] + [swap_over(block, 2 * (k + 1), 0) for k, block in enumerate(sent)]


def reduce_z(terms):
    rows = D // PARTS
    return merge(terms, [(rows, D, jnp.float32)], [(0, 0, 0, rows, D, summed(4, 0, 0))])[0]


def reduce_core_edges(halves):
    half = D // 2
    return merge(
        core_terms(halves),
        [(D, D, jnp.bfloat16), (D, half, jnp.bfloat16), (D, half, jnp.bfloat16)],
        [
            (0, 0, 0, half, half, summed(2, 0, 0)),
            (0, half, 0, half, half, summed(2, D, 0)),
            (0, 0, half, D, half, summed(2, 0, half)),
            (1, 0, 0, half, half, summed(2, half, 0)),
            (1, half, 0, half, half, summed(2, D + half, 0)),
            (2, 0, 0, D, half, summed(2, D, half)),
        ],
    )


def edge_terms(near, left, right):
    return [near, swap_over(left, 1, 0), swap_over(right, 0, 2)]


def edge_sums(row):
    half = D // 2
    return ((0, [(0, row, 0), (1, row, 0)]), (half, [(0, row, half), (2, row, 0)]))


def plane_edge_terms(near, left, right):
    return [near, swap_over(left, 0, 2), swap_over(right, 1, 0)]


def reduce_edges_plane(terms):
    half = D // 2
    kept = [(0, 0, col, half, half, parts) for col, parts in edge_sums(0)]
    sent = [
        (1 + k, 0, 0, half, half, parts) for k, (_, parts) in enumerate(edge_sums(half))
    ]
    return merge(
        terms,
        [(half, D, jnp.bfloat16), (half, half, jnp.bfloat16), (half, half, jnp.bfloat16)],
        kept + sent,
    )


def reduce_plane_edges(terms):
    rows, half = D // PARTS, D // 2
    return merge(
        terms,
        [(rows, D, jnp.bfloat16)] * 4,
        [
            (k, 0, col, rows, half, parts)
            for k in range(4)
            for col, parts in edge_sums(k * rows)
        ],
    )


def reduce_edges(terms):
    rows, half = D // PARTS, D // 2
    return merge(
        terms,
        [(half, D, jnp.bfloat16)] * 2,
        [
            (k // 2, (2 * (k % 2) + q) * rows, col, rows, half, parts)
            for k in range(4)
            for q in range(2)
            for col, parts in edge_sums(q * half + k * rows)
        ],
    )


def reduce_edges_z(terms):
    rows, half = D // PARTS, D // 2
    return merge(
        terms,
        [(rows, D, jnp.bfloat16), (rows, half, jnp.bfloat16), (rows, half, jnp.bfloat16)],
        [
            (0, 0, 0, rows, D, summed(2, 0, 0)),
            (1, 0, 0, rows, half, summed(2, rows, 0)),
            (2, 0, 0, rows, half, summed(2, rows, half)),
        ],
    )


def reduce_edges_last(terms):
    rows, half = D // PARTS, D // 2
    return merge(
        terms,
        [(rows, D, jnp.float32)],
        [(0, 0, col, rows, half, parts) for col, parts in edge_sums(0)],
    )[0]


def add_swapped(values, over_dp, over_tensor):
    return values + swap_over(values, over_dp, over_tensor)


ROWS = 256


def dot_nt(left_side, right_side):
    return lax.dot_general(
        left_side, right_side, (((1,), (1,)), ((), ())), preferred_element_type=jnp.float32
    )


def row_block(array):
    return pl.BlockSpec((ROWS, array.shape[1]), lambda i: (i, 0))


def call_rows(kernel, steps, inputs, outputs, flops, transcendentals=0, scratch=()):
    arrays = [
        pltpu.with_memory_space_constraint(array, pltpu.HBM) if far else array
        for array, _, *far in inputs
    ]
    shapes = [jax.ShapeDtypeStruct(shape, dtype) for shape, dtype, *_ in outputs]
    moved = sum(a.size * a.dtype.itemsize for a in arrays + shapes)
    shapes = [
        pltpu.HBM(shape.shape, shape.dtype) if len(output) > 3 else shape
        for shape, output in zip(shapes, outputs)
    ]
    return pl.pallas_call(
        kernel,
        grid=(steps,),
        in_specs=[spec for _, spec, *_ in inputs],
        out_specs=[output[2] for output in outputs],
        out_shape=shapes,
        scratch_shapes=scratch,
        compiler_params=pltpu.CompilerParams(vmem_limit_bytes=VMEM_LIMIT),
        cost_estimate=pl.CostEstimate(
            flops=int(1.0 * flops), bytes_accessed=moved, transcendentals=transcendentals
        ),
    )(*arrays)


def norm_rows(summed):
    centred = summed - jnp.mean(summed, -1, keepdims=True)
    inverse = lax.rsqrt(jnp.mean(centred * centred, -1, keepdims=True) + NORM_EPS)
    return centred * inverse, inverse


def norm_pull(gradient, unit_rows, inverse, gain_row):
    scaled = gradient * gain_row
    return inverse * (
        scaled
        - jnp.mean(scaled, -1, keepdims=True)
        - unit_rows * jnp.mean(scaled * unit_rows, -1, keepdims=True)
    )


def add_rows(ref, rows):
    sums = [jnp.sum(row, 0, keepdims=True) for row in rows]
    start = pl.program_id(0) == 0
    for place, total in enumerate(sums):
        kept = jnp.where(start, 0.0, ref[place : place + 1, :])
        ref[place : place + 1, :] = kept + total


def settle(moves, refs, whole_ref, sems):
    @pl.when(pl.program_id(0) == 0)
    def _():
        move_all(moves, refs, whole_ref, sems)

    return [whole_ref.at[j] for j in range(whole_ref.shape[0])]


def pair_masks(length):
    wide = 2 * HEAD_DIM
    lower = lax.broadcasted_iota(jnp.int32, (length, wide), 1) < HEAD_DIM
    top = lax.broadcasted_iota(jnp.int32, (2 * length, wide), 0) < length
    left = lax.broadcasted_iota(jnp.int32, (2 * length, wide), 1) < HEAD_DIM
    return lower, top == left


def stacked(pair, own):
    return jnp.where(own, jnp.concatenate([pair, pair], 0), jnp.zeros((), pair.dtype))


def attention_kernel(place, total_count, length, *refs):
    rows_ref, across_ref, down_ref, bias_ref, vec_ref = refs[:5]
    outs = refs[5 + total_count : 12 + total_count]
    packed_ref, probs_ref, attended_ref, unit_ref, inverse_ref, low_ref, whole_ref = outs
    scores_ref, sems, *raw = refs[12 + total_count :]

    @pl.when(pl.program_id(0) == 0)
    def _():
        copies = [
            pltpu.make_async_copy(source, to, sems.at[k])
            for k, (source, to) in enumerate(zip(refs[5 : 5 + total_count], raw))
        ]
        for copy in copies:
            copy.start()
        for copy in copies:
            copy.wait()
        place(raw, whole_ref)

    weights = [whole_ref.at[kind] for kind in range(4)]
    wide = 2 * HEAD_DIM
    pairs = HEADS // 2
    rows = rows_ref[...]
    for kind in range(3):
        part = product(rows, weights[kind][...]) + bias_ref[kind : kind + 1, :]
        part = part.astype(jnp.bfloat16)
        if kind == 0:
            part = part * jnp.bfloat16(HEAD_DIM ** (-0.5))
        packed_ref[:, kind * D : (kind + 1) * D] = part
    _, own = pair_masks(length)
    ones = own.astype(jnp.bfloat16)
    steps = [(p, i) for p in range(ROWS // length) for i in range(pairs)]

    def pair_of(p, i, kind):
        span = slice(p * length, (p + 1) * length)
        return packed_ref[span, kind * D + i * wide : kind * D + (i + 1) * wide]

    for at, (p, i) in enumerate(steps):
        scores_ref[at] = dot_nt(pair_of(p, i, 0), stacked(pair_of(p, i, 1), own))
    for at, (p, i) in enumerate(steps):
        allowed = down_ref[p] == across_ref[p]
        for half in range(2):
            lanes = slice(half * length, (half + 1) * length)
            scores = jnp.where(allowed, scores_ref[at, :, lanes], MASKED)
            probs_ref[p, i, :, lanes] = jnp.exp(
                scores - jnp.max(scores, -1, keepdims=True)
            ).astype(jnp.bfloat16)
    for p, i in steps:
        mixed = product(
            probs_ref[p, i], jnp.concatenate([stacked(pair_of(p, i, 2), own), ones], 1)
        )
        attended_ref[p * length : (p + 1) * length, i * wide : (i + 1) * wide] = (
            mixed[:, :wide] / mixed[:, wide:]
        ).astype(jnp.bfloat16)
    summed = rows.astype(jnp.float32) + vec_ref[0:1, :]
    summed = summed + dot_nt(attended_ref[...], weights[3][...])
    unit, inverse = norm_rows(summed)
    unit_ref[...] = unit
    inverse_ref[...] = inverse
    low_ref[...] = (unit * vec_ref[1:2, :] + vec_ref[2:3, :]).astype(jnp.bfloat16)


def gelu_parts(values):
    size = jnp.abs(values)
    decay = jnp.exp2(values * values * (-0.5 / math.log(2.0)))
    t = 1.0 / (1.0 + size * (0.3275911 * 0.5**0.5))
    poly = t * (
        0.127414796
        + t * (-0.142248368 + t * (0.7107068705 + t * (-0.7265760135 + t * 0.5307027145)))
    )
    result = jnp.maximum(values, 0.0) - size * (poly * decay)
    rest = decay * (poly - size * (0.5 / math.pi) ** 0.5)
    return result, jnp.where(values > 0, 1.0 - rest, rest)


def up_kernel(place, shards, *refs):
    low_ref, bias_ref = refs[:2]
    act_ref, slope_ref, whole_ref, sems = refs[-4:]
    weights = settle(place, refs[2:-4], whole_ref, sems)
    width = weights[0].shape[1]
    chunk = 256
    low = low_ref[...]
    for j in range(shards):
        for c in range(0, width, chunk):
            pre = product(low, weights[j][:, c : c + chunk]) + bias_ref[j : j + 1, c : c + chunk]
            result, slope = gelu_parts(pre)
            at = j * width + c
            act_ref[:, at : at + chunk] = result.astype(jnp.bfloat16)
            slope_ref[:, at : at + chunk] = slope.astype(jnp.bfloat16)


def down_kernel(place, shards, *refs):
    act_ref, unit_ref, grad_ref, vec_ref = refs[:4]
    out_ref, dz_ref, low_ref, sums_ref, whole_ref, sems = refs[-6:]
    weights = settle(place, refs[4:-6], whole_ref, sems)
    width = weights[0].shape[1]
    summed = unit_ref[...] * vec_ref[1:2, :] + vec_ref[2:3, :] + vec_ref[3:4, :]
    for j in range(shards):
        summed = summed + dot_nt(act_ref[:, j * width : (j + 1) * width], weights[j][...])
    unit, inverse = norm_rows(summed)
    gain = vec_ref[4:5, :]
    out_ref[...] = unit * gain + vec_ref[5:6, :]
    gradient = grad_ref[...]
    dz = norm_pull(gradient, unit, inverse, gain)
    dz_ref[...] = dz
    low_ref[...] = dz.astype(jnp.bfloat16)
    add_rows(sums_ref, (gradient * unit, gradient, dz))


def hidden_back_kernel(shards, *refs):
    low_ref, slope_ref, whole_ref, dpre_ref, bias_sums_ref = refs
    width = whole_ref.shape[2]
    low = low_ref[...]
    for j in range(shards):
        span = slice(j * width, (j + 1) * width)
        dpre = product(low, whole_ref[j]) * slope_ref[:, span].astype(jnp.float32)
        dpre = dpre.astype(jnp.bfloat16)
        dpre_ref[:, span] = dpre
        total = jnp.sum(dpre.astype(jnp.float32), 0, keepdims=True)
        kept = jnp.where(pl.program_id(0) == 0, 0.0, bias_sums_ref[j : j + 1, :])
        bias_sums_ref[j : j + 1, :] = kept + total


def back_kernel(shards, *refs):
    dpre_ref, dz_ref, unit_ref, inverse_ref, vec_ref, up_ref, first_ref = refs[:7]
    dz1_ref, low1_ref, datt_ref, sums_ref = refs[7:]
    width = up_ref.shape[2]
    gradient = dz_ref[...]
    for j in range(shards):
        gradient = gradient + dot_nt(dpre_ref[:, j * width : (j + 1) * width], up_ref[j])
    unit = unit_ref[...]
    dz1 = norm_pull(gradient, unit, inverse_ref[...], vec_ref[1:2, :])
    dz1_ref[...] = dz1
    low1 = dz1.astype(jnp.bfloat16)
    low1_ref[...] = low1
    add_rows(sums_ref, (gradient * unit, gradient, dz1))
    datt_ref[...] = product(low1, first_ref[3]).astype(jnp.bfloat16)


def attention_back_kernel(length, *refs):
    datt_ref, attended_ref, packed_ref, probs_ref, dpacked_ref, sums_ref, up_ref, grad_ref = refs
    wide = 2 * HEAD_DIM
    lower, own = pair_masks(length)
    ones = own.astype(jnp.bfloat16)
    steps = [(p, i) for p in range(ROWS // length) for i in range(HEADS // 2)]

    def pair_of(p, i, kind):
        span = slice(p * length, (p + 1) * length)
        return packed_ref[span, kind * D + i * wide : kind * D + (i + 1) * wide]

    def keep(p, i, kind, grad):
        span = slice(p * length, (p + 1) * length)
        dpacked_ref[span, kind * D + i * wide : kind * D + (i + 1) * wide] = grad.astype(
            jnp.bfloat16
        )

    for place, (p, i) in enumerate(steps):
        span = slice(p * length, (p + 1) * length)
        lanes = slice(i * wide, (i + 1) * wide)
        upstream = datt_ref[span, lanes].astype(jnp.float32) / product(probs_ref[p, i], ones)
        up_ref[place, :, :wide] = upstream.astype(jnp.bfloat16)
        up_ref[place, :, wide:] = (upstream * attended_ref[span, lanes].astype(jnp.float32)).astype(
            jnp.bfloat16
        )
    for place, (p, i) in enumerate(steps):
        centred = dot_nt(
            up_ref[place], jnp.concatenate([stacked(pair_of(p, i, 2), own), -ones], 1)
        )
        grad_ref[place] = (probs_ref[p, i].astype(jnp.float32) * centred).astype(jnp.bfloat16)
    for place, (p, i) in enumerate(steps):
        grad_scores = grad_ref[place]
        keep(
            p, i, 0,
            product(grad_scores, stacked(pair_of(p, i, 1), own)) * HEAD_DIM ** (-0.5),
        )
        both = transposed_times(grad_scores, pair_of(p, i, 0))
        keep(p, i, 1, jnp.where(lower, both[:length], both[length:]))
        both = transposed_times(probs_ref[p, i], up_ref[place, :, :wide])
        keep(p, i, 2, jnp.where(lower, both[:length], both[length:]))
    total = jnp.sum(dpacked_ref[...].astype(jnp.float32), 0, keepdims=True)
    kept = jnp.where(pl.program_id(0) == 0, 0.0, sums_ref[0:1, :])
    sums_ref[0:1, :] = kept + total


def weight_kernel(odd, count, *refs):
    lefts, refs = refs[:2] if count > 1 else refs[:1], refs[2 if count > 1 else 1 :]
    rights, (out_ref, *turned) = refs[:count], refs[count:]
    start = pl.program_id(0) == 0

    @pl.when(start)
    def _():
        for left, kept in zip(lefts, turned):
            kept[...] = left[...].T

    at = 0
    for place, right in enumerate(rights):
        half = right.shape[1] // 2
        values = right[...] if count == 1 else right[:, half:] if odd else right[:, :half]
        grad = product(turned[place == count - 1 and count > 1][...], values)
        out_ref[0, :, at : at + values.shape[1]] = grad.astype(jnp.bfloat16)
        at += values.shape[1]


def weight_half(odd, lefts, rights):
    count = len(rights)
    single = count == 1
    specs = []
    for array, width, before in rights:
        if single:
            specs.append(pl.BlockSpec((array.shape[0], width), lambda i: (0, 2 * i + odd)))
        else:
            specs.append(pl.BlockSpec((array.shape[0], 2 * width), lambda i, b=before: (0, b + i)))
    arrays = [*lefts, *[array for array, _, _ in rights]]
    tokens = lefts[0].shape[0]
    (half,) = pl.pallas_call(
        functools.partial(weight_kernel, odd, count),
        grid=(2,),
        in_specs=[pl.BlockSpec(memory_space=pltpu.VMEM) for _ in lefts] + specs,
        out_specs=[pl.BlockSpec((1, D, D), lambda i: (i, 0, 0))],
        out_shape=[jax.ShapeDtypeStruct((2, D, D), jnp.bfloat16)],
        scratch_shapes=[pltpu.VMEM((D, tokens), jnp.bfloat16) for _ in lefts],
        compiler_params=pltpu.CompilerParams(vmem_limit_bytes=VMEM_LIMIT),
        cost_estimate=pl.CostEstimate(
            flops=4 * tokens * D * D,
            bytes_accessed=sum(2 * array.size for array in arrays),
            transcendentals=0,
        ),
    )(*arrays)
    return half


def weight_halves(lefts, rights):
    return [weight_half(odd, lefts, rights) for odd in (1, 0)]


def two_terms(values):
    top = values.astype(jnp.bfloat16)
    return top, (values - top.astype(jnp.float32)).astype(jnp.bfloat16)


def adam_kernel(*refs):
    grad_ref, master_ref, left_ref, right_ref, first_ref, second_ref = refs[:6]
    master_out, first_out, second_out = refs[6:]
    bias_first = 1.0 - DECAY_FIRST**ADAM_STEP
    bias_second = 1.0 - DECAY_SECOND**ADAM_STEP
    count = grad_ref.shape[0]
    lefts = [two_terms(left_ref[k]) for k in range(count)]
    rights = [two_terms(right_ref[k]) for k in range(count)]
    turned = []
    for k in range(count):
        grad = product(grad_ref[k].astype(jnp.bfloat16), rights[k][0])
        grad = grad + product(grad_ref[k].astype(jnp.bfloat16), rights[k][1])
        if grad_ref.dtype != jnp.bfloat16:
            grad = grad + product(two_terms(grad_ref[k])[1], rights[k][0])
        turned.append(grad)
    directions = []
    for k in range(count):
        top, rest = two_terms(turned[k])
        rotated = (
            transposed_times(lefts[k][0], top)
            + transposed_times(lefts[k][0], rest)
            + transposed_times(lefts[k][1], top)
        )
        first = DECAY_FIRST * first_ref[k] + (1.0 - DECAY_FIRST) * rotated
        second = DECAY_SECOND * second_ref[k] + (1.0 - DECAY_SECOND) * rotated * rotated
        first_out[k] = first
        second_out[k] = second
        directions.append(first / bias_first / (jnp.sqrt(second / bias_second) + ADAM_EPS))
    backs = [
        product(lefts[k][0], directions[k].astype(jnp.bfloat16)).astype(jnp.bfloat16)
        for k in range(count)
    ]
    for k in range(count):
        update = times_transposed(backs[k], rights[k][0])
        master_out[k] = master_ref[k] - MATRIX_RATE * update


def two_terms(values):
    top = values.astype(jnp.bfloat16)
    return top, (values - top.astype(jnp.float32)).astype(jnp.bfloat16)


def unpermuted(values, selector_ref):
    top, rest = two_terms(values)
    return dot_nt(top, selector_ref[...]) + dot_nt(rest, selector_ref[...])


def enter_kernel(tokens_ref, grad_ref, vectors_ref, selector_ref, rows_ref, out_ref, d_rows_ref):
    selector = selector_ref[...]
    rows_ref[...] = product(tokens_ref[...], selector).astype(jnp.bfloat16)
    top, rest = two_terms(grad_ref[...])
    out_ref[...] = product(top, selector) + product(rest, selector)

    @pl.when(pl.program_id(0) == 0)
    def _():
        rows = vectors_ref[...]
        permuted = jnp.zeros(rows.shape, jnp.float32)
        for _ in range(3):
            term = rows.astype(jnp.bfloat16)
            rows = rows - term.astype(jnp.float32)
            permuted = permuted + product(term, selector)
        d_rows_ref[...] = permuted


def layer_kernel(out_ref, selector_ref, layer_ref):
    layer_ref[...] = unpermuted(out_ref[...], selector_ref)


def input_kernel(dz1_ref, dpacked_ref, selector_ref, whole_ref, input_ref):
    gradient = dz1_ref[...]
    for kind in range(3):
        gradient = gradient + dot_nt(dpacked_ref[:, kind * D : (kind + 1) * D], whole_ref[kind])
    input_ref[...] = unpermuted(gradient, selector_ref)


def vector_kernel(shards, *refs):
    base_ref, first_ref, second_ref, hidden_ref, columns_ref, selector_ref, out_ref = refs
    base = base_ref[0]
    rows = jnp.concatenate(
        [
            first_ref[0:1, :],
            second_ref[0:1, :],
            first_ref[2:3, :],
            second_ref[2:3, :],
            first_ref[1:2, :],
            second_ref[1:2, :],
            jnp.zeros((2, D), jnp.float32),
        ],
        0,
    )
    natural = jnp.zeros((8, D), jnp.float32)
    for _ in range(3):
        term = rows.astype(jnp.bfloat16)
        rows = rows - term.astype(jnp.float32)
        natural = natural + dot_nt(term, selector_ref[...])
    hidden = FF // D
    out_ref[...] = jnp.zeros(out_ref.shape, jnp.float32)
    for at, row in ((0, 0), (1, 1), (4, 2), (5 + hidden, 3), (6 + hidden, 4), (7 + hidden, 5)):
        out_ref[at : at + 1, :] = natural[row : row + 1, :]
    width = D // shards
    for j in range(shards):
        out_ref[5 + j : 6 + j, :] = hidden_ref[pl.ds(j ^ base, 1), :]
        for at, kind in ((2, 0), (3, 2)):
            parts = [
                jnp.where(
                    (j ^ base) == k,
                    columns_ref[0:1, kind * D + k * width : kind * D + (k + 1) * width],
                    0.0,
                )
                for k in range(shards)
            ]
            out_ref[at : at + 1, j * width : (j + 1) * width] = sum(parts)


def adam_kernel(*refs):
    grad_ref, master_ref, left_ref, right_ref, first_ref, second_ref = refs[:6]
    master_out, first_out, second_out = refs[6:]
    bias_first = 1.0 - DECAY_FIRST**ADAM_STEP
    bias_second = 1.0 - DECAY_SECOND**ADAM_STEP
    count = grad_ref.shape[0]
    lefts = [two_terms(left_ref[k]) for k in range(count)]
    rights = [two_terms(right_ref[k]) for k in range(count)]
    turned = []
    for k in range(count):
        top, rest = two_terms(grad_ref[k].astype(jnp.float32))
        turned.append(
            product(top, rights[k][0]) + product(top, rights[k][1]) + product(rest, rights[k][0])
        )
    directions = []
    for k in range(count):
        top, rest = two_terms(turned[k])
        rotated = (
            transposed_times(lefts[k][0], top)
            + transposed_times(lefts[k][0], rest)
            + transposed_times(lefts[k][1], top)
        )
        first = DECAY_FIRST * first_ref[k] + (1.0 - DECAY_FIRST) * rotated
        second = DECAY_SECOND * second_ref[k] + (1.0 - DECAY_SECOND) * rotated * rotated
        first_out[k] = first
        second_out[k] = second
        directions.append(first / bias_first / (jnp.sqrt(second / bias_second) + ADAM_EPS))
    backs = []
    for k in range(count):
        top, rest = two_terms(directions[k])
        backs.append(
            product(lefts[k][0], top) + product(lefts[k][0], rest) + product(lefts[k][1], top)
        )
    for k in range(count):
        top, rest = two_terms(backs[k])
        update = (
            times_transposed(top, rights[k][0])
            + times_transposed(rest, rights[k][0])
            + times_transposed(top, rights[k][1])
        )
        master_out[k] = master_ref[k] - MATRIX_RATE * update


def natural_kernel(shards, *refs):
    out_ref, dz1_ref, dpacked_ref, selector_ref, whole_ref, layer_ref, input_ref = refs
    weights = [whole_ref.at[j] for j in range(shards)]
    head_width = D // shards
    gradient = dz1_ref[...]
    for j in range(shards):
        own = [
            dpacked_ref[:, kind * D + j * head_width : kind * D + (j + 1) * head_width]
            for kind in range(3)
        ]
        gradient = gradient + dot_nt(jnp.concatenate(own, 1), weights[j][:, : 3 * head_width])
    for source, ref in ((out_ref[...], layer_ref), (gradient, input_ref)):
        top = source.astype(jnp.bfloat16)
        rest = (source - top.astype(jnp.float32)).astype(jnp.bfloat16)
        ref[...] = dot_nt(top, selector_ref[...]) + dot_nt(rest, selector_ref[...])


def together(*values):
    return lax.optimization_barrier(values)


def local(
    tokens,
    segments,
    out_grad,
    owner,
    master,
    left_basis,
    right_basis,
    first_moment,
    second_moment,
    vectors,
    vector_first,
    vector_second,
):
    shards = lax.axis_size("tensor")
    dp_size = lax.axis_size("dp")
    direct = dp_size == PARTS and shards == 4
    tensor_rank = lax.axis_index("tensor")
    dp_rank = lax.axis_index("dp")
    local_heads = HEADS // shards
    head_width = local_heads * HEAD_DIM
    up_width = FF // shards
    width_qkv = 3 * head_width
    block_size = master.shape[-1]
    slots = master.shape[1]
    row_count = tokens.shape[0]
    length = segments.shape[1]
    pack_count = row_count // length
    own_segments = lax.dynamic_slice_in_dim(segments, tensor_rank * pack_count, pack_count, 0)
    qkv_tiles, out_tiles, up_tiles = tile_counts(shards, block_size)
    tile_total = owner.shape[0]

    group_base = tensor_rank if direct else 0
    order = feature_order(dp_rank if direct else 0)
    selector = (lax.iota(jnp.int32, D)[:, None] == order[None, :]).astype(jnp.bfloat16)

    steps = row_count // ROWS
    f32, bf16 = jnp.float32, jnp.bfloat16
    rows_spec = lambda width: pl.BlockSpec((ROWS, width), lambda i: (i, 0))
    full = lambda array: (array, pl.BlockSpec(memory_space=pltpu.VMEM))
    raw = lambda array: (array, pl.BlockSpec(memory_space=pl.ANY))
    by_rows = lambda array: (array, row_block(array))
    far_rows = lambda array: (array, row_block(array), "far")
    group_order = lax.iota(jnp.int32, shards) ^ group_base
    below = vectors[: 5 * D].reshape(5, D)
    above = vectors[5 * D + FF :].reshape(3, D)
    d_rows = jnp.stack(
        [below[4], below[0], above[1], above[0], below[1], above[2], below[0], below[0]]
    )
    bias_q = below[2].reshape(shards, head_width)[group_order]
    bias_v = below[3].reshape(shards, head_width)[group_order]
    bias_up = vectors[5 * D : 5 * D + FF].reshape(shards, up_width)[group_order]
    rows_in, grad_out, d_rows = call_rows(
        enter_kernel,
        steps,
        [far_rows(tokens), far_rows(out_grad), full(d_rows), full(selector)],
        [
            ((row_count, D), bf16, rows_spec(D), "far"),
            ((row_count, D), f32, rows_spec(D), "far"),
            ((8, D), f32, pl.BlockSpec(memory_space=pltpu.VMEM)),
        ],
        6 * row_count * D * D,
    )

    def flipped(index):
        from_out = (index >= qkv_tiles) & (index < qkv_tiles + out_tiles)
        return (from_out | (index >= qkv_tiles + out_tiles + up_tiles))[:, None, None]

    own_tiles = lax.dynamic_slice_in_dim(owner, dp_rank * slots, slots, 0)
    own_flip = flipped(own_tiles)
    sent = master[0].astype(jnp.bfloat16)
    sent = jnp.where(own_flip, jnp.swapaxes(sent, 1, 2), sent)
    placing = (lax.iota(jnp.int32, tile_total)[:, None] == owner[None, :]).astype(jnp.bfloat16)
    if direct:
        parts = sent.reshape(slots, PARTS, SUB * block_size).swapaxes(0, 1)
        parts = lax.all_to_all(parts, "dp", 0, 0, tiled=True).reshape(tile_total, -1)
        tiles = product(placing, parts).astype(jnp.bfloat16)
        slab = slabs_from_tiles(tiles.reshape(tile_total, 1, SUB, block_size), shards, block_size)[0]
        half, rows = D // 2, D // PARTS
        first_slab, up_slab, down_slab = (slab[:, k * D : (k + 1) * D] for k in range(3))
        near_left, near_right = down_slab[:, :half], down_slab[:, half:]
        *blocks, near_left, near_right, rows_in, grad_out, d_rows, bias_up = together(
            *from_z(first_slab),
            swap_over(near_left, 0, 2),
            swap_over(near_right, 1, 0),
            rows_in,
            grad_out,
            d_rows,
            bias_up,
        )
        left, right, down_near = merge(
            [first_slab, *blocks, down_slab, near_left, near_right],
            [(half, half, bf16), (half, half, bf16), (2 * rows, D, bf16)],
            [(k, z * rows, 0, rows, half, [(z, 0, k * half)]) for k in range(2) for z in range(4)]
            + [
                (2, 0, 0, rows, D, [(4, 0, 0)]),
                (2, rows, 0, rows, half, [(5, 0, 0)]),
                (2, rows, half, rows, half, [(6, 0, 0)]),
            ],
        )
        left, right, down_near, up_slab = together(left, right, down_near, up_slab)
        up_beside = swap_over(up_slab, 2, 0)
        (up_pair,) = merge(
            [up_slab, up_beside],
            [(2 * rows, D, bf16)],
            [(0, z * rows, 0, rows, D, [(z, 0, 0)]) for z in range(2)],
        )
        left_across, right_beside, up_pair = together(
            swap_over(left, 0, 2), swap_over(right, 1, 0), up_pair
        )
        near, left, right = merge(
            [left, left_across, right, right_beside],
            [(D, D, bf16), (D, half, bf16), (D, half, bf16)],
            [
                (out, q * half, col, half, half, [(2 * k + q, 0, 0)])
                for k in range(2)
                for q in range(2)
                for out, col in ((0, k * half), (1 + k, 0))
            ],
        )
        near, down_near = together(near, down_near)
        down_beside = swap_over(down_near, 2, 0)
        near_there, beside, across, up_far, down_beside = together(
            swap_over(near, 0, 1),
            swap_over(left, 1, 0),
            swap_over(right, 0, 2),
            swap_over(up_pair, 4, 0),
            down_beside,
        )
        up_z, down_pair = merge(
            [up_pair, up_far, down_near, down_beside],
            [(half, D, bf16)] * 2,
            [
                (k, z * 2 * rows, 0, 2 * rows, D, [(2 * k + z, 0, 0)])
                for k in range(2)
                for z in range(2)
            ],
        )
        first = [near, beside, across, near_there] + over_core([beside, across])[2:]
        up = [up_z, swap_over(up_z, 1, 0), swap_over(up_z, 0, 2), swap_over(up_z, 1, 2)]
        down_far = swap_over(down_pair, 4, 0)
        places = (place_first, plane_moves(), edges_moves())
        pieces = [first, None, None]
    else:
        gathered = lax.all_gather(sent, "dp", axis=0, tiled=True).reshape(tile_total, -1)
        tiles = product(placing, gathered).astype(jnp.bfloat16)
        slabs = slabs_from_tiles(
            tiles.reshape(tile_total, PARTS, SUB, block_size), shards, block_size
        )
        whole = jnp.concatenate([slabs[part_of_block(k)] for k in range(PARTS)], 0)
        every = lax.all_gather(whole, "tensor", axis=0)
        pieces = [
            [every[j][:, k * D : (k + 1) * D] for j in range(shards)] for k in range(3)
        ]
        places = (place_kinds, groups_moves(shards), groups_moves(shards))

    packs_step = ROWS // length
    bias_qkv = jnp.stack(
        [bias_q.reshape(D), jnp.zeros((D,), jnp.float32), bias_v.reshape(D)]
    )
    pairs = HEADS // 2
    probs_spec = pl.BlockSpec((packs_step, pairs, length, 2 * length), lambda i: (i, 0, 0, 0))
    sums_spec = lambda width: pl.BlockSpec((8, width), lambda i: (0, 0))
    square = 2 * row_count * D * D

    whole_out = ((shards, D, D), bf16, pl.BlockSpec(memory_space=pltpu.VMEM))
    packed, probs, attended, unit_first, inverse_first, normed_low, whole_first = call_rows(
        functools.partial(attention_kernel, places[0], len(pieces[0]), length),
        steps,
        [
            far_rows(rows_in),
            (own_segments[:, None, :], pl.BlockSpec((packs_step, 1, length), lambda i: (i, 0, 0))),
            (own_segments[:, :, None], pl.BlockSpec((packs_step, length, 1), lambda i: (i, 0, 0))),
            full(bias_qkv),
            full(d_rows),
            *[raw(w) + (("far",) if w.shape == (D, D) else ()) for w in pieces[0]],
        ],
        [
            ((row_count, 3 * D), bf16, rows_spec(3 * D), "far"),
            ((pack_count, pairs, length, 2 * length), bf16, probs_spec, "far"),
            ((row_count, D), bf16, rows_spec(D)),
            ((row_count, D), f32, rows_spec(D), "far"),
            ((row_count, 1), f32, rows_spec(1), "far"),
            ((row_count, D), bf16, rows_spec(D), "far"),
            whole_out,
        ],
        4 * square + 4 * row_count * length * D,
        row_count * length * HEADS,
        [
            pltpu.VMEM((packs_step * pairs, length, 2 * length), f32),
            pltpu.SemaphoreType.DMA((len(pieces[0]),)),
            *[pltpu.VMEM(w.shape, bf16) for w in pieces[0]],
        ],
    )
    if direct:
        *up, up_there, down_far, normed_low = together(
            *up, swap_over(up[0], 0, 1), down_far, normed_low
        )
        down_near, near_left, near_right = merge(
            [down_pair, down_far],
            [(D, D, bf16), (D, half, bf16), (D, half, bf16)],
            [(0, z * half, 0, half, D, [(z, 0, 0)]) for z in range(2)]
            + [
                (1 + k, z * half, 0, half, half, [(z, 0, k * half)])
                for k in range(2)
                for z in range(2)
            ],
        )
        down = [down_near, swap_over(near_left, 1, 0), swap_over(near_right, 0, 2)]
        pieces[1] = up + [up_there] + over_core(up[1:])[3:]
    activated, slope, whole_up = call_rows(
        functools.partial(up_kernel, places[1], shards),
        steps,
        [far_rows(normed_low), full(bias_up), *[raw(w) for w in pieces[1]]],
        [
            ((row_count, FF), bf16, rows_spec(FF)),
            ((row_count, FF), bf16, rows_spec(FF), "far"),
            whole_out,
        ],
        4 * square,
        2 * row_count * FF,
        [pltpu.SemaphoreType.DMA((len(places[1]),))],
    )
    if direct:
        *down, activated = together(*down, activated)
        pieces[2] = over_core(down)
    layer_out, grad_second, second_low, sums_second, whole_down = call_rows(
        functools.partial(down_kernel, places[2], shards),
        steps,
        [
            by_rows(activated),
            far_rows(unit_first),
            far_rows(grad_out),
            full(d_rows),
            *[raw(w) for w in pieces[2]],
        ],
        [
            ((row_count, D), f32, rows_spec(D), "far"),
            ((row_count, D), f32, rows_spec(D)),
            ((row_count, D), bf16, rows_spec(D)),
            ((8, D), f32, sums_spec(D)),
            whole_out,
        ],
        4 * square,
        0,
        [pltpu.SemaphoreType.DMA((len(places[2]),))],
    )
    grad_w_down = weight_halves([second_low], [(activated, up_width, 0)])
    if direct:
        down_parts = reduce_core_plane(grad_w_down)
        second_low, *down_parts = together(second_low, *down_parts)
        down_parts = reduce_plane(*down_parts)
    grad_pre, grad_bias_up = call_rows(
        functools.partial(hidden_back_kernel, shards),
        steps,
        [by_rows(second_low), far_rows(slope), full(whole_down)],
        [((row_count, FF), bf16, rows_spec(FF)), ((8, up_width), f32, sums_spec(up_width))],
        4 * square,
    )
    grad_w_up = weight_halves([normed_low], [(grad_pre, up_width, 0)])
    grad_first, first_low, grad_attended, sums_first = call_rows(
        functools.partial(back_kernel, shards),
        steps,
        [
            by_rows(grad_pre),
            by_rows(grad_second),
            far_rows(unit_first),
            far_rows(inverse_first),
            full(d_rows),
            full(whole_up),
            full(whole_first),
        ],
        [
            ((row_count, D), f32, rows_spec(D), "far"),
            ((row_count, D), bf16, rows_spec(D)),
            ((row_count, D), bf16, rows_spec(D)),
            ((8, D), f32, sums_spec(D)),
        ],
        20 * square,
    )
    if direct:
        up_parts = reduce_core_edges(grad_w_up)
        grad_attended, *parts = together(grad_attended, *up_parts, *down_parts)
        up_terms = edge_terms(*parts[:3])
        down_terms = [parts[3], swap_over(parts[4], 4, 0)]
    grad_packed, column_sums = call_rows(
        functools.partial(attention_back_kernel, length),
        steps,
        [by_rows(grad_attended), by_rows(attended), far_rows(packed), (probs, probs_spec, "far")],
        [
            ((row_count, 3 * D), bf16, rows_spec(3 * D)),
            ((8, 3 * D), f32, sums_spec(3 * D)),
        ],
        8 * square,
        0,
        [pltpu.VMEM((packs_step * pairs, length, 2 * length), bf16)] * 2,
    )
    (vector_rows,) = call_rows(
        functools.partial(vector_kernel, shards),
        1,
        [
            (
                lax.convert_element_type(group_base, jnp.int32).reshape(1),
                pl.BlockSpec(memory_space=pltpu.SMEM),
            ),
            full(sums_first),
            full(sums_second),
            full(grad_bias_up),
            full(column_sums),
            full(selector),
        ],
        [((16, D), f32, pl.BlockSpec(memory_space=pltpu.VMEM))],
        48 * D * D,
    )
    rights = [(grad_packed, head_width, k * shards // 2) for k in range(3)]
    rights.append((attended, head_width, 0))
    grad_w_first = [weight_half(1, [rows_in, first_low], rights)]
    if direct:
        first_low, vector_rows, *others = together(
            first_low, vector_rows, grad_w_first[0], *down_terms, *up_terms
        )
        grad_w_first, down_terms, up_terms = others[:1], others[1:3], others[3:]
        up_near, up_far, first_low = together(*reduce_edges(up_terms), first_low)
        up_terms = [up_near, swap_over(up_far, 4, 0)]
        down_terms = halve_z(*down_terms)
        down_terms = [down_terms[0], swap_over(down_terms[1], 2, 0)]
    else:
        vector_rows = lax.psum(vector_rows, ("dp", "tensor"))
    grad_w_first.append(weight_half(0, [rows_in, first_low], rights))
    if direct:
        first_parts = reduce_core_edges(grad_w_first)
        *first_parts, grad_first = together(*first_parts, grad_first)
        first_terms = edge_terms(*first_parts)
    (input_grad,) = call_rows(
        input_kernel,
        steps,
        [far_rows(grad_first), by_rows(grad_packed), full(selector), full(whole_first)],
        [((row_count, D), f32, rows_spec(D), "far")],
        40 * square,
    )
    if direct:
        *others, input_grad, layer_out = together(
            *first_terms, *down_terms, input_grad, layer_out
        )
        first_terms, down_terms = others[:3], others[3:]
        first_terms = plane_edge_terms(*reduce_edges_plane(first_terms))
        first_terms[0], *up_terms = together(first_terms[0], *up_terms)
        up_terms = halve_z(*up_terms)
        up_terms = [up_terms[0], swap_over(up_terms[1], 2, 0)]
        down_own = add_z(*down_terms)
    (layer_out,) = call_rows(
        layer_kernel,
        steps,
        [far_rows(layer_out), full(selector)],
        [((row_count, D), f32, rows_spec(D), "far")],
        2 * square,
    )
    if direct:
        *first_terms, layer_out = together(*first_terms, layer_out)
        *parts, vector_rows = together(*reduce_plane_edges(first_terms), vector_rows)
        first_terms = z_terms(*parts)
        first_terms[0], *up_terms = together(first_terms[0], *up_terms)
        vector_rows = add_swapped(add_swapped(vector_rows, 0, 1), 0, 2)
        up_terms = plane_edge_terms(*reduce_edges_z(up_terms))
        up_own = reduce_edges_last(up_terms)
        *first_terms, vector_rows = together(*first_terms, vector_rows)
        first_own = reduce_z(first_terms)
        slab_grad = jnp.concatenate([first_own, up_own, down_own], 1).astype(jnp.bfloat16)
        tile_grad = tiles_from_slabs(slab_grad[None], shards, block_size).reshape(tile_total, -1)
        slot_grad = transposed_times(placing, tile_grad).astype(jnp.bfloat16)
        slot_grad, vector_rows = together(slot_grad, vector_rows)
        slot_grad = lax.all_to_all(
            slot_grad.reshape(PARTS, slots, SUB * block_size), "dp", 0, 0, tiled=True
        )
        vector_rows = add_swapped(add_swapped(vector_rows, 1, 0), 2, 0)
        slot_grad, vector_rows = together(slot_grad, vector_rows)
        vector_rows = add_swapped(vector_rows, 4, 0)
        owned_grads = slot_grad.swapaxes(0, 1).reshape(slots, block_size, block_size)
    else:
        every = jnp.stack(
            [
                jnp.concatenate(
                    [half[1 - j % 2][j // 2] for half in (grad_w_first, grad_w_up, grad_w_down)], 1
                )
                for j in range(shards)
            ]
        ).astype(jnp.float32)
        mine = lax.psum_scatter(every, "tensor", scatter_dimension=0, tiled=True)[0]
        blocks = mine.reshape(PARTS, D // PARTS, -1)
        blocks = jnp.stack([blocks[(p % 2) * 4 + p // 2] for p in range(PARTS)])
        tile_grad = tiles_from_slabs(blocks, shards, block_size)
        slot_grad = tile_grad.reshape(tile_total, block_size, block_size)[owner]
        owned_grads = lax.psum_scatter(slot_grad, "dp", scatter_dimension=0, tiled=True)
    owned_grads = jnp.where(own_flip, jnp.swapaxes(owned_grads, 1, 2), owned_grads)

    bias_first = 1.0 - DECAY_FIRST**ADAM_STEP
    bias_second = 1.0 - DECAY_SECOND**ADAM_STEP
    step_slots = max(k for k in (1, 2, 3, 4, 6, 12) if slots % k == 0)
    slots_spec = pl.BlockSpec((step_slots, block_size, block_size), lambda i: (i, 0, 0))
    slot_out = ((slots, block_size, block_size), f32, slots_spec, "far")
    new_master, new_first, new_second = call_rows(
        adam_kernel,
        slots // step_slots,
        [
            (array, slots_spec, "far")
            for array in (
                owned_grads,
                master[0],
                left_basis[0],
                right_basis[0],
                first_moment[0],
                second_moment[0],
            )
        ],
        [slot_out] * 3,
        22 * slots * block_size**3,
        slots * block_size**2,
    )
    vector_grad = vector_rows[: vectors.shape[0] // D].reshape(-1)
    new_vector_first = DECAY_FIRST * vector_first + (1.0 - DECAY_FIRST) * vector_grad
    new_vector_second = (
        DECAY_SECOND * vector_second + (1.0 - DECAY_SECOND) * vector_grad * vector_grad
    )
    new_vectors = vectors - VECTOR_RATE * (new_vector_first / bias_first) / (
        jnp.sqrt(new_vector_second / bias_second) + ADAM_EPS
    )
    return (
        layer_out,
        input_grad,
        new_master[None],
        new_first[None],
        new_second[None],
        new_vectors,
        new_vector_first,
        new_vector_second,
    )


def solution(mesh):
    return jax.shard_map(
        local,
        mesh=mesh,
        in_specs=(
            P(("dp", "tensor"), None),
            P("dp", None),
            P(("dp", "tensor"), None),
            P(),
            P("tensor", "dp", None, None),
            P("tensor", "dp", None, None),
            P("tensor", "dp", None, None),
            P("tensor", "dp", None, None),
            P("tensor", "dp", None, None),
            P(),
            P(),
            P(),
        ),
        out_specs=(
            P(("dp", "tensor"), None),
            P(("dp", "tensor"), None),
            P("tensor", "dp", None, None),
            P("tensor", "dp", None, None),
            P("tensor", "dp", None, None),
            P(),
            P(),
            P(),
        ),
        check_vma=False,
    )
```

```python
import functools
import math

import jax
import jax.numpy as jnp
from jax import lax
from jax.experimental import pallas as pl
from jax.experimental.pallas import tpu as pltpu
from jax.sharding import PartitionSpec as P

HEADS = 12
HEAD_DIM = 64
D = 768
FF = 3072
ADAM_STEP = 3


NORM_EPS = 1e-12
ADAM_EPS = 1e-08
MATRIX_RATE = 0.01
VECTOR_RATE = 0.1
DECAY_FIRST = 0.5
DECAY_SECOND = 0.5
MASKED = -1e30


def product(left_side, right_side):
    return jnp.dot(left_side, right_side, preferred_element_type=jnp.float32)


def times_transposed(left_side, right_side):
    return lax.dot_general(
        left_side, right_side, (((1,), (1,)), ((), ())), preferred_element_type=jnp.float32
    )


def transposed_times(left_side, right_side):
    return lax.dot_general(
        left_side, right_side, (((0,), (0,)), ((), ())), preferred_element_type=jnp.float32
    )


VMEM_LIMIT = 16 * 1024 * 1024

PARTS = 8
SUB = 12


def part_of_block(block):
    return (block % 4) * 2 + block // 4


def feature_order(rank):
    place = lax.iota(jnp.int32, D)
    part = part_of_block(place // (D // PARTS)) ^ rank
    inner = place % (D // PARTS)
    return (inner // SUB) * (PARTS * SUB) + part * SUB + inner % SUB


def tile_counts(shards, block_size):
    rows = D // block_size
    qkv = rows * (3 * D // shards // block_size)
    out = rows * (D // shards // block_size)
    up = rows * (FF // shards // block_size)
    return (qkv, out, up)


def slabs_from_tiles(tiles, shards, block_size):
    cut = tiles.shape[1]
    qkv, out, up = tile_counts(shards, block_size)
    rows = D // block_size

    def by_rows(part):
        cols = part.shape[0] // rows
        part = part.reshape(rows, cols, cut, SUB, block_size)
        return part.transpose(2, 0, 3, 1, 4).reshape(cut, rows * SUB, cols * block_size)

    def by_cols(part):
        cols = part.shape[0] // rows
        part = part.reshape(cols, rows, cut, SUB, block_size)
        return part.transpose(2, 1, 3, 0, 4).reshape(cut, rows * SUB, cols * block_size)

    return jnp.concatenate(
        [
            by_rows(tiles[:qkv]),
            by_cols(tiles[qkv : qkv + out]),
            by_rows(tiles[qkv + out : qkv + out + up]),
            by_cols(tiles[qkv + out + up :]),
        ],
        2,
    )


def tiles_from_slabs(slabs, shards, block_size):
    cut = slabs.shape[0]
    rows = D // block_size
    width_qkv, width_out, width_up = 3 * D // shards, D // shards, FF // shards

    def by_rows(part):
        cols = part.shape[2] // block_size
        part = part.reshape(cut, rows, SUB, cols, block_size)
        return part.transpose(1, 3, 0, 2, 4).reshape(rows * cols, cut, SUB, block_size)

    def by_cols(part):
        cols = part.shape[2] // block_size
        part = part.reshape(cut, rows, SUB, cols, block_size)
        return part.transpose(3, 1, 0, 2, 4).reshape(rows * cols, cut, SUB, block_size)

    first = width_qkv + width_out
    second = first + width_up
    return jnp.concatenate(
        [
            by_rows(slabs[:, :, :width_qkv]),
            by_cols(slabs[:, :, width_qkv:first]),
            by_rows(slabs[:, :, first:second]),
            by_cols(slabs[:, :, second:]),
        ],
        0,
    )


def swap_over(values, over_dp, over_tensor):
    dp, tensor = lax.axis_size("dp"), lax.axis_size("tensor")
    pairs = [
        (a * tensor + b, (a ^ over_dp) * tensor + (b ^ over_tensor))
        for a in range(dp)
        for b in range(tensor)
    ]
    return lax.ppermute(values, ("dp", "tensor"), pairs)


def merge(terms, outs, segments):
    chunk = D // PARTS

    def kernel(*refs):
        for out, row, col, rows, cols, parts in segments:

            def step(k, carry, out=out, row=row, col=col, cols=cols, parts=parts):
                pieces = [
                    refs[term][pl.ds(pl.multiple_of(at + k * chunk, 32), chunk), left : left + cols]
                    for term, at, left in parts
                ]
                if len(pieces) > 1:
                    value = sum(piece.astype(jnp.float32) for piece in pieces)
                else:
                    value = pieces[0]
                to = refs[len(terms) + out]
                to[pl.ds(pl.multiple_of(row + k * chunk, 32), chunk), col : col + cols] = (
                    value.astype(to.dtype)
                )
                return carry

            lax.fori_loop(0, rows // chunk, step, 0)

    spec = pl.BlockSpec(memory_space=pltpu.VMEM)
    size = sum(term.size for term in terms)
    return pl.pallas_call(
        kernel,
        in_specs=[spec] * len(terms),
        out_specs=[spec] * len(outs),
        out_shape=[jax.ShapeDtypeStruct((rows, cols), dtype) for rows, cols, dtype in outs],
        compiler_params=pltpu.CompilerParams(vmem_limit_bytes=VMEM_LIMIT),
        cost_estimate=pl.CostEstimate(flops=size, bytes_accessed=4 * size, transcendentals=0),
    )(*terms)


def from_z(block):
    return [swap_over(block, 2 * k, 0) for k in (1, 2, 3)]


def over_core(blocks):
    return blocks + [swap_over(block, 0, 1) for block in blocks]


def put(out_ref, lead, row, col, ref, at, left, rows, cols):
    chunk = min(rows, D // 2)

    def step(k, carry):
        to = pl.multiple_of(row + k * chunk, 32)
        source = pl.multiple_of(at + k * chunk, 32)
        out_ref[lead, pl.ds(to, chunk), col : col + cols] = ref[
            pl.ds(source, chunk), left : left + cols
        ]
        return carry

    lax.fori_loop(0, rows // chunk, step, 0)


def place_first(refs, out_ref):
    count = len(refs) // 2
    half, width = D // 2, D // 4
    for core in range(2):
        near, beside, across = refs[core * count : (core + 1) * count]
        for y in range(2):
            col = (2 * y + core) * width
            for kind in range(2):
                left = kind * width
                put(out_ref, kind, 0, col, near, y * half, left, half, width)
                put(out_ref, kind, half, col, beside, y * half, left, half, width)
                if y:
                    put(out_ref, 2 + kind, 0, col, across, 0, left, D, width)
                else:
                    put(out_ref, 2 + kind, 0, col, near, 0, half + left, D, width)


def edges_moves():
    rows, half = D // PARTS, D // 2
    moves = []
    for core in range(2):
        near, beside, across = range(3 * core, 3 * core + 3)
        for y in range(2):
            group = 2 * y + core
            for z in range(4):
                for x in range(2):
                    to, by_y, by_x = x * half + z * rows, (2 * z + y) * rows, (2 * z + x) * rows
                    moves.append((group, to, 0, beside if x else near, by_y, 0, rows, half))
                    source = (across, by_x, 0) if y else (near, by_x, half)
                    moves.append((group, to, half, *source, rows, half))
    return moves


def plane_moves():
    half = D // 2
    return [
        (2 * y + core, x * half, 0, 4 * core + 2 * y + x, 0, 0, half, D)
        for core in range(2)
        for y in range(2)
        for x in range(2)
    ]


def groups_moves(count):
    return [(group, 0, 0, group, 0, 0, D, D) for group in range(count)]


def move_all(moves, refs, out_ref, sems):
    copies = [
        pltpu.make_async_copy(
            refs[ref].at[pl.ds(at, rows), pl.ds(left, cols)],
            out_ref.at[lead, pl.ds(row, rows), pl.ds(col, cols)],
            sems.at[k],
        )
        for k, (lead, row, col, ref, at, left, rows, cols) in enumerate(moves)
    ]
    for copy in copies:
        copy.start()
    for copy in copies:
        copy.wait()


def place_kinds(refs, out_ref):
    width = D // len(refs)
    for group, ref in enumerate(refs):
        for kind in range(4):
            put(out_ref, kind, 0, group * width, ref, 0, kind * width, D, width)


def core_terms(halves):
    odd, even = halves
    return [even.reshape(2 * D, D), swap_over(odd, 0, 1).reshape(2 * D, D)]


def summed(count, row, col):
    return [(term, row, col) for term in range(count)]


def reduce_core_plane(halves):
    half = D // 2
    return merge(
        core_terms(halves),
        [(half, D, jnp.bfloat16)] * 4,
        [(k, 0, 0, half, D, summed(2, k * half, 0)) for k in range(4)],
    )


def reduce_plane(near, beside, across, opposite):
    pair = D // 4
    terms = [near, swap_over(beside, 1, 0), swap_over(across, 0, 2), swap_over(opposite, 1, 2)]
    return merge(
        terms,
        [(pair, D, jnp.bfloat16)] * 2,
        [(k, 0, 0, pair, D, summed(4, k * pair, 0)) for k in range(2)],
    )


def halve_z(near, received):
    rows = near.shape[0] // 2
    return merge(
        [near, received],
        [(rows, D, jnp.bfloat16)] * 2,
        [(k, 0, 0, rows, D, summed(2, k * rows, 0)) for k in range(2)],
    )


def add_z(near, received):
    rows = near.shape[0]
    return merge(
        [near, received], [(rows, D, jnp.float32)], [(0, 0, 0, rows, D, summed(2, 0, 0))]
    )[0]


def z_terms(own, *sent):
    return [own] + [swap_over(block, 2 * (k + 1), 0) for k, block in enumerate(sent)]


def reduce_z(terms):
    rows = D // PARTS
    return merge(terms, [(rows, D, jnp.float32)], [(0, 0, 0, rows, D, summed(4, 0, 0))])[0]


def reduce_core_edges(halves):
    half = D // 2
    return merge(
        core_terms(halves),
        [(D, D, jnp.bfloat16), (D, half, jnp.bfloat16), (D, half, jnp.bfloat16)],
        [
            (0, 0, 0, half, half, summed(2, 0, 0)),
            (0, half, 0, half, half, summed(2, D, 0)),
            (0, 0, half, D, half, summed(2, 0, half)),
            (1, 0, 0, half, half, summed(2, half, 0)),
            (1, half, 0, half, half, summed(2, D + half, 0)),
            (2, 0, 0, D, half, summed(2, D, half)),
        ],
    )


def edge_terms(near, left, right):
    return [near, swap_over(left, 1, 0), swap_over(right, 0, 2)]


def edge_sums(row):
    half = D // 2
    return ((0, [(0, row, 0), (1, row, 0)]), (half, [(0, row, half), (2, row, 0)]))


def plane_edge_terms(near, left, right):
    return [near, swap_over(left, 0, 2), swap_over(right, 1, 0)]


def reduce_edges_plane(terms):
    half = D // 2
    kept = [(0, 0, col, half, half, parts) for col, parts in edge_sums(0)]
    sent = [
        (1 + k, 0, 0, half, half, parts) for k, (_, parts) in enumerate(edge_sums(half))
    ]
    return merge(
        terms,
        [(half, D, jnp.bfloat16), (half, half, jnp.bfloat16), (half, half, jnp.bfloat16)],
        kept + sent,
    )


def reduce_plane_edges(terms):
    rows, half = D // PARTS, D // 2
    return merge(
        terms,
        [(rows, D, jnp.bfloat16)] * 4,
        [
            (k, 0, col, rows, half, parts)
            for k in range(4)
            for col, parts in edge_sums(k * rows)
        ],
    )


def reduce_edges(terms):
    rows, half = D // PARTS, D // 2
    return merge(
        terms,
        [(half, D, jnp.bfloat16)] * 2,
        [
            (k // 2, (2 * (k % 2) + q) * rows, col, rows, half, parts)
            for k in range(4)
            for q in range(2)
            for col, parts in edge_sums(q * half + k * rows)
        ],
    )


def reduce_edges_z(terms):
    rows, half = D // PARTS, D // 2
    return merge(
        terms,
        [(rows, D, jnp.bfloat16), (rows, half, jnp.bfloat16), (rows, half, jnp.bfloat16)],
        [
            (0, 0, 0, rows, D, summed(2, 0, 0)),
            (1, 0, 0, rows, half, summed(2, rows, 0)),
            (2, 0, 0, rows, half, summed(2, rows, half)),
        ],
    )


def reduce_edges_last(terms):
    rows, half = D // PARTS, D // 2
    return merge(
        terms,
        [(rows, D, jnp.float32)],
        [(0, 0, col, rows, half, parts) for col, parts in edge_sums(0)],
    )[0]


def add_swapped(values, over_dp, over_tensor):
    return values + swap_over(values, over_dp, over_tensor)


ROWS = 256


def dot_nt(left_side, right_side):
    return lax.dot_general(
        left_side, right_side, (((1,), (1,)), ((), ())), preferred_element_type=jnp.float32
    )


def row_block(array):
    return pl.BlockSpec((ROWS, array.shape[1]), lambda i: (i, 0))


def call_rows(kernel, steps, inputs, outputs, flops, transcendentals=0, scratch=()):
    arrays = [
        pltpu.with_memory_space_constraint(array, pltpu.HBM) if far else array
        for array, _, *far in inputs
    ]
    shapes = [jax.ShapeDtypeStruct(shape, dtype) for shape, dtype, *_ in outputs]
    moved = sum(a.size * a.dtype.itemsize for a in arrays + shapes)
    shapes = [
        pltpu.HBM(shape.shape, shape.dtype) if len(output) > 3 else shape
        for shape, output in zip(shapes, outputs)
    ]
    return pl.pallas_call(
        kernel,
        grid=(steps,),
        in_specs=[spec for _, spec, *_ in inputs],
        out_specs=[output[2] for output in outputs],
        out_shape=shapes,
        scratch_shapes=scratch,
        compiler_params=pltpu.CompilerParams(vmem_limit_bytes=VMEM_LIMIT),
        cost_estimate=pl.CostEstimate(
            flops=int(1.0 * flops), bytes_accessed=moved, transcendentals=transcendentals
        ),
    )(*arrays)


def norm_rows(summed):
    centred = summed - jnp.mean(summed, -1, keepdims=True)
    inverse = lax.rsqrt(jnp.mean(centred * centred, -1, keepdims=True) + NORM_EPS)
    return centred * inverse, inverse


def norm_pull(gradient, unit_rows, inverse, gain_row):
    scaled = gradient * gain_row
    return inverse * (
        scaled
        - jnp.mean(scaled, -1, keepdims=True)
        - unit_rows * jnp.mean(scaled * unit_rows, -1, keepdims=True)
    )


def add_rows(ref, rows):
    sums = [jnp.sum(row, 0, keepdims=True) for row in rows]
    start = pl.program_id(0) == 0
    for place, total in enumerate(sums):
        kept = jnp.where(start, 0.0, ref[place : place + 1, :])
        ref[place : place + 1, :] = kept + total


def settle(moves, refs, whole_ref, sems):
    @pl.when(pl.program_id(0) == 0)
    def _():
        move_all(moves, refs, whole_ref, sems)

    return [whole_ref.at[j] for j in range(whole_ref.shape[0])]


def pair_masks(length):
    wide = 2 * HEAD_DIM
    lower = lax.broadcasted_iota(jnp.int32, (length, wide), 1) < HEAD_DIM
    top = lax.broadcasted_iota(jnp.int32, (2 * length, wide), 0) < length
    left = lax.broadcasted_iota(jnp.int32, (2 * length, wide), 1) < HEAD_DIM
    return lower, top == left


def stacked(pair, own):
    return jnp.where(own, jnp.concatenate([pair, pair], 0), jnp.zeros((), pair.dtype))


def attention_kernel(place, total_count, length, *refs):
    rows_ref, across_ref, down_ref, bias_ref, vec_ref = refs[:5]
    outs = refs[5 + total_count : 12 + total_count]
    packed_ref, probs_ref, attended_ref, unit_ref, inverse_ref, low_ref, whole_ref = outs
    scores_ref, sems, *raw = refs[12 + total_count :]

    @pl.when(pl.program_id(0) == 0)
    def _():
        copies = [
            pltpu.make_async_copy(source, to, sems.at[k])
            for k, (source, to) in enumerate(zip(refs[5 : 5 + total_count], raw))
        ]
        for copy in copies:
            copy.start()
        for copy in copies:
            copy.wait()
        place(raw, whole_ref)

    weights = [whole_ref.at[kind] for kind in range(4)]
    wide = 2 * HEAD_DIM
    pairs = HEADS // 2
    rows = rows_ref[...]
    for kind in range(3):
        part = product(rows, weights[kind][...]) + bias_ref[kind : kind + 1, :]
        part = part.astype(jnp.bfloat16)
        if kind == 0:
            part = part * jnp.bfloat16(HEAD_DIM ** (-0.5))
        packed_ref[:, kind * D : (kind + 1) * D] = part
    _, own = pair_masks(length)
    ones = own.astype(jnp.bfloat16)
    steps = [(p, i) for p in range(ROWS // length) for i in range(pairs)]

    def pair_of(p, i, kind):
        span = slice(p * length, (p + 1) * length)
        return packed_ref[span, kind * D + i * wide : kind * D + (i + 1) * wide]

    for at, (p, i) in enumerate(steps):
        scores_ref[at] = dot_nt(pair_of(p, i, 0), stacked(pair_of(p, i, 1), own))
    for at, (p, i) in enumerate(steps):
        allowed = down_ref[p] == across_ref[p]
        for half in range(2):
            lanes = slice(half * length, (half + 1) * length)
            scores = jnp.where(allowed, scores_ref[at, :, lanes], MASKED)
            probs_ref[p, i, :, lanes] = jnp.exp(
                scores - jnp.max(scores, -1, keepdims=True)
            ).astype(jnp.bfloat16)
    for p, i in steps:
        mixed = product(
            probs_ref[p, i], jnp.concatenate([stacked(pair_of(p, i, 2), own), ones], 1)
        )
        attended_ref[p * length : (p + 1) * length, i * wide : (i + 1) * wide] = (
            mixed[:, :wide] / mixed[:, wide:]
        ).astype(jnp.bfloat16)
    summed = rows.astype(jnp.float32) + vec_ref[0:1, :]
    summed = summed + dot_nt(attended_ref[...], weights[3][...])
    unit, inverse = norm_rows(summed)
    unit_ref[...] = unit
    inverse_ref[...] = inverse
    low_ref[...] = (unit * vec_ref[1:2, :] + vec_ref[2:3, :]).astype(jnp.bfloat16)


def gelu_parts(values):
    size = jnp.abs(values)
    decay = jnp.exp2(values * values * (-0.5 / math.log(2.0)))
    t = 1.0 / (1.0 + size * (0.3275911 * 0.5**0.5))
    poly = t * (
        0.127414796
        + t * (-0.142248368 + t * (0.7107068705 + t * (-0.7265760135 + t * 0.5307027145)))
    )
    result = jnp.maximum(values, 0.0) - size * (poly * decay)
    rest = decay * (poly - size * (0.5 / math.pi) ** 0.5)
    return result, jnp.where(values > 0, 1.0 - rest, rest)


def up_kernel(place, shards, *refs):
    low_ref, bias_ref = refs[:2]
    act_ref, slope_ref, whole_ref, sems = refs[-4:]
    weights = settle(place, refs[2:-4], whole_ref, sems)
    width = weights[0].shape[1]
    chunk = 256
    low = low_ref[...]
    for j in range(shards):
        for c in range(0, width, chunk):
            pre = product(low, weights[j][:, c : c + chunk]) + bias_ref[j : j + 1, c : c + chunk]
            result, slope = gelu_parts(pre)
            at = j * width + c
            act_ref[:, at : at + chunk] = result.astype(jnp.bfloat16)
            slope_ref[:, at : at + chunk] = slope.astype(jnp.bfloat16)


def down_kernel(place, shards, *refs):
    act_ref, unit_ref, grad_ref, vec_ref = refs[:4]
    out_ref, dz_ref, low_ref, sums_ref, whole_ref, sems = refs[-6:]
    weights = settle(place, refs[4:-6], whole_ref, sems)
    width = weights[0].shape[1]
    summed = unit_ref[...] * vec_ref[1:2, :] + vec_ref[2:3, :] + vec_ref[3:4, :]
    for j in range(shards):
        summed = summed + dot_nt(act_ref[:, j * width : (j + 1) * width], weights[j][...])
    unit, inverse = norm_rows(summed)
    gain = vec_ref[4:5, :]
    out_ref[...] = unit * gain + vec_ref[5:6, :]
    gradient = grad_ref[...]
    dz = norm_pull(gradient, unit, inverse, gain)
    dz_ref[...] = dz
    low_ref[...] = dz.astype(jnp.bfloat16)
    add_rows(sums_ref, (gradient * unit, gradient, dz))


def hidden_back_kernel(shards, *refs):
    low_ref, slope_ref, whole_ref, dpre_ref, bias_sums_ref = refs
    width = whole_ref.shape[2]
    low = low_ref[...]
    for j in range(shards):
        span = slice(j * width, (j + 1) * width)
        dpre = product(low, whole_ref[j]) * slope_ref[:, span].astype(jnp.float32)
        dpre = dpre.astype(jnp.bfloat16)
        dpre_ref[:, span] = dpre
        total = jnp.sum(dpre.astype(jnp.float32), 0, keepdims=True)
        kept = jnp.where(pl.program_id(0) == 0, 0.0, bias_sums_ref[j : j + 1, :])
        bias_sums_ref[j : j + 1, :] = kept + total


def back_kernel(shards, *refs):
    dpre_ref, dz_ref, unit_ref, inverse_ref, vec_ref, up_ref, first_ref = refs[:7]
    dz1_ref, low1_ref, datt_ref, sums_ref = refs[7:]
    width = up_ref.shape[2]
    gradient = dz_ref[...]
    for j in range(shards):
        gradient = gradient + dot_nt(dpre_ref[:, j * width : (j + 1) * width], up_ref[j])
    unit = unit_ref[...]
    dz1 = norm_pull(gradient, unit, inverse_ref[...], vec_ref[1:2, :])
    dz1_ref[...] = dz1
    low1 = dz1.astype(jnp.bfloat16)
    low1_ref[...] = low1
    add_rows(sums_ref, (gradient * unit, gradient, dz1))
    datt_ref[...] = product(low1, first_ref[3]).astype(jnp.bfloat16)


def attention_back_kernel(length, *refs):
    datt_ref, attended_ref, packed_ref, probs_ref, dpacked_ref, sums_ref, up_ref, grad_ref = refs
    wide = 2 * HEAD_DIM
    lower, own = pair_masks(length)
    ones = own.astype(jnp.bfloat16)
    steps = [(p, i) for p in range(ROWS // length) for i in range(HEADS // 2)]

    def pair_of(p, i, kind):
        span = slice(p * length, (p + 1) * length)
        return packed_ref[span, kind * D + i * wide : kind * D + (i + 1) * wide]

    def keep(p, i, kind, grad):
        span = slice(p * length, (p + 1) * length)
        dpacked_ref[span, kind * D + i * wide : kind * D + (i + 1) * wide] = grad.astype(
            jnp.bfloat16
        )

    for place, (p, i) in enumerate(steps):
        span = slice(p * length, (p + 1) * length)
        lanes = slice(i * wide, (i + 1) * wide)
        upstream = datt_ref[span, lanes].astype(jnp.float32) / product(probs_ref[p, i], ones)
        up_ref[place, :, :wide] = upstream.astype(jnp.bfloat16)
        up_ref[place, :, wide:] = (upstream * attended_ref[span, lanes].astype(jnp.float32)).astype(
            jnp.bfloat16
        )
    for place, (p, i) in enumerate(steps):
        centred = dot_nt(
            up_ref[place], jnp.concatenate([stacked(pair_of(p, i, 2), own), -ones], 1)
        )
        grad_ref[place] = (probs_ref[p, i].astype(jnp.float32) * centred).astype(jnp.bfloat16)
    for place, (p, i) in enumerate(steps):
        grad_scores = grad_ref[place]
        keep(
            p, i, 0,
            product(grad_scores, stacked(pair_of(p, i, 1), own)) * HEAD_DIM ** (-0.5),
        )
        both = transposed_times(grad_scores, pair_of(p, i, 0))
        keep(p, i, 1, jnp.where(lower, both[:length], both[length:]))
        both = transposed_times(probs_ref[p, i], up_ref[place, :, :wide])
        keep(p, i, 2, jnp.where(lower, both[:length], both[length:]))
    total = jnp.sum(dpacked_ref[...].astype(jnp.float32), 0, keepdims=True)
    kept = jnp.where(pl.program_id(0) == 0, 0.0, sums_ref[0:1, :])
    sums_ref[0:1, :] = kept + total


def weight_kernel(odd, count, *refs):
    lefts = refs[: 2 if count > 1 else 1]
    rights, out_ref = refs[len(lefts) : -1], refs[-1]
    if count == 1:
        out_ref[0] = transposed_times(lefts[0][...], rights[0][...]).astype(jnp.bfloat16)
    else:
        half = rights[0].shape[1] // 2
        span = slice(half, 2 * half) if odd else slice(0, half)
        values = jnp.concatenate([right[:, span] for right in rights[:-1]], 1)
        width = values.shape[1]
        out_ref[0, :, :width] = transposed_times(lefts[0][...], values).astype(jnp.bfloat16)
        out_ref[0, :, width:] = transposed_times(lefts[1][...], rights[-1][:, span]).astype(
            jnp.bfloat16
        )


def weight_half(odd, lefts, rights):
    count = len(rights)
    single = count == 1
    specs = []
    for array, width, before in rights:
        if single:
            specs.append(pl.BlockSpec((array.shape[0], width), lambda i: (0, 2 * i + odd)))
        else:
            specs.append(pl.BlockSpec((array.shape[0], 2 * width), lambda i, b=before: (0, b + i)))
    arrays = [*lefts, *[array for array, _, _ in rights]]
    tokens = lefts[0].shape[0]
    (half,) = pl.pallas_call(
        functools.partial(weight_kernel, odd, count),
        grid=(2,),
        in_specs=[pl.BlockSpec(memory_space=pltpu.VMEM) for _ in lefts] + specs,
        out_specs=[pl.BlockSpec((1, D, D), lambda i: (i, 0, 0))],
        out_shape=[jax.ShapeDtypeStruct((2, D, D), jnp.bfloat16)],
        compiler_params=pltpu.CompilerParams(vmem_limit_bytes=VMEM_LIMIT),
        cost_estimate=pl.CostEstimate(
            flops=4 * tokens * D * D,
            bytes_accessed=sum(2 * array.size for array in arrays),
            transcendentals=0,
        ),
    )(*arrays)
    return half


def weight_halves(lefts, rights):
    return [weight_half(odd, lefts, rights) for odd in (1, 0)]


def two_terms(values):
    top = values.astype(jnp.bfloat16)
    return top, (values - top.astype(jnp.float32)).astype(jnp.bfloat16)


def adam_kernel(*refs):
    grad_ref, master_ref, left_ref, right_ref, first_ref, second_ref = refs[:6]
    master_out, first_out, second_out = refs[6:]
    bias_first = 1.0 - DECAY_FIRST**ADAM_STEP
    bias_second = 1.0 - DECAY_SECOND**ADAM_STEP
    count = grad_ref.shape[0]
    lefts = [two_terms(left_ref[k]) for k in range(count)]
    rights = [two_terms(right_ref[k]) for k in range(count)]
    turned = []
    for k in range(count):
        grad = product(grad_ref[k].astype(jnp.bfloat16), rights[k][0])
        grad = grad + product(grad_ref[k].astype(jnp.bfloat16), rights[k][1])
        if grad_ref.dtype != jnp.bfloat16:
            grad = grad + product(two_terms(grad_ref[k])[1], rights[k][0])
        turned.append(grad)
    directions = []
    for k in range(count):
        top, rest = two_terms(turned[k])
        rotated = (
            transposed_times(lefts[k][0], top)
            + transposed_times(lefts[k][0], rest)
            + transposed_times(lefts[k][1], top)
        )
        first = DECAY_FIRST * first_ref[k] + (1.0 - DECAY_FIRST) * rotated
        second = DECAY_SECOND * second_ref[k] + (1.0 - DECAY_SECOND) * rotated * rotated
        first_out[k] = first
        second_out[k] = second
        directions.append(first / bias_first / (jnp.sqrt(second / bias_second) + ADAM_EPS))
    backs = [
        product(lefts[k][0], directions[k].astype(jnp.bfloat16)).astype(jnp.bfloat16)
        for k in range(count)
    ]
    for k in range(count):
        update = times_transposed(backs[k], rights[k][0])
        master_out[k] = master_ref[k] - MATRIX_RATE * update


def two_terms(values):
    top = values.astype(jnp.bfloat16)
    return top, (values - top.astype(jnp.float32)).astype(jnp.bfloat16)


def unpermuted(values, selector_ref):
    top, rest = two_terms(values)
    return dot_nt(top, selector_ref[...]) + dot_nt(rest, selector_ref[...])


def enter_kernel(tokens_ref, grad_ref, vectors_ref, selector_ref, rows_ref, out_ref, d_rows_ref):
    selector = selector_ref[...]
    rows_ref[...] = product(tokens_ref[...], selector).astype(jnp.bfloat16)
    top, rest = two_terms(grad_ref[...])
    out_ref[...] = product(top, selector) + product(rest, selector)

    @pl.when(pl.program_id(0) == 0)
    def _():
        rows = vectors_ref[...]
        permuted = jnp.zeros(rows.shape, jnp.float32)
        for _ in range(3):
            term = rows.astype(jnp.bfloat16)
            rows = rows - term.astype(jnp.float32)
            permuted = permuted + product(term, selector)
        d_rows_ref[...] = permuted


def layer_kernel(out_ref, selector_ref, layer_ref):
    layer_ref[...] = unpermuted(out_ref[...], selector_ref)


def input_kernel(dz1_ref, dpacked_ref, selector_ref, whole_ref, input_ref):
    gradient = dz1_ref[...]
    for kind in range(3):
        gradient = gradient + dot_nt(dpacked_ref[:, kind * D : (kind + 1) * D], whole_ref[kind])
    input_ref[...] = unpermuted(gradient, selector_ref)


def vector_kernel(shards, *refs):
    base_ref, first_ref, second_ref, hidden_ref, columns_ref, selector_ref, out_ref = refs
    base = base_ref[0]
    rows = jnp.concatenate(
        [
            first_ref[0:1, :],
            second_ref[0:1, :],
            first_ref[2:3, :],
            second_ref[2:3, :],
            first_ref[1:2, :],
            second_ref[1:2, :],
            jnp.zeros((2, D), jnp.float32),
        ],
        0,
    )
    natural = jnp.zeros((8, D), jnp.float32)
    for _ in range(3):
        term = rows.astype(jnp.bfloat16)
        rows = rows - term.astype(jnp.float32)
        natural = natural + dot_nt(term, selector_ref[...])
    hidden = FF // D
    out_ref[...] = jnp.zeros(out_ref.shape, jnp.float32)
    for at, row in ((0, 0), (1, 1), (4, 2), (5 + hidden, 3), (6 + hidden, 4), (7 + hidden, 5)):
        out_ref[at : at + 1, :] = natural[row : row + 1, :]
    width = D // shards
    for j in range(shards):
        out_ref[5 + j : 6 + j, :] = hidden_ref[pl.ds(j ^ base, 1), :]
        for at, kind in ((2, 0), (3, 2)):
            parts = [
                jnp.where(
                    (j ^ base) == k,
                    columns_ref[0:1, kind * D + k * width : kind * D + (k + 1) * width],
                    0.0,
                )
                for k in range(shards)
            ]
            out_ref[at : at + 1, j * width : (j + 1) * width] = sum(parts)


def adam_kernel(*refs):
    grad_ref, master_ref, left_ref, right_ref, first_ref, second_ref = refs[:6]
    master_out, first_out, second_out = refs[6:]
    bias_first = 1.0 - DECAY_FIRST**ADAM_STEP
    bias_second = 1.0 - DECAY_SECOND**ADAM_STEP
    count = grad_ref.shape[0]
    lefts = [two_terms(left_ref[k]) for k in range(count)]
    rights = [two_terms(right_ref[k]) for k in range(count)]
    turned = []
    for k in range(count):
        top, rest = two_terms(grad_ref[k].astype(jnp.float32))
        turned.append(
            product(top, rights[k][0]) + product(top, rights[k][1]) + product(rest, rights[k][0])
        )
    directions = []
    for k in range(count):
        top, rest = two_terms(turned[k])
        rotated = (
            transposed_times(lefts[k][0], top)
            + transposed_times(lefts[k][0], rest)
            + transposed_times(lefts[k][1], top)
        )
        first = DECAY_FIRST * first_ref[k] + (1.0 - DECAY_FIRST) * rotated
        second = DECAY_SECOND * second_ref[k] + (1.0 - DECAY_SECOND) * rotated * rotated
        first_out[k] = first
        second_out[k] = second
        directions.append(first / bias_first / (jnp.sqrt(second / bias_second) + ADAM_EPS))
    backs = []
    for k in range(count):
        top, rest = two_terms(directions[k])
        backs.append(
            product(lefts[k][0], top) + product(lefts[k][0], rest) + product(lefts[k][1], top)
        )
    for k in range(count):
        top, rest = two_terms(backs[k])
        update = (
            times_transposed(top, rights[k][0])
            + times_transposed(rest, rights[k][0])
            + times_transposed(top, rights[k][1])
        )
        master_out[k] = master_ref[k] - MATRIX_RATE * update


def natural_kernel(shards, *refs):
    out_ref, dz1_ref, dpacked_ref, selector_ref, whole_ref, layer_ref, input_ref = refs
    weights = [whole_ref.at[j] for j in range(shards)]
    head_width = D // shards
    gradient = dz1_ref[...]
    for j in range(shards):
        own = [
            dpacked_ref[:, kind * D + j * head_width : kind * D + (j + 1) * head_width]
            for kind in range(3)
        ]
        gradient = gradient + dot_nt(jnp.concatenate(own, 1), weights[j][:, : 3 * head_width])
    for source, ref in ((out_ref[...], layer_ref), (gradient, input_ref)):
        top = source.astype(jnp.bfloat16)
        rest = (source - top.astype(jnp.float32)).astype(jnp.bfloat16)
        ref[...] = dot_nt(top, selector_ref[...]) + dot_nt(rest, selector_ref[...])


def together(*values):
    return lax.optimization_barrier(values)


def local(
    tokens,
    segments,
    out_grad,
    owner,
    master,
    left_basis,
    right_basis,
    first_moment,
    second_moment,
    vectors,
    vector_first,
    vector_second,
):
    shards = lax.axis_size("tensor")
    dp_size = lax.axis_size("dp")
    direct = dp_size == PARTS and shards == 4
    tensor_rank = lax.axis_index("tensor")
    dp_rank = lax.axis_index("dp")
    local_heads = HEADS // shards
    head_width = local_heads * HEAD_DIM
    up_width = FF // shards
    width_qkv = 3 * head_width
    block_size = master.shape[-1]
    slots = master.shape[1]
    row_count = tokens.shape[0]
    length = segments.shape[1]
    pack_count = row_count // length
    own_segments = lax.dynamic_slice_in_dim(segments, tensor_rank * pack_count, pack_count, 0)
    qkv_tiles, out_tiles, up_tiles = tile_counts(shards, block_size)
    tile_total = owner.shape[0]

    group_base = tensor_rank if direct else 0
    order = feature_order(dp_rank if direct else 0)
    selector = (lax.iota(jnp.int32, D)[:, None] == order[None, :]).astype(jnp.bfloat16)

    steps = row_count // ROWS
    f32, bf16 = jnp.float32, jnp.bfloat16
    rows_spec = lambda width: pl.BlockSpec((ROWS, width), lambda i: (i, 0))
    full = lambda array: (array, pl.BlockSpec(memory_space=pltpu.VMEM))
    raw = lambda array: (array, pl.BlockSpec(memory_space=pl.ANY))
    by_rows = lambda array: (array, row_block(array))
    far_rows = lambda array: (array, row_block(array), "far")
    group_order = lax.iota(jnp.int32, shards) ^ group_base
    below = vectors[: 5 * D].reshape(5, D)
    above = vectors[5 * D + FF :].reshape(3, D)
    d_rows = jnp.stack(
        [below[4], below[0], above[1], above[0], below[1], above[2], below[0], below[0]]
    )
    bias_q = below[2].reshape(shards, head_width)[group_order]
    bias_v = below[3].reshape(shards, head_width)[group_order]
    bias_up = vectors[5 * D : 5 * D + FF].reshape(shards, up_width)[group_order]
    rows_in, grad_out, d_rows = call_rows(
        enter_kernel,
        steps,
        [far_rows(tokens), far_rows(out_grad), full(d_rows), full(selector)],
        [
            ((row_count, D), bf16, rows_spec(D), "far"),
            ((row_count, D), f32, rows_spec(D), "far"),
            ((8, D), f32, pl.BlockSpec(memory_space=pltpu.VMEM)),
        ],
        6 * row_count * D * D,
    )

    def flipped(index):
        from_out = (index >= qkv_tiles) & (index < qkv_tiles + out_tiles)
        return (from_out | (index >= qkv_tiles + out_tiles + up_tiles))[:, None, None]

    own_tiles = lax.dynamic_slice_in_dim(owner, dp_rank * slots, slots, 0)
    own_flip = flipped(own_tiles)
    sent = master[0].astype(jnp.bfloat16)
    sent = jnp.where(own_flip, jnp.swapaxes(sent, 1, 2), sent)
    placing = (lax.iota(jnp.int32, tile_total)[:, None] == owner[None, :]).astype(jnp.bfloat16)
    if direct:
        parts = sent.reshape(slots, PARTS, SUB * block_size).swapaxes(0, 1)
        parts = lax.all_to_all(parts, "dp", 0, 0, tiled=True).reshape(tile_total, -1)
        tiles = product(placing, parts).astype(jnp.bfloat16)
        slab = slabs_from_tiles(tiles.reshape(tile_total, 1, SUB, block_size), shards, block_size)[0]
        half, rows = D // 2, D // PARTS
        first_slab, up_slab, down_slab = (slab[:, k * D : (k + 1) * D] for k in range(3))
        near_left, near_right = down_slab[:, :half], down_slab[:, half:]
        *blocks, near_left, near_right, rows_in, grad_out, d_rows, bias_up = together(
            *from_z(first_slab),
            swap_over(near_left, 0, 2),
            swap_over(near_right, 1, 0),
            rows_in,
            grad_out,
            d_rows,
            bias_up,
        )
        left, right, down_near = merge(
            [first_slab, *blocks, down_slab, near_left, near_right],
            [(half, half, bf16), (half, half, bf16), (2 * rows, D, bf16)],
            [(k, z * rows, 0, rows, half, [(z, 0, k * half)]) for k in range(2) for z in range(4)]
            + [
                (2, 0, 0, rows, D, [(4, 0, 0)]),
                (2, rows, 0, rows, half, [(5, 0, 0)]),
                (2, rows, half, rows, half, [(6, 0, 0)]),
            ],
        )
        left, right, down_near, up_slab = together(left, right, down_near, up_slab)
        up_beside = swap_over(up_slab, 2, 0)
        (up_pair,) = merge(
            [up_slab, up_beside],
            [(2 * rows, D, bf16)],
            [(0, z * rows, 0, rows, D, [(z, 0, 0)]) for z in range(2)],
        )
        left_across, right_beside, up_pair = together(
            swap_over(left, 0, 2), swap_over(right, 1, 0), up_pair
        )
        near, left, right = merge(
            [left, left_across, right, right_beside],
            [(D, D, bf16), (D, half, bf16), (D, half, bf16)],
            [
                (out, q * half, col, half, half, [(2 * k + q, 0, 0)])
                for k in range(2)
                for q in range(2)
                for out, col in ((0, k * half), (1 + k, 0))
            ],
        )
        near, down_near = together(near, down_near)
        down_beside = swap_over(down_near, 2, 0)
        near_there, beside, across, up_far, down_beside = together(
            swap_over(near, 0, 1),
            swap_over(left, 1, 0),
            swap_over(right, 0, 2),
            swap_over(up_pair, 4, 0),
            down_beside,
        )
        up_z, down_pair = merge(
            [up_pair, up_far, down_near, down_beside],
            [(half, D, bf16)] * 2,
            [
                (k, z * 2 * rows, 0, 2 * rows, D, [(2 * k + z, 0, 0)])
                for k in range(2)
                for z in range(2)
            ],
        )
        first = [near, beside, across, near_there] + over_core([beside, across])[2:]
        up = [up_z, swap_over(up_z, 1, 0), swap_over(up_z, 0, 2), swap_over(up_z, 1, 2)]
        down_far = swap_over(down_pair, 4, 0)
        places = (place_first, plane_moves(), edges_moves())
        pieces = [first, None, None]
    else:
        gathered = lax.all_gather(sent, "dp", axis=0, tiled=True).reshape(tile_total, -1)
        tiles = product(placing, gathered).astype(jnp.bfloat16)
        slabs = slabs_from_tiles(
            tiles.reshape(tile_total, PARTS, SUB, block_size), shards, block_size
        )
        whole = jnp.concatenate([slabs[part_of_block(k)] for k in range(PARTS)], 0)
        every = lax.all_gather(whole, "tensor", axis=0)
        pieces = [
            [every[j][:, k * D : (k + 1) * D] for j in range(shards)] for k in range(3)
        ]
        places = (place_kinds, groups_moves(shards), groups_moves(shards))

    packs_step = ROWS // length
    bias_qkv = jnp.stack(
        [bias_q.reshape(D), jnp.zeros((D,), jnp.float32), bias_v.reshape(D)]
    )
    pairs = HEADS // 2
    probs_spec = pl.BlockSpec((packs_step, pairs, length, 2 * length), lambda i: (i, 0, 0, 0))
    sums_spec = lambda width: pl.BlockSpec((8, width), lambda i: (0, 0))
    square = 2 * row_count * D * D

    whole_out = ((shards, D, D), bf16, pl.BlockSpec(memory_space=pltpu.VMEM))
    packed, probs, attended, unit_first, inverse_first, normed_low, whole_first = call_rows(
        functools.partial(attention_kernel, places[0], len(pieces[0]), length),
        steps,
        [
            far_rows(rows_in),
            (own_segments[:, None, :], pl.BlockSpec((packs_step, 1, length), lambda i: (i, 0, 0))),
            (own_segments[:, :, None], pl.BlockSpec((packs_step, length, 1), lambda i: (i, 0, 0))),
            full(bias_qkv),
            full(d_rows),
            *[raw(w) + (("far",) if w.shape == (D, D) else ()) for w in pieces[0]],
        ],
        [
            ((row_count, 3 * D), bf16, rows_spec(3 * D), "far"),
            ((pack_count, pairs, length, 2 * length), bf16, probs_spec, "far"),
            ((row_count, D), bf16, rows_spec(D)),
            ((row_count, D), f32, rows_spec(D), "far"),
            ((row_count, 1), f32, rows_spec(1), "far"),
            ((row_count, D), bf16, rows_spec(D), "far"),
            whole_out,
        ],
        4 * square + 4 * row_count * length * D,
        row_count * length * HEADS,
        [
            pltpu.VMEM((packs_step * pairs, length, 2 * length), f32),
            pltpu.SemaphoreType.DMA((len(pieces[0]),)),
            *[pltpu.VMEM(w.shape, bf16) for w in pieces[0]],
        ],
    )
    if direct:
        up[0], normed_low = together(up[0], normed_low)
        *up, up_there, down_far, normed_low = together(
            *up, swap_over(up[0], 0, 1), down_far, normed_low
        )
        down_near, near_left, near_right = merge(
            [down_pair, down_far],
            [(D, D, bf16), (D, half, bf16), (D, half, bf16)],
            [(0, z * half, 0, half, D, [(z, 0, 0)]) for z in range(2)]
            + [
                (1 + k, z * half, 0, half, half, [(z, 0, k * half)])
                for k in range(2)
                for z in range(2)
            ],
        )
        down = [down_near, swap_over(near_left, 1, 0), swap_over(near_right, 0, 2)]
        pieces[1] = up + [up_there] + over_core(up[1:])[3:]
    activated, slope, whole_up = call_rows(
        functools.partial(up_kernel, places[1], shards),
        steps,
        [far_rows(normed_low), full(bias_up), *[raw(w) for w in pieces[1]]],
        [
            ((row_count, FF), bf16, rows_spec(FF)),
            ((row_count, FF), bf16, rows_spec(FF), "far"),
            whole_out,
        ],
        4 * square,
        2 * row_count * FF,
        [pltpu.SemaphoreType.DMA((len(places[1]),))],
    )
    if direct:
        *down, activated = together(*down, activated)
        pieces[2] = over_core(down)
    layer_out, grad_second, second_low, sums_second, whole_down = call_rows(
        functools.partial(down_kernel, places[2], shards),
        steps,
        [
            by_rows(activated),
            far_rows(unit_first),
            far_rows(grad_out),
            full(d_rows),
            *[raw(w) for w in pieces[2]],
        ],
        [
            ((row_count, D), f32, rows_spec(D), "far"),
            ((row_count, D), f32, rows_spec(D)),
            ((row_count, D), bf16, rows_spec(D)),
            ((8, D), f32, sums_spec(D)),
            whole_out,
        ],
        4 * square,
        0,
        [pltpu.SemaphoreType.DMA((len(places[2]),))],
    )
    grad_w_down = weight_halves([second_low], [(activated, up_width, 0)])
    if direct:
        down_parts = reduce_core_plane(grad_w_down)
        second_low, *down_parts = together(second_low, *down_parts)
        down_parts = reduce_plane(*down_parts)
    grad_pre, grad_bias_up = call_rows(
        functools.partial(hidden_back_kernel, shards),
        steps,
        [by_rows(second_low), far_rows(slope), full(whole_down)],
        [((row_count, FF), bf16, rows_spec(FF)), ((8, up_width), f32, sums_spec(up_width))],
        4 * square,
    )
    grad_w_up = weight_halves([normed_low], [(grad_pre, up_width, 0)])
    grad_first, first_low, grad_attended, sums_first = call_rows(
        functools.partial(back_kernel, shards),
        steps,
        [
            by_rows(grad_pre),
            by_rows(grad_second),
            far_rows(unit_first),
            far_rows(inverse_first),
            full(d_rows),
            full(whole_up),
            full(whole_first),
        ],
        [
            ((row_count, D), f32, rows_spec(D), "far"),
            ((row_count, D), bf16, rows_spec(D)),
            ((row_count, D), bf16, rows_spec(D)),
            ((8, D), f32, sums_spec(D)),
        ],
        20 * square,
    )
    if direct:
        up_parts = reduce_core_edges(grad_w_up)
        grad_attended, *parts = together(grad_attended, *up_parts, *down_parts)
        up_terms = edge_terms(*parts[:3])
        down_terms = [parts[3], swap_over(parts[4], 4, 0)]
    grad_packed, column_sums = call_rows(
        functools.partial(attention_back_kernel, length),
        steps,
        [by_rows(grad_attended), by_rows(attended), far_rows(packed), (probs, probs_spec, "far")],
        [
            ((row_count, 3 * D), bf16, rows_spec(3 * D)),
            ((8, 3 * D), f32, sums_spec(3 * D)),
        ],
        8 * square,
        0,
        [pltpu.VMEM((packs_step * pairs, length, 2 * length), bf16)] * 2,
    )
    rights = [(grad_packed, head_width, k * shards // 2) for k in range(3)]
    rights.append((attended, head_width, 0))
    grad_w_first = [weight_half(1, [rows_in, first_low], rights)]
    if direct:
        first_low, grad_w_first[0], *others = together(
            first_low, grad_w_first[0], *up_terms, *down_terms
        )
        up_terms, down_terms = others[:3], others[3:]
        up_near, up_far, first_low = together(*reduce_edges(up_terms), first_low)
        up_terms = [up_near, swap_over(up_far, 4, 0)]
    grad_w_first.append(weight_half(0, [rows_in, first_low], rights))
    if direct:
        first_parts = reduce_core_edges(grad_w_first)
        *first_parts, grad_first = together(*first_parts, grad_first)
        first_terms = edge_terms(*first_parts)
    (input_grad,) = call_rows(
        input_kernel,
        steps,
        [far_rows(grad_first), by_rows(grad_packed), full(selector), full(whole_first)],
        [((row_count, D), f32, rows_spec(D), "far")],
        40 * square,
    )
    if direct:
        *first_terms, input_grad, layer_out = together(*first_terms, input_grad, layer_out)
        first_terms = plane_edge_terms(*reduce_edges_plane(first_terms))
        first_terms[0], *others = together(
            first_terms[0],
            *up_terms,
            *down_terms,
            sums_first,
            sums_second,
            grad_bias_up,
            column_sums,
        )
        up_terms, down_terms = others[:2], others[2:4]
        sums_first, sums_second, grad_bias_up, column_sums = others[4:]
        up_terms = halve_z(*up_terms)
        up_terms = [up_terms[0], swap_over(up_terms[1], 2, 0)]
        down_terms = halve_z(*down_terms)
        down_terms = [down_terms[0], swap_over(down_terms[1], 2, 0)]
    (vector_rows,) = call_rows(
        functools.partial(vector_kernel, shards),
        1,
        [
            (
                lax.convert_element_type(group_base, jnp.int32).reshape(1),
                pl.BlockSpec(memory_space=pltpu.SMEM),
            ),
            full(sums_first),
            full(sums_second),
            full(grad_bias_up),
            full(column_sums),
            full(selector),
        ],
        [((16, D), f32, pl.BlockSpec(memory_space=pltpu.VMEM))],
        48 * D * D,
    )
    (layer_out,) = call_rows(
        layer_kernel,
        steps,
        [far_rows(layer_out), full(selector)],
        [((row_count, D), f32, rows_spec(D), "far")],
        2 * square,
    )
    if direct:
        *first_terms, layer_out = together(*first_terms, layer_out)
        *parts, vector_rows = together(*reduce_plane_edges(first_terms), vector_rows)
        first_terms = z_terms(*parts)
        first_terms[0], *others = together(first_terms[0], *up_terms, *down_terms)
        up_terms, down_terms = others[:2], others[2:]
        down_own = add_z(*down_terms)
        vector_rows = add_swapped(add_swapped(vector_rows, 0, 1), 0, 2)
        up_terms = plane_edge_terms(*reduce_edges_z(up_terms))
        up_own = reduce_edges_last(up_terms)
        *first_terms, vector_rows = together(*first_terms, vector_rows)
        first_own = reduce_z(first_terms)
        slab_grad = jnp.concatenate([first_own, up_own, down_own], 1).astype(jnp.bfloat16)
        tile_grad = tiles_from_slabs(slab_grad[None], shards, block_size).reshape(tile_total, -1)
        slot_grad = transposed_times(placing, tile_grad).astype(jnp.bfloat16)
        slot_grad, vector_rows = together(slot_grad, vector_rows)
        slot_grad = lax.all_to_all(
            slot_grad.reshape(PARTS, slots, SUB * block_size), "dp", 0, 0, tiled=True
        )
        vector_rows = add_swapped(add_swapped(vector_rows, 1, 0), 2, 0)
        slot_grad, vector_rows = together(slot_grad, vector_rows)
        vector_rows = add_swapped(vector_rows, 4, 0)
        owned_grads = slot_grad.swapaxes(0, 1).reshape(slots, block_size, block_size)
    else:
        every = jnp.stack(
            [
                jnp.concatenate(
                    [half[1 - j % 2][j // 2] for half in (grad_w_first, grad_w_up, grad_w_down)], 1
                )
                for j in range(shards)
            ]
        ).astype(jnp.float32)
        mine = lax.psum_scatter(every, "tensor", scatter_dimension=0, tiled=True)[0]
        blocks = mine.reshape(PARTS, D // PARTS, -1)
        blocks = jnp.stack([blocks[(p % 2) * 4 + p // 2] for p in range(PARTS)])
        tile_grad = tiles_from_slabs(blocks, shards, block_size)
        slot_grad = tile_grad.reshape(tile_total, block_size, block_size)[owner]
        owned_grads = lax.psum_scatter(slot_grad, "dp", scatter_dimension=0, tiled=True)
    owned_grads = jnp.where(own_flip, jnp.swapaxes(owned_grads, 1, 2), owned_grads)

    bias_first = 1.0 - DECAY_FIRST**ADAM_STEP
    bias_second = 1.0 - DECAY_SECOND**ADAM_STEP
    step_slots = max(k for k in (1, 2, 3, 4, 6, 12) if slots % k == 0)
    slots_spec = pl.BlockSpec((step_slots, block_size, block_size), lambda i: (i, 0, 0))
    slot_out = ((slots, block_size, block_size), f32, slots_spec, "far")
    new_master, new_first, new_second = call_rows(
        adam_kernel,
        slots // step_slots,
        [
            (array, slots_spec, "far")
            for array in (
                owned_grads,
                master[0],
                left_basis[0],
                right_basis[0],
                first_moment[0],
                second_moment[0],
            )
        ],
        [slot_out] * 3,
        22 * slots * block_size**3,
        slots * block_size**2,
    )
    if not direct:
        vector_rows = lax.psum(vector_rows, ("dp", "tensor"))
    vector_grad = vector_rows[: vectors.shape[0] // D].reshape(-1)
    new_vector_first = DECAY_FIRST * vector_first + (1.0 - DECAY_FIRST) * vector_grad
    new_vector_second = (
        DECAY_SECOND * vector_second + (1.0 - DECAY_SECOND) * vector_grad * vector_grad
    )
    new_vectors = vectors - VECTOR_RATE * (new_vector_first / bias_first) / (
        jnp.sqrt(new_vector_second / bias_second) + ADAM_EPS
    )
    return (
        layer_out,
        input_grad,
        new_master[None],
        new_first[None],
        new_second[None],
        new_vectors,
        new_vector_first,
        new_vector_second,
    )


def solution(mesh):
    return jax.shard_map(
        local,
        mesh=mesh,
        in_specs=(
            P(("dp", "tensor"), None),
            P("dp", None),
            P(("dp", "tensor"), None),
            P(),
            P("tensor", "dp", None, None),
            P("tensor", "dp", None, None),
            P("tensor", "dp", None, None),
            P("tensor", "dp", None, None),
            P("tensor", "dp", None, None),
            P(),
            P(),
            P(),
        ),
        out_specs=(
            P(("dp", "tensor"), None),
            P(("dp", "tensor"), None),
            P("tensor", "dp", None, None),
            P("tensor", "dp", None, None),
            P("tensor", "dp", None, None),
            P(),
            P(),
            P(),
        ),
        check_vma=False,
    )
```

```python
import functools
import math

import jax
import jax.numpy as jnp
from jax import lax
from jax.experimental import pallas as pl
from jax.experimental.pallas import tpu as pltpu
from jax.sharding import PartitionSpec as P

HEADS = 12
HEAD_DIM = 64
D = 768
FF = 3072
ADAM_STEP = 3


NORM_EPS = 1e-12
ADAM_EPS = 1e-08
MATRIX_RATE = 0.01
VECTOR_RATE = 0.1
DECAY_FIRST = 0.5
DECAY_SECOND = 0.5
MASKED = -1e30


def product(left_side, right_side):
    return jnp.dot(left_side, right_side, preferred_element_type=jnp.float32)


def times_transposed(left_side, right_side):
    return lax.dot_general(
        left_side, right_side, (((1,), (1,)), ((), ())), preferred_element_type=jnp.float32
    )


def transposed_times(left_side, right_side):
    return lax.dot_general(
        left_side, right_side, (((0,), (0,)), ((), ())), preferred_element_type=jnp.float32
    )


VMEM_LIMIT = 16 * 1024 * 1024

PARTS = 8
SUB = 12


def part_of_block(block):
    return (block % 4) * 2 + block // 4


def feature_order(rank):
    place = lax.iota(jnp.int32, D)
    part = part_of_block(place // (D // PARTS)) ^ rank
    inner = place % (D // PARTS)
    return (inner // SUB) * (PARTS * SUB) + part * SUB + inner % SUB


def tile_counts(shards, block_size):
    rows = D // block_size
    qkv = rows * (3 * D // shards // block_size)
    out = rows * (D // shards // block_size)
    up = rows * (FF // shards // block_size)
    return (qkv, out, up)


def slabs_from_tiles(tiles, shards, block_size):
    cut = tiles.shape[1]
    qkv, out, up = tile_counts(shards, block_size)
    rows = D // block_size

    def by_rows(part):
        cols = part.shape[0] // rows
        part = part.reshape(rows, cols, cut, SUB, block_size)
        return part.transpose(2, 0, 3, 1, 4).reshape(cut, rows * SUB, cols * block_size)

    def by_cols(part):
        cols = part.shape[0] // rows
        part = part.reshape(cols, rows, cut, SUB, block_size)
        return part.transpose(2, 1, 3, 0, 4).reshape(cut, rows * SUB, cols * block_size)

    return jnp.concatenate(
        [
            by_rows(tiles[:qkv]),
            by_cols(tiles[qkv : qkv + out]),
            by_rows(tiles[qkv + out : qkv + out + up]),
            by_cols(tiles[qkv + out + up :]),
        ],
        2,
    )


def tiles_from_slabs(slabs, shards, block_size):
    cut = slabs.shape[0]
    rows = D // block_size
    width_qkv, width_out, width_up = 3 * D // shards, D // shards, FF // shards

    def by_rows(part):
        cols = part.shape[2] // block_size
        part = part.reshape(cut, rows, SUB, cols, block_size)
        return part.transpose(1, 3, 0, 2, 4).reshape(rows * cols, cut, SUB, block_size)

    def by_cols(part):
        cols = part.shape[2] // block_size
        part = part.reshape(cut, rows, SUB, cols, block_size)
        return part.transpose(3, 1, 0, 2, 4).reshape(rows * cols, cut, SUB, block_size)

    first = width_qkv + width_out
    second = first + width_up
    return jnp.concatenate(
        [
            by_rows(slabs[:, :, :width_qkv]),
            by_cols(slabs[:, :, width_qkv:first]),
            by_rows(slabs[:, :, first:second]),
            by_cols(slabs[:, :, second:]),
        ],
        0,
    )


def swap_over(values, over_dp, over_tensor):
    dp, tensor = lax.axis_size("dp"), lax.axis_size("tensor")
    pairs = [
        (a * tensor + b, (a ^ over_dp) * tensor + (b ^ over_tensor))
        for a in range(dp)
        for b in range(tensor)
    ]
    return lax.ppermute(values, ("dp", "tensor"), pairs)


def merge(terms, outs, segments):
    chunk = D // PARTS

    def kernel(*refs):
        for out, row, col, rows, cols, parts in segments:

            def step(k, carry, out=out, row=row, col=col, cols=cols, parts=parts):
                pieces = [
                    refs[term][pl.ds(pl.multiple_of(at + k * chunk, 32), chunk), left : left + cols]
                    for term, at, left in parts
                ]
                if len(pieces) > 1:
                    value = sum(piece.astype(jnp.float32) for piece in pieces)
                else:
                    value = pieces[0]
                to = refs[len(terms) + out]
                to[pl.ds(pl.multiple_of(row + k * chunk, 32), chunk), col : col + cols] = (
                    value.astype(to.dtype)
                )
                return carry

            lax.fori_loop(0, rows // chunk, step, 0)

    spec = pl.BlockSpec(memory_space=pltpu.VMEM)
    size = sum(term.size for term in terms)
    return pl.pallas_call(
        kernel,
        in_specs=[spec] * len(terms),
        out_specs=[spec] * len(outs),
        out_shape=[jax.ShapeDtypeStruct((rows, cols), dtype) for rows, cols, dtype in outs],
        compiler_params=pltpu.CompilerParams(vmem_limit_bytes=VMEM_LIMIT),
        cost_estimate=pl.CostEstimate(flops=size, bytes_accessed=4 * size, transcendentals=0),
    )(*terms)


def from_z(block):
    return [swap_over(block, 2 * k, 0) for k in (1, 2, 3)]


def over_core(blocks):
    return blocks + [swap_over(block, 0, 1) for block in blocks]


def put(out_ref, lead, row, col, ref, at, left, rows, cols):
    chunk = min(rows, D // 2)

    def step(k, carry):
        to = pl.multiple_of(row + k * chunk, 32)
        source = pl.multiple_of(at + k * chunk, 32)
        out_ref[lead, pl.ds(to, chunk), col : col + cols] = ref[
            pl.ds(source, chunk), left : left + cols
        ]
        return carry

    lax.fori_loop(0, rows // chunk, step, 0)


def place_first(refs, out_ref):
    count = len(refs) // 2
    half, width = D // 2, D // 4
    for core in range(2):
        near, beside, across = refs[core * count : (core + 1) * count]
        for y in range(2):
            col = (2 * y + core) * width
            for kind in range(2):
                left = kind * width
                put(out_ref, kind, 0, col, near, y * half, left, half, width)
                put(out_ref, kind, half, col, beside, y * half, left, half, width)
                if y:
                    put(out_ref, 2 + kind, 0, col, across, 0, left, D, width)
                else:
                    put(out_ref, 2 + kind, 0, col, near, 0, half + left, D, width)


def edges_moves():
    rows, half = D // PARTS, D // 2
    moves = []
    for core in range(2):
        near, beside, across = range(3 * core, 3 * core + 3)
        for y in range(2):
            group = 2 * y + core
            for z in range(4):
                for x in range(2):
                    to, by_y, by_x = x * half + z * rows, (2 * z + y) * rows, (2 * z + x) * rows
                    moves.append((group, to, 0, beside if x else near, by_y, 0, rows, half))
                    source = (across, by_x, 0) if y else (near, by_x, half)
                    moves.append((group, to, half, *source, rows, half))
    return moves


def plane_moves():
    half = D // 2
    return [
        (2 * y + core, x * half, 0, 4 * core + 2 * y + x, 0, 0, half, D)
        for core in range(2)
        for y in range(2)
        for x in range(2)
    ]


def groups_moves(count):
    return [(group, 0, 0, group, 0, 0, D, D) for group in range(count)]


def move_all(moves, refs, out_ref, sems):
    copies = [
        pltpu.make_async_copy(
            refs[ref].at[pl.ds(at, rows), pl.ds(left, cols)],
            out_ref.at[lead, pl.ds(row, rows), pl.ds(col, cols)],
            sems.at[k],
        )
        for k, (lead, row, col, ref, at, left, rows, cols) in enumerate(moves)
    ]
    for copy in copies:
        copy.start()
    for copy in copies:
        copy.wait()


def place_kinds(refs, out_ref):
    width = D // len(refs)
    for group, ref in enumerate(refs):
        for kind in range(4):
            put(out_ref, kind, 0, group * width, ref, 0, kind * width, D, width)


def core_terms(halves):
    odd, even = halves
    return [even.reshape(2 * D, D), swap_over(odd, 0, 1).reshape(2 * D, D)]


def summed(count, row, col):
    return [(term, row, col) for term in range(count)]


def reduce_core_plane(halves):
    half = D // 2
    return merge(
        core_terms(halves),
        [(half, D, jnp.bfloat16)] * 4,
        [(k, 0, 0, half, D, summed(2, k * half, 0)) for k in range(4)],
    )


def reduce_plane(near, beside, across, opposite):
    pair = D // 4
    terms = [near, swap_over(beside, 1, 0), swap_over(across, 0, 2), swap_over(opposite, 1, 2)]
    return merge(
        terms,
        [(pair, D, jnp.bfloat16)] * 2,
        [(k, 0, 0, pair, D, summed(4, k * pair, 0)) for k in range(2)],
    )


def halve_z(near, received):
    rows = near.shape[0] // 2
    return merge(
        [near, received],
        [(rows, D, jnp.bfloat16)] * 2,
        [(k, 0, 0, rows, D, summed(2, k * rows, 0)) for k in range(2)],
    )


def add_z(near, received):
    rows = near.shape[0]
    return merge(
        [near, received], [(rows, D, jnp.float32)], [(0, 0, 0, rows, D, summed(2, 0, 0))]
    )[0]


def z_terms(own, *sent):
    return [own] + [swap_over(block, 2 * (k + 1), 0) for k, block in enumerate(sent)]


def reduce_z(terms):
    rows = D // PARTS
    return merge(terms, [(rows, D, jnp.float32)], [(0, 0, 0, rows, D, summed(4, 0, 0))])[0]


def reduce_core_edges(halves):
    half = D // 2
    return merge(
        core_terms(halves),
        [(D, D, jnp.bfloat16), (D, half, jnp.bfloat16), (D, half, jnp.bfloat16)],
        [
            (0, 0, 0, half, half, summed(2, 0, 0)),
            (0, half, 0, half, half, summed(2, D, 0)),
            (0, 0, half, D, half, summed(2, 0, half)),
            (1, 0, 0, half, half, summed(2, half, 0)),
            (1, half, 0, half, half, summed(2, D + half, 0)),
            (2, 0, 0, D, half, summed(2, D, half)),
        ],
    )


def edge_terms(near, left, right):
    return [near, swap_over(left, 1, 0), swap_over(right, 0, 2)]


def edge_sums(row):
    half = D // 2
    return ((0, [(0, row, 0), (1, row, 0)]), (half, [(0, row, half), (2, row, 0)]))


def plane_edge_terms(near, left, right):
    return [near, swap_over(left, 0, 2), swap_over(right, 1, 0)]


def reduce_edges_plane(terms):
    half = D // 2
    kept = [(0, 0, col, half, half, parts) for col, parts in edge_sums(0)]
    sent = [
        (1 + k, 0, 0, half, half, parts) for k, (_, parts) in enumerate(edge_sums(half))
    ]
    return merge(
        terms,
        [(half, D, jnp.bfloat16), (half, half, jnp.bfloat16), (half, half, jnp.bfloat16)],
        kept + sent,
    )


def reduce_plane_edges(terms):
    rows, half = D // PARTS, D // 2
    return merge(
        terms,
        [(rows, D, jnp.bfloat16)] * 4,
        [
            (k, 0, col, rows, half, parts)
            for k in range(4)
            for col, parts in edge_sums(k * rows)
        ],
    )


def reduce_edges(terms):
    rows, half = D // PARTS, D // 2
    return merge(
        terms,
        [(half, D, jnp.bfloat16)] * 2,
        [
            (k // 2, (2 * (k % 2) + q) * rows, col, rows, half, parts)
            for k in range(4)
            for q in range(2)
            for col, parts in edge_sums(q * half + k * rows)
        ],
    )


def reduce_edges_z(terms):
    rows, half = D // PARTS, D // 2
    return merge(
        terms,
        [(rows, D, jnp.bfloat16), (rows, half, jnp.bfloat16), (rows, half, jnp.bfloat16)],
        [
            (0, 0, 0, rows, D, summed(2, 0, 0)),
            (1, 0, 0, rows, half, summed(2, rows, 0)),
            (2, 0, 0, rows, half, summed(2, rows, half)),
        ],
    )


def reduce_edges_last(terms):
    rows, half = D // PARTS, D // 2
    return merge(
        terms,
        [(rows, D, jnp.float32)],
        [(0, 0, col, rows, half, parts) for col, parts in edge_sums(0)],
    )[0]


def add_swapped(values, over_dp, over_tensor):
    return values + swap_over(values, over_dp, over_tensor)


ROWS = 256


def dot_nt(left_side, right_side):
    return lax.dot_general(
        left_side, right_side, (((1,), (1,)), ((), ())), preferred_element_type=jnp.float32
    )


def row_block(array):
    return pl.BlockSpec((ROWS, array.shape[1]), lambda i: (i, 0))


def call_rows(kernel, steps, inputs, outputs, flops, transcendentals=0, scratch=()):
    arrays = [
        pltpu.with_memory_space_constraint(array, pltpu.HBM) if far else array
        for array, _, *far in inputs
    ]
    shapes = [jax.ShapeDtypeStruct(shape, dtype) for shape, dtype, *_ in outputs]
    moved = sum(a.size * a.dtype.itemsize for a in arrays + shapes)
    shapes = [
        pltpu.HBM(shape.shape, shape.dtype) if len(output) > 3 else shape
        for shape, output in zip(shapes, outputs)
    ]
    return pl.pallas_call(
        kernel,
        grid=(steps,),
        in_specs=[spec for _, spec, *_ in inputs],
        out_specs=[output[2] for output in outputs],
        out_shape=shapes,
        scratch_shapes=scratch,
        compiler_params=pltpu.CompilerParams(vmem_limit_bytes=VMEM_LIMIT),
        cost_estimate=pl.CostEstimate(
            flops=int(1.0 * flops), bytes_accessed=moved, transcendentals=transcendentals
        ),
    )(*arrays)


def norm_rows(summed):
    centred = summed - jnp.mean(summed, -1, keepdims=True)
    inverse = lax.rsqrt(jnp.mean(centred * centred, -1, keepdims=True) + NORM_EPS)
    return centred * inverse, inverse


def norm_pull(gradient, unit_rows, inverse, gain_row):
    scaled = gradient * gain_row
    return inverse * (
        scaled
        - jnp.mean(scaled, -1, keepdims=True)
        - unit_rows * jnp.mean(scaled * unit_rows, -1, keepdims=True)
    )


def add_rows(ref, rows):
    sums = [jnp.sum(row, 0, keepdims=True) for row in rows]
    start = pl.program_id(0) == 0
    for place, total in enumerate(sums):
        kept = jnp.where(start, 0.0, ref[place : place + 1, :])
        ref[place : place + 1, :] = kept + total


def settle(moves, refs, whole_ref, sems):
    @pl.when(pl.program_id(0) == 0)
    def _():
        move_all(moves, refs, whole_ref, sems)

    return [whole_ref.at[j] for j in range(whole_ref.shape[0])]


def pair_masks(length):
    wide = 2 * HEAD_DIM
    lower = lax.broadcasted_iota(jnp.int32, (length, wide), 1) < HEAD_DIM
    top = lax.broadcasted_iota(jnp.int32, (2 * length, wide), 0) < length
    left = lax.broadcasted_iota(jnp.int32, (2 * length, wide), 1) < HEAD_DIM
    return lower, top == left


def stacked(pair, own):
    return jnp.where(own, jnp.concatenate([pair, pair], 0), jnp.zeros((), pair.dtype))


def attention_kernel(place, total_count, length, *refs):
    rows_ref, across_ref, down_ref, bias_ref, vec_ref = refs[:5]
    outs = refs[5 + total_count : 12 + total_count]
    packed_ref, probs_ref, attended_ref, unit_ref, inverse_ref, low_ref, whole_ref = outs
    scores_ref, sems, *raw = refs[12 + total_count :]

    @pl.when(pl.program_id(0) == 0)
    def _():
        copies = [
            pltpu.make_async_copy(source, to, sems.at[k])
            for k, (source, to) in enumerate(zip(refs[5 : 5 + total_count], raw))
        ]
        for copy in copies:
            copy.start()
        for copy in copies:
            copy.wait()
        place(raw, whole_ref)

    weights = [whole_ref.at[kind] for kind in range(4)]
    wide = 2 * HEAD_DIM
    pairs = HEADS // 2
    rows = rows_ref[...]
    for kind in range(3):
        part = product(rows, weights[kind][...]) + bias_ref[kind : kind + 1, :]
        part = part.astype(jnp.bfloat16)
        if kind == 0:
            part = part * jnp.bfloat16(HEAD_DIM ** (-0.5))
        packed_ref[:, kind * D : (kind + 1) * D] = part
    _, own = pair_masks(length)
    ones = own.astype(jnp.bfloat16)
    steps = [(p, i) for p in range(ROWS // length) for i in range(pairs)]

    def pair_of(p, i, kind):
        span = slice(p * length, (p + 1) * length)
        return packed_ref[span, kind * D + i * wide : kind * D + (i + 1) * wide]

    for at, (p, i) in enumerate(steps):
        scores_ref[at] = dot_nt(pair_of(p, i, 0), stacked(pair_of(p, i, 1), own))
    for at, (p, i) in enumerate(steps):
        allowed = down_ref[p] == across_ref[p]
        for half in range(2):
            lanes = slice(half * length, (half + 1) * length)
            scores = jnp.where(allowed, scores_ref[at, :, lanes], MASKED)
            probs_ref[p, i, :, lanes] = jnp.exp(
                scores - jnp.max(scores, -1, keepdims=True)
            ).astype(jnp.bfloat16)
    for p, i in steps:
        mixed = product(
            probs_ref[p, i], jnp.concatenate([stacked(pair_of(p, i, 2), own), ones], 1)
        )
        attended_ref[p * length : (p + 1) * length, i * wide : (i + 1) * wide] = (
            mixed[:, :wide] / mixed[:, wide:]
        ).astype(jnp.bfloat16)
    summed = rows.astype(jnp.float32) + vec_ref[0:1, :]
    summed = summed + dot_nt(attended_ref[...], weights[3][...])
    unit, inverse = norm_rows(summed)
    unit_ref[...] = unit
    inverse_ref[...] = inverse
    low_ref[...] = (unit * vec_ref[1:2, :] + vec_ref[2:3, :]).astype(jnp.bfloat16)


def gelu_parts(values):
    size = jnp.abs(values)
    decay = jnp.exp2(values * values * (-0.5 / math.log(2.0)))
    t = 1.0 / (1.0 + size * (0.3275911 * 0.5**0.5))
    poly = t * (
        0.127414796
        + t * (-0.142248368 + t * (0.7107068705 + t * (-0.7265760135 + t * 0.5307027145)))
    )
    result = jnp.maximum(values, 0.0) - size * (poly * decay)
    rest = decay * (poly - size * (0.5 / math.pi) ** 0.5)
    return result, jnp.where(values > 0, 1.0 - rest, rest)


def up_kernel(place, shards, *refs):
    low_ref, bias_ref = refs[:2]
    act_ref, slope_ref, whole_ref, sems = refs[-4:]
    weights = settle(place, refs[2:-4], whole_ref, sems)
    width = weights[0].shape[1]
    chunk = 256
    low = low_ref[...]
    for j in range(shards):
        for c in range(0, width, chunk):
            pre = product(low, weights[j][:, c : c + chunk]) + bias_ref[j : j + 1, c : c + chunk]
            result, slope = gelu_parts(pre)
            at = j * width + c
            act_ref[:, at : at + chunk] = result.astype(jnp.bfloat16)
            slope_ref[:, at : at + chunk] = slope.astype(jnp.bfloat16)


def down_kernel(place, shards, *refs):
    act_ref, unit_ref, grad_ref, vec_ref = refs[:4]
    out_ref, dz_ref, low_ref, sums_ref, whole_ref, sems = refs[-6:]
    weights = settle(place, refs[4:-6], whole_ref, sems)
    width = weights[0].shape[1]
    summed = unit_ref[...] * vec_ref[1:2, :] + vec_ref[2:3, :] + vec_ref[3:4, :]
    for j in range(shards):
        summed = summed + dot_nt(act_ref[:, j * width : (j + 1) * width], weights[j][...])
    unit, inverse = norm_rows(summed)
    gain = vec_ref[4:5, :]
    out_ref[...] = unit * gain + vec_ref[5:6, :]
    gradient = grad_ref[...]
    dz = norm_pull(gradient, unit, inverse, gain)
    dz_ref[...] = dz
    low_ref[...] = dz.astype(jnp.bfloat16)
    add_rows(sums_ref, (gradient * unit, gradient, dz))


def hidden_back_kernel(shards, *refs):
    low_ref, slope_ref, whole_ref, dpre_ref, bias_sums_ref = refs
    width = whole_ref.shape[2]
    low = low_ref[...]
    for j in range(shards):
        span = slice(j * width, (j + 1) * width)
        dpre = product(low, whole_ref[j]) * slope_ref[:, span].astype(jnp.float32)
        dpre = dpre.astype(jnp.bfloat16)
        dpre_ref[:, span] = dpre
        total = jnp.sum(dpre.astype(jnp.float32), 0, keepdims=True)
        kept = jnp.where(pl.program_id(0) == 0, 0.0, bias_sums_ref[j : j + 1, :])
        bias_sums_ref[j : j + 1, :] = kept + total


def back_kernel(shards, *refs):
    dpre_ref, dz_ref, unit_ref, inverse_ref, vec_ref, up_ref, first_ref = refs[:7]
    dz1_ref, low1_ref, datt_ref, sums_ref = refs[7:]
    width = up_ref.shape[2]
    gradient = dz_ref[...]
    for j in range(shards):
        gradient = gradient + dot_nt(dpre_ref[:, j * width : (j + 1) * width], up_ref[j])
    unit = unit_ref[...]
    dz1 = norm_pull(gradient, unit, inverse_ref[...], vec_ref[1:2, :])
    dz1_ref[...] = dz1
    low1 = dz1.astype(jnp.bfloat16)
    low1_ref[...] = low1
    add_rows(sums_ref, (gradient * unit, gradient, dz1))
    datt_ref[...] = product(low1, first_ref[3]).astype(jnp.bfloat16)


def attention_back_kernel(length, *refs):
    datt_ref, attended_ref, packed_ref, probs_ref, dpacked_ref, sums_ref, up_ref, grad_ref = refs
    wide = 2 * HEAD_DIM
    lower, own = pair_masks(length)
    ones = own.astype(jnp.bfloat16)
    steps = [(p, i) for p in range(ROWS // length) for i in range(HEADS // 2)]

    def pair_of(p, i, kind):
        span = slice(p * length, (p + 1) * length)
        return packed_ref[span, kind * D + i * wide : kind * D + (i + 1) * wide]

    def keep(p, i, kind, grad):
        span = slice(p * length, (p + 1) * length)
        dpacked_ref[span, kind * D + i * wide : kind * D + (i + 1) * wide] = grad.astype(
            jnp.bfloat16
        )

    for place, (p, i) in enumerate(steps):
        span = slice(p * length, (p + 1) * length)
        lanes = slice(i * wide, (i + 1) * wide)
        upstream = datt_ref[span, lanes].astype(jnp.float32) / product(probs_ref[p, i], ones)
        up_ref[place, :, :wide] = upstream.astype(jnp.bfloat16)
        up_ref[place, :, wide:] = (upstream * attended_ref[span, lanes].astype(jnp.float32)).astype(
            jnp.bfloat16
        )
    for place, (p, i) in enumerate(steps):
        centred = dot_nt(
            up_ref[place], jnp.concatenate([stacked(pair_of(p, i, 2), own), -ones], 1)
        )
        grad_ref[place] = (probs_ref[p, i].astype(jnp.float32) * centred).astype(jnp.bfloat16)
    for place, (p, i) in enumerate(steps):
        grad_scores = grad_ref[place]
        keep(
            p, i, 0,
            product(grad_scores, stacked(pair_of(p, i, 1), own)) * HEAD_DIM ** (-0.5),
        )
        both = transposed_times(grad_scores, pair_of(p, i, 0))
        keep(p, i, 1, jnp.where(lower, both[:length], both[length:]))
        both = transposed_times(probs_ref[p, i], up_ref[place, :, :wide])
        keep(p, i, 2, jnp.where(lower, both[:length], both[length:]))
    total = jnp.sum(dpacked_ref[...].astype(jnp.float32), 0, keepdims=True)
    kept = jnp.where(pl.program_id(0) == 0, 0.0, sums_ref[0:1, :])
    sums_ref[0:1, :] = kept + total


def weight_kernel(odd, count, *refs):
    lefts = refs[: 2 if count > 1 else 1]
    rights, out_ref = refs[len(lefts) : -1], refs[-1]
    if count == 1:
        out_ref[0] = transposed_times(lefts[0][...], rights[0][...]).astype(jnp.bfloat16)
    else:
        half = rights[0].shape[1] // 2
        span = slice(half, 2 * half) if odd else slice(0, half)
        values = jnp.concatenate([right[:, span] for right in rights[:-1]], 1)
        width = values.shape[1]
        out_ref[0, :, :width] = transposed_times(lefts[0][...], values).astype(jnp.bfloat16)
        out_ref[0, :, width:] = transposed_times(lefts[1][...], rights[-1][:, span]).astype(
            jnp.bfloat16
        )


def weight_half(odd, lefts, rights):
    count = len(rights)
    single = count == 1
    specs = []
    for array, width, before in rights:
        if single:
            specs.append(pl.BlockSpec((array.shape[0], width), lambda i: (0, 2 * i + odd)))
        else:
            specs.append(pl.BlockSpec((array.shape[0], 2 * width), lambda i, b=before: (0, b + i)))
    arrays = [*lefts, *[array for array, _, _ in rights]]
    tokens = lefts[0].shape[0]
    (half,) = pl.pallas_call(
        functools.partial(weight_kernel, odd, count),
        grid=(2,),
        in_specs=[pl.BlockSpec(memory_space=pltpu.VMEM) for _ in lefts] + specs,
        out_specs=[pl.BlockSpec((1, D, D), lambda i: (i, 0, 0))],
        out_shape=[jax.ShapeDtypeStruct((2, D, D), jnp.bfloat16)],
        compiler_params=pltpu.CompilerParams(vmem_limit_bytes=VMEM_LIMIT),
        cost_estimate=pl.CostEstimate(
            flops=4 * tokens * D * D,
            bytes_accessed=sum(2 * array.size for array in arrays),
            transcendentals=0,
        ),
    )(*arrays)
    return half


def weight_halves(lefts, rights):
    return [weight_half(odd, lefts, rights) for odd in (1, 0)]


def two_terms(values):
    top = values.astype(jnp.bfloat16)
    return top, (values - top.astype(jnp.float32)).astype(jnp.bfloat16)


def adam_kernel(*refs):
    flip_ref, grad_ref, master_ref, left_ref, right_ref, first_ref, second_ref = refs[:7]
    master_out, first_out, second_out = refs[7:]
    bias_first = 1.0 - DECAY_FIRST**ADAM_STEP
    bias_second = 1.0 - DECAY_SECOND**ADAM_STEP
    count = grad_ref.shape[0]
    lefts = [two_terms(left_ref[k]) for k in range(count)]
    rights = [two_terms(right_ref[k]) for k in range(count)]
    turned = []
    for k in range(count):
        tile = grad_ref[k].astype(jnp.float32)
        flip = flip_ref[pl.program_id(0) * count + k] > 0
        tile = jnp.where(flip, tile.T, tile)
        top, rest = two_terms(tile)
        grad = product(top, rights[k][0]) + product(top, rights[k][1])
        if grad_ref.dtype != jnp.bfloat16:
            grad = grad + product(rest, rights[k][0])
        turned.append(grad)
    directions = []
    for k in range(count):
        top, rest = two_terms(turned[k])
        rotated = (
            transposed_times(lefts[k][0], top)
            + transposed_times(lefts[k][0], rest)
            + transposed_times(lefts[k][1], top)
        )
        first = DECAY_FIRST * first_ref[k] + (1.0 - DECAY_FIRST) * rotated
        second = DECAY_SECOND * second_ref[k] + (1.0 - DECAY_SECOND) * rotated * rotated
        first_out[k] = first
        second_out[k] = second
        directions.append(first / bias_first / (jnp.sqrt(second / bias_second) + ADAM_EPS))
    backs = [
        product(lefts[k][0], directions[k].astype(jnp.bfloat16)).astype(jnp.bfloat16)
        for k in range(count)
    ]
    for k in range(count):
        update = times_transposed(backs[k], rights[k][0])
        master_out[k] = master_ref[k] - MATRIX_RATE * update


def unpermuted(values, selector_ref):
    top, rest = two_terms(values)
    return dot_nt(top, selector_ref[...]) + dot_nt(rest, selector_ref[...])


def enter_kernel(tokens_ref, grad_ref, vectors_ref, selector_ref, rows_ref, out_ref, d_rows_ref):
    selector = selector_ref[...]
    rows_ref[...] = product(tokens_ref[...], selector).astype(jnp.bfloat16)
    top, rest = two_terms(grad_ref[...])
    out_ref[...] = product(top, selector) + product(rest, selector)

    @pl.when(pl.program_id(0) == 0)
    def _():
        rows = vectors_ref[...]
        permuted = jnp.zeros(rows.shape, jnp.float32)
        for _ in range(3):
            term = rows.astype(jnp.bfloat16)
            rows = rows - term.astype(jnp.float32)
            permuted = permuted + product(term, selector)
        d_rows_ref[...] = permuted


def layer_kernel(out_ref, selector_ref, layer_ref):
    layer_ref[...] = unpermuted(out_ref[...], selector_ref)


def input_kernel(dz1_ref, dpacked_ref, selector_ref, whole_ref, input_ref):
    gradient = dz1_ref[...]
    for kind in range(3):
        gradient = gradient + dot_nt(dpacked_ref[:, kind * D : (kind + 1) * D], whole_ref[kind])
    input_ref[...] = unpermuted(gradient, selector_ref)


def vector_kernel(shards, *refs):
    base_ref, first_ref, second_ref, hidden_ref, columns_ref, selector_ref, out_ref = refs
    base = base_ref[0]
    rows = jnp.concatenate(
        [
            first_ref[0:1, :],
            second_ref[0:1, :],
            first_ref[2:3, :],
            second_ref[2:3, :],
            first_ref[1:2, :],
            second_ref[1:2, :],
            jnp.zeros((2, D), jnp.float32),
        ],
        0,
    )
    natural = jnp.zeros((8, D), jnp.float32)
    for _ in range(3):
        term = rows.astype(jnp.bfloat16)
        rows = rows - term.astype(jnp.float32)
        natural = natural + dot_nt(term, selector_ref[...])
    hidden = FF // D
    out_ref[...] = jnp.zeros(out_ref.shape, jnp.float32)
    for at, row in ((0, 0), (1, 1), (4, 2), (5 + hidden, 3), (6 + hidden, 4), (7 + hidden, 5)):
        out_ref[at : at + 1, :] = natural[row : row + 1, :]
    width = D // shards
    for j in range(shards):
        out_ref[5 + j : 6 + j, :] = hidden_ref[pl.ds(j ^ base, 1), :]
        for at, kind in ((2, 0), (3, 2)):
            parts = [
                jnp.where(
                    (j ^ base) == k,
                    columns_ref[0:1, kind * D + k * width : kind * D + (k + 1) * width],
                    0.0,
                )
                for k in range(shards)
            ]
            out_ref[at : at + 1, j * width : (j + 1) * width] = sum(parts)


def together(*values):
    return lax.optimization_barrier(values)


def local(
    tokens,
    segments,
    out_grad,
    owner,
    master,
    left_basis,
    right_basis,
    first_moment,
    second_moment,
    vectors,
    vector_first,
    vector_second,
):
    shards = lax.axis_size("tensor")
    dp_size = lax.axis_size("dp")
    direct = dp_size == PARTS and shards == 4
    tensor_rank = lax.axis_index("tensor")
    dp_rank = lax.axis_index("dp")
    local_heads = HEADS // shards
    head_width = local_heads * HEAD_DIM
    up_width = FF // shards
    width_qkv = 3 * head_width
    block_size = master.shape[-1]
    slots = master.shape[1]
    row_count = tokens.shape[0]
    length = segments.shape[1]
    pack_count = row_count // length
    own_segments = lax.dynamic_slice_in_dim(segments, tensor_rank * pack_count, pack_count, 0)
    qkv_tiles, out_tiles, up_tiles = tile_counts(shards, block_size)
    tile_total = owner.shape[0]

    group_base = tensor_rank if direct else 0
    order = feature_order(dp_rank if direct else 0)
    selector = (lax.iota(jnp.int32, D)[:, None] == order[None, :]).astype(jnp.bfloat16)

    steps = row_count // ROWS
    f32, bf16 = jnp.float32, jnp.bfloat16
    rows_spec = lambda width: pl.BlockSpec((ROWS, width), lambda i: (i, 0))
    full = lambda array: (array, pl.BlockSpec(memory_space=pltpu.VMEM))
    raw = lambda array: (array, pl.BlockSpec(memory_space=pl.ANY))
    by_rows = lambda array: (array, row_block(array))
    far_rows = lambda array: (array, row_block(array), "far")
    group_order = lax.iota(jnp.int32, shards) ^ group_base
    below = vectors[: 5 * D].reshape(5, D)
    above = vectors[5 * D + FF :].reshape(3, D)
    d_rows = jnp.stack(
        [below[4], below[0], above[1], above[0], below[1], above[2], below[0], below[0]]
    )
    bias_q = below[2].reshape(shards, head_width)[group_order]
    bias_v = below[3].reshape(shards, head_width)[group_order]
    bias_up = vectors[5 * D : 5 * D + FF].reshape(shards, up_width)[group_order]
    rows_in, grad_out, d_rows = call_rows(
        enter_kernel,
        steps,
        [far_rows(tokens), far_rows(out_grad), full(d_rows), full(selector)],
        [
            ((row_count, D), bf16, rows_spec(D), "far"),
            ((row_count, D), f32, rows_spec(D), "far"),
            ((8, D), f32, pl.BlockSpec(memory_space=pltpu.VMEM)),
        ],
        6 * row_count * D * D,
    )

    def flipped(index):
        from_out = (index >= qkv_tiles) & (index < qkv_tiles + out_tiles)
        return (from_out | (index >= qkv_tiles + out_tiles + up_tiles))[:, None, None]

    own_tiles = lax.dynamic_slice_in_dim(owner, dp_rank * slots, slots, 0)
    own_flip = flipped(own_tiles)
    sent = master[0].astype(jnp.bfloat16)
    sent = jnp.where(own_flip, jnp.swapaxes(sent, 1, 2), sent)
    placing = (lax.iota(jnp.int32, tile_total)[:, None] == owner[None, :]).astype(jnp.bfloat16)
    if direct:
        parts = sent.reshape(slots, PARTS, SUB * block_size).swapaxes(0, 1)
        parts = lax.all_to_all(parts, "dp", 0, 0, tiled=True).reshape(tile_total, -1)
        tiles = product(placing, parts).astype(jnp.bfloat16)
        slab = slabs_from_tiles(tiles.reshape(tile_total, 1, SUB, block_size), shards, block_size)[0]
        half, rows = D // 2, D // PARTS
        first_slab, up_slab, down_slab = (slab[:, k * D : (k + 1) * D] for k in range(3))
        near_left, near_right = down_slab[:, :half], down_slab[:, half:]
        *blocks, near_left, near_right, rows_in, grad_out, d_rows, bias_up = together(
            *from_z(first_slab),
            swap_over(near_left, 0, 2),
            swap_over(near_right, 1, 0),
            rows_in,
            grad_out,
            d_rows,
            bias_up,
        )
        left, right, down_near = merge(
            [first_slab, *blocks, down_slab, near_left, near_right],
            [(half, half, bf16), (half, half, bf16), (2 * rows, D, bf16)],
            [(k, z * rows, 0, rows, half, [(z, 0, k * half)]) for k in range(2) for z in range(4)]
            + [
                (2, 0, 0, rows, D, [(4, 0, 0)]),
                (2, rows, 0, rows, half, [(5, 0, 0)]),
                (2, rows, half, rows, half, [(6, 0, 0)]),
            ],
        )
        left, right, down_near, up_slab = together(left, right, down_near, up_slab)
        up_beside = swap_over(up_slab, 2, 0)
        (up_pair,) = merge(
            [up_slab, up_beside],
            [(2 * rows, D, bf16)],
            [(0, z * rows, 0, rows, D, [(z, 0, 0)]) for z in range(2)],
        )
        left_across, right_beside, up_pair = together(
            swap_over(left, 0, 2), swap_over(right, 1, 0), up_pair
        )
        near, left, right = merge(
            [left, left_across, right, right_beside],
            [(D, D, bf16), (D, half, bf16), (D, half, bf16)],
            [
                (out, q * half, col, half, half, [(2 * k + q, 0, 0)])
                for k in range(2)
                for q in range(2)
                for out, col in ((0, k * half), (1 + k, 0))
            ],
        )
        near, down_near = together(near, down_near)
        down_beside = swap_over(down_near, 2, 0)
        near_there, beside, across, up_far, down_beside = together(
            swap_over(near, 0, 1),
            swap_over(left, 1, 0),
            swap_over(right, 0, 2),
            swap_over(up_pair, 4, 0),
            down_beside,
        )
        up_z, down_pair = merge(
            [up_pair, up_far, down_near, down_beside],
            [(half, D, bf16)] * 2,
            [
                (k, z * 2 * rows, 0, 2 * rows, D, [(2 * k + z, 0, 0)])
                for k in range(2)
                for z in range(2)
            ],
        )
        first = [near, beside, across, near_there] + over_core([beside, across])[2:]
        up = [up_z, swap_over(up_z, 1, 0), swap_over(up_z, 0, 2), swap_over(up_z, 1, 2)]
        down_far = swap_over(down_pair, 4, 0)
        places = (place_first, plane_moves(), edges_moves())
        pieces = [first, None, None]
    else:
        gathered = lax.all_gather(sent, "dp", axis=0, tiled=True).reshape(tile_total, -1)
        tiles = product(placing, gathered).astype(jnp.bfloat16)
        slabs = slabs_from_tiles(
            tiles.reshape(tile_total, PARTS, SUB, block_size), shards, block_size
        )
        whole = jnp.concatenate([slabs[part_of_block(k)] for k in range(PARTS)], 0)
        every = lax.all_gather(whole, "tensor", axis=0)
        pieces = [
            [every[j][:, k * D : (k + 1) * D] for j in range(shards)] for k in range(3)
        ]
        places = (place_kinds, groups_moves(shards), groups_moves(shards))

    packs_step = ROWS // length
    bias_qkv = jnp.stack(
        [bias_q.reshape(D), jnp.zeros((D,), jnp.float32), bias_v.reshape(D)]
    )
    pairs = HEADS // 2
    probs_spec = pl.BlockSpec((packs_step, pairs, length, 2 * length), lambda i: (i, 0, 0, 0))
    sums_spec = lambda width: pl.BlockSpec((8, width), lambda i: (0, 0))
    square = 2 * row_count * D * D

    whole_out = ((shards, D, D), bf16, pl.BlockSpec(memory_space=pltpu.VMEM))
    packed, probs, attended, unit_first, inverse_first, normed_low, whole_first = call_rows(
        functools.partial(attention_kernel, places[0], len(pieces[0]), length),
        steps,
        [
            far_rows(rows_in),
            (own_segments[:, None, :], pl.BlockSpec((packs_step, 1, length), lambda i: (i, 0, 0))),
            (own_segments[:, :, None], pl.BlockSpec((packs_step, length, 1), lambda i: (i, 0, 0))),
            full(bias_qkv),
            full(d_rows),
            *[raw(w) + (("far",) if w.shape == (D, D) else ()) for w in pieces[0]],
        ],
        [
            ((row_count, 3 * D), bf16, rows_spec(3 * D), "far"),
            ((pack_count, pairs, length, 2 * length), bf16, probs_spec, "far"),
            ((row_count, D), bf16, rows_spec(D)),
            ((row_count, D), f32, rows_spec(D), "far"),
            ((row_count, 1), f32, rows_spec(1), "far"),
            ((row_count, D), bf16, rows_spec(D), "far"),
            whole_out,
        ],
        4 * square + 4 * row_count * length * D,
        row_count * length * HEADS,
        [
            pltpu.VMEM((packs_step * pairs, length, 2 * length), f32),
            pltpu.SemaphoreType.DMA((len(pieces[0]),)),
            *[pltpu.VMEM(w.shape, bf16) for w in pieces[0]],
        ],
    )
    if direct:
        up[0], normed_low = together(up[0], normed_low)
        *up, up_there, down_far, normed_low = together(
            *up, swap_over(up[0], 0, 1), down_far, normed_low
        )
        down_near, near_left, near_right = merge(
            [down_pair, down_far],
            [(D, D, bf16), (D, half, bf16), (D, half, bf16)],
            [(0, z * half, 0, half, D, [(z, 0, 0)]) for z in range(2)]
            + [
                (1 + k, z * half, 0, half, half, [(z, 0, k * half)])
                for k in range(2)
                for z in range(2)
            ],
        )
        down = [down_near, swap_over(near_left, 1, 0), swap_over(near_right, 0, 2)]
        pieces[1] = up + [up_there] + over_core(up[1:])[3:]
    activated, slope, whole_up = call_rows(
        functools.partial(up_kernel, places[1], shards),
        steps,
        [far_rows(normed_low), full(bias_up), *[raw(w) for w in pieces[1]]],
        [
            ((row_count, FF), bf16, rows_spec(FF)),
            ((row_count, FF), bf16, rows_spec(FF), "far"),
            whole_out,
        ],
        4 * square,
        2 * row_count * FF,
        [pltpu.SemaphoreType.DMA((len(places[1]),))],
    )
    if direct:
        *down, activated = together(*down, activated)
        pieces[2] = over_core(down)
    layer_out, grad_second, second_low, sums_second, whole_down = call_rows(
        functools.partial(down_kernel, places[2], shards),
        steps,
        [
            by_rows(activated),
            far_rows(unit_first),
            far_rows(grad_out),
            full(d_rows),
            *[raw(w) for w in pieces[2]],
        ],
        [
            ((row_count, D), f32, rows_spec(D), "far"),
            ((row_count, D), f32, rows_spec(D)),
            ((row_count, D), bf16, rows_spec(D)),
            ((8, D), f32, sums_spec(D)),
            whole_out,
        ],
        4 * square,
        0,
        [pltpu.SemaphoreType.DMA((len(places[2]),))],
    )
    grad_w_down = weight_halves([second_low], [(activated, up_width, 0)])
    if direct:
        down_parts = reduce_core_plane(grad_w_down)
        second_low, *down_parts = together(second_low, *down_parts)
        down_parts = reduce_plane(*down_parts)
    grad_pre, grad_bias_up = call_rows(
        functools.partial(hidden_back_kernel, shards),
        steps,
        [by_rows(second_low), far_rows(slope), full(whole_down)],
        [((row_count, FF), bf16, rows_spec(FF)), ((8, up_width), f32, sums_spec(up_width))],
        4 * square,
    )
    grad_w_up = weight_halves([normed_low], [(grad_pre, up_width, 0)])
    grad_first, first_low, grad_attended, sums_first = call_rows(
        functools.partial(back_kernel, shards),
        steps,
        [
            by_rows(grad_pre),
            by_rows(grad_second),
            far_rows(unit_first),
            far_rows(inverse_first),
            full(d_rows),
            full(whole_up),
            full(whole_first),
        ],
        [
            ((row_count, D), f32, rows_spec(D), "far"),
            ((row_count, D), bf16, rows_spec(D)),
            ((row_count, D), bf16, rows_spec(D)),
            ((8, D), f32, sums_spec(D)),
        ],
        20 * square,
    )
    if direct:
        up_parts = reduce_core_edges(grad_w_up)
        grad_attended, *parts = together(grad_attended, *up_parts, *down_parts)
        up_terms = edge_terms(*parts[:3])
        down_terms = [parts[3], swap_over(parts[4], 4, 0)]
    grad_packed, column_sums = call_rows(
        functools.partial(attention_back_kernel, length),
        steps,
        [by_rows(grad_attended), by_rows(attended), far_rows(packed), (probs, probs_spec, "far")],
        [
            ((row_count, 3 * D), bf16, rows_spec(3 * D)),
            ((8, 3 * D), f32, sums_spec(3 * D)),
        ],
        8 * square,
        0,
        [pltpu.VMEM((packs_step * pairs, length, 2 * length), bf16)] * 2,
    )
    rights = [(grad_packed, head_width, k * shards // 2) for k in range(3)]
    rights.append((attended, head_width, 0))
    grad_w_first = [weight_half(1, [rows_in, first_low], rights)]
    if direct:
        first_low, grad_w_first[0], *others = together(
            first_low, grad_w_first[0], *up_terms, *down_terms
        )
        up_terms, down_terms = others[:3], others[3:]
        up_near, up_far, first_low = together(*reduce_edges(up_terms), first_low)
        up_terms = [up_near, swap_over(up_far, 4, 0)]
    grad_w_first.append(weight_half(0, [rows_in, first_low], rights))
    if direct:
        first_parts = reduce_core_edges(grad_w_first)
        *first_parts, grad_first = together(*first_parts, grad_first)
        first_terms = edge_terms(*first_parts)
    (input_grad,) = call_rows(
        input_kernel,
        steps,
        [far_rows(grad_first), by_rows(grad_packed), full(selector), full(whole_first)],
        [((row_count, D), f32, rows_spec(D), "far")],
        40 * square,
    )
    if direct:
        *first_terms, input_grad, layer_out = together(*first_terms, input_grad, layer_out)
        first_terms = plane_edge_terms(*reduce_edges_plane(first_terms))
        first_terms[0], *others = together(
            first_terms[0],
            *up_terms,
            *down_terms,
            sums_first,
            sums_second,
            grad_bias_up,
            column_sums,
        )
        up_terms, down_terms = others[:2], others[2:4]
        sums_first, sums_second, grad_bias_up, column_sums = others[4:]
        up_terms = halve_z(*up_terms)
        up_terms = [up_terms[0], swap_over(up_terms[1], 2, 0)]
        down_terms = halve_z(*down_terms)
        down_terms = [down_terms[0], swap_over(down_terms[1], 2, 0)]
    (vector_rows,) = call_rows(
        functools.partial(vector_kernel, shards),
        1,
        [
            (
                lax.convert_element_type(group_base, jnp.int32).reshape(1),
                pl.BlockSpec(memory_space=pltpu.SMEM),
            ),
            full(sums_first),
            full(sums_second),
            full(grad_bias_up),
            full(column_sums),
            full(selector),
        ],
        [((16, D), f32, pl.BlockSpec(memory_space=pltpu.VMEM))],
        48 * D * D,
    )
    (layer_out,) = call_rows(
        layer_kernel,
        steps,
        [far_rows(layer_out), full(selector)],
        [((row_count, D), f32, rows_spec(D), "far")],
        2 * square,
    )
    if direct:
        *first_terms, layer_out = together(*first_terms, layer_out)
        *parts, vector_rows = together(*reduce_plane_edges(first_terms), vector_rows)
        first_terms = z_terms(*parts)
        first_terms[0], *others = together(first_terms[0], *up_terms, *down_terms)
        up_terms, down_terms = others[:2], others[2:]
        down_own = add_z(*down_terms)
        vector_rows = add_swapped(add_swapped(vector_rows, 0, 1), 0, 2)
        up_terms = plane_edge_terms(*reduce_edges_z(up_terms))
        up_own = reduce_edges_last(up_terms)
        *first_terms, vector_rows = together(*first_terms, vector_rows)
        first_own = reduce_z(first_terms)
        slab_grad = jnp.concatenate([first_own, up_own, down_own], 1).astype(jnp.bfloat16)
        tile_grad = tiles_from_slabs(slab_grad[None], shards, block_size).reshape(tile_total, -1)
        slot_grad = transposed_times(placing, tile_grad).astype(jnp.bfloat16)
        slot_grad, vector_rows = together(slot_grad, vector_rows)
        slot_grad = lax.all_to_all(
            slot_grad.reshape(PARTS, slots, SUB * block_size), "dp", 0, 0, tiled=True
        )
        vector_rows = add_swapped(add_swapped(vector_rows, 1, 0), 2, 0)
        slot_grad, vector_rows = together(slot_grad, vector_rows)
        vector_rows = add_swapped(vector_rows, 4, 0)
        owned_grads = slot_grad.swapaxes(0, 1).reshape(slots, block_size, block_size)
    else:
        every = jnp.stack(
            [
                jnp.concatenate(
                    [half[1 - j % 2][j // 2] for half in (grad_w_first, grad_w_up, grad_w_down)], 1
                )
                for j in range(shards)
            ]
        ).astype(jnp.float32)
        mine = lax.psum_scatter(every, "tensor", scatter_dimension=0, tiled=True)[0]
        blocks = mine.reshape(PARTS, D // PARTS, -1)
        blocks = jnp.stack([blocks[(p % 2) * 4 + p // 2] for p in range(PARTS)])
        tile_grad = tiles_from_slabs(blocks, shards, block_size)
        slot_grad = tile_grad.reshape(tile_total, block_size, block_size)[owner]
        owned_grads = lax.psum_scatter(slot_grad, "dp", scatter_dimension=0, tiled=True)

    bias_first = 1.0 - DECAY_FIRST**ADAM_STEP
    bias_second = 1.0 - DECAY_SECOND**ADAM_STEP
    step_slots = max(k for k in (1, 2, 3, 4, 6, 12) if slots % k == 0)
    slots_spec = pl.BlockSpec((step_slots, block_size, block_size), lambda i: (i, 0, 0))
    slot_out = ((slots, block_size, block_size), f32, slots_spec, "far")
    new_master, new_first, new_second = call_rows(
        adam_kernel,
        slots // step_slots,
        [(own_flip.astype(jnp.int32).reshape(slots), pl.BlockSpec(memory_space=pltpu.SMEM))]
        + [
            (array, slots_spec, "far")
            for array in (
                owned_grads,
                master[0],
                left_basis[0],
                right_basis[0],
                first_moment[0],
                second_moment[0],
            )
        ],
        [slot_out] * 3,
        22 * slots * block_size**3,
        slots * block_size**2,
    )
    if not direct:
        vector_rows = lax.psum(vector_rows, ("dp", "tensor"))
    vector_grad = vector_rows[: vectors.shape[0] // D].reshape(-1)
    new_vector_first = DECAY_FIRST * vector_first + (1.0 - DECAY_FIRST) * vector_grad
    new_vector_second = (
        DECAY_SECOND * vector_second + (1.0 - DECAY_SECOND) * vector_grad * vector_grad
    )
    new_vectors = vectors - VECTOR_RATE * (new_vector_first / bias_first) / (
        jnp.sqrt(new_vector_second / bias_second) + ADAM_EPS
    )
    return (
        layer_out,
        input_grad,
        new_master[None],
        new_first[None],
        new_second[None],
        new_vectors,
        new_vector_first,
        new_vector_second,
    )


def solution(mesh):
    return jax.shard_map(
        local,
        mesh=mesh,
        in_specs=(
            P(("dp", "tensor"), None),
            P("dp", None),
            P(("dp", "tensor"), None),
            P(),
            P("tensor", "dp", None, None),
            P("tensor", "dp", None, None),
            P("tensor", "dp", None, None),
            P("tensor", "dp", None, None),
            P("tensor", "dp", None, None),
            P(),
            P(),
            P(),
        ),
        out_specs=(
            P(("dp", "tensor"), None),
            P(("dp", "tensor"), None),
            P("tensor", "dp", None, None),
            P("tensor", "dp", None, None),
            P("tensor", "dp", None, None),
            P(),
            P(),
            P(),
        ),
        check_vma=False,
    )
```

```python
import functools
import math

import jax
import jax.numpy as jnp
from jax import lax
from jax.experimental import pallas as pl
from jax.experimental.pallas import tpu as pltpu
from jax.sharding import PartitionSpec as P

HEADS = 12
HEAD_DIM = 64
D = 768
FF = 3072
ADAM_STEP = 3


NORM_EPS = 1e-12
ADAM_EPS = 1e-08
MATRIX_RATE = 0.01
VECTOR_RATE = 0.1
DECAY_FIRST = 0.5
DECAY_SECOND = 0.5
MASKED = -1e30


def product(left_side, right_side):
    return jnp.dot(left_side, right_side, preferred_element_type=jnp.float32)


def times_transposed(left_side, right_side):
    return lax.dot_general(
        left_side, right_side, (((1,), (1,)), ((), ())), preferred_element_type=jnp.float32
    )


def transposed_times(left_side, right_side):
    return lax.dot_general(
        left_side, right_side, (((0,), (0,)), ((), ())), preferred_element_type=jnp.float32
    )


VMEM_LIMIT = 16 * 1024 * 1024

PARTS = 8
SUB = 12


def part_of_block(block):
    return (block % 4) * 2 + block // 4


def feature_order(rank):
    place = lax.iota(jnp.int32, D)
    part = part_of_block(place // (D // PARTS)) ^ rank
    inner = place % (D // PARTS)
    return (inner // SUB) * (PARTS * SUB) + part * SUB + inner % SUB


def tile_counts(shards, block_size):
    rows = D // block_size
    qkv = rows * (3 * D // shards // block_size)
    out = rows * (D // shards // block_size)
    up = rows * (FF // shards // block_size)
    return (qkv, out, up)


def slabs_from_tiles(tiles, shards, block_size):
    cut = tiles.shape[1]
    qkv, out, up = tile_counts(shards, block_size)
    rows = D // block_size

    def by_rows(part):
        cols = part.shape[0] // rows
        part = part.reshape(rows, cols, cut, SUB, block_size)
        return part.transpose(2, 0, 3, 1, 4).reshape(cut, rows * SUB, cols * block_size)

    def by_cols(part):
        cols = part.shape[0] // rows
        part = part.reshape(cols, rows, cut, SUB, block_size)
        return part.transpose(2, 1, 3, 0, 4).reshape(cut, rows * SUB, cols * block_size)

    return jnp.concatenate(
        [
            by_rows(tiles[:qkv]),
            by_cols(tiles[qkv : qkv + out]),
            by_rows(tiles[qkv + out : qkv + out + up]),
            by_cols(tiles[qkv + out + up :]),
        ],
        2,
    )


def tiles_from_slabs(slabs, shards, block_size):
    cut = slabs.shape[0]
    rows = D // block_size
    width_qkv, width_out, width_up = 3 * D // shards, D // shards, FF // shards

    def by_rows(part):
        cols = part.shape[2] // block_size
        part = part.reshape(cut, rows, SUB, cols, block_size)
        return part.transpose(1, 3, 0, 2, 4).reshape(rows * cols, cut, SUB, block_size)

    def by_cols(part):
        cols = part.shape[2] // block_size
        part = part.reshape(cut, rows, SUB, cols, block_size)
        return part.transpose(3, 1, 0, 2, 4).reshape(rows * cols, cut, SUB, block_size)

    first = width_qkv + width_out
    second = first + width_up
    return jnp.concatenate(
        [
            by_rows(slabs[:, :, :width_qkv]),
            by_cols(slabs[:, :, width_qkv:first]),
            by_rows(slabs[:, :, first:second]),
            by_cols(slabs[:, :, second:]),
        ],
        0,
    )


def swap_over(values, over_dp, over_tensor):
    dp, tensor = lax.axis_size("dp"), lax.axis_size("tensor")
    pairs = [
        (a * tensor + b, (a ^ over_dp) * tensor + (b ^ over_tensor))
        for a in range(dp)
        for b in range(tensor)
    ]
    return lax.ppermute(values, ("dp", "tensor"), pairs)


def merge(terms, outs, segments):
    chunk = D // PARTS

    def kernel(*refs):
        for out, row, col, rows, cols, parts in segments:

            def step(k, carry, out=out, row=row, col=col, cols=cols, parts=parts):
                pieces = [
                    refs[term][pl.ds(pl.multiple_of(at + k * chunk, 32), chunk), left : left + cols]
                    for term, at, left in parts
                ]
                if len(pieces) > 1:
                    value = sum(piece.astype(jnp.float32) for piece in pieces)
                else:
                    value = pieces[0]
                to = refs[len(terms) + out]
                to[pl.ds(pl.multiple_of(row + k * chunk, 32), chunk), col : col + cols] = (
                    value.astype(to.dtype)
                )
                return carry

            lax.fori_loop(0, rows // chunk, step, 0)

    spec = pl.BlockSpec(memory_space=pltpu.VMEM)
    size = sum(term.size for term in terms)
    return pl.pallas_call(
        kernel,
        in_specs=[spec] * len(terms),
        out_specs=[spec] * len(outs),
        out_shape=[jax.ShapeDtypeStruct((rows, cols), dtype) for rows, cols, dtype in outs],
        compiler_params=pltpu.CompilerParams(vmem_limit_bytes=VMEM_LIMIT),
        cost_estimate=pl.CostEstimate(flops=size, bytes_accessed=4 * size, transcendentals=0),
    )(*terms)


def from_z(block):
    return [swap_over(block, 2 * k, 0) for k in (1, 2, 3)]


def over_core(blocks):
    return blocks + [swap_over(block, 0, 1) for block in blocks]


def put(out_ref, lead, row, col, ref, at, left, rows, cols):
    chunk = min(rows, D // 2)

    def step(k, carry):
        to = pl.multiple_of(row + k * chunk, 32)
        source = pl.multiple_of(at + k * chunk, 32)
        out_ref[lead, pl.ds(to, chunk), col : col + cols] = ref[
            pl.ds(source, chunk), left : left + cols
        ]
        return carry

    lax.fori_loop(0, rows // chunk, step, 0)


def place_first(refs, out_ref):
    count = len(refs) // 2
    half, width = D // 2, D // 4
    for core in range(2):
        near, beside, across = refs[core * count : (core + 1) * count]
        for y in range(2):
            col = (2 * y + core) * width
            for kind in range(2):
                left = kind * width
                put(out_ref, kind, 0, col, near, y * half, left, half, width)
                put(out_ref, kind, half, col, beside, y * half, left, half, width)
                if y:
                    put(out_ref, 2 + kind, 0, col, across, 0, left, D, width)
                else:
                    put(out_ref, 2 + kind, 0, col, near, 0, half + left, D, width)


def edges_moves():
    rows, half = D // PARTS, D // 2
    moves = []
    for core in range(2):
        near, beside, across = range(3 * core, 3 * core + 3)
        for y in range(2):
            group = 2 * y + core
            for z in range(4):
                for x in range(2):
                    to, by_y, by_x = x * half + z * rows, (2 * z + y) * rows, (2 * z + x) * rows
                    moves.append((group, to, 0, beside if x else near, by_y, 0, rows, half))
                    source = (across, by_x, 0) if y else (near, by_x, half)
                    moves.append((group, to, half, *source, rows, half))
    return moves


def plane_moves():
    half = D // 2
    return [
        (2 * y + core, x * half, 0, 4 * core + 2 * y + x, 0, 0, half, D)
        for core in range(2)
        for y in range(2)
        for x in range(2)
    ]


def groups_moves(count):
    return [(group, 0, 0, group, 0, 0, D, D) for group in range(count)]


def move_copies(moves, refs, out_ref, sems):
    copies = [[] for _ in range(out_ref.shape[0])]
    for k, (lead, row, col, ref, at, left, rows, cols) in enumerate(moves):
        copies[lead].append(
            pltpu.make_async_copy(
                refs[ref].at[pl.ds(at, rows), pl.ds(left, cols)],
                out_ref.at[lead, pl.ds(row, rows), pl.ds(col, cols)],
                sems.at[k],
            )
        )
    return copies


def place_kinds(refs, out_ref):
    width = D // len(refs)
    for group, ref in enumerate(refs):
        for kind in range(4):
            put(out_ref, kind, 0, group * width, ref, 0, kind * width, D, width)


def core_terms(halves):
    odd, even = halves
    return [even.reshape(2 * D, D), swap_over(odd, 0, 1).reshape(2 * D, D)]


def summed(count, row, col):
    return [(term, row, col) for term in range(count)]


def reduce_core_plane(halves):
    half = D // 2
    return merge(
        core_terms(halves),
        [(half, D, jnp.bfloat16)] * 4,
        [(k, 0, 0, half, D, summed(2, k * half, 0)) for k in range(4)],
    )


def reduce_plane(near, beside, across, opposite):
    pair = D // 4
    terms = [near, swap_over(beside, 1, 0), swap_over(across, 0, 2), swap_over(opposite, 1, 2)]
    return merge(
        terms,
        [(pair, D, jnp.bfloat16)] * 2,
        [(k, 0, 0, pair, D, summed(4, k * pair, 0)) for k in range(2)],
    )


def halve_z(near, received):
    rows = near.shape[0] // 2
    return merge(
        [near, received],
        [(rows, D, jnp.bfloat16)] * 2,
        [(k, 0, 0, rows, D, summed(2, k * rows, 0)) for k in range(2)],
    )


def add_z(near, received):
    rows = near.shape[0]
    return merge(
        [near, received], [(rows, D, jnp.float32)], [(0, 0, 0, rows, D, summed(2, 0, 0))]
    )[0]


def z_terms(own, *sent):
    return [own] + [swap_over(block, 2 * (k + 1), 0) for k, block in enumerate(sent)]


def reduce_z(terms):
    rows = D // PARTS
    return merge(terms, [(rows, D, jnp.float32)], [(0, 0, 0, rows, D, summed(4, 0, 0))])[0]


def reduce_core_edges(halves):
    half = D // 2
    return merge(
        core_terms(halves),
        [(D, D, jnp.bfloat16), (D, half, jnp.bfloat16), (D, half, jnp.bfloat16)],
        [
            (0, 0, 0, half, half, summed(2, 0, 0)),
            (0, half, 0, half, half, summed(2, D, 0)),
            (0, 0, half, D, half, summed(2, 0, half)),
            (1, 0, 0, half, half, summed(2, half, 0)),
            (1, half, 0, half, half, summed(2, D + half, 0)),
            (2, 0, 0, D, half, summed(2, D, half)),
        ],
    )


def edge_terms(near, left, right):
    return [near, swap_over(left, 1, 0), swap_over(right, 0, 2)]


def edge_sums(row):
    half = D // 2
    return ((0, [(0, row, 0), (1, row, 0)]), (half, [(0, row, half), (2, row, 0)]))


def plane_edge_terms(near, left, right):
    return [near, swap_over(left, 0, 2), swap_over(right, 1, 0)]


def reduce_edges_plane(terms):
    half = D // 2
    kept = [(0, 0, col, half, half, parts) for col, parts in edge_sums(0)]
    sent = [
        (1 + k, 0, 0, half, half, parts) for k, (_, parts) in enumerate(edge_sums(half))
    ]
    return merge(
        terms,
        [(half, D, jnp.bfloat16), (half, half, jnp.bfloat16), (half, half, jnp.bfloat16)],
        kept + sent,
    )


def reduce_plane_edges(terms):
    rows, half = D // PARTS, D // 2
    return merge(
        terms,
        [(rows, D, jnp.bfloat16)] * 4,
        [
            (k, 0, col, rows, half, parts)
            for k in range(4)
            for col, parts in edge_sums(k * rows)
        ],
    )


def reduce_edges(terms):
    rows, half = D // PARTS, D // 2
    return merge(
        terms,
        [(half, D, jnp.bfloat16)] * 2,
        [
            (k // 2, (2 * (k % 2) + q) * rows, col, rows, half, parts)
            for k in range(4)
            for q in range(2)
            for col, parts in edge_sums(q * half + k * rows)
        ],
    )


def reduce_edges_z(terms):
    rows, half = D // PARTS, D // 2
    return merge(
        terms,
        [(rows, D, jnp.bfloat16), (rows, half, jnp.bfloat16), (rows, half, jnp.bfloat16)],
        [
            (0, 0, 0, rows, D, summed(2, 0, 0)),
            (1, 0, 0, rows, half, summed(2, rows, 0)),
            (2, 0, 0, rows, half, summed(2, rows, half)),
        ],
    )


def reduce_edges_last(terms):
    rows, half = D // PARTS, D // 2
    return merge(
        terms,
        [(rows, D, jnp.float32)],
        [(0, 0, col, rows, half, parts) for col, parts in edge_sums(0)],
    )[0]


def add_swapped(values, over_dp, over_tensor):
    return values + swap_over(values, over_dp, over_tensor)


ROWS = 256


def dot_nt(left_side, right_side):
    return lax.dot_general(
        left_side, right_side, (((1,), (1,)), ((), ())), preferred_element_type=jnp.float32
    )


def row_block(array):
    return pl.BlockSpec((ROWS, array.shape[1]), lambda i: (i, 0))


def call_rows(kernel, steps, inputs, outputs, flops, transcendentals=0, scratch=()):
    arrays = [
        pltpu.with_memory_space_constraint(array, pltpu.HBM) if far else array
        for array, _, *far in inputs
    ]
    shapes = [jax.ShapeDtypeStruct(shape, dtype) for shape, dtype, *_ in outputs]
    moved = sum(a.size * a.dtype.itemsize for a in arrays + shapes)
    shapes = [
        pltpu.HBM(shape.shape, shape.dtype) if len(output) > 3 else shape
        for shape, output in zip(shapes, outputs)
    ]
    return pl.pallas_call(
        kernel,
        grid=(steps,),
        in_specs=[spec for _, spec, *_ in inputs],
        out_specs=[output[2] for output in outputs],
        out_shape=shapes,
        scratch_shapes=scratch,
        compiler_params=pltpu.CompilerParams(vmem_limit_bytes=VMEM_LIMIT),
        cost_estimate=pl.CostEstimate(
            flops=int(1.0 * flops), bytes_accessed=moved, transcendentals=transcendentals
        ),
    )(*arrays)


def norm_rows(summed):
    centred = summed - jnp.mean(summed, -1, keepdims=True)
    inverse = lax.rsqrt(jnp.mean(centred * centred, -1, keepdims=True) + NORM_EPS)
    return centred * inverse, inverse


def norm_pull(gradient, unit_rows, inverse, gain_row):
    scaled = gradient * gain_row
    return inverse * (
        scaled
        - jnp.mean(scaled, -1, keepdims=True)
        - unit_rows * jnp.mean(scaled * unit_rows, -1, keepdims=True)
    )


def add_rows(ref, rows):
    sums = [jnp.sum(row, 0, keepdims=True) for row in rows]
    start = pl.program_id(0) == 0
    for place, total in enumerate(sums):
        kept = jnp.where(start, 0.0, ref[place : place + 1, :])
        ref[place : place + 1, :] = kept + total


def settle(moves, refs, whole_ref, sems):
    first = pl.program_id(0) == 0
    copies = move_copies(moves, refs, whole_ref, sems)

    @pl.when(first)
    def _():
        for group in copies:
            for copy in group:
                copy.start()

    def weight(j):
        @pl.when(first)
        def _():
            for copy in copies[j]:
                copy.wait()

        return whole_ref.at[j]

    return weight


def pair_masks(length):
    wide = 2 * HEAD_DIM
    lower = lax.broadcasted_iota(jnp.int32, (length, wide), 1) < HEAD_DIM
    top = lax.broadcasted_iota(jnp.int32, (2 * length, wide), 0) < length
    left = lax.broadcasted_iota(jnp.int32, (2 * length, wide), 1) < HEAD_DIM
    return lower, top == left


def stacked(pair, own):
    return jnp.where(own, jnp.concatenate([pair, pair], 0), jnp.zeros((), pair.dtype))


def attention_kernel(place, total_count, length, *refs):
    rows_ref, across_ref, down_ref, bias_ref, vec_ref = refs[:5]
    outs = refs[5 + total_count : 12 + total_count]
    packed_ref, probs_ref, attended_ref, unit_ref, inverse_ref, low_ref, whole_ref = outs
    scores_ref, sems, *raw = refs[12 + total_count :]

    @pl.when(pl.program_id(0) == 0)
    def _():
        copies = [
            pltpu.make_async_copy(source, to, sems.at[k])
            for k, (source, to) in enumerate(zip(refs[5 : 5 + total_count], raw))
        ]
        for copy in copies:
            copy.start()
        for copy in copies:
            copy.wait()
        place(raw, whole_ref)

    weights = [whole_ref.at[kind] for kind in range(4)]
    wide = 2 * HEAD_DIM
    pairs = HEADS // 2
    rows = rows_ref[...]
    for kind in range(3):
        part = product(rows, weights[kind][...]) + bias_ref[kind : kind + 1, :]
        part = part.astype(jnp.bfloat16)
        if kind == 0:
            part = part * jnp.bfloat16(HEAD_DIM ** (-0.5))
        packed_ref[:, kind * D : (kind + 1) * D] = part
    _, own = pair_masks(length)
    ones = own.astype(jnp.bfloat16)
    steps = [(p, i) for p in range(ROWS // length) for i in range(pairs)]

    def pair_of(p, i, kind):
        span = slice(p * length, (p + 1) * length)
        return packed_ref[span, kind * D + i * wide : kind * D + (i + 1) * wide]

    for at, (p, i) in enumerate(steps):
        scores_ref[at] = dot_nt(pair_of(p, i, 0), stacked(pair_of(p, i, 1), own))
    for at, (p, i) in enumerate(steps):
        allowed = down_ref[p] == across_ref[p]
        for half in range(2):
            lanes = slice(half * length, (half + 1) * length)
            scores = jnp.where(allowed, scores_ref[at, :, lanes], MASKED)
            probs_ref[p, i, :, lanes] = jnp.exp(
                scores - jnp.max(scores, -1, keepdims=True)
            ).astype(jnp.bfloat16)
    for p, i in steps:
        mixed = product(
            probs_ref[p, i], jnp.concatenate([stacked(pair_of(p, i, 2), own), ones], 1)
        )
        attended_ref[p * length : (p + 1) * length, i * wide : (i + 1) * wide] = (
            mixed[:, :wide] / mixed[:, wide:]
        ).astype(jnp.bfloat16)
    summed = rows.astype(jnp.float32) + vec_ref[0:1, :]
    summed = summed + dot_nt(attended_ref[...], weights[3][...])
    unit, inverse = norm_rows(summed)
    unit_ref[...] = unit
    inverse_ref[...] = inverse
    low_ref[...] = (unit * vec_ref[1:2, :] + vec_ref[2:3, :]).astype(jnp.bfloat16)


def gelu_parts(values):
    size = jnp.abs(values)
    decay = jnp.exp2(values * values * (-0.5 / math.log(2.0)))
    t = 1.0 / (1.0 + size * (0.3275911 * 0.5**0.5))
    poly = t * (
        0.127414796
        + t * (-0.142248368 + t * (0.7107068705 + t * (-0.7265760135 + t * 0.5307027145)))
    )
    result = jnp.maximum(values, 0.0) - size * (poly * decay)
    rest = decay * (poly - size * (0.5 / math.pi) ** 0.5)
    return result, jnp.where(values > 0, 1.0 - rest, rest)


def up_kernel(place, shards, *refs):
    low_ref, bias_ref = refs[:2]
    act_ref, slope_ref, whole_ref, sems = refs[-4:]
    weight = settle(place, refs[2:-4], whole_ref, sems)
    width = whole_ref.shape[2]
    chunk = 256
    low = low_ref[...]
    for j in range(shards):
        group_ref = weight(j)
        for c in range(0, width, chunk):
            pre = product(low, group_ref[:, c : c + chunk]) + bias_ref[j : j + 1, c : c + chunk]
            result, slope = gelu_parts(pre)
            at = j * width + c
            act_ref[:, at : at + chunk] = result.astype(jnp.bfloat16)
            slope_ref[:, at : at + chunk] = slope.astype(jnp.bfloat16)


def down_kernel(place, shards, *refs):
    act_ref, unit_ref, grad_ref, vec_ref = refs[:4]
    out_ref, dz_ref, low_ref, sums_ref, whole_ref, sems = refs[-6:]
    weight = settle(place, refs[4:-6], whole_ref, sems)
    width = whole_ref.shape[2]
    summed = unit_ref[...] * vec_ref[1:2, :] + vec_ref[2:3, :] + vec_ref[3:4, :]
    for j in range(shards):
        summed = summed + dot_nt(act_ref[:, j * width : (j + 1) * width], weight(j)[...])
    unit, inverse = norm_rows(summed)
    gain = vec_ref[4:5, :]
    out_ref[...] = unit * gain + vec_ref[5:6, :]
    gradient = grad_ref[...]
    dz = norm_pull(gradient, unit, inverse, gain)
    dz_ref[...] = dz
    low_ref[...] = dz.astype(jnp.bfloat16)
    add_rows(sums_ref, (gradient * unit, gradient, dz))


def hidden_back_kernel(shards, *refs):
    low_ref, slope_ref, whole_ref, dpre_ref, bias_sums_ref = refs
    width = whole_ref.shape[2]
    low = low_ref[...]
    for j in range(shards):
        span = slice(j * width, (j + 1) * width)
        dpre = product(low, whole_ref[j]) * slope_ref[:, span].astype(jnp.float32)
        dpre = dpre.astype(jnp.bfloat16)
        dpre_ref[:, span] = dpre
        total = jnp.sum(dpre.astype(jnp.float32), 0, keepdims=True)
        kept = jnp.where(pl.program_id(0) == 0, 0.0, bias_sums_ref[j : j + 1, :])
        bias_sums_ref[j : j + 1, :] = kept + total


def back_kernel(shards, *refs):
    dpre_ref, dz_ref, unit_ref, inverse_ref, vec_ref, up_ref, first_ref = refs[:7]
    dz1_ref, low1_ref, datt_ref, sums_ref = refs[7:]
    width = up_ref.shape[2]
    gradient = dz_ref[...]
    for j in range(shards):
        gradient = gradient + dot_nt(dpre_ref[:, j * width : (j + 1) * width], up_ref[j])
    unit = unit_ref[...]
    dz1 = norm_pull(gradient, unit, inverse_ref[...], vec_ref[1:2, :])
    dz1_ref[...] = dz1
    low1 = dz1.astype(jnp.bfloat16)
    low1_ref[...] = low1
    add_rows(sums_ref, (gradient * unit, gradient, dz1))
    datt_ref[...] = product(low1, first_ref[3]).astype(jnp.bfloat16)


def attention_back_kernel(length, *refs):
    datt_ref, attended_ref, packed_ref, probs_ref, dpacked_ref, sums_ref, up_ref, grad_ref = refs
    wide = 2 * HEAD_DIM
    lower, own = pair_masks(length)
    ones = own.astype(jnp.bfloat16)
    steps = [(p, i) for p in range(ROWS // length) for i in range(HEADS // 2)]

    def pair_of(p, i, kind):
        span = slice(p * length, (p + 1) * length)
        return packed_ref[span, kind * D + i * wide : kind * D + (i + 1) * wide]

    def keep(p, i, kind, grad):
        span = slice(p * length, (p + 1) * length)
        dpacked_ref[span, kind * D + i * wide : kind * D + (i + 1) * wide] = grad.astype(
            jnp.bfloat16
        )

    for place, (p, i) in enumerate(steps):
        span = slice(p * length, (p + 1) * length)
        lanes = slice(i * wide, (i + 1) * wide)
        upstream = datt_ref[span, lanes].astype(jnp.float32) / product(probs_ref[p, i], ones)
        up_ref[place, :, :wide] = upstream.astype(jnp.bfloat16)
        up_ref[place, :, wide:] = (upstream * attended_ref[span, lanes].astype(jnp.float32)).astype(
            jnp.bfloat16
        )
    for place, (p, i) in enumerate(steps):
        centred = dot_nt(
            up_ref[place], jnp.concatenate([stacked(pair_of(p, i, 2), own), -ones], 1)
        )
        grad_ref[place] = (probs_ref[p, i].astype(jnp.float32) * centred).astype(jnp.bfloat16)
    for place, (p, i) in enumerate(steps):
        grad_scores = grad_ref[place]
        keep(
            p, i, 0,
            product(grad_scores, stacked(pair_of(p, i, 1), own)) * HEAD_DIM ** (-0.5),
        )
        both = transposed_times(grad_scores, pair_of(p, i, 0))
        keep(p, i, 1, jnp.where(lower, both[:length], both[length:]))
        both = transposed_times(probs_ref[p, i], up_ref[place, :, :wide])
        keep(p, i, 2, jnp.where(lower, both[:length], both[length:]))
    total = jnp.sum(dpacked_ref[...].astype(jnp.float32), 0, keepdims=True)
    kept = jnp.where(pl.program_id(0) == 0, 0.0, sums_ref[0:1, :])
    sums_ref[0:1, :] = kept + total


def weight_kernel(odd, count, *refs):
    lefts = refs[: 2 if count > 1 else 1]
    rights, out_ref = refs[len(lefts) : -1], refs[-1]
    if count == 1:
        out_ref[0] = transposed_times(lefts[0][...], rights[0][...]).astype(jnp.bfloat16)
    else:
        half = rights[0].shape[1] // 2
        span = slice(half, 2 * half) if odd else slice(0, half)
        values = jnp.concatenate([right[:, span] for right in rights[:-1]], 1)
        width = values.shape[1]
        out_ref[0, :, :width] = transposed_times(lefts[0][...], values).astype(jnp.bfloat16)
        out_ref[0, :, width:] = transposed_times(lefts[1][...], rights[-1][:, span]).astype(
            jnp.bfloat16
        )


def weight_half(odd, lefts, rights):
    count = len(rights)
    single = count == 1
    specs = []
    for array, width, before in rights:
        if single:
            specs.append(pl.BlockSpec((array.shape[0], width), lambda i: (0, 2 * i + odd)))
        else:
            specs.append(pl.BlockSpec((array.shape[0], 2 * width), lambda i, b=before: (0, b + i)))
    arrays = [*lefts, *[array for array, _, _ in rights]]
    tokens = lefts[0].shape[0]
    (half,) = pl.pallas_call(
        functools.partial(weight_kernel, odd, count),
        grid=(2,),
        in_specs=[pl.BlockSpec(memory_space=pltpu.VMEM) for _ in lefts] + specs,
        out_specs=[pl.BlockSpec((1, D, D), lambda i: (i, 0, 0))],
        out_shape=[jax.ShapeDtypeStruct((2, D, D), jnp.bfloat16)],
        compiler_params=pltpu.CompilerParams(vmem_limit_bytes=VMEM_LIMIT),
        cost_estimate=pl.CostEstimate(
            flops=4 * tokens * D * D,
            bytes_accessed=sum(2 * array.size for array in arrays),
            transcendentals=0,
        ),
    )(*arrays)
    return half


def weight_halves(lefts, rights):
    return [weight_half(odd, lefts, rights) for odd in (1, 0)]


def two_terms(values):
    top = values.astype(jnp.bfloat16)
    return top, (values - top.astype(jnp.float32)).astype(jnp.bfloat16)


def adam_kernel(*refs):
    flip_ref, grad_ref, master_ref, left_ref, right_ref, first_ref, second_ref = refs[:7]
    master_out, first_out, second_out = refs[7:]
    bias_first = 1.0 - DECAY_FIRST**ADAM_STEP
    bias_second = 1.0 - DECAY_SECOND**ADAM_STEP
    count = grad_ref.shape[0]
    lefts = [two_terms(left_ref[k]) for k in range(count)]
    rights = [two_terms(right_ref[k]) for k in range(count)]
    turned = []
    for k in range(count):
        tile = grad_ref[k].astype(jnp.float32)
        flip = flip_ref[pl.program_id(0) * count + k] > 0
        tile = jnp.where(flip, tile.T, tile)
        top, rest = two_terms(tile)
        grad = product(top, rights[k][0]) + product(top, rights[k][1])
        if grad_ref.dtype != jnp.bfloat16:
            grad = grad + product(rest, rights[k][0])
        turned.append(grad)
    directions = []
    for k in range(count):
        top, rest = two_terms(turned[k])
        rotated = (
            transposed_times(lefts[k][0], top)
            + transposed_times(lefts[k][0], rest)
            + transposed_times(lefts[k][1], top)
        )
        first = DECAY_FIRST * first_ref[k] + (1.0 - DECAY_FIRST) * rotated
        second = DECAY_SECOND * second_ref[k] + (1.0 - DECAY_SECOND) * rotated * rotated
        first_out[k] = first
        second_out[k] = second
        directions.append(first / bias_first / (jnp.sqrt(second / bias_second) + ADAM_EPS))
    backs = [
        product(lefts[k][0], directions[k].astype(jnp.bfloat16)).astype(jnp.bfloat16)
        for k in range(count)
    ]
    for k in range(count):
        update = times_transposed(backs[k], rights[k][0])
        master_out[k] = master_ref[k] - MATRIX_RATE * update


def unpermuted(values, selector_ref):
    top, rest = two_terms(values)
    return dot_nt(top, selector_ref[...]) + dot_nt(rest, selector_ref[...])


def enter_kernel(tokens_ref, grad_ref, vectors_ref, selector_ref, rows_ref, out_ref, d_rows_ref):
    selector = selector_ref[...]
    rows_ref[...] = product(tokens_ref[...], selector).astype(jnp.bfloat16)
    top, rest = two_terms(grad_ref[...])
    out_ref[...] = product(top, selector) + product(rest, selector)

    @pl.when(pl.program_id(0) == 0)
    def _():
        rows = vectors_ref[...]
        permuted = jnp.zeros(rows.shape, jnp.float32)
        for _ in range(3):
            term = rows.astype(jnp.bfloat16)
            rows = rows - term.astype(jnp.float32)
            permuted = permuted + product(term, selector)
        d_rows_ref[...] = permuted


def layer_kernel(out_ref, selector_ref, layer_ref):
    layer_ref[...] = unpermuted(out_ref[...], selector_ref)


def input_kernel(dz1_ref, dpacked_ref, selector_ref, whole_ref, input_ref):
    gradient = dz1_ref[...]
    for kind in range(3):
        gradient = gradient + dot_nt(dpacked_ref[:, kind * D : (kind + 1) * D], whole_ref[kind])
    input_ref[...] = unpermuted(gradient, selector_ref)


def vector_kernel(shards, *refs):
    base_ref, first_ref, second_ref, hidden_ref, columns_ref, selector_ref, out_ref = refs
    base = base_ref[0]
    rows = jnp.concatenate(
        [
            first_ref[0:1, :],
            second_ref[0:1, :],
            first_ref[2:3, :],
            second_ref[2:3, :],
            first_ref[1:2, :],
            second_ref[1:2, :],
            jnp.zeros((2, D), jnp.float32),
        ],
        0,
    )
    natural = jnp.zeros((8, D), jnp.float32)
    for _ in range(3):
        term = rows.astype(jnp.bfloat16)
        rows = rows - term.astype(jnp.float32)
        natural = natural + dot_nt(term, selector_ref[...])
    hidden = FF // D
    out_ref[...] = jnp.zeros(out_ref.shape, jnp.float32)
    for at, row in ((0, 0), (1, 1), (4, 2), (5 + hidden, 3), (6 + hidden, 4), (7 + hidden, 5)):
        out_ref[at : at + 1, :] = natural[row : row + 1, :]
    width = D // shards
    for j in range(shards):
        out_ref[5 + j : 6 + j, :] = hidden_ref[pl.ds(j ^ base, 1), :]
        for at, kind in ((2, 0), (3, 2)):
            parts = [
                jnp.where(
                    (j ^ base) == k,
                    columns_ref[0:1, kind * D + k * width : kind * D + (k + 1) * width],
                    0.0,
                )
                for k in range(shards)
            ]
            out_ref[at : at + 1, j * width : (j + 1) * width] = sum(parts)


def together(*values):
    return lax.optimization_barrier(values)


def local(
    tokens,
    segments,
    out_grad,
    owner,
    master,
    left_basis,
    right_basis,
    first_moment,
    second_moment,
    vectors,
    vector_first,
    vector_second,
):
    shards = lax.axis_size("tensor")
    dp_size = lax.axis_size("dp")
    direct = dp_size == PARTS and shards == 4
    tensor_rank = lax.axis_index("tensor")
    dp_rank = lax.axis_index("dp")
    local_heads = HEADS // shards
    head_width = local_heads * HEAD_DIM
    up_width = FF // shards
    width_qkv = 3 * head_width
    block_size = master.shape[-1]
    slots = master.shape[1]
    row_count = tokens.shape[0]
    length = segments.shape[1]
    pack_count = row_count // length
    own_segments = lax.dynamic_slice_in_dim(segments, tensor_rank * pack_count, pack_count, 0)
    qkv_tiles, out_tiles, up_tiles = tile_counts(shards, block_size)
    tile_total = owner.shape[0]

    group_base = tensor_rank if direct else 0
    order = feature_order(dp_rank if direct else 0)
    selector = (lax.iota(jnp.int32, D)[:, None] == order[None, :]).astype(jnp.bfloat16)

    steps = row_count // ROWS
    f32, bf16 = jnp.float32, jnp.bfloat16
    rows_spec = lambda width: pl.BlockSpec((ROWS, width), lambda i: (i, 0))
    full = lambda array: (array, pl.BlockSpec(memory_space=pltpu.VMEM))
    raw = lambda array: (array, pl.BlockSpec(memory_space=pl.ANY))
    by_rows = lambda array: (array, row_block(array))
    far_rows = lambda array: (array, row_block(array), "far")
    group_order = lax.iota(jnp.int32, shards) ^ group_base
    below = vectors[: 5 * D].reshape(5, D)
    above = vectors[5 * D + FF :].reshape(3, D)
    d_rows = jnp.stack(
        [below[4], below[0], above[1], above[0], below[1], above[2], below[0], below[0]]
    )
    bias_q = below[2].reshape(shards, head_width)[group_order]
    bias_v = below[3].reshape(shards, head_width)[group_order]
    bias_up = vectors[5 * D : 5 * D + FF].reshape(shards, up_width)[group_order]
    rows_in, grad_out, d_rows = call_rows(
        enter_kernel,
        steps,
        [far_rows(tokens), far_rows(out_grad), full(d_rows), full(selector)],
        [
            ((row_count, D), bf16, rows_spec(D), "far"),
            ((row_count, D), f32, rows_spec(D), "far"),
            ((8, D), f32, pl.BlockSpec(memory_space=pltpu.VMEM)),
        ],
        6 * row_count * D * D,
    )

    def flipped(index):
        from_out = (index >= qkv_tiles) & (index < qkv_tiles + out_tiles)
        return (from_out | (index >= qkv_tiles + out_tiles + up_tiles))[:, None, None]

    own_tiles = lax.dynamic_slice_in_dim(owner, dp_rank * slots, slots, 0)
    own_flip = flipped(own_tiles)
    sent = master[0].astype(jnp.bfloat16)
    sent = jnp.where(own_flip, jnp.swapaxes(sent, 1, 2), sent)
    placing = (lax.iota(jnp.int32, tile_total)[:, None] == owner[None, :]).astype(jnp.bfloat16)
    if direct:
        parts = sent.reshape(slots, PARTS, SUB * block_size).swapaxes(0, 1)
        parts = lax.all_to_all(parts, "dp", 0, 0, tiled=True).reshape(tile_total, -1)
        tiles = product(placing, parts).astype(jnp.bfloat16)
        slab = slabs_from_tiles(tiles.reshape(tile_total, 1, SUB, block_size), shards, block_size)[0]
        half, rows = D // 2, D // PARTS
        first_slab, up_slab, down_slab = (slab[:, k * D : (k + 1) * D] for k in range(3))
        near_left, near_right = down_slab[:, :half], down_slab[:, half:]
        *blocks, near_left, near_right, rows_in, grad_out, d_rows, bias_up = together(
            *from_z(first_slab),
            swap_over(near_left, 0, 2),
            swap_over(near_right, 1, 0),
            rows_in,
            grad_out,
            d_rows,
            bias_up,
        )
        left, right, down_near = merge(
            [first_slab, *blocks, down_slab, near_left, near_right],
            [(half, half, bf16), (half, half, bf16), (2 * rows, D, bf16)],
            [(k, z * rows, 0, rows, half, [(z, 0, k * half)]) for k in range(2) for z in range(4)]
            + [
                (2, 0, 0, rows, D, [(4, 0, 0)]),
                (2, rows, 0, rows, half, [(5, 0, 0)]),
                (2, rows, half, rows, half, [(6, 0, 0)]),
            ],
        )
        left, right, down_near, up_slab = together(left, right, down_near, up_slab)
        up_beside = swap_over(up_slab, 2, 0)
        (up_pair,) = merge(
            [up_slab, up_beside],
            [(2 * rows, D, bf16)],
            [(0, z * rows, 0, rows, D, [(z, 0, 0)]) for z in range(2)],
        )
        left_across, right_beside, up_pair = together(
            swap_over(left, 0, 2), swap_over(right, 1, 0), up_pair
        )
        near, left, right = merge(
            [left, left_across, right, right_beside],
            [(D, D, bf16), (D, half, bf16), (D, half, bf16)],
            [
                (out, q * half, col, half, half, [(2 * k + q, 0, 0)])
                for k in range(2)
                for q in range(2)
                for out, col in ((0, k * half), (1 + k, 0))
            ],
        )
        near, down_near = together(near, down_near)
        down_beside = swap_over(down_near, 2, 0)
        near_there, beside, across, up_far, down_beside = together(
            swap_over(near, 0, 1),
            swap_over(left, 1, 0),
            swap_over(right, 0, 2),
            swap_over(up_pair, 4, 0),
            down_beside,
        )
        up_z, down_pair = merge(
            [up_pair, up_far, down_near, down_beside],
            [(half, D, bf16)] * 2,
            [
                (k, z * 2 * rows, 0, 2 * rows, D, [(2 * k + z, 0, 0)])
                for k in range(2)
                for z in range(2)
            ],
        )
        first = [near, beside, across, near_there] + over_core([beside, across])[2:]
        up = [up_z, swap_over(up_z, 1, 0), swap_over(up_z, 0, 2), swap_over(up_z, 1, 2)]
        down_far = swap_over(down_pair, 4, 0)
        places = (place_first, plane_moves(), edges_moves())
        pieces = [first, None, None]
    else:
        gathered = lax.all_gather(sent, "dp", axis=0, tiled=True).reshape(tile_total, -1)
        tiles = product(placing, gathered).astype(jnp.bfloat16)
        slabs = slabs_from_tiles(
            tiles.reshape(tile_total, PARTS, SUB, block_size), shards, block_size
        )
        whole = jnp.concatenate([slabs[part_of_block(k)] for k in range(PARTS)], 0)
        every = lax.all_gather(whole, "tensor", axis=0)
        pieces = [
            [every[j][:, k * D : (k + 1) * D] for j in range(shards)] for k in range(3)
        ]
        places = (place_kinds, groups_moves(shards), groups_moves(shards))

    packs_step = ROWS // length
    bias_qkv = jnp.stack(
        [bias_q.reshape(D), jnp.zeros((D,), jnp.float32), bias_v.reshape(D)]
    )
    pairs = HEADS // 2
    probs_spec = pl.BlockSpec((packs_step, pairs, length, 2 * length), lambda i: (i, 0, 0, 0))
    sums_spec = lambda width: pl.BlockSpec((8, width), lambda i: (0, 0))
    square = 2 * row_count * D * D

    whole_out = ((shards, D, D), bf16, pl.BlockSpec(memory_space=pltpu.VMEM))
    packed, probs, attended, unit_first, inverse_first, normed_low, whole_first = call_rows(
        functools.partial(attention_kernel, places[0], len(pieces[0]), length),
        steps,
        [
            far_rows(rows_in),
            (own_segments[:, None, :], pl.BlockSpec((packs_step, 1, length), lambda i: (i, 0, 0))),
            (own_segments[:, :, None], pl.BlockSpec((packs_step, length, 1), lambda i: (i, 0, 0))),
            full(bias_qkv),
            full(d_rows),
            *[raw(w) + (("far",) if w.shape == (D, D) else ()) for w in pieces[0]],
        ],
        [
            ((row_count, 3 * D), bf16, rows_spec(3 * D), "far"),
            ((pack_count, pairs, length, 2 * length), bf16, probs_spec, "far"),
            ((row_count, D), bf16, rows_spec(D)),
            ((row_count, D), f32, rows_spec(D), "far"),
            ((row_count, 1), f32, rows_spec(1), "far"),
            ((row_count, D), bf16, rows_spec(D), "far"),
            whole_out,
        ],
        4 * square + 4 * row_count * length * D,
        row_count * length * HEADS,
        [
            pltpu.VMEM((packs_step * pairs, length, 2 * length), f32),
            pltpu.SemaphoreType.DMA((len(pieces[0]),)),
            *[pltpu.VMEM(w.shape, bf16) for w in pieces[0]],
        ],
    )
    if direct:
        up[0], normed_low = together(up[0], normed_low)
        *up, up_there, down_far, normed_low = together(
            *up, swap_over(up[0], 0, 1), down_far, normed_low
        )
        down_near, near_left, near_right = merge(
            [down_pair, down_far],
            [(D, D, bf16), (D, half, bf16), (D, half, bf16)],
            [(0, z * half, 0, half, D, [(z, 0, 0)]) for z in range(2)]
            + [
                (1 + k, z * half, 0, half, half, [(z, 0, k * half)])
                for k in range(2)
                for z in range(2)
            ],
        )
        down = [down_near, swap_over(near_left, 1, 0), swap_over(near_right, 0, 2)]
        pieces[1] = up + [up_there] + over_core(up[1:])[3:]
    activated, slope, whole_up = call_rows(
        functools.partial(up_kernel, places[1], shards),
        steps,
        [far_rows(normed_low), full(bias_up), *[raw(w) for w in pieces[1]]],
        [
            ((row_count, FF), bf16, rows_spec(FF)),
            ((row_count, FF), bf16, rows_spec(FF), "far"),
            whole_out,
        ],
        4 * square,
        2 * row_count * FF,
        [pltpu.SemaphoreType.DMA((len(places[1]),))],
    )
    if direct:
        *down, activated = together(*down, activated)
        pieces[2] = over_core(down)
    layer_out, grad_second, second_low, sums_second, whole_down = call_rows(
        functools.partial(down_kernel, places[2], shards),
        steps,
        [
            by_rows(activated),
            far_rows(unit_first),
            far_rows(grad_out),
            full(d_rows),
            *[raw(w) for w in pieces[2]],
        ],
        [
            ((row_count, D), f32, rows_spec(D), "far"),
            ((row_count, D), f32, rows_spec(D)),
            ((row_count, D), bf16, rows_spec(D)),
            ((8, D), f32, sums_spec(D)),
            whole_out,
        ],
        4 * square,
        0,
        [pltpu.SemaphoreType.DMA((len(places[2]),))],
    )
    grad_w_down = weight_halves([second_low], [(activated, up_width, 0)])
    if direct:
        down_parts = reduce_core_plane(grad_w_down)
        second_low, *down_parts = together(second_low, *down_parts)
        down_parts = reduce_plane(*down_parts)
    grad_pre, grad_bias_up = call_rows(
        functools.partial(hidden_back_kernel, shards),
        steps,
        [by_rows(second_low), far_rows(slope), full(whole_down)],
        [((row_count, FF), bf16, rows_spec(FF)), ((8, up_width), f32, sums_spec(up_width))],
        4 * square,
    )
    grad_w_up = weight_halves([normed_low], [(grad_pre, up_width, 0)])
    grad_first, first_low, grad_attended, sums_first = call_rows(
        functools.partial(back_kernel, shards),
        steps,
        [
            by_rows(grad_pre),
            by_rows(grad_second),
            far_rows(unit_first),
            far_rows(inverse_first),
            full(d_rows),
            full(whole_up),
            full(whole_first),
        ],
        [
            ((row_count, D), f32, rows_spec(D), "far"),
            ((row_count, D), bf16, rows_spec(D)),
            ((row_count, D), bf16, rows_spec(D)),
            ((8, D), f32, sums_spec(D)),
        ],
        20 * square,
    )
    if direct:
        up_parts = reduce_core_edges(grad_w_up)
        grad_attended, *parts = together(grad_attended, *up_parts, *down_parts)
        up_terms = edge_terms(*parts[:3])
        down_terms = [parts[3], swap_over(parts[4], 4, 0)]
    grad_packed, column_sums = call_rows(
        functools.partial(attention_back_kernel, length),
        steps,
        [by_rows(grad_attended), by_rows(attended), far_rows(packed), (probs, probs_spec, "far")],
        [
            ((row_count, 3 * D), bf16, rows_spec(3 * D)),
            ((8, 3 * D), f32, sums_spec(3 * D)),
        ],
        8 * square,
        0,
        [pltpu.VMEM((packs_step * pairs, length, 2 * length), bf16)] * 2,
    )
    rights = [(grad_packed, head_width, k * shards // 2) for k in range(3)]
    rights.append((attended, head_width, 0))
    grad_w_first = [weight_half(1, [rows_in, first_low], rights)]
    if direct:
        first_low, grad_w_first[0], *others = together(
            first_low, grad_w_first[0], *up_terms, *down_terms
        )
        up_terms, down_terms = others[:3], others[3:]
        up_near, up_far, first_low = together(*reduce_edges(up_terms), first_low)
        up_terms = [up_near, swap_over(up_far, 4, 0)]
    grad_w_first.append(weight_half(0, [rows_in, first_low], rights))
    if direct:
        first_parts = reduce_core_edges(grad_w_first)
        *first_parts, grad_first = together(*first_parts, grad_first)
        first_terms = edge_terms(*first_parts)
    (input_grad,) = call_rows(
        input_kernel,
        steps,
        [far_rows(grad_first), by_rows(grad_packed), full(selector), full(whole_first)],
        [((row_count, D), f32, rows_spec(D), "far")],
        40 * square,
    )
    if direct:
        *first_terms, input_grad, layer_out = together(*first_terms, input_grad, layer_out)
        first_terms = plane_edge_terms(*reduce_edges_plane(first_terms))
        first_terms[0], *others = together(
            first_terms[0],
            *up_terms,
            *down_terms,
            sums_first,
            sums_second,
            grad_bias_up,
            column_sums,
        )
        up_terms, down_terms = others[:2], others[2:4]
        sums_first, sums_second, grad_bias_up, column_sums = others[4:]
        up_terms = halve_z(*up_terms)
        up_terms = [up_terms[0], swap_over(up_terms[1], 2, 0)]
        down_terms = halve_z(*down_terms)
        down_terms = [down_terms[0], swap_over(down_terms[1], 2, 0)]
    (vector_rows,) = call_rows(
        functools.partial(vector_kernel, shards),
        1,
        [
            (
                lax.convert_element_type(group_base, jnp.int32).reshape(1),
                pl.BlockSpec(memory_space=pltpu.SMEM),
            ),
            full(sums_first),
            full(sums_second),
            full(grad_bias_up),
            full(column_sums),
            full(selector),
        ],
        [((16, D), f32, pl.BlockSpec(memory_space=pltpu.VMEM))],
        48 * D * D,
    )
    (layer_out,) = call_rows(
        layer_kernel,
        steps,
        [far_rows(layer_out), full(selector)],
        [((row_count, D), f32, rows_spec(D), "far")],
        2 * square,
    )
    if direct:
        *first_terms, layer_out = together(*first_terms, layer_out)
        *parts, vector_rows = together(*reduce_plane_edges(first_terms), vector_rows)
        first_terms = z_terms(*parts)
        first_terms[0], *others = together(first_terms[0], *up_terms, *down_terms)
        up_terms, down_terms = others[:2], others[2:]
        down_own = add_z(*down_terms)
        vector_rows = add_swapped(add_swapped(vector_rows, 0, 1), 0, 2)
        up_terms = plane_edge_terms(*reduce_edges_z(up_terms))
        up_own = reduce_edges_last(up_terms)
        *first_terms, vector_rows = together(*first_terms, vector_rows)
        first_own = reduce_z(first_terms)
        slab_grad = jnp.concatenate([first_own, up_own, down_own], 1).astype(jnp.bfloat16)
        tile_grad = tiles_from_slabs(slab_grad[None], shards, block_size).reshape(tile_total, -1)
        slot_grad = transposed_times(placing, tile_grad).astype(jnp.bfloat16)
        slot_grad, vector_rows = together(slot_grad, vector_rows)
        slot_grad = lax.all_to_all(
            slot_grad.reshape(PARTS, slots, SUB * block_size), "dp", 0, 0, tiled=True
        )
        vector_rows = add_swapped(add_swapped(vector_rows, 1, 0), 2, 0)
        slot_grad, vector_rows = together(slot_grad, vector_rows)
        vector_rows = add_swapped(vector_rows, 4, 0)
        owned_grads = slot_grad.swapaxes(0, 1).reshape(slots, block_size, block_size)
    else:
        every = jnp.stack(
            [
                jnp.concatenate(
                    [half[1 - j % 2][j // 2] for half in (grad_w_first, grad_w_up, grad_w_down)], 1
                )
                for j in range(shards)
            ]
        ).astype(jnp.float32)
        mine = lax.psum_scatter(every, "tensor", scatter_dimension=0, tiled=True)[0]
        blocks = mine.reshape(PARTS, D // PARTS, -1)
        blocks = jnp.stack([blocks[(p % 2) * 4 + p // 2] for p in range(PARTS)])
        tile_grad = tiles_from_slabs(blocks, shards, block_size)
        slot_grad = tile_grad.reshape(tile_total, block_size, block_size)[owner]
        owned_grads = lax.psum_scatter(slot_grad, "dp", scatter_dimension=0, tiled=True)

    bias_first = 1.0 - DECAY_FIRST**ADAM_STEP
    bias_second = 1.0 - DECAY_SECOND**ADAM_STEP
    step_slots = max(k for k in (1, 2, 3, 4, 6, 12) if slots % k == 0)
    slots_spec = pl.BlockSpec((step_slots, block_size, block_size), lambda i: (i, 0, 0))
    slot_out = ((slots, block_size, block_size), f32, slots_spec, "far")
    new_master, new_first, new_second = call_rows(
        adam_kernel,
        slots // step_slots,
        [(own_flip.astype(jnp.int32).reshape(slots), pl.BlockSpec(memory_space=pltpu.SMEM))]
        + [
            (array, slots_spec, "far")
            for array in (
                owned_grads,
                master[0],
                left_basis[0],
                right_basis[0],
                first_moment[0],
                second_moment[0],
            )
        ],
        [slot_out] * 3,
        22 * slots * block_size**3,
        slots * block_size**2,
    )
    if not direct:
        vector_rows = lax.psum(vector_rows, ("dp", "tensor"))
    vector_grad = vector_rows[: vectors.shape[0] // D].reshape(-1)
    new_vector_first = DECAY_FIRST * vector_first + (1.0 - DECAY_FIRST) * vector_grad
    new_vector_second = (
        DECAY_SECOND * vector_second + (1.0 - DECAY_SECOND) * vector_grad * vector_grad
    )
    new_vectors = vectors - VECTOR_RATE * (new_vector_first / bias_first) / (
        jnp.sqrt(new_vector_second / bias_second) + ADAM_EPS
    )
    return (
        layer_out,
        input_grad,
        new_master[None],
        new_first[None],
        new_second[None],
        new_vectors,
        new_vector_first,
        new_vector_second,
    )


def solution(mesh):
    return jax.shard_map(
        local,
        mesh=mesh,
        in_specs=(
            P(("dp", "tensor"), None),
            P("dp", None),
            P(("dp", "tensor"), None),
            P(),
            P("tensor", "dp", None, None),
            P("tensor", "dp", None, None),
            P("tensor", "dp", None, None),
            P("tensor", "dp", None, None),
            P("tensor", "dp", None, None),
            P(),
            P(),
            P(),
        ),
        out_specs=(
            P(("dp", "tensor"), None),
            P(("dp", "tensor"), None),
            P("tensor", "dp", None, None),
            P("tensor", "dp", None, None),
            P("tensor", "dp", None, None),
            P(),
            P(),
            P(),
        ),
        check_vma=False,
    )
```

```python
import functools
import math

import jax
import jax.numpy as jnp
from jax import lax
from jax.experimental import pallas as pl
from jax.experimental.pallas import tpu as pltpu
from jax.sharding import PartitionSpec as P

HEADS = 12
HEAD_DIM = 64
D = 768
FF = 3072
ADAM_STEP = 3


NORM_EPS = 1e-12
ADAM_EPS = 1e-08
MATRIX_RATE = 0.01
VECTOR_RATE = 0.1
DECAY_FIRST = 0.5
DECAY_SECOND = 0.5
MASKED = -1e30


def product(left_side, right_side):
    return jnp.dot(left_side, right_side, preferred_element_type=jnp.float32)


def times_transposed(left_side, right_side):
    return lax.dot_general(
        left_side, right_side, (((1,), (1,)), ((), ())), preferred_element_type=jnp.float32
    )


def transposed_times(left_side, right_side):
    return lax.dot_general(
        left_side, right_side, (((0,), (0,)), ((), ())), preferred_element_type=jnp.float32
    )


VMEM_LIMIT = 16 * 1024 * 1024

PARTS = 8
SUB = 12


def part_of_block(block):
    return (block % 4) * 2 + block // 4


def feature_order(rank):
    place = lax.iota(jnp.int32, D)
    part = part_of_block(place // (D // PARTS)) ^ rank
    inner = place % (D // PARTS)
    return (inner // SUB) * (PARTS * SUB) + part * SUB + inner % SUB


def tile_counts(shards, block_size):
    rows = D // block_size
    qkv = rows * (3 * D // shards // block_size)
    out = rows * (D // shards // block_size)
    up = rows * (FF // shards // block_size)
    return (qkv, out, up)


def slabs_from_tiles(tiles, shards, block_size):
    cut = tiles.shape[1]
    qkv, out, up = tile_counts(shards, block_size)
    rows = D // block_size

    def by_rows(part):
        cols = part.shape[0] // rows
        part = part.reshape(rows, cols, cut, SUB, block_size)
        return part.transpose(2, 0, 3, 1, 4).reshape(cut, rows * SUB, cols * block_size)

    def by_cols(part):
        cols = part.shape[0] // rows
        part = part.reshape(cols, rows, cut, SUB, block_size)
        return part.transpose(2, 1, 3, 0, 4).reshape(cut, rows * SUB, cols * block_size)

    return jnp.concatenate(
        [
            by_rows(tiles[:qkv]),
            by_cols(tiles[qkv : qkv + out]),
            by_rows(tiles[qkv + out : qkv + out + up]),
            by_cols(tiles[qkv + out + up :]),
        ],
        2,
    )


def tiles_from_slabs(slabs, shards, block_size):
    cut = slabs.shape[0]
    rows = D // block_size
    width_qkv, width_out, width_up = 3 * D // shards, D // shards, FF // shards

    def by_rows(part):
        cols = part.shape[2] // block_size
        part = part.reshape(cut, rows, SUB, cols, block_size)
        return part.transpose(1, 3, 0, 2, 4).reshape(rows * cols, cut, SUB, block_size)

    def by_cols(part):
        cols = part.shape[2] // block_size
        part = part.reshape(cut, rows, SUB, cols, block_size)
        return part.transpose(3, 1, 0, 2, 4).reshape(rows * cols, cut, SUB, block_size)

    first = width_qkv + width_out
    second = first + width_up
    return jnp.concatenate(
        [
            by_rows(slabs[:, :, :width_qkv]),
            by_cols(slabs[:, :, width_qkv:first]),
            by_rows(slabs[:, :, first:second]),
            by_cols(slabs[:, :, second:]),
        ],
        0,
    )


def swap_over(values, over_dp, over_tensor):
    dp, tensor = lax.axis_size("dp"), lax.axis_size("tensor")
    pairs = [
        (a * tensor + b, (a ^ over_dp) * tensor + (b ^ over_tensor))
        for a in range(dp)
        for b in range(tensor)
    ]
    return lax.ppermute(values, ("dp", "tensor"), pairs)


def merge(terms, outs, segments):
    chunk = D // PARTS

    def kernel(*refs):
        for out, row, col, rows, cols, parts in segments:

            def step(k, carry, out=out, row=row, col=col, cols=cols, parts=parts):
                pieces = [
                    refs[term][pl.ds(pl.multiple_of(at + k * chunk, 32), chunk), left : left + cols]
                    for term, at, left in parts
                ]
                if len(pieces) > 1:
                    value = sum(piece.astype(jnp.float32) for piece in pieces)
                else:
                    value = pieces[0]
                to = refs[len(terms) + out]
                to[pl.ds(pl.multiple_of(row + k * chunk, 32), chunk), col : col + cols] = (
                    value.astype(to.dtype)
                )
                return carry

            lax.fori_loop(0, rows // chunk, step, 0)

    spec = pl.BlockSpec(memory_space=pltpu.VMEM)
    size = sum(term.size for term in terms)
    return pl.pallas_call(
        kernel,
        in_specs=[spec] * len(terms),
        out_specs=[spec] * len(outs),
        out_shape=[jax.ShapeDtypeStruct((rows, cols), dtype) for rows, cols, dtype in outs],
        compiler_params=pltpu.CompilerParams(vmem_limit_bytes=VMEM_LIMIT),
        cost_estimate=pl.CostEstimate(flops=size, bytes_accessed=4 * size, transcendentals=0),
    )(*terms)


def from_z(block):
    return [swap_over(block, 2 * k, 0) for k in (1, 2, 3)]


def over_core(blocks):
    return blocks + [swap_over(block, 0, 1) for block in blocks]


def put(out_ref, lead, row, col, ref, at, left, rows, cols):
    chunk = min(rows, D // 2)

    def step(k, carry):
        to = pl.multiple_of(row + k * chunk, 32)
        source = pl.multiple_of(at + k * chunk, 32)
        out_ref[lead, pl.ds(to, chunk), col : col + cols] = ref[
            pl.ds(source, chunk), left : left + cols
        ]
        return carry

    lax.fori_loop(0, rows // chunk, step, 0)


def place_first(refs, out_ref):
    count = len(refs) // 2
    half, width = D // 2, D // 4
    for core in range(2):
        near, beside, across = refs[core * count : (core + 1) * count]
        for y in range(2):
            col = (2 * y + core) * width
            for kind in range(2):
                left = kind * width
                put(out_ref, kind, 0, col, near, y * half, left, half, width)
                put(out_ref, kind, half, col, beside, y * half, left, half, width)
                if y:
                    put(out_ref, 2 + kind, 0, col, across, 0, left, D, width)
                else:
                    put(out_ref, 2 + kind, 0, col, near, 0, half + left, D, width)


def edges_moves():
    rows, half = D // PARTS, D // 2
    moves = []
    for core in range(2):
        near, beside, across = range(3 * core, 3 * core + 3)
        for y in range(2):
            group = 2 * y + core
            for z in range(4):
                for x in range(2):
                    to, by_y, by_x = x * half + z * rows, (2 * z + y) * rows, (2 * z + x) * rows
                    moves.append((group, to, 0, beside if x else near, by_y, 0, rows, half))
                    source = (across, by_x, 0) if y else (near, by_x, half)
                    moves.append((group, to, half, *source, rows, half))
    return moves


def plane_moves():
    half = D // 2
    return [
        (2 * y + core, x * half, 0, 4 * core + 2 * y + x, 0, 0, half, D)
        for core in range(2)
        for y in range(2)
        for x in range(2)
    ]


def groups_moves(count):
    return [(group, 0, 0, group, 0, 0, D, D) for group in range(count)]


def move_all(moves, refs, out_ref, sems):
    copies = [
        pltpu.make_async_copy(
            refs[ref].at[pl.ds(at, rows), pl.ds(left, cols)],
            out_ref.at[lead, pl.ds(row, rows), pl.ds(col, cols)],
            sems.at[k],
        )
        for k, (lead, row, col, ref, at, left, rows, cols) in enumerate(moves)
    ]
    for copy in copies:
        copy.start()
    for copy in copies:
        copy.wait()


def place_kinds(refs, out_ref):
    width = D // len(refs)
    for group, ref in enumerate(refs):
        for kind in range(4):
            put(out_ref, kind, 0, group * width, ref, 0, kind * width, D, width)


def core_terms(halves):
    odd, even = halves
    return [even.reshape(2 * D, D), swap_over(odd, 0, 1).reshape(2 * D, D)]


def summed(count, row, col):
    return [(term, row, col) for term in range(count)]


def reduce_core_plane(halves):
    half = D // 2
    return merge(
        core_terms(halves),
        [(half, D, jnp.bfloat16)] * 4,
        [(k, 0, 0, half, D, summed(2, k * half, 0)) for k in range(4)],
    )


def reduce_plane(near, beside, across, opposite):
    pair = D // 4
    terms = [near, swap_over(beside, 1, 0), swap_over(across, 0, 2), swap_over(opposite, 1, 2)]
    return merge(
        terms,
        [(pair, D, jnp.bfloat16)] * 2,
        [(k, 0, 0, pair, D, summed(4, k * pair, 0)) for k in range(2)],
    )


def halve_z(near, received):
    rows = near.shape[0] // 2
    return merge(
        [near, received],
        [(rows, D, jnp.bfloat16)] * 2,
        [(k, 0, 0, rows, D, summed(2, k * rows, 0)) for k in range(2)],
    )


def add_z(near, received):
    rows = near.shape[0]
    return merge(
        [near, received], [(rows, D, jnp.float32)], [(0, 0, 0, rows, D, summed(2, 0, 0))]
    )[0]


def z_terms(own, *sent):
    return [own] + [swap_over(block, 2 * (k + 1), 0) for k, block in enumerate(sent)]


def reduce_z(terms):
    rows = D // PARTS
    return merge(terms, [(rows, D, jnp.float32)], [(0, 0, 0, rows, D, summed(4, 0, 0))])[0]


def reduce_core_edges(halves):
    half = D // 2
    return merge(
        core_terms(halves),
        [(D, D, jnp.bfloat16), (D, half, jnp.bfloat16), (D, half, jnp.bfloat16)],
        [
            (0, 0, 0, half, half, summed(2, 0, 0)),
            (0, half, 0, half, half, summed(2, D, 0)),
            (0, 0, half, D, half, summed(2, 0, half)),
            (1, 0, 0, half, half, summed(2, half, 0)),
            (1, half, 0, half, half, summed(2, D + half, 0)),
            (2, 0, 0, D, half, summed(2, D, half)),
        ],
    )


def edge_terms(near, left, right):
    return [near, swap_over(left, 1, 0), swap_over(right, 0, 2)]


def edge_sums(row):
    half = D // 2
    return ((0, [(0, row, 0), (1, row, 0)]), (half, [(0, row, half), (2, row, 0)]))


def plane_edge_terms(near, left, right):
    return [near, swap_over(left, 0, 2), swap_over(right, 1, 0)]


def reduce_edges_plane(terms):
    half = D // 2
    kept = [(0, 0, col, half, half, parts) for col, parts in edge_sums(0)]
    sent = [
        (1 + k, 0, 0, half, half, parts) for k, (_, parts) in enumerate(edge_sums(half))
    ]
    return merge(
        terms,
        [(half, D, jnp.bfloat16), (half, half, jnp.bfloat16), (half, half, jnp.bfloat16)],
        kept + sent,
    )


def reduce_plane_edges(terms):
    rows, half = D // PARTS, D // 2
    return merge(
        terms,
        [(rows, D, jnp.bfloat16)] * 4,
        [
            (k, 0, col, rows, half, parts)
            for k in range(4)
            for col, parts in edge_sums(k * rows)
        ],
    )


def reduce_edges(terms):
    rows, half = D // PARTS, D // 2
    return merge(
        terms,
        [(half, D, jnp.bfloat16)] * 2,
        [
            (k // 2, (2 * (k % 2) + q) * rows, col, rows, half, parts)
            for k in range(4)
            for q in range(2)
            for col, parts in edge_sums(q * half + k * rows)
        ],
    )


def reduce_edges_z(terms):
    rows, half = D // PARTS, D // 2
    return merge(
        terms,
        [(rows, D, jnp.bfloat16), (rows, half, jnp.bfloat16), (rows, half, jnp.bfloat16)],
        [
            (0, 0, 0, rows, D, summed(2, 0, 0)),
            (1, 0, 0, rows, half, summed(2, rows, 0)),
            (2, 0, 0, rows, half, summed(2, rows, half)),
        ],
    )


def reduce_edges_last(terms):
    rows, half = D // PARTS, D // 2
    return merge(
        terms,
        [(rows, D, jnp.float32)],
        [(0, 0, col, rows, half, parts) for col, parts in edge_sums(0)],
    )[0]


def add_swapped(values, over_dp, over_tensor):
    return values + swap_over(values, over_dp, over_tensor)


ROWS = 256


def dot_nt(left_side, right_side):
    return lax.dot_general(
        left_side, right_side, (((1,), (1,)), ((), ())), preferred_element_type=jnp.float32
    )


def row_block(array):
    return pl.BlockSpec((ROWS, array.shape[1]), lambda i: (i, 0))


def call_rows(kernel, steps, inputs, outputs, flops, transcendentals=0, scratch=()):
    arrays = [
        pltpu.with_memory_space_constraint(array, pltpu.HBM) if far else array
        for array, _, *far in inputs
    ]
    shapes = [jax.ShapeDtypeStruct(shape, dtype) for shape, dtype, *_ in outputs]
    moved = sum(a.size * a.dtype.itemsize for a in arrays + shapes)
    shapes = [
        pltpu.HBM(shape.shape, shape.dtype) if len(output) > 3 else shape
        for shape, output in zip(shapes, outputs)
    ]
    return pl.pallas_call(
        kernel,
        grid=(steps,),
        in_specs=[spec for _, spec, *_ in inputs],
        out_specs=[output[2] for output in outputs],
        out_shape=shapes,
        scratch_shapes=scratch,
        compiler_params=pltpu.CompilerParams(vmem_limit_bytes=VMEM_LIMIT),
        cost_estimate=pl.CostEstimate(
            flops=int(1.0 * flops), bytes_accessed=moved, transcendentals=transcendentals
        ),
    )(*arrays)


def norm_rows(summed):
    centred = summed - jnp.mean(summed, -1, keepdims=True)
    inverse = lax.rsqrt(jnp.mean(centred * centred, -1, keepdims=True) + NORM_EPS)
    return centred * inverse, inverse


def norm_pull(gradient, unit_rows, inverse, gain_row):
    scaled = gradient * gain_row
    return inverse * (
        scaled
        - jnp.mean(scaled, -1, keepdims=True)
        - unit_rows * jnp.mean(scaled * unit_rows, -1, keepdims=True)
    )


def add_rows(ref, rows):
    sums = [jnp.sum(row, 0, keepdims=True) for row in rows]
    start = pl.program_id(0) == 0
    for place, total in enumerate(sums):
        kept = jnp.where(start, 0.0, ref[place : place + 1, :])
        ref[place : place + 1, :] = kept + total


def settle(moves, refs, whole_ref, sems):
    @pl.when(pl.program_id(0) == 0)
    def _():
        move_all(moves, refs, whole_ref, sems)

    return [whole_ref.at[j] for j in range(whole_ref.shape[0])]


def pair_masks(length):
    wide = 2 * HEAD_DIM
    lower = lax.broadcasted_iota(jnp.int32, (length, wide), 1) < HEAD_DIM
    top = lax.broadcasted_iota(jnp.int32, (2 * length, wide), 0) < length
    left = lax.broadcasted_iota(jnp.int32, (2 * length, wide), 1) < HEAD_DIM
    return lower, top == left


def stacked(pair, own):
    return jnp.where(own, jnp.concatenate([pair, pair], 0), jnp.zeros((), pair.dtype))


def attention_kernel(place, total_count, length, *refs):
    rows_ref, across_ref, down_ref, bias_ref, vec_ref = refs[:5]
    outs = refs[5 + total_count : 12 + total_count]
    packed_ref, probs_ref, attended_ref, unit_ref, inverse_ref, low_ref, whole_ref = outs
    scores_ref, sems, *raw = refs[12 + total_count :]

    @pl.when(pl.program_id(0) == 0)
    def _():
        copies = [
            pltpu.make_async_copy(source, to, sems.at[k])
            for k, (source, to) in enumerate(zip(refs[5 : 5 + total_count], raw))
        ]
        for copy in copies:
            copy.start()
        for copy in copies:
            copy.wait()
        place(raw, whole_ref)

    weights = [whole_ref.at[kind] for kind in range(4)]
    wide = 2 * HEAD_DIM
    pairs = HEADS // 2
    rows = rows_ref[...]
    for kind in range(3):
        part = product(rows, weights[kind][...]) + bias_ref[kind : kind + 1, :]
        part = part.astype(jnp.bfloat16)
        if kind == 0:
            part = part * jnp.bfloat16(HEAD_DIM ** (-0.5))
        packed_ref[:, kind * D : (kind + 1) * D] = part
    _, own = pair_masks(length)
    steps = [(p, i) for p in range(ROWS // length) for i in range(pairs)]

    def pair_of(p, i, kind):
        span = slice(p * length, (p + 1) * length)
        return packed_ref[span, kind * D + i * wide : kind * D + (i + 1) * wide]

    for at, (p, i) in enumerate(steps):
        scores_ref[at] = dot_nt(pair_of(p, i, 0), stacked(pair_of(p, i, 1), own))
    for at, (p, i) in enumerate(steps):
        allowed = down_ref[p] == across_ref[p]
        for half in range(2):
            lanes = slice(half * length, (half + 1) * length)
            scores = jnp.where(allowed, scores_ref[at, :, lanes], MASKED)
            raised = jnp.exp(scores - jnp.max(scores, -1, keepdims=True))
            probs_ref[p, i, :, lanes] = (
                raised * (1.0 / jnp.sum(raised, -1, keepdims=True))
            ).astype(jnp.bfloat16)
    for p, i in steps:
        mixed = product(probs_ref[p, i], stacked(pair_of(p, i, 2), own))
        attended_ref[p * length : (p + 1) * length, i * wide : (i + 1) * wide] = mixed.astype(
            jnp.bfloat16
        )
    summed = rows.astype(jnp.float32) + vec_ref[0:1, :]
    summed = summed + dot_nt(attended_ref[...], weights[3][...])
    unit, inverse = norm_rows(summed)
    unit_ref[...] = unit
    inverse_ref[...] = inverse
    low_ref[...] = (unit * vec_ref[1:2, :] + vec_ref[2:3, :]).astype(jnp.bfloat16)


def gelu_parts(values):
    size = jnp.abs(values)
    decay = jnp.exp2(values * values * (-0.5 / math.log(2.0)))
    t = 1.0 / (1.0 + size * (0.3275911 * 0.5**0.5))
    poly = t * (
        0.127414796
        + t * (-0.142248368 + t * (0.7107068705 + t * (-0.7265760135 + t * 0.5307027145)))
    )
    result = jnp.maximum(values, 0.0) - size * (poly * decay)
    rest = decay * (poly - size * (0.5 / math.pi) ** 0.5)
    return result, jnp.where(values > 0, 1.0 - rest, rest)


def up_kernel(place, shards, *refs):
    low_ref, bias_ref = refs[:2]
    act_ref, slope_ref, whole_ref, sems = refs[-4:]
    weights = settle(place, refs[2:-4], whole_ref, sems)
    width = weights[0].shape[1]
    chunk = 256
    low = low_ref[...]
    for j in range(shards):
        for c in range(0, width, chunk):
            pre = product(low, weights[j][:, c : c + chunk]) + bias_ref[j : j + 1, c : c + chunk]
            result, slope = gelu_parts(pre)
            at = j * width + c
            act_ref[:, at : at + chunk] = result.astype(jnp.bfloat16)
            slope_ref[:, at : at + chunk] = slope.astype(jnp.bfloat16)


def down_kernel(place, shards, *refs):
    act_ref, unit_ref, grad_ref, vec_ref = refs[:4]
    out_ref, dz_ref, low_ref, sums_ref, whole_ref, sems = refs[-6:]
    weights = settle(place, refs[4:-6], whole_ref, sems)
    width = weights[0].shape[1]
    summed = unit_ref[...] * vec_ref[1:2, :] + vec_ref[2:3, :] + vec_ref[3:4, :]
    for j in range(shards):
        summed = summed + dot_nt(act_ref[:, j * width : (j + 1) * width], weights[j][...])
    unit, inverse = norm_rows(summed)
    gain = vec_ref[4:5, :]
    out_ref[...] = unit * gain + vec_ref[5:6, :]
    gradient = grad_ref[...]
    dz = norm_pull(gradient, unit, inverse, gain)
    dz_ref[...] = dz
    low_ref[...] = dz.astype(jnp.bfloat16)
    add_rows(sums_ref, (gradient * unit, gradient, dz))


def hidden_back_kernel(shards, *refs):
    low_ref, slope_ref, whole_ref, dpre_ref, bias_sums_ref = refs
    width = whole_ref.shape[2]
    low = low_ref[...]
    for j in range(shards):
        span = slice(j * width, (j + 1) * width)
        dpre = product(low, whole_ref[j]) * slope_ref[:, span].astype(jnp.float32)
        dpre = dpre.astype(jnp.bfloat16)
        dpre_ref[:, span] = dpre
        total = jnp.sum(dpre.astype(jnp.float32), 0, keepdims=True)
        kept = jnp.where(pl.program_id(0) == 0, 0.0, bias_sums_ref[j : j + 1, :])
        bias_sums_ref[j : j + 1, :] = kept + total


def back_kernel(shards, *refs):
    dpre_ref, dz_ref, unit_ref, inverse_ref, vec_ref, up_ref, first_ref = refs[:7]
    dz1_ref, low1_ref, datt_ref, sums_ref = refs[7:]
    width = up_ref.shape[2]
    gradient = dz_ref[...]
    for j in range(shards):
        gradient = gradient + dot_nt(dpre_ref[:, j * width : (j + 1) * width], up_ref[j])
    unit = unit_ref[...]
    dz1 = norm_pull(gradient, unit, inverse_ref[...], vec_ref[1:2, :])
    dz1_ref[...] = dz1
    low1 = dz1.astype(jnp.bfloat16)
    low1_ref[...] = low1
    add_rows(sums_ref, (gradient * unit, gradient, dz1))
    datt_ref[...] = product(low1, first_ref[3]).astype(jnp.bfloat16)


def attention_back_kernel(length, *refs):
    datt_ref, attended_ref, packed_ref, probs_ref, dpacked_ref, sums_ref, up_ref, grad_ref = refs
    wide = 2 * HEAD_DIM
    lower, own = pair_masks(length)
    ones = own.astype(jnp.bfloat16)
    steps = [(p, i) for p in range(ROWS // length) for i in range(HEADS // 2)]

    def pair_of(p, i, kind):
        span = slice(p * length, (p + 1) * length)
        return packed_ref[span, kind * D + i * wide : kind * D + (i + 1) * wide]

    def keep(p, i, kind, grad):
        span = slice(p * length, (p + 1) * length)
        dpacked_ref[span, kind * D + i * wide : kind * D + (i + 1) * wide] = grad.astype(
            jnp.bfloat16
        )

    for place, (p, i) in enumerate(steps):
        span = slice(p * length, (p + 1) * length)
        lanes = slice(i * wide, (i + 1) * wide)
        upstream = datt_ref[span, lanes]
        up_ref[place, :, :wide] = upstream
        up_ref[place, :, wide:] = (
            upstream.astype(jnp.float32) * attended_ref[span, lanes].astype(jnp.float32)
        ).astype(jnp.bfloat16)
    for place, (p, i) in enumerate(steps):
        centred = dot_nt(
            up_ref[place], jnp.concatenate([stacked(pair_of(p, i, 2), own), -ones], 1)
        )
        grad_ref[place] = (probs_ref[p, i].astype(jnp.float32) * centred).astype(jnp.bfloat16)
    for place, (p, i) in enumerate(steps):
        grad_scores = grad_ref[place]
        keep(
            p, i, 0,
            product(grad_scores, stacked(pair_of(p, i, 1), own)) * HEAD_DIM ** (-0.5),
        )
        both = transposed_times(grad_scores, pair_of(p, i, 0))
        keep(p, i, 1, jnp.where(lower, both[:length], both[length:]))
        both = transposed_times(probs_ref[p, i], up_ref[place, :, :wide])
        keep(p, i, 2, jnp.where(lower, both[:length], both[length:]))
    total = jnp.sum(dpacked_ref[...].astype(jnp.float32), 0, keepdims=True)
    kept = jnp.where(pl.program_id(0) == 0, 0.0, sums_ref[0:1, :])
    sums_ref[0:1, :] = kept + total


def weight_kernel(odd, count, *refs):
    lefts = refs[: 2 if count > 1 else 1]
    rights, out_ref = refs[len(lefts) : -1], refs[-1]
    if count == 1:
        out_ref[0] = transposed_times(lefts[0][...], rights[0][...]).astype(jnp.bfloat16)
    else:
        half = rights[0].shape[1] // 2
        span = slice(half, 2 * half) if odd else slice(0, half)
        values = jnp.concatenate([right[:, span] for right in rights[:-1]], 1)
        width = values.shape[1]
        out_ref[0, :, :width] = transposed_times(lefts[0][...], values).astype(jnp.bfloat16)
        out_ref[0, :, width:] = transposed_times(lefts[1][...], rights[-1][:, span]).astype(
            jnp.bfloat16
        )


def weight_half(odd, lefts, rights):
    count = len(rights)
    single = count == 1
    specs = []
    for array, width, before in rights:
        if single:
            specs.append(pl.BlockSpec((array.shape[0], width), lambda i: (0, 2 * i + odd)))
        else:
            specs.append(pl.BlockSpec((array.shape[0], 2 * width), lambda i, b=before: (0, b + i)))
    arrays = [*lefts, *[array for array, _, _ in rights]]
    tokens = lefts[0].shape[0]
    (half,) = pl.pallas_call(
        functools.partial(weight_kernel, odd, count),
        grid=(2,),
        in_specs=[pl.BlockSpec(memory_space=pltpu.VMEM) for _ in lefts] + specs,
        out_specs=[pl.BlockSpec((1, D, D), lambda i: (i, 0, 0))],
        out_shape=[jax.ShapeDtypeStruct((2, D, D), jnp.bfloat16)],
        compiler_params=pltpu.CompilerParams(vmem_limit_bytes=VMEM_LIMIT),
        cost_estimate=pl.CostEstimate(
            flops=4 * tokens * D * D,
            bytes_accessed=sum(2 * array.size for array in arrays),
            transcendentals=0,
        ),
    )(*arrays)
    return half


def weight_halves(lefts, rights):
    return [weight_half(odd, lefts, rights) for odd in (1, 0)]


def two_terms(values):
    top = values.astype(jnp.bfloat16)
    return top, (values - top.astype(jnp.float32)).astype(jnp.bfloat16)


def adam_kernel(*refs):
    flip_ref, grad_ref, master_ref, left_ref, right_ref, first_ref, second_ref = refs[:7]
    master_out, first_out, second_out = refs[7:]
    bias_first = 1.0 - DECAY_FIRST**ADAM_STEP
    bias_second = 1.0 - DECAY_SECOND**ADAM_STEP
    count = grad_ref.shape[0]
    lefts = [two_terms(left_ref[k]) for k in range(count)]
    rights = [two_terms(right_ref[k]) for k in range(count)]
    turned = []
    for k in range(count):
        tile = grad_ref[k].astype(jnp.float32)
        flip = flip_ref[pl.program_id(0) * count + k] > 0
        tile = jnp.where(flip, tile.T, tile)
        top, rest = two_terms(tile)
        grad = product(top, rights[k][0]) + product(top, rights[k][1])
        if grad_ref.dtype != jnp.bfloat16:
            grad = grad + product(rest, rights[k][0])
        turned.append(grad)
    directions = []
    for k in range(count):
        top, rest = two_terms(turned[k])
        rotated = (
            transposed_times(lefts[k][0], top)
            + transposed_times(lefts[k][0], rest)
            + transposed_times(lefts[k][1], top)
        )
        first = DECAY_FIRST * first_ref[k] + (1.0 - DECAY_FIRST) * rotated
        second = DECAY_SECOND * second_ref[k] + (1.0 - DECAY_SECOND) * rotated * rotated
        first_out[k] = first
        second_out[k] = second
        directions.append(first / bias_first / (jnp.sqrt(second / bias_second) + ADAM_EPS))
    backs = [
        product(lefts[k][0], directions[k].astype(jnp.bfloat16)).astype(jnp.bfloat16)
        for k in range(count)
    ]
    for k in range(count):
        update = times_transposed(backs[k], rights[k][0])
        master_out[k] = master_ref[k] - MATRIX_RATE * update


def unpermuted(values, selector_ref):
    top, rest = two_terms(values)
    return dot_nt(top, selector_ref[...]) + dot_nt(rest, selector_ref[...])


def enter_kernel(tokens_ref, grad_ref, vectors_ref, selector_ref, rows_ref, out_ref, d_rows_ref):
    selector = selector_ref[...]
    rows_ref[...] = product(tokens_ref[...], selector).astype(jnp.bfloat16)
    top, rest = two_terms(grad_ref[...])
    out_ref[...] = product(top, selector) + product(rest, selector)

    @pl.when(pl.program_id(0) == 0)
    def _():
        rows = vectors_ref[...]
        permuted = jnp.zeros(rows.shape, jnp.float32)
        for _ in range(3):
            term = rows.astype(jnp.bfloat16)
            rows = rows - term.astype(jnp.float32)
            permuted = permuted + product(term, selector)
        d_rows_ref[...] = permuted


def layer_kernel(out_ref, selector_ref, layer_ref):
    layer_ref[...] = unpermuted(out_ref[...], selector_ref)


def input_kernel(dz1_ref, dpacked_ref, selector_ref, whole_ref, input_ref):
    gradient = dz1_ref[...]
    for kind in range(3):
        gradient = gradient + dot_nt(dpacked_ref[:, kind * D : (kind + 1) * D], whole_ref[kind])
    input_ref[...] = unpermuted(gradient, selector_ref)


def vector_kernel(shards, *refs):
    base_ref, first_ref, second_ref, hidden_ref, columns_ref, selector_ref, out_ref = refs
    base = base_ref[0]
    rows = jnp.concatenate(
        [
            first_ref[0:1, :],
            second_ref[0:1, :],
            first_ref[2:3, :],
            second_ref[2:3, :],
            first_ref[1:2, :],
            second_ref[1:2, :],
            jnp.zeros((2, D), jnp.float32),
        ],
        0,
    )
    natural = jnp.zeros((8, D), jnp.float32)
    for _ in range(3):
        term = rows.astype(jnp.bfloat16)
        rows = rows - term.astype(jnp.float32)
        natural = natural + dot_nt(term, selector_ref[...])
    hidden = FF // D
    out_ref[...] = jnp.zeros(out_ref.shape, jnp.float32)
    for at, row in ((0, 0), (1, 1), (4, 2), (5 + hidden, 3), (6 + hidden, 4), (7 + hidden, 5)):
        out_ref[at : at + 1, :] = natural[row : row + 1, :]
    width = D // shards
    for j in range(shards):
        out_ref[5 + j : 6 + j, :] = hidden_ref[pl.ds(j ^ base, 1), :]
        for at, kind in ((2, 0), (3, 2)):
            parts = [
                jnp.where(
                    (j ^ base) == k,
                    columns_ref[0:1, kind * D + k * width : kind * D + (k + 1) * width],
                    0.0,
                )
                for k in range(shards)
            ]
            out_ref[at : at + 1, j * width : (j + 1) * width] = sum(parts)


def together(*values):
    return lax.optimization_barrier(values)


def local(
    tokens,
    segments,
    out_grad,
    owner,
    master,
    left_basis,
    right_basis,
    first_moment,
    second_moment,
    vectors,
    vector_first,
    vector_second,
):
    shards = lax.axis_size("tensor")
    dp_size = lax.axis_size("dp")
    direct = dp_size == PARTS and shards == 4
    tensor_rank = lax.axis_index("tensor")
    dp_rank = lax.axis_index("dp")
    local_heads = HEADS // shards
    head_width = local_heads * HEAD_DIM
    up_width = FF // shards
    width_qkv = 3 * head_width
    block_size = master.shape[-1]
    slots = master.shape[1]
    row_count = tokens.shape[0]
    length = segments.shape[1]
    pack_count = row_count // length
    own_segments = lax.dynamic_slice_in_dim(segments, tensor_rank * pack_count, pack_count, 0)
    qkv_tiles, out_tiles, up_tiles = tile_counts(shards, block_size)
    tile_total = owner.shape[0]

    group_base = tensor_rank if direct else 0
    order = feature_order(dp_rank if direct else 0)
    selector = (lax.iota(jnp.int32, D)[:, None] == order[None, :]).astype(jnp.bfloat16)

    steps = row_count // ROWS
    f32, bf16 = jnp.float32, jnp.bfloat16
    rows_spec = lambda width: pl.BlockSpec((ROWS, width), lambda i: (i, 0))
    full = lambda array: (array, pl.BlockSpec(memory_space=pltpu.VMEM))
    raw = lambda array: (array, pl.BlockSpec(memory_space=pl.ANY))
    by_rows = lambda array: (array, row_block(array))
    far_rows = lambda array: (array, row_block(array), "far")
    group_order = lax.iota(jnp.int32, shards) ^ group_base
    below = vectors[: 5 * D].reshape(5, D)
    above = vectors[5 * D + FF :].reshape(3, D)
    d_rows = jnp.stack(
        [below[4], below[0], above[1], above[0], below[1], above[2], below[0], below[0]]
    )
    bias_q = below[2].reshape(shards, head_width)[group_order]
    bias_v = below[3].reshape(shards, head_width)[group_order]
    bias_up = vectors[5 * D : 5 * D + FF].reshape(shards, up_width)[group_order]
    rows_in, grad_out, d_rows = call_rows(
        enter_kernel,
        steps,
        [far_rows(tokens), far_rows(out_grad), full(d_rows), full(selector)],
        [
            ((row_count, D), bf16, rows_spec(D), "far"),
            ((row_count, D), f32, rows_spec(D), "far"),
            ((8, D), f32, pl.BlockSpec(memory_space=pltpu.VMEM)),
        ],
        6 * row_count * D * D,
    )

    def flipped(index):
        from_out = (index >= qkv_tiles) & (index < qkv_tiles + out_tiles)
        return (from_out | (index >= qkv_tiles + out_tiles + up_tiles))[:, None, None]

    own_tiles = lax.dynamic_slice_in_dim(owner, dp_rank * slots, slots, 0)
    own_flip = flipped(own_tiles)
    sent = master[0].astype(jnp.bfloat16)
    sent = jnp.where(own_flip, jnp.swapaxes(sent, 1, 2), sent)
    placing = (lax.iota(jnp.int32, tile_total)[:, None] == owner[None, :]).astype(jnp.bfloat16)
    if direct:
        parts = sent.reshape(slots, PARTS, SUB * block_size).swapaxes(0, 1)
        parts = lax.all_to_all(parts, "dp", 0, 0, tiled=True).reshape(tile_total, -1)
        tiles = product(placing, parts).astype(jnp.bfloat16)
        slab = slabs_from_tiles(tiles.reshape(tile_total, 1, SUB, block_size), shards, block_size)[0]
        half, rows = D // 2, D // PARTS
        first_slab, up_slab, down_slab = (slab[:, k * D : (k + 1) * D] for k in range(3))
        near_left, near_right = down_slab[:, :half], down_slab[:, half:]
        *blocks, near_left, near_right, rows_in, grad_out, d_rows, bias_up = together(
            *from_z(first_slab),
            swap_over(near_left, 0, 2),
            swap_over(near_right, 1, 0),
            rows_in,
            grad_out,
            d_rows,
            bias_up,
        )
        left, right, down_near = merge(
            [first_slab, *blocks, down_slab, near_left, near_right],
            [(half, half, bf16), (half, half, bf16), (2 * rows, D, bf16)],
            [(k, z * rows, 0, rows, half, [(z, 0, k * half)]) for k in range(2) for z in range(4)]
            + [
                (2, 0, 0, rows, D, [(4, 0, 0)]),
                (2, rows, 0, rows, half, [(5, 0, 0)]),
                (2, rows, half, rows, half, [(6, 0, 0)]),
            ],
        )
        left, right, down_near, up_slab = together(left, right, down_near, up_slab)
        up_beside = swap_over(up_slab, 2, 0)
        (up_pair,) = merge(
            [up_slab, up_beside],
            [(2 * rows, D, bf16)],
            [(0, z * rows, 0, rows, D, [(z, 0, 0)]) for z in range(2)],
        )
        left_across, right_beside, up_pair = together(
            swap_over(left, 0, 2), swap_over(right, 1, 0), up_pair
        )
        near, left, right = merge(
            [left, left_across, right, right_beside],
            [(D, D, bf16), (D, half, bf16), (D, half, bf16)],
            [
                (out, q * half, col, half, half, [(2 * k + q, 0, 0)])
                for k in range(2)
                for q in range(2)
                for out, col in ((0, k * half), (1 + k, 0))
            ],
        )
        near, down_near = together(near, down_near)
        down_beside = swap_over(down_near, 2, 0)
        near_there, beside, across, up_far, down_beside = together(
            swap_over(near, 0, 1),
            swap_over(left, 1, 0),
            swap_over(right, 0, 2),
            swap_over(up_pair, 4, 0),
            down_beside,
        )
        up_z, down_pair = merge(
            [up_pair, up_far, down_near, down_beside],
            [(half, D, bf16)] * 2,
            [
                (k, z * 2 * rows, 0, 2 * rows, D, [(2 * k + z, 0, 0)])
                for k in range(2)
                for z in range(2)
            ],
        )
        first = [near, beside, across, near_there] + over_core([beside, across])[2:]
        up = [up_z, swap_over(up_z, 1, 0), swap_over(up_z, 0, 2), swap_over(up_z, 1, 2)]
        down_far = swap_over(down_pair, 4, 0)
        places = (place_first, plane_moves(), edges_moves())
        pieces = [first, None, None]
    else:
        gathered = lax.all_gather(sent, "dp", axis=0, tiled=True).reshape(tile_total, -1)
        tiles = product(placing, gathered).astype(jnp.bfloat16)
        slabs = slabs_from_tiles(
            tiles.reshape(tile_total, PARTS, SUB, block_size), shards, block_size
        )
        whole = jnp.concatenate([slabs[part_of_block(k)] for k in range(PARTS)], 0)
        every = lax.all_gather(whole, "tensor", axis=0)
        pieces = [
            [every[j][:, k * D : (k + 1) * D] for j in range(shards)] for k in range(3)
        ]
        places = (place_kinds, groups_moves(shards), groups_moves(shards))

    packs_step = ROWS // length
    bias_qkv = jnp.stack(
        [bias_q.reshape(D), jnp.zeros((D,), jnp.float32), bias_v.reshape(D)]
    )
    pairs = HEADS // 2
    probs_spec = pl.BlockSpec((packs_step, pairs, length, 2 * length), lambda i: (i, 0, 0, 0))
    sums_spec = lambda width: pl.BlockSpec((8, width), lambda i: (0, 0))
    square = 2 * row_count * D * D

    whole_out = ((shards, D, D), bf16, pl.BlockSpec(memory_space=pltpu.VMEM))
    packed, probs, attended, unit_first, inverse_first, normed_low, whole_first = call_rows(
        functools.partial(attention_kernel, places[0], len(pieces[0]), length),
        steps,
        [
            far_rows(rows_in),
            (own_segments[:, None, :], pl.BlockSpec((packs_step, 1, length), lambda i: (i, 0, 0))),
            (own_segments[:, :, None], pl.BlockSpec((packs_step, length, 1), lambda i: (i, 0, 0))),
            full(bias_qkv),
            full(d_rows),
            *[raw(w) + (("far",) if w.shape == (D, D) else ()) for w in pieces[0]],
        ],
        [
            ((row_count, 3 * D), bf16, rows_spec(3 * D), "far"),
            ((pack_count, pairs, length, 2 * length), bf16, probs_spec, "far"),
            ((row_count, D), bf16, rows_spec(D)),
            ((row_count, D), f32, rows_spec(D), "far"),
            ((row_count, 1), f32, rows_spec(1), "far"),
            ((row_count, D), bf16, rows_spec(D), "far"),
            whole_out,
        ],
        4 * square + 4 * row_count * length * D,
        row_count * length * HEADS,
        [
            pltpu.VMEM((packs_step * pairs, length, 2 * length), f32),
            pltpu.SemaphoreType.DMA((len(pieces[0]),)),
            *[pltpu.VMEM(w.shape, bf16) for w in pieces[0]],
        ],
    )
    if direct:
        up[0], normed_low = together(up[0], normed_low)
        *up, up_there, down_far, normed_low = together(
            *up, swap_over(up[0], 0, 1), down_far, normed_low
        )
        down_near, near_left, near_right = merge(
            [down_pair, down_far],
            [(D, D, bf16), (D, half, bf16), (D, half, bf16)],
            [(0, z * half, 0, half, D, [(z, 0, 0)]) for z in range(2)]
            + [
                (1 + k, z * half, 0, half, half, [(z, 0, k * half)])
                for k in range(2)
                for z in range(2)
            ],
        )
        down = [down_near, swap_over(near_left, 1, 0), swap_over(near_right, 0, 2)]
        pieces[1] = up + [up_there] + over_core(up[1:])[3:]
    activated, slope, whole_up = call_rows(
        functools.partial(up_kernel, places[1], shards),
        steps,
        [far_rows(normed_low), full(bias_up), *[raw(w) for w in pieces[1]]],
        [
            ((row_count, FF), bf16, rows_spec(FF)),
            ((row_count, FF), bf16, rows_spec(FF), "far"),
            whole_out,
        ],
        4 * square,
        2 * row_count * FF,
        [pltpu.SemaphoreType.DMA((len(places[1]),))],
    )
    if direct:
        *down, activated = together(*down, activated)
        pieces[2] = over_core(down)
    layer_out, grad_second, second_low, sums_second, whole_down = call_rows(
        functools.partial(down_kernel, places[2], shards),
        steps,
        [
            by_rows(activated),
            far_rows(unit_first),
            far_rows(grad_out),
            full(d_rows),
            *[raw(w) for w in pieces[2]],
        ],
        [
            ((row_count, D), f32, rows_spec(D), "far"),
            ((row_count, D), f32, rows_spec(D)),
            ((row_count, D), bf16, rows_spec(D)),
            ((8, D), f32, sums_spec(D)),
            whole_out,
        ],
        4 * square,
        0,
        [pltpu.SemaphoreType.DMA((len(places[2]),))],
    )
    grad_w_down = weight_halves([second_low], [(activated, up_width, 0)])
    if direct:
        down_parts = reduce_core_plane(grad_w_down)
        second_low, *down_parts = together(second_low, *down_parts)
        down_parts = reduce_plane(*down_parts)
    grad_pre, grad_bias_up = call_rows(
        functools.partial(hidden_back_kernel, shards),
        steps,
        [by_rows(second_low), far_rows(slope), full(whole_down)],
        [((row_count, FF), bf16, rows_spec(FF)), ((8, up_width), f32, sums_spec(up_width))],
        4 * square,
    )
    grad_w_up = weight_halves([normed_low], [(grad_pre, up_width, 0)])
    grad_first, first_low, grad_attended, sums_first = call_rows(
        functools.partial(back_kernel, shards),
        steps,
        [
            by_rows(grad_pre),
            by_rows(grad_second),
            far_rows(unit_first),
            far_rows(inverse_first),
            full(d_rows),
            full(whole_up),
            full(whole_first),
        ],
        [
            ((row_count, D), f32, rows_spec(D), "far"),
            ((row_count, D), bf16, rows_spec(D)),
            ((row_count, D), bf16, rows_spec(D)),
            ((8, D), f32, sums_spec(D)),
        ],
        20 * square,
    )
    if direct:
        up_parts = reduce_core_edges(grad_w_up)
        grad_attended, *parts = together(grad_attended, *up_parts, *down_parts)
        up_terms = edge_terms(*parts[:3])
        down_terms = [parts[3], swap_over(parts[4], 4, 0)]
    grad_packed, column_sums = call_rows(
        functools.partial(attention_back_kernel, length),
        steps,
        [by_rows(grad_attended), by_rows(attended), far_rows(packed), (probs, probs_spec, "far")],
        [
            ((row_count, 3 * D), bf16, rows_spec(3 * D)),
            ((8, 3 * D), f32, sums_spec(3 * D)),
        ],
        8 * square,
        0,
        [pltpu.VMEM((packs_step * pairs, length, 2 * length), bf16)] * 2,
    )
    rights = [(grad_packed, head_width, k * shards // 2) for k in range(3)]
    rights.append((attended, head_width, 0))
    grad_w_first = [weight_half(1, [rows_in, first_low], rights)]
    if direct:
        first_low, grad_w_first[0], *others = together(
            first_low, grad_w_first[0], *up_terms, *down_terms
        )
        up_terms, down_terms = others[:3], others[3:]
        up_near, up_far, first_low = together(*reduce_edges(up_terms), first_low)
        up_terms = [up_near, swap_over(up_far, 4, 0)]
    grad_w_first.append(weight_half(0, [rows_in, first_low], rights))
    if direct:
        first_parts = reduce_core_edges(grad_w_first)
        *first_parts, grad_first = together(*first_parts, grad_first)
        first_terms = edge_terms(*first_parts)
    (input_grad,) = call_rows(
        input_kernel,
        steps,
        [far_rows(grad_first), by_rows(grad_packed), full(selector), full(whole_first)],
        [((row_count, D), f32, rows_spec(D), "far")],
        40 * square,
    )
    if direct:
        *first_terms, input_grad, layer_out = together(*first_terms, input_grad, layer_out)
        first_terms = plane_edge_terms(*reduce_edges_plane(first_terms))
        first_terms[0], *others = together(
            first_terms[0],
            *up_terms,
            *down_terms,
            sums_first,
            sums_second,
            grad_bias_up,
            column_sums,
        )
        up_terms, down_terms = others[:2], others[2:4]
        sums_first, sums_second, grad_bias_up, column_sums = others[4:]
        up_terms = halve_z(*up_terms)
        up_terms = [up_terms[0], swap_over(up_terms[1], 2, 0)]
        down_terms = halve_z(*down_terms)
        down_terms = [down_terms[0], swap_over(down_terms[1], 2, 0)]
    (vector_rows,) = call_rows(
        functools.partial(vector_kernel, shards),
        1,
        [
            (
                lax.convert_element_type(group_base, jnp.int32).reshape(1),
                pl.BlockSpec(memory_space=pltpu.SMEM),
            ),
            full(sums_first),
            full(sums_second),
            full(grad_bias_up),
            full(column_sums),
            full(selector),
        ],
        [((16, D), f32, pl.BlockSpec(memory_space=pltpu.VMEM))],
        48 * D * D,
    )
    (layer_out,) = call_rows(
        layer_kernel,
        steps,
        [far_rows(layer_out), full(selector)],
        [((row_count, D), f32, rows_spec(D), "far")],
        2 * square,
    )
    if direct:
        *first_terms, layer_out = together(*first_terms, layer_out)
        *parts, vector_rows = together(*reduce_plane_edges(first_terms), vector_rows)
        first_terms = z_terms(*parts)
        first_terms[0], *others = together(first_terms[0], *up_terms, *down_terms)
        up_terms, down_terms = others[:2], others[2:]
        down_own = add_z(*down_terms)
        vector_rows = add_swapped(add_swapped(vector_rows, 0, 1), 0, 2)
        up_terms = plane_edge_terms(*reduce_edges_z(up_terms))
        up_own = reduce_edges_last(up_terms)
        *first_terms, vector_rows = together(*first_terms, vector_rows)
        first_own = reduce_z(first_terms)
        slab_grad = jnp.concatenate([first_own, up_own, down_own], 1).astype(jnp.bfloat16)
        tile_grad = tiles_from_slabs(slab_grad[None], shards, block_size).reshape(tile_total, -1)
        slot_grad = transposed_times(placing, tile_grad).astype(jnp.bfloat16)
        slot_grad, vector_rows = together(slot_grad, vector_rows)
        slot_grad = lax.all_to_all(
            slot_grad.reshape(PARTS, slots, SUB * block_size), "dp", 0, 0, tiled=True
        )
        vector_rows = add_swapped(add_swapped(vector_rows, 1, 0), 2, 0)
        slot_grad, vector_rows = together(slot_grad, vector_rows)
        vector_rows = add_swapped(vector_rows, 4, 0)
        owned_grads = slot_grad.swapaxes(0, 1).reshape(slots, block_size, block_size)
    else:
        every = jnp.stack(
            [
                jnp.concatenate(
                    [half[1 - j % 2][j // 2] for half in (grad_w_first, grad_w_up, grad_w_down)], 1
                )
                for j in range(shards)
            ]
        ).astype(jnp.float32)
        mine = lax.psum_scatter(every, "tensor", scatter_dimension=0, tiled=True)[0]
        blocks = mine.reshape(PARTS, D // PARTS, -1)
        blocks = jnp.stack([blocks[(p % 2) * 4 + p // 2] for p in range(PARTS)])
        tile_grad = tiles_from_slabs(blocks, shards, block_size)
        slot_grad = tile_grad.reshape(tile_total, block_size, block_size)[owner]
        owned_grads = lax.psum_scatter(slot_grad, "dp", scatter_dimension=0, tiled=True)

    bias_first = 1.0 - DECAY_FIRST**ADAM_STEP
    bias_second = 1.0 - DECAY_SECOND**ADAM_STEP
    step_slots = max(k for k in (1, 2, 3, 4, 6, 12) if slots % k == 0)
    slots_spec = pl.BlockSpec((step_slots, block_size, block_size), lambda i: (i, 0, 0))
    slot_out = ((slots, block_size, block_size), f32, slots_spec, "far")
    new_master, new_first, new_second = call_rows(
        adam_kernel,
        slots // step_slots,
        [(own_flip.astype(jnp.int32).reshape(slots), pl.BlockSpec(memory_space=pltpu.SMEM))]
        + [
            (array, slots_spec, "far")
            for array in (
                owned_grads,
                master[0],
                left_basis[0],
                right_basis[0],
                first_moment[0],
                second_moment[0],
            )
        ],
        [slot_out] * 3,
        22 * slots * block_size**3,
        slots * block_size**2,
    )
    if not direct:
        vector_rows = lax.psum(vector_rows, ("dp", "tensor"))
    vector_grad = vector_rows[: vectors.shape[0] // D].reshape(-1)
    new_vector_first = DECAY_FIRST * vector_first + (1.0 - DECAY_FIRST) * vector_grad
    new_vector_second = (
        DECAY_SECOND * vector_second + (1.0 - DECAY_SECOND) * vector_grad * vector_grad
    )
    new_vectors = vectors - VECTOR_RATE * (new_vector_first / bias_first) / (
        jnp.sqrt(new_vector_second / bias_second) + ADAM_EPS
    )
    return (
        layer_out,
        input_grad,
        new_master[None],
        new_first[None],
        new_second[None],
        new_vectors,
        new_vector_first,
        new_vector_second,
    )


def solution(mesh):
    return jax.shard_map(
        local,
        mesh=mesh,
        in_specs=(
            P(("dp", "tensor"), None),
            P("dp", None),
            P(("dp", "tensor"), None),
            P(),
            P("tensor", "dp", None, None),
            P("tensor", "dp", None, None),
            P("tensor", "dp", None, None),
            P("tensor", "dp", None, None),
            P("tensor", "dp", None, None),
            P(),
            P(),
            P(),
        ),
        out_specs=(
            P(("dp", "tensor"), None),
            P(("dp", "tensor"), None),
            P("tensor", "dp", None, None),
            P("tensor", "dp", None, None),
            P("tensor", "dp", None, None),
            P(),
            P(),
            P(),
        ),
        check_vma=False,
    )
```

```python
import functools
import math

import jax
import jax.numpy as jnp
from jax import lax
from jax.experimental import pallas as pl
from jax.experimental.pallas import tpu as pltpu
from jax.sharding import PartitionSpec as P

HEADS = 12
HEAD_DIM = 64
D = 768
FF = 3072
ADAM_STEP = 3


NORM_EPS = 1e-12
ADAM_EPS = 1e-08
MATRIX_RATE = 0.01
VECTOR_RATE = 0.1
DECAY_FIRST = 0.5
DECAY_SECOND = 0.5
MASKED = -1e30


def product(left_side, right_side):
    return jnp.dot(left_side, right_side, preferred_element_type=jnp.float32)


def times_transposed(left_side, right_side):
    return lax.dot_general(
        left_side, right_side, (((1,), (1,)), ((), ())), preferred_element_type=jnp.float32
    )


def transposed_times(left_side, right_side):
    return lax.dot_general(
        left_side, right_side, (((0,), (0,)), ((), ())), preferred_element_type=jnp.float32
    )


VMEM_LIMIT = 16 * 1024 * 1024

PARTS = 8
SUB = 12


def part_of_block(block):
    return (block % 4) * 2 + block // 4


def feature_order(rank):
    place = lax.iota(jnp.int32, D)
    part = part_of_block(place // (D // PARTS)) ^ rank
    inner = place % (D // PARTS)
    return (inner // SUB) * (PARTS * SUB) + part * SUB + inner % SUB


def tile_counts(shards, block_size):
    rows = D // block_size
    qkv = rows * (3 * D // shards // block_size)
    out = rows * (D // shards // block_size)
    up = rows * (FF // shards // block_size)
    return (qkv, out, up)


def slabs_from_tiles(tiles, shards, block_size):
    cut = tiles.shape[1]
    qkv, out, up = tile_counts(shards, block_size)
    rows = D // block_size

    def by_rows(part):
        cols = part.shape[0] // rows
        part = part.reshape(rows, cols, cut, SUB, block_size)
        return part.transpose(2, 0, 3, 1, 4).reshape(cut, rows * SUB, cols * block_size)

    def by_cols(part):
        cols = part.shape[0] // rows
        part = part.reshape(cols, rows, cut, SUB, block_size)
        return part.transpose(2, 1, 3, 0, 4).reshape(cut, rows * SUB, cols * block_size)

    return jnp.concatenate(
        [
            by_rows(tiles[:qkv]),
            by_cols(tiles[qkv : qkv + out]),
            by_rows(tiles[qkv + out : qkv + out + up]),
            by_cols(tiles[qkv + out + up :]),
        ],
        2,
    )


def tiles_from_slabs(slabs, shards, block_size):
    cut = slabs.shape[0]
    rows = D // block_size
    width_qkv, width_out, width_up = 3 * D // shards, D // shards, FF // shards

    def by_rows(part):
        cols = part.shape[2] // block_size
        part = part.reshape(cut, rows, SUB, cols, block_size)
        return part.transpose(1, 3, 0, 2, 4).reshape(rows * cols, cut, SUB, block_size)

    def by_cols(part):
        cols = part.shape[2] // block_size
        part = part.reshape(cut, rows, SUB, cols, block_size)
        return part.transpose(3, 1, 0, 2, 4).reshape(rows * cols, cut, SUB, block_size)

    first = width_qkv + width_out
    second = first + width_up
    return jnp.concatenate(
        [
            by_rows(slabs[:, :, :width_qkv]),
            by_cols(slabs[:, :, width_qkv:first]),
            by_rows(slabs[:, :, first:second]),
            by_cols(slabs[:, :, second:]),
        ],
        0,
    )


def swap_over(values, over_dp, over_tensor):
    dp, tensor = lax.axis_size("dp"), lax.axis_size("tensor")
    pairs = [
        (a * tensor + b, (a ^ over_dp) * tensor + (b ^ over_tensor))
        for a in range(dp)
        for b in range(tensor)
    ]
    return lax.ppermute(values, ("dp", "tensor"), pairs)


def merge(terms, outs, segments):
    chunk = D // PARTS

    def kernel(*refs):
        for out, row, col, rows, cols, parts in segments:

            def step(k, carry, out=out, row=row, col=col, cols=cols, parts=parts):
                pieces = [
                    refs[term][pl.ds(pl.multiple_of(at + k * chunk, 32), chunk), left : left + cols]
                    for term, at, left in parts
                ]
                if len(pieces) > 1:
                    value = sum(piece.astype(jnp.float32) for piece in pieces)
                else:
                    value = pieces[0]
                to = refs[len(terms) + out]
                to[pl.ds(pl.multiple_of(row + k * chunk, 32), chunk), col : col + cols] = (
                    value.astype(to.dtype)
                )
                return carry

            lax.fori_loop(0, rows // chunk, step, 0)

    spec = pl.BlockSpec(memory_space=pltpu.VMEM)
    size = sum(term.size for term in terms)
    return pl.pallas_call(
        kernel,
        in_specs=[spec] * len(terms),
        out_specs=[spec] * len(outs),
        out_shape=[jax.ShapeDtypeStruct((rows, cols), dtype) for rows, cols, dtype in outs],
        compiler_params=pltpu.CompilerParams(vmem_limit_bytes=VMEM_LIMIT),
        cost_estimate=pl.CostEstimate(flops=size, bytes_accessed=4 * size, transcendentals=0),
    )(*terms)


def from_z(block):
    return [swap_over(block, 2 * k, 0) for k in (1, 2, 3)]


def over_core(blocks):
    return blocks + [swap_over(block, 0, 1) for block in blocks]


def put(out_ref, lead, row, col, ref, at, left, rows, cols):
    chunk = min(rows, D // 2)

    def step(k, carry):
        to = pl.multiple_of(row + k * chunk, 32)
        source = pl.multiple_of(at + k * chunk, 32)
        out_ref[lead, pl.ds(to, chunk), col : col + cols] = ref[
            pl.ds(source, chunk), left : left + cols
        ]
        return carry

    lax.fori_loop(0, rows // chunk, step, 0)


def place_first(refs, out_ref):
    count = len(refs) // 2
    half, width = D // 2, D // 4
    for core in range(2):
        near, beside, across = refs[core * count : (core + 1) * count]
        for y in range(2):
            col = (2 * y + core) * width
            for kind in range(2):
                left = kind * width
                put(out_ref, kind, 0, col, near, y * half, left, half, width)
                put(out_ref, kind, half, col, beside, y * half, left, half, width)
                if y:
                    put(out_ref, 2 + kind, 0, col, across, 0, left, D, width)
                else:
                    put(out_ref, 2 + kind, 0, col, near, 0, half + left, D, width)


def edges_moves():
    rows, half = D // PARTS, D // 2
    moves = []
    for core in range(2):
        near, beside, across = range(3 * core, 3 * core + 3)
        for y in range(2):
            group = 2 * y + core
            for z in range(4):
                for x in range(2):
                    to, by_y, by_x = x * half + z * rows, (2 * z + y) * rows, (2 * z + x) * rows
                    moves.append((group, to, 0, beside if x else near, by_y, 0, rows, half))
                    source = (across, by_x, 0) if y else (near, by_x, half)
                    moves.append((group, to, half, *source, rows, half))
    return moves


def plane_moves():
    half = D // 2
    return [
        (2 * y + core, x * half, 0, 4 * core + 2 * y + x, 0, 0, half, D)
        for core in range(2)
        for y in range(2)
        for x in range(2)
    ]


def groups_moves(count):
    return [(group, 0, 0, group, 0, 0, D, D) for group in range(count)]


def move_all(moves, refs, out_ref, sems):
    copies = [
        pltpu.make_async_copy(
            refs[ref].at[pl.ds(at, rows), pl.ds(left, cols)],
            out_ref.at[lead, pl.ds(row, rows), pl.ds(col, cols)],
            sems.at[k],
        )
        for k, (lead, row, col, ref, at, left, rows, cols) in enumerate(moves)
    ]
    for copy in copies:
        copy.start()
    for copy in copies:
        copy.wait()


def place_kinds(refs, out_ref):
    width = D // len(refs)
    for group, ref in enumerate(refs):
        for kind in range(4):
            put(out_ref, kind, 0, group * width, ref, 0, kind * width, D, width)


def core_terms(halves):
    odd, even = halves
    return [even.reshape(2 * D, D), swap_over(odd, 0, 1).reshape(2 * D, D)]


def summed(count, row, col):
    return [(term, row, col) for term in range(count)]


def reduce_core_plane(halves):
    half = D // 2
    return merge(
        core_terms(halves),
        [(half, D, jnp.bfloat16)] * 4,
        [(k, 0, 0, half, D, summed(2, k * half, 0)) for k in range(4)],
    )


def reduce_plane(near, beside, across, opposite):
    pair = D // 4
    terms = [near, swap_over(beside, 1, 0), swap_over(across, 0, 2), swap_over(opposite, 1, 2)]
    return merge(
        terms,
        [(pair, D, jnp.bfloat16)] * 2,
        [(k, 0, 0, pair, D, summed(4, k * pair, 0)) for k in range(2)],
    )


def halve_z(near, received):
    rows = near.shape[0] // 2
    return merge(
        [near, received],
        [(rows, D, jnp.bfloat16)] * 2,
        [(k, 0, 0, rows, D, summed(2, k * rows, 0)) for k in range(2)],
    )


def add_z(near, received):
    rows = near.shape[0]
    return merge(
        [near, received], [(rows, D, jnp.float32)], [(0, 0, 0, rows, D, summed(2, 0, 0))]
    )[0]


def z_terms(own, *sent):
    return [own] + [swap_over(block, 2 * (k + 1), 0) for k, block in enumerate(sent)]


def reduce_z(terms):
    rows = D // PARTS
    return merge(terms, [(rows, D, jnp.float32)], [(0, 0, 0, rows, D, summed(4, 0, 0))])[0]


def reduce_core_edges(halves):
    half = D // 2
    return merge(
        core_terms(halves),
        [(D, D, jnp.bfloat16), (D, half, jnp.bfloat16), (D, half, jnp.bfloat16)],
        [
            (0, 0, 0, half, half, summed(2, 0, 0)),
            (0, half, 0, half, half, summed(2, D, 0)),
            (0, 0, half, D, half, summed(2, 0, half)),
            (1, 0, 0, half, half, summed(2, half, 0)),
            (1, half, 0, half, half, summed(2, D + half, 0)),
            (2, 0, 0, D, half, summed(2, D, half)),
        ],
    )


def edge_terms(near, left, right):
    return [near, swap_over(left, 1, 0), swap_over(right, 0, 2)]


def edge_sums(row):
    half = D // 2
    return ((0, [(0, row, 0), (1, row, 0)]), (half, [(0, row, half), (2, row, 0)]))


def plane_edge_terms(near, left, right):
    return [near, swap_over(left, 0, 2), swap_over(right, 1, 0)]


def reduce_edges_plane(terms):
    half = D // 2
    kept = [(0, 0, col, half, half, parts) for col, parts in edge_sums(0)]
    sent = [
        (1 + k, 0, 0, half, half, parts) for k, (_, parts) in enumerate(edge_sums(half))
    ]
    return merge(
        terms,
        [(half, D, jnp.bfloat16), (half, half, jnp.bfloat16), (half, half, jnp.bfloat16)],
        kept + sent,
    )


def reduce_plane_edges(terms):
    rows, half = D // PARTS, D // 2
    return merge(
        terms,
        [(rows, D, jnp.bfloat16)] * 4,
        [
            (k, 0, col, rows, half, parts)
            for k in range(4)
            for col, parts in edge_sums(k * rows)
        ],
    )


def reduce_edges(terms):
    rows, half = D // PARTS, D // 2
    return merge(
        terms,
        [(half, D, jnp.bfloat16)] * 2,
        [
            (k // 2, (2 * (k % 2) + q) * rows, col, rows, half, parts)
            for k in range(4)
            for q in range(2)
            for col, parts in edge_sums(q * half + k * rows)
        ],
    )


def reduce_edges_z(terms):
    rows, half = D // PARTS, D // 2
    return merge(
        terms,
        [(rows, D, jnp.bfloat16), (rows, half, jnp.bfloat16), (rows, half, jnp.bfloat16)],
        [
            (0, 0, 0, rows, D, summed(2, 0, 0)),
            (1, 0, 0, rows, half, summed(2, rows, 0)),
            (2, 0, 0, rows, half, summed(2, rows, half)),
        ],
    )


def reduce_edges_last(terms):
    rows, half = D // PARTS, D // 2
    return merge(
        terms,
        [(rows, D, jnp.float32)],
        [(0, 0, col, rows, half, parts) for col, parts in edge_sums(0)],
    )[0]


def add_swapped(values, over_dp, over_tensor):
    return values + swap_over(values, over_dp, over_tensor)


ROWS = 256


def dot_nt(left_side, right_side):
    return lax.dot_general(
        left_side, right_side, (((1,), (1,)), ((), ())), preferred_element_type=jnp.float32
    )


def row_block(array):
    return pl.BlockSpec((ROWS, array.shape[1]), lambda i: (i, 0))


def call_rows(kernel, steps, inputs, outputs, flops, transcendentals=0, scratch=()):
    arrays = [
        pltpu.with_memory_space_constraint(array, pltpu.HBM) if far else array
        for array, _, *far in inputs
    ]
    shapes = [jax.ShapeDtypeStruct(shape, dtype) for shape, dtype, *_ in outputs]
    moved = sum(a.size * a.dtype.itemsize for a in arrays + shapes)
    shapes = [
        pltpu.HBM(shape.shape, shape.dtype) if len(output) > 3 else shape
        for shape, output in zip(shapes, outputs)
    ]
    return pl.pallas_call(
        kernel,
        grid=(steps,),
        in_specs=[spec for _, spec, *_ in inputs],
        out_specs=[output[2] for output in outputs],
        out_shape=shapes,
        scratch_shapes=scratch,
        compiler_params=pltpu.CompilerParams(vmem_limit_bytes=VMEM_LIMIT),
        cost_estimate=pl.CostEstimate(
            flops=int(1.0 * flops), bytes_accessed=moved, transcendentals=transcendentals
        ),
    )(*arrays)


def norm_rows(summed):
    centred = summed - jnp.mean(summed, -1, keepdims=True)
    inverse = lax.rsqrt(jnp.mean(centred * centred, -1, keepdims=True) + NORM_EPS)
    return centred * inverse, inverse


def norm_pull(gradient, unit_rows, inverse, gain_row):
    scaled = gradient * gain_row
    return inverse * (
        scaled
        - jnp.mean(scaled, -1, keepdims=True)
        - unit_rows * jnp.mean(scaled * unit_rows, -1, keepdims=True)
    )


def add_rows(ref, rows):
    sums = [jnp.sum(row, 0, keepdims=True) for row in rows]
    start = pl.program_id(0) == 0
    for place, total in enumerate(sums):
        kept = jnp.where(start, 0.0, ref[place : place + 1, :])
        ref[place : place + 1, :] = kept + total


def settle(moves, refs, whole_ref, sems):
    @pl.when(pl.program_id(0) == 0)
    def _():
        move_all(moves, refs, whole_ref, sems)

    return [whole_ref.at[j] for j in range(whole_ref.shape[0])]


def pair_masks(length):
    wide = 2 * HEAD_DIM
    lower = lax.broadcasted_iota(jnp.int32, (length, wide), 1) < HEAD_DIM
    top = lax.broadcasted_iota(jnp.int32, (2 * length, wide), 0) < length
    left = lax.broadcasted_iota(jnp.int32, (2 * length, wide), 1) < HEAD_DIM
    return lower, top == left


def stacked(pair, own):
    return jnp.where(own, jnp.concatenate([pair, pair], 0), jnp.zeros((), pair.dtype))


def attention_kernel(place, total_count, length, *refs):
    rows_ref, across_ref, down_ref, bias_ref, vec_ref = refs[:5]
    outs = refs[5 + total_count : 12 + total_count]
    packed_ref, probs_ref, attended_ref, unit_ref, inverse_ref, low_ref, whole_ref = outs
    scores_ref, sems, *raw = refs[12 + total_count :]

    @pl.when(pl.program_id(0) == 0)
    def _():
        copies = [
            pltpu.make_async_copy(source, to, sems.at[k])
            for k, (source, to) in enumerate(zip(refs[5 : 5 + total_count], raw))
        ]
        for copy in copies:
            copy.start()
        for copy in copies:
            copy.wait()
        place(raw, whole_ref)

    weights = [whole_ref.at[kind] for kind in range(4)]
    wide = 2 * HEAD_DIM
    pairs = HEADS // 2
    rows = rows_ref[...]
    for kind in range(3):
        part = product(rows, weights[kind][...]) + bias_ref[kind : kind + 1, :]
        part = part.astype(jnp.bfloat16)
        if kind == 0:
            part = part * jnp.bfloat16(HEAD_DIM ** (-0.5))
        packed_ref[:, kind * D : (kind + 1) * D] = part
    _, own = pair_masks(length)
    steps = [(p, i) for p in range(ROWS // length) for i in range(pairs)]

    def pair_of(p, i, kind):
        span = slice(p * length, (p + 1) * length)
        return packed_ref[span, kind * D + i * wide : kind * D + (i + 1) * wide]

    for at, (p, i) in enumerate(steps):
        scores_ref[at] = dot_nt(pair_of(p, i, 0), stacked(pair_of(p, i, 1), own))
    for at, (p, i) in enumerate(steps):
        allowed = down_ref[p] == across_ref[p]
        for half in range(2):
            lanes = slice(half * length, (half + 1) * length)
            scores = jnp.where(allowed, scores_ref[at, :, lanes], MASKED)
            raised = jnp.exp(scores - jnp.max(scores, -1, keepdims=True))
            probs_ref[p, i, :, lanes] = (
                raised * (1.0 / jnp.sum(raised, -1, keepdims=True))
            ).astype(jnp.bfloat16)
    for p, i in steps:
        mixed = product(probs_ref[p, i], stacked(pair_of(p, i, 2), own))
        attended_ref[p * length : (p + 1) * length, i * wide : (i + 1) * wide] = mixed.astype(
            jnp.bfloat16
        )
    summed = rows.astype(jnp.float32) + vec_ref[0:1, :]
    summed = summed + dot_nt(attended_ref[...], weights[3][...])
    unit, inverse = norm_rows(summed)
    unit_ref[...] = unit
    inverse_ref[...] = inverse
    low_ref[...] = (unit * vec_ref[1:2, :] + vec_ref[2:3, :]).astype(jnp.bfloat16)


def gelu_parts(values):
    size = jnp.abs(values)
    decay = jnp.exp2(values * values * (-0.5 / math.log(2.0)))
    t = 1.0 / (1.0 + size * (0.3275911 * 0.5**0.5))
    poly = t * (
        0.127414796
        + t * (-0.142248368 + t * (0.7107068705 + t * (-0.7265760135 + t * 0.5307027145)))
    )
    result = jnp.maximum(values, 0.0) - size * (poly * decay)
    rest = decay * (poly - size * (0.5 / math.pi) ** 0.5)
    return result, jnp.where(values > 0, 1.0 - rest, rest)


def up_kernel(place, shards, *refs):
    low_ref, bias_ref = refs[:2]
    act_ref, slope_ref, whole_ref, sems = refs[-4:]
    weights = settle(place, refs[2:-4], whole_ref, sems)
    width = weights[0].shape[1]
    chunk = 256
    low = low_ref[...]
    for j in range(shards):
        for c in range(0, width, chunk):
            pre = product(low, weights[j][:, c : c + chunk]) + bias_ref[j : j + 1, c : c + chunk]
            result, slope = gelu_parts(pre)
            at = j * width + c
            act_ref[:, at : at + chunk] = result.astype(jnp.bfloat16)
            slope_ref[:, at : at + chunk] = slope.astype(jnp.bfloat16)


def down_kernel(place, shards, *refs):
    act_ref, unit_ref, grad_ref, vec_ref = refs[:4]
    out_ref, dz_ref, low_ref, sums_ref, whole_ref, sems = refs[-6:]
    weights = settle(place, refs[4:-6], whole_ref, sems)
    width = weights[0].shape[1]
    summed = unit_ref[...] * vec_ref[1:2, :] + vec_ref[2:3, :] + vec_ref[3:4, :]
    for j in range(shards):
        summed = summed + dot_nt(act_ref[:, j * width : (j + 1) * width], weights[j][...])
    unit, inverse = norm_rows(summed)
    gain = vec_ref[4:5, :]
    out_ref[...] = unit * gain + vec_ref[5:6, :]
    gradient = grad_ref[...]
    dz = norm_pull(gradient, unit, inverse, gain)
    dz_ref[...] = dz
    low_ref[...] = dz.astype(jnp.bfloat16)
    add_rows(sums_ref, (gradient * unit, gradient, dz))


def hidden_back_kernel(shards, *refs):
    low_ref, slope_ref, whole_ref, dpre_ref, bias_sums_ref = refs
    width = whole_ref.shape[2]
    low = low_ref[...]
    for j in range(shards):
        span = slice(j * width, (j + 1) * width)
        dpre = product(low, whole_ref[j]) * slope_ref[:, span].astype(jnp.float32)
        dpre = dpre.astype(jnp.bfloat16)
        dpre_ref[:, span] = dpre
        total = jnp.sum(dpre.astype(jnp.float32), 0, keepdims=True)
        kept = jnp.where(pl.program_id(0) == 0, 0.0, bias_sums_ref[j : j + 1, :])
        bias_sums_ref[j : j + 1, :] = kept + total


def back_kernel(shards, *refs):
    dpre_ref, dz_ref, unit_ref, inverse_ref, vec_ref, up_ref, first_ref = refs[:7]
    dz1_ref, low1_ref, datt_ref, sums_ref = refs[7:]
    width = up_ref.shape[2]
    gradient = dz_ref[...]
    for j in range(shards):
        gradient = gradient + dot_nt(dpre_ref[:, j * width : (j + 1) * width], up_ref[j])
    unit = unit_ref[...]
    dz1 = norm_pull(gradient, unit, inverse_ref[...], vec_ref[1:2, :])
    dz1_ref[...] = dz1
    low1 = dz1.astype(jnp.bfloat16)
    low1_ref[...] = low1
    add_rows(sums_ref, (gradient * unit, gradient, dz1))
    datt_ref[...] = product(low1, first_ref[3]).astype(jnp.bfloat16)


def attention_back_kernel(length, *refs):
    datt_ref, attended_ref, packed_ref, probs_ref, dpacked_ref, sums_ref, up_ref, grad_ref = refs
    wide = 2 * HEAD_DIM
    lower, own = pair_masks(length)
    ones = own.astype(jnp.bfloat16)
    steps = [(p, i) for p in range(ROWS // length) for i in range(HEADS // 2)]

    def pair_of(p, i, kind):
        span = slice(p * length, (p + 1) * length)
        return packed_ref[span, kind * D + i * wide : kind * D + (i + 1) * wide]

    def keep(p, i, kind, grad):
        span = slice(p * length, (p + 1) * length)
        dpacked_ref[span, kind * D + i * wide : kind * D + (i + 1) * wide] = grad.astype(
            jnp.bfloat16
        )

    for place, (p, i) in enumerate(steps):
        span = slice(p * length, (p + 1) * length)
        lanes = slice(i * wide, (i + 1) * wide)
        upstream = datt_ref[span, lanes]
        up_ref[place, :, :wide] = upstream
        up_ref[place, :, wide:] = (
            upstream.astype(jnp.float32) * attended_ref[span, lanes].astype(jnp.float32)
        ).astype(jnp.bfloat16)
    for place, (p, i) in enumerate(steps):
        centred = dot_nt(
            up_ref[place], jnp.concatenate([stacked(pair_of(p, i, 2), own), -ones], 1)
        )
        grad_ref[place] = (probs_ref[p, i].astype(jnp.float32) * centred).astype(jnp.bfloat16)
    for place, (p, i) in enumerate(steps):
        grad_scores = grad_ref[place]
        keep(
            p, i, 0,
            product(grad_scores, stacked(pair_of(p, i, 1), own)) * HEAD_DIM ** (-0.5),
        )
        both = transposed_times(grad_scores, pair_of(p, i, 0))
        keep(p, i, 1, jnp.where(lower, both[:length], both[length:]))
        both = transposed_times(probs_ref[p, i], up_ref[place, :, :wide])
        keep(p, i, 2, jnp.where(lower, both[:length], both[length:]))
    total = jnp.sum(dpacked_ref[...].astype(jnp.float32), 0, keepdims=True)
    kept = jnp.where(pl.program_id(0) == 0, 0.0, sums_ref[0:1, :])
    sums_ref[0:1, :] = kept + total


def weight_kernel(odd, count, *refs):
    lefts = refs[: 2 if count > 1 else 1]
    rights, out_ref = refs[len(lefts) : -1], refs[-1]
    if count == 1:
        out_ref[0] = transposed_times(lefts[0][...], rights[0][...]).astype(jnp.bfloat16)
    else:
        half = rights[0].shape[1] // 2
        span = slice(half, 2 * half) if odd else slice(0, half)
        values = jnp.concatenate([right[:, span] for right in rights[:-1]], 1)
        width = values.shape[1]
        out_ref[0, :, :width] = transposed_times(lefts[0][...], values).astype(jnp.bfloat16)
        out_ref[0, :, width:] = transposed_times(lefts[1][...], rights[-1][:, span]).astype(
            jnp.bfloat16
        )


def weight_half(odd, lefts, rights):
    count = len(rights)
    single = count == 1
    specs = []
    for array, width, before in rights:
        if single:
            specs.append(pl.BlockSpec((array.shape[0], width), lambda i: (0, 2 * i + odd)))
        else:
            specs.append(pl.BlockSpec((array.shape[0], 2 * width), lambda i, b=before: (0, b + i)))
    arrays = [*lefts, *[array for array, _, _ in rights]]
    tokens = lefts[0].shape[0]
    (half,) = pl.pallas_call(
        functools.partial(weight_kernel, odd, count),
        grid=(2,),
        in_specs=[pl.BlockSpec(memory_space=pltpu.VMEM) for _ in lefts] + specs,
        out_specs=[pl.BlockSpec((1, D, D), lambda i: (i, 0, 0))],
        out_shape=[jax.ShapeDtypeStruct((2, D, D), jnp.bfloat16)],
        compiler_params=pltpu.CompilerParams(vmem_limit_bytes=VMEM_LIMIT),
        cost_estimate=pl.CostEstimate(
            flops=4 * tokens * D * D,
            bytes_accessed=sum(2 * array.size for array in arrays),
            transcendentals=0,
        ),
    )(*arrays)
    return half


def weight_halves(lefts, rights):
    return [weight_half(odd, lefts, rights) for odd in (1, 0)]


def two_terms(values):
    top = values.astype(jnp.bfloat16)
    return top, (values - top.astype(jnp.float32)).astype(jnp.bfloat16)


def adam_kernel(*refs):
    flip_ref, grad_ref, master_ref, left_ref, right_ref, first_ref, second_ref = refs[:7]
    master_out, first_out, second_out = refs[7:]
    bias_first = 1.0 - DECAY_FIRST**ADAM_STEP
    bias_second = 1.0 - DECAY_SECOND**ADAM_STEP
    count = grad_ref.shape[0]
    lefts = [two_terms(left_ref[k]) for k in range(count)]
    rights = [two_terms(right_ref[k]) for k in range(count)]
    turned = []
    for k in range(count):
        tile = grad_ref[k].astype(jnp.float32)
        flip = flip_ref[pl.program_id(0) * count + k] > 0
        tile = jnp.where(flip, tile.T, tile)
        top, rest = two_terms(tile)
        grad = product(top, rights[k][0]) + product(top, rights[k][1])
        if grad_ref.dtype != jnp.bfloat16:
            grad = grad + product(rest, rights[k][0])
        turned.append(grad)
    directions = []
    for k in range(count):
        top, rest = two_terms(turned[k])
        rotated = (
            transposed_times(lefts[k][0], top)
            + transposed_times(lefts[k][0], rest)
            + transposed_times(lefts[k][1], top)
        )
        first = DECAY_FIRST * first_ref[k] + (1.0 - DECAY_FIRST) * rotated
        second = DECAY_SECOND * second_ref[k] + (1.0 - DECAY_SECOND) * rotated * rotated
        first_out[k] = first
        second_out[k] = second
        directions.append(first / bias_first / (jnp.sqrt(second / bias_second) + ADAM_EPS))
    backs = [
        product(lefts[k][0], directions[k].astype(jnp.bfloat16)).astype(jnp.bfloat16)
        for k in range(count)
    ]
    for k in range(count):
        update = times_transposed(backs[k], rights[k][0])
        master_out[k] = master_ref[k] - MATRIX_RATE * update


def unpermuted(values, selector_ref):
    top, rest = two_terms(values)
    return dot_nt(top, selector_ref[...]) + dot_nt(rest, selector_ref[...])


def enter_kernel(tokens_ref, grad_ref, vectors_ref, selector_ref, rows_ref, out_ref, d_rows_ref):
    selector = selector_ref[...]
    rows_ref[...] = product(tokens_ref[...], selector).astype(jnp.bfloat16)
    top, rest = two_terms(grad_ref[...])
    out_ref[...] = product(top, selector) + product(rest, selector)

    @pl.when(pl.program_id(0) == 0)
    def _():
        rows = vectors_ref[...]
        permuted = jnp.zeros(rows.shape, jnp.float32)
        for _ in range(3):
            term = rows.astype(jnp.bfloat16)
            rows = rows - term.astype(jnp.float32)
            permuted = permuted + product(term, selector)
        d_rows_ref[...] = permuted


def layer_kernel(out_ref, selector_ref, layer_ref):
    layer_ref[...] = unpermuted(out_ref[...], selector_ref)


def input_kernel(dz1_ref, dpacked_ref, selector_ref, whole_ref, input_ref):
    gradient = dz1_ref[...]
    for kind in range(3):
        gradient = gradient + dot_nt(dpacked_ref[:, kind * D : (kind + 1) * D], whole_ref[kind])
    input_ref[...] = unpermuted(gradient, selector_ref)


def vector_kernel(shards, *refs):
    base_ref, first_ref, second_ref, hidden_ref, columns_ref, selector_ref, out_ref = refs
    base = base_ref[0]
    rows = jnp.concatenate(
        [
            first_ref[0:1, :],
            second_ref[0:1, :],
            first_ref[2:3, :],
            second_ref[2:3, :],
            first_ref[1:2, :],
            second_ref[1:2, :],
            jnp.zeros((2, D), jnp.float32),
        ],
        0,
    )
    natural = jnp.zeros((8, D), jnp.float32)
    for _ in range(3):
        term = rows.astype(jnp.bfloat16)
        rows = rows - term.astype(jnp.float32)
        natural = natural + dot_nt(term, selector_ref[...])
    hidden = FF // D
    out_ref[...] = jnp.zeros(out_ref.shape, jnp.float32)
    for at, row in ((0, 0), (1, 1), (4, 2), (5 + hidden, 3), (6 + hidden, 4), (7 + hidden, 5)):
        out_ref[at : at + 1, :] = natural[row : row + 1, :]
    width = D // shards
    for j in range(shards):
        out_ref[5 + j : 6 + j, :] = hidden_ref[pl.ds(j ^ base, 1), :]
        for at, kind in ((2, 0), (3, 2)):
            parts = [
                jnp.where(
                    (j ^ base) == k,
                    columns_ref[0:1, kind * D + k * width : kind * D + (k + 1) * width],
                    0.0,
                )
                for k in range(shards)
            ]
            out_ref[at : at + 1, j * width : (j + 1) * width] = sum(parts)


def together(*values):
    return lax.optimization_barrier(values)


def local(
    tokens,
    segments,
    out_grad,
    owner,
    master,
    left_basis,
    right_basis,
    first_moment,
    second_moment,
    vectors,
    vector_first,
    vector_second,
):
    shards = lax.axis_size("tensor")
    dp_size = lax.axis_size("dp")
    direct = dp_size == PARTS and shards == 4
    tensor_rank = lax.axis_index("tensor")
    dp_rank = lax.axis_index("dp")
    local_heads = HEADS // shards
    head_width = local_heads * HEAD_DIM
    up_width = FF // shards
    width_qkv = 3 * head_width
    block_size = master.shape[-1]
    slots = master.shape[1]
    row_count = tokens.shape[0]
    length = segments.shape[1]
    pack_count = row_count // length
    own_segments = lax.dynamic_slice_in_dim(segments, tensor_rank * pack_count, pack_count, 0)
    qkv_tiles, out_tiles, up_tiles = tile_counts(shards, block_size)
    tile_total = owner.shape[0]

    group_base = tensor_rank if direct else 0
    order = feature_order(dp_rank if direct else 0)
    selector = (lax.iota(jnp.int32, D)[:, None] == order[None, :]).astype(jnp.bfloat16)

    steps = row_count // ROWS
    f32, bf16 = jnp.float32, jnp.bfloat16
    rows_spec = lambda width: pl.BlockSpec((ROWS, width), lambda i: (i, 0))
    full = lambda array: (array, pl.BlockSpec(memory_space=pltpu.VMEM))
    raw = lambda array: (array, pl.BlockSpec(memory_space=pl.ANY))
    by_rows = lambda array: (array, row_block(array))
    far_rows = lambda array: (array, row_block(array), "far")
    group_order = lax.iota(jnp.int32, shards) ^ group_base
    below = vectors[: 5 * D].reshape(5, D)
    above = vectors[5 * D + FF :].reshape(3, D)
    d_rows = jnp.stack(
        [below[4], below[0], above[1], above[0], below[1], above[2], below[0], below[0]]
    )
    bias_q = below[2].reshape(shards, head_width)[group_order]
    bias_v = below[3].reshape(shards, head_width)[group_order]
    bias_up = vectors[5 * D : 5 * D + FF].reshape(shards, up_width)[group_order]
    rows_in, grad_out, d_rows = call_rows(
        enter_kernel,
        steps,
        [far_rows(tokens), far_rows(out_grad), full(d_rows), full(selector)],
        [
            ((row_count, D), bf16, rows_spec(D), "far"),
            ((row_count, D), f32, rows_spec(D), "far"),
            ((8, D), f32, pl.BlockSpec(memory_space=pltpu.VMEM)),
        ],
        6 * row_count * D * D,
    )

    def flipped(index):
        from_out = (index >= qkv_tiles) & (index < qkv_tiles + out_tiles)
        return (from_out | (index >= qkv_tiles + out_tiles + up_tiles))[:, None, None]

    own_tiles = lax.dynamic_slice_in_dim(owner, dp_rank * slots, slots, 0)
    own_flip = flipped(own_tiles)
    sent = master[0].astype(jnp.bfloat16)
    sent = jnp.where(own_flip, jnp.swapaxes(sent, 1, 2), sent)
    placing = (lax.iota(jnp.int32, tile_total)[:, None] == owner[None, :]).astype(jnp.bfloat16)
    if direct:
        parts = sent.reshape(slots, PARTS, SUB * block_size).swapaxes(0, 1)
        parts = lax.all_to_all(parts, "dp", 0, 0, tiled=True).reshape(tile_total, -1)
        tiles = product(placing, parts).astype(jnp.bfloat16)
        slab = slabs_from_tiles(tiles.reshape(tile_total, 1, SUB, block_size), shards, block_size)[0]
        half, rows = D // 2, D // PARTS
        first_slab, up_slab, down_slab = (slab[:, k * D : (k + 1) * D] for k in range(3))
        near_left, near_right = down_slab[:, :half], down_slab[:, half:]
        *blocks, near_left, near_right, rows_in, grad_out, d_rows, bias_up = together(
            *from_z(first_slab),
            swap_over(near_left, 0, 2),
            swap_over(near_right, 1, 0),
            rows_in,
            grad_out,
            d_rows,
            bias_up,
        )
        left, right, down_near = merge(
            [first_slab, *blocks, down_slab, near_left, near_right],
            [(half, half, bf16), (half, half, bf16), (2 * rows, D, bf16)],
            [(k, z * rows, 0, rows, half, [(z, 0, k * half)]) for k in range(2) for z in range(4)]
            + [
                (2, 0, 0, rows, D, [(4, 0, 0)]),
                (2, rows, 0, rows, half, [(5, 0, 0)]),
                (2, rows, half, rows, half, [(6, 0, 0)]),
            ],
        )
        left, right, down_near, up_slab = together(left, right, down_near, up_slab)
        up_beside = swap_over(up_slab, 2, 0)
        (up_pair,) = merge(
            [up_slab, up_beside],
            [(2 * rows, D, bf16)],
            [(0, z * rows, 0, rows, D, [(z, 0, 0)]) for z in range(2)],
        )
        left_across, right_beside, up_pair = together(
            swap_over(left, 0, 2), swap_over(right, 1, 0), up_pair
        )
        near, left, right = merge(
            [left, left_across, right, right_beside],
            [(D, D, bf16), (D, half, bf16), (D, half, bf16)],
            [
                (out, q * half, col, half, half, [(2 * k + q, 0, 0)])
                for k in range(2)
                for q in range(2)
                for out, col in ((0, k * half), (1 + k, 0))
            ],
        )
        near, down_near = together(near, down_near)
        down_beside = swap_over(down_near, 2, 0)
        near_there, beside, across, up_far, down_beside = together(
            swap_over(near, 0, 1),
            swap_over(left, 1, 0),
            swap_over(right, 0, 2),
            swap_over(up_pair, 4, 0),
            down_beside,
        )
        up_z, down_pair = merge(
            [up_pair, up_far, down_near, down_beside],
            [(half, D, bf16)] * 2,
            [
                (k, z * 2 * rows, 0, 2 * rows, D, [(2 * k + z, 0, 0)])
                for k in range(2)
                for z in range(2)
            ],
        )
        first = [near, beside, across, near_there] + over_core([beside, across])[2:]
        up = [up_z, swap_over(up_z, 1, 0), swap_over(up_z, 0, 2), swap_over(up_z, 1, 2)]
        down_far = swap_over(down_pair, 4, 0)
        places = (place_first, plane_moves(), edges_moves())
        pieces = [first, None, None]
    else:
        gathered = lax.all_gather(sent, "dp", axis=0, tiled=True).reshape(tile_total, -1)
        tiles = product(placing, gathered).astype(jnp.bfloat16)
        slabs = slabs_from_tiles(
            tiles.reshape(tile_total, PARTS, SUB, block_size), shards, block_size
        )
        whole = jnp.concatenate([slabs[part_of_block(k)] for k in range(PARTS)], 0)
        every = lax.all_gather(whole, "tensor", axis=0)
        pieces = [
            [every[j][:, k * D : (k + 1) * D] for j in range(shards)] for k in range(3)
        ]
        places = (place_kinds, groups_moves(shards), groups_moves(shards))

    packs_step = ROWS // length
    bias_qkv = jnp.stack(
        [bias_q.reshape(D), jnp.zeros((D,), jnp.float32), bias_v.reshape(D)]
    )
    pairs = HEADS // 2
    probs_spec = pl.BlockSpec((packs_step, pairs, length, 2 * length), lambda i: (i, 0, 0, 0))
    sums_spec = lambda width: pl.BlockSpec((8, width), lambda i: (0, 0))
    square = 2 * row_count * D * D

    whole_out = ((shards, D, D), bf16, pl.BlockSpec(memory_space=pltpu.VMEM))
    packed, probs, attended, unit_first, inverse_first, normed_low, whole_first = call_rows(
        functools.partial(attention_kernel, places[0], len(pieces[0]), length),
        steps,
        [
            far_rows(rows_in),
            (own_segments[:, None, :], pl.BlockSpec((packs_step, 1, length), lambda i: (i, 0, 0))),
            (own_segments[:, :, None], pl.BlockSpec((packs_step, length, 1), lambda i: (i, 0, 0))),
            full(bias_qkv),
            full(d_rows),
            *[raw(w) + (("far",) if w.shape == (D, D) else ()) for w in pieces[0]],
        ],
        [
            ((row_count, 3 * D), bf16, rows_spec(3 * D), "far"),
            ((pack_count, pairs, length, 2 * length), bf16, probs_spec, "far"),
            ((row_count, D), bf16, rows_spec(D)),
            ((row_count, D), f32, rows_spec(D), "far"),
            ((row_count, 1), f32, rows_spec(1), "far"),
            ((row_count, D), bf16, rows_spec(D), "far"),
            whole_out,
        ],
        4 * square + 4 * row_count * length * D,
        row_count * length * HEADS,
        [
            pltpu.VMEM((packs_step * pairs, length, 2 * length), f32),
            pltpu.SemaphoreType.DMA((len(pieces[0]),)),
            *[pltpu.VMEM(w.shape, bf16) for w in pieces[0]],
        ],
    )
    if direct:
        up[0], normed_low = together(up[0], normed_low)
        *up, up_there, down_far, normed_low = together(
            *up, swap_over(up[0], 0, 1), down_far, normed_low
        )
        down_near, near_left, near_right = merge(
            [down_pair, down_far],
            [(D, D, bf16), (D, half, bf16), (D, half, bf16)],
            [(0, z * half, 0, half, D, [(z, 0, 0)]) for z in range(2)]
            + [
                (1 + k, z * half, 0, half, half, [(z, 0, k * half)])
                for k in range(2)
                for z in range(2)
            ],
        )
        down = [down_near, swap_over(near_left, 1, 0), swap_over(near_right, 0, 2)]
        pieces[1] = up + [up_there] + over_core(up[1:])[3:]
    activated, slope, whole_up = call_rows(
        functools.partial(up_kernel, places[1], shards),
        steps,
        [far_rows(normed_low), full(bias_up), *[raw(w) for w in pieces[1]]],
        [
            ((row_count, FF), bf16, rows_spec(FF)),
            ((row_count, FF), bf16, rows_spec(FF), "far"),
            whole_out,
        ],
        40 * square,
        2 * row_count * FF,
        [pltpu.SemaphoreType.DMA((len(places[1]),))],
    )
    if direct:
        *down, down_there, activated = together(*down, swap_over(down[0], 0, 1), activated)
        pieces[2] = down + [down_there] + over_core(down[1:])[2:]
    layer_out, grad_second, second_low, sums_second, whole_down = call_rows(
        functools.partial(down_kernel, places[2], shards),
        steps,
        [
            by_rows(activated),
            far_rows(unit_first),
            far_rows(grad_out),
            full(d_rows),
            *[raw(w) for w in pieces[2]],
        ],
        [
            ((row_count, D), f32, rows_spec(D), "far"),
            ((row_count, D), f32, rows_spec(D)),
            ((row_count, D), bf16, rows_spec(D)),
            ((8, D), f32, sums_spec(D)),
            whole_out,
        ],
        4 * square,
        0,
        [pltpu.SemaphoreType.DMA((len(places[2]),))],
    )
    grad_w_down = weight_halves([second_low], [(activated, up_width, 0)])
    if direct:
        down_parts = reduce_core_plane(grad_w_down)
        second_low, *down_parts = together(second_low, *down_parts)
        down_parts = reduce_plane(*down_parts)
    grad_pre, grad_bias_up = call_rows(
        functools.partial(hidden_back_kernel, shards),
        steps,
        [by_rows(second_low), far_rows(slope), full(whole_down)],
        [((row_count, FF), bf16, rows_spec(FF)), ((8, up_width), f32, sums_spec(up_width))],
        4 * square,
    )
    grad_w_up = weight_halves([normed_low], [(grad_pre, up_width, 0)])
    grad_first, first_low, grad_attended, sums_first = call_rows(
        functools.partial(back_kernel, shards),
        steps,
        [
            by_rows(grad_pre),
            by_rows(grad_second),
            far_rows(unit_first),
            far_rows(inverse_first),
            full(d_rows),
            full(whole_up),
            full(whole_first),
        ],
        [
            ((row_count, D), f32, rows_spec(D), "far"),
            ((row_count, D), bf16, rows_spec(D)),
            ((row_count, D), bf16, rows_spec(D)),
            ((8, D), f32, sums_spec(D)),
        ],
        20 * square,
    )
    if direct:
        up_parts = reduce_core_edges(grad_w_up)
        grad_attended, *parts = together(grad_attended, *up_parts, *down_parts)
        up_terms = edge_terms(*parts[:3])
        down_terms = [parts[3], swap_over(parts[4], 4, 0)]
    grad_packed, column_sums = call_rows(
        functools.partial(attention_back_kernel, length),
        steps,
        [by_rows(grad_attended), by_rows(attended), far_rows(packed), (probs, probs_spec, "far")],
        [
            ((row_count, 3 * D), bf16, rows_spec(3 * D)),
            ((8, 3 * D), f32, sums_spec(3 * D)),
        ],
        8 * square,
        0,
        [pltpu.VMEM((packs_step * pairs, length, 2 * length), bf16)] * 2,
    )
    rights = [(grad_packed, head_width, k * shards // 2) for k in range(3)]
    rights.append((attended, head_width, 0))
    grad_w_first = [weight_half(1, [rows_in, first_low], rights)]
    if direct:
        first_low, grad_w_first[0], *others = together(
            first_low, grad_w_first[0], *up_terms, *down_terms
        )
        up_terms, down_terms = others[:3], others[3:]
        up_near, up_far, first_low = together(*reduce_edges(up_terms), first_low)
        up_terms = [up_near, swap_over(up_far, 4, 0)]
    grad_w_first.append(weight_half(0, [rows_in, first_low], rights))
    if direct:
        first_parts = reduce_core_edges(grad_w_first)
        *first_parts, grad_first = together(*first_parts, grad_first)
        first_terms = edge_terms(*first_parts)
    (input_grad,) = call_rows(
        input_kernel,
        steps,
        [far_rows(grad_first), by_rows(grad_packed), full(selector), full(whole_first)],
        [((row_count, D), f32, rows_spec(D), "far")],
        40 * square,
    )
    if direct:
        *first_terms, input_grad, layer_out = together(*first_terms, input_grad, layer_out)
        first_terms = plane_edge_terms(*reduce_edges_plane(first_terms))
        first_terms[0], *others = together(
            first_terms[0],
            *up_terms,
            *down_terms,
            sums_first,
            sums_second,
            grad_bias_up,
            column_sums,
        )
        up_terms, down_terms = others[:2], others[2:4]
        sums_first, sums_second, grad_bias_up, column_sums = others[4:]
        up_terms = halve_z(*up_terms)
        up_terms = [up_terms[0], swap_over(up_terms[1], 2, 0)]
        down_terms = halve_z(*down_terms)
        down_terms = [down_terms[0], swap_over(down_terms[1], 2, 0)]
    (vector_rows,) = call_rows(
        functools.partial(vector_kernel, shards),
        1,
        [
            (
                lax.convert_element_type(group_base, jnp.int32).reshape(1),
                pl.BlockSpec(memory_space=pltpu.SMEM),
            ),
            full(sums_first),
            full(sums_second),
            full(grad_bias_up),
            full(column_sums),
            full(selector),
        ],
        [((16, D), f32, pl.BlockSpec(memory_space=pltpu.VMEM))],
        48 * D * D,
    )
    (layer_out,) = call_rows(
        layer_kernel,
        steps,
        [far_rows(layer_out), full(selector)],
        [((row_count, D), f32, rows_spec(D), "far")],
        2 * square,
    )
    if direct:
        *first_terms, layer_out = together(*first_terms, layer_out)
        *parts, vector_rows = together(*reduce_plane_edges(first_terms), vector_rows)
        first_terms = z_terms(*parts)
        first_terms[0], *others = together(first_terms[0], *up_terms, *down_terms)
        up_terms, down_terms = others[:2], others[2:]
        down_own = add_z(*down_terms)
        vector_rows = add_swapped(add_swapped(vector_rows, 0, 1), 0, 2)
        up_terms = plane_edge_terms(*reduce_edges_z(up_terms))
        up_own = reduce_edges_last(up_terms)
        *first_terms, vector_rows = together(*first_terms, vector_rows)
        first_own = reduce_z(first_terms)
        slab_grad = jnp.concatenate([first_own, up_own, down_own], 1).astype(jnp.bfloat16)
        tile_grad = tiles_from_slabs(slab_grad[None], shards, block_size).reshape(tile_total, -1)
        slot_grad = transposed_times(placing, tile_grad).astype(jnp.bfloat16)
        slot_grad, vector_rows = together(slot_grad, vector_rows)
        slot_grad = lax.all_to_all(
            slot_grad.reshape(PARTS, slots, SUB * block_size), "dp", 0, 0, tiled=True
        )
        vector_rows = add_swapped(add_swapped(vector_rows, 1, 0), 2, 0)
        slot_grad, vector_rows = together(slot_grad, vector_rows)
        vector_rows = add_swapped(vector_rows, 4, 0)
        owned_grads = slot_grad.swapaxes(0, 1).reshape(slots, block_size, block_size)
    else:
        every = jnp.stack(
            [
                jnp.concatenate(
                    [half[1 - j % 2][j // 2] for half in (grad_w_first, grad_w_up, grad_w_down)], 1
                )
                for j in range(shards)
            ]
        ).astype(jnp.float32)
        mine = lax.psum_scatter(every, "tensor", scatter_dimension=0, tiled=True)[0]
        blocks = mine.reshape(PARTS, D // PARTS, -1)
        blocks = jnp.stack([blocks[(p % 2) * 4 + p // 2] for p in range(PARTS)])
        tile_grad = tiles_from_slabs(blocks, shards, block_size)
        slot_grad = tile_grad.reshape(tile_total, block_size, block_size)[owner]
        owned_grads = lax.psum_scatter(slot_grad, "dp", scatter_dimension=0, tiled=True)

    bias_first = 1.0 - DECAY_FIRST**ADAM_STEP
    bias_second = 1.0 - DECAY_SECOND**ADAM_STEP
    step_slots = max(k for k in (1, 2, 3, 4, 6, 12) if slots % k == 0)
    slots_spec = pl.BlockSpec((step_slots, block_size, block_size), lambda i: (i, 0, 0))
    slot_out = ((slots, block_size, block_size), f32, slots_spec, "far")
    new_master, new_first, new_second = call_rows(
        adam_kernel,
        slots // step_slots,
        [(own_flip.astype(jnp.int32).reshape(slots), pl.BlockSpec(memory_space=pltpu.SMEM))]
        + [
            (array, slots_spec, "far")
            for array in (
                owned_grads,
                master[0],
                left_basis[0],
                right_basis[0],
                first_moment[0],
                second_moment[0],
            )
        ],
        [slot_out] * 3,
        22 * slots * block_size**3,
        slots * block_size**2,
    )
    if not direct:
        vector_rows = lax.psum(vector_rows, ("dp", "tensor"))
    vector_grad = vector_rows[: vectors.shape[0] // D].reshape(-1)
    new_vector_first = DECAY_FIRST * vector_first + (1.0 - DECAY_FIRST) * vector_grad
    new_vector_second = (
        DECAY_SECOND * vector_second + (1.0 - DECAY_SECOND) * vector_grad * vector_grad
    )
    new_vectors = vectors - VECTOR_RATE * (new_vector_first / bias_first) / (
        jnp.sqrt(new_vector_second / bias_second) + ADAM_EPS
    )
    return (
        layer_out,
        input_grad,
        new_master[None],
        new_first[None],
        new_second[None],
        new_vectors,
        new_vector_first,
        new_vector_second,
    )


def solution(mesh):
    return jax.shard_map(
        local,
        mesh=mesh,
        in_specs=(
            P(("dp", "tensor"), None),
            P("dp", None),
            P(("dp", "tensor"), None),
            P(),
            P("tensor", "dp", None, None),
            P("tensor", "dp", None, None),
            P("tensor", "dp", None, None),
            P("tensor", "dp", None, None),
            P("tensor", "dp", None, None),
            P(),
            P(),
            P(),
        ),
        out_specs=(
            P(("dp", "tensor"), None),
            P(("dp", "tensor"), None),
            P("tensor", "dp", None, None),
            P("tensor", "dp", None, None),
            P("tensor", "dp", None, None),
            P(),
            P(),
            P(),
        ),
        check_vma=False,
    )
```

```python
import functools
import math

import jax
import jax.numpy as jnp
from jax import lax
from jax.experimental import pallas as pl
from jax.experimental.pallas import tpu as pltpu
from jax.sharding import PartitionSpec as P

HEADS = 12
HEAD_DIM = 64
D = 768
FF = 3072
ADAM_STEP = 3


NORM_EPS = 1e-12
ADAM_EPS = 1e-08
MATRIX_RATE = 0.01
VECTOR_RATE = 0.1
DECAY_FIRST = 0.5
DECAY_SECOND = 0.5
MASKED = -1e30


def product(left_side, right_side):
    return jnp.dot(left_side, right_side, preferred_element_type=jnp.float32)


def times_transposed(left_side, right_side):
    return lax.dot_general(
        left_side, right_side, (((1,), (1,)), ((), ())), preferred_element_type=jnp.float32
    )


def transposed_times(left_side, right_side):
    return lax.dot_general(
        left_side, right_side, (((0,), (0,)), ((), ())), preferred_element_type=jnp.float32
    )


VMEM_LIMIT = 16 * 1024 * 1024

PARTS = 8
SUB = 12


def part_of_block(block):
    return (block % 4) * 2 + block // 4


def feature_order(rank):
    place = lax.iota(jnp.int32, D)
    part = part_of_block(place // (D // PARTS)) ^ rank
    inner = place % (D // PARTS)
    return (inner // SUB) * (PARTS * SUB) + part * SUB + inner % SUB


def tile_counts(shards, block_size):
    rows = D // block_size
    qkv = rows * (3 * D // shards // block_size)
    out = rows * (D // shards // block_size)
    up = rows * (FF // shards // block_size)
    return (qkv, out, up)


def slabs_from_tiles(tiles, shards, block_size):
    cut = tiles.shape[1]
    qkv, out, up = tile_counts(shards, block_size)
    rows = D // block_size

    def by_rows(part):
        cols = part.shape[0] // rows
        part = part.reshape(rows, cols, cut, SUB, block_size)
        return part.transpose(2, 0, 3, 1, 4).reshape(cut, rows * SUB, cols * block_size)

    def by_cols(part):
        cols = part.shape[0] // rows
        part = part.reshape(cols, rows, cut, SUB, block_size)
        return part.transpose(2, 1, 3, 0, 4).reshape(cut, rows * SUB, cols * block_size)

    return jnp.concatenate(
        [
            by_rows(tiles[:qkv]),
            by_cols(tiles[qkv : qkv + out]),
            by_rows(tiles[qkv + out : qkv + out + up]),
            by_cols(tiles[qkv + out + up :]),
        ],
        2,
    )


def tiles_from_slabs(slabs, shards, block_size):
    cut = slabs.shape[0]
    rows = D // block_size
    width_qkv, width_out, width_up = 3 * D // shards, D // shards, FF // shards

    def by_rows(part):
        cols = part.shape[2] // block_size
        part = part.reshape(cut, rows, SUB, cols, block_size)
        return part.transpose(1, 3, 0, 2, 4).reshape(rows * cols, cut, SUB, block_size)

    def by_cols(part):
        cols = part.shape[2] // block_size
        part = part.reshape(cut, rows, SUB, cols, block_size)
        return part.transpose(3, 1, 0, 2, 4).reshape(rows * cols, cut, SUB, block_size)

    first = width_qkv + width_out
    second = first + width_up
    return jnp.concatenate(
        [
            by_rows(slabs[:, :, :width_qkv]),
            by_cols(slabs[:, :, width_qkv:first]),
            by_rows(slabs[:, :, first:second]),
            by_cols(slabs[:, :, second:]),
        ],
        0,
    )


def swap_over(values, over_dp, over_tensor):
    dp, tensor = lax.axis_size("dp"), lax.axis_size("tensor")
    pairs = [
        (a * tensor + b, (a ^ over_dp) * tensor + (b ^ over_tensor))
        for a in range(dp)
        for b in range(tensor)
    ]
    return lax.ppermute(values, ("dp", "tensor"), pairs)


def merge(terms, outs, segments):
    chunk = D // PARTS

    def kernel(*refs):
        for out, row, col, rows, cols, parts in segments:

            def step(k, carry, out=out, row=row, col=col, cols=cols, parts=parts):
                pieces = [
                    refs[term][pl.ds(pl.multiple_of(at + k * chunk, 32), chunk), left : left + cols]
                    for term, at, left in parts
                ]
                if len(pieces) > 1:
                    value = sum(piece.astype(jnp.float32) for piece in pieces)
                else:
                    value = pieces[0]
                to = refs[len(terms) + out]
                to[pl.ds(pl.multiple_of(row + k * chunk, 32), chunk), col : col + cols] = (
                    value.astype(to.dtype)
                )
                return carry

            lax.fori_loop(0, rows // chunk, step, 0)

    spec = pl.BlockSpec(memory_space=pltpu.VMEM)
    size = sum(term.size for term in terms)
    return pl.pallas_call(
        kernel,
        in_specs=[spec] * len(terms),
        out_specs=[spec] * len(outs),
        out_shape=[jax.ShapeDtypeStruct((rows, cols), dtype) for rows, cols, dtype in outs],
        compiler_params=pltpu.CompilerParams(vmem_limit_bytes=VMEM_LIMIT),
        cost_estimate=pl.CostEstimate(flops=size, bytes_accessed=4 * size, transcendentals=0),
    )(*terms)


def from_z(block):
    return [swap_over(block, 2 * k, 0) for k in (1, 2, 3)]


def over_core(blocks):
    return blocks + [swap_over(block, 0, 1) for block in blocks]


def put(out_ref, lead, row, col, ref, at, left, rows, cols):
    chunk = min(rows, D // 2)

    def step(k, carry):
        to = pl.multiple_of(row + k * chunk, 32)
        source = pl.multiple_of(at + k * chunk, 32)
        out_ref[lead, pl.ds(to, chunk), col : col + cols] = ref[
            pl.ds(source, chunk), left : left + cols
        ]
        return carry

    lax.fori_loop(0, rows // chunk, step, 0)


def place_first(refs, out_ref):
    count = len(refs) // 2
    half, width = D // 2, D // 4
    for core in range(2):
        near, beside, across = refs[core * count : (core + 1) * count]
        for y in range(2):
            col = (2 * y + core) * width
            for kind in range(2):
                left = kind * width
                put(out_ref, kind, 0, col, near, y * half, left, half, width)
                put(out_ref, kind, half, col, beside, y * half, left, half, width)
                if y:
                    put(out_ref, 2 + kind, 0, col, across, 0, left, D, width)
                else:
                    put(out_ref, 2 + kind, 0, col, near, 0, half + left, D, width)


def edges_moves():
    rows, half = D // PARTS, D // 2
    moves = []
    for core in range(2):
        near, beside, across = range(3 * core, 3 * core + 3)
        for y in range(2):
            group = 2 * y + core
            for z in range(4):
                for x in range(2):
                    to, by_y, by_x = x * half + z * rows, (2 * z + y) * rows, (2 * z + x) * rows
                    moves.append((group, to, 0, beside if x else near, by_y, 0, rows, half))
                    source = (across, by_x, 0) if y else (near, by_x, half)
                    moves.append((group, to, half, *source, rows, half))
    return moves


def plane_moves():
    half = D // 2
    return [
        (2 * y + core, x * half, 0, 4 * core + 2 * y + x, 0, 0, half, D)
        for core in range(2)
        for y in range(2)
        for x in range(2)
    ]


def groups_moves(count):
    return [(group, 0, 0, group, 0, 0, D, D) for group in range(count)]


def move_all(moves, refs, out_ref, sems):
    copies = [
        pltpu.make_async_copy(
            refs[ref].at[pl.ds(at, rows), pl.ds(left, cols)],
            out_ref.at[lead, pl.ds(row, rows), pl.ds(col, cols)],
            sems.at[k],
        )
        for k, (lead, row, col, ref, at, left, rows, cols) in enumerate(moves)
    ]
    for copy in copies:
        copy.start()
    for copy in copies:
        copy.wait()


def place_kinds(refs, out_ref):
    width = D // len(refs)
    for group, ref in enumerate(refs):
        for kind in range(4):
            put(out_ref, kind, 0, group * width, ref, 0, kind * width, D, width)


def core_terms(halves):
    odd, even = halves
    return [even.reshape(2 * D, D), swap_over(odd, 0, 1).reshape(2 * D, D)]


def summed(count, row, col):
    return [(term, row, col) for term in range(count)]


def reduce_core_plane(halves):
    half = D // 2
    return merge(
        core_terms(halves),
        [(half, D, jnp.bfloat16)] * 4,
        [(k, 0, 0, half, D, summed(2, k * half, 0)) for k in range(4)],
    )


def reduce_plane(near, beside, across, opposite):
    pair = D // 4
    terms = [near, swap_over(beside, 1, 0), swap_over(across, 0, 2), swap_over(opposite, 1, 2)]
    return merge(
        terms,
        [(pair, D, jnp.bfloat16)] * 2,
        [(k, 0, 0, pair, D, summed(4, k * pair, 0)) for k in range(2)],
    )


def halve_z(near, received):
    rows = near.shape[0] // 2
    return merge(
        [near, received],
        [(rows, D, jnp.bfloat16)] * 2,
        [(k, 0, 0, rows, D, summed(2, k * rows, 0)) for k in range(2)],
    )


def add_z(near, received):
    rows = near.shape[0]
    return merge(
        [near, received], [(rows, D, jnp.float32)], [(0, 0, 0, rows, D, summed(2, 0, 0))]
    )[0]


def z_terms(own, *sent):
    return [own] + [swap_over(block, 2 * (k + 1), 0) for k, block in enumerate(sent)]


def reduce_z(terms):
    rows = D // PARTS
    return merge(terms, [(rows, D, jnp.float32)], [(0, 0, 0, rows, D, summed(4, 0, 0))])[0]


def reduce_core_edges(halves):
    half = D // 2
    return merge(
        core_terms(halves),
        [(D, D, jnp.bfloat16), (D, half, jnp.bfloat16), (D, half, jnp.bfloat16)],
        [
            (0, 0, 0, half, half, summed(2, 0, 0)),
            (0, half, 0, half, half, summed(2, D, 0)),
            (0, 0, half, D, half, summed(2, 0, half)),
            (1, 0, 0, half, half, summed(2, half, 0)),
            (1, half, 0, half, half, summed(2, D + half, 0)),
            (2, 0, 0, D, half, summed(2, D, half)),
        ],
    )


def edge_terms(near, left, right):
    return [near, swap_over(left, 1, 0), swap_over(right, 0, 2)]


def edge_sums(row):
    half = D // 2
    return ((0, [(0, row, 0), (1, row, 0)]), (half, [(0, row, half), (2, row, 0)]))


def plane_edge_terms(near, left, right):
    return [near, swap_over(left, 0, 2), swap_over(right, 1, 0)]


def reduce_edges_plane(terms):
    half = D // 2
    kept = [(0, 0, col, half, half, parts) for col, parts in edge_sums(0)]
    sent = [
        (1 + k, 0, 0, half, half, parts) for k, (_, parts) in enumerate(edge_sums(half))
    ]
    return merge(
        terms,
        [(half, D, jnp.bfloat16), (half, half, jnp.bfloat16), (half, half, jnp.bfloat16)],
        kept + sent,
    )


def reduce_plane_edges(terms):
    rows, half = D // PARTS, D // 2
    return merge(
        terms,
        [(rows, D, jnp.bfloat16)] * 4,
        [
            (k, 0, col, rows, half, parts)
            for k in range(4)
            for col, parts in edge_sums(k * rows)
        ],
    )


def reduce_edges(terms):
    rows, half = D // PARTS, D // 2
    return merge(
        terms,
        [(half, D, jnp.bfloat16)] * 2,
        [
            (k // 2, (2 * (k % 2) + q) * rows, col, rows, half, parts)
            for k in range(4)
            for q in range(2)
            for col, parts in edge_sums(q * half + k * rows)
        ],
    )


def reduce_edges_z(terms):
    rows, half = D // PARTS, D // 2
    return merge(
        terms,
        [(rows, D, jnp.bfloat16), (rows, half, jnp.bfloat16), (rows, half, jnp.bfloat16)],
        [
            (0, 0, 0, rows, D, summed(2, 0, 0)),
            (1, 0, 0, rows, half, summed(2, rows, 0)),
            (2, 0, 0, rows, half, summed(2, rows, half)),
        ],
    )


def reduce_edges_last(terms):
    rows, half = D // PARTS, D // 2
    return merge(
        terms,
        [(rows, D, jnp.float32)],
        [(0, 0, col, rows, half, parts) for col, parts in edge_sums(0)],
    )[0]


def add_swapped(values, over_dp, over_tensor):
    return values + swap_over(values, over_dp, over_tensor)


ROWS = 256


def dot_nt(left_side, right_side):
    return lax.dot_general(
        left_side, right_side, (((1,), (1,)), ((), ())), preferred_element_type=jnp.float32
    )


def row_block(array):
    return pl.BlockSpec((ROWS, array.shape[1]), lambda i: (i, 0))


def call_rows(kernel, steps, inputs, outputs, flops, transcendentals=0, scratch=()):
    arrays = [
        pltpu.with_memory_space_constraint(array, pltpu.HBM) if far else array
        for array, _, *far in inputs
    ]
    shapes = [jax.ShapeDtypeStruct(shape, dtype) for shape, dtype, *_ in outputs]
    moved = sum(a.size * a.dtype.itemsize for a in arrays + shapes)
    shapes = [
        pltpu.HBM(shape.shape, shape.dtype) if len(output) > 3 else shape
        for shape, output in zip(shapes, outputs)
    ]
    return pl.pallas_call(
        kernel,
        grid=(steps,),
        in_specs=[spec for _, spec, *_ in inputs],
        out_specs=[output[2] for output in outputs],
        out_shape=shapes,
        scratch_shapes=scratch,
        compiler_params=pltpu.CompilerParams(vmem_limit_bytes=VMEM_LIMIT),
        cost_estimate=pl.CostEstimate(
            flops=int(1.0 * flops), bytes_accessed=moved, transcendentals=transcendentals
        ),
    )(*arrays)


def norm_rows(summed):
    centred = summed - jnp.mean(summed, -1, keepdims=True)
    inverse = lax.rsqrt(jnp.mean(centred * centred, -1, keepdims=True) + NORM_EPS)
    return centred * inverse, inverse


def norm_pull(gradient, unit_rows, inverse, gain_row):
    scaled = gradient * gain_row
    return inverse * (
        scaled
        - jnp.mean(scaled, -1, keepdims=True)
        - unit_rows * jnp.mean(scaled * unit_rows, -1, keepdims=True)
    )


def add_rows(ref, rows):
    sums = [jnp.sum(row, 0, keepdims=True) for row in rows]
    start = pl.program_id(0) == 0
    for place, total in enumerate(sums):
        kept = jnp.where(start, 0.0, ref[place : place + 1, :])
        ref[place : place + 1, :] = kept + total


def settle(moves, refs, whole_ref, sems):
    @pl.when(pl.program_id(0) == 0)
    def _():
        move_all(moves, refs, whole_ref, sems)

    return [whole_ref.at[j] for j in range(whole_ref.shape[0])]


def pair_masks(length):
    wide = 2 * HEAD_DIM
    lower = lax.broadcasted_iota(jnp.int32, (length, wide), 1) < HEAD_DIM
    top = lax.broadcasted_iota(jnp.int32, (2 * length, wide), 0) < length
    left = lax.broadcasted_iota(jnp.int32, (2 * length, wide), 1) < HEAD_DIM
    return lower, top == left


def stacked(pair, own):
    return jnp.where(own, jnp.concatenate([pair, pair], 0), jnp.zeros((), pair.dtype))


def attention_kernel(place, total_count, length, *refs):
    rows_ref, across_ref, down_ref, bias_ref, vec_ref = refs[:5]
    outs = refs[5 + total_count : 12 + total_count]
    packed_ref, probs_ref, attended_ref, unit_ref, inverse_ref, low_ref, whole_ref = outs
    scores_ref, sems, *raw = refs[12 + total_count :]

    @pl.when(pl.program_id(0) == 0)
    def _():
        copies = [
            pltpu.make_async_copy(source, to, sems.at[k])
            for k, (source, to) in enumerate(zip(refs[5 : 5 + total_count], raw))
        ]
        for copy in copies:
            copy.start()
        for copy in copies:
            copy.wait()
        place(raw, whole_ref)

    weights = [whole_ref.at[kind] for kind in range(4)]
    wide = 2 * HEAD_DIM
    pairs = HEADS // 2
    rows = rows_ref[...]
    for kind in range(3):
        part = product(rows, weights[kind][...]) + bias_ref[kind : kind + 1, :]
        part = part.astype(jnp.bfloat16)
        if kind == 0:
            part = part * jnp.bfloat16(HEAD_DIM ** (-0.5))
        packed_ref[:, kind * D : (kind + 1) * D] = part
    _, own = pair_masks(length)
    steps = [(p, i) for p in range(ROWS // length) for i in range(pairs)]

    def pair_of(p, i, kind):
        span = slice(p * length, (p + 1) * length)
        return packed_ref[span, kind * D + i * wide : kind * D + (i + 1) * wide]

    for at, (p, i) in enumerate(steps):
        scores_ref[at] = dot_nt(pair_of(p, i, 0), stacked(pair_of(p, i, 1), own))
    for at, (p, i) in enumerate(steps):
        allowed = down_ref[p] == across_ref[p]
        for half in range(2):
            lanes = slice(half * length, (half + 1) * length)
            scores = jnp.where(allowed, scores_ref[at, :, lanes], MASKED)
            raised = jnp.exp(scores - jnp.max(scores, -1, keepdims=True))
            probs_ref[p, i, :, lanes] = (
                raised * (1.0 / jnp.sum(raised, -1, keepdims=True))
            ).astype(jnp.bfloat16)
    for p, i in steps:
        mixed = product(probs_ref[p, i], stacked(pair_of(p, i, 2), own))
        attended_ref[p * length : (p + 1) * length, i * wide : (i + 1) * wide] = mixed.astype(
            jnp.bfloat16
        )
    summed = rows.astype(jnp.float32) + vec_ref[0:1, :]
    summed = summed + dot_nt(attended_ref[...], weights[3][...])
    unit, inverse = norm_rows(summed)
    unit_ref[...] = unit
    inverse_ref[...] = inverse
    low_ref[...] = (unit * vec_ref[1:2, :] + vec_ref[2:3, :]).astype(jnp.bfloat16)


def gelu_parts(values):
    size = jnp.abs(values)
    decay = jnp.exp2(values * values * (-0.5 / math.log(2.0)))
    t = 1.0 / (1.0 + size * (0.3275911 * 0.5**0.5))
    poly = t * (
        0.127414796
        + t * (-0.142248368 + t * (0.7107068705 + t * (-0.7265760135 + t * 0.5307027145)))
    )
    result = jnp.maximum(values, 0.0) - size * (poly * decay)
    rest = decay * (poly - size * (0.5 / math.pi) ** 0.5)
    return result, jnp.where(values > 0, 1.0 - rest, rest)


def up_kernel(place, shards, *refs):
    low_ref, bias_ref = refs[:2]
    act_ref, slope_ref, whole_ref, sems = refs[-4:]
    weights = settle(place, refs[2:-4], whole_ref, sems)
    width = weights[0].shape[1]
    chunk = 256
    low = low_ref[...]
    for j in range(shards):
        for c in range(0, width, chunk):
            pre = product(low, weights[j][:, c : c + chunk]) + bias_ref[j : j + 1, c : c + chunk]
            result, slope = gelu_parts(pre)
            at = j * width + c
            act_ref[:, at : at + chunk] = result.astype(jnp.bfloat16)
            slope_ref[:, at : at + chunk] = slope.astype(jnp.bfloat16)


def down_kernel(place, shards, *refs):
    act_ref, unit_ref, grad_ref, vec_ref = refs[:4]
    out_ref, dz_ref, low_ref, sums_ref, whole_ref, sems = refs[-6:]
    weights = settle(place, refs[4:-6], whole_ref, sems)
    width = weights[0].shape[1]
    summed = unit_ref[...] * vec_ref[1:2, :] + vec_ref[2:3, :] + vec_ref[3:4, :]
    for j in range(shards):
        summed = summed + dot_nt(act_ref[:, j * width : (j + 1) * width], weights[j][...])
    unit, inverse = norm_rows(summed)
    gain = vec_ref[4:5, :]
    out_ref[...] = unit * gain + vec_ref[5:6, :]
    gradient = grad_ref[...]
    dz = norm_pull(gradient, unit, inverse, gain)
    dz_ref[...] = dz
    low_ref[...] = dz.astype(jnp.bfloat16)
    add_rows(sums_ref, (gradient * unit, gradient, dz))


def hidden_back_kernel(shards, *refs):
    low_ref, slope_ref, whole_ref, dpre_ref, bias_sums_ref = refs
    width = whole_ref.shape[2]
    low = low_ref[...]
    for j in range(shards):
        span = slice(j * width, (j + 1) * width)
        dpre = product(low, whole_ref[j]) * slope_ref[:, span].astype(jnp.float32)
        dpre = dpre.astype(jnp.bfloat16)
        dpre_ref[:, span] = dpre
        total = jnp.sum(dpre.astype(jnp.float32), 0, keepdims=True)
        kept = jnp.where(pl.program_id(0) == 0, 0.0, bias_sums_ref[j : j + 1, :])
        bias_sums_ref[j : j + 1, :] = kept + total


def back_kernel(shards, *refs):
    dpre_ref, dz_ref, unit_ref, inverse_ref, vec_ref, up_ref, first_ref = refs[:7]
    dz1_ref, low1_ref, datt_ref, sums_ref = refs[7:]
    width = up_ref.shape[2]
    gradient = dz_ref[...]
    for j in range(shards):
        gradient = gradient + dot_nt(dpre_ref[:, j * width : (j + 1) * width], up_ref[j])
    unit = unit_ref[...]
    dz1 = norm_pull(gradient, unit, inverse_ref[...], vec_ref[1:2, :])
    dz1_ref[...] = dz1
    low1 = dz1.astype(jnp.bfloat16)
    low1_ref[...] = low1
    add_rows(sums_ref, (gradient * unit, gradient, dz1))
    datt_ref[...] = product(low1, first_ref[3]).astype(jnp.bfloat16)


def attention_back_kernel(length, *refs):
    datt_ref, attended_ref, packed_ref, probs_ref, dpacked_ref, sums_ref, up_ref, grad_ref = refs
    wide = 2 * HEAD_DIM
    lower, own = pair_masks(length)
    ones = own.astype(jnp.bfloat16)
    steps = [(p, i) for p in range(ROWS // length) for i in range(HEADS // 2)]

    def pair_of(p, i, kind):
        span = slice(p * length, (p + 1) * length)
        return packed_ref[span, kind * D + i * wide : kind * D + (i + 1) * wide]

    def keep(p, i, kind, grad):
        span = slice(p * length, (p + 1) * length)
        dpacked_ref[span, kind * D + i * wide : kind * D + (i + 1) * wide] = grad.astype(
            jnp.bfloat16
        )

    for place, (p, i) in enumerate(steps):
        span = slice(p * length, (p + 1) * length)
        lanes = slice(i * wide, (i + 1) * wide)
        upstream = datt_ref[span, lanes]
        up_ref[place, :, :wide] = upstream
        up_ref[place, :, wide:] = (
            upstream.astype(jnp.float32) * attended_ref[span, lanes].astype(jnp.float32)
        ).astype(jnp.bfloat16)
    for place, (p, i) in enumerate(steps):
        centred = dot_nt(
            up_ref[place], jnp.concatenate([stacked(pair_of(p, i, 2), own), -ones], 1)
        )
        grad_ref[place] = (probs_ref[p, i].astype(jnp.float32) * centred).astype(jnp.bfloat16)
    for place, (p, i) in enumerate(steps):
        grad_scores = grad_ref[place]
        keep(
            p, i, 0,
            product(grad_scores, stacked(pair_of(p, i, 1), own)) * HEAD_DIM ** (-0.5),
        )
        both = transposed_times(grad_scores, pair_of(p, i, 0))
        keep(p, i, 1, jnp.where(lower, both[:length], both[length:]))
        both = transposed_times(probs_ref[p, i], up_ref[place, :, :wide])
        keep(p, i, 2, jnp.where(lower, both[:length], both[length:]))
    total = jnp.sum(dpacked_ref[...].astype(jnp.float32), 0, keepdims=True)
    kept = jnp.where(pl.program_id(0) == 0, 0.0, sums_ref[0:1, :])
    sums_ref[0:1, :] = kept + total


def weight_kernel(odd, count, *refs):
    lefts = refs[: 2 if count > 1 else 1]
    rights, out_ref = refs[len(lefts) : -1], refs[-1]
    if count == 1:
        out_ref[0] = transposed_times(lefts[0][...], rights[0][...]).astype(jnp.bfloat16)
    else:
        half = rights[0].shape[1] // 2
        span = slice(half, 2 * half) if odd else slice(0, half)
        values = jnp.concatenate([right[:, span] for right in rights[:-1]], 1)
        width = values.shape[1]
        out_ref[0, :, :width] = transposed_times(lefts[0][...], values).astype(jnp.bfloat16)
        out_ref[0, :, width:] = transposed_times(lefts[1][...], rights[-1][:, span]).astype(
            jnp.bfloat16
        )


def weight_half(odd, lefts, rights):
    count = len(rights)
    single = count == 1
    specs = []
    for array, width, before in rights:
        if single:
            specs.append(pl.BlockSpec((array.shape[0], width), lambda i: (0, 2 * i + odd)))
        else:
            specs.append(pl.BlockSpec((array.shape[0], 2 * width), lambda i, b=before: (0, b + i)))
    arrays = [*lefts, *[array for array, _, _ in rights]]
    tokens = lefts[0].shape[0]
    (half,) = pl.pallas_call(
        functools.partial(weight_kernel, odd, count),
        grid=(2,),
        in_specs=[pl.BlockSpec(memory_space=pltpu.VMEM) for _ in lefts] + specs,
        out_specs=[pl.BlockSpec((1, D, D), lambda i: (i, 0, 0))],
        out_shape=[jax.ShapeDtypeStruct((2, D, D), jnp.bfloat16)],
        compiler_params=pltpu.CompilerParams(vmem_limit_bytes=VMEM_LIMIT),
        cost_estimate=pl.CostEstimate(
            flops=4 * tokens * D * D,
            bytes_accessed=sum(2 * array.size for array in arrays),
            transcendentals=0,
        ),
    )(*arrays)
    return half


def weight_halves(lefts, rights):
    return [weight_half(odd, lefts, rights) for odd in (1, 0)]


def two_terms(values):
    top = values.astype(jnp.bfloat16)
    return top, (values - top.astype(jnp.float32)).astype(jnp.bfloat16)


def adam_kernel(*refs):
    flip_ref, grad_ref, master_ref, left_ref, right_ref, first_ref, second_ref = refs[:7]
    master_out, first_out, second_out = refs[7:]
    bias_first = 1.0 - DECAY_FIRST**ADAM_STEP
    bias_second = 1.0 - DECAY_SECOND**ADAM_STEP
    count = grad_ref.shape[0]
    lefts = [two_terms(left_ref[k]) for k in range(count)]
    rights = [two_terms(right_ref[k]) for k in range(count)]
    turned = []
    for k in range(count):
        tile = grad_ref[k].astype(jnp.float32)
        flip = flip_ref[pl.program_id(0) * count + k] > 0
        tile = jnp.where(flip, tile.T, tile)
        top, rest = two_terms(tile)
        grad = product(top, rights[k][0]) + product(top, rights[k][1])
        if grad_ref.dtype != jnp.bfloat16:
            grad = grad + product(rest, rights[k][0])
        turned.append(grad)
    directions = []
    for k in range(count):
        top, rest = two_terms(turned[k])
        rotated = (
            transposed_times(lefts[k][0], top)
            + transposed_times(lefts[k][0], rest)
            + transposed_times(lefts[k][1], top)
        )
        first = DECAY_FIRST * first_ref[k] + (1.0 - DECAY_FIRST) * rotated
        second = DECAY_SECOND * second_ref[k] + (1.0 - DECAY_SECOND) * rotated * rotated
        first_out[k] = first
        second_out[k] = second
        directions.append(first / bias_first / (jnp.sqrt(second / bias_second) + ADAM_EPS))
    backs = [
        product(lefts[k][0], directions[k].astype(jnp.bfloat16)).astype(jnp.bfloat16)
        for k in range(count)
    ]
    for k in range(count):
        update = times_transposed(backs[k], rights[k][0])
        master_out[k] = master_ref[k] - MATRIX_RATE * update


def unpermuted(values, selector_ref):
    top, rest = two_terms(values)
    return dot_nt(top, selector_ref[...]) + dot_nt(rest, selector_ref[...])


def enter_kernel(tokens_ref, grad_ref, vectors_ref, selector_ref, rows_ref, out_ref, d_rows_ref):
    selector = selector_ref[...]
    rows_ref[...] = product(tokens_ref[...], selector).astype(jnp.bfloat16)
    top, rest = two_terms(grad_ref[...])
    out_ref[...] = product(top, selector) + product(rest, selector)

    @pl.when(pl.program_id(0) == 0)
    def _():
        rows = vectors_ref[...]
        permuted = jnp.zeros(rows.shape, jnp.float32)
        for _ in range(3):
            term = rows.astype(jnp.bfloat16)
            rows = rows - term.astype(jnp.float32)
            permuted = permuted + product(term, selector)
        d_rows_ref[...] = permuted


def layer_kernel(out_ref, selector_ref, layer_ref):
    layer_ref[...] = unpermuted(out_ref[...], selector_ref)


def input_kernel(dz1_ref, dpacked_ref, selector_ref, whole_ref, input_ref):
    gradient = dz1_ref[...]
    for kind in range(3):
        gradient = gradient + dot_nt(dpacked_ref[:, kind * D : (kind + 1) * D], whole_ref[kind])
    input_ref[...] = unpermuted(gradient, selector_ref)


def vector_kernel(shards, *refs):
    base_ref, first_ref, second_ref, hidden_ref, columns_ref, selector_ref, out_ref = refs
    base = base_ref[0]
    rows = jnp.concatenate(
        [
            first_ref[0:1, :],
            second_ref[0:1, :],
            first_ref[2:3, :],
            second_ref[2:3, :],
            first_ref[1:2, :],
            second_ref[1:2, :],
            jnp.zeros((2, D), jnp.float32),
        ],
        0,
    )
    natural = jnp.zeros((8, D), jnp.float32)
    for _ in range(3):
        term = rows.astype(jnp.bfloat16)
        rows = rows - term.astype(jnp.float32)
        natural = natural + dot_nt(term, selector_ref[...])
    hidden = FF // D
    out_ref[...] = jnp.zeros(out_ref.shape, jnp.float32)
    for at, row in ((0, 0), (1, 1), (4, 2), (5 + hidden, 3), (6 + hidden, 4), (7 + hidden, 5)):
        out_ref[at : at + 1, :] = natural[row : row + 1, :]
    width = D // shards
    for j in range(shards):
        out_ref[5 + j : 6 + j, :] = hidden_ref[pl.ds(j ^ base, 1), :]
        for at, kind in ((2, 0), (3, 2)):
            parts = [
                jnp.where(
                    (j ^ base) == k,
                    columns_ref[0:1, kind * D + k * width : kind * D + (k + 1) * width],
                    0.0,
                )
                for k in range(shards)
            ]
            out_ref[at : at + 1, j * width : (j + 1) * width] = sum(parts)


def together(*values):
    return lax.optimization_barrier(values)


def local(
    tokens,
    segments,
    out_grad,
    owner,
    master,
    left_basis,
    right_basis,
    first_moment,
    second_moment,
    vectors,
    vector_first,
    vector_second,
):
    shards = lax.axis_size("tensor")
    dp_size = lax.axis_size("dp")
    direct = dp_size == PARTS and shards == 4
    tensor_rank = lax.axis_index("tensor")
    dp_rank = lax.axis_index("dp")
    local_heads = HEADS // shards
    head_width = local_heads * HEAD_DIM
    up_width = FF // shards
    width_qkv = 3 * head_width
    block_size = master.shape[-1]
    slots = master.shape[1]
    row_count = tokens.shape[0]
    length = segments.shape[1]
    pack_count = row_count // length
    own_segments = lax.dynamic_slice_in_dim(segments, tensor_rank * pack_count, pack_count, 0)
    qkv_tiles, out_tiles, up_tiles = tile_counts(shards, block_size)
    tile_total = owner.shape[0]

    group_base = tensor_rank if direct else 0
    order = feature_order(dp_rank if direct else 0)
    selector = (lax.iota(jnp.int32, D)[:, None] == order[None, :]).astype(jnp.bfloat16)

    steps = row_count // ROWS
    f32, bf16 = jnp.float32, jnp.bfloat16
    rows_spec = lambda width: pl.BlockSpec((ROWS, width), lambda i: (i, 0))
    full = lambda array: (array, pl.BlockSpec(memory_space=pltpu.VMEM))
    raw = lambda array: (array, pl.BlockSpec(memory_space=pl.ANY))
    by_rows = lambda array: (array, row_block(array))
    far_rows = lambda array: (array, row_block(array), "far")
    group_order = lax.iota(jnp.int32, shards) ^ group_base
    below = vectors[: 5 * D].reshape(5, D)
    above = vectors[5 * D + FF :].reshape(3, D)
    d_rows = jnp.stack(
        [below[4], below[0], above[1], above[0], below[1], above[2], below[0], below[0]]
    )
    bias_q = below[2].reshape(shards, head_width)[group_order]
    bias_v = below[3].reshape(shards, head_width)[group_order]
    bias_up = vectors[5 * D : 5 * D + FF].reshape(shards, up_width)[group_order]
    rows_in, grad_out, d_rows = call_rows(
        enter_kernel,
        steps,
        [far_rows(tokens), far_rows(out_grad), full(d_rows), full(selector)],
        [
            ((row_count, D), bf16, rows_spec(D), "far"),
            ((row_count, D), f32, rows_spec(D), "far"),
            ((8, D), f32, pl.BlockSpec(memory_space=pltpu.VMEM)),
        ],
        6 * row_count * D * D,
    )

    def flipped(index):
        from_out = (index >= qkv_tiles) & (index < qkv_tiles + out_tiles)
        return (from_out | (index >= qkv_tiles + out_tiles + up_tiles))[:, None, None]

    own_tiles = lax.dynamic_slice_in_dim(owner, dp_rank * slots, slots, 0)
    own_flip = flipped(own_tiles)
    sent = master[0].astype(jnp.bfloat16)
    sent = jnp.where(own_flip, jnp.swapaxes(sent, 1, 2), sent)
    placing = (lax.iota(jnp.int32, tile_total)[:, None] == owner[None, :]).astype(jnp.bfloat16)
    if direct:
        parts = sent.reshape(slots, PARTS, SUB * block_size).swapaxes(0, 1)
        parts = lax.all_to_all(parts, "dp", 0, 0, tiled=True).reshape(tile_total, -1)
        tiles = product(placing, parts).astype(jnp.bfloat16)
        slab = slabs_from_tiles(tiles.reshape(tile_total, 1, SUB, block_size), shards, block_size)[0]
        half, rows = D // 2, D // PARTS
        first_slab, up_slab, down_slab = (slab[:, k * D : (k + 1) * D] for k in range(3))
        near_left, near_right = down_slab[:, :half], down_slab[:, half:]
        *blocks, near_left, near_right, rows_in, grad_out, d_rows, bias_up = together(
            *from_z(first_slab),
            swap_over(near_left, 0, 2),
            swap_over(near_right, 1, 0),
            rows_in,
            grad_out,
            d_rows,
            bias_up,
        )
        left, right, down_near = merge(
            [first_slab, *blocks, down_slab, near_left, near_right],
            [(half, half, bf16), (half, half, bf16), (2 * rows, D, bf16)],
            [(k, z * rows, 0, rows, half, [(z, 0, k * half)]) for k in range(2) for z in range(4)]
            + [
                (2, 0, 0, rows, D, [(4, 0, 0)]),
                (2, rows, 0, rows, half, [(5, 0, 0)]),
                (2, rows, half, rows, half, [(6, 0, 0)]),
            ],
        )
        left, right, down_near, up_slab = together(left, right, down_near, up_slab)
        up_beside = swap_over(up_slab, 2, 0)
        (up_pair,) = merge(
            [up_slab, up_beside],
            [(2 * rows, D, bf16)],
            [(0, z * rows, 0, rows, D, [(z, 0, 0)]) for z in range(2)],
        )
        left_across, right_beside, up_pair = together(
            swap_over(left, 0, 2), swap_over(right, 1, 0), up_pair
        )
        near, left, right = merge(
            [left, left_across, right, right_beside],
            [(D, D, bf16), (D, half, bf16), (D, half, bf16)],
            [
                (out, q * half, col, half, half, [(2 * k + q, 0, 0)])
                for k in range(2)
                for q in range(2)
                for out, col in ((0, k * half), (1 + k, 0))
            ],
        )
        near, down_near = together(near, down_near)
        down_beside = swap_over(down_near, 2, 0)
        near_there, beside, across, up_far, down_beside = together(
            swap_over(near, 0, 1),
            swap_over(left, 1, 0),
            swap_over(right, 0, 2),
            swap_over(up_pair, 4, 0),
            down_beside,
        )
        up_z, down_pair = merge(
            [up_pair, up_far, down_near, down_beside],
            [(half, D, bf16)] * 2,
            [
                (k, z * 2 * rows, 0, 2 * rows, D, [(2 * k + z, 0, 0)])
                for k in range(2)
                for z in range(2)
            ],
        )
        first = [near, beside, across, near_there] + over_core([beside, across])[2:]
        up = [up_z, swap_over(up_z, 1, 0), swap_over(up_z, 0, 2), swap_over(up_z, 1, 2)]
        down_far = swap_over(down_pair, 4, 0)
        places = (place_first, plane_moves(), edges_moves())
        pieces = [first, None, None]
    else:
        gathered = lax.all_gather(sent, "dp", axis=0, tiled=True).reshape(tile_total, -1)
        tiles = product(placing, gathered).astype(jnp.bfloat16)
        slabs = slabs_from_tiles(
            tiles.reshape(tile_total, PARTS, SUB, block_size), shards, block_size
        )
        whole = jnp.concatenate([slabs[part_of_block(k)] for k in range(PARTS)], 0)
        every = lax.all_gather(whole, "tensor", axis=0)
        pieces = [
            [every[j][:, k * D : (k + 1) * D] for j in range(shards)] for k in range(3)
        ]
        places = (place_kinds, groups_moves(shards), groups_moves(shards))

    packs_step = ROWS // length
    bias_qkv = jnp.stack(
        [bias_q.reshape(D), jnp.zeros((D,), jnp.float32), bias_v.reshape(D)]
    )
    pairs = HEADS // 2
    probs_spec = pl.BlockSpec((packs_step, pairs, length, 2 * length), lambda i: (i, 0, 0, 0))
    sums_spec = lambda width: pl.BlockSpec((8, width), lambda i: (0, 0))
    square = 2 * row_count * D * D

    whole_out = ((shards, D, D), bf16, pl.BlockSpec(memory_space=pltpu.VMEM))
    packed, probs, attended, unit_first, inverse_first, normed_low, whole_first = call_rows(
        functools.partial(attention_kernel, places[0], len(pieces[0]), length),
        steps,
        [
            far_rows(rows_in),
            (own_segments[:, None, :], pl.BlockSpec((packs_step, 1, length), lambda i: (i, 0, 0))),
            (own_segments[:, :, None], pl.BlockSpec((packs_step, length, 1), lambda i: (i, 0, 0))),
            full(bias_qkv),
            full(d_rows),
            *[raw(w) + (("far",) if w.shape == (D, D) else ()) for w in pieces[0]],
        ],
        [
            ((row_count, 3 * D), bf16, rows_spec(3 * D), "far"),
            ((pack_count, pairs, length, 2 * length), bf16, probs_spec, "far"),
            ((row_count, D), bf16, rows_spec(D)),
            ((row_count, D), f32, rows_spec(D), "far"),
            ((row_count, 1), f32, rows_spec(1), "far"),
            ((row_count, D), bf16, rows_spec(D), "far"),
            whole_out,
        ],
        4 * square + 4 * row_count * length * D,
        row_count * length * HEADS,
        [
            pltpu.VMEM((packs_step * pairs, length, 2 * length), f32),
            pltpu.SemaphoreType.DMA((len(pieces[0]),)),
            *[pltpu.VMEM(w.shape, bf16) for w in pieces[0]],
        ],
    )
    if direct:
        up[0], normed_low = together(up[0], normed_low)
        *up, up_there, down_far, normed_low = together(
            *up, swap_over(up[0], 0, 1), down_far, normed_low
        )
        down_near, near_left, near_right = merge(
            [down_pair, down_far],
            [(D, D, bf16), (D, half, bf16), (D, half, bf16)],
            [(0, z * half, 0, half, D, [(z, 0, 0)]) for z in range(2)]
            + [
                (1 + k, z * half, 0, half, half, [(z, 0, k * half)])
                for k in range(2)
                for z in range(2)
            ],
        )
        down = [down_near, swap_over(near_left, 1, 0), swap_over(near_right, 0, 2)]
        pieces[1] = up + [up_there] + over_core(up[1:])[3:]
    activated, slope, whole_up = call_rows(
        functools.partial(up_kernel, places[1], shards),
        steps,
        [far_rows(normed_low), full(bias_up), *[raw(w) for w in pieces[1]]],
        [
            ((row_count, FF), bf16, rows_spec(FF)),
            ((row_count, FF), bf16, rows_spec(FF)),
            whole_out,
        ],
        40 * square,
        2 * row_count * FF,
        [pltpu.SemaphoreType.DMA((len(places[1]),))],
    )
    if direct:
        *down, down_there, activated = together(*down, swap_over(down[0], 0, 1), activated)
        pieces[2] = down + [down_there] + over_core(down[1:])[2:]
    layer_out, grad_second, second_low, sums_second, whole_down = call_rows(
        functools.partial(down_kernel, places[2], shards),
        steps,
        [
            by_rows(activated),
            far_rows(unit_first),
            far_rows(grad_out),
            full(d_rows),
            *[raw(w) for w in pieces[2]],
        ],
        [
            ((row_count, D), f32, rows_spec(D), "far"),
            ((row_count, D), f32, rows_spec(D)),
            ((row_count, D), bf16, rows_spec(D)),
            ((8, D), f32, sums_spec(D)),
            whole_out,
        ],
        4 * square,
        0,
        [pltpu.SemaphoreType.DMA((len(places[2]),))],
    )
    grad_w_down = weight_halves([second_low], [(activated, up_width, 0)])
    if direct:
        down_parts = reduce_core_plane(grad_w_down)
        second_low, *down_parts = together(second_low, *down_parts)
        down_parts = reduce_plane(*down_parts)
    grad_pre, grad_bias_up = call_rows(
        functools.partial(hidden_back_kernel, shards),
        steps,
        [by_rows(second_low), by_rows(slope), full(whole_down)],
        [((row_count, FF), bf16, rows_spec(FF)), ((8, up_width), f32, sums_spec(up_width))],
        4 * square,
    )
    grad_w_up = weight_halves([normed_low], [(grad_pre, up_width, 0)])
    grad_first, first_low, grad_attended, sums_first = call_rows(
        functools.partial(back_kernel, shards),
        steps,
        [
            by_rows(grad_pre),
            by_rows(grad_second),
            far_rows(unit_first),
            far_rows(inverse_first),
            full(d_rows),
            full(whole_up),
            full(whole_first),
        ],
        [
            ((row_count, D), f32, rows_spec(D), "far"),
            ((row_count, D), bf16, rows_spec(D)),
            ((row_count, D), bf16, rows_spec(D)),
            ((8, D), f32, sums_spec(D)),
        ],
        20 * square,
    )
    if direct:
        up_parts = reduce_core_edges(grad_w_up)
        grad_attended, *parts = together(grad_attended, *up_parts, *down_parts)
        up_terms = edge_terms(*parts[:3])
        down_terms = [parts[3], swap_over(parts[4], 4, 0)]
    grad_packed, column_sums = call_rows(
        functools.partial(attention_back_kernel, length),
        steps,
        [by_rows(grad_attended), by_rows(attended), far_rows(packed), (probs, probs_spec, "far")],
        [
            ((row_count, 3 * D), bf16, rows_spec(3 * D)),
            ((8, 3 * D), f32, sums_spec(3 * D)),
        ],
        8 * square,
        0,
        [pltpu.VMEM((packs_step * pairs, length, 2 * length), bf16)] * 2,
    )
    rights = [(grad_packed, head_width, k * shards // 2) for k in range(3)]
    rights.append((attended, head_width, 0))
    grad_w_first = [weight_half(1, [rows_in, first_low], rights)]
    if direct:
        first_low, grad_w_first[0], *others = together(
            first_low, grad_w_first[0], *up_terms, *down_terms
        )
        up_terms, down_terms = others[:3], others[3:]
        up_near, up_far, first_low = together(*reduce_edges(up_terms), first_low)
        up_terms = [up_near, swap_over(up_far, 4, 0)]
    grad_w_first.append(weight_half(0, [rows_in, first_low], rights))
    if direct:
        first_parts = reduce_core_edges(grad_w_first)
        *first_parts, grad_first = together(*first_parts, grad_first)
        first_terms = edge_terms(*first_parts)
    (input_grad,) = call_rows(
        input_kernel,
        steps,
        [far_rows(grad_first), by_rows(grad_packed), full(selector), full(whole_first)],
        [((row_count, D), f32, rows_spec(D), "far")],
        40 * square,
    )
    if direct:
        *first_terms, input_grad, layer_out = together(*first_terms, input_grad, layer_out)
        first_terms = plane_edge_terms(*reduce_edges_plane(first_terms))
        first_terms[0], *others = together(
            first_terms[0],
            *up_terms,
            *down_terms,
            sums_first,
            sums_second,
            grad_bias_up,
            column_sums,
        )
        up_terms, down_terms = others[:2], others[2:4]
        sums_first, sums_second, grad_bias_up, column_sums = others[4:]
        up_terms = halve_z(*up_terms)
        up_terms = [up_terms[0], swap_over(up_terms[1], 2, 0)]
        down_terms = halve_z(*down_terms)
        down_terms = [down_terms[0], swap_over(down_terms[1], 2, 0)]
    (vector_rows,) = call_rows(
        functools.partial(vector_kernel, shards),
        1,
        [
            (
                lax.convert_element_type(group_base, jnp.int32).reshape(1),
                pl.BlockSpec(memory_space=pltpu.SMEM),
            ),
            full(sums_first),
            full(sums_second),
            full(grad_bias_up),
            full(column_sums),
            full(selector),
        ],
        [((16, D), f32, pl.BlockSpec(memory_space=pltpu.VMEM))],
        48 * D * D,
    )
    (layer_out,) = call_rows(
        layer_kernel,
        steps,
        [far_rows(layer_out), full(selector)],
        [((row_count, D), f32, rows_spec(D), "far")],
        2 * square,
    )
    if direct:
        *first_terms, layer_out = together(*first_terms, layer_out)
        *parts, vector_rows = together(*reduce_plane_edges(first_terms), vector_rows)
        first_terms = z_terms(*parts)
        first_terms[0], *others = together(first_terms[0], *up_terms, *down_terms)
        up_terms, down_terms = others[:2], others[2:]
        down_own = add_z(*down_terms)
        vector_rows = add_swapped(add_swapped(vector_rows, 0, 1), 0, 2)
        up_terms = plane_edge_terms(*reduce_edges_z(up_terms))
        up_own = reduce_edges_last(up_terms)
        *first_terms, vector_rows = together(*first_terms, vector_rows)
        first_own = reduce_z(first_terms)
        slab_grad = jnp.concatenate([first_own, up_own, down_own], 1).astype(jnp.bfloat16)
        tile_grad = tiles_from_slabs(slab_grad[None], shards, block_size).reshape(tile_total, -1)
        slot_grad = transposed_times(placing, tile_grad).astype(jnp.bfloat16)
        slot_grad, vector_rows = together(slot_grad, vector_rows)
        slot_grad = lax.all_to_all(
            slot_grad.reshape(PARTS, slots, SUB * block_size), "dp", 0, 0, tiled=True
        )
        vector_rows = add_swapped(add_swapped(vector_rows, 1, 0), 2, 0)
        slot_grad, vector_rows = together(slot_grad, vector_rows)
        vector_rows = add_swapped(vector_rows, 4, 0)
        owned_grads = slot_grad.swapaxes(0, 1).reshape(slots, block_size, block_size)
    else:
        every = jnp.stack(
            [
                jnp.concatenate(
                    [half[1 - j % 2][j // 2] for half in (grad_w_first, grad_w_up, grad_w_down)], 1
                )
                for j in range(shards)
            ]
        ).astype(jnp.float32)
        mine = lax.psum_scatter(every, "tensor", scatter_dimension=0, tiled=True)[0]
        blocks = mine.reshape(PARTS, D // PARTS, -1)
        blocks = jnp.stack([blocks[(p % 2) * 4 + p // 2] for p in range(PARTS)])
        tile_grad = tiles_from_slabs(blocks, shards, block_size)
        slot_grad = tile_grad.reshape(tile_total, block_size, block_size)[owner]
        owned_grads = lax.psum_scatter(slot_grad, "dp", scatter_dimension=0, tiled=True)

    bias_first = 1.0 - DECAY_FIRST**ADAM_STEP
    bias_second = 1.0 - DECAY_SECOND**ADAM_STEP
    step_slots = max(k for k in (1, 2, 3, 4, 6, 12) if slots % k == 0)
    slots_spec = pl.BlockSpec((step_slots, block_size, block_size), lambda i: (i, 0, 0))
    slot_out = ((slots, block_size, block_size), f32, slots_spec, "far")
    new_master, new_first, new_second = call_rows(
        adam_kernel,
        slots // step_slots,
        [(own_flip.astype(jnp.int32).reshape(slots), pl.BlockSpec(memory_space=pltpu.SMEM))]
        + [
            (array, slots_spec, "far")
            for array in (
                owned_grads,
                master[0],
                left_basis[0],
                right_basis[0],
                first_moment[0],
                second_moment[0],
            )
        ],
        [slot_out] * 3,
        22 * slots * block_size**3,
        slots * block_size**2,
    )
    if not direct:
        vector_rows = lax.psum(vector_rows, ("dp", "tensor"))
    vector_grad = vector_rows[: vectors.shape[0] // D].reshape(-1)
    new_vector_first = DECAY_FIRST * vector_first + (1.0 - DECAY_FIRST) * vector_grad
    new_vector_second = (
        DECAY_SECOND * vector_second + (1.0 - DECAY_SECOND) * vector_grad * vector_grad
    )
    new_vectors = vectors - VECTOR_RATE * (new_vector_first / bias_first) / (
        jnp.sqrt(new_vector_second / bias_second) + ADAM_EPS
    )
    return (
        layer_out,
        input_grad,
        new_master[None],
        new_first[None],
        new_second[None],
        new_vectors,
        new_vector_first,
        new_vector_second,
    )


def solution(mesh):
    return jax.shard_map(
        local,
        mesh=mesh,
        in_specs=(
            P(("dp", "tensor"), None),
            P("dp", None),
            P(("dp", "tensor"), None),
            P(),
            P("tensor", "dp", None, None),
            P("tensor", "dp", None, None),
            P("tensor", "dp", None, None),
            P("tensor", "dp", None, None),
            P("tensor", "dp", None, None),
            P(),
            P(),
            P(),
        ),
        out_specs=(
            P(("dp", "tensor"), None),
            P(("dp", "tensor"), None),
            P("tensor", "dp", None, None),
            P("tensor", "dp", None, None),
            P("tensor", "dp", None, None),
            P(),
            P(),
            P(),
        ),
        check_vma=False,
    )
```
